32 devices in a mesh: head: 4 (over x, core), blk: 8 (over z, y).
Axes of the slice: x: 2, y: 2, z: 4, core: 2. Of those that a mesh axis runs over, the one named last changes fastest.
Arguments:
- inputs: bfloat16 [4096, 512], P(('blk', 'head')), may hold values from -6 to 6
- ln1_gain: bfloat16 [512], P('blk'), may hold values from 0.5 to 1.5
- w_qkv: bfloat16 [512, 1536], P('blk'), may hold values from -0.25 to 0.25
- w_out: bfloat16 [512, 512], P('blk'), may hold values from -2 to 2
- ln2_gain: bfloat16 [512], P('blk'), may hold values from 0.5 to 1.5
- w_router: bfloat16 [512, 8], P('blk'), may hold values from -0.25 to 0.25
- expert_in: bfloat16 [8, 512, 2048], P('blk'), may hold values from -0.25 to 0.25
- expert_out: bfloat16 [8, 2048, 512], P('blk'), may hold values from -2 to 2
- routes: int32 [4096, 2], P(('blk', 'head')), may hold values from 0 to 7, all different within a row
- priority: int32 [32, 128], P(('blk', 'head')), may hold values from 0 to 127, each once within a row
- doc_lengths: int32 [16], replicated, may hold values from 1 to 2048, 4096 in all
- d_out: float32 [4096, 512], P(('blk', 'head')), may hold values from -6 to 6
Outputs:
- output: bfloat16 [4096, 512], P(('blk', 'head'))
- d_inputs: float32 [4096, 512], P(('blk', 'head'))
- d_ln1_gain: float32 [512], P('blk')
- d_w_qkv: float32 [512, 1536], P('blk')
- d_w_out: float32 [512, 512], P('blk')
- d_ln2_gain: float32 [512], P('blk')
- d_w_router: float32 [512, 8], P('blk')
- d_expert_in: float32 [8, 512, 2048], P('blk')
- d_expert_out: float32 [8, 2048, 512], P('blk')
The draws below stay inside these ranges and needn't reach their ends.
Inputs may be any that keep to these rules, and one draw needn't show every extreme that they name: `routes`: each token names two different experts. `priority`: each row holds every rank from 0 to 127 once. `doc_lengths`: the documents' lengths sum to 4096; the longest has exactly 2048 tokens.
All inputs are finite; a program needn't handle non-finite values.
Results may differ from the reference program's by a relative error of at most 0.022.
Values may be sent and summed in bfloat16 or wider, within the bound.
A program may use at most 128 MiB of HBM per device.

```python
import math
import jax
import jax.numpy as jnp
import numpy as np
from jax import lax

D = 512
H = 8
HS = 64
FF = 2048
TOK_DEV = 128
KEY_BLOCK = 2048
DOCS = 16
EXPERTS = 8
TOKENS = 4096
CAP = 32
DOC_MOST = 2048


def steps_of(own_key, extent, pieces, smallest, high):
    def one(axis_at, parts):
        steps = jax.random.uniform(jax.random.fold_in(jax.random.fold_in(own_key, 6), axis_at), (parts,), jnp.float32, smallest / len(pieces), high / len(pieces))
        return jnp.repeat(jnp.exp(steps), extent[axis_at] // parts).reshape((-1,) + (1,) * (len(extent) - axis_at - 1))

    level = one(*pieces[0])
    for cut in pieces[1:]:
        level = level * one(*cut)
    return level


def different_ones(stream_key, rows, amount, top, lift):
    sequence = jax.random.permutation(jax.random.fold_in(stream_key, 1), amount)
    pull = sequence
    for power in range(3):
        pull = pull * pull // amount
    pull = pull * lift // amount
    lots = jax.random.randint(jax.random.fold_in(stream_key, 2), (rows, amount), 0, 4096) + pull
    holders = jax.random.permutation(jax.random.fold_in(stream_key, 3), rows)[jnp.arange(amount) % rows]
    lots = jnp.where(jnp.arange(rows)[:, None] == holders[None, :], 1 << 14, lots)
    score = lots * amount + jnp.arange(amount)
    return lax.top_k(score.astype(jnp.int32), top)[1].astype(jnp.int32)


def split_up(number_of, total, bound, skew):
    weights = [(1 << 20) // math.isqrt(rank ** skew) + 1 for rank in range(2, number_of + 1)]
    spare, holding = total - bound - (number_of - 1), [1] * (number_of - 1)
    while spare > 0:
        free = [i for i in range(number_of - 1) if holding[i] < bound]
        whole, budget = sum([weights[i] for i in free]), spare
        for i in free:
            more = min(bound - holding[i], max(1, budget * weights[i] // whole), spare)
            holding[i] = holding[i] + more
            spare = spare - more
    return np.array([bound] + holding)


def ragged_sizes(stream_key, number_of, total, most, slope):
    if number_of == 2:
        one = jax.random.randint(stream_key, (), max(1, total - most), min(most, total - 1) + 1)
        return jnp.stack([one, total - one])
    lengths = jnp.asarray(split_up(number_of, total, most, slope), jnp.int32)
    pairs = (number_of - 1) // 2
    giver, taker = lengths[1:1 + 2 * pairs:2], lengths[2:2 + 2 * pairs:2]
    slack = jnp.minimum(giver - 1, most - taker)
    shifted = jax.random.randint(jax.random.fold_in(stream_key, 1), (pairs,), 0, 1 << 20) % (slack + 1)
    lengths = lengths.at[1:1 + 2 * pairs:2].set(giver - shifted).at[2:2 + 2 * pairs:2].set(taker + shifted)
    return lengths[jax.random.permutation(jax.random.fold_in(stream_key, 2), number_of)]


def noise(key, extent, scale, reach, shards=(), kind=jnp.bfloat16):
    drawn = jax.random.normal(key, extent, jnp.float32) * scale
    if len(shards) > 0:
        drawn = steps_of(key, extent, shards, -0.22, 0.18) * drawn
    return jnp.clip(drawn, min=-reach, max=reach).astype(kind)


def setup_inputs(seed: int = 0) -> dict:
    arg_keys = jax.random.split(jax.random.key(seed), 13)
    return {
        "inputs": noise(arg_keys[0], (TOKENS, D), 1.0, 6.0, ((0, 32),)),
        "ln1_gain": jnp.clip(1.0 + 0.1 * jax.random.normal(arg_keys[1], (D,), jnp.float32), 0.5, 1.5).astype(jnp.bfloat16),
        "w_qkv": noise(arg_keys[2], (D, 3 * D), D ** -0.5, 0.25, ((0, 8),)),
        "w_out": noise(arg_keys[3], (D, D), (max(D // 64, 1)) ** -0.5, 2.0, ((0, 8),)),
        "ln2_gain": jnp.clip(1.0 + 0.1 * jax.random.normal(arg_keys[4], (D,), jnp.float32), 0.5, 1.5).astype(jnp.bfloat16),
        "w_router": noise(arg_keys[5], (D, EXPERTS), D ** -0.5, 0.25, ((0, 8),)),
        "expert_in": noise(arg_keys[6], (EXPERTS, D, FF), D ** -0.5, 0.25, ((0, 8),)),
        "expert_out": noise(arg_keys[7], (EXPERTS, FF, D), (max(FF // 256, 1)) ** -0.5, 2.0, ((0, 8),)),
        "routes": different_ones(arg_keys[8], TOKENS, EXPERTS, 2, 2048),
        "priority": jax.vmap(lambda own: jax.random.permutation(own, TOK_DEV))(jax.random.split(arg_keys[9], (TOKENS // TOK_DEV))).reshape((TOKENS // TOK_DEV, TOK_DEV)).astype(jnp.int32),
        "doc_lengths": ragged_sizes(arg_keys[10], DOCS, TOKENS, DOC_MOST, 2).astype(jnp.int32),
        "d_out": noise(arg_keys[11], (TOKENS, D), 1.0, 6.0, ((0, 32),), jnp.float32),
    }


@jax.custom_vjp
def low(v):
    return lax.optimization_barrier(v.astype(jnp.bfloat16)).astype(jnp.float32)

@jax.custom_vjp
def low_back(v):
    return v

def low_keep(v):
    return (low(v), None)

def low_pass(kept, grad):
    return (grad,)

def back_keep(v):
    return (v, None)

def back_low(kept, grad):
    return (low(grad),)
low.defvjp(low_keep, low_pass)
low_back.defvjp(back_keep, back_low)
PRECISE = lax.Precision.HIGHEST
MASKED = -1e+30
EPSILON = 1e-06

def layer_norm(values, gain):
    average = lax.optimization_barrier(jnp.mean(values, axis=-1, keepdims=True))
    centred = values - average
    spread = lax.optimization_barrier(jnp.mean(centred * centred, axis=-1, keepdims=True))
    return centred * lax.rsqrt(spread + EPSILON) * gain

def gelu_exact(values):
    return jax.nn.gelu(values, approximate=False)

def router(row_block, weight):
    return jax.nn.softmax(jnp.dot(row_block, weight, precision=PRECISE), axis=-1)

def doc_index(positions, doc_lengths):
    starts = (jnp.cumsum(doc_lengths) - doc_lengths).astype(jnp.int32)
    at_most = (starts[None, :] <= positions[:, None]).astype(jnp.int32)
    return (lax.optimization_barrier(jnp.sum(at_most, axis=1)) - 1).astype(jnp.int32)

def slot_table(route_rows, ranking, capacity):
    token_count = route_rows.shape[0]
    expert = jnp.transpose(route_rows).reshape(-1).astype(jnp.int32)
    pair_order = (jnp.arange(2, dtype=jnp.int32)[:, None] * token_count + ranking[None, :]).reshape(-1).astype(jnp.int32)
    before = (expert[:, None] == expert[None, :]) & (pair_order[None, :] < pair_order[:, None])
    position = lax.optimization_barrier(jnp.sum(before.astype(jnp.int32), axis=1)).astype(jnp.int32)
    slot_ids = jnp.where(position < capacity, expert * capacity + position, -1)
    return slot_ids.astype(jnp.int32).reshape(2, token_count)

def attention(queries, keys, values, doc_ids):
    blocks = TOKENS // KEY_BLOCK
    head_ids = jnp.repeat(jnp.arange(H, dtype=jnp.int32), blocks)
    query_items = queries.reshape(H * blocks, KEY_BLOCK, HS)
    doc_items = jnp.tile(doc_ids.reshape(blocks, KEY_BLOCK), (H, 1))
    scale_factor = HS ** (-0.5)

    def one_block(block_item):
        query_block, query_docs, head_id = block_item
        key_rows = lax.dynamic_index_in_dim(keys, head_id, 0, keepdims=False)
        value_rows = lax.dynamic_index_in_dim(values, head_id, 0, keepdims=False)
        scores = low_back(jnp.dot(query_block, key_rows.T, precision=PRECISE) * scale_factor)
        scores = jnp.where(query_docs[:, None] == doc_ids[None, :], scores, MASKED)
        log_total = jax.nn.logsumexp(scores, axis=1, keepdims=True)
        weights = jnp.exp(scores - log_total)
        return jnp.dot(low(weights), value_rows, precision=PRECISE)
    mixed_rows = lax.map(jax.checkpoint(one_block), (query_items, doc_items, head_ids))
    return mixed_rows.reshape(H, TOKENS, HS)

def forward(inputs, ln1_gain, w_qkv, w_out, ln2_gain, w_router, expert_in, expert_out, routes, priority, doc_lengths):
    normed = low(layer_norm(inputs, ln1_gain))
    qkv_rows = low_back(low(jnp.dot(normed, w_qkv, precision=PRECISE)))

    def heads_first(column_block):
        return column_block.reshape(TOKENS, H, HS).transpose(1, 0, 2)
    queries = heads_first(qkv_rows[:, :D])
    keys = heads_first(qkv_rows[:, D:2 * D])
    values = heads_first(qkv_rows[:, 2 * D:])
    doc_ids = doc_index(jnp.arange(TOKENS, dtype=jnp.int32), doc_lengths)
    mixed_heads = attention(queries, keys, values, doc_ids)
    mixed_rows = low_back(low(mixed_heads.transpose(1, 0, 2).reshape(TOKENS, D)))
    attended = low_back(jnp.dot(mixed_rows, w_out, precision=PRECISE))
    hidden_one = inputs + attended
    routed = low(layer_norm(hidden_one, ln2_gain))
    router_probs = router(routed, w_router)
    groups = TOKENS // TOK_DEV
    group_routes = routes.reshape(groups, TOK_DEV, 2)
    slot_ids = jax.vmap(lambda route_rows, ranking: slot_table(route_rows, ranking, CAP))(group_routes, priority)
    select = (slot_ids[..., None] == jnp.arange(EXPERTS * CAP, dtype=jnp.int32)).astype(jnp.float32)
    token_groups = routed.reshape(groups, TOK_DEV, D)
    slot_rows = low_back(jnp.einsum('gkts,gtd->gsd', select, token_groups, precision=PRECISE))
    expert_rows = slot_rows.reshape(groups, EXPERTS, CAP, D).transpose(1, 0, 2, 3).reshape(EXPERTS, groups * CAP, D)

    def one_expert(expert_item):
        rows_in, weight_in, weight_out = expert_item
        pre_act = low_back(jnp.dot(rows_in, weight_in, precision=PRECISE))
        hidden_act = low(gelu_exact(pre_act))
        return low_back(low(jnp.dot(hidden_act, weight_out, precision=PRECISE)))
    expert_outs = lax.map(jax.checkpoint(one_expert), (expert_rows, expert_in, expert_out))
    slot_outs = expert_outs.reshape(EXPERTS, groups, CAP, D).transpose(1, 0, 2, 3).reshape(groups, EXPERTS * CAP, D)
    pair_outs = jnp.einsum('gkts,gsd->gktd', select, slot_outs, precision=PRECISE)
    route_hot = (group_routes[..., None] == jnp.arange(EXPERTS, dtype=jnp.int32)).astype(jnp.float32)
    gate_vals = lax.optimization_barrier(jnp.sum(router_probs.reshape(groups, TOK_DEV, 1, EXPERTS) * route_hot, axis=-1))
    mixture = lax.optimization_barrier(jnp.sum(jnp.transpose(gate_vals, (0, 2, 1))[..., None] * pair_outs, axis=1))
    return hidden_one + mixture.reshape(TOKENS, D)

def reference(inputs, ln1_gain, w_qkv, w_out, ln2_gain, w_router, expert_in, expert_out, routes, priority, doc_lengths, d_out):
    floats = [array_in.astype(jnp.float32) for array_in in (inputs, ln1_gain, w_qkv, w_out, ln2_gain, w_router, expert_in, expert_out)]

    def float_part(*arrays):
        return forward(*arrays, routes, priority, doc_lengths)
    result, pull_back = jax.vjp(float_part, *floats)
    grads = pull_back(d_out.astype(jnp.float32))
    return (result.astype(jnp.bfloat16), grads[0], grads[1], grads[2], grads[3], grads[4], grads[5], grads[6], grads[7])
```

```python
import functools
import math

import jax
import jax.numpy as jnp
from jax import lax
from jax.experimental import pallas as pl
from jax.experimental.pallas import tpu as pltpu
from jax.sharding import PartitionSpec as P

HS = 64
KEY_BLOCK = 2048


PRECISE = lax.Precision.HIGHEST
MASKED = -1e30
EPSILON = 1e-06


def layer_norm(values, gain):
    average = jnp.mean(values, axis=-1, keepdims=True)
    centred = values - average
    spread = jnp.mean(centred * centred, axis=-1, keepdims=True)
    return centred * lax.rsqrt(spread + EPSILON) * gain


def gelu_exact(values):
    return jax.nn.gelu(values, approximate=False)


def router(row_block, weight):
    return jax.nn.softmax(jnp.dot(row_block, weight, precision=PRECISE), axis=-1)


def doc_index(positions, doc_lengths):
    places = jnp.arange(doc_lengths.shape[0], dtype=jnp.int32)
    starts = jnp.sum(jnp.where(places[None, :] < places[:, None], doc_lengths[None, :], 0), axis=1)
    at_most = (starts[None, :] <= positions[:, None]).astype(jnp.int32)
    return jnp.sum(at_most, axis=1) - 1


def slot_table(route_rows, ranking, capacity):
    token_count = route_rows.shape[0]
    expert = jnp.transpose(route_rows).reshape(-1)
    pair_order = (jnp.arange(2, dtype=jnp.int32)[:, None] * token_count + ranking[None, :]).reshape(
        -1
    )
    before = (expert[:, None] == expert[None, :]) & (pair_order[None, :] < pair_order[:, None])
    position = jnp.sum(before.astype(jnp.int32), axis=1)
    slot_ids = jnp.where(position < capacity, expert * capacity + position, -1)
    return slot_ids.reshape(2, token_count)


def keep_state(current):
    return current


def local(
    inputs,
    ln1_gain,
    w_qkv,
    w_out,
    ln2_gain,
    w_router,
    expert_in,
    expert_out,
    routes,
    priority,
    doc_lengths,
    d_out,
):
    blk_size = lax.axis_size("blk")
    tok_rows = inputs.shape[0]
    model_width = inputs.shape[1]
    capacity = 2 * tok_rows // blk_size
    slot_total = blk_size * capacity
    gain_one, qkv_weight, out_weight, gain_two, router_weight = (
        lax.all_gather(ln1_gain, "blk", axis=0, tiled=True),
        lax.all_gather(w_qkv, "blk", axis=0, tiled=True),
        lax.all_gather(w_out, "blk", axis=0, tiled=True),
        lax.all_gather(ln2_gain, "blk", axis=0, tiled=True),
        lax.all_gather(w_router, "blk", axis=0, tiled=True),
    )
    input_rows = inputs.astype(jnp.float32)
    normed_one, norm_one_pull = jax.vjp(layer_norm, input_rows, gain_one.astype(jnp.float32))
    normed_low = normed_one.astype(jnp.bfloat16)
    qkv_rows = jnp.dot(normed_low, qkv_weight, preferred_element_type=jnp.float32).astype(
        jnp.bfloat16
    )
    query_heads, key_heads, value_heads = (
        lax.all_to_all(qkv_rows[:, :model_width], "head", split_axis=1, concat_axis=0, tiled=True),
        lax.all_to_all(
            qkv_rows[:, model_width : 2 * model_width],
            "head",
            split_axis=1,
            concat_axis=0,
            tiled=True,
        ),
        lax.all_to_all(
            qkv_rows[:, 2 * model_width :], "head", split_axis=1, concat_axis=0, tiled=True
        ),
    )
    span_rows = query_heads.shape[0]
    head_count = query_heads.shape[1] // HS
    key_all, value_all = (
        lax.all_gather(key_heads, "blk", axis=0, tiled=True),
        lax.all_gather(value_heads, "blk", axis=0, tiled=True),
    )
    total_rows = key_all.shape[0]
    block_count = total_rows // KEY_BLOCK
    scale_factor = HS ** (-0.5)
    query_pos = lax.axis_index("blk") * span_rows + jnp.arange(span_rows, dtype=jnp.int32)
    query_docs = doc_index(query_pos, doc_lengths)
    queries = query_heads.reshape(span_rows, head_count, HS)

    def block_parts(block_index, key_source, value_source):
        first_key = block_index * KEY_BLOCK
        key_rows = lax.dynamic_slice_in_dim(key_source, first_key, KEY_BLOCK, 0).reshape(
            KEY_BLOCK, head_count, HS
        )
        value_rows = lax.dynamic_slice_in_dim(value_source, first_key, KEY_BLOCK, 0).reshape(
            KEY_BLOCK, head_count, HS
        )
        key_docs = doc_index(first_key + jnp.arange(KEY_BLOCK, dtype=jnp.int32), doc_lengths)
        is_live = (key_docs[0] <= query_docs[-1]) & (key_docs[-1] >= query_docs[0])
        same_doc = query_docs[:, None] == key_docs[None, :]
        return (first_key, key_rows, value_rows, same_doc, is_live)

    def block_scores(key_rows, same_doc):
        raw_scores = (
            jnp.einsum("qhd,khd->hqk", queries, key_rows, preferred_element_type=jnp.float32)
            * scale_factor
        )
        return jnp.where(same_doc[None], raw_scores, MASKED)

    def stat_step(block_index, loop_state):
        first_key, key_rows, value_rows, same_doc, is_live = block_parts(
            block_index, key_all, value_all
        )

        def stat_update(current):
            running_max, running_sum = current
            scores = block_scores(key_rows, same_doc)
            new_max = jnp.maximum(running_max, jnp.max(scores, axis=2))
            exp_terms = jnp.where(same_doc[None], jnp.exp(scores - new_max[:, :, None]), 0.0)
            return (
                new_max,
                running_sum * jnp.exp(running_max - new_max) + jnp.sum(exp_terms, axis=2),
            )

        return lax.cond(is_live, stat_update, keep_state, loop_state)

    start_state = (
        jnp.full((head_count, span_rows), MASKED, jnp.float32),
        jnp.zeros((head_count, span_rows), jnp.float32),
    )
    running_max, running_sum = lax.fori_loop(0, block_count, stat_step, start_state)
    log_total = running_max + jnp.log(running_sum)

    def out_step(block_index, loop_state):
        first_key, key_rows, value_rows, same_doc, is_live = block_parts(
            block_index, key_all, value_all
        )

        def out_update(current):
            scores = block_scores(key_rows, same_doc)
            weights = jnp.where(
                same_doc[None], jnp.exp(scores - log_total[:, :, None]), 0.0
            ).astype(jnp.bfloat16)
            return current + jnp.einsum(
                "hqk,khd->qhd", weights, value_rows, preferred_element_type=jnp.float32
            )

        return lax.cond(is_live, out_update, keep_state, loop_state)

    mixed_full = lax.fori_loop(
        0, block_count, out_step, jnp.zeros((span_rows, head_count, HS), jnp.float32)
    )
    mixed_low = mixed_full.reshape(span_rows, head_count * HS).astype(jnp.bfloat16)
    mixed_tokens = lax.all_to_all(mixed_low, "head", split_axis=0, concat_axis=1, tiled=True)
    attended = jnp.dot(mixed_tokens, out_weight, preferred_element_type=jnp.float32)
    hidden_one = input_rows + attended
    normed_two, norm_two_pull = jax.vjp(layer_norm, hidden_one, gain_two.astype(jnp.float32))
    routed_low = normed_two.astype(jnp.bfloat16)
    router_probs, router_pull = jax.vjp(
        router, routed_low.astype(jnp.float32), router_weight.astype(jnp.float32)
    )
    slot_ids = slot_table(routes, priority[0], capacity)
    select = (
        slot_ids[:, :, None] == jnp.arange(slot_total, dtype=jnp.int32)[None, None, :]
    ).astype(jnp.bfloat16)
    send_rows = jnp.einsum(
        "kts,td->sd", select, routed_low, preferred_element_type=jnp.float32
    ).astype(jnp.bfloat16)
    expert_rows = lax.all_to_all(
        send_rows.reshape(blk_size, capacity, model_width),
        "blk",
        split_axis=0,
        concat_axis=0,
        tiled=True,
    ).reshape(slot_total, model_width)
    weight_in = expert_in[0]
    weight_out = expert_out[0]
    pre_act = jnp.dot(expert_rows, weight_in, preferred_element_type=jnp.float32)
    hidden_act, gelu_pull = jax.vjp(gelu_exact, pre_act)
    hidden_low = hidden_act.astype(jnp.bfloat16)
    expert_result = jnp.dot(hidden_low, weight_out, preferred_element_type=jnp.float32).astype(
        jnp.bfloat16
    )
    slot_result = lax.all_to_all(
        expert_result.reshape(blk_size, capacity, model_width),
        "blk",
        split_axis=0,
        concat_axis=0,
        tiled=True,
    ).reshape(slot_total, model_width)
    pair_result = jnp.einsum("kts,sd->ktd", select, slot_result, preferred_element_type=jnp.float32)
    route_hot = (routes[:, :, None] == jnp.arange(blk_size, dtype=jnp.int32)[None, None, :]).astype(
        jnp.float32
    )
    gate_vals = jnp.sum(router_probs[:, None, :] * route_hot, axis=2)
    mixture = gate_vals[:, 0, None] * pair_result[0] + gate_vals[:, 1, None] * pair_result[1]
    output = (hidden_one + mixture).astype(jnp.bfloat16)
    d_gates = jnp.transpose(jnp.sum(d_out[None] * pair_result, axis=2))
    d_probs = jnp.sum(d_gates[:, :, None] * route_hot, axis=1)
    pair_grads = (jnp.transpose(gate_vals)[:, :, None] * d_out[None]).astype(jnp.bfloat16)
    slot_grads = jnp.einsum(
        "kts,ktd->sd", select, pair_grads, preferred_element_type=jnp.float32
    ).astype(jnp.bfloat16)
    result_grads = lax.all_to_all(
        slot_grads.reshape(blk_size, capacity, model_width),
        "blk",
        split_axis=0,
        concat_axis=0,
        tiled=True,
    ).reshape(slot_total, model_width)
    d_hidden_act = jnp.dot(result_grads, weight_out.T, preferred_element_type=jnp.float32)
    d_weight_out = jnp.dot(hidden_low.T, result_grads, preferred_element_type=jnp.float32)
    d_preact = gelu_pull(d_hidden_act)[0].astype(jnp.bfloat16)
    d_weight_in = jnp.dot(expert_rows.T, d_preact, preferred_element_type=jnp.float32)
    row_grads = jnp.dot(d_preact, weight_in.T, preferred_element_type=jnp.float32).astype(
        jnp.bfloat16
    )
    slot_back = lax.all_to_all(
        row_grads.reshape(blk_size, capacity, model_width),
        "blk",
        split_axis=0,
        concat_axis=0,
        tiled=True,
    ).reshape(slot_total, model_width)
    d_routed = jnp.einsum("kts,sd->td", select, slot_back, preferred_element_type=jnp.float32)
    d_routed_router, d_router = router_pull(d_probs)
    d_hidden_norm, d_gain_two = norm_two_pull(d_routed + d_routed_router)
    d_hidden_one = d_out + d_hidden_norm
    attn_grads = d_hidden_one.astype(jnp.bfloat16)
    d_out_weight = jnp.dot(mixed_tokens.T, attn_grads, preferred_element_type=jnp.float32)
    mixed_grads = jnp.dot(attn_grads, out_weight.T, preferred_element_type=jnp.float32).astype(
        jnp.bfloat16
    )
    head_grads = lax.all_to_all(mixed_grads, "head", split_axis=1, concat_axis=0, tiled=True)
    out_grads = head_grads.reshape(span_rows, head_count, HS)
    row_delta = jnp.transpose(jnp.sum(out_grads.astype(jnp.float32) * mixed_full, axis=2))
    key_back, value_back = (
        lax.all_gather(key_heads, "blk", axis=0, tiled=True),
        lax.all_gather(value_heads, "blk", axis=0, tiled=True),
    )

    def grad_step(block_index, loop_state):
        first_key, key_rows, value_rows, same_doc, is_live = block_parts(
            block_index, key_back, value_back
        )

        def grad_update(current):
            query_grad, key_grad, value_grad = current
            scores = block_scores(key_rows, same_doc)
            weights = jnp.where(same_doc[None], jnp.exp(scores - log_total[:, :, None]), 0.0)
            value_part = jnp.einsum(
                "hqk,qhd->khd",
                weights.astype(jnp.bfloat16),
                out_grads,
                preferred_element_type=jnp.float32,
            )
            weight_grads = jnp.einsum(
                "qhd,khd->hqk", out_grads, value_rows, preferred_element_type=jnp.float32
            )
            score_grads = (weights * (weight_grads - row_delta[:, :, None])).astype(jnp.bfloat16)
            query_grad = (
                query_grad
                + jnp.einsum(
                    "hqk,khd->qhd", score_grads, key_rows, preferred_element_type=jnp.float32
                )
                * scale_factor
            )
            key_part = (
                jnp.einsum("hqk,qhd->khd", score_grads, queries, preferred_element_type=jnp.float32)
                * scale_factor
            )
            key_grad = lax.dynamic_update_slice_in_dim(
                key_grad, key_part.reshape(KEY_BLOCK, head_count * HS), first_key, 0
            )
            value_grad = lax.dynamic_update_slice_in_dim(
                value_grad, value_part.reshape(KEY_BLOCK, head_count * HS), first_key, 0
            )
            return (query_grad, key_grad, value_grad)

        return lax.cond(is_live, grad_update, keep_state, loop_state)

    start_grads = (
        jnp.zeros((span_rows, head_count, HS), jnp.float32),
        jnp.zeros((total_rows, head_count * HS), jnp.float32),
        jnp.zeros((total_rows, head_count * HS), jnp.float32),
    )
    query_grad, key_grad, value_grad = lax.fori_loop(0, block_count, grad_step, start_grads)
    key_own, value_own = (
        lax.psum_scatter(
            key_grad.astype(jnp.bfloat16), "blk", scatter_dimension=0, tiled=True
        ).astype(jnp.float32),
        lax.psum_scatter(
            value_grad.astype(jnp.bfloat16), "blk", scatter_dimension=0, tiled=True
        ).astype(jnp.float32),
    )
    query_tokens_grad, key_tokens_grad, value_tokens_grad = (
        lax.all_to_all(
            query_grad.reshape(span_rows, head_count * HS).astype(jnp.bfloat16),
            "head",
            split_axis=0,
            concat_axis=1,
            tiled=True,
        ),
        lax.all_to_all(
            key_own.astype(jnp.bfloat16), "head", split_axis=0, concat_axis=1, tiled=True
        ),
        lax.all_to_all(
            value_own.astype(jnp.bfloat16), "head", split_axis=0, concat_axis=1, tiled=True
        ),
    )
    qkv_grads = jnp.concatenate([query_tokens_grad, key_tokens_grad, value_tokens_grad], axis=1)
    d_qkv_weight = jnp.dot(normed_low.T, qkv_grads, preferred_element_type=jnp.float32)
    normed_grads = jnp.dot(qkv_grads, qkv_weight.T, preferred_element_type=jnp.float32)
    d_inputs_norm, d_gain_one = norm_one_pull(normed_grads)
    d_inputs = d_hidden_one + d_inputs_norm
    gain_one_sum, qkv_sum, out_sum, gain_two_sum, router_sum = (
        lax.psum_scatter(
            d_gain_one.astype(jnp.bfloat16), "blk", scatter_dimension=0, tiled=True
        ).astype(jnp.float32),
        lax.psum_scatter(
            d_qkv_weight.astype(jnp.bfloat16), "blk", scatter_dimension=0, tiled=True
        ).astype(jnp.float32),
        lax.psum_scatter(
            d_out_weight.astype(jnp.bfloat16), "blk", scatter_dimension=0, tiled=True
        ).astype(jnp.float32),
        lax.psum_scatter(
            d_gain_two.astype(jnp.bfloat16), "blk", scatter_dimension=0, tiled=True
        ).astype(jnp.float32),
        lax.psum_scatter(
            d_router.astype(jnp.bfloat16), "blk", scatter_dimension=0, tiled=True
        ).astype(jnp.float32),
    )
    gain_one_all, qkv_all, out_all, gain_two_all, router_all, expert_in_all, expert_out_all = (
        lax.psum(gain_one_sum.astype(jnp.bfloat16), "head").astype(jnp.float32),
        lax.psum(qkv_sum.astype(jnp.bfloat16), "head").astype(jnp.float32),
        lax.psum(out_sum.astype(jnp.bfloat16), "head").astype(jnp.float32),
        lax.psum(gain_two_sum.astype(jnp.bfloat16), "head").astype(jnp.float32),
        lax.psum(router_sum.astype(jnp.bfloat16), "head").astype(jnp.float32),
        lax.psum(d_weight_in[None].astype(jnp.bfloat16), "head").astype(jnp.float32),
        lax.psum(d_weight_out[None].astype(jnp.bfloat16), "head").astype(jnp.float32),
    )
    return (
        output,
        d_inputs,
        gain_one_all,
        qkv_all,
        out_all,
        gain_two_all,
        router_all,
        expert_in_all,
        expert_out_all,
    )


MESH = pl.DeviceIdType.MESH
LANES = 128
HALF = LANES // 2
VMEM_LIMIT = 50 * 2**20
F32 = jnp.float32
BF16 = jnp.bfloat16


def dot(left, right, dims=(1, 0)):
    return lax.dot_general(
        left, right, (((dims[0],), (dims[1],)), ((), ())), preferred_element_type=F32
    )


def remote(src, dst, send_sem, recv_sem, head, blk):
    return pltpu.make_async_remote_copy(
        src_ref=src,
        dst_ref=dst,
        send_sem=send_sem,
        recv_sem=recv_sem,
        device_id={"head": head, "blk": blk},
        device_id_type=MESH,
    )


def arrived(ref, sem):
    pltpu.make_async_copy(ref, ref, sem).wait()


def greet(peers):
    barrier = pltpu.get_barrier_semaphore()
    for head, blk in peers:
        pl.semaphore_signal(
            barrier, inc=1, device_id={"head": head, "blk": blk}, device_id_type=MESH
        )
    pl.semaphore_wait(barrier, len(peers))


def lane_ids(shape):
    return lax.broadcasted_iota(jnp.int32, shape, len(shape) - 1)


def centre(values):
    average = jnp.mean(values, axis=-1, keepdims=True)
    centred = values - average
    spread = jnp.mean(centred * centred, axis=-1, keepdims=True)
    scale = lax.rsqrt(spread + EPSILON)
    return centred * scale, scale


def centre_back(grad, xhat, scale):
    middle = jnp.mean(grad, axis=-1, keepdims=True)
    along = jnp.mean(grad * xhat, axis=-1, keepdims=True)
    return (grad - middle - xhat * along) * scale


def split_high_low(column, lanes):
    high = column.astype(BF16)
    low = (column - high.astype(F32)).astype(BF16)
    return jnp.where(lanes < HALF, high.astype(F32), low.astype(F32)).astype(BF16)


def join_high_low(matrix, start):
    return matrix[:, start : start + 1].astype(F32) + matrix[
        :, start + HALF : start + HALF + 1
    ].astype(F32)


def place():
    head, blk = lax.axis_index("head"), lax.axis_index("blk")
    return head, blk, blk // 2, lax.rem(blk, 2)


def around(index, step, size):
    return lax.rem(index + step, size)


def qkv_kernel(
    heads, blks,
    x_ref, w_ref, g1_ref, wo_ref, wr_ref, g2_ref,
    q_out, kv_out, xa_out, wa_out, wo_out,
    gain_tile, xall, wall, wo_own, wo_all, kvall, kv_other, qall,
    x_send, x_recv, w_send, w_recv, o_send, o_recv, p_send, p_recv,
    k_send, k_recv, q_recv, out_sem,
):
    head, blk, z, y = place()
    planes = blks // 2
    model = x_ref.shape[1]
    rows = w_ref.shape[0]
    part = rows // heads
    greet(
        [(around(head, k, heads), blk) for k in range(1, heads)]
        + [(head, around(blk, k, blks)) for k in range(1, blks)]
    )
    lanes = lane_ids((rows, LANES))
    gain_tile[...] = jnp.zeros_like(gain_tile)
    gain_tile[0:1, 0:rows] = g1_ref[...].astype(F32)
    gain = jnp.transpose(jnp.broadcast_to(gain_tile[0:1, :], (LANES, LANES)))[:rows]

    def columns(which):
        start = pl.multiple_of(which * model + head * LANES, LANES)
        return w_ref[:, pl.ds(start, LANES)].astype(F32) * gain

    key_cols = columns(1)
    value_cols = pltpu.roll(columns(2), HALF, 1)
    wall[blk, :, 0:LANES] = jnp.where(lanes < HALF, key_cols, value_cols).astype(BF16)
    wall[blk, :, LANES : 2 * LANES] = jnp.where(lanes < HALF, value_cols, key_cols).astype(BF16)
    wall[blk, :, 2 * LANES : 3 * LANES] = (columns(0) * HS ** (-0.5)).astype(BF16)
    w_copies = [
        remote(wall.at[blk], wall.at[blk], w_send.at[k], w_recv.at[k], head, around(blk, k, blks))
        for k in range(1, blks)
    ]
    for copy in w_copies:
        copy.start()
    xhat, _ = centre(x_ref[...].astype(F32))
    xall[head] = xhat.astype(BF16)
    x_copies = [
        remote(xall.at[head], xall.at[head], x_send.at[k], x_recv.at[k], around(head, k, heads), blk)
        for k in range(1, heads)
    ]
    for copy in x_copies:
        copy.start()
    wo_own[...] = jnp.zeros_like(wo_own)
    wo_own[:, 0:model] = wo_ref[...]
    wo_own[:, model : model + wr_ref.shape[1]] = wr_ref[...]
    wo_own[:, model + wr_ref.shape[1] : model + wr_ref.shape[1] + 1] = g2_ref[...]
    wo_all[blk, head] = wo_own[pl.ds(pl.multiple_of(head * part, part), part), :]
    o_copies = [
        remote(
            wo_all.at[blk, head], wo_all.at[blk, head],
            o_send.at[k], o_recv.at[k], head, around(blk, k, blks),
        )
        for k in range(1, blks)
    ]
    for copy in o_copies:
        copy.start()
    for copy in x_copies:
        copy.wait()
    for copy in w_copies:
        copy.wait()
    weight = wall[...].reshape(model, 3 * LANES)
    tokens = x_ref.shape[0]
    even = y == 0
    for piece in range(heads):
        made = dot(xall[piece], weight).astype(BF16)
        first, second = made[:, 0:LANES], made[:, LANES : 2 * LANES]
        span = slice(piece * tokens, (piece + 1) * tokens)
        kvall[blk, span, :] = jnp.where(even, first, second)
        kv_other[span, :] = jnp.where(even, second, first)
        qall[y, span, :] = made[:, 2 * LANES : 3 * LANES]
    above, below = z < planes - 1, z > 0
    own = kvall.at[blk]

    def outward(slot, step, across):
        target = 2 * (z + step) + around(y, across, 2)
        return remote(kv_other if across else own, own, k_send.at[slot], k_recv.at[blk], head, target)

    def onward(slot, step, side):
        from_span = 2 * (z - step) + side
        ref = kvall.at[from_span]
        return remote(ref, ref, k_send.at[slot], k_recv.at[from_span], head, 2 * (z + step) + y)

    sides = ((1, above, below, 0), (-1, below, above, 2))
    for step, there, _, slot in sides:

        @pl.when(there)
        def _():
            outward(slot, step, 0).start()
            outward(slot + 1, step, 1).start()

    to_pair = outward(4, 0, 1)
    to_pair.start()
    q_pair = remote(qall.at[y], qall.at[y], k_send.at[5], q_recv, head, 2 * z + around(y, 1, 2))
    q_pair.start()
    for copy in o_copies:
        copy.wait()
    p_copies = [
        remote(
            wo_all.at[:, head], wo_all.at[:, head],
            p_send.at[k], p_recv.at[k], around(head, k, heads), blk,
        )
        for k in range(1, heads)
    ]
    for copy in p_copies:
        copy.start()
    for step, there, back, slot in sides:

        @pl.when(back)
        def _():
            for side in range(2):
                span = 2 * (z - step) + side
                arrived(kvall.at[span], k_recv.at[span])

        @pl.when(jnp.logical_and(there, back))
        def _():
            for side in range(2):
                onward(6 + slot + side, step, side).start()

    far = jnp.zeros(kv_other.shape, BF16)
    for other in range(planes):
        for side in range(2):
            span = 2 * other + side

            @pl.when(jnp.logical_or(z - other > 2, other - z > 2))
            def _():
                kvall[span] = far

            @pl.when(jnp.logical_or(z - other == 2, other - z == 2))
            def _():
                arrived(kvall.at[span], k_recv.at[span])

    pair = 2 * z + around(y, 1, 2)
    arrived(kvall.at[pair], k_recv.at[pair])
    q_pair.wait()
    for copy in p_copies:
        copy.wait()
    outs = [
        pltpu.make_async_copy(src, dst, out_sem.at[i])
        for i, (src, dst) in enumerate(
            ((qall, q_out), (kvall, kv_out), (xall, xa_out), (wall, wa_out), (wo_all, wo_out))
        )
    ]
    for copy in outs:
        copy.start()
    to_pair.wait_send()
    for step, there, back, slot in sides:

        @pl.when(there)
        def _():
            outward(slot, step, 0).wait_send()
            outward(slot + 1, step, 1).wait_send()

        @pl.when(jnp.logical_and(there, back))
        def _():
            for side in range(2):
                onward(6 + slot + side, step, side).wait_send()

    for copy in outs:
        copy.wait()


def vmem_specs(count):
    return [pl.BlockSpec(memory_space=pltpu.VMEM)] * count


def any_specs(count):
    return [pl.BlockSpec(memory_space=pl.ANY)] * count


def dma(*shape):
    return pltpu.SemaphoreType.DMA(shape)


def call_qkv(x, w_qkv, g1, w_out, w_router, g2, heads, blks):
    tokens, model = x.shape
    rows = w_qkv.shape[0]
    span = tokens * heads
    wide = model + LANES
    part = rows // heads
    return pl.pallas_call(
        functools.partial(qkv_kernel, heads, blks),
        out_shape=(
            jax.ShapeDtypeStruct((2, span, LANES), BF16),
            jax.ShapeDtypeStruct((blks, span, LANES), BF16),
            jax.ShapeDtypeStruct((heads, tokens, model), BF16),
            jax.ShapeDtypeStruct((blks, rows, 3 * LANES), BF16),
            jax.ShapeDtypeStruct((blks, heads, part, wide), BF16),
        ),
        in_specs=vmem_specs(6),
        out_specs=tuple(any_specs(5)),
        scratch_shapes=[
            pltpu.VMEM((8, LANES), F32),
            pltpu.VMEM((heads, tokens, model), BF16),
            pltpu.VMEM((blks, rows, 3 * LANES), BF16),
            pltpu.VMEM((rows, wide), BF16),
            pltpu.VMEM((blks, heads, part, wide), BF16),
            pltpu.VMEM((blks, span, LANES), BF16),
            pltpu.VMEM((span, LANES), BF16),
            pltpu.VMEM((2, span, LANES), BF16),
            dma(heads), dma(heads), dma(blks), dma(blks), dma(blks), dma(blks), dma(heads), dma(heads),
            dma(10), dma(blks), pltpu.SemaphoreType.DMA, dma(5),
        ],
        compiler_params=pltpu.CompilerParams(
            collective_id=1, has_side_effects=True, vmem_limit_bytes=VMEM_LIMIT
        ),
        name="qkv",
    )(x, w_qkv, g1.reshape(1, rows), w_out, w_router, g2.reshape(rows, 1))


QUERY_TILE = 256
KEY_TILE = 512


def tile_docs(doc_ref, first, size):
    token = first + lane_ids((1, size))
    last = first + size - 1
    start = jnp.int32(0)
    low_row, high_row = jnp.zeros((1, size), jnp.int32), jnp.zeros((1, size), jnp.int32)
    low = low_last = high = jnp.int32(0)
    for index in range(doc_ref.shape[0]):
        end = start + doc_ref[index]
        low_row = jnp.where(token >= start, start, low_row)
        high_row = jnp.where(token >= start, end, high_row)
        low = jnp.where(first >= start, start, low)
        low_last = jnp.where(last >= start, start, low_last)
        high = jnp.where(last >= start, end, high)
        start = end
    return low_row, high_row, low, high, low == low_last


def key_columns(doc_ref, kv_ref, kvt, z, span):
    _, _, low, _, _ = tile_docs(doc_ref, z * span, LANES)
    _, _, _, high, _ = tile_docs(doc_ref, (z + 1) * span - LANES, LANES)
    for block in range(kv_ref.shape[0]):
        size = kv_ref.shape[1]

        @pl.when(jnp.logical_and(block * size < high, (block + 1) * size > low))
        def _():
            kvt[:, block * size : (block + 1) * size] = jnp.transpose(kv_ref[block])


def forward_kernel(doc_ref, q_ref, kv_ref, o_out, ob_out, lse_out, kvt):
    _, _, z, y = place()
    total = q_ref.shape[0] * q_ref.shape[1]
    key_columns(doc_ref, kv_ref, kvt, z, total)
    lanes = lane_ids((QUERY_TILE, LANES))
    tiles_per_span = q_ref.shape[1] // QUERY_TILE
    key_lanes = (lanes < HALF) == (y == 0)
    for tile in range(total // QUERY_TILE):
        inner = tile % tiles_per_span * QUERY_TILE
        query = q_ref[tile // tiles_per_span, inner : inner + QUERY_TILE, :]
        query = jnp.where(key_lanes, query, jnp.zeros_like(query))
        low_row, high_row, low, high, single = tile_docs(
            doc_ref, z * total + tile * QUERY_TILE, QUERY_TILE
        )

        def step(block, carry, query=query, low_row=low_row, high_row=high_row):
            biggest, weight, mixed = carry
            first = pl.multiple_of(block * KEY_TILE, KEY_TILE)
            scores = dot(kv_ref[block], query, (1, 1))
            key = first + lax.broadcasted_iota(jnp.int32, scores.shape, 0)
            inside = jnp.logical_and(key >= low_row, key < high_row)
            scores = jnp.where(inside, scores, MASKED)
            bigger = jnp.maximum(biggest, jnp.max(scores, axis=0, keepdims=True))
            fade = jnp.exp(biggest - bigger)
            terms = jnp.where(inside, jnp.exp(scores - bigger), 0.0)
            weight = weight * fade + jnp.sum(terms, axis=0, keepdims=True)
            mixed = mixed * fade + dot(kvt[:, pl.ds(first, KEY_TILE)], terms.astype(BF16))
            return bigger, weight, mixed

        biggest, weight, mixed = lax.fori_loop(
            low // KEY_TILE,
            (high + KEY_TILE - 1) // KEY_TILE,
            step,
            (
                jnp.full((1, QUERY_TILE), MASKED, F32),
                jnp.zeros((1, QUERY_TILE), F32),
                jnp.zeros((LANES, QUERY_TILE), F32),
            ),
        )
        result = jnp.transpose(mixed / weight)
        o_out[tile] = result
        ob_out[tile] = result.astype(BF16)
        lse_out[tile] = jnp.broadcast_to(biggest + jnp.log(weight), (8, QUERY_TILE))


def call_forward(doc_lengths, q, kv):
    blks, span, _ = kv.shape
    tiles = 2 * span // QUERY_TILE
    return pl.pallas_call(
        forward_kernel,
        out_shape=(
            jax.ShapeDtypeStruct((tiles, QUERY_TILE, LANES), F32),
            jax.ShapeDtypeStruct((tiles, QUERY_TILE, LANES), BF16),
            jax.ShapeDtypeStruct((tiles, 8, QUERY_TILE), F32),
        ),
        in_specs=[pl.BlockSpec(memory_space=pltpu.SMEM)] + vmem_specs(2),
        out_specs=tuple(vmem_specs(3)),
        scratch_shapes=[pltpu.VMEM((LANES, blks * span), BF16)],
        compiler_params=pltpu.CompilerParams(vmem_limit_bytes=VMEM_LIMIT),
        name="attend",
    )(doc_lengths, q, kv)


def backward_kernel(doc_ref, q_ref, kv_ref, do_ref, o_ref, lse_ref, dq_out, dkv_out, kvt, dkv):
    _, _, z, y = place()
    total = q_ref.shape[0] * q_ref.shape[1]
    key_columns(doc_ref, kv_ref, kvt, z, total)
    dkv[...] = jnp.zeros_like(dkv)
    lanes = lane_ids((QUERY_TILE, LANES))
    tiles_per_span = q_ref.shape[1] // QUERY_TILE
    key_lanes = (lanes < HALF) == (y == 0)
    for tile in range(total // QUERY_TILE):
        inner = tile % tiles_per_span * QUERY_TILE
        query = q_ref[tile // tiles_per_span, inner : inner + QUERY_TILE, :]
        query = jnp.where(key_lanes, query, jnp.zeros_like(query))
        out_grad = do_ref[tile]
        out_grad = jnp.where(key_lanes, jnp.zeros_like(out_grad), out_grad)
        delta = jnp.sum(
            jnp.transpose(out_grad.astype(F32) * o_ref[tile]), axis=0, keepdims=True
        )
        log_total = lse_ref[tile, 0:1, :]
        low_row, high_row, low, high, single = tile_docs(
            doc_ref, z * total + tile * QUERY_TILE, QUERY_TILE
        )

        def step(
            block, mixed, query=query, out_grad=out_grad, delta=delta, log_total=log_total,
            low_row=low_row, high_row=high_row,
        ):
            first = pl.multiple_of(block * KEY_TILE, KEY_TILE)
            scores = dot(kv_ref[block], query, (1, 1))
            key = first + lax.broadcasted_iota(jnp.int32, scores.shape, 0)
            inside = jnp.logical_and(key >= low_row, key < high_row)
            weights = jnp.where(inside, jnp.exp(scores - log_total), 0.0)
            weight_grads = dot(kv_ref[block], out_grad, (1, 1))
            score_grads = (weights * (weight_grads - delta)).astype(BF16)
            dkv[block] += dot(score_grads, query) + dot(weights.astype(BF16), out_grad)
            return mixed + dot(kvt[:, pl.ds(first, KEY_TILE)], score_grads)

        mixed = lax.fori_loop(
            low // KEY_TILE,
            (high + KEY_TILE - 1) // KEY_TILE,
            step,
            jnp.zeros((LANES, QUERY_TILE), F32),
        )
        dq_out[tile] = jnp.transpose(mixed).astype(BF16)
    for block in range(dkv.shape[0]):
        dkv_out[block] = dkv[block].astype(BF16)


def call_backward(doc_lengths, q, kv, d_o, o, lse):
    blks, span, _ = kv.shape
    tiles = 2 * span // QUERY_TILE
    return pl.pallas_call(
        backward_kernel,
        out_shape=(
            jax.ShapeDtypeStruct((tiles, QUERY_TILE, LANES), BF16),
            jax.ShapeDtypeStruct((blks, span, LANES), BF16),
        ),
        in_specs=[pl.BlockSpec(memory_space=pltpu.SMEM)] + vmem_specs(5),
        out_specs=tuple(vmem_specs(2)),
        scratch_shapes=[
            pltpu.VMEM((LANES, blks * span), BF16),
            pltpu.VMEM((blks, span, LANES), F32),
        ],
        compiler_params=pltpu.CompilerParams(vmem_limit_bytes=VMEM_LIMIT),
        name="attend_back",
    )(doc_lengths, q, kv, d_o.reshape(tiles, QUERY_TILE, LANES), o, lse)


def gelu_parts(values):
    share = 0.5 * (1.0 + lax.erf(values * (2.0**-0.5)))
    slope = share + values * jnp.exp(-0.5 * values * values) * (2.0 * math.pi) ** -0.5
    return values * share, slope


def positions(expert_rows, expert_cols, rank_row, rank_col):
    def count(mask, axis):
        return jnp.sum(mask.astype(F32), axis=axis, keepdims=True)

    row = [None, None]
    col = [None, None]
    before = rank_col < rank_row
    after = rank_row < rank_col
    for choice in range(2):
        row[choice] = count((expert_cols[choice] == expert_rows[choice]) & before, 0)
        col[choice] = count((expert_rows[choice] == expert_cols[choice]) & after, 1)
    row[1] = row[1] + count(expert_cols[0] == expert_rows[1], 0)
    col[1] = col[1] + count(expert_rows[0] == expert_cols[1], 1)
    return row, col


def middle_kernel(
    heads, blks,
    x_ref, o_ref, wo_ref, routes_ref, rank_ref, d_out_ref, win_ref, wout_ref,
    out_ref, dh_ref, do_out, grads_ref, rows_out,
    o_all, dos, doa, rs, ra, po, pa, dr, da, dms, dma_all, rx, acc_out, acc_row, mix,
    o_send, o_recv, dos_send, dos_recv, r_send, r_recv, po_send, po_recv,
    dr_send, dr_recv, dm_send, dm_recv, rx_send, rx_recv, out_sem,
):
    head, blk, z, y = place()
    tokens, model = x_ref.shape
    capacity = 2 * tokens // blks
    slots = capacity * blks
    plane = [(k % heads, k // heads) for k in range(1, 2 * heads)]
    greet(
        [(around(head, kh, heads), 2 * z + around(y, ky, 2)) for kh, ky in plane]
        + [(head, around(blk, k, blks)) for k in range(1, blks) if True]
    )

    def plane_copies(src_of, dst, send, recv):
        copies = []
        for k, (kh, ky) in enumerate(plane):
            to_head, to_y = around(head, kh, heads), around(y, ky, 2)
            copies.append(
                remote(src_of(to_y, to_head), dst, send.at[k], recv.at[k], to_head, 2 * z + to_y)
            )
        return copies

    def blk_copies(src, dst, send, recv):
        return [
            remote(
                src.at[around(blk, k, blks)], dst.at[blk],
                send.at[k], recv.at[k], head, around(blk, k, blks),
            )
            for k in range(1, blks)
        ]

    def start(copies):
        for copy in copies:
            copy.start()

    def finish(copies):
        for copy in copies:
            copy.wait()

    o_copies = plane_copies(lambda to_y, to_head: o_ref.at[to_y, to_head], o_all.at[y, head], o_send, o_recv)
    start(o_copies)
    o_all[y, head] = o_ref[y, head]

    lanes = lane_ids((tokens, LANES))
    routes = routes_ref[...].astype(F32)
    e_cols = [routes[:, 0:1], routes[:, 1:2]]
    e_mix = jnp.transpose(jnp.where(lanes == 0, e_cols[0], e_cols[1]))
    e_rows = [e_mix[0:1, :], e_mix[1:2, :]]
    rank_row = rank_ref[...].astype(F32)
    rank_col = jnp.transpose(jnp.broadcast_to(rank_row, (tokens, tokens)))[:, 0:1]
    pos_rows, pos_cols = positions(e_rows, e_cols, rank_row, rank_col)

    def slot_of(expert, position):
        return jnp.where(position < capacity, expert * capacity + position, -1.0).astype(jnp.int32)

    slot_rows = [slot_of(e, p) for e, p in zip(e_rows, pos_rows)]
    slot_cols = [slot_of(e, p) for e, p in zip(e_cols, pos_cols)]
    slot_down = lax.broadcasted_iota(jnp.int32, (slots, tokens), 0)
    slot_across = lane_ids((tokens, slots))
    pick = [(slot_down == s).astype(BF16) for s in slot_rows]
    put = [(slot_across == s).astype(BF16) for s in slot_cols]
    pick_any = pick[0] + pick[1]
    put_any = put[0] + put[1]

    d_out = d_out_ref[...]
    dos[...] = dot(pick_any, d_out.astype(BF16)).astype(BF16).reshape(dos.shape)
    dos_copies = blk_copies(dos, doa, dos_send, dos_recv)
    start(dos_copies)
    doa[blk] = dos[blk]

    weight_out = jnp.concatenate(
        [wo_ref[(b ^ 1) * HALF : ((b ^ 1) + 1) * HALF, 0:model] for b in range(blks)], axis=0
    )
    small = wo_ref[:, model : model + LANES]
    small_across = jnp.concatenate(
        [
            jnp.transpose(small[i * LANES : (i + 1) * LANES].astype(F32))
            for i in range(model // LANES)
        ],
        axis=1,
    )
    gain = small_across[blks : blks + 1, :]

    finish(o_copies)
    for piece in range(heads):
        mix[:, piece * LANES : (piece + 1) * LANES] = jnp.where(
            lanes < HALF, o_all[1, piece], o_all[0, piece]
        )
    mixed = mix[...]
    hidden = x_ref[...].astype(F32) + dot(mixed, weight_out)
    xhat, scale = centre(hidden)
    routed = (xhat * gain).astype(BF16)
    logits = jnp.where(lanes < blks, dot(routed, small), MASKED)
    powers = jnp.exp(logits - jnp.max(logits, axis=1, keepdims=True))
    probs = powers / jnp.sum(powers, axis=1, keepdims=True)
    lanes_f = lanes.astype(F32)
    hots = [lanes_f == e for e in e_cols]
    gates = [jnp.sum(jnp.where(hot, probs, 0.0), axis=1, keepdims=True) for hot in hots]
    gate_mats = [split_high_low(g, lanes) for g in gates]

    rs[:, :, 0:model] = dot(pick_any, routed).astype(BF16).reshape(blks, capacity, model)
    rs[:, :, model : model + LANES] = (
        (dot(pick[0], gate_mats[0]) + dot(pick[1], gate_mats[1]))
        .astype(BF16)
        .reshape(blks, capacity, LANES)
    )
    r_copies = blk_copies(rs, ra, r_send, r_recv)
    start(r_copies)
    ra[blk] = rs[blk]
    acc_out[...] = jnp.zeros_like(acc_out)
    acc_row[...] = jnp.zeros_like(acc_row)
    finish(dos_copies)
    finish(r_copies)

    arrived_rows = ra[...].reshape(slots, model + LANES)
    out_rows = doa[...].reshape(slots, model)
    gate_col = join_high_low(arrived_rows, model)
    rx[head, :, 0:model] = arrived_rows[:, 0:model]
    rx[head, :, model : 2 * model] = (out_rows.astype(F32) * gate_col).astype(BF16)
    half_ff = wout_ref.shape[0] // 4

    @pl.loop(0, 4)
    def _(chunk):
        first = pl.multiple_of(chunk * half_ff, half_ff)
        into = win_ref[:, pl.ds(first, half_ff)]
        outof = wout_ref[pl.ds(first, half_ff), :]
        act, slope = gelu_parts(dot(rx[head, :, 0:model], into))
        acc_out[...] += dot(act.astype(BF16), outof)
        d_act = dot(rx[head, :, model : 2 * model], outof, (1, 1))
        acc_row[...] += dot((slope * d_act).astype(BF16), into, (1, 1))

    result = acc_out[...].astype(BF16)
    d_gate = jnp.sum(out_rows.astype(F32) * result.astype(F32), axis=1, keepdims=True)
    dr[:, :, 0:model] = acc_row[...].astype(BF16).reshape(blks, capacity, model)
    dr[:, :, model : model + LANES] = split_high_low(d_gate, lane_ids((slots, LANES))).reshape(
        blks, capacity, LANES
    )
    dr_copies = blk_copies(dr, da, dr_send, dr_recv)
    start(dr_copies)
    da[blk] = dr[blk]
    po[...] = result.reshape(blks, capacity, model)
    po_copies = blk_copies(po, pa, po_send, po_recv)
    start(po_copies)
    pa[blk] = po[blk]
    core = lax.rem(head, 2)
    sibling, across = head - core + 1 - core, around(head, 2, heads)
    to_sibling = remote(rx.at[head], rx.at[head], rx_send.at[0], rx_recv.at[0], sibling, blk)
    to_across = remote(rx.at[head], rx.at[head], rx_send.at[1], rx_recv.at[1], across, blk)
    to_across.start()
    to_sibling.start()

    finish(dr_copies)
    back = da[...].reshape(slots, model + LANES)
    d_routed = dot(put_any, back[:, 0:model])
    back_gate = back[:, model : model + LANES]
    d_gates = [join_high_low(dot(p, back_gate), 0) for p in put]
    d_probs = jnp.where(hots[0], d_gates[0], 0.0) + jnp.where(hots[1], d_gates[1], 0.0)
    d_logits = probs * (d_probs - jnp.sum(probs * d_probs, axis=1, keepdims=True))
    d_high = d_logits.astype(BF16)
    d_low = (d_logits - d_high.astype(F32)).astype(BF16)
    d_routed = d_routed + dot(d_high, small, (1, 1)) + dot(d_low, small, (1, 1))
    d_hidden = d_out + centre_back(d_routed * gain, xhat, scale)
    dh_ref[...] = d_hidden
    d_attn = d_hidden.astype(BF16)
    d_mixed = dot(d_attn, weight_out, (1, 1)).astype(BF16)
    for piece in range(heads):
        dms[piece] = d_mixed[:, piece * LANES : (piece + 1) * LANES]
    dm_copies = plane_copies(lambda to_y, to_head: dms.at[to_head], dma_all.at[y, head], dm_send, dm_recv)
    start(dm_copies)
    dma_all[y, head] = dms[head]

    d_weight = dot(mixed, d_attn, (0, 0)).astype(BF16)
    for b in range(blks):
        grads_ref[b, :, 0:model] = d_weight[(b ^ 1) * HALF : ((b ^ 1) + 1) * HALF, :]
    last = (lanes == blks).astype(BF16)
    d_small = dot(routed, d_high, (0, 0)) + dot((d_routed * xhat).astype(BF16), last, (0, 0))
    grads_ref[:, :, model : model + LANES] = d_small.astype(BF16).reshape(blks, HALF, LANES)
    finish(po_copies)
    parts = pa[...].reshape(slots, model)
    mixture = gates[0] * dot(put[0], parts) + gates[1] * dot(put[1], parts)
    out_ref[...] = (hidden + mixture).astype(BF16)

    arrived(rx.at[across], rx_recv.at[1])
    forward = remote(rx.at[across], rx.at[across], rx_send.at[2], rx_recv.at[2], sibling, blk)
    forward.start()
    finish(dm_copies)
    do_copy = pltpu.make_async_copy(dma_all, do_out, out_sem.at[0])
    do_copy.start()
    to_sibling.wait()
    to_across.wait_send()
    forward.wait()
    rows_copy = pltpu.make_async_copy(rx, rows_out, out_sem.at[1])
    rows_copy.start()
    do_copy.wait()
    rows_copy.wait()


def call_middle(x, o, wo, routes, rank, d_out, win, wout, heads, blks):
    tokens, model = x.shape
    capacity = 2 * tokens // blks
    slots = capacity * blks
    wide = model + LANES

    def rows(width):
        return pltpu.VMEM((blks, capacity, width), BF16)

    def block(*lead):
        return pltpu.VMEM((*lead, tokens, LANES), BF16)

    return pl.pallas_call(
        functools.partial(middle_kernel, heads, blks),
        out_shape=(
            jax.ShapeDtypeStruct((tokens, model), BF16),
            jax.ShapeDtypeStruct((tokens, model), F32),
            jax.ShapeDtypeStruct((2, heads, tokens, LANES), BF16),
            jax.ShapeDtypeStruct((blks, model // blks, wide), BF16),
            jax.ShapeDtypeStruct((heads, slots, 2 * model), BF16),
        ),
        in_specs=vmem_specs(8),
        out_specs=(*vmem_specs(2), *any_specs(1), *vmem_specs(1), *any_specs(1)),
        scratch_shapes=[
            block(2, heads), rows(model), rows(model), rows(wide), rows(wide), rows(model), rows(model),
            rows(wide), rows(wide), block(heads), block(2, heads),
            pltpu.VMEM((heads, slots, 2 * model), BF16),
            pltpu.VMEM((slots, model), F32), pltpu.VMEM((slots, model), F32),
            pltpu.VMEM((tokens, model), BF16),
            dma(2 * heads), dma(2 * heads), dma(blks), dma(blks), dma(blks), dma(blks), dma(blks), dma(blks),
            dma(blks), dma(blks), dma(2 * heads), dma(2 * heads), dma(3), dma(3), dma(2),
        ],
        compiler_params=pltpu.CompilerParams(
            collective_id=2, has_side_effects=True, vmem_limit_bytes=VMEM_LIMIT
        ),
        name="experts",
    )(x, o, wo, routes, rank, d_out, win, wout)


def last_kernel(
    heads, blks,
    x_ref, dh_ref, dq_ref, dkv_ref, xa_ref, wa_ref, w_ref, g1_ref, grads_ref, rx_ref, win_ref, wout_ref,
    dx_ref, dw_ref, shared_ref, din_out, dout_out,
    gain_tile, far_all, near_send_buf, near_all, pair_all, dq_all, us, ua, gs, ga, gh, w1, w2s, w2, w3,
    din_own, dout_own, din_other, dout_other,
    q_send, q_recv, pair_send, pair_recv, far_send, far_recv, near_send, near_recv,
    u_send, u_recv, g_send, g_recv, gh_send, gh_recv, w1_send, w1_recv, w2_send, w2_recv,
    w3_send, w3_recv, e_send, e_recv, out_sem,
):
    head, blk, z, y = place()
    planes = blks // 2
    tokens, model = x_ref.shape
    rows = w_ref.shape[0]
    greet(
        [(around(head, k, heads), blk) for k in range(1, heads)]
        + [(head, around(blk, k, blks)) for k in range(1, blks)]
    )

    def start(copies):
        for copy in copies:
            copy.start()

    def finish(copies):
        for copy in copies:
            copy.wait()

    other_y = around(y, 1, 2)
    pair = 2 * z + other_y
    above, below = z < planes - 1, z > 0
    directions = ((1, above, below, 0), (-1, below, above, 2))

    def far_copy(step, slot, side):
        span = 2 * (z + 2 * step) + side
        return remote(
            dkv_ref.at[span], far_all.at[slot + side],
            far_send.at[slot + side], far_recv.at[slot + side], head, 2 * (z + step) + y,
        )

    def near_copy(step, slot, side):
        return remote(
            near_send_buf.at[slot + side], near_all.at[slot // 2, y],
            near_send.at[slot + side], near_recv.at[slot // 2, y], head, 2 * (z + step) + side,
        )

    def two_away(step):
        return z + 2 * step < planes if step > 0 else z + 2 * step >= 0

    for step, there, back, slot in directions:

        @pl.when(two_away(step))
        def _():
            for side in range(2):
                far_copy(step, slot, side).start()

    pair_copy = remote(dkv_ref.at[pair], pair_all, pair_send, pair_recv, head, pair)
    pair_copy.start()
    q_copy = remote(dq_ref.at[other_y], dq_all, q_send, q_recv, head, pair)
    q_copy.start()
    w1_copies = [
        remote(
            grads_ref.at[:, around(head, k, heads)], w1.at[head],
            w1_send.at[k], w1_recv.at[k], around(head, k, heads), blk,
        )
        for k in range(1, heads)
    ]
    start(w1_copies)
    w1[head] = grads_ref[:, head]

    core = lax.rem(head, 2)
    sibling = head - core + 1 - core
    ff_half = wout_ref.shape[0] // 2
    ff_step = ff_half // 4

    def expert_chunk(chunk):
        here = pl.multiple_of(core * ff_half + chunk * ff_step, ff_step)
        there = pl.multiple_of(chunk * ff_step, ff_step)
        into = win_ref[:, pl.ds(here, ff_step)]
        outof = wout_ref[pl.ds(here, ff_step), :]
        d_in = jnp.zeros((model, ff_step), F32)
        d_out = jnp.zeros((ff_step, model), F32)
        for source in range(heads):
            rows_in = rx_ref[source, :, 0:model]
            grads_out = rx_ref[source, :, model : 2 * model]
            act, slope = gelu_parts(dot(rows_in, into))
            d_act = dot(grads_out, outof, (1, 1))
            d_in = d_in + dot(rows_in, (slope * d_act).astype(BF16), (0, 0))
            d_out = d_out + dot(act.astype(BF16), grads_out, (0, 0))
        din_own[:, pl.ds(there, ff_step)] = d_in.astype(BF16)
        dout_own[pl.ds(there, ff_step), :] = d_out.astype(BF16)

    @pl.loop(0, 2)
    def _(chunk):
        expert_chunk(chunk)

    for step, there, back, slot in directions:

        @pl.when(there)
        def _():
            for side in range(2):
                near_send_buf[slot + side] = dkv_ref[2 * (z + step) + side]

        @pl.when(jnp.logical_and(there, back))
        def _():
            for side in range(2):
                arrived(far_all.at[slot + side], far_recv.at[slot + side])
                near_send_buf[slot + side] = (
                    near_send_buf[slot + side].astype(F32) + far_all[slot + side].astype(F32)
                ).astype(BF16)

        @pl.when(there)
        def _():
            for side in range(2):
                near_copy(step, slot, side).start()

    @pl.loop(2, 4)
    def _(chunk):
        expert_chunk(chunk)

    e_copies = [
        remote(din_own, din_other, e_send.at[0], e_recv.at[0], sibling, blk),
        remote(dout_own, dout_other, e_send.at[1], e_recv.at[1], sibling, blk),
    ]
    start(e_copies)

    pair_copy.wait()
    q_copy.wait()
    for step, there, back, slot in directions:

        @pl.when(back)
        def _():
            for side in range(2):
                arrived(near_all.at[slot // 2, side], near_recv.at[slot // 2, side])

        @pl.when(jnp.logical_not(back))
        def _():
            near_all[slot // 2] = jnp.zeros(near_all.shape[1:], BF16)

    lanes = lane_ids((tokens, LANES))
    even = y == 0
    weight = wa_ref[...].reshape(model, 3 * LANES)
    g_sum = jnp.zeros((model, 3 * LANES), F32)
    for piece in range(heads):
        span = slice(piece * tokens, (piece + 1) * tokens)
        own = dkv_ref[blk, span, :].astype(F32)
        other = pair_all[span, :].astype(F32)
        kv_grads = [
            jnp.where(even, own, other) + near_all[0, 0, span, :].astype(F32) + near_all[1, 0, span, :].astype(F32),
            jnp.where(even, other, own) + near_all[0, 1, span, :].astype(F32) + near_all[1, 1, span, :].astype(F32),
        ]
        q_own = dq_ref[y, span, :]
        q_other = dq_all[span, :]
        own_lanes = (lanes < HALF) == even
        q_grads = jnp.where(own_lanes, q_own, q_other)
        made = jnp.concatenate([kv_grads[0].astype(BF16), kv_grads[1].astype(BF16), q_grads], axis=1)
        us[piece] = dot(made, weight, (1, 1)).astype(BF16)
        g_sum = g_sum + dot(xa_ref[piece], made, (0, 0))
    u_copies = [
        remote(
            us.at[around(head, k, heads)], ua.at[head],
            u_send.at[k], u_recv.at[k], around(head, k, heads), blk,
        )
        for k in range(1, heads)
    ]
    start(u_copies)
    ua[head] = us[head]
    gs[...] = g_sum.astype(BF16).reshape(gs.shape)
    g_copies = [
        remote(
            gs.at[around(blk, k, blks)], ga.at[blk],
            g_send.at[k], g_recv.at[k], head, around(blk, k, blks),
        )
        for k in range(1, blks)
    ]
    start(g_copies)
    ga[blk] = gs[blk]

    finish(w1_copies)
    summed = w1[0].astype(F32)
    for source in range(1, heads):
        summed = summed + w1[source].astype(F32)
    w2s[...] = summed.astype(BF16)
    w2_copies = [
        remote(
            w2s.at[around(blk, k, blks)], w2.at[blk],
            w2_send.at[k], w2_recv.at[k], head, around(blk, k, blks),
        )
        for k in range(1, blks)
    ]
    start(w2_copies)
    w2[blk] = w2s[blk]

    finish(e_copies)
    wide_out = [
        pltpu.make_async_copy(din_own, din_out.at[core], out_sem.at[0]),
        pltpu.make_async_copy(din_other, din_out.at[1 - core], out_sem.at[1]),
        pltpu.make_async_copy(dout_own, dout_out.at[core], out_sem.at[2]),
        pltpu.make_async_copy(dout_other, dout_out.at[1 - core], out_sem.at[3]),
    ]
    start(wide_out)

    finish(u_copies)
    grad = ua[0].astype(F32)
    for source in range(1, heads):
        grad = grad + ua[source].astype(F32)
    xhat, scale = centre(x_ref[...].astype(F32))
    dx_ref[...] = dh_ref[...] + centre_back(grad, xhat, scale)

    finish(g_copies)
    total = ga[0].astype(F32)
    for source in range(1, blks):
        total = total + ga[source].astype(F32)
    gh[head] = total.astype(BF16)
    gh_copies = [
        remote(gh.at[head], gh.at[head], gh_send.at[k], gh_recv.at[k], around(head, k, heads), blk)
        for k in range(1, heads)
    ]
    start(gh_copies)
    finish(w2_copies)
    part = w2[0].astype(F32)
    for source in range(1, blks):
        part = part + w2[source].astype(F32)
    w3[head] = part.astype(BF16)
    w3_copies = [
        remote(w3.at[head], w3.at[head], w3_send.at[k], w3_recv.at[k], around(head, k, heads), blk)
        for k in range(1, heads)
    ]
    start(w3_copies)

    gain_tile[...] = jnp.zeros_like(gain_tile)
    gain_tile[0:1, 0:rows] = g1_ref[...].astype(F32)
    gain = jnp.transpose(jnp.broadcast_to(gain_tile[0:1, :], (LANES, LANES)))[:rows]
    low_half = lane_ids((rows, LANES)) < HALF
    finish(gh_copies)
    d_gain = jnp.zeros((rows, LANES), F32)
    for source in range(heads):
        both = [gh[source, :, i * LANES : (i + 1) * LANES].astype(F32) for i in range(3)]
        grads = (
            both[2] * HS ** (-0.5),
            jnp.where(low_half, both[0], both[1]),
            pltpu.roll(jnp.where(low_half, both[1], both[0]), HALF, 1),
        )
        for which, value in enumerate(grads):
            columns = slice(which * model + source * LANES, which * model + (source + 1) * LANES)
            d_gain = d_gain + value * w_ref[:, columns].astype(F32)
            dw_ref[:, columns] = value * gain
    finish(w3_copies)
    shared = w3[...].reshape(rows, w3.shape[-1]).astype(F32)
    shared_ref[:, 0:model] = shared[:, 0:model]
    gain_col = jnp.sum(d_gain, axis=1, keepdims=True)
    shared_ref[:, model : model + LANES] = jnp.where(
        lane_ids((rows, LANES)) == blks + 1, gain_col, shared[:, model : model + LANES]
    )
    for step, there, back, slot in directions:

        @pl.when(two_away(step))
        def _():
            for side in range(2):
                far_copy(step, slot, side).wait_send()

        @pl.when(there)
        def _():
            for side in range(2):
                near_copy(step, slot, side).wait_send()

    finish(wide_out)


def call_last(x, dh, dq, dkv, xa, wa, w_qkv, g1, grads, rx, win, wout, heads, blks):
    tokens, model = x.shape
    span = tokens * heads
    rows = w_qkv.shape[0]
    wide = model + LANES
    part = rows // heads
    ff = wout.shape[0]

    def block(*lead):
        return pltpu.VMEM((*lead, span, LANES), BF16)

    return pl.pallas_call(
        functools.partial(last_kernel, heads, blks),
        out_shape=(
            jax.ShapeDtypeStruct((tokens, model), F32),
            jax.ShapeDtypeStruct((rows, 3 * model), F32),
            jax.ShapeDtypeStruct((rows, wide), F32),
            jax.ShapeDtypeStruct((2, model, ff // 2), BF16),
            jax.ShapeDtypeStruct((2, ff // 2, model), BF16),
        ),
        in_specs=vmem_specs(12),
        out_specs=(*vmem_specs(3), *any_specs(2)),
        scratch_shapes=[
            pltpu.VMEM((8, LANES), F32),
            block(4), block(4), block(2, 2), block(), block(),
            pltpu.VMEM((heads, tokens, model), BF16), pltpu.VMEM((heads, tokens, model), BF16),
            pltpu.VMEM((blks, rows, 3 * LANES), BF16), pltpu.VMEM((blks, rows, 3 * LANES), BF16),
            pltpu.VMEM((heads, rows, 3 * LANES), BF16),
            pltpu.VMEM((heads, blks, part, wide), BF16), pltpu.VMEM((blks, part, wide), BF16),
            pltpu.VMEM((blks, part, wide), BF16), pltpu.VMEM((heads, part, wide), BF16),
            pltpu.VMEM((model, ff // 2), BF16), pltpu.VMEM((ff // 2, model), BF16),
            pltpu.VMEM((model, ff // 2), BF16), pltpu.VMEM((ff // 2, model), BF16),
            pltpu.SemaphoreType.DMA, pltpu.SemaphoreType.DMA, pltpu.SemaphoreType.DMA, pltpu.SemaphoreType.DMA,
            dma(4), dma(4), dma(4), dma(2, 2),
            dma(heads), dma(heads), dma(blks), dma(blks), dma(heads), dma(heads), dma(heads), dma(heads),
            dma(blks), dma(blks), dma(heads), dma(heads), dma(2), dma(2), dma(4),
        ],
        compiler_params=pltpu.CompilerParams(
            collective_id=3, has_side_effects=True, vmem_limit_bytes=VMEM_LIMIT
        ),
        name="last",
    )(
        x, dh, dq.reshape(2, span, LANES), dkv, xa, wa, w_qkv, g1.reshape(1, rows),
        grads.reshape(blks, heads, part, wide), rx, win, wout,
    )


def local_kernels(
    inputs, ln1_gain, w_qkv, w_out, ln2_gain, w_router,
    expert_in, expert_out, routes, priority, doc_lengths, d_out,
):
    heads, blks = lax.axis_size("head"), lax.axis_size("blk")
    model = inputs.shape[1]
    tokens = inputs.shape[0]
    win, wout = expert_in[0], expert_out[0]
    q, kv, xa, wa, wo = call_qkv(inputs, w_qkv, ln1_gain, w_out, w_router, ln2_gain, heads, blks)
    o, o_low, lse = call_forward(doc_lengths, q, kv)
    output, dh, d_o, grads, rx = call_middle(
        inputs, o_low.reshape(2, heads, tokens, LANES), wo.reshape(model, model + LANES),
        routes, priority, d_out, win, wout, heads, blks,
    )
    dq, dkv = call_backward(doc_lengths, q, kv, d_o, o, lse)
    d_inputs, d_qkv, shared, d_in, d_out_weight = call_last(
        inputs, dh, dq, dkv, xa, wa, w_qkv, ln1_gain, grads, rx, win, wout, heads, blks
    )
    return (
        output,
        d_inputs,
        shared[:, model + blks + 1],
        d_qkv,
        shared[:, :model],
        shared[:, model + blks],
        shared[:, model : model + blks],
        jnp.concatenate([d_in[0], d_in[1]], axis=1).astype(F32)[None],
        d_out_weight.reshape(wout.shape).astype(F32)[None],
    )


def solution(mesh):
    in_specs = (
        P(("blk", "head"), None),
        P("blk"),
        P("blk", None),
        P("blk", None),
        P("blk"),
        P("blk", None),
        P("blk", None, None),
        P("blk", None, None),
        P(("blk", "head"), None),
        P(("blk", "head"), None),
        P(),
        P(("blk", "head"), None),
    )
    out_specs = (
        P(("blk", "head"), None),
        P(("blk", "head"), None),
        P("blk"),
        P("blk", None),
        P("blk", None),
        P("blk"),
        P("blk", None),
        P("blk", None, None),
        P("blk", None, None),
    )
    fits = mesh.shape["head"] == 4 and mesh.shape["blk"] == 8
    body = local_kernels if fits else local
    return jax.shard_map(body, mesh=mesh, in_specs=in_specs, out_specs=out_specs, check_vma=False)
```

```python
import functools
import math

import jax
import jax.numpy as jnp
from jax import lax
from jax.experimental import pallas as pl
from jax.experimental.pallas import tpu as pltpu
from jax.sharding import PartitionSpec as P

HS = 64
KEY_BLOCK = 2048


PRECISE = lax.Precision.HIGHEST
MASKED = -1e30
EPSILON = 1e-06


def layer_norm(values, gain):
    average = jnp.mean(values, axis=-1, keepdims=True)
    centred = values - average
    spread = jnp.mean(centred * centred, axis=-1, keepdims=True)
    return centred * lax.rsqrt(spread + EPSILON) * gain


def gelu_exact(values):
    return jax.nn.gelu(values, approximate=False)


def router(row_block, weight):
    return jax.nn.softmax(jnp.dot(row_block, weight, precision=PRECISE), axis=-1)


def doc_index(positions, doc_lengths):
    places = jnp.arange(doc_lengths.shape[0], dtype=jnp.int32)
    starts = jnp.sum(jnp.where(places[None, :] < places[:, None], doc_lengths[None, :], 0), axis=1)
    at_most = (starts[None, :] <= positions[:, None]).astype(jnp.int32)
    return jnp.sum(at_most, axis=1) - 1


def slot_table(route_rows, ranking, capacity):
    token_count = route_rows.shape[0]
    expert = jnp.transpose(route_rows).reshape(-1)
    pair_order = (jnp.arange(2, dtype=jnp.int32)[:, None] * token_count + ranking[None, :]).reshape(
        -1
    )
    before = (expert[:, None] == expert[None, :]) & (pair_order[None, :] < pair_order[:, None])
    position = jnp.sum(before.astype(jnp.int32), axis=1)
    slot_ids = jnp.where(position < capacity, expert * capacity + position, -1)
    return slot_ids.reshape(2, token_count)


def keep_state(current):
    return current


def local(
    inputs,
    ln1_gain,
    w_qkv,
    w_out,
    ln2_gain,
    w_router,
    expert_in,
    expert_out,
    routes,
    priority,
    doc_lengths,
    d_out,
):
    blk_size = lax.axis_size("blk")
    tok_rows = inputs.shape[0]
    model_width = inputs.shape[1]
    capacity = 2 * tok_rows // blk_size
    slot_total = blk_size * capacity
    gain_one, qkv_weight, out_weight, gain_two, router_weight = (
        lax.all_gather(ln1_gain, "blk", axis=0, tiled=True),
        lax.all_gather(w_qkv, "blk", axis=0, tiled=True),
        lax.all_gather(w_out, "blk", axis=0, tiled=True),
        lax.all_gather(ln2_gain, "blk", axis=0, tiled=True),
        lax.all_gather(w_router, "blk", axis=0, tiled=True),
    )
    input_rows = inputs.astype(jnp.float32)
    normed_one, norm_one_pull = jax.vjp(layer_norm, input_rows, gain_one.astype(jnp.float32))
    normed_low = normed_one.astype(jnp.bfloat16)
    qkv_rows = jnp.dot(normed_low, qkv_weight, preferred_element_type=jnp.float32).astype(
        jnp.bfloat16
    )
    query_heads, key_heads, value_heads = (
        lax.all_to_all(qkv_rows[:, :model_width], "head", split_axis=1, concat_axis=0, tiled=True),
        lax.all_to_all(
            qkv_rows[:, model_width : 2 * model_width],
            "head",
            split_axis=1,
            concat_axis=0,
            tiled=True,
        ),
        lax.all_to_all(
            qkv_rows[:, 2 * model_width :], "head", split_axis=1, concat_axis=0, tiled=True
        ),
    )
    span_rows = query_heads.shape[0]
    head_count = query_heads.shape[1] // HS
    key_all, value_all = (
        lax.all_gather(key_heads, "blk", axis=0, tiled=True),
        lax.all_gather(value_heads, "blk", axis=0, tiled=True),
    )
    total_rows = key_all.shape[0]
    block_count = total_rows // KEY_BLOCK
    scale_factor = HS ** (-0.5)
    query_pos = lax.axis_index("blk") * span_rows + jnp.arange(span_rows, dtype=jnp.int32)
    query_docs = doc_index(query_pos, doc_lengths)
    queries = query_heads.reshape(span_rows, head_count, HS)

    def block_parts(block_index, key_source, value_source):
        first_key = block_index * KEY_BLOCK
        key_rows = lax.dynamic_slice_in_dim(key_source, first_key, KEY_BLOCK, 0).reshape(
            KEY_BLOCK, head_count, HS
        )
        value_rows = lax.dynamic_slice_in_dim(value_source, first_key, KEY_BLOCK, 0).reshape(
            KEY_BLOCK, head_count, HS
        )
        key_docs = doc_index(first_key + jnp.arange(KEY_BLOCK, dtype=jnp.int32), doc_lengths)
        is_live = (key_docs[0] <= query_docs[-1]) & (key_docs[-1] >= query_docs[0])
        same_doc = query_docs[:, None] == key_docs[None, :]
        return (first_key, key_rows, value_rows, same_doc, is_live)

    def block_scores(key_rows, same_doc):
        raw_scores = (
            jnp.einsum("qhd,khd->hqk", queries, key_rows, preferred_element_type=jnp.float32)
            * scale_factor
        )
        return jnp.where(same_doc[None], raw_scores, MASKED)

    def stat_step(block_index, loop_state):
        first_key, key_rows, value_rows, same_doc, is_live = block_parts(
            block_index, key_all, value_all
        )

        def stat_update(current):
            running_max, running_sum = current
            scores = block_scores(key_rows, same_doc)
            new_max = jnp.maximum(running_max, jnp.max(scores, axis=2))
            exp_terms = jnp.where(same_doc[None], jnp.exp(scores - new_max[:, :, None]), 0.0)
            return (
                new_max,
                running_sum * jnp.exp(running_max - new_max) + jnp.sum(exp_terms, axis=2),
            )

        return lax.cond(is_live, stat_update, keep_state, loop_state)

    start_state = (
        jnp.full((head_count, span_rows), MASKED, jnp.float32),
        jnp.zeros((head_count, span_rows), jnp.float32),
    )
    running_max, running_sum = lax.fori_loop(0, block_count, stat_step, start_state)
    log_total = running_max + jnp.log(running_sum)

    def out_step(block_index, loop_state):
        first_key, key_rows, value_rows, same_doc, is_live = block_parts(
            block_index, key_all, value_all
        )

        def out_update(current):
            scores = block_scores(key_rows, same_doc)
            weights = jnp.where(
                same_doc[None], jnp.exp(scores - log_total[:, :, None]), 0.0
            ).astype(jnp.bfloat16)
            return current + jnp.einsum(
                "hqk,khd->qhd", weights, value_rows, preferred_element_type=jnp.float32
            )

        return lax.cond(is_live, out_update, keep_state, loop_state)

    mixed_full = lax.fori_loop(
        0, block_count, out_step, jnp.zeros((span_rows, head_count, HS), jnp.float32)
    )
    mixed_low = mixed_full.reshape(span_rows, head_count * HS).astype(jnp.bfloat16)
    mixed_tokens = lax.all_to_all(mixed_low, "head", split_axis=0, concat_axis=1, tiled=True)
    attended = jnp.dot(mixed_tokens, out_weight, preferred_element_type=jnp.float32)
    hidden_one = input_rows + attended
    normed_two, norm_two_pull = jax.vjp(layer_norm, hidden_one, gain_two.astype(jnp.float32))
    routed_low = normed_two.astype(jnp.bfloat16)
    router_probs, router_pull = jax.vjp(
        router, routed_low.astype(jnp.float32), router_weight.astype(jnp.float32)
    )
    slot_ids = slot_table(routes, priority[0], capacity)
    select = (
        slot_ids[:, :, None] == jnp.arange(slot_total, dtype=jnp.int32)[None, None, :]
    ).astype(jnp.bfloat16)
    send_rows = jnp.einsum(
        "kts,td->sd", select, routed_low, preferred_element_type=jnp.float32
    ).astype(jnp.bfloat16)
    expert_rows = lax.all_to_all(
        send_rows.reshape(blk_size, capacity, model_width),
        "blk",
        split_axis=0,
        concat_axis=0,
        tiled=True,
    ).reshape(slot_total, model_width)
    weight_in = expert_in[0]
    weight_out = expert_out[0]
    pre_act = jnp.dot(expert_rows, weight_in, preferred_element_type=jnp.float32)
    hidden_act, gelu_pull = jax.vjp(gelu_exact, pre_act)
    hidden_low = hidden_act.astype(jnp.bfloat16)
    expert_result = jnp.dot(hidden_low, weight_out, preferred_element_type=jnp.float32).astype(
        jnp.bfloat16
    )
    slot_result = lax.all_to_all(
        expert_result.reshape(blk_size, capacity, model_width),
        "blk",
        split_axis=0,
        concat_axis=0,
        tiled=True,
    ).reshape(slot_total, model_width)
    pair_result = jnp.einsum("kts,sd->ktd", select, slot_result, preferred_element_type=jnp.float32)
    route_hot = (routes[:, :, None] == jnp.arange(blk_size, dtype=jnp.int32)[None, None, :]).astype(
        jnp.float32
    )
    gate_vals = jnp.sum(router_probs[:, None, :] * route_hot, axis=2)
    mixture = gate_vals[:, 0, None] * pair_result[0] + gate_vals[:, 1, None] * pair_result[1]
    output = (hidden_one + mixture).astype(jnp.bfloat16)
    d_gates = jnp.transpose(jnp.sum(d_out[None] * pair_result, axis=2))
    d_probs = jnp.sum(d_gates[:, :, None] * route_hot, axis=1)
    pair_grads = (jnp.transpose(gate_vals)[:, :, None] * d_out[None]).astype(jnp.bfloat16)
    slot_grads = jnp.einsum(
        "kts,ktd->sd", select, pair_grads, preferred_element_type=jnp.float32
    ).astype(jnp.bfloat16)
    result_grads = lax.all_to_all(
        slot_grads.reshape(blk_size, capacity, model_width),
        "blk",
        split_axis=0,
        concat_axis=0,
        tiled=True,
    ).reshape(slot_total, model_width)
    d_hidden_act = jnp.dot(result_grads, weight_out.T, preferred_element_type=jnp.float32)
    d_weight_out = jnp.dot(hidden_low.T, result_grads, preferred_element_type=jnp.float32)
    d_preact = gelu_pull(d_hidden_act)[0].astype(jnp.bfloat16)
    d_weight_in = jnp.dot(expert_rows.T, d_preact, preferred_element_type=jnp.float32)
    row_grads = jnp.dot(d_preact, weight_in.T, preferred_element_type=jnp.float32).astype(
        jnp.bfloat16
    )
    slot_back = lax.all_to_all(
        row_grads.reshape(blk_size, capacity, model_width),
        "blk",
        split_axis=0,
        concat_axis=0,
        tiled=True,
    ).reshape(slot_total, model_width)
    d_routed = jnp.einsum("kts,sd->td", select, slot_back, preferred_element_type=jnp.float32)
    d_routed_router, d_router = router_pull(d_probs)
    d_hidden_norm, d_gain_two = norm_two_pull(d_routed + d_routed_router)
    d_hidden_one = d_out + d_hidden_norm
    attn_grads = d_hidden_one.astype(jnp.bfloat16)
    d_out_weight = jnp.dot(mixed_tokens.T, attn_grads, preferred_element_type=jnp.float32)
    mixed_grads = jnp.dot(attn_grads, out_weight.T, preferred_element_type=jnp.float32).astype(
        jnp.bfloat16
    )
    head_grads = lax.all_to_all(mixed_grads, "head", split_axis=1, concat_axis=0, tiled=True)
    out_grads = head_grads.reshape(span_rows, head_count, HS)
    row_delta = jnp.transpose(jnp.sum(out_grads.astype(jnp.float32) * mixed_full, axis=2))
    key_back, value_back = (
        lax.all_gather(key_heads, "blk", axis=0, tiled=True),
        lax.all_gather(value_heads, "blk", axis=0, tiled=True),
    )

    def grad_step(block_index, loop_state):
        first_key, key_rows, value_rows, same_doc, is_live = block_parts(
            block_index, key_back, value_back
        )

        def grad_update(current):
            query_grad, key_grad, value_grad = current
            scores = block_scores(key_rows, same_doc)
            weights = jnp.where(same_doc[None], jnp.exp(scores - log_total[:, :, None]), 0.0)
            value_part = jnp.einsum(
                "hqk,qhd->khd",
                weights.astype(jnp.bfloat16),
                out_grads,
                preferred_element_type=jnp.float32,
            )
            weight_grads = jnp.einsum(
                "qhd,khd->hqk", out_grads, value_rows, preferred_element_type=jnp.float32
            )
            score_grads = (weights * (weight_grads - row_delta[:, :, None])).astype(jnp.bfloat16)
            query_grad = (
                query_grad
                + jnp.einsum(
                    "hqk,khd->qhd", score_grads, key_rows, preferred_element_type=jnp.float32
                )
                * scale_factor
            )
            key_part = (
                jnp.einsum("hqk,qhd->khd", score_grads, queries, preferred_element_type=jnp.float32)
                * scale_factor
            )
            key_grad = lax.dynamic_update_slice_in_dim(
                key_grad, key_part.reshape(KEY_BLOCK, head_count * HS), first_key, 0
            )
            value_grad = lax.dynamic_update_slice_in_dim(
                value_grad, value_part.reshape(KEY_BLOCK, head_count * HS), first_key, 0
            )
            return (query_grad, key_grad, value_grad)

        return lax.cond(is_live, grad_update, keep_state, loop_state)

    start_grads = (
        jnp.zeros((span_rows, head_count, HS), jnp.float32),
        jnp.zeros((total_rows, head_count * HS), jnp.float32),
        jnp.zeros((total_rows, head_count * HS), jnp.float32),
    )
    query_grad, key_grad, value_grad = lax.fori_loop(0, block_count, grad_step, start_grads)
    key_own, value_own = (
        lax.psum_scatter(
            key_grad.astype(jnp.bfloat16), "blk", scatter_dimension=0, tiled=True
        ).astype(jnp.float32),
        lax.psum_scatter(
            value_grad.astype(jnp.bfloat16), "blk", scatter_dimension=0, tiled=True
        ).astype(jnp.float32),
    )
    query_tokens_grad, key_tokens_grad, value_tokens_grad = (
        lax.all_to_all(
            query_grad.reshape(span_rows, head_count * HS).astype(jnp.bfloat16),
            "head",
            split_axis=0,
            concat_axis=1,
            tiled=True,
        ),
        lax.all_to_all(
            key_own.astype(jnp.bfloat16), "head", split_axis=0, concat_axis=1, tiled=True
        ),
        lax.all_to_all(
            value_own.astype(jnp.bfloat16), "head", split_axis=0, concat_axis=1, tiled=True
        ),
    )
    qkv_grads = jnp.concatenate([query_tokens_grad, key_tokens_grad, value_tokens_grad], axis=1)
    d_qkv_weight = jnp.dot(normed_low.T, qkv_grads, preferred_element_type=jnp.float32)
    normed_grads = jnp.dot(qkv_grads, qkv_weight.T, preferred_element_type=jnp.float32)
    d_inputs_norm, d_gain_one = norm_one_pull(normed_grads)
    d_inputs = d_hidden_one + d_inputs_norm
    gain_one_sum, qkv_sum, out_sum, gain_two_sum, router_sum = (
        lax.psum_scatter(
            d_gain_one.astype(jnp.bfloat16), "blk", scatter_dimension=0, tiled=True
        ).astype(jnp.float32),
        lax.psum_scatter(
            d_qkv_weight.astype(jnp.bfloat16), "blk", scatter_dimension=0, tiled=True
        ).astype(jnp.float32),
        lax.psum_scatter(
            d_out_weight.astype(jnp.bfloat16), "blk", scatter_dimension=0, tiled=True
        ).astype(jnp.float32),
        lax.psum_scatter(
            d_gain_two.astype(jnp.bfloat16), "blk", scatter_dimension=0, tiled=True
        ).astype(jnp.float32),
        lax.psum_scatter(
            d_router.astype(jnp.bfloat16), "blk", scatter_dimension=0, tiled=True
        ).astype(jnp.float32),
    )
    gain_one_all, qkv_all, out_all, gain_two_all, router_all, expert_in_all, expert_out_all = (
        lax.psum(gain_one_sum.astype(jnp.bfloat16), "head").astype(jnp.float32),
        lax.psum(qkv_sum.astype(jnp.bfloat16), "head").astype(jnp.float32),
        lax.psum(out_sum.astype(jnp.bfloat16), "head").astype(jnp.float32),
        lax.psum(gain_two_sum.astype(jnp.bfloat16), "head").astype(jnp.float32),
        lax.psum(router_sum.astype(jnp.bfloat16), "head").astype(jnp.float32),
        lax.psum(d_weight_in[None].astype(jnp.bfloat16), "head").astype(jnp.float32),
        lax.psum(d_weight_out[None].astype(jnp.bfloat16), "head").astype(jnp.float32),
    )
    return (
        output,
        d_inputs,
        gain_one_all,
        qkv_all,
        out_all,
        gain_two_all,
        router_all,
        expert_in_all,
        expert_out_all,
    )


MESH = pl.DeviceIdType.MESH
LANES = 128
HALF = LANES // 2
MIB = 2**20
F32 = jnp.float32
BF16 = jnp.bfloat16


def dot(left, right, dims=(1, 0)):
    return lax.dot_general(
        left, right, (((dims[0],), (dims[1],)), ((), ())), preferred_element_type=F32
    )


def remote(src, dst, send_sem, recv_sem, head, blk):
    return pltpu.make_async_remote_copy(
        src_ref=src,
        dst_ref=dst,
        send_sem=send_sem,
        recv_sem=recv_sem,
        device_id={"head": head, "blk": blk},
        device_id_type=MESH,
    )


def arrived(ref, sem):
    pltpu.make_async_copy(ref, ref, sem).wait()


def greet(peers):
    barrier = pltpu.get_barrier_semaphore()
    for head, blk in peers:
        pl.semaphore_signal(
            barrier, inc=1, device_id={"head": head, "blk": blk}, device_id_type=MESH
        )
    pl.semaphore_wait(barrier, len(peers))


def lane_ids(shape):
    return lax.broadcasted_iota(jnp.int32, shape, len(shape) - 1)


def centre(values):
    average = jnp.mean(values, axis=-1, keepdims=True)
    centred = values - average
    spread = jnp.mean(centred * centred, axis=-1, keepdims=True)
    scale = lax.rsqrt(spread + EPSILON)
    return centred * scale, scale


def centre_back(grad, xhat, scale):
    middle = jnp.mean(grad, axis=-1, keepdims=True)
    along = jnp.mean(grad * xhat, axis=-1, keepdims=True)
    return (grad - middle - xhat * along) * scale


def split_high_low(column, lanes):
    high = column.astype(BF16)
    low = (column - high.astype(F32)).astype(BF16)
    return jnp.where(lanes < HALF, high.astype(F32), low.astype(F32)).astype(BF16)


def join_high_low(matrix, start):
    return matrix[:, start : start + 1].astype(F32) + matrix[
        :, start + HALF : start + HALF + 1
    ].astype(F32)


def place():
    head, blk = lax.axis_index("head"), lax.axis_index("blk")
    return head, blk, blk // 2, lax.rem(blk, 2)


def around(index, step, size):
    return lax.rem(index + step, size)


def qkv_kernel(
    heads, blks,
    x_hbm, w_hbm, g1_hbm, wo_hbm, wr_hbm, g2_hbm,
    qall, kvall, xall, wall, wo_all,
    x_ref, w_ref, rows_in, g1_ref, g2_ref, wr_ref, wo_own, kv_other, in_sem,
    x_send, x_recv, w_send, w_recv, o_send, o_recv, p_send, p_recv,
    k_send, k_recv, q_recv,
):
    head, blk, z, y = place()
    planes = blks // 2
    model = x_ref.shape[1]
    rows = w_ref.shape[0]
    part = rows // heads
    experts = wr_ref.shape[0]
    wanted = (
        (w_hbm, w_ref), (g1_hbm, g1_ref), (g2_hbm, g2_ref), (wr_hbm, wr_ref), (x_hbm, x_ref),
        (wo_hbm, wo_own.at[:, pl.ds(0, model)]),
    )
    fetched = [
        pltpu.make_async_copy(src, dst, in_sem.at[i]) for i, (src, dst) in enumerate(wanted)
    ]
    for copy in fetched:
        copy.start()
    rows_in[...] = jnp.zeros_like(rows_in)
    greet(
        [(around(head, k, heads), blk) for k in range(1, heads)]
        + [(head, around(blk, k, blks)) for k in range(1, blks)]
    )
    lanes = lane_ids((rows, LANES))
    for copy in fetched:
        copy.wait()
    rows_in[0:experts, 0:rows] = wr_ref[...].astype(F32)
    rows_in[experts : experts + 1, 0:rows] = g2_ref[...].astype(F32)
    rows_in[experts + 1 : experts + 2, 0:rows] = g1_ref[...].astype(F32)
    vectors = jnp.transpose(rows_in[...])[:rows]
    gain = vectors[:, experts + 1 : experts + 2]

    def columns(which):
        start = pl.multiple_of(which * model + head * LANES, LANES)
        return w_ref[:, pl.ds(start, LANES)].astype(F32) * gain

    key_cols = columns(1)
    value_cols = pltpu.roll(columns(2), HALF, 1)
    wall[blk, :, 0:LANES] = jnp.where(lanes < HALF, key_cols, value_cols).astype(BF16)
    wall[blk, :, LANES : 2 * LANES] = jnp.where(lanes < HALF, value_cols, key_cols).astype(BF16)
    wall[blk, :, 2 * LANES : 3 * LANES] = (columns(0) * HS ** (-0.5)).astype(BF16)
    w_copies = [
        remote(wall.at[blk], wall.at[blk], w_send.at[k], w_recv.at[k], head, around(blk, k, blks))
        for k in range(1, blks)
    ]
    for copy in w_copies:
        copy.start()
    xhat, _ = centre(x_ref[...].astype(F32))
    xall[head] = xhat.astype(BF16)
    x_copies = [
        remote(xall.at[head], xall.at[head], x_send.at[k], x_recv.at[k], around(head, k, heads), blk)
        for k in range(1, heads)
    ]
    for copy in x_copies:
        copy.start()
    wo_own[:, model : model + LANES] = vectors.astype(BF16)
    wo_all[blk, head] = wo_own[pl.ds(pl.multiple_of(head * part, part), part), :]
    o_copies = [
        remote(
            wo_all.at[blk, head], wo_all.at[blk, head],
            o_send.at[k], o_recv.at[k], head, around(blk, k, blks),
        )
        for k in range(1, blks)
    ]
    for copy in o_copies:
        copy.start()
    for copy in x_copies:
        copy.wait()
    for copy in w_copies:
        copy.wait()
    weight = wall[...].reshape(model, 3 * LANES)
    tokens = x_ref.shape[0]
    even = y == 0
    for piece in range(heads):
        made = dot(xall[piece], weight).astype(BF16)
        first, second = made[:, 0:LANES], made[:, LANES : 2 * LANES]
        span = slice(piece * tokens, (piece + 1) * tokens)
        kvall[blk, span, :] = jnp.where(even, first, second)
        kv_other[span, :] = jnp.where(even, second, first)
        qall[y, span, :] = made[:, 2 * LANES : 3 * LANES]
    above, below = z < planes - 1, z > 0
    own = kvall.at[blk]

    def outward(slot, step, across):
        target = 2 * (z + step) + around(y, across, 2)
        return remote(kv_other if across else own, own, k_send.at[slot], k_recv.at[blk], head, target)

    def onward(slot, step, side):
        from_span = 2 * (z - step) + side
        ref = kvall.at[from_span]
        return remote(ref, ref, k_send.at[slot], k_recv.at[from_span], head, 2 * (z + step) + y)

    sides = ((1, above, below, 0), (-1, below, above, 2))
    for step, there, _, slot in sides:

        @pl.when(there)
        def _():
            outward(slot, step, 0).start()
            outward(slot + 1, step, 1).start()

    to_pair = outward(4, 0, 1)
    to_pair.start()
    q_pair = remote(qall.at[y], qall.at[y], k_send.at[5], q_recv, head, 2 * z + around(y, 1, 2))
    q_pair.start()
    for copy in o_copies:
        copy.wait()
    p_copies = [
        remote(
            wo_all.at[:, head], wo_all.at[:, head],
            p_send.at[k], p_recv.at[k], around(head, k, heads), blk,
        )
        for k in range(1, heads)
    ]
    for copy in p_copies:
        copy.start()
    for step, there, back, slot in sides:

        @pl.when(back)
        def _():
            for side in range(2):
                span = 2 * (z - step) + side
                arrived(kvall.at[span], k_recv.at[span])

        @pl.when(jnp.logical_and(there, back))
        def _():
            for side in range(2):
                onward(6 + slot + side, step, side).start()

    far = jnp.zeros(kv_other.shape, BF16)
    for other in range(planes):
        for side in range(2):
            span = 2 * other + side

            @pl.when(jnp.logical_or(z - other > 2, other - z > 2))
            def _():
                kvall[span] = far

            @pl.when(jnp.logical_or(z - other == 2, other - z == 2))
            def _():
                arrived(kvall.at[span], k_recv.at[span])

    pair = 2 * z + around(y, 1, 2)
    arrived(kvall.at[pair], k_recv.at[pair])
    q_pair.wait()
    for copy in p_copies:
        copy.wait()
    to_pair.wait_send()
    for step, there, back, slot in sides:

        @pl.when(there)
        def _():
            outward(slot, step, 0).wait_send()
            outward(slot + 1, step, 1).wait_send()

        @pl.when(jnp.logical_and(there, back))
        def _():
            for side in range(2):
                onward(6 + slot + side, step, side).wait_send()


def vmem_specs(count):
    return [pl.BlockSpec(memory_space=pltpu.VMEM)] * count


def hbm_specs(count):
    return [pl.BlockSpec(memory_space=pltpu.HBM)] * count


def in_hbm(*arrays):
    return [pltpu.with_memory_space_constraint(array, pltpu.HBM) for array in arrays]


def dma(*shape):
    return pltpu.SemaphoreType.DMA(shape)


def call_qkv(x, w_qkv, g1, w_out, w_router, g2, heads, blks):
    tokens, model = x.shape
    rows = w_qkv.shape[0]
    span = tokens * heads
    wide = model + LANES
    part = rows // heads
    return pl.pallas_call(
        functools.partial(qkv_kernel, heads, blks),
        out_shape=(
            jax.ShapeDtypeStruct((2, span, LANES), BF16),
            jax.ShapeDtypeStruct((blks, span, LANES), BF16),
            jax.ShapeDtypeStruct((heads, tokens, model), BF16),
            jax.ShapeDtypeStruct((blks, rows, 3 * LANES), BF16),
            jax.ShapeDtypeStruct((blks, heads, part, wide), BF16),
        ),
        in_specs=hbm_specs(6),
        out_specs=tuple(vmem_specs(5)),
        scratch_shapes=[
            pltpu.VMEM((tokens, model), BF16),
            pltpu.VMEM((rows, 3 * model), BF16),
            pltpu.VMEM((LANES, LANES), F32),
            pltpu.VMEM((1, rows), BF16),
            pltpu.VMEM((1, rows), BF16),
            pltpu.VMEM((w_router.shape[1], rows), BF16),
            pltpu.VMEM((rows, wide), BF16),
            pltpu.VMEM((span, LANES), BF16),
            dma(6),
            dma(heads), dma(heads), dma(blks), dma(blks), dma(blks), dma(blks), dma(heads), dma(heads),
            dma(10), dma(blks), pltpu.SemaphoreType.DMA,
        ],
        compiler_params=pltpu.CompilerParams(
            collective_id=1, has_side_effects=True, vmem_limit_bytes=16 * MIB
        ),
        name="qkv",
    )(*in_hbm(x, w_qkv, g1.reshape(1, rows), w_out, w_router.T, g2.reshape(1, rows)))


QUERY_TILE = 256
KEY_TILE = 512


def tile_docs(doc_ref, first, size):
    token = first + lane_ids((1, size))
    last = first + size - 1
    start = jnp.int32(0)
    low_row, high_row = jnp.zeros((1, size), jnp.int32), jnp.zeros((1, size), jnp.int32)
    low = low_last = high = jnp.int32(0)
    for index in range(doc_ref.shape[0]):
        end = start + doc_ref[index]
        low_row = jnp.where(token >= start, start, low_row)
        high_row = jnp.where(token >= start, end, high_row)
        low = jnp.where(first >= start, start, low)
        low_last = jnp.where(last >= start, start, low_last)
        high = jnp.where(last >= start, end, high)
        start = end
    return low_row, high_row, low, high, low == low_last


def key_columns(doc_ref, kv_ref, kvt, z, span):
    _, _, low, _, _ = tile_docs(doc_ref, z * span, LANES)
    _, _, _, high, _ = tile_docs(doc_ref, (z + 1) * span - LANES, LANES)
    for block in range(kv_ref.shape[0]):
        size = kv_ref.shape[1]

        @pl.when(jnp.logical_and(block * size < high, (block + 1) * size > low))
        def _():
            kvt[:, block * size : (block + 1) * size] = jnp.transpose(kv_ref[block])


def forward_kernel(doc_hbm, q_ref, kv_ref, o_out, ob_out, lse_out, kvt, doc_ref, doc_sem):
    _, _, z, y = place()
    pltpu.make_async_copy(doc_hbm, doc_ref, doc_sem).start()
    pltpu.make_async_copy(doc_hbm, doc_ref, doc_sem).wait()
    total = q_ref.shape[0] * q_ref.shape[1]
    key_columns(doc_ref, kv_ref, kvt, z, total)
    lanes = lane_ids((QUERY_TILE, LANES))
    tiles_per_span = q_ref.shape[1] // QUERY_TILE
    key_lanes = (lanes < HALF) == (y == 0)
    for tile in range(total // QUERY_TILE):
        inner = tile % tiles_per_span * QUERY_TILE
        query = q_ref[tile // tiles_per_span, inner : inner + QUERY_TILE, :]
        query = jnp.where(key_lanes, query, jnp.zeros_like(query))
        low_row, high_row, low, high, single = tile_docs(
            doc_ref, z * total + tile * QUERY_TILE, QUERY_TILE
        )

        def step(block, carry, query=query, low_row=low_row, high_row=high_row):
            biggest, weight, mixed = carry
            first = pl.multiple_of(block * KEY_TILE, KEY_TILE)
            scores = dot(kv_ref[block], query, (1, 1))
            key = first + lax.broadcasted_iota(jnp.int32, scores.shape, 0)
            inside = jnp.logical_and(key >= low_row, key < high_row)
            scores = jnp.where(inside, scores, MASKED)
            bigger = jnp.maximum(biggest, jnp.max(scores, axis=0, keepdims=True))
            fade = jnp.exp(biggest - bigger)
            terms = jnp.where(inside, jnp.exp(scores - bigger), 0.0)
            weight = weight * fade + jnp.sum(terms, axis=0, keepdims=True)
            mixed = mixed * fade + dot(kvt[:, pl.ds(first, KEY_TILE)], terms.astype(BF16))
            return bigger, weight, mixed

        biggest, weight, mixed = lax.fori_loop(
            low // KEY_TILE,
            (high + KEY_TILE - 1) // KEY_TILE,
            step,
            (
                jnp.full((1, QUERY_TILE), MASKED, F32),
                jnp.zeros((1, QUERY_TILE), F32),
                jnp.zeros((LANES, QUERY_TILE), F32),
            ),
        )
        result = jnp.transpose(mixed / weight)
        o_out[tile] = result
        ob_out[tile] = result.astype(BF16)
        lse_out[tile] = jnp.broadcast_to(biggest + jnp.log(weight), (8, QUERY_TILE))


def call_forward(doc_lengths, q, kv):
    blks, span, _ = kv.shape
    tiles = 2 * span // QUERY_TILE
    return pl.pallas_call(
        forward_kernel,
        out_shape=(
            jax.ShapeDtypeStruct((tiles, QUERY_TILE, LANES), F32),
            jax.ShapeDtypeStruct((tiles, QUERY_TILE, LANES), BF16),
            jax.ShapeDtypeStruct((tiles, 8, QUERY_TILE), F32),
        ),
        in_specs=hbm_specs(1) + vmem_specs(2),
        out_specs=tuple(vmem_specs(3)),
        scratch_shapes=[
            pltpu.VMEM((LANES, blks * span), BF16),
            pltpu.SMEM(doc_lengths.shape, jnp.int32),
            pltpu.SemaphoreType.DMA,
        ],
        compiler_params=pltpu.CompilerParams(vmem_limit_bytes=16 * MIB),
        name="attend",
    )(*in_hbm(doc_lengths), q, kv)


def backward_kernel(
    doc_hbm, q_ref, kv_ref, do_ref, o_ref, lse_ref, dq_out, dkv_out, kvt, dkv, doc_ref, doc_sem
):
    _, _, z, y = place()
    pltpu.make_async_copy(doc_hbm, doc_ref, doc_sem).start()
    pltpu.make_async_copy(doc_hbm, doc_ref, doc_sem).wait()
    total = q_ref.shape[0] * q_ref.shape[1]
    key_columns(doc_ref, kv_ref, kvt, z, total)
    dkv[...] = jnp.zeros_like(dkv)
    lanes = lane_ids((QUERY_TILE, LANES))
    tiles_per_span = q_ref.shape[1] // QUERY_TILE
    key_lanes = (lanes < HALF) == (y == 0)
    for tile in range(total // QUERY_TILE):
        inner = tile % tiles_per_span * QUERY_TILE
        query = q_ref[tile // tiles_per_span, inner : inner + QUERY_TILE, :]
        query = jnp.where(key_lanes, query, jnp.zeros_like(query))
        out_grad = do_ref[tile]
        out_grad = jnp.where(key_lanes, jnp.zeros_like(out_grad), out_grad)
        delta = jnp.sum(
            jnp.transpose(out_grad.astype(F32) * o_ref[tile]), axis=0, keepdims=True
        )
        log_total = lse_ref[tile, 0:1, :]
        low_row, high_row, low, high, single = tile_docs(
            doc_ref, z * total + tile * QUERY_TILE, QUERY_TILE
        )

        def step(
            block, mixed, query=query, out_grad=out_grad, delta=delta, log_total=log_total,
            low_row=low_row, high_row=high_row,
        ):
            first = pl.multiple_of(block * KEY_TILE, KEY_TILE)
            scores = dot(kv_ref[block], query, (1, 1))
            key = first + lax.broadcasted_iota(jnp.int32, scores.shape, 0)
            inside = jnp.logical_and(key >= low_row, key < high_row)
            weights = jnp.where(inside, jnp.exp(scores - log_total), 0.0)
            weight_grads = dot(kv_ref[block], out_grad, (1, 1))
            score_grads = (weights * (weight_grads - delta)).astype(BF16)
            dkv[block] += dot(score_grads, query) + dot(weights.astype(BF16), out_grad)
            return mixed + dot(kvt[:, pl.ds(first, KEY_TILE)], score_grads)

        mixed = lax.fori_loop(
            low // KEY_TILE,
            (high + KEY_TILE - 1) // KEY_TILE,
            step,
            jnp.zeros((LANES, QUERY_TILE), F32),
        )
        dq_out[tile] = jnp.transpose(mixed).astype(BF16)
    for block in range(dkv.shape[0]):
        dkv_out[block] = dkv[block].astype(BF16)


def call_backward(doc_lengths, q, kv, d_o, o, lse):
    blks, span, _ = kv.shape
    tiles = 2 * span // QUERY_TILE
    return pl.pallas_call(
        backward_kernel,
        out_shape=(
            jax.ShapeDtypeStruct((tiles, QUERY_TILE, LANES), BF16),
            jax.ShapeDtypeStruct((blks, span, LANES), BF16),
        ),
        in_specs=hbm_specs(1) + vmem_specs(5),
        out_specs=tuple(vmem_specs(2)),
        scratch_shapes=[
            pltpu.VMEM((LANES, blks * span), BF16),
            pltpu.VMEM((blks, span, LANES), F32),
            pltpu.SMEM(doc_lengths.shape, jnp.int32),
            pltpu.SemaphoreType.DMA,
        ],
        compiler_params=pltpu.CompilerParams(vmem_limit_bytes=16 * MIB),
        name="attend_back",
    )(*in_hbm(doc_lengths), q, kv, d_o.reshape(tiles, QUERY_TILE, LANES), o, lse)


def gelu_parts(values):
    share = 0.5 * (1.0 + lax.erf(values * (2.0**-0.5)))
    slope = share + values * jnp.exp(-0.5 * values * values) * (2.0 * math.pi) ** -0.5
    return values * share, slope


def positions(expert_rows, expert_cols, rank_row, rank_col):
    def count(mask, axis):
        return jnp.sum(mask.astype(F32), axis=axis, keepdims=True)

    row = [None, None]
    col = [None, None]
    before = rank_col < rank_row
    after = rank_row < rank_col
    for choice in range(2):
        row[choice] = count((expert_cols[choice] == expert_rows[choice]) & before, 0)
        col[choice] = count((expert_rows[choice] == expert_cols[choice]) & after, 1)
    row[1] = row[1] + count(expert_cols[0] == expert_rows[1], 0)
    col[1] = col[1] + count(expert_rows[0] == expert_cols[1], 1)
    return row, col


def middle_kernel(
    heads, blks,
    x_hbm, o_ref, wo_ref, routes_hbm, rank_hbm, d_out_hbm, win_hbm, wout_hbm,
    out_ref, dh_ref, dma_all, grads_ref, rx,
    x_ref, routes_ref, rank_ref, d_out_ref, win_ref, wout_ref, rows_in, in_sem,
    o_all, dos, doa, rs, ra, po, pa, dr, da, dms, acc_out, acc_row, mix,
    o_send, o_recv, dos_send, dos_recv, r_send, r_recv, po_send, po_recv,
    dr_send, dr_recv, dm_send, dm_recv, rx_send, rx_recv,
):
    head, blk, z, y = place()
    tokens, model = x_ref.shape
    capacity = 2 * tokens // blks
    slots = capacity * blks
    plane = [(k % heads, k // heads) for k in range(1, 2 * heads)]
    wanted = (
        (routes_hbm, routes_ref), (rank_hbm, rank_ref), (d_out_hbm, d_out_ref), (x_hbm, x_ref),
        (win_hbm, win_ref), (wout_hbm, wout_ref),
    )
    fetched = [
        pltpu.make_async_copy(src, dst, in_sem.at[i]) for i, (src, dst) in enumerate(wanted)
    ]
    for copy in fetched:
        copy.start()
    greet(
        [(around(head, kh, heads), 2 * z + around(y, ky, 2)) for kh, ky in plane]
        + [(head, around(blk, k, blks)) for k in range(1, blks)]
    )

    def plane_copies(src_of, dst, send, recv):
        copies = []
        for k, (kh, ky) in enumerate(plane):
            to_head, to_y = around(head, kh, heads), around(y, ky, 2)
            copies.append(
                remote(src_of(to_y, to_head), dst, send.at[k], recv.at[k], to_head, 2 * z + to_y)
            )
        return copies

    def blk_copies(src, dst, send, recv):
        return [
            remote(
                src.at[around(blk, k, blks)], dst.at[blk],
                send.at[k], recv.at[k], head, around(blk, k, blks),
            )
            for k in range(1, blks)
        ]

    def start(copies):
        for copy in copies:
            copy.start()

    def finish(copies):
        for copy in copies:
            copy.wait()

    o_copies = plane_copies(lambda to_y, to_head: o_ref.at[to_y, to_head], o_all.at[y, head], o_send, o_recv)
    start(o_copies)
    o_all[y, head] = o_ref[y, head]

    lanes = lane_ids((tokens, LANES))
    for copy in fetched[:4]:
        copy.wait()
    e_rows = [routes_ref[i : i + 1, :].astype(F32) for i in range(2)]
    rank_row = rank_ref[...].astype(F32)
    rows_in[...] = jnp.zeros_like(rows_in)
    rows_in[0:1, :], rows_in[1:2, :], rows_in[2:3, :] = *e_rows, rank_row
    columns = jnp.transpose(rows_in[...])
    e_cols = [columns[:, 0:1], columns[:, 1:2]]
    rank_col = columns[:, 2:3]
    pos_rows, pos_cols = positions(e_rows, e_cols, rank_row, rank_col)

    def slot_of(expert, position):
        return jnp.where(position < capacity, expert * capacity + position, -1.0).astype(jnp.int32)

    slot_rows = [slot_of(e, p) for e, p in zip(e_rows, pos_rows)]
    slot_cols = [slot_of(e, p) for e, p in zip(e_cols, pos_cols)]
    slot_down = lax.broadcasted_iota(jnp.int32, (slots, tokens), 0)
    slot_across = lane_ids((tokens, slots))
    pick = [(slot_down == s).astype(BF16) for s in slot_rows]
    put = [(slot_across == s).astype(BF16) for s in slot_cols]
    pick_any = pick[0] + pick[1]
    put_any = put[0] + put[1]

    d_out = d_out_ref[...]
    dos[...] = dot(pick_any, d_out.astype(BF16)).astype(BF16).reshape(dos.shape)
    dos_copies = blk_copies(dos, doa, dos_send, dos_recv)
    start(dos_copies)
    doa[blk] = dos[blk]

    weight_out = jnp.concatenate(
        [wo_ref[(b ^ 1) * HALF : ((b ^ 1) + 1) * HALF, 0:model] for b in range(blks)], axis=0
    )
    small = wo_ref[:, model : model + LANES]
    small_across = jnp.concatenate(
        [
            jnp.transpose(small[i * LANES : (i + 1) * LANES].astype(F32))
            for i in range(model // LANES)
        ],
        axis=1,
    )
    gain = small_across[blks : blks + 1, :]

    finish(o_copies)
    for piece in range(heads):
        mix[:, piece * LANES : (piece + 1) * LANES] = jnp.where(
            lanes < HALF, o_all[1, piece], o_all[0, piece]
        )
    mixed = mix[...]
    hidden = x_ref[...].astype(F32) + dot(mixed, weight_out)
    xhat, scale = centre(hidden)
    routed = (xhat * gain).astype(BF16)
    logits = jnp.where(lanes < blks, dot(routed, small), MASKED)
    powers = jnp.exp(logits - jnp.max(logits, axis=1, keepdims=True))
    probs = powers / jnp.sum(powers, axis=1, keepdims=True)
    lanes_f = lanes.astype(F32)
    hots = [lanes_f == e for e in e_cols]
    gates = [jnp.sum(jnp.where(hot, probs, 0.0), axis=1, keepdims=True) for hot in hots]
    gate_mats = [split_high_low(g, lanes) for g in gates]

    rs[:, :, 0:model] = dot(pick_any, routed).astype(BF16).reshape(blks, capacity, model)
    rs[:, :, model : model + LANES] = (
        (dot(pick[0], gate_mats[0]) + dot(pick[1], gate_mats[1]))
        .astype(BF16)
        .reshape(blks, capacity, LANES)
    )
    r_copies = blk_copies(rs, ra, r_send, r_recv)
    start(r_copies)
    ra[blk] = rs[blk]
    acc_out[...] = jnp.zeros_like(acc_out)
    acc_row[...] = jnp.zeros_like(acc_row)
    finish(dos_copies)
    finish(r_copies)

    arrived_rows = ra[...].reshape(slots, model + LANES)
    out_rows = doa[...].reshape(slots, model)
    gate_col = join_high_low(arrived_rows, model)
    rx[head, :, 0:model] = arrived_rows[:, 0:model]
    rx[head, :, model : 2 * model] = (out_rows.astype(F32) * gate_col).astype(BF16)
    half_ff = wout_ref.shape[0] // 4
    for copy in fetched[4:]:
        copy.wait()

    @pl.loop(0, 4)
    def _(chunk):
        first = pl.multiple_of(chunk * half_ff, half_ff)
        into = win_ref[:, pl.ds(first, half_ff)]
        outof = wout_ref[pl.ds(first, half_ff), :]
        act, slope = gelu_parts(dot(rx[head, :, 0:model], into))
        acc_out[...] += dot(act.astype(BF16), outof)
        d_act = dot(rx[head, :, model : 2 * model], outof, (1, 1))
        acc_row[...] += dot((slope * d_act).astype(BF16), into, (1, 1))

    result = acc_out[...].astype(BF16)
    d_gate = jnp.sum(out_rows.astype(F32) * result.astype(F32), axis=1, keepdims=True)
    dr[:, :, 0:model] = acc_row[...].astype(BF16).reshape(blks, capacity, model)
    dr[:, :, model : model + LANES] = split_high_low(d_gate, lane_ids((slots, LANES))).reshape(
        blks, capacity, LANES
    )
    dr_copies = blk_copies(dr, da, dr_send, dr_recv)
    start(dr_copies)
    da[blk] = dr[blk]
    po[...] = result.reshape(blks, capacity, model)
    po_copies = blk_copies(po, pa, po_send, po_recv)
    pa[blk] = po[blk]
    core = lax.rem(head, 2)
    sibling, across = head - core + 1 - core, around(head, 2, heads)
    to_sibling = remote(rx.at[head], rx.at[head], rx_send.at[0], rx_recv.at[0], sibling, blk)
    to_across = remote(rx.at[head], rx.at[head], rx_send.at[1], rx_recv.at[1], across, blk)
    to_across.start()
    to_sibling.start()

    finish(dr_copies)
    start(po_copies)
    back = da[...].reshape(slots, model + LANES)
    d_routed = dot(put_any, back[:, 0:model])
    back_gate = back[:, model : model + LANES]
    d_gates = [join_high_low(dot(p, back_gate), 0) for p in put]
    d_probs = jnp.where(hots[0], d_gates[0], 0.0) + jnp.where(hots[1], d_gates[1], 0.0)
    d_logits = probs * (d_probs - jnp.sum(probs * d_probs, axis=1, keepdims=True))
    d_high = d_logits.astype(BF16)
    d_low = (d_logits - d_high.astype(F32)).astype(BF16)
    d_routed = d_routed + dot(d_high, small, (1, 1)) + dot(d_low, small, (1, 1))
    d_hidden = d_out + centre_back(d_routed * gain, xhat, scale)
    dh_ref[...] = d_hidden
    d_attn = d_hidden.astype(BF16)
    d_mixed = dot(d_attn, weight_out, (1, 1)).astype(BF16)
    for piece in range(heads):
        dms[piece] = d_mixed[:, piece * LANES : (piece + 1) * LANES]
    dm_copies = plane_copies(lambda to_y, to_head: dms.at[to_head], dma_all.at[y, head], dm_send, dm_recv)
    start(dm_copies)
    dma_all[y, head] = dms[head]

    d_weight = dot(mixed, d_attn, (0, 0)).astype(BF16)
    for b in range(blks):
        grads_ref[b, :, 0:model] = d_weight[(b ^ 1) * HALF : ((b ^ 1) + 1) * HALF, :]
    last = (lanes == blks).astype(BF16)
    d_small = dot(routed, d_high, (0, 0)) + dot((d_routed * xhat).astype(BF16), last, (0, 0))
    grads_ref[:, :, model : model + LANES] = d_small.astype(BF16).reshape(blks, HALF, LANES)
    finish(po_copies)
    parts = pa[...].reshape(slots, model)
    mixture = gates[0] * dot(put[0], parts) + gates[1] * dot(put[1], parts)
    out_ref[...] = (hidden + mixture).astype(BF16)

    arrived(rx.at[across], rx_recv.at[1])
    forward = remote(rx.at[across], rx.at[across], rx_send.at[2], rx_recv.at[2], sibling, blk)
    forward.start()
    finish(dm_copies)
    to_sibling.wait()
    to_across.wait_send()
    forward.wait()


def call_middle(x, o, wo, routes, rank, d_out, win, wout, heads, blks):
    tokens, model = x.shape
    capacity = 2 * tokens // blks
    slots = capacity * blks
    wide = model + LANES

    def rows(width):
        return pltpu.VMEM((blks, capacity, width), BF16)

    def block(*lead):
        return pltpu.VMEM((*lead, tokens, LANES), BF16)

    return pl.pallas_call(
        functools.partial(middle_kernel, heads, blks),
        out_shape=(
            jax.ShapeDtypeStruct((tokens, model), BF16),
            jax.ShapeDtypeStruct((tokens, model), F32),
            jax.ShapeDtypeStruct((2, heads, tokens, LANES), BF16),
            jax.ShapeDtypeStruct((blks, model // blks, wide), BF16),
            jax.ShapeDtypeStruct((heads, slots, 2 * model), BF16),
        ),
        in_specs=hbm_specs(1) + vmem_specs(2) + hbm_specs(5),
        out_specs=tuple(vmem_specs(5)),
        scratch_shapes=[
            pltpu.VMEM((tokens, model), BF16),
            pltpu.VMEM((2, tokens), jnp.int32),
            pltpu.VMEM((1, tokens), jnp.int32),
            pltpu.VMEM((tokens, model), F32),
            pltpu.VMEM(win.shape, BF16),
            pltpu.VMEM(wout.shape, BF16),
            pltpu.VMEM((tokens, tokens), F32),
            dma(6),
            block(2, heads), rows(model), rows(model), rows(wide), rows(wide), rows(model), rows(model),
            rows(wide), rows(wide), block(heads),
            pltpu.VMEM((slots, model), F32), pltpu.VMEM((slots, model), F32),
            pltpu.VMEM((tokens, model), BF16),
            dma(2 * heads), dma(2 * heads), dma(blks), dma(blks), dma(blks), dma(blks), dma(blks), dma(blks),
            dma(blks), dma(blks), dma(2 * heads), dma(2 * heads), dma(3), dma(3),
        ],
        compiler_params=pltpu.CompilerParams(
            collective_id=2, has_side_effects=True, vmem_limit_bytes=20 * MIB
        ),
        name="experts",
    )(*in_hbm(x), o, wo, *in_hbm(routes.T, rank, d_out, win, wout))


def last_kernel(
    heads, blks,
    x_hbm, dh_ref, dq_ref, dkv_ref, xa_ref, wa_ref, w_hbm, g1_hbm, grads_ref, rx_ref, win_hbm, wout_hbm,
    dx_ref, dw_ref, shared_ref, din_ref, dout_ref,
    x_ref, w_ref, g1_ref, win_ref, wout_ref, in_sem,
    gain_tile, far_all, near_send_buf, near_all, pair_all, dq_all, us, ua, gs, ga, gh, w1, w2s, w2, w3,
    q_send, q_recv, pair_send, pair_recv, far_send, far_recv, near_send, near_recv,
    u_send, u_recv, g_send, g_recv, gh_send, gh_recv, w1_send, w1_recv, w2_send, w2_recv,
    w3_send, w3_recv, e_send, e_recv,
):
    head, blk, z, y = place()
    planes = blks // 2
    tokens, model = x_ref.shape
    rows = w_ref.shape[0]
    wanted = (
        (win_hbm, win_ref), (wout_hbm, wout_ref), (x_hbm, x_ref), (w_hbm, w_ref), (g1_hbm, g1_ref)
    )
    fetched = [
        pltpu.make_async_copy(src, dst, in_sem.at[i]) for i, (src, dst) in enumerate(wanted)
    ]
    for copy in fetched:
        copy.start()
    greet(
        [(around(head, k, heads), blk) for k in range(1, heads)]
        + [(head, around(blk, k, blks)) for k in range(1, blks)]
    )

    def start(copies):
        for copy in copies:
            copy.start()

    def finish(copies):
        for copy in copies:
            copy.wait()

    other_y = around(y, 1, 2)
    pair = 2 * z + other_y
    above, below = z < planes - 1, z > 0
    directions = ((1, above, below, 0), (-1, below, above, 2))

    def far_copy(step, slot, side):
        span = 2 * (z + 2 * step) + side
        return remote(
            dkv_ref.at[span], far_all.at[slot + side],
            far_send.at[slot + side], far_recv.at[slot + side], head, 2 * (z + step) + y,
        )

    def near_copy(step, slot, side):
        return remote(
            near_send_buf.at[slot + side], near_all.at[slot // 2, y],
            near_send.at[slot + side], near_recv.at[slot // 2, y], head, 2 * (z + step) + side,
        )

    def two_away(step):
        return z + 2 * step < planes if step > 0 else z + 2 * step >= 0

    for step, there, back, slot in directions:

        @pl.when(two_away(step))
        def _():
            for side in range(2):
                far_copy(step, slot, side).start()

    pair_copy = remote(dkv_ref.at[pair], pair_all, pair_send, pair_recv, head, pair)
    pair_copy.start()
    q_copy = remote(dq_ref.at[other_y], dq_all, q_send, q_recv, head, pair)
    q_copy.start()
    w1_copies = [
        remote(
            grads_ref.at[:, around(head, k, heads)], w1.at[head],
            w1_send.at[k], w1_recv.at[k], around(head, k, heads), blk,
        )
        for k in range(1, heads)
    ]
    start(w1_copies)
    w1[head] = grads_ref[:, head]

    core = lax.rem(head, 2)
    sibling = head - core + 1 - core
    ff_half = wout_ref.shape[0] // 2
    ff_step = ff_half // 4

    def expert_chunk(chunk):
        here = pl.multiple_of(core * ff_half + chunk * ff_step, ff_step)
        there = pl.multiple_of(chunk * ff_step, ff_step)
        into = win_ref[:, pl.ds(here, ff_step)]
        outof = wout_ref[pl.ds(here, ff_step), :]
        d_in = jnp.zeros((model, ff_step), F32)
        d_out = jnp.zeros((ff_step, model), F32)
        for source in range(heads):
            rows_in = rx_ref[source, :, 0:model]
            grads_out = rx_ref[source, :, model : 2 * model]
            act, slope = gelu_parts(dot(rows_in, into))
            d_act = dot(grads_out, outof, (1, 1))
            d_in = d_in + dot(rows_in, (slope * d_act).astype(BF16), (0, 0))
            d_out = d_out + dot(act.astype(BF16), grads_out, (0, 0))
        din_ref[core, :, pl.ds(there, ff_step)] = d_in.astype(BF16)
        dout_ref[core, pl.ds(there, ff_step), :] = d_out.astype(BF16)

    finish(fetched)

    @pl.loop(0, 2)
    def _(chunk):
        expert_chunk(chunk)

    for step, there, back, slot in directions:

        @pl.when(there)
        def _():
            for side in range(2):
                near_send_buf[slot + side] = dkv_ref[2 * (z + step) + side]

        @pl.when(jnp.logical_and(there, back))
        def _():
            for side in range(2):
                arrived(far_all.at[slot + side], far_recv.at[slot + side])
                near_send_buf[slot + side] = (
                    near_send_buf[slot + side].astype(F32) + far_all[slot + side].astype(F32)
                ).astype(BF16)

        @pl.when(there)
        def _():
            for side in range(2):
                near_copy(step, slot, side).start()

    @pl.loop(2, 4)
    def _(chunk):
        expert_chunk(chunk)

    e_copies = [
        remote(din_ref.at[core], din_ref.at[core], e_send.at[0], e_recv.at[0], sibling, blk),
        remote(dout_ref.at[core], dout_ref.at[core], e_send.at[1], e_recv.at[1], sibling, blk),
    ]
    start(e_copies)

    pair_copy.wait()
    q_copy.wait()
    for step, there, back, slot in directions:

        @pl.when(back)
        def _():
            for side in range(2):
                arrived(near_all.at[slot // 2, side], near_recv.at[slot // 2, side])

        @pl.when(jnp.logical_not(back))
        def _():
            near_all[slot // 2] = jnp.zeros(near_all.shape[1:], BF16)

    lanes = lane_ids((tokens, LANES))
    even = y == 0
    weight = wa_ref[...].reshape(model, 3 * LANES)
    g_sum = jnp.zeros((model, 3 * LANES), F32)
    for piece in range(heads):
        span = slice(piece * tokens, (piece + 1) * tokens)
        own = dkv_ref[blk, span, :].astype(F32)
        other = pair_all[span, :].astype(F32)
        kv_grads = [
            jnp.where(even, own, other) + near_all[0, 0, span, :].astype(F32) + near_all[1, 0, span, :].astype(F32),
            jnp.where(even, other, own) + near_all[0, 1, span, :].astype(F32) + near_all[1, 1, span, :].astype(F32),
        ]
        q_own = dq_ref[y, span, :]
        q_other = dq_all[span, :]
        own_lanes = (lanes < HALF) == even
        q_grads = jnp.where(own_lanes, q_own, q_other)
        made = jnp.concatenate([kv_grads[0].astype(BF16), kv_grads[1].astype(BF16), q_grads], axis=1)
        us[piece] = dot(made, weight, (1, 1)).astype(BF16)
        g_sum = g_sum + dot(xa_ref[piece], made, (0, 0))
    u_copies = [
        remote(
            us.at[around(head, k, heads)], ua.at[head],
            u_send.at[k], u_recv.at[k], around(head, k, heads), blk,
        )
        for k in range(1, heads)
    ]
    start(u_copies)
    ua[head] = us[head]
    gs[...] = g_sum.astype(BF16).reshape(gs.shape)
    g_copies = [
        remote(
            gs.at[around(blk, k, blks)], ga.at[blk],
            g_send.at[k], g_recv.at[k], head, around(blk, k, blks),
        )
        for k in range(1, blks)
    ]
    start(g_copies)
    ga[blk] = gs[blk]

    finish(w1_copies)
    summed = w1[0].astype(F32)
    for source in range(1, heads):
        summed = summed + w1[source].astype(F32)
    w2s[...] = summed.astype(BF16)
    w2_copies = [
        remote(
            w2s.at[around(blk, k, blks)], w2.at[blk],
            w2_send.at[k], w2_recv.at[k], head, around(blk, k, blks),
        )
        for k in range(1, blks)
    ]
    start(w2_copies)
    w2[blk] = w2s[blk]

    finish(u_copies)
    grad = ua[0].astype(F32)
    for source in range(1, heads):
        grad = grad + ua[source].astype(F32)
    xhat, scale = centre(x_ref[...].astype(F32))
    dx_ref[...] = dh_ref[...] + centre_back(grad, xhat, scale)

    finish(g_copies)
    total = ga[0].astype(F32)
    for source in range(1, blks):
        total = total + ga[source].astype(F32)
    gh[head] = total.astype(BF16)
    gh_copies = [
        remote(gh.at[head], gh.at[head], gh_send.at[k], gh_recv.at[k], around(head, k, heads), blk)
        for k in range(1, heads)
    ]
    start(gh_copies)
    finish(w2_copies)
    part = w2[0].astype(F32)
    for source in range(1, blks):
        part = part + w2[source].astype(F32)
    w3[head] = part.astype(BF16)
    w3_copies = [
        remote(w3.at[head], w3.at[head], w3_send.at[k], w3_recv.at[k], around(head, k, heads), blk)
        for k in range(1, heads)
    ]
    start(w3_copies)

    gain_tile[...] = jnp.zeros_like(gain_tile)
    gain_tile[0:1, 0:rows] = g1_ref[...].astype(F32)
    gain = jnp.transpose(jnp.broadcast_to(gain_tile[0:1, :], (LANES, LANES)))[:rows]
    low_half = lane_ids((rows, LANES)) < HALF
    finish(gh_copies)
    d_gain = jnp.zeros((rows, LANES), F32)
    for source in range(heads):
        both = [gh[source, :, i * LANES : (i + 1) * LANES].astype(F32) for i in range(3)]
        grads = (
            both[2] * HS ** (-0.5),
            jnp.where(low_half, both[0], both[1]),
            pltpu.roll(jnp.where(low_half, both[1], both[0]), HALF, 1),
        )
        for which, value in enumerate(grads):
            columns = slice(which * model + source * LANES, which * model + (source + 1) * LANES)
            d_gain = d_gain + value * w_ref[:, columns].astype(F32)
            dw_ref[:, columns] = value * gain
    finish(w3_copies)
    shared = w3[...].reshape(rows, w3.shape[-1]).astype(F32)
    shared_ref[:, 0:model] = shared[:, 0:model]
    gain_col = jnp.sum(d_gain, axis=1, keepdims=True)
    shared_ref[:, model : model + LANES] = jnp.where(
        lane_ids((rows, LANES)) == blks + 1, gain_col, shared[:, model : model + LANES]
    )
    for step, there, back, slot in directions:

        @pl.when(two_away(step))
        def _():
            for side in range(2):
                far_copy(step, slot, side).wait_send()

        @pl.when(there)
        def _():
            for side in range(2):
                near_copy(step, slot, side).wait_send()

    finish(e_copies)


def call_last(x, dh, dq, dkv, xa, wa, w_qkv, g1, grads, rx, win, wout, heads, blks):
    tokens, model = x.shape
    span = tokens * heads
    rows = w_qkv.shape[0]
    wide = model + LANES
    part = rows // heads
    ff = wout.shape[0]

    def block(*lead):
        return pltpu.VMEM((*lead, span, LANES), BF16)

    return pl.pallas_call(
        functools.partial(last_kernel, heads, blks),
        out_shape=(
            jax.ShapeDtypeStruct((tokens, model), F32),
            jax.ShapeDtypeStruct((rows, 3 * model), F32),
            jax.ShapeDtypeStruct((rows, wide), F32),
            jax.ShapeDtypeStruct((2, model, ff // 2), BF16),
            jax.ShapeDtypeStruct((2, ff // 2, model), BF16),
        ),
        in_specs=hbm_specs(1) + vmem_specs(5) + hbm_specs(2) + vmem_specs(2) + hbm_specs(2),
        out_specs=tuple(vmem_specs(5)),
        scratch_shapes=[
            pltpu.VMEM((tokens, model), BF16),
            pltpu.VMEM((rows, 3 * model), BF16),
            pltpu.VMEM((1, rows), BF16),
            pltpu.VMEM(win.shape, BF16),
            pltpu.VMEM(wout.shape, BF16),
            dma(5),
            pltpu.VMEM((8, LANES), F32),
            block(4), block(4), block(2, 2), block(), block(),
            pltpu.VMEM((heads, tokens, model), BF16), pltpu.VMEM((heads, tokens, model), BF16),
            pltpu.VMEM((blks, rows, 3 * LANES), BF16), pltpu.VMEM((blks, rows, 3 * LANES), BF16),
            pltpu.VMEM((heads, rows, 3 * LANES), BF16),
            pltpu.VMEM((heads, blks, part, wide), BF16), pltpu.VMEM((blks, part, wide), BF16),
            pltpu.VMEM((blks, part, wide), BF16), pltpu.VMEM((heads, part, wide), BF16),
            pltpu.SemaphoreType.DMA, pltpu.SemaphoreType.DMA, pltpu.SemaphoreType.DMA, pltpu.SemaphoreType.DMA,
            dma(4), dma(4), dma(4), dma(2, 2),
            dma(heads), dma(heads), dma(blks), dma(blks), dma(heads), dma(heads), dma(heads), dma(heads),
            dma(blks), dma(blks), dma(heads), dma(heads), dma(2), dma(2),
        ],
        compiler_params=pltpu.CompilerParams(
            collective_id=3, has_side_effects=True, vmem_limit_bytes=24 * MIB
        ),
        name="last",
    )(
        *in_hbm(x), dh, dq.reshape(2, span, LANES), dkv, xa, wa, *in_hbm(w_qkv, g1.reshape(1, rows)),
        grads.reshape(blks, heads, part, wide), rx, *in_hbm(win, wout),
    )


def finish_kernel(
    experts,
    dx_ref, dw_ref, shared_ref, din_ref, dout_ref,
    dx_out, g1_out, dw_out, dwo_out, g2_out, wr_out, din_out, dout_out,
    tile, wr, g2, g1, din, dout, sem, wide_sem,
):
    rows = shared_ref.shape[0]
    model = dx_ref.shape[1]
    copies = [
        pltpu.make_async_copy(dx_ref, dx_out, sem.at[0]),
        pltpu.make_async_copy(dw_ref, dw_out, sem.at[1]),
        pltpu.make_async_copy(shared_ref.at[:, pl.ds(0, model)], dwo_out, sem.at[2]),
    ]
    for copy in copies:
        copy.start()
    half = dout_ref.shape[1]
    quarter = half // 2
    for piece in range(4):
        down = slice(piece * quarter, (piece + 1) * quarter)
        dout[down, :] = dout_ref[piece // 2, (piece % 2) * quarter : (piece % 2 + 1) * quarter, :].astype(F32)
        copies.append(pltpu.make_async_copy(dout.at[down], dout_out.at[down], wide_sem.at[piece]))
        copies[-1].start()
    step = model // 4
    for piece in range(4):
        down = slice(piece * step, (piece + 1) * step)
        for side in range(2):
            din[down, side * half : (side + 1) * half] = din_ref[side, down, :].astype(F32)
        copies.append(pltpu.make_async_copy(din.at[down], din_out.at[down], wide_sem.at[4 + piece]))
        copies[-1].start()
    tile[...] = jnp.zeros_like(tile)
    tile[0:rows, :] = shared_ref[:, model : model + LANES]
    across = jnp.transpose(tile[...])[:, 0:rows]
    wr[...] = across[0:experts]
    g2[...] = across[experts : experts + 1]
    g1[...] = across[experts + 1 : experts + 2]
    for index, (src, dst) in enumerate(((wr, wr_out), (g2, g2_out), (g1, g1_out))):
        copies.append(pltpu.make_async_copy(src, dst, sem.at[3 + index]))
        copies[-1].start()
    for copy in copies:
        copy.wait()


def call_finish(dx, dw, shared, d_in, d_out):
    rows = shared.shape[0]
    model = dx.shape[1]
    experts = model // rows
    ff = 2 * d_out.shape[1]
    return pl.pallas_call(
        functools.partial(finish_kernel, experts),
        out_shape=(
            jax.ShapeDtypeStruct(dx.shape, F32),
            jax.ShapeDtypeStruct((1, rows), F32),
            jax.ShapeDtypeStruct(dw.shape, F32),
            jax.ShapeDtypeStruct((rows, model), F32),
            jax.ShapeDtypeStruct((1, rows), F32),
            jax.ShapeDtypeStruct((experts, rows), F32),
            jax.ShapeDtypeStruct((model, ff), F32),
            jax.ShapeDtypeStruct((ff, model), F32),
        ),
        in_specs=vmem_specs(5),
        out_specs=tuple(hbm_specs(8)),
        scratch_shapes=[
            pltpu.VMEM((LANES, LANES), F32),
            pltpu.VMEM((experts, rows), F32),
            pltpu.VMEM((1, rows), F32),
            pltpu.VMEM((1, rows), F32),
            pltpu.VMEM((model, ff), F32),
            pltpu.VMEM((ff, model), F32),
            dma(6),
            dma(8),
        ],
        compiler_params=pltpu.CompilerParams(vmem_limit_bytes=16 * MIB),
        name="finish",
    )(dx, dw, shared, d_in, d_out)


def local_kernels(
    inputs, ln1_gain, w_qkv, w_out, ln2_gain, w_router,
    expert_in, expert_out, routes, priority, doc_lengths, d_out,
):
    heads, blks = lax.axis_size("head"), lax.axis_size("blk")
    model = inputs.shape[1]
    tokens = inputs.shape[0]
    win, wout = expert_in[0], expert_out[0]
    q, kv, xa, wa, wo = call_qkv(inputs, w_qkv, ln1_gain, w_out, w_router, ln2_gain, heads, blks)
    o, o_low, lse = call_forward(doc_lengths, q, kv)
    output, dh, d_o, grads, rx = call_middle(
        inputs, o_low.reshape(2, heads, tokens, LANES), wo.reshape(model, model + LANES),
        routes, priority, d_out, win, wout, heads, blks,
    )
    dq, dkv = call_backward(doc_lengths, q, kv, d_o, o, lse)
    ends = call_last(
        inputs, dh, dq, dkv, xa, wa, w_qkv, ln1_gain, grads, rx, win, wout, heads, blks
    )
    d_inputs, d_gain_one, d_qkv, d_out_proj, d_gain_two, d_router, d_in, d_out_weight = call_finish(*ends)
    return (
        output,
        d_inputs,
        d_gain_one.reshape(-1),
        d_qkv,
        d_out_proj,
        d_gain_two.reshape(-1),
        d_router.T,
        d_in[None],
        d_out_weight[None],
    )


def solution(mesh):
    in_specs = (
        P(("blk", "head"), None),
        P("blk"),
        P("blk", None),
        P("blk", None),
        P("blk"),
        P("blk", None),
        P("blk", None, None),
        P("blk", None, None),
        P(("blk", "head"), None),
        P(("blk", "head"), None),
        P(),
        P(("blk", "head"), None),
    )
    out_specs = (
        P(("blk", "head"), None),
        P(("blk", "head"), None),
        P("blk"),
        P("blk", None),
        P("blk", None),
        P("blk"),
        P("blk", None),
        P("blk", None, None),
        P("blk", None, None),
    )
    fits = mesh.shape["head"] == 4 and mesh.shape["blk"] == 8
    body = local_kernels if fits else local
    return jax.shard_map(body, mesh=mesh, in_specs=in_specs, out_specs=out_specs, check_vma=False)
```

```python
import functools
import math

import jax
import jax.numpy as jnp
from jax import lax
from jax.experimental import pallas as pl
from jax.experimental.pallas import tpu as pltpu
from jax.sharding import PartitionSpec as P

HS = 64
KEY_BLOCK = 2048


PRECISE = lax.Precision.HIGHEST
MASKED = -1e30
EPSILON = 1e-06


def layer_norm(values, gain):
    average = jnp.mean(values, axis=-1, keepdims=True)
    centred = values - average
    spread = jnp.mean(centred * centred, axis=-1, keepdims=True)
    return centred * lax.rsqrt(spread + EPSILON) * gain


def gelu_exact(values):
    return jax.nn.gelu(values, approximate=False)


def router(row_block, weight):
    return jax.nn.softmax(jnp.dot(row_block, weight, precision=PRECISE), axis=-1)


def doc_index(positions, doc_lengths):
    places = jnp.arange(doc_lengths.shape[0], dtype=jnp.int32)
    starts = jnp.sum(jnp.where(places[None, :] < places[:, None], doc_lengths[None, :], 0), axis=1)
    at_most = (starts[None, :] <= positions[:, None]).astype(jnp.int32)
    return jnp.sum(at_most, axis=1) - 1


def slot_table(route_rows, ranking, capacity):
    token_count = route_rows.shape[0]
    expert = jnp.transpose(route_rows).reshape(-1)
    pair_order = (jnp.arange(2, dtype=jnp.int32)[:, None] * token_count + ranking[None, :]).reshape(
        -1
    )
    before = (expert[:, None] == expert[None, :]) & (pair_order[None, :] < pair_order[:, None])
    position = jnp.sum(before.astype(jnp.int32), axis=1)
    slot_ids = jnp.where(position < capacity, expert * capacity + position, -1)
    return slot_ids.reshape(2, token_count)


def keep_state(current):
    return current


def local(
    inputs,
    ln1_gain,
    w_qkv,
    w_out,
    ln2_gain,
    w_router,
    expert_in,
    expert_out,
    routes,
    priority,
    doc_lengths,
    d_out,
):
    blk_size = lax.axis_size("blk")
    tok_rows = inputs.shape[0]
    model_width = inputs.shape[1]
    capacity = 2 * tok_rows // blk_size
    slot_total = blk_size * capacity
    gain_one, qkv_weight, out_weight, gain_two, router_weight = (
        lax.all_gather(ln1_gain, "blk", axis=0, tiled=True),
        lax.all_gather(w_qkv, "blk", axis=0, tiled=True),
        lax.all_gather(w_out, "blk", axis=0, tiled=True),
        lax.all_gather(ln2_gain, "blk", axis=0, tiled=True),
        lax.all_gather(w_router, "blk", axis=0, tiled=True),
    )
    input_rows = inputs.astype(jnp.float32)
    normed_one, norm_one_pull = jax.vjp(layer_norm, input_rows, gain_one.astype(jnp.float32))
    normed_low = normed_one.astype(jnp.bfloat16)
    qkv_rows = jnp.dot(normed_low, qkv_weight, preferred_element_type=jnp.float32).astype(
        jnp.bfloat16
    )
    query_heads, key_heads, value_heads = (
        lax.all_to_all(qkv_rows[:, :model_width], "head", split_axis=1, concat_axis=0, tiled=True),
        lax.all_to_all(
            qkv_rows[:, model_width : 2 * model_width],
            "head",
            split_axis=1,
            concat_axis=0,
            tiled=True,
        ),
        lax.all_to_all(
            qkv_rows[:, 2 * model_width :], "head", split_axis=1, concat_axis=0, tiled=True
        ),
    )
    span_rows = query_heads.shape[0]
    head_count = query_heads.shape[1] // HS
    key_all, value_all = (
        lax.all_gather(key_heads, "blk", axis=0, tiled=True),
        lax.all_gather(value_heads, "blk", axis=0, tiled=True),
    )
    total_rows = key_all.shape[0]
    block_count = total_rows // KEY_BLOCK
    scale_factor = HS ** (-0.5)
    query_pos = lax.axis_index("blk") * span_rows + jnp.arange(span_rows, dtype=jnp.int32)
    query_docs = doc_index(query_pos, doc_lengths)
    queries = query_heads.reshape(span_rows, head_count, HS)

    def block_parts(block_index, key_source, value_source):
        first_key = block_index * KEY_BLOCK
        key_rows = lax.dynamic_slice_in_dim(key_source, first_key, KEY_BLOCK, 0).reshape(
            KEY_BLOCK, head_count, HS
        )
        value_rows = lax.dynamic_slice_in_dim(value_source, first_key, KEY_BLOCK, 0).reshape(
            KEY_BLOCK, head_count, HS
        )
        key_docs = doc_index(first_key + jnp.arange(KEY_BLOCK, dtype=jnp.int32), doc_lengths)
        is_live = (key_docs[0] <= query_docs[-1]) & (key_docs[-1] >= query_docs[0])
        same_doc = query_docs[:, None] == key_docs[None, :]
        return (first_key, key_rows, value_rows, same_doc, is_live)

    def block_scores(key_rows, same_doc):
        raw_scores = (
            jnp.einsum("qhd,khd->hqk", queries, key_rows, preferred_element_type=jnp.float32)
            * scale_factor
        )
        return jnp.where(same_doc[None], raw_scores, MASKED)

    def stat_step(block_index, loop_state):
        first_key, key_rows, value_rows, same_doc, is_live = block_parts(
            block_index, key_all, value_all
        )

        def stat_update(current):
            running_max, running_sum = current
            scores = block_scores(key_rows, same_doc)
            new_max = jnp.maximum(running_max, jnp.max(scores, axis=2))
            exp_terms = jnp.where(same_doc[None], jnp.exp(scores - new_max[:, :, None]), 0.0)
            return (
                new_max,
                running_sum * jnp.exp(running_max - new_max) + jnp.sum(exp_terms, axis=2),
            )

        return lax.cond(is_live, stat_update, keep_state, loop_state)

    start_state = (
        jnp.full((head_count, span_rows), MASKED, jnp.float32),
        jnp.zeros((head_count, span_rows), jnp.float32),
    )
    running_max, running_sum = lax.fori_loop(0, block_count, stat_step, start_state)
    log_total = running_max + jnp.log(running_sum)

    def out_step(block_index, loop_state):
        first_key, key_rows, value_rows, same_doc, is_live = block_parts(
            block_index, key_all, value_all
        )

        def out_update(current):
            scores = block_scores(key_rows, same_doc)
            weights = jnp.where(
                same_doc[None], jnp.exp(scores - log_total[:, :, None]), 0.0
            ).astype(jnp.bfloat16)
            return current + jnp.einsum(
                "hqk,khd->qhd", weights, value_rows, preferred_element_type=jnp.float32
            )

        return lax.cond(is_live, out_update, keep_state, loop_state)

    mixed_full = lax.fori_loop(
        0, block_count, out_step, jnp.zeros((span_rows, head_count, HS), jnp.float32)
    )
    mixed_low = mixed_full.reshape(span_rows, head_count * HS).astype(jnp.bfloat16)
    mixed_tokens = lax.all_to_all(mixed_low, "head", split_axis=0, concat_axis=1, tiled=True)
    attended = jnp.dot(mixed_tokens, out_weight, preferred_element_type=jnp.float32)
    hidden_one = input_rows + attended
    normed_two, norm_two_pull = jax.vjp(layer_norm, hidden_one, gain_two.astype(jnp.float32))
    routed_low = normed_two.astype(jnp.bfloat16)
    router_probs, router_pull = jax.vjp(
        router, routed_low.astype(jnp.float32), router_weight.astype(jnp.float32)
    )
    slot_ids = slot_table(routes, priority[0], capacity)
    select = (
        slot_ids[:, :, None] == jnp.arange(slot_total, dtype=jnp.int32)[None, None, :]
    ).astype(jnp.bfloat16)
    send_rows = jnp.einsum(
        "kts,td->sd", select, routed_low, preferred_element_type=jnp.float32
    ).astype(jnp.bfloat16)
    expert_rows = lax.all_to_all(
        send_rows.reshape(blk_size, capacity, model_width),
        "blk",
        split_axis=0,
        concat_axis=0,
        tiled=True,
    ).reshape(slot_total, model_width)
    weight_in = expert_in[0]
    weight_out = expert_out[0]
    pre_act = jnp.dot(expert_rows, weight_in, preferred_element_type=jnp.float32)
    hidden_act, gelu_pull = jax.vjp(gelu_exact, pre_act)
    hidden_low = hidden_act.astype(jnp.bfloat16)
    expert_result = jnp.dot(hidden_low, weight_out, preferred_element_type=jnp.float32).astype(
        jnp.bfloat16
    )
    slot_result = lax.all_to_all(
        expert_result.reshape(blk_size, capacity, model_width),
        "blk",
        split_axis=0,
        concat_axis=0,
        tiled=True,
    ).reshape(slot_total, model_width)
    pair_result = jnp.einsum("kts,sd->ktd", select, slot_result, preferred_element_type=jnp.float32)
    route_hot = (routes[:, :, None] == jnp.arange(blk_size, dtype=jnp.int32)[None, None, :]).astype(
        jnp.float32
    )
    gate_vals = jnp.sum(router_probs[:, None, :] * route_hot, axis=2)
    mixture = gate_vals[:, 0, None] * pair_result[0] + gate_vals[:, 1, None] * pair_result[1]
    output = (hidden_one + mixture).astype(jnp.bfloat16)
    d_gates = jnp.transpose(jnp.sum(d_out[None] * pair_result, axis=2))
    d_probs = jnp.sum(d_gates[:, :, None] * route_hot, axis=1)
    pair_grads = (jnp.transpose(gate_vals)[:, :, None] * d_out[None]).astype(jnp.bfloat16)
    slot_grads = jnp.einsum(
        "kts,ktd->sd", select, pair_grads, preferred_element_type=jnp.float32
    ).astype(jnp.bfloat16)
    result_grads = lax.all_to_all(
        slot_grads.reshape(blk_size, capacity, model_width),
        "blk",
        split_axis=0,
        concat_axis=0,
        tiled=True,
    ).reshape(slot_total, model_width)
    d_hidden_act = jnp.dot(result_grads, weight_out.T, preferred_element_type=jnp.float32)
    d_weight_out = jnp.dot(hidden_low.T, result_grads, preferred_element_type=jnp.float32)
    d_preact = gelu_pull(d_hidden_act)[0].astype(jnp.bfloat16)
    d_weight_in = jnp.dot(expert_rows.T, d_preact, preferred_element_type=jnp.float32)
    row_grads = jnp.dot(d_preact, weight_in.T, preferred_element_type=jnp.float32).astype(
        jnp.bfloat16
    )
    slot_back = lax.all_to_all(
        row_grads.reshape(blk_size, capacity, model_width),
        "blk",
        split_axis=0,
        concat_axis=0,
        tiled=True,
    ).reshape(slot_total, model_width)
    d_routed = jnp.einsum("kts,sd->td", select, slot_back, preferred_element_type=jnp.float32)
    d_routed_router, d_router = router_pull(d_probs)
    d_hidden_norm, d_gain_two = norm_two_pull(d_routed + d_routed_router)
    d_hidden_one = d_out + d_hidden_norm
    attn_grads = d_hidden_one.astype(jnp.bfloat16)
    d_out_weight = jnp.dot(mixed_tokens.T, attn_grads, preferred_element_type=jnp.float32)
    mixed_grads = jnp.dot(attn_grads, out_weight.T, preferred_element_type=jnp.float32).astype(
        jnp.bfloat16
    )
    head_grads = lax.all_to_all(mixed_grads, "head", split_axis=1, concat_axis=0, tiled=True)
    out_grads = head_grads.reshape(span_rows, head_count, HS)
    row_delta = jnp.transpose(jnp.sum(out_grads.astype(jnp.float32) * mixed_full, axis=2))
    key_back, value_back = (
        lax.all_gather(key_heads, "blk", axis=0, tiled=True),
        lax.all_gather(value_heads, "blk", axis=0, tiled=True),
    )

    def grad_step(block_index, loop_state):
        first_key, key_rows, value_rows, same_doc, is_live = block_parts(
            block_index, key_back, value_back
        )

        def grad_update(current):
            query_grad, key_grad, value_grad = current
            scores = block_scores(key_rows, same_doc)
            weights = jnp.where(same_doc[None], jnp.exp(scores - log_total[:, :, None]), 0.0)
            value_part = jnp.einsum(
                "hqk,qhd->khd",
                weights.astype(jnp.bfloat16),
                out_grads,
                preferred_element_type=jnp.float32,
            )
            weight_grads = jnp.einsum(
                "qhd,khd->hqk", out_grads, value_rows, preferred_element_type=jnp.float32
            )
            score_grads = (weights * (weight_grads - row_delta[:, :, None])).astype(jnp.bfloat16)
            query_grad = (
                query_grad
                + jnp.einsum(
                    "hqk,khd->qhd", score_grads, key_rows, preferred_element_type=jnp.float32
                )
                * scale_factor
            )
            key_part = (
                jnp.einsum("hqk,qhd->khd", score_grads, queries, preferred_element_type=jnp.float32)
                * scale_factor
            )
            key_grad = lax.dynamic_update_slice_in_dim(
                key_grad, key_part.reshape(KEY_BLOCK, head_count * HS), first_key, 0
            )
            value_grad = lax.dynamic_update_slice_in_dim(
                value_grad, value_part.reshape(KEY_BLOCK, head_count * HS), first_key, 0
            )
            return (query_grad, key_grad, value_grad)

        return lax.cond(is_live, grad_update, keep_state, loop_state)

    start_grads = (
        jnp.zeros((span_rows, head_count, HS), jnp.float32),
        jnp.zeros((total_rows, head_count * HS), jnp.float32),
        jnp.zeros((total_rows, head_count * HS), jnp.float32),
    )
    query_grad, key_grad, value_grad = lax.fori_loop(0, block_count, grad_step, start_grads)
    key_own, value_own = (
        lax.psum_scatter(
            key_grad.astype(jnp.bfloat16), "blk", scatter_dimension=0, tiled=True
        ).astype(jnp.float32),
        lax.psum_scatter(
            value_grad.astype(jnp.bfloat16), "blk", scatter_dimension=0, tiled=True
        ).astype(jnp.float32),
    )
    query_tokens_grad, key_tokens_grad, value_tokens_grad = (
        lax.all_to_all(
            query_grad.reshape(span_rows, head_count * HS).astype(jnp.bfloat16),
            "head",
            split_axis=0,
            concat_axis=1,
            tiled=True,
        ),
        lax.all_to_all(
            key_own.astype(jnp.bfloat16), "head", split_axis=0, concat_axis=1, tiled=True
        ),
        lax.all_to_all(
            value_own.astype(jnp.bfloat16), "head", split_axis=0, concat_axis=1, tiled=True
        ),
    )
    qkv_grads = jnp.concatenate([query_tokens_grad, key_tokens_grad, value_tokens_grad], axis=1)
    d_qkv_weight = jnp.dot(normed_low.T, qkv_grads, preferred_element_type=jnp.float32)
    normed_grads = jnp.dot(qkv_grads, qkv_weight.T, preferred_element_type=jnp.float32)
    d_inputs_norm, d_gain_one = norm_one_pull(normed_grads)
    d_inputs = d_hidden_one + d_inputs_norm
    gain_one_sum, qkv_sum, out_sum, gain_two_sum, router_sum = (
        lax.psum_scatter(
            d_gain_one.astype(jnp.bfloat16), "blk", scatter_dimension=0, tiled=True
        ).astype(jnp.float32),
        lax.psum_scatter(
            d_qkv_weight.astype(jnp.bfloat16), "blk", scatter_dimension=0, tiled=True
        ).astype(jnp.float32),
        lax.psum_scatter(
            d_out_weight.astype(jnp.bfloat16), "blk", scatter_dimension=0, tiled=True
        ).astype(jnp.float32),
        lax.psum_scatter(
            d_gain_two.astype(jnp.bfloat16), "blk", scatter_dimension=0, tiled=True
        ).astype(jnp.float32),
        lax.psum_scatter(
            d_router.astype(jnp.bfloat16), "blk", scatter_dimension=0, tiled=True
        ).astype(jnp.float32),
    )
    gain_one_all, qkv_all, out_all, gain_two_all, router_all, expert_in_all, expert_out_all = (
        lax.psum(gain_one_sum.astype(jnp.bfloat16), "head").astype(jnp.float32),
        lax.psum(qkv_sum.astype(jnp.bfloat16), "head").astype(jnp.float32),
        lax.psum(out_sum.astype(jnp.bfloat16), "head").astype(jnp.float32),
        lax.psum(gain_two_sum.astype(jnp.bfloat16), "head").astype(jnp.float32),
        lax.psum(router_sum.astype(jnp.bfloat16), "head").astype(jnp.float32),
        lax.psum(d_weight_in[None].astype(jnp.bfloat16), "head").astype(jnp.float32),
        lax.psum(d_weight_out[None].astype(jnp.bfloat16), "head").astype(jnp.float32),
    )
    return (
        output,
        d_inputs,
        gain_one_all,
        qkv_all,
        out_all,
        gain_two_all,
        router_all,
        expert_in_all,
        expert_out_all,
    )


MESH = pl.DeviceIdType.MESH
LANES = 128
HALF = LANES // 2
MIB = 2**20
F32 = jnp.float32
BF16 = jnp.bfloat16


def dot(left, right, dims=(1, 0)):
    return lax.dot_general(
        left, right, (((dims[0],), (dims[1],)), ((), ())), preferred_element_type=F32
    )


def remote(src, dst, send_sem, recv_sem, head, blk):
    return pltpu.make_async_remote_copy(
        src_ref=src,
        dst_ref=dst,
        send_sem=send_sem,
        recv_sem=recv_sem,
        device_id={"head": head, "blk": blk},
        device_id_type=MESH,
    )


def arrived(ref, sem):
    pltpu.make_async_copy(ref, ref, sem).wait()


def greet(peers):
    barrier = pltpu.get_barrier_semaphore()
    for head, blk in peers:
        pl.semaphore_signal(
            barrier, inc=1, device_id={"head": head, "blk": blk}, device_id_type=MESH
        )
    pl.semaphore_wait(barrier, len(peers))


def lane_ids(shape):
    return lax.broadcasted_iota(jnp.int32, shape, len(shape) - 1)


def centre(values):
    average = jnp.mean(values, axis=-1, keepdims=True)
    centred = values - average
    spread = jnp.mean(centred * centred, axis=-1, keepdims=True)
    scale = lax.rsqrt(spread + EPSILON)
    return centred * scale, scale


def centre_back(grad, xhat, scale):
    middle = jnp.mean(grad, axis=-1, keepdims=True)
    along = jnp.mean(grad * xhat, axis=-1, keepdims=True)
    return (grad - middle - xhat * along) * scale


def split_high_low(column, lanes):
    high = column.astype(BF16)
    low = (column - high.astype(F32)).astype(BF16)
    return jnp.where(lanes < HALF, high.astype(F32), low.astype(F32)).astype(BF16)


def join_high_low(matrix, start):
    return matrix[:, start : start + 1].astype(F32) + matrix[
        :, start + HALF : start + HALF + 1
    ].astype(F32)


def place():
    head, blk = lax.axis_index("head"), lax.axis_index("blk")
    return head, blk, blk // 2, lax.rem(blk, 2)


def around(index, step, size):
    return lax.rem(index + step, size)


def qkv_kernel(
    heads, blks,
    x_hbm, w_hbm, g1_hbm, wo_hbm, wr_hbm, g2_hbm, docs_hbm,
    qall, kvall, xall, wall, wo_all, kvt, bounds,
    x_ref, w_ref, rows_in, g1_ref, g2_ref, wr_ref, docs_ref, wo_own, kv_other, in_sem,
    x_send, x_recv, w_send, w_recv, o_send, o_recv, p_send, p_recv,
    k_send, k_recv, q_recv,
):
    head, blk, z, y = place()
    planes = blks // 2
    model = x_ref.shape[1]
    rows = w_ref.shape[0]
    part = rows // heads
    experts = wr_ref.shape[0]
    wanted = (
        (w_hbm, w_ref), (g1_hbm, g1_ref), (g2_hbm, g2_ref), (wr_hbm, wr_ref), (x_hbm, x_ref),
        (wo_hbm, wo_own.at[:, pl.ds(0, model)]), (docs_hbm, docs_ref),
    )
    fetched = [
        pltpu.make_async_copy(src, dst, in_sem.at[i]) for i, (src, dst) in enumerate(wanted)
    ]
    for copy in fetched:
        copy.start()
    rows_in[...] = jnp.zeros_like(rows_in)
    greet(
        [(around(head, k, heads), blk) for k in range(1, heads)]
        + [(head, around(blk, k, blks)) for k in range(1, blks)]
    )
    lanes = lane_ids((rows, LANES))
    for copy in fetched:
        copy.wait()
    rows_in[0:experts, 0:rows] = wr_ref[...].astype(F32)
    rows_in[experts : experts + 1, 0:rows] = g2_ref[...].astype(F32)
    rows_in[experts + 1 : experts + 2, 0:rows] = g1_ref[...].astype(F32)
    vectors = jnp.transpose(rows_in[...])[:rows]
    gain = vectors[:, experts + 1 : experts + 2]

    def columns(which):
        start = pl.multiple_of(which * model + head * LANES, LANES)
        return w_ref[:, pl.ds(start, LANES)].astype(F32) * gain

    key_cols = columns(1)
    value_cols = pltpu.roll(columns(2), HALF, 1)
    wall[blk, :, 0:LANES] = jnp.where(lanes < HALF, key_cols, value_cols).astype(BF16)
    wall[blk, :, LANES : 2 * LANES] = jnp.where(lanes < HALF, value_cols, key_cols).astype(BF16)
    wall[blk, :, 2 * LANES : 3 * LANES] = (columns(0) * HS ** (-0.5)).astype(BF16)
    w_copies = [
        remote(wall.at[blk], wall.at[blk], w_send.at[k], w_recv.at[k], head, around(blk, k, blks))
        for k in range(1, blks)
    ]
    for copy in w_copies:
        copy.start()
    xhat, _ = centre(x_ref[...].astype(F32))
    xall[head] = xhat.astype(BF16)
    x_copies = [
        remote(xall.at[head], xall.at[head], x_send.at[k], x_recv.at[k], around(head, k, heads), blk)
        for k in range(1, heads)
    ]
    for copy in x_copies:
        copy.start()
    wo_own[:, model : model + LANES] = vectors.astype(BF16)
    wo_all[blk, head] = wo_own[pl.ds(pl.multiple_of(head * part, part), part), :]
    o_copies = [
        remote(
            wo_all.at[blk, head], wo_all.at[blk, head],
            o_send.at[k], o_recv.at[k], head, around(blk, k, blks),
        )
        for k in range(1, blks)
    ]
    for copy in o_copies:
        copy.start()
    document_bounds(docs_ref, bounds, z)
    for copy in x_copies:
        copy.wait()
    for copy in w_copies:
        copy.wait()
    weight = wall[...].reshape(model, 3 * LANES)
    tokens = x_ref.shape[0]
    even = y == 0
    for piece in range(heads):
        made = dot(xall[piece], weight).astype(BF16)
        first, second = made[:, 0:LANES], made[:, LANES : 2 * LANES]
        span = slice(piece * tokens, (piece + 1) * tokens)
        kvall[blk, span, :] = jnp.where(even, first, second)
        kv_other[span, :] = jnp.where(even, second, first)
        qall[y, span, :] = made[:, 2 * LANES : 3 * LANES]
    above, below = z < planes - 1, z > 0
    own = kvall.at[blk]

    def turn(span):
        size = kvall.shape[1]
        kvt[:, pl.ds(pl.multiple_of(span * size, size), size)] = jnp.transpose(kvall[span])

    def outward(slot, step, across):
        target = 2 * (z + step) + around(y, across, 2)
        return remote(kv_other if across else own, own, k_send.at[slot], k_recv.at[blk], head, target)

    def onward(slot, step, side):
        from_span = 2 * (z - step) + side
        ref = kvall.at[from_span]
        return remote(ref, ref, k_send.at[slot], k_recv.at[from_span], head, 2 * (z + step) + y)

    sides = ((1, above, below, 0), (-1, below, above, 2))
    for step, there, _, slot in sides:

        @pl.when(there)
        def _():
            outward(slot, step, 0).start()
            outward(slot + 1, step, 1).start()

    to_pair = outward(4, 0, 1)
    to_pair.start()
    q_pair = remote(qall.at[y], qall.at[y], k_send.at[5], q_recv, head, 2 * z + around(y, 1, 2))
    q_pair.start()
    turn(blk)
    for copy in o_copies:
        copy.wait()
    p_copies = [
        remote(
            wo_all.at[:, head], wo_all.at[:, head],
            p_send.at[k], p_recv.at[k], around(head, k, heads), blk,
        )
        for k in range(1, heads)
    ]
    for copy in p_copies:
        copy.start()
    pair = 2 * z + around(y, 1, 2)
    arrived(kvall.at[pair], k_recv.at[pair])
    turn(pair)
    for step, there, back, slot in sides:

        @pl.when(back)
        def _():
            for side in range(2):
                span = 2 * (z - step) + side
                arrived(kvall.at[span], k_recv.at[span])

        @pl.when(jnp.logical_and(there, back))
        def _():
            for side in range(2):
                onward(6 + slot + side, step, side).start()

    for step, there, back, slot in sides:

        @pl.when(back)
        def _():
            for side in range(2):
                turn(2 * (z - step) + side)

    for other in range(planes):
        for side in range(2):
            span = 2 * other + side

            @pl.when(jnp.logical_or(z - other == 2, other - z == 2))
            def _():
                arrived(kvall.at[span], k_recv.at[span])
                turn(span)

    q_pair.wait()
    for copy in p_copies:
        copy.wait()
    to_pair.wait_send()
    for step, there, back, slot in sides:

        @pl.when(there)
        def _():
            outward(slot, step, 0).wait_send()
            outward(slot + 1, step, 1).wait_send()

        @pl.when(jnp.logical_and(there, back))
        def _():
            for side in range(2):
                onward(6 + slot + side, step, side).wait_send()


def document_bounds(docs_ref, bounds, z):
    count = docs_ref.shape[1]
    lengths = docs_ref[...].astype(F32)
    doc = lax.broadcasted_iota(jnp.int32, (count, count), 0)
    other = lane_ids((count, count))
    start = jnp.sum(jnp.where(other < doc, lengths, 0.0), axis=1, keepdims=True)
    end = jnp.sum(jnp.where(other <= doc, lengths, 0.0), axis=1, keepdims=True)
    queries = bounds.shape[1]
    token = (z * queries + lane_ids((count, queries))).astype(F32)
    begun = start <= token
    bounds[...] = jnp.zeros_like(bounds)
    bounds[0:1, :] = jnp.max(jnp.where(begun, start, 0.0), axis=0, keepdims=True).astype(jnp.int32)
    bounds[1:2, :] = jnp.max(jnp.where(begun, end, 0.0), axis=0, keepdims=True).astype(jnp.int32)


def vmem_specs(count):
    return [pl.BlockSpec(memory_space=pltpu.VMEM)] * count


def hbm_specs(count):
    return [pl.BlockSpec(memory_space=pltpu.HBM)] * count


def in_hbm(*arrays):
    return [pltpu.with_memory_space_constraint(array, pltpu.HBM) for array in arrays]


def dma(*shape):
    return pltpu.SemaphoreType.DMA(shape)


def call_qkv(x, w_qkv, g1, w_out, w_router, g2, doc_lengths, heads, blks):
    tokens, model = x.shape
    rows = w_qkv.shape[0]
    span = tokens * heads
    wide = model + LANES
    part = rows // heads
    return pl.pallas_call(
        functools.partial(qkv_kernel, heads, blks),
        out_shape=(
            jax.ShapeDtypeStruct((2, span, LANES), BF16),
            jax.ShapeDtypeStruct((blks, span, LANES), BF16),
            jax.ShapeDtypeStruct((heads, tokens, model), BF16),
            jax.ShapeDtypeStruct((blks, rows, 3 * LANES), BF16),
            jax.ShapeDtypeStruct((blks, heads, part, wide), BF16),
            jax.ShapeDtypeStruct((LANES, blks * span), BF16),
            jax.ShapeDtypeStruct((8, 2 * span), jnp.int32),
        ),
        in_specs=hbm_specs(7),
        out_specs=tuple(vmem_specs(7)),
        scratch_shapes=[
            pltpu.VMEM((tokens, model), BF16),
            pltpu.VMEM((rows, 3 * model), BF16),
            pltpu.VMEM((LANES, LANES), F32),
            pltpu.VMEM((1, rows), BF16),
            pltpu.VMEM((1, rows), BF16),
            pltpu.VMEM((w_router.shape[1], rows), BF16),
            pltpu.VMEM((1, doc_lengths.shape[0]), jnp.int32),
            pltpu.VMEM((rows, wide), BF16),
            pltpu.VMEM((span, LANES), BF16),
            dma(7),
            dma(heads), dma(heads), dma(blks), dma(blks), dma(blks), dma(blks), dma(heads), dma(heads),
            dma(10), dma(blks), pltpu.SemaphoreType.DMA,
        ],
        compiler_params=pltpu.CompilerParams(
            collective_id=1, has_side_effects=True, vmem_limit_bytes=16 * MIB
        ),
        name="qkv",
    )(
        *in_hbm(
            x, w_qkv, g1.reshape(1, rows), w_out, w_router.T, g2.reshape(1, rows),
            doc_lengths.reshape(1, -1),
        )
    )


QUERY_TILE = 256
CHAINS = 2


def masked_queries(q_ref, tile, key_lanes, query_tile):
    tiles_per_span = q_ref.shape[1] // query_tile
    inner = tile % tiles_per_span * query_tile
    query = q_ref[tile // tiles_per_span, inner : inner + query_tile, :]
    return jnp.where(key_lanes, query, jnp.zeros_like(query))


def group_blocks(bounds_ref, group, size, key_tile):
    first, last = group * size, (group + 1) * size
    low = jnp.min(bounds_ref[0:1, first : first + LANES])
    high = jnp.max(bounds_ref[1:2, last - LANES : last])
    return low // key_tile, (high + key_tile - 1) // key_tile


def inside_document(bounds_ref, tile, first, shape):
    key = first + lax.broadcasted_iota(jnp.int32, shape, 0)
    columns = slice(tile * shape[1], (tile + 1) * shape[1])
    return jnp.logical_and(key >= bounds_ref[0:1, columns], key < bounds_ref[1:2, columns])


def forward_kernel(bounds_ref, q_ref, kv_ref, kvt_ref, o_out, ob_out, lse_out):
    _, _, z, y = place()
    key_tile = kv_ref.shape[1]
    total = q_ref.shape[0] * q_ref.shape[1]
    key_lanes = (lane_ids((QUERY_TILE, LANES)) < HALF) == (y == 0)
    group_size = CHAINS * QUERY_TILE
    for group in range(total // group_size):
        tiles = range(group * CHAINS, (group + 1) * CHAINS)
        queries = [masked_queries(q_ref, tile, key_lanes, QUERY_TILE) for tile in tiles]
        low, high = group_blocks(bounds_ref, group, group_size, key_tile)

        def step(block, carry, queries=queries, tiles=tiles):
            first = pl.multiple_of(block * key_tile, key_tile)
            keys = kv_ref[block]
            keys_across = kvt_ref[:, pl.ds(first, key_tile)]
            scores = [dot(keys, query, (1, 1)) for query in queries]
            made = []
            for tile, score, (biggest, weight, mixed) in zip(tiles, scores, carry):
                inside = inside_document(bounds_ref, tile, first, score.shape)
                score = jnp.where(inside, score, MASKED)
                bigger = jnp.maximum(biggest, jnp.max(score, axis=0, keepdims=True))
                fade = jnp.exp(biggest - bigger)
                terms = jnp.exp(score - bigger)
                weight = weight * fade + jnp.sum(terms, axis=0, keepdims=True)
                made.append((bigger, weight, mixed * fade + dot(keys_across, terms.astype(BF16))))
            return tuple(made)

        start = (
            jnp.full((1, QUERY_TILE), MASKED, F32),
            jnp.zeros((1, QUERY_TILE), F32),
            jnp.zeros((LANES, QUERY_TILE), F32),
        )
        ends = lax.fori_loop(low, high, step, (start,) * CHAINS)
        for tile, (biggest, weight, mixed) in zip(tiles, ends):
            result = jnp.transpose(mixed / weight)
            o_out[tile] = result
            ob_out[tile] = result.astype(BF16)
            lse_out[tile] = jnp.broadcast_to(biggest + jnp.log(weight), (8, QUERY_TILE))


def call_forward(bounds, q, kv, kvt):
    blks, span, _ = kv.shape
    tiles = 2 * span // QUERY_TILE
    return pl.pallas_call(
        forward_kernel,
        out_shape=(
            jax.ShapeDtypeStruct((tiles, QUERY_TILE, LANES), F32),
            jax.ShapeDtypeStruct((tiles, QUERY_TILE, LANES), BF16),
            jax.ShapeDtypeStruct((tiles, 8, QUERY_TILE), F32),
        ),
        in_specs=vmem_specs(4),
        out_specs=tuple(vmem_specs(3)),
        compiler_params=pltpu.CompilerParams(vmem_limit_bytes=16 * MIB),
        name="attend",
    )(bounds, q, kv, kvt)


def backward_kernel(
    bounds_ref, q_ref, kv_ref, kvt_ref, do_ref, o_ref, lse_ref, dq_out, dkv_out, dkv
):
    _, _, z, y = place()
    key_tile = kv_ref.shape[1]
    total = q_ref.shape[0] * q_ref.shape[1]
    dkv[...] = jnp.zeros_like(dkv)
    key_lanes = (lane_ids((QUERY_TILE, LANES)) < HALF) == (y == 0)
    group_size = CHAINS * QUERY_TILE
    for group in range(total // group_size):
        tiles = range(group * CHAINS, (group + 1) * CHAINS)
        queries, out_grads, deltas, log_totals = [], [], [], []
        for tile in tiles:
            queries.append(masked_queries(q_ref, tile, key_lanes, QUERY_TILE))
            out_grad = do_ref[tile]
            out_grads.append(jnp.where(key_lanes, jnp.zeros_like(out_grad), out_grad))
            product = jnp.transpose(out_grads[-1].astype(F32) * o_ref[tile])
            deltas.append(jnp.sum(product, axis=0, keepdims=True))
            log_totals.append(lse_ref[tile, 0:1, :])
        low, high = group_blocks(bounds_ref, group, group_size, key_tile)

        def step(
            block, carry, queries=queries, out_grads=out_grads, deltas=deltas,
            log_totals=log_totals, tiles=tiles,
        ):
            first = pl.multiple_of(block * key_tile, key_tile)
            keys = kv_ref[block]
            keys_across = kvt_ref[:, pl.ds(first, key_tile)]
            scores = [dot(keys, query, (1, 1)) for query in queries]
            weight_grads = [dot(keys, out_grad, (1, 1)) for out_grad in out_grads]
            pieces, score_grads = [], []
            for i, tile in enumerate(tiles):
                inside = inside_document(bounds_ref, tile, first, scores[i].shape)
                weights = jnp.exp(jnp.where(inside, scores[i], MASKED) - log_totals[i])
                score_grads.append((weights * (weight_grads[i] - deltas[i])).astype(BF16))
                pieces.append(weights.astype(BF16))
            wide = jnp.concatenate(score_grads + pieces, axis=1)
            dkv[block] += dot(wide, jnp.concatenate(queries + out_grads, axis=0))
            return tuple(c + dot(keys_across, s) for c, s in zip(carry, score_grads))

        zero = jnp.zeros((LANES, QUERY_TILE), F32)
        ends = lax.fori_loop(low, high, step, (zero,) * CHAINS)
        for tile, mixed in zip(tiles, ends):
            dq_out[tile] = jnp.transpose(mixed).astype(BF16)
    for block in range(dkv.shape[0]):
        dkv_out[block] = dkv[block].astype(BF16)


def call_backward(bounds, q, kv, kvt, d_o, o, lse):
    blks, span, _ = kv.shape
    tiles = 2 * span // QUERY_TILE
    return pl.pallas_call(
        backward_kernel,
        out_shape=(
            jax.ShapeDtypeStruct((tiles, QUERY_TILE, LANES), BF16),
            jax.ShapeDtypeStruct((blks, span, LANES), BF16),
        ),
        in_specs=vmem_specs(7),
        out_specs=tuple(vmem_specs(2)),
        scratch_shapes=[pltpu.VMEM((blks, span, LANES), F32)],
        compiler_params=pltpu.CompilerParams(vmem_limit_bytes=16 * MIB),
        name="attend_back",
    )(bounds, q, kv, kvt, d_o.reshape(tiles, QUERY_TILE, LANES), o, lse)


def gelu_parts(values):
    share = 0.5 * (1.0 + lax.erf(values * (2.0**-0.5)))
    slope = share + values * jnp.exp(-0.5 * values * values) * (2.0 * math.pi) ** -0.5
    return values * share, slope


def positions(expert_rows, expert_cols, rank_row, rank_col):
    def count(mask, axis):
        return jnp.sum(mask.astype(F32), axis=axis, keepdims=True)

    row = [None, None]
    col = [None, None]
    before = rank_col < rank_row
    after = rank_row < rank_col
    for choice in range(2):
        row[choice] = count((expert_cols[choice] == expert_rows[choice]) & before, 0)
        col[choice] = count((expert_rows[choice] == expert_cols[choice]) & after, 1)
    row[1] = row[1] + count(expert_cols[0] == expert_rows[1], 0)
    col[1] = col[1] + count(expert_rows[0] == expert_cols[1], 1)
    return row, col


def middle_kernel(
    heads, blks,
    x_hbm, o_ref, wo_ref, routes_hbm, rank_hbm, d_out_hbm, win_hbm, wout_hbm,
    out_ref, dh_ref, dma_all, grads_ref, rx,
    x_ref, routes_ref, rank_ref, d_out_ref, win_ref, wout_ref, rows_in, in_sem,
    o_all, dos, doa, rs, ra, po, pa, dr, da, dms, acc_out, acc_row, mix,
    o_send, o_recv, dos_send, dos_recv, r_send, r_recv, po_send, po_recv,
    dr_send, dr_recv, dm_send, dm_recv, rx_send, rx_recv,
):
    head, blk, z, y = place()
    tokens, model = x_ref.shape
    capacity = 2 * tokens // blks
    slots = capacity * blks
    plane = [(k % heads, k // heads) for k in range(1, 2 * heads)]
    wanted = (
        (routes_hbm, routes_ref), (rank_hbm, rank_ref), (d_out_hbm, d_out_ref), (x_hbm, x_ref),
        (win_hbm, win_ref), (wout_hbm, wout_ref),
    )
    fetched = [
        pltpu.make_async_copy(src, dst, in_sem.at[i]) for i, (src, dst) in enumerate(wanted)
    ]
    for copy in fetched:
        copy.start()
    greet(
        [(around(head, kh, heads), 2 * z + around(y, ky, 2)) for kh, ky in plane]
        + [(head, around(blk, k, blks)) for k in range(1, blks)]
    )

    def plane_copies(src_of, dst, send, recv):
        copies = []
        for k, (kh, ky) in enumerate(plane):
            to_head, to_y = around(head, kh, heads), around(y, ky, 2)
            copies.append(
                remote(src_of(to_y, to_head), dst, send.at[k], recv.at[k], to_head, 2 * z + to_y)
            )
        return copies

    def blk_copies(src, dst, send, recv):
        return [
            remote(
                src.at[around(blk, k, blks)], dst.at[blk],
                send.at[k], recv.at[k], head, around(blk, k, blks),
            )
            for k in range(1, blks)
        ]

    def start(copies):
        for copy in copies:
            copy.start()

    def finish(copies):
        for copy in copies:
            copy.wait()

    o_copies = plane_copies(lambda to_y, to_head: o_ref.at[to_y, to_head], o_all.at[y, head], o_send, o_recv)
    start(o_copies)
    o_all[y, head] = o_ref[y, head]

    lanes = lane_ids((tokens, LANES))
    for copy in fetched[:4]:
        copy.wait()
    e_rows = [routes_ref[i : i + 1, :].astype(F32) for i in range(2)]
    rank_row = rank_ref[...].astype(F32)
    rows_in[...] = jnp.zeros_like(rows_in)
    rows_in[0:1, :], rows_in[1:2, :], rows_in[2:3, :] = *e_rows, rank_row
    columns = jnp.transpose(rows_in[...])
    e_cols = [columns[:, 0:1], columns[:, 1:2]]
    rank_col = columns[:, 2:3]
    pos_rows, pos_cols = positions(e_rows, e_cols, rank_row, rank_col)

    def slot_of(expert, position):
        return jnp.where(position < capacity, expert * capacity + position, -1.0).astype(jnp.int32)

    slot_rows = [slot_of(e, p) for e, p in zip(e_rows, pos_rows)]
    slot_cols = [slot_of(e, p) for e, p in zip(e_cols, pos_cols)]
    slot_down = lax.broadcasted_iota(jnp.int32, (slots, tokens), 0)
    slot_across = lane_ids((tokens, slots))
    pick = [(slot_down == s).astype(BF16) for s in slot_rows]
    put = [(slot_across == s).astype(BF16) for s in slot_cols]
    pick_any = pick[0] + pick[1]
    put_any = put[0] + put[1]

    d_out = d_out_ref[...]
    dos[...] = dot(pick_any, d_out.astype(BF16)).astype(BF16).reshape(dos.shape)
    dos_copies = blk_copies(dos, doa, dos_send, dos_recv)
    start(dos_copies)
    doa[blk] = dos[blk]

    weight_out = jnp.concatenate(
        [wo_ref[(b ^ 1) * HALF : ((b ^ 1) + 1) * HALF, 0:model] for b in range(blks)], axis=0
    )
    small = wo_ref[:, model : model + LANES]
    small_across = jnp.concatenate(
        [
            jnp.transpose(small[i * LANES : (i + 1) * LANES].astype(F32))
            for i in range(model // LANES)
        ],
        axis=1,
    )
    gain = small_across[blks : blks + 1, :]

    finish(o_copies)
    for piece in range(heads):
        mix[:, piece * LANES : (piece + 1) * LANES] = jnp.where(
            lanes < HALF, o_all[1, piece], o_all[0, piece]
        )
    mixed = mix[...]
    hidden = x_ref[...].astype(F32) + dot(mixed, weight_out)
    xhat, scale = centre(hidden)
    routed = (xhat * gain).astype(BF16)
    logits = jnp.where(lanes < blks, dot(routed, small), MASKED)
    powers = jnp.exp(logits - jnp.max(logits, axis=1, keepdims=True))
    probs = powers / jnp.sum(powers, axis=1, keepdims=True)
    lanes_f = lanes.astype(F32)
    hots = [lanes_f == e for e in e_cols]
    gates = [jnp.sum(jnp.where(hot, probs, 0.0), axis=1, keepdims=True) for hot in hots]
    gate_mats = [split_high_low(g, lanes) for g in gates]

    rs[:, :, 0:model] = dot(pick_any, routed).astype(BF16).reshape(blks, capacity, model)
    rs[:, :, model : model + LANES] = (
        (dot(pick[0], gate_mats[0]) + dot(pick[1], gate_mats[1]))
        .astype(BF16)
        .reshape(blks, capacity, LANES)
    )
    r_copies = blk_copies(rs, ra, r_send, r_recv)
    start(r_copies)
    ra[blk] = rs[blk]
    acc_out[...] = jnp.zeros_like(acc_out)
    acc_row[...] = jnp.zeros_like(acc_row)
    finish(dos_copies)
    finish(r_copies)

    arrived_rows = ra[...].reshape(slots, model + LANES)
    out_rows = doa[...].reshape(slots, model)
    gate_col = join_high_low(arrived_rows, model)
    rx[head, :, 0:model] = arrived_rows[:, 0:model]
    rx[head, :, model : 2 * model] = (out_rows.astype(F32) * gate_col).astype(BF16)
    half_ff = wout_ref.shape[0] // 4
    for copy in fetched[4:]:
        copy.wait()

    @pl.loop(0, 4)
    def _(chunk):
        first = pl.multiple_of(chunk * half_ff, half_ff)
        into = win_ref[:, pl.ds(first, half_ff)]
        outof = wout_ref[pl.ds(first, half_ff), :]
        act, slope = gelu_parts(dot(rx[head, :, 0:model], into))
        acc_out[...] += dot(act.astype(BF16), outof)
        d_act = dot(rx[head, :, model : 2 * model], outof, (1, 1))
        acc_row[...] += dot((slope * d_act).astype(BF16), into, (1, 1))

    result = acc_out[...].astype(BF16)
    d_gate = jnp.sum(out_rows.astype(F32) * result.astype(F32), axis=1, keepdims=True)
    dr[:, :, 0:model] = acc_row[...].astype(BF16).reshape(blks, capacity, model)
    dr[:, :, model : model + LANES] = split_high_low(d_gate, lane_ids((slots, LANES))).reshape(
        blks, capacity, LANES
    )
    dr_copies = blk_copies(dr, da, dr_send, dr_recv)
    start(dr_copies)
    da[blk] = dr[blk]
    po[...] = result.reshape(blks, capacity, model)
    po_copies = blk_copies(po, pa, po_send, po_recv)
    pa[blk] = po[blk]
    core = lax.rem(head, 2)
    sibling, across = head - core + 1 - core, around(head, 2, heads)
    to_sibling = remote(rx.at[head], rx.at[head], rx_send.at[0], rx_recv.at[0], sibling, blk)
    to_across = remote(rx.at[head], rx.at[head], rx_send.at[1], rx_recv.at[1], across, blk)
    to_across.start()
    to_sibling.start()

    finish(dr_copies)
    start(po_copies)
    back = da[...].reshape(slots, model + LANES)
    d_routed = dot(put_any, back[:, 0:model])
    back_gate = back[:, model : model + LANES]
    d_gates = [join_high_low(dot(p, back_gate), 0) for p in put]
    d_probs = jnp.where(hots[0], d_gates[0], 0.0) + jnp.where(hots[1], d_gates[1], 0.0)
    d_logits = probs * (d_probs - jnp.sum(probs * d_probs, axis=1, keepdims=True))
    d_high = d_logits.astype(BF16)
    d_low = (d_logits - d_high.astype(F32)).astype(BF16)
    d_routed = d_routed + dot(d_high, small, (1, 1)) + dot(d_low, small, (1, 1))
    d_hidden = d_out + centre_back(d_routed * gain, xhat, scale)
    dh_ref[...] = d_hidden
    d_attn = d_hidden.astype(BF16)
    d_mixed = dot(d_attn, weight_out, (1, 1)).astype(BF16)
    for piece in range(heads):
        dms[piece] = d_mixed[:, piece * LANES : (piece + 1) * LANES]
    dm_copies = plane_copies(lambda to_y, to_head: dms.at[to_head], dma_all.at[y, head], dm_send, dm_recv)
    start(dm_copies)
    dma_all[y, head] = dms[head]

    d_weight = dot(mixed, d_attn, (0, 0)).astype(BF16)
    for b in range(blks):
        grads_ref[b, :, 0:model] = d_weight[(b ^ 1) * HALF : ((b ^ 1) + 1) * HALF, :]
    last = (lanes == blks).astype(BF16)
    d_small = dot(routed, d_high, (0, 0)) + dot((d_routed * xhat).astype(BF16), last, (0, 0))
    grads_ref[:, :, model : model + LANES] = d_small.astype(BF16).reshape(blks, HALF, LANES)
    finish(po_copies)
    parts = pa[...].reshape(slots, model)
    mixture = gates[0] * dot(put[0], parts) + gates[1] * dot(put[1], parts)
    out_ref[...] = (hidden + mixture).astype(BF16)

    arrived(rx.at[across], rx_recv.at[1])
    forward = remote(rx.at[across], rx.at[across], rx_send.at[2], rx_recv.at[2], sibling, blk)
    forward.start()
    finish(dm_copies)
    to_sibling.wait()
    to_across.wait_send()
    forward.wait()


def call_middle(x, o, wo, routes, rank, d_out, win, wout, heads, blks):
    tokens, model = x.shape
    capacity = 2 * tokens // blks
    slots = capacity * blks
    wide = model + LANES

    def rows(width):
        return pltpu.VMEM((blks, capacity, width), BF16)

    def block(*lead):
        return pltpu.VMEM((*lead, tokens, LANES), BF16)

    return pl.pallas_call(
        functools.partial(middle_kernel, heads, blks),
        out_shape=(
            jax.ShapeDtypeStruct((tokens, model), BF16),
            jax.ShapeDtypeStruct((tokens, model), F32),
            jax.ShapeDtypeStruct((2, heads, tokens, LANES), BF16),
            jax.ShapeDtypeStruct((blks, model // blks, wide), BF16),
            jax.ShapeDtypeStruct((heads, slots, 2 * model), BF16),
        ),
        in_specs=hbm_specs(1) + vmem_specs(2) + hbm_specs(5),
        out_specs=tuple(vmem_specs(5)),
        scratch_shapes=[
            pltpu.VMEM((tokens, model), BF16),
            pltpu.VMEM((2, tokens), jnp.int32),
            pltpu.VMEM((1, tokens), jnp.int32),
            pltpu.VMEM((tokens, model), F32),
            pltpu.VMEM(win.shape, BF16),
            pltpu.VMEM(wout.shape, BF16),
            pltpu.VMEM((tokens, tokens), F32),
            dma(6),
            block(2, heads), rows(model), rows(model), rows(wide), rows(wide), rows(model), rows(model),
            rows(wide), rows(wide), block(heads),
            pltpu.VMEM((slots, model), F32), pltpu.VMEM((slots, model), F32),
            pltpu.VMEM((tokens, model), BF16),
            dma(2 * heads), dma(2 * heads), dma(blks), dma(blks), dma(blks), dma(blks), dma(blks), dma(blks),
            dma(blks), dma(blks), dma(2 * heads), dma(2 * heads), dma(3), dma(3),
        ],
        compiler_params=pltpu.CompilerParams(
            collective_id=2, has_side_effects=True, vmem_limit_bytes=20 * MIB
        ),
        name="experts",
    )(*in_hbm(x), o, wo, *in_hbm(routes.T, rank, d_out, win, wout))


def last_kernel(
    heads, blks,
    x_hbm, dh_ref, dq_ref, dkv_ref, xa_ref, wa_ref, w_hbm, g1_hbm, grads_ref, rx_ref, win_hbm, wout_hbm,
    dx_ref, dw_ref, shared_ref, din_ref, dout_ref,
    x_ref, w_ref, g1_ref, win_ref, wout_ref, in_sem,
    gain_tile, far_all, near_send_buf, near_all, pair_all, dq_all, us, ua, gs, ga, gh, w1, w2s, w2, w3,
    q_send, q_recv, pair_send, pair_recv, far_send, far_recv, near_send, near_recv,
    u_send, u_recv, g_send, g_recv, gh_send, gh_recv, w1_send, w1_recv, w2_send, w2_recv,
    w3_send, w3_recv, e_send, e_recv,
):
    head, blk, z, y = place()
    planes = blks // 2
    tokens, model = x_ref.shape
    rows = w_ref.shape[0]
    wanted = (
        (win_hbm, win_ref), (wout_hbm, wout_ref), (x_hbm, x_ref), (w_hbm, w_ref), (g1_hbm, g1_ref)
    )
    fetched = [
        pltpu.make_async_copy(src, dst, in_sem.at[i]) for i, (src, dst) in enumerate(wanted)
    ]
    for copy in fetched:
        copy.start()
    greet(
        [(around(head, k, heads), blk) for k in range(1, heads)]
        + [(head, around(blk, k, blks)) for k in range(1, blks)]
    )

    def start(copies):
        for copy in copies:
            copy.start()

    def finish(copies):
        for copy in copies:
            copy.wait()

    other_y = around(y, 1, 2)
    pair = 2 * z + other_y
    above, below = z < planes - 1, z > 0
    directions = ((1, above, below, 0), (-1, below, above, 2))

    def far_copy(step, slot, side):
        span = 2 * (z + 2 * step) + side
        return remote(
            dkv_ref.at[span], far_all.at[slot + side],
            far_send.at[slot + side], far_recv.at[slot + side], head, 2 * (z + step) + y,
        )

    def near_copy(step, slot, side):
        return remote(
            near_send_buf.at[slot + side], near_all.at[slot // 2, y],
            near_send.at[slot + side], near_recv.at[slot // 2, y], head, 2 * (z + step) + side,
        )

    def two_away(step):
        return z + 2 * step < planes if step > 0 else z + 2 * step >= 0

    for step, there, back, slot in directions:

        @pl.when(two_away(step))
        def _():
            for side in range(2):
                far_copy(step, slot, side).start()

    pair_copy = remote(dkv_ref.at[pair], pair_all, pair_send, pair_recv, head, pair)
    pair_copy.start()
    q_copy = remote(dq_ref.at[other_y], dq_all, q_send, q_recv, head, pair)
    q_copy.start()
    w1_copies = [
        remote(
            grads_ref.at[:, around(head, k, heads)], w1.at[head],
            w1_send.at[k], w1_recv.at[k], around(head, k, heads), blk,
        )
        for k in range(1, heads)
    ]
    start(w1_copies)
    w1[head] = grads_ref[:, head]

    core = lax.rem(head, 2)
    sibling = head - core + 1 - core
    ff_half = wout_ref.shape[0] // 2
    ff_step = ff_half // 4

    def expert_chunk(chunk):
        here = pl.multiple_of(core * ff_half + chunk * ff_step, ff_step)
        there = pl.multiple_of(chunk * ff_step, ff_step)
        into = win_ref[:, pl.ds(here, ff_step)]
        outof = wout_ref[pl.ds(here, ff_step), :]
        d_in = jnp.zeros((model, ff_step), F32)
        d_out = jnp.zeros((ff_step, model), F32)
        for source in range(heads):
            rows_in = rx_ref[source, :, 0:model]
            grads_out = rx_ref[source, :, model : 2 * model]
            act, slope = gelu_parts(dot(rows_in, into))
            d_act = dot(grads_out, outof, (1, 1))
            d_in = d_in + dot(rows_in, (slope * d_act).astype(BF16), (0, 0))
            d_out = d_out + dot(act.astype(BF16), grads_out, (0, 0))
        din_ref[core, :, pl.ds(there, ff_step)] = d_in.astype(BF16)
        dout_ref[core, pl.ds(there, ff_step), :] = d_out.astype(BF16)

    finish(fetched)

    @pl.loop(0, 2)
    def _(chunk):
        expert_chunk(chunk)

    for step, there, back, slot in directions:

        @pl.when(there)
        def _():
            for side in range(2):
                near_send_buf[slot + side] = dkv_ref[2 * (z + step) + side]

        @pl.when(jnp.logical_and(there, back))
        def _():
            for side in range(2):
                arrived(far_all.at[slot + side], far_recv.at[slot + side])
                near_send_buf[slot + side] = (
                    near_send_buf[slot + side].astype(F32) + far_all[slot + side].astype(F32)
                ).astype(BF16)

        @pl.when(there)
        def _():
            for side in range(2):
                near_copy(step, slot, side).start()

    @pl.loop(2, 4)
    def _(chunk):
        expert_chunk(chunk)

    e_copies = [
        remote(din_ref.at[core], din_ref.at[core], e_send.at[0], e_recv.at[0], sibling, blk),
        remote(dout_ref.at[core], dout_ref.at[core], e_send.at[1], e_recv.at[1], sibling, blk),
    ]
    start(e_copies)

    pair_copy.wait()
    q_copy.wait()
    for step, there, back, slot in directions:

        @pl.when(back)
        def _():
            for side in range(2):
                arrived(near_all.at[slot // 2, side], near_recv.at[slot // 2, side])

        @pl.when(jnp.logical_not(back))
        def _():
            near_all[slot // 2] = jnp.zeros(near_all.shape[1:], BF16)

    lanes = lane_ids((tokens, LANES))
    even = y == 0
    weight = wa_ref[...].reshape(model, 3 * LANES)
    g_sum = jnp.zeros((model, 3 * LANES), F32)
    for piece in range(heads):
        span = slice(piece * tokens, (piece + 1) * tokens)
        own = dkv_ref[blk, span, :].astype(F32)
        other = pair_all[span, :].astype(F32)
        kv_grads = [
            jnp.where(even, own, other) + near_all[0, 0, span, :].astype(F32) + near_all[1, 0, span, :].astype(F32),
            jnp.where(even, other, own) + near_all[0, 1, span, :].astype(F32) + near_all[1, 1, span, :].astype(F32),
        ]
        q_own = dq_ref[y, span, :]
        q_other = dq_all[span, :]
        own_lanes = (lanes < HALF) == even
        q_grads = jnp.where(own_lanes, q_own, q_other)
        made = jnp.concatenate([kv_grads[0].astype(BF16), kv_grads[1].astype(BF16), q_grads], axis=1)
        us[piece] = dot(made, weight, (1, 1)).astype(BF16)
        g_sum = g_sum + dot(xa_ref[piece], made, (0, 0))
    u_copies = [
        remote(
            us.at[around(head, k, heads)], ua.at[head],
            u_send.at[k], u_recv.at[k], around(head, k, heads), blk,
        )
        for k in range(1, heads)
    ]
    start(u_copies)
    ua[head] = us[head]
    gs[...] = g_sum.astype(BF16).reshape(gs.shape)
    g_copies = [
        remote(
            gs.at[around(blk, k, blks)], ga.at[blk],
            g_send.at[k], g_recv.at[k], head, around(blk, k, blks),
        )
        for k in range(1, blks)
    ]
    start(g_copies)
    ga[blk] = gs[blk]

    finish(w1_copies)
    summed = w1[0].astype(F32)
    for source in range(1, heads):
        summed = summed + w1[source].astype(F32)
    w2s[...] = summed.astype(BF16)
    w2_copies = [
        remote(
            w2s.at[around(blk, k, blks)], w2.at[blk],
            w2_send.at[k], w2_recv.at[k], head, around(blk, k, blks),
        )
        for k in range(1, blks)
    ]
    start(w2_copies)
    w2[blk] = w2s[blk]

    finish(u_copies)
    grad = ua[0].astype(F32)
    for source in range(1, heads):
        grad = grad + ua[source].astype(F32)
    xhat, scale = centre(x_ref[...].astype(F32))
    dx_ref[...] = dh_ref[...] + centre_back(grad, xhat, scale)

    finish(g_copies)
    total = ga[0].astype(F32)
    for source in range(1, blks):
        total = total + ga[source].astype(F32)
    gh[head] = total.astype(BF16)
    gh_copies = [
        remote(gh.at[head], gh.at[head], gh_send.at[k], gh_recv.at[k], around(head, k, heads), blk)
        for k in range(1, heads)
    ]
    start(gh_copies)
    finish(w2_copies)
    part = w2[0].astype(F32)
    for source in range(1, blks):
        part = part + w2[source].astype(F32)
    w3[head] = part.astype(BF16)
    w3_copies = [
        remote(w3.at[head], w3.at[head], w3_send.at[k], w3_recv.at[k], around(head, k, heads), blk)
        for k in range(1, heads)
    ]
    start(w3_copies)

    gain_tile[...] = jnp.zeros_like(gain_tile)
    gain_tile[0:1, 0:rows] = g1_ref[...].astype(F32)
    gain = jnp.transpose(jnp.broadcast_to(gain_tile[0:1, :], (LANES, LANES)))[:rows]
    low_half = lane_ids((rows, LANES)) < HALF
    finish(gh_copies)
    d_gain = jnp.zeros((rows, LANES), F32)
    for source in range(heads):
        both = [gh[source, :, i * LANES : (i + 1) * LANES].astype(F32) for i in range(3)]
        grads = (
            both[2] * HS ** (-0.5),
            jnp.where(low_half, both[0], both[1]),
            pltpu.roll(jnp.where(low_half, both[1], both[0]), HALF, 1),
        )
        for which, value in enumerate(grads):
            columns = slice(which * model + source * LANES, which * model + (source + 1) * LANES)
            d_gain = d_gain + value * w_ref[:, columns].astype(F32)
            dw_ref[:, columns] = value * gain
    finish(w3_copies)
    shared = w3[...].reshape(rows, w3.shape[-1]).astype(F32)
    shared_ref[:, 0:model] = shared[:, 0:model]
    gain_col = jnp.sum(d_gain, axis=1, keepdims=True)
    shared_ref[:, model : model + LANES] = jnp.where(
        lane_ids((rows, LANES)) == blks + 1, gain_col, shared[:, model : model + LANES]
    )
    for step, there, back, slot in directions:

        @pl.when(two_away(step))
        def _():
            for side in range(2):
                far_copy(step, slot, side).wait_send()

        @pl.when(there)
        def _():
            for side in range(2):
                near_copy(step, slot, side).wait_send()

    finish(e_copies)


def call_last(x, dh, dq, dkv, xa, wa, w_qkv, g1, grads, rx, win, wout, heads, blks):
    tokens, model = x.shape
    span = tokens * heads
    rows = w_qkv.shape[0]
    wide = model + LANES
    part = rows // heads
    ff = wout.shape[0]

    def block(*lead):
        return pltpu.VMEM((*lead, span, LANES), BF16)

    return pl.pallas_call(
        functools.partial(last_kernel, heads, blks),
        out_shape=(
            jax.ShapeDtypeStruct((tokens, model), F32),
            jax.ShapeDtypeStruct((rows, 3 * model), F32),
            jax.ShapeDtypeStruct((rows, wide), F32),
            jax.ShapeDtypeStruct((2, model, ff // 2), BF16),
            jax.ShapeDtypeStruct((2, ff // 2, model), BF16),
        ),
        in_specs=hbm_specs(1) + vmem_specs(5) + hbm_specs(2) + vmem_specs(2) + hbm_specs(2),
        out_specs=tuple(vmem_specs(5)),
        scratch_shapes=[
            pltpu.VMEM((tokens, model), BF16),
            pltpu.VMEM((rows, 3 * model), BF16),
            pltpu.VMEM((1, rows), BF16),
            pltpu.VMEM(win.shape, BF16),
            pltpu.VMEM(wout.shape, BF16),
            dma(5),
            pltpu.VMEM((8, LANES), F32),
            block(4), block(4), block(2, 2), block(), block(),
            pltpu.VMEM((heads, tokens, model), BF16), pltpu.VMEM((heads, tokens, model), BF16),
            pltpu.VMEM((blks, rows, 3 * LANES), BF16), pltpu.VMEM((blks, rows, 3 * LANES), BF16),
            pltpu.VMEM((heads, rows, 3 * LANES), BF16),
            pltpu.VMEM((heads, blks, part, wide), BF16), pltpu.VMEM((blks, part, wide), BF16),
            pltpu.VMEM((blks, part, wide), BF16), pltpu.VMEM((heads, part, wide), BF16),
            pltpu.SemaphoreType.DMA, pltpu.SemaphoreType.DMA, pltpu.SemaphoreType.DMA, pltpu.SemaphoreType.DMA,
            dma(4), dma(4), dma(4), dma(2, 2),
            dma(heads), dma(heads), dma(blks), dma(blks), dma(heads), dma(heads), dma(heads), dma(heads),
            dma(blks), dma(blks), dma(heads), dma(heads), dma(2), dma(2),
        ],
        compiler_params=pltpu.CompilerParams(
            collective_id=3, has_side_effects=True, vmem_limit_bytes=24 * MIB
        ),
        name="last",
    )(
        *in_hbm(x), dh, dq.reshape(2, span, LANES), dkv, xa, wa, *in_hbm(w_qkv, g1.reshape(1, rows)),
        grads.reshape(blks, heads, part, wide), rx, *in_hbm(win, wout),
    )


def finish_kernel(
    experts,
    y_ref, dx_ref, dw_ref, shared_ref, din_ref, dout_ref,
    y_out, dx_out, g1_out, dw_out, dwo_out, g2_out, wr_out, din_out, dout_out,
    tile, wr, g2, g1, din, dout, sem, wide_sem,
):
    rows = shared_ref.shape[0]
    model = dx_ref.shape[1]
    copies = [
        pltpu.make_async_copy(dx_ref, dx_out, sem.at[0]),
        pltpu.make_async_copy(dw_ref, dw_out, sem.at[1]),
        pltpu.make_async_copy(shared_ref.at[:, pl.ds(0, model)], dwo_out, sem.at[2]),
        pltpu.make_async_copy(y_ref, y_out, sem.at[6]),
    ]
    for copy in copies:
        copy.start()
    half = dout_ref.shape[1]
    quarter = half // 2
    for piece in range(4):
        down = slice(piece * quarter, (piece + 1) * quarter)
        dout[down, :] = dout_ref[piece // 2, (piece % 2) * quarter : (piece % 2 + 1) * quarter, :].astype(F32)
        copies.append(pltpu.make_async_copy(dout.at[down], dout_out.at[down], wide_sem.at[piece]))
        copies[-1].start()
    step = model // 4
    for piece in range(4):
        down = slice(piece * step, (piece + 1) * step)
        for side in range(2):
            din[down, side * half : (side + 1) * half] = din_ref[side, down, :].astype(F32)
        copies.append(pltpu.make_async_copy(din.at[down], din_out.at[down], wide_sem.at[4 + piece]))
        copies[-1].start()
    tile[...] = jnp.zeros_like(tile)
    tile[0:rows, :] = shared_ref[:, model : model + LANES]
    across = jnp.transpose(tile[...])[:, 0:rows]
    wr[...] = across[0:experts]
    g2[...] = across[experts : experts + 1]
    g1[...] = across[experts + 1 : experts + 2]
    for index, (src, dst) in enumerate(((wr, wr_out), (g2, g2_out), (g1, g1_out))):
        copies.append(pltpu.make_async_copy(src, dst, sem.at[3 + index]))
        copies[-1].start()
    for copy in copies:
        copy.wait()


def call_finish(output, dx, dw, shared, d_in, d_out):
    rows = shared.shape[0]
    model = dx.shape[1]
    experts = model // rows
    ff = 2 * d_out.shape[1]
    return pl.pallas_call(
        functools.partial(finish_kernel, experts),
        out_shape=(
            jax.ShapeDtypeStruct(output.shape, BF16),
            jax.ShapeDtypeStruct(dx.shape, F32),
            jax.ShapeDtypeStruct((1, rows), F32),
            jax.ShapeDtypeStruct(dw.shape, F32),
            jax.ShapeDtypeStruct((rows, model), F32),
            jax.ShapeDtypeStruct((1, rows), F32),
            jax.ShapeDtypeStruct((experts, rows), F32),
            jax.ShapeDtypeStruct((model, ff), F32),
            jax.ShapeDtypeStruct((ff, model), F32),
        ),
        in_specs=vmem_specs(6),
        out_specs=tuple(hbm_specs(9)),
        scratch_shapes=[
            pltpu.VMEM((LANES, LANES), F32),
            pltpu.VMEM((experts, rows), F32),
            pltpu.VMEM((1, rows), F32),
            pltpu.VMEM((1, rows), F32),
            pltpu.VMEM((model, ff), F32),
            pltpu.VMEM((ff, model), F32),
            dma(7),
            dma(8),
        ],
        compiler_params=pltpu.CompilerParams(vmem_limit_bytes=16 * MIB),
        name="finish",
    )(output, dx, dw, shared, d_in, d_out)


def local_kernels(
    inputs, ln1_gain, w_qkv, w_out, ln2_gain, w_router,
    expert_in, expert_out, routes, priority, doc_lengths, d_out,
):
    heads, blks = lax.axis_size("head"), lax.axis_size("blk")
    model = inputs.shape[1]
    tokens = inputs.shape[0]
    win, wout = expert_in[0], expert_out[0]
    q, kv, xa, wa, wo, kvt, bounds = call_qkv(
        inputs, w_qkv, ln1_gain, w_out, w_router, ln2_gain, doc_lengths, heads, blks
    )
    o, o_low, lse = call_forward(bounds, q, kv, kvt)
    output, dh, d_o, grads, rx = call_middle(
        inputs, o_low.reshape(2, heads, tokens, LANES), wo.reshape(model, model + LANES),
        routes, priority, d_out, win, wout, heads, blks,
    )
    dq, dkv = call_backward(bounds, q, kv, kvt, d_o, o, lse)
    ends = call_last(
        inputs, dh, dq, dkv, xa, wa, w_qkv, ln1_gain, grads, rx, win, wout, heads, blks
    )
    output, d_inputs, d_gain_one, d_qkv, d_out_proj, d_gain_two, d_router, d_in, d_out_weight = call_finish(output, *ends)
    return (
        output,
        d_inputs,
        d_gain_one.reshape(-1),
        d_qkv,
        d_out_proj,
        d_gain_two.reshape(-1),
        d_router.T,
        d_in[None],
        d_out_weight[None],
    )


def solution(mesh):
    in_specs = (
        P(("blk", "head"), None),
        P("blk"),
        P("blk", None),
        P("blk", None),
        P("blk"),
        P("blk", None),
        P("blk", None, None),
        P("blk", None, None),
        P(("blk", "head"), None),
        P(("blk", "head"), None),
        P(),
        P(("blk", "head"), None),
    )
    out_specs = (
        P(("blk", "head"), None),
        P(("blk", "head"), None),
        P("blk"),
        P("blk", None),
        P("blk", None),
        P("blk"),
        P("blk", None),
        P("blk", None, None),
        P("blk", None, None),
    )
    fits = mesh.shape["head"] == 4 and mesh.shape["blk"] == 8
    body = local_kernels if fits else local
    return jax.shard_map(body, mesh=mesh, in_specs=in_specs, out_specs=out_specs, check_vma=False)
```

```python
import functools
import math

import jax
import jax.numpy as jnp
from jax import lax
from jax.experimental import pallas as pl
from jax.experimental.pallas import tpu as pltpu
from jax.sharding import PartitionSpec as P

HS = 64
KEY_BLOCK = 2048


PRECISE = lax.Precision.HIGHEST
MASKED = -1e30
EPSILON = 1e-06


def layer_norm(values, gain):
    average = jnp.mean(values, axis=-1, keepdims=True)
    centred = values - average
    spread = jnp.mean(centred * centred, axis=-1, keepdims=True)
    return centred * lax.rsqrt(spread + EPSILON) * gain


def gelu_exact(values):
    return jax.nn.gelu(values, approximate=False)


def router(row_block, weight):
    return jax.nn.softmax(jnp.dot(row_block, weight, precision=PRECISE), axis=-1)


def doc_index(positions, doc_lengths):
    places = jnp.arange(doc_lengths.shape[0], dtype=jnp.int32)
    starts = jnp.sum(jnp.where(places[None, :] < places[:, None], doc_lengths[None, :], 0), axis=1)
    at_most = (starts[None, :] <= positions[:, None]).astype(jnp.int32)
    return jnp.sum(at_most, axis=1) - 1


def slot_table(route_rows, ranking, capacity):
    token_count = route_rows.shape[0]
    expert = jnp.transpose(route_rows).reshape(-1)
    pair_order = (jnp.arange(2, dtype=jnp.int32)[:, None] * token_count + ranking[None, :]).reshape(
        -1
    )
    before = (expert[:, None] == expert[None, :]) & (pair_order[None, :] < pair_order[:, None])
    position = jnp.sum(before.astype(jnp.int32), axis=1)
    slot_ids = jnp.where(position < capacity, expert * capacity + position, -1)
    return slot_ids.reshape(2, token_count)


def keep_state(current):
    return current


def local(
    inputs,
    ln1_gain,
    w_qkv,
    w_out,
    ln2_gain,
    w_router,
    expert_in,
    expert_out,
    routes,
    priority,
    doc_lengths,
    d_out,
):
    blk_size = lax.axis_size("blk")
    tok_rows = inputs.shape[0]
    model_width = inputs.shape[1]
    capacity = 2 * tok_rows // blk_size
    slot_total = blk_size * capacity
    gain_one, qkv_weight, out_weight, gain_two, router_weight = (
        lax.all_gather(ln1_gain, "blk", axis=0, tiled=True),
        lax.all_gather(w_qkv, "blk", axis=0, tiled=True),
        lax.all_gather(w_out, "blk", axis=0, tiled=True),
        lax.all_gather(ln2_gain, "blk", axis=0, tiled=True),
        lax.all_gather(w_router, "blk", axis=0, tiled=True),
    )
    input_rows = inputs.astype(jnp.float32)
    normed_one, norm_one_pull = jax.vjp(layer_norm, input_rows, gain_one.astype(jnp.float32))
    normed_low = normed_one.astype(jnp.bfloat16)
    qkv_rows = jnp.dot(normed_low, qkv_weight, preferred_element_type=jnp.float32).astype(
        jnp.bfloat16
    )
    query_heads, key_heads, value_heads = (
        lax.all_to_all(qkv_rows[:, :model_width], "head", split_axis=1, concat_axis=0, tiled=True),
        lax.all_to_all(
            qkv_rows[:, model_width : 2 * model_width],
            "head",
            split_axis=1,
            concat_axis=0,
            tiled=True,
        ),
        lax.all_to_all(
            qkv_rows[:, 2 * model_width :], "head", split_axis=1, concat_axis=0, tiled=True
        ),
    )
    span_rows = query_heads.shape[0]
    head_count = query_heads.shape[1] // HS
    key_all, value_all = (
        lax.all_gather(key_heads, "blk", axis=0, tiled=True),
        lax.all_gather(value_heads, "blk", axis=0, tiled=True),
    )
    total_rows = key_all.shape[0]
    block_count = total_rows // KEY_BLOCK
    scale_factor = HS ** (-0.5)
    query_pos = lax.axis_index("blk") * span_rows + jnp.arange(span_rows, dtype=jnp.int32)
    query_docs = doc_index(query_pos, doc_lengths)
    queries = query_heads.reshape(span_rows, head_count, HS)

    def block_parts(block_index, key_source, value_source):
        first_key = block_index * KEY_BLOCK
        key_rows = lax.dynamic_slice_in_dim(key_source, first_key, KEY_BLOCK, 0).reshape(
            KEY_BLOCK, head_count, HS
        )
        value_rows = lax.dynamic_slice_in_dim(value_source, first_key, KEY_BLOCK, 0).reshape(
            KEY_BLOCK, head_count, HS
        )
        key_docs = doc_index(first_key + jnp.arange(KEY_BLOCK, dtype=jnp.int32), doc_lengths)
        is_live = (key_docs[0] <= query_docs[-1]) & (key_docs[-1] >= query_docs[0])
        same_doc = query_docs[:, None] == key_docs[None, :]
        return (first_key, key_rows, value_rows, same_doc, is_live)

    def block_scores(key_rows, same_doc):
        raw_scores = (
            jnp.einsum("qhd,khd->hqk", queries, key_rows, preferred_element_type=jnp.float32)
            * scale_factor
        )
        return jnp.where(same_doc[None], raw_scores, MASKED)

    def stat_step(block_index, loop_state):
        first_key, key_rows, value_rows, same_doc, is_live = block_parts(
            block_index, key_all, value_all
        )

        def stat_update(current):
            running_max, running_sum = current
            scores = block_scores(key_rows, same_doc)
            new_max = jnp.maximum(running_max, jnp.max(scores, axis=2))
            exp_terms = jnp.where(same_doc[None], jnp.exp(scores - new_max[:, :, None]), 0.0)
            return (
                new_max,
                running_sum * jnp.exp(running_max - new_max) + jnp.sum(exp_terms, axis=2),
            )

        return lax.cond(is_live, stat_update, keep_state, loop_state)

    start_state = (
        jnp.full((head_count, span_rows), MASKED, jnp.float32),
        jnp.zeros((head_count, span_rows), jnp.float32),
    )
    running_max, running_sum = lax.fori_loop(0, block_count, stat_step, start_state)
    log_total = running_max + jnp.log(running_sum)

    def out_step(block_index, loop_state):
        first_key, key_rows, value_rows, same_doc, is_live = block_parts(
            block_index, key_all, value_all
        )

        def out_update(current):
            scores = block_scores(key_rows, same_doc)
            weights = jnp.where(
                same_doc[None], jnp.exp(scores - log_total[:, :, None]), 0.0
            ).astype(jnp.bfloat16)
            return current + jnp.einsum(
                "hqk,khd->qhd", weights, value_rows, preferred_element_type=jnp.float32
            )

        return lax.cond(is_live, out_update, keep_state, loop_state)

    mixed_full = lax.fori_loop(
        0, block_count, out_step, jnp.zeros((span_rows, head_count, HS), jnp.float32)
    )
    mixed_low = mixed_full.reshape(span_rows, head_count * HS).astype(jnp.bfloat16)
    mixed_tokens = lax.all_to_all(mixed_low, "head", split_axis=0, concat_axis=1, tiled=True)
    attended = jnp.dot(mixed_tokens, out_weight, preferred_element_type=jnp.float32)
    hidden_one = input_rows + attended
    normed_two, norm_two_pull = jax.vjp(layer_norm, hidden_one, gain_two.astype(jnp.float32))
    routed_low = normed_two.astype(jnp.bfloat16)
    router_probs, router_pull = jax.vjp(
        router, routed_low.astype(jnp.float32), router_weight.astype(jnp.float32)
    )
    slot_ids = slot_table(routes, priority[0], capacity)
    select = (
        slot_ids[:, :, None] == jnp.arange(slot_total, dtype=jnp.int32)[None, None, :]
    ).astype(jnp.bfloat16)
    send_rows = jnp.einsum(
        "kts,td->sd", select, routed_low, preferred_element_type=jnp.float32
    ).astype(jnp.bfloat16)
    expert_rows = lax.all_to_all(
        send_rows.reshape(blk_size, capacity, model_width),
        "blk",
        split_axis=0,
        concat_axis=0,
        tiled=True,
    ).reshape(slot_total, model_width)
    weight_in = expert_in[0]
    weight_out = expert_out[0]
    pre_act = jnp.dot(expert_rows, weight_in, preferred_element_type=jnp.float32)
    hidden_act, gelu_pull = jax.vjp(gelu_exact, pre_act)
    hidden_low = hidden_act.astype(jnp.bfloat16)
    expert_result = jnp.dot(hidden_low, weight_out, preferred_element_type=jnp.float32).astype(
        jnp.bfloat16
    )
    slot_result = lax.all_to_all(
        expert_result.reshape(blk_size, capacity, model_width),
        "blk",
        split_axis=0,
        concat_axis=0,
        tiled=True,
    ).reshape(slot_total, model_width)
    pair_result = jnp.einsum("kts,sd->ktd", select, slot_result, preferred_element_type=jnp.float32)
    route_hot = (routes[:, :, None] == jnp.arange(blk_size, dtype=jnp.int32)[None, None, :]).astype(
        jnp.float32
    )
    gate_vals = jnp.sum(router_probs[:, None, :] * route_hot, axis=2)
    mixture = gate_vals[:, 0, None] * pair_result[0] + gate_vals[:, 1, None] * pair_result[1]
    output = (hidden_one + mixture).astype(jnp.bfloat16)
    d_gates = jnp.transpose(jnp.sum(d_out[None] * pair_result, axis=2))
    d_probs = jnp.sum(d_gates[:, :, None] * route_hot, axis=1)
    pair_grads = (jnp.transpose(gate_vals)[:, :, None] * d_out[None]).astype(jnp.bfloat16)
    slot_grads = jnp.einsum(
        "kts,ktd->sd", select, pair_grads, preferred_element_type=jnp.float32
    ).astype(jnp.bfloat16)
    result_grads = lax.all_to_all(
        slot_grads.reshape(blk_size, capacity, model_width),
        "blk",
        split_axis=0,
        concat_axis=0,
        tiled=True,
    ).reshape(slot_total, model_width)
    d_hidden_act = jnp.dot(result_grads, weight_out.T, preferred_element_type=jnp.float32)
    d_weight_out = jnp.dot(hidden_low.T, result_grads, preferred_element_type=jnp.float32)
    d_preact = gelu_pull(d_hidden_act)[0].astype(jnp.bfloat16)
    d_weight_in = jnp.dot(expert_rows.T, d_preact, preferred_element_type=jnp.float32)
    row_grads = jnp.dot(d_preact, weight_in.T, preferred_element_type=jnp.float32).astype(
        jnp.bfloat16
    )
    slot_back = lax.all_to_all(
        row_grads.reshape(blk_size, capacity, model_width),
        "blk",
        split_axis=0,
        concat_axis=0,
        tiled=True,
    ).reshape(slot_total, model_width)
    d_routed = jnp.einsum("kts,sd->td", select, slot_back, preferred_element_type=jnp.float32)
    d_routed_router, d_router = router_pull(d_probs)
    d_hidden_norm, d_gain_two = norm_two_pull(d_routed + d_routed_router)
    d_hidden_one = d_out + d_hidden_norm
    attn_grads = d_hidden_one.astype(jnp.bfloat16)
    d_out_weight = jnp.dot(mixed_tokens.T, attn_grads, preferred_element_type=jnp.float32)
    mixed_grads = jnp.dot(attn_grads, out_weight.T, preferred_element_type=jnp.float32).astype(
        jnp.bfloat16
    )
    head_grads = lax.all_to_all(mixed_grads, "head", split_axis=1, concat_axis=0, tiled=True)
    out_grads = head_grads.reshape(span_rows, head_count, HS)
    row_delta = jnp.transpose(jnp.sum(out_grads.astype(jnp.float32) * mixed_full, axis=2))
    key_back, value_back = (
        lax.all_gather(key_heads, "blk", axis=0, tiled=True),
        lax.all_gather(value_heads, "blk", axis=0, tiled=True),
    )

    def grad_step(block_index, loop_state):
        first_key, key_rows, value_rows, same_doc, is_live = block_parts(
            block_index, key_back, value_back
        )

        def grad_update(current):
            query_grad, key_grad, value_grad = current
            scores = block_scores(key_rows, same_doc)
            weights = jnp.where(same_doc[None], jnp.exp(scores - log_total[:, :, None]), 0.0)
            value_part = jnp.einsum(
                "hqk,qhd->khd",
                weights.astype(jnp.bfloat16),
                out_grads,
                preferred_element_type=jnp.float32,
            )
            weight_grads = jnp.einsum(
                "qhd,khd->hqk", out_grads, value_rows, preferred_element_type=jnp.float32
            )
            score_grads = (weights * (weight_grads - row_delta[:, :, None])).astype(jnp.bfloat16)
            query_grad = (
                query_grad
                + jnp.einsum(
                    "hqk,khd->qhd", score_grads, key_rows, preferred_element_type=jnp.float32
                )
                * scale_factor
            )
            key_part = (
                jnp.einsum("hqk,qhd->khd", score_grads, queries, preferred_element_type=jnp.float32)
                * scale_factor
            )
            key_grad = lax.dynamic_update_slice_in_dim(
                key_grad, key_part.reshape(KEY_BLOCK, head_count * HS), first_key, 0
            )
            value_grad = lax.dynamic_update_slice_in_dim(
                value_grad, value_part.reshape(KEY_BLOCK, head_count * HS), first_key, 0
            )
            return (query_grad, key_grad, value_grad)

        return lax.cond(is_live, grad_update, keep_state, loop_state)

    start_grads = (
        jnp.zeros((span_rows, head_count, HS), jnp.float32),
        jnp.zeros((total_rows, head_count * HS), jnp.float32),
        jnp.zeros((total_rows, head_count * HS), jnp.float32),
    )
    query_grad, key_grad, value_grad = lax.fori_loop(0, block_count, grad_step, start_grads)
    key_own, value_own = (
        lax.psum_scatter(
            key_grad.astype(jnp.bfloat16), "blk", scatter_dimension=0, tiled=True
        ).astype(jnp.float32),
        lax.psum_scatter(
            value_grad.astype(jnp.bfloat16), "blk", scatter_dimension=0, tiled=True
        ).astype(jnp.float32),
    )
    query_tokens_grad, key_tokens_grad, value_tokens_grad = (
        lax.all_to_all(
            query_grad.reshape(span_rows, head_count * HS).astype(jnp.bfloat16),
            "head",
            split_axis=0,
            concat_axis=1,
            tiled=True,
        ),
        lax.all_to_all(
            key_own.astype(jnp.bfloat16), "head", split_axis=0, concat_axis=1, tiled=True
        ),
        lax.all_to_all(
            value_own.astype(jnp.bfloat16), "head", split_axis=0, concat_axis=1, tiled=True
        ),
    )
    qkv_grads = jnp.concatenate([query_tokens_grad, key_tokens_grad, value_tokens_grad], axis=1)
    d_qkv_weight = jnp.dot(normed_low.T, qkv_grads, preferred_element_type=jnp.float32)
    normed_grads = jnp.dot(qkv_grads, qkv_weight.T, preferred_element_type=jnp.float32)
    d_inputs_norm, d_gain_one = norm_one_pull(normed_grads)
    d_inputs = d_hidden_one + d_inputs_norm
    gain_one_sum, qkv_sum, out_sum, gain_two_sum, router_sum = (
        lax.psum_scatter(
            d_gain_one.astype(jnp.bfloat16), "blk", scatter_dimension=0, tiled=True
        ).astype(jnp.float32),
        lax.psum_scatter(
            d_qkv_weight.astype(jnp.bfloat16), "blk", scatter_dimension=0, tiled=True
        ).astype(jnp.float32),
        lax.psum_scatter(
            d_out_weight.astype(jnp.bfloat16), "blk", scatter_dimension=0, tiled=True
        ).astype(jnp.float32),
        lax.psum_scatter(
            d_gain_two.astype(jnp.bfloat16), "blk", scatter_dimension=0, tiled=True
        ).astype(jnp.float32),
        lax.psum_scatter(
            d_router.astype(jnp.bfloat16), "blk", scatter_dimension=0, tiled=True
        ).astype(jnp.float32),
    )
    gain_one_all, qkv_all, out_all, gain_two_all, router_all, expert_in_all, expert_out_all = (
        lax.psum(gain_one_sum.astype(jnp.bfloat16), "head").astype(jnp.float32),
        lax.psum(qkv_sum.astype(jnp.bfloat16), "head").astype(jnp.float32),
        lax.psum(out_sum.astype(jnp.bfloat16), "head").astype(jnp.float32),
        lax.psum(gain_two_sum.astype(jnp.bfloat16), "head").astype(jnp.float32),
        lax.psum(router_sum.astype(jnp.bfloat16), "head").astype(jnp.float32),
        lax.psum(d_weight_in[None].astype(jnp.bfloat16), "head").astype(jnp.float32),
        lax.psum(d_weight_out[None].astype(jnp.bfloat16), "head").astype(jnp.float32),
    )
    return (
        output,
        d_inputs,
        gain_one_all,
        qkv_all,
        out_all,
        gain_two_all,
        router_all,
        expert_in_all,
        expert_out_all,
    )


MESH = pl.DeviceIdType.MESH
LANES = 128
HALF = LANES // 2
MIB = 2**20
F32 = jnp.float32
BF16 = jnp.bfloat16


def dot(left, right, dims=(1, 0)):
    return lax.dot_general(
        left, right, (((dims[0],), (dims[1],)), ((), ())), preferred_element_type=F32
    )


def remote(src, dst, send_sem, recv_sem, head, blk):
    return pltpu.make_async_remote_copy(
        src_ref=src,
        dst_ref=dst,
        send_sem=send_sem,
        recv_sem=recv_sem,
        device_id={"head": head, "blk": blk},
        device_id_type=MESH,
    )


def arrived(ref, sem):
    pltpu.make_async_copy(ref, ref, sem).wait()


def greet(peers):
    barrier = pltpu.get_barrier_semaphore()
    for head, blk in peers:
        pl.semaphore_signal(
            barrier, inc=1, device_id={"head": head, "blk": blk}, device_id_type=MESH
        )
    return len(peers)


def meet(count):
    pl.semaphore_wait(pltpu.get_barrier_semaphore(), count)


def halves(values, lanes_kept):
    rows = values.shape[0] // 2
    moved = pltpu.roll(values[rows:], HALF, 1)
    return jnp.where(lanes_kept, values[:rows], moved)


def lane_ids(shape):
    return lax.broadcasted_iota(jnp.int32, shape, len(shape) - 1)


def centre(values):
    average = jnp.mean(values, axis=-1, keepdims=True)
    centred = values - average
    spread = jnp.mean(centred * centred, axis=-1, keepdims=True)
    scale = lax.rsqrt(spread + EPSILON)
    return centred * scale, scale


def centre_back(grad, xhat, scale):
    middle = jnp.mean(grad, axis=-1, keepdims=True)
    along = jnp.mean(grad * xhat, axis=-1, keepdims=True)
    return (grad - middle - xhat * along) * scale


def split_high_low(column, lanes):
    high = column.astype(BF16)
    low = (column - high.astype(F32)).astype(BF16)
    return jnp.where(lanes < HALF, high.astype(F32), low.astype(F32)).astype(BF16)


def join_high_low(matrix, start):
    return matrix[:, start : start + 1].astype(F32) + matrix[
        :, start + HALF : start + HALF + 1
    ].astype(F32)


def place():
    head, blk = lax.axis_index("head"), lax.axis_index("blk")
    return head, blk, blk // 2, lax.rem(blk, 2)


def around(index, step, size):
    return lax.rem(index + step, size)


def qkv_kernel(
    heads, blks,
    x_hbm, w_hbm, g1_hbm, wo_hbm, wr_hbm, g2_hbm, docs_hbm,
    qall, kvall, xall, wall, wo_all, kvt, bounds,
    x_ref, w_ref, rows_in, g1_ref, g2_ref, wr_ref, docs_ref, wo_own, kv_other, in_sem,
    x_send, x_recv, w_send, w_recv, o_send, o_recv, p_send, p_recv,
    k_send, k_recv, q_recv,
):
    head, blk, z, y = place()
    planes = blks // 2
    model = x_ref.shape[1]
    rows = w_ref.shape[0]
    part = rows // heads
    experts = wr_ref.shape[0]
    wanted = (
        (w_hbm, w_ref), (g1_hbm, g1_ref), (g2_hbm, g2_ref), (wr_hbm, wr_ref), (x_hbm, x_ref),
        (wo_hbm, wo_own.at[:, pl.ds(0, model)]), (docs_hbm, docs_ref),
    )
    fetched = [
        pltpu.make_async_copy(src, dst, in_sem.at[i]) for i, (src, dst) in enumerate(wanted)
    ]
    for copy in fetched:
        copy.start()
    rows_in[...] = jnp.zeros_like(rows_in)
    met = greet(
        [(around(head, k, heads), blk) for k in range(1, heads)]
        + [(head, around(blk, k, blks)) for k in range(1, blks)]
    )
    lanes = lane_ids((rows, LANES))
    for copy in fetched:
        copy.wait()
    rows_in[0:experts, 0:rows] = wr_ref[...].astype(F32)
    rows_in[experts : experts + 1, 0:rows] = g2_ref[...].astype(F32)
    rows_in[experts + 1 : experts + 2, 0:rows] = g1_ref[...].astype(F32)
    vectors = jnp.transpose(rows_in[...])[:rows]
    gain = vectors[:, experts + 1 : experts + 2]

    def columns(which):
        start = pl.multiple_of(which * model + head * LANES, LANES)
        return w_ref[:, pl.ds(start, LANES)].astype(F32) * gain

    key_cols = columns(1)
    value_cols = pltpu.roll(columns(2), HALF, 1)
    wall[blk, :, 0:LANES] = jnp.where(lanes < HALF, key_cols, value_cols).astype(BF16)
    wall[blk, :, LANES : 2 * LANES] = jnp.where(lanes < HALF, value_cols, key_cols).astype(BF16)
    wall[blk, :, 2 * LANES : 3 * LANES] = (columns(0) * HS ** (-0.5)).astype(BF16)
    w_copies = [
        remote(wall.at[blk], wall.at[blk], w_send.at[k], w_recv.at[k], head, around(blk, k, blks))
        for k in range(1, blks)
    ]
    xhat, _ = centre(x_ref[...].astype(F32))
    xall[head] = xhat.astype(BF16)
    meet(met)
    for copy in w_copies:
        copy.start()
    x_copies = [
        remote(xall.at[head], xall.at[head], x_send.at[k], x_recv.at[k], around(head, k, heads), blk)
        for k in range(1, heads)
    ]
    for copy in x_copies:
        copy.start()
    wo_own[:, model : model + LANES] = vectors.astype(BF16)
    wo_all[blk, head] = wo_own[pl.ds(pl.multiple_of(head * part, part), part), :]
    o_copies = [
        remote(
            wo_all.at[blk, head], wo_all.at[blk, head],
            o_send.at[k], o_recv.at[k], head, around(blk, k, blks),
        )
        for k in range(1, blks)
    ]
    for copy in o_copies:
        copy.start()
    document_bounds(docs_ref, bounds, z)
    for copy in x_copies:
        copy.wait()
    for copy in w_copies:
        copy.wait()
    weight = wall[...].reshape(model, 3 * LANES)
    tokens = x_ref.shape[0]
    even = y == 0
    above, below = z < planes - 1, z > 0
    half_span = kvall.shape[1] // 2
    sides = ((1, above, below, 0), (-1, below, above, 4))

    def half_of(ref, half):
        return ref.at[pl.ds(half * half_span, half_span)]

    def outward(slot, step, across, half):
        target = 2 * (z + step) + around(y, across, 2)
        return remote(
            half_of(kv_other if across else kvall.at[blk], half), half_of(kvall.at[blk], half),
            k_send.at[slot], k_recv.at[blk, half], head, target,
        )

    def onward(slot, step, side, half):
        from_span = 2 * (z - step) + side
        ref = half_of(kvall.at[from_span], half)
        return remote(ref, ref, k_send.at[slot], k_recv.at[from_span, half], head, 2 * (z + step) + y)

    def await_half(span, half):
        arrived(half_of(kvall.at[span], half), k_recv.at[span, half])

    def turn(span):
        size = kvall.shape[1]
        kvt[:, pl.ds(pl.multiple_of(span * size, size), size)] = jnp.transpose(kvall[span])

    for half in range(2):
        for piece in range(half * heads // 2, (half + 1) * heads // 2):
            made = dot(xall[piece], weight).astype(BF16)
            first, second = made[:, 0:LANES], made[:, LANES : 2 * LANES]
            span = slice(piece * tokens, (piece + 1) * tokens)
            kvall[blk, span, :] = jnp.where(even, first, second)
            kv_other[span, :] = jnp.where(even, second, first)
            qall[y, span, :] = made[:, 2 * LANES : 3 * LANES]
        for step, there, _, slot in sides:

            @pl.when(there)
            def _():
                outward(slot + 2 * half, step, 0, half).start()
                outward(slot + 2 * half + 1, step, 1, half).start()

        outward(8 + half, 0, 1, half).start()
    q_pair = remote(qall.at[y], qall.at[y], k_send.at[10], q_recv, head, 2 * z + around(y, 1, 2))
    q_pair.start()
    turn(blk)
    for copy in o_copies:
        copy.wait()
    p_copies = [
        remote(
            wo_all.at[:, head], wo_all.at[:, head],
            p_send.at[k], p_recv.at[k], around(head, k, heads), blk,
        )
        for k in range(1, heads)
    ]
    for copy in p_copies:
        copy.start()
    for half in range(2):
        for step, there, back, slot in sides:

            @pl.when(back)
            def _():
                for side in range(2):
                    await_half(2 * (z - step) + side, half)

            @pl.when(jnp.logical_and(there, back))
            def _():
                for side in range(2):
                    onward(11 + slot + 2 * half + side, step, side, half).start()

    pair = 2 * z + around(y, 1, 2)
    for half in range(2):
        await_half(pair, half)
    turn(pair)
    for step, there, back, slot in sides:

        @pl.when(back)
        def _():
            for side in range(2):
                turn(2 * (z - step) + side)

    for other in range(planes):
        for side in range(2):
            span = 2 * other + side

            @pl.when(jnp.logical_or(z - other == 2, other - z == 2))
            def _():
                for half in range(2):
                    await_half(span, half)
                turn(span)

    q_pair.wait()
    for copy in p_copies:
        copy.wait()
    for half in range(2):
        outward(8 + half, 0, 1, half).wait_send()
        for step, there, back, slot in sides:

            @pl.when(there)
            def _():
                outward(slot + 2 * half, step, 0, half).wait_send()
                outward(slot + 2 * half + 1, step, 1, half).wait_send()

            @pl.when(jnp.logical_and(there, back))
            def _():
                for side in range(2):
                    onward(11 + slot + 2 * half + side, step, side, half).wait_send()


def document_bounds(docs_ref, bounds, z):
    count = docs_ref.shape[1]
    lengths = docs_ref[...].astype(F32)
    doc = lax.broadcasted_iota(jnp.int32, (count, count), 0)
    other = lane_ids((count, count))
    start = jnp.sum(jnp.where(other < doc, lengths, 0.0), axis=1, keepdims=True)
    end = jnp.sum(jnp.where(other <= doc, lengths, 0.0), axis=1, keepdims=True)
    queries = bounds.shape[1]
    token = (z * queries + lane_ids((count, queries))).astype(F32)
    begun = start <= token
    bounds[...] = jnp.zeros_like(bounds)
    bounds[0:1, :] = jnp.max(jnp.where(begun, start, 0.0), axis=0, keepdims=True).astype(jnp.int32)
    bounds[1:2, :] = jnp.max(jnp.where(begun, end, 0.0), axis=0, keepdims=True).astype(jnp.int32)


def vmem_specs(count):
    return [pl.BlockSpec(memory_space=pltpu.VMEM)] * count


def hbm_specs(count):
    return [pl.BlockSpec(memory_space=pltpu.HBM)] * count


def in_hbm(*arrays):
    return [pltpu.with_memory_space_constraint(array, pltpu.HBM) for array in arrays]


def dma(*shape):
    return pltpu.SemaphoreType.DMA(shape)


def call_qkv(x, w_qkv, g1, w_out, w_router, g2, doc_lengths, heads, blks):
    tokens, model = x.shape
    rows = w_qkv.shape[0]
    span = tokens * heads
    wide = model + LANES
    part = rows // heads
    return pl.pallas_call(
        functools.partial(qkv_kernel, heads, blks),
        out_shape=(
            jax.ShapeDtypeStruct((2, span, LANES), BF16),
            jax.ShapeDtypeStruct((blks, span, LANES), BF16),
            jax.ShapeDtypeStruct((heads, tokens, model), BF16),
            jax.ShapeDtypeStruct((blks, rows, 3 * LANES), BF16),
            jax.ShapeDtypeStruct((blks, heads, part, wide), BF16),
            jax.ShapeDtypeStruct((LANES, blks * span), BF16),
            jax.ShapeDtypeStruct((8, 2 * span), jnp.int32),
        ),
        in_specs=hbm_specs(7),
        out_specs=tuple(vmem_specs(7)),
        scratch_shapes=[
            pltpu.VMEM((tokens, model), BF16),
            pltpu.VMEM((rows, 3 * model), BF16),
            pltpu.VMEM((LANES, LANES), F32),
            pltpu.VMEM((1, rows), BF16),
            pltpu.VMEM((1, rows), BF16),
            pltpu.VMEM((w_router.shape[1], rows), BF16),
            pltpu.VMEM((1, doc_lengths.shape[0]), jnp.int32),
            pltpu.VMEM((rows, wide), BF16),
            pltpu.VMEM((span, LANES), BF16),
            dma(7),
            dma(heads), dma(heads), dma(blks), dma(blks), dma(blks), dma(blks), dma(heads), dma(heads),
            dma(19), dma(blks, 2), pltpu.SemaphoreType.DMA,
        ],
        compiler_params=pltpu.CompilerParams(
            collective_id=1, has_side_effects=True, vmem_limit_bytes=16 * MIB
        ),
        name="qkv",
    )(
        *in_hbm(
            x, w_qkv, g1.reshape(1, rows), w_out, w_router.T, g2.reshape(1, rows),
            doc_lengths.reshape(1, -1),
        )
    )


QUERY_TILE = 256
CHAINS = 2


def masked_queries(q_ref, tile, key_lanes, query_tile):
    tiles_per_span = q_ref.shape[1] // query_tile
    inner = tile % tiles_per_span * query_tile
    query = q_ref[tile // tiles_per_span, inner : inner + query_tile, :]
    return jnp.where(key_lanes, query, jnp.zeros_like(query))


def group_blocks(bounds_ref, group, size, key_tile):
    first, last = group * size, (group + 1) * size
    low = jnp.min(bounds_ref[0:1, first : first + LANES])
    high = jnp.max(bounds_ref[1:2, last - LANES : last])
    return low // key_tile, (high + key_tile - 1) // key_tile


def inside_document(bounds_ref, tile, first, shape):
    key = first + lax.broadcasted_iota(jnp.int32, shape, 0)
    columns = slice(tile * shape[1], (tile + 1) * shape[1])
    return jnp.logical_and(key >= bounds_ref[0:1, columns], key < bounds_ref[1:2, columns])


def forward_kernel(bounds_ref, q_ref, kv_ref, kvt_ref, o_out, ob_out, lse_out):
    _, _, z, y = place()
    key_tile = kv_ref.shape[1]
    total = q_ref.shape[0] * q_ref.shape[1]
    key_lanes = (lane_ids((QUERY_TILE, LANES)) < HALF) == (y == 0)
    value_lanes = (lane_ids((HALF, LANES)) < HALF) == (y == 1)
    group_size = CHAINS * QUERY_TILE
    for group in range(total // group_size):
        tiles = range(group * CHAINS, (group + 1) * CHAINS)
        queries = [masked_queries(q_ref, tile, key_lanes, QUERY_TILE) for tile in tiles]
        low, high = group_blocks(bounds_ref, group, group_size, key_tile)

        def step(block, carry, queries=queries, tiles=tiles):
            first = pl.multiple_of(block * key_tile, key_tile)
            keys = kv_ref[block]
            keys_across = kvt_ref[:, pl.ds(first, key_tile)]
            scores = [dot(keys, query, (1, 1)) for query in queries]
            made = []
            for tile, score, (biggest, weight, mixed) in zip(tiles, scores, carry):
                inside = inside_document(bounds_ref, tile, first, score.shape)
                score = jnp.where(inside, score, MASKED)
                bigger = jnp.maximum(biggest, jnp.max(score, axis=0, keepdims=True))
                fade = jnp.exp(biggest - bigger)
                terms = jnp.exp(score - bigger)
                weight = weight * fade + jnp.sum(terms, axis=0, keepdims=True)
                made.append((bigger, weight, mixed * fade + dot(keys_across, terms.astype(BF16))))
            return tuple(made)

        start = (
            jnp.full((1, QUERY_TILE), MASKED, F32),
            jnp.zeros((1, QUERY_TILE), F32),
            jnp.zeros((LANES, QUERY_TILE), F32),
        )
        ends = lax.fori_loop(low, high, step, (start,) * CHAINS)
        for tile, (biggest, weight, mixed) in zip(tiles, ends):
            result = jnp.transpose(mixed / weight)
            o_out[tile] = result
            for part in range(QUERY_TILE // LANES):
                block = result[part * LANES : (part + 1) * LANES]
                ob_out[tile, part] = halves(block, value_lanes).astype(BF16)
            lse_out[tile] = jnp.broadcast_to(biggest + jnp.log(weight), (8, QUERY_TILE))


def call_forward(bounds, q, kv, kvt):
    blks, span, _ = kv.shape
    tiles = 2 * span // QUERY_TILE
    return pl.pallas_call(
        forward_kernel,
        out_shape=(
            jax.ShapeDtypeStruct((tiles, QUERY_TILE, LANES), F32),
            jax.ShapeDtypeStruct((tiles, QUERY_TILE // LANES, HALF, LANES), BF16),
            jax.ShapeDtypeStruct((tiles, 8, QUERY_TILE), F32),
        ),
        in_specs=vmem_specs(4),
        out_specs=tuple(vmem_specs(3)),
        compiler_params=pltpu.CompilerParams(vmem_limit_bytes=16 * MIB),
        name="attend",
    )(bounds, q, kv, kvt)


def backward_kernel(
    bounds_ref, q_ref, kv_ref, kvt_ref, do_ref, o_ref, lse_ref, dq_out, dkv_out, dkv
):
    _, _, z, y = place()
    key_tile = kv_ref.shape[1]
    total = q_ref.shape[0] * q_ref.shape[1]
    dkv[...] = jnp.zeros_like(dkv)
    key_lanes = (lane_ids((QUERY_TILE, LANES)) < HALF) == (y == 0)
    group_size = CHAINS * QUERY_TILE
    for group in range(total // group_size):
        tiles = range(group * CHAINS, (group + 1) * CHAINS)
        queries, out_grads, deltas, log_totals = [], [], [], []
        for tile in tiles:
            queries.append(masked_queries(q_ref, tile, key_lanes, QUERY_TILE))
            parts = []
            for part in range(QUERY_TILE // LANES):
                packed = do_ref[tile, part].astype(F32)
                parts += [packed, pltpu.roll(packed, HALF, 1)]
            out_grad = jnp.concatenate(parts, axis=0)
            out_grads.append(jnp.where(key_lanes, 0.0, out_grad).astype(BF16))
            product = jnp.transpose(out_grads[-1].astype(F32) * o_ref[tile])
            deltas.append(jnp.sum(product, axis=0, keepdims=True))
            log_totals.append(lse_ref[tile, 0:1, :])
        low, high = group_blocks(bounds_ref, group, group_size, key_tile)

        def step(
            block, carry, queries=queries, out_grads=out_grads, deltas=deltas,
            log_totals=log_totals, tiles=tiles,
        ):
            first = pl.multiple_of(block * key_tile, key_tile)
            keys = kv_ref[block]
            keys_across = kvt_ref[:, pl.ds(first, key_tile)]
            scores = [dot(keys, query, (1, 1)) for query in queries]
            weight_grads = [dot(keys, out_grad, (1, 1)) for out_grad in out_grads]
            pieces, score_grads = [], []
            for i, tile in enumerate(tiles):
                inside = inside_document(bounds_ref, tile, first, scores[i].shape)
                weights = jnp.exp(jnp.where(inside, scores[i], MASKED) - log_totals[i])
                score_grads.append((weights * (weight_grads[i] - deltas[i])).astype(BF16))
                pieces.append(weights.astype(BF16))
            wide = jnp.concatenate(score_grads + pieces, axis=1)
            dkv[block] += dot(wide, jnp.concatenate(queries + out_grads, axis=0))
            return tuple(c + dot(keys_across, s) for c, s in zip(carry, score_grads))

        zero = jnp.zeros((LANES, QUERY_TILE), F32)
        ends = lax.fori_loop(low, high, step, (zero,) * CHAINS)
        for tile, mixed in zip(tiles, ends):
            dq_out[tile] = jnp.transpose(mixed).astype(BF16)
    for block in range(dkv.shape[0]):
        dkv_out[block] = dkv[block].astype(BF16)


def call_backward(bounds, q, kv, kvt, d_o, o, lse):
    blks, span, _ = kv.shape
    tiles = 2 * span // QUERY_TILE
    return pl.pallas_call(
        backward_kernel,
        out_shape=(
            jax.ShapeDtypeStruct((tiles, QUERY_TILE, LANES), BF16),
            jax.ShapeDtypeStruct((blks, span, LANES), BF16),
        ),
        in_specs=vmem_specs(7),
        out_specs=tuple(vmem_specs(2)),
        scratch_shapes=[pltpu.VMEM((blks, span, LANES), F32)],
        compiler_params=pltpu.CompilerParams(vmem_limit_bytes=16 * MIB),
        name="attend_back",
    )(bounds, q, kv, kvt, d_o.reshape(tiles, QUERY_TILE // LANES, HALF, LANES), o, lse)


def gelu_parts(values):
    share = 0.5 * (1.0 + lax.erf(values * (2.0**-0.5)))
    slope = share + values * jnp.exp(-0.5 * values * values) * (2.0 * math.pi) ** -0.5
    return values * share, slope


def positions(expert_rows, expert_cols, rank_row, rank_col):
    def count(mask, axis):
        return jnp.sum(mask.astype(F32), axis=axis, keepdims=True)

    row = [None, None]
    col = [None, None]
    before = rank_col < rank_row
    after = rank_row < rank_col
    for choice in range(2):
        row[choice] = count((expert_cols[choice] == expert_rows[choice]) & before, 0)
        col[choice] = count((expert_rows[choice] == expert_cols[choice]) & after, 1)
    row[1] = row[1] + count(expert_cols[0] == expert_rows[1], 0)
    col[1] = col[1] + count(expert_rows[0] == expert_cols[1], 1)
    return row, col


def own_columns(rows_ref, turned, blk, capacity):
    blks, _, slots = rows_ref.shape
    rows = jnp.concatenate(
        [rows_ref[...].reshape(blks, slots), jnp.zeros((LANES - blks, slots), F32)], axis=0
    )
    for piece in range(slots // LANES):
        columns = slice(piece * LANES, (piece + 1) * LANES)
        turned[columns, :] = jnp.transpose(rows[:, columns])
    own = turned[pl.ds(pl.multiple_of(blk * capacity, capacity), capacity), :]
    return jnp.concatenate([own[:, source : source + 1] for source in range(blks)], axis=0)


def middle_kernel(
    heads, blks,
    x_hbm, o_ref, wo_ref, routes_hbm, rank_hbm, d_out_hbm, win_hbm, wout_hbm,
    out_ref, dh_ref, dma_all, grads_ref, rx,
    x_ref, routes_ref, rank_ref, d_out_ref, win_ref, wout_ref, rows_in, in_sem,
    o_all, dos, doa, rs, ra, po, pa, dr, da, dms, acc_out, acc_row, mix, gate_rows, d_gate_rows, turned,
    o_send, o_recv, dos_send, dos_recv, r_send, r_recv, po_send, po_recv,
    dr_send, dr_recv, dm_send, dm_recv, rx_send, rx_recv, g_send, g_recv, dg_send, dg_recv,
):
    head, blk, z, y = place()
    tokens, model = x_ref.shape
    capacity = 2 * tokens // blks
    slots = capacity * blks
    plane = [(k % heads, k // heads) for k in range(1, 2 * heads)]
    wanted = (
        (routes_hbm, routes_ref), (rank_hbm, rank_ref), (d_out_hbm, d_out_ref), (x_hbm, x_ref),
        (win_hbm, win_ref), (wout_hbm, wout_ref),
    )
    fetched = [
        pltpu.make_async_copy(src, dst, in_sem.at[i]) for i, (src, dst) in enumerate(wanted)
    ]
    for copy in fetched:
        copy.start()
    met = greet(
        [(around(head, kh, heads), 2 * z + around(y, ky, 2)) for kh, ky in plane]
        + [(head, around(blk, k, blks)) for k in range(1, blks)]
    )
    meet(met)

    def plane_copies(src_of, dst, send, recv):
        copies = []
        for k, (kh, ky) in enumerate(plane):
            to_head, to_y = around(head, kh, heads), around(y, ky, 2)
            copies.append(
                remote(src_of(to_y, to_head), dst, send.at[k], recv.at[k], to_head, 2 * z + to_y)
            )
        return copies

    def blk_copies(src, dst, send, recv):
        return [
            remote(
                src.at[around(blk, k, blks)], dst.at[blk],
                send.at[k], recv.at[k], head, around(blk, k, blks),
            )
            for k in range(1, blks)
        ]

    def start(copies):
        for copy in copies:
            copy.start()

    def finish(copies):
        for copy in copies:
            copy.wait()

    o_copies = plane_copies(lambda to_y, to_head: o_ref.at[to_y, to_head], o_all.at[y, head], o_send, o_recv)
    start(o_copies)
    o_all[y, head] = o_ref[y, head]

    lanes = lane_ids((tokens, LANES))
    for copy in fetched[:4]:
        copy.wait()
    e_rows = [routes_ref[i : i + 1, :].astype(F32) for i in range(2)]
    rank_row = rank_ref[...].astype(F32)
    rows_in[...] = jnp.zeros_like(rows_in)
    rows_in[0:1, :], rows_in[1:2, :], rows_in[2:3, :] = *e_rows, rank_row
    columns = jnp.transpose(rows_in[...])
    e_cols = [columns[:, 0:1], columns[:, 1:2]]
    rank_col = columns[:, 2:3]
    pos_rows, pos_cols = positions(e_rows, e_cols, rank_row, rank_col)

    def slot_of(expert, position):
        return jnp.where(position < capacity, expert * capacity + position, -1.0).astype(jnp.int32)

    slot_rows = [slot_of(e, p) for e, p in zip(e_rows, pos_rows)]
    slot_cols = [slot_of(e, p) for e, p in zip(e_cols, pos_cols)]
    slot_down = lax.broadcasted_iota(jnp.int32, (slots, tokens), 0)
    slot_across = lane_ids((tokens, slots))
    pick = [(slot_down == s).astype(BF16) for s in slot_rows]
    put = [(slot_across == s).astype(BF16) for s in slot_cols]
    pick_any = pick[0] + pick[1]
    put_any = put[0] + put[1]

    d_out = d_out_ref[...]
    dos[...] = dot(pick_any, d_out.astype(BF16)).astype(BF16).reshape(dos.shape)
    dos_copies = blk_copies(dos, doa, dos_send, dos_recv)
    start(dos_copies)
    doa[blk] = dos[blk]

    weight_out = jnp.concatenate(
        [wo_ref[(b ^ 1) * HALF : ((b ^ 1) + 1) * HALF, 0:model] for b in range(blks)], axis=0
    )
    small = wo_ref[:, model : model + LANES]
    small_across = jnp.concatenate(
        [
            jnp.transpose(small[i * LANES : (i + 1) * LANES].astype(F32))
            for i in range(model // LANES)
        ],
        axis=1,
    )
    gain = small_across[blks : blks + 1, :]

    finish(o_copies)
    low_lanes = lanes[:HALF] < HALF
    for piece in range(heads):
        columns = slice(piece * LANES, (piece + 1) * LANES)
        first, second = o_all[1, piece].astype(F32), o_all[0, piece].astype(F32)
        mix[:HALF, columns] = jnp.where(low_lanes, first, second).astype(BF16)
        swapped = pltpu.roll(jnp.where(low_lanes, second, first), HALF, 1)
        mix[HALF:, columns] = swapped.astype(BF16)
    mixed = mix[...]
    hidden = x_ref[...].astype(F32) + dot(mixed, weight_out)
    xhat, scale = centre(hidden)
    routed = (xhat * gain).astype(BF16)
    rs[...] = dot(pick_any, routed).astype(BF16).reshape(rs.shape)
    r_copies = blk_copies(rs, ra, r_send, r_recv)
    start(r_copies)
    ra[blk] = rs[blk]
    logits = jnp.where(lanes < blks, dot(routed, small), MASKED)
    powers = jnp.exp(logits - jnp.max(logits, axis=1, keepdims=True))
    probs = powers / jnp.sum(powers, axis=1, keepdims=True)
    lanes_f = lanes.astype(F32)
    hots = [lanes_f == e for e in e_cols]
    gates = [jnp.sum(jnp.where(hot, probs, 0.0), axis=1, keepdims=True) for hot in hots]
    gate_high = [g.astype(BF16).astype(F32) for g in gates]
    gate_across = jnp.transpose(
        jnp.where(lanes == 0, gate_high[0], jnp.where(lanes == 1, gates[0] - gate_high[0], 0.0))
        + jnp.where(lanes == 2, gate_high[1], jnp.where(lanes == 3, gates[1] - gate_high[1], 0.0))
    ).astype(BF16)
    by_slot = (dot(gate_across, put[0]), dot(gate_across, put[1]))
    gate_rows[blk] = by_slot[0][0:1] + by_slot[0][1:2] + by_slot[1][2:3] + by_slot[1][3:4]
    g_copies = [
        remote(
            gate_rows.at[blk], gate_rows.at[blk],
            g_send.at[k], g_recv.at[k], head, around(blk, k, blks),
        )
        for k in range(1, blks)
    ]
    start(g_copies)
    acc_out[...] = jnp.zeros_like(acc_out)
    acc_row[...] = jnp.zeros_like(acc_row)
    finish(dos_copies)
    finish(r_copies)

    out_rows = doa[...].reshape(slots, model)
    rx[head, :, 0:model] = ra[...].reshape(slots, model)
    finish(g_copies)
    gate_col = own_columns(gate_rows, turned, blk, capacity)
    rx[head, :, model : 2 * model] = (out_rows.astype(F32) * gate_col).astype(BF16)
    half_ff = wout_ref.shape[0] // 4
    for copy in fetched[4:]:
        copy.wait()

    @pl.loop(0, 4)
    def _(chunk):
        first = pl.multiple_of(chunk * half_ff, half_ff)
        into = win_ref[:, pl.ds(first, half_ff)]
        outof = wout_ref[pl.ds(first, half_ff), :]
        act, slope = gelu_parts(dot(rx[head, :, 0:model], into))
        acc_out[...] += dot(act.astype(BF16), outof)
        d_act = dot(rx[head, :, model : 2 * model], outof, (1, 1))
        acc_row[...] += dot((slope * d_act).astype(BF16), into, (1, 1))

    result = acc_out[...].astype(BF16)
    d_gate = jnp.sum(out_rows.astype(F32) * result.astype(F32), axis=1, keepdims=True)
    dr[...] = acc_row[...].astype(BF16).reshape(dr.shape)
    dr_copies = blk_copies(dr, da, dr_send, dr_recv)
    start(dr_copies)
    da[blk] = dr[blk]
    d_wide = jnp.broadcast_to(d_gate, (slots, LANES))
    d_gate_rows[blk] = jnp.concatenate(
        [jnp.transpose(d_wide[i * LANES : (i + 1) * LANES])[0:1] for i in range(slots // LANES)],
        axis=1,
    )
    dg_copies = [
        remote(
            d_gate_rows.at[blk], d_gate_rows.at[blk],
            dg_send.at[k], dg_recv.at[k], head, around(blk, k, blks),
        )
        for k in range(1, blks)
    ]
    start(dg_copies)
    po[...] = result.reshape(blks, capacity, model)
    po_copies = blk_copies(po, pa, po_send, po_recv)
    pa[blk] = po[blk]
    core = lax.rem(head, 2)
    sibling, across = head - core + 1 - core, around(head, 2, heads)
    to_sibling = remote(rx.at[head], rx.at[head], rx_send.at[0], rx_recv.at[0], sibling, blk)
    to_across = remote(rx.at[head], rx.at[head], rx_send.at[1], rx_recv.at[1], across, blk)
    to_across.start()
    to_sibling.start()

    finish(dg_copies)
    back_gate = own_columns(d_gate_rows, turned, blk, capacity)
    back_gate = split_high_low(back_gate, lane_ids((slots, LANES)))
    d_gates = [join_high_low(dot(p, back_gate), 0) for p in put]
    d_probs = jnp.where(hots[0], d_gates[0], 0.0) + jnp.where(hots[1], d_gates[1], 0.0)
    d_logits = probs * (d_probs - jnp.sum(probs * d_probs, axis=1, keepdims=True))
    d_high = d_logits.astype(BF16)
    d_low = (d_logits - d_high.astype(F32)).astype(BF16)
    d_router_part = dot(d_high, small, (1, 1)) + dot(d_low, small, (1, 1))
    finish(dr_copies)
    start(po_copies)
    d_routed = dot(put_any, da[...].reshape(slots, model)) + d_router_part
    d_hidden = d_out + centre_back(d_routed * gain, xhat, scale)
    dh_ref[...] = d_hidden
    d_attn = d_hidden.astype(BF16)
    d_mixed = dot(d_attn, weight_out, (1, 1))
    for piece in range(heads):
        block = d_mixed[:, piece * LANES : (piece + 1) * LANES]
        for to_y in range(2):
            dms[to_y, piece] = halves(block, low_lanes == (to_y == 1)).astype(BF16)
    dm_copies = plane_copies(lambda to_y, to_head: dms.at[to_y, to_head], dma_all.at[y, head], dm_send, dm_recv)
    start(dm_copies)
    dma_all[y, head] = dms[y, head]

    d_weight = dot(mixed, d_attn, (0, 0)).astype(BF16)
    for b in range(blks):
        grads_ref[b, :, 0:model] = d_weight[(b ^ 1) * HALF : ((b ^ 1) + 1) * HALF, :]
    last = (lanes == blks).astype(BF16)
    d_small = dot(routed, d_high, (0, 0)) + dot((d_routed * xhat).astype(BF16), last, (0, 0))
    grads_ref[:, :, model : model + LANES] = d_small.astype(BF16).reshape(blks, HALF, LANES)
    finish(po_copies)
    parts = pa[...].reshape(slots, model)
    mixture = gates[0] * dot(put[0], parts) + gates[1] * dot(put[1], parts)
    out_ref[...] = (hidden + mixture).astype(BF16)

    arrived(rx.at[across], rx_recv.at[1])
    forward = remote(rx.at[across], rx.at[across], rx_send.at[2], rx_recv.at[2], sibling, blk)
    forward.start()
    finish(dm_copies)
    to_sibling.wait()
    to_across.wait_send()
    forward.wait()


def call_middle(x, o, wo, routes, rank, d_out, win, wout, heads, blks):
    tokens, model = x.shape
    capacity = 2 * tokens // blks
    slots = capacity * blks
    wide = model + LANES

    def rows(width):
        return pltpu.VMEM((blks, capacity, width), BF16)

    def block(*lead):
        return pltpu.VMEM((*lead, tokens // 2, LANES), BF16)

    return pl.pallas_call(
        functools.partial(middle_kernel, heads, blks),
        out_shape=(
            jax.ShapeDtypeStruct((tokens, model), BF16),
            jax.ShapeDtypeStruct((tokens, model), F32),
            jax.ShapeDtypeStruct((2, heads, tokens // 2, LANES), BF16),
            jax.ShapeDtypeStruct((blks, model // blks, wide), BF16),
            jax.ShapeDtypeStruct((heads, slots, 2 * model), BF16),
        ),
        in_specs=hbm_specs(1) + vmem_specs(2) + hbm_specs(5),
        out_specs=tuple(vmem_specs(5)),
        scratch_shapes=[
            pltpu.VMEM((tokens, model), BF16),
            pltpu.VMEM((2, tokens), jnp.int32),
            pltpu.VMEM((1, tokens), jnp.int32),
            pltpu.VMEM((tokens, model), F32),
            pltpu.VMEM(win.shape, BF16),
            pltpu.VMEM(wout.shape, BF16),
            pltpu.VMEM((tokens, tokens), F32),
            dma(6),
            block(2, heads), rows(model), rows(model), rows(model), rows(model), rows(model), rows(model),
            rows(model), rows(model), block(2, heads),
            pltpu.VMEM((slots, model), F32), pltpu.VMEM((slots, model), F32),
            pltpu.VMEM((tokens, model), BF16),
            pltpu.VMEM((blks, 1, slots), F32), pltpu.VMEM((blks, 1, slots), F32),
            pltpu.VMEM((slots, LANES), F32),
            dma(2 * heads), dma(2 * heads), dma(blks), dma(blks), dma(blks), dma(blks), dma(blks), dma(blks),
            dma(blks), dma(blks), dma(2 * heads), dma(2 * heads), dma(3), dma(3),
            dma(blks), dma(blks), dma(blks), dma(blks),
        ],
        compiler_params=pltpu.CompilerParams(
            collective_id=2, has_side_effects=True, vmem_limit_bytes=20 * MIB
        ),
        name="experts",
    )(*in_hbm(x), o, wo, *in_hbm(routes.T, rank, d_out, win, wout))


def last_kernel(
    heads, blks,
    x_hbm, dh_ref, dq_ref, dkv_ref, xa_ref, wa_ref, w_hbm, g1_hbm, grads_ref, rx_ref, win_hbm, wout_hbm,
    dx_ref, dw_ref, shared_ref, din_ref, dout_ref,
    x_ref, w_ref, g1_ref, win_ref, wout_ref, in_sem,
    gain_tile, far_all, near_send_buf, near_all, pair_all, dq_all, us, ua, gs, ga, gh, w1, w2s, w2, w3,
    q_send, q_recv, pair_send, pair_recv, far_send, far_recv, near_send, near_recv,
    u_send, u_recv, g_send, g_recv, gh_send, gh_recv, w1_send, w1_recv, w2_send, w2_recv,
    w3_send, w3_recv, e_send, e_recv,
):
    head, blk, z, y = place()
    planes = blks // 2
    tokens, model = x_ref.shape
    rows = w_ref.shape[0]
    wanted = (
        (win_hbm, win_ref), (wout_hbm, wout_ref), (x_hbm, x_ref), (w_hbm, w_ref), (g1_hbm, g1_ref)
    )
    fetched = [
        pltpu.make_async_copy(src, dst, in_sem.at[i]) for i, (src, dst) in enumerate(wanted)
    ]
    for copy in fetched:
        copy.start()
    met = greet(
        [(around(head, k, heads), blk) for k in range(1, heads)]
        + [(head, around(blk, k, blks)) for k in range(1, blks)]
    )
    meet(met)

    def start(copies):
        for copy in copies:
            copy.start()

    def finish(copies):
        for copy in copies:
            copy.wait()

    other_y = around(y, 1, 2)
    pair = 2 * z + other_y
    above, below = z < planes - 1, z > 0
    directions = ((1, above, below, 0), (-1, below, above, 2))

    def far_copy(step, slot, side):
        span = 2 * (z + 2 * step) + side
        return remote(
            dkv_ref.at[span], far_all.at[slot + side],
            far_send.at[slot + side], far_recv.at[slot + side], head, 2 * (z + step) + y,
        )

    def near_copy(step, slot, side):
        return remote(
            near_send_buf.at[slot + side], near_all.at[slot // 2, y],
            near_send.at[slot + side], near_recv.at[slot // 2, y], head, 2 * (z + step) + side,
        )

    def two_away(step):
        return z + 2 * step < planes if step > 0 else z + 2 * step >= 0

    for step, there, back, slot in directions:

        @pl.when(two_away(step))
        def _():
            for side in range(2):
                far_copy(step, slot, side).start()

    pair_copy = remote(dkv_ref.at[pair], pair_all, pair_send, pair_recv, head, pair)
    pair_copy.start()
    q_copy = remote(dq_ref.at[other_y], dq_all, q_send, q_recv, head, pair)
    q_copy.start()
    w1_copies = [
        remote(
            grads_ref.at[:, around(head, k, heads)], w1.at[head],
            w1_send.at[k], w1_recv.at[k], around(head, k, heads), blk,
        )
        for k in range(1, heads)
    ]
    start(w1_copies)
    w1[head] = grads_ref[:, head]

    core = lax.rem(head, 2)
    sibling = head - core + 1 - core
    ff_half = wout_ref.shape[0] // 2
    ff_step = ff_half // 4

    def expert_chunk(chunk):
        here = pl.multiple_of(core * ff_half + chunk * ff_step, ff_step)
        there = pl.multiple_of(chunk * ff_step, ff_step)
        into = win_ref[:, pl.ds(here, ff_step)]
        outof = wout_ref[pl.ds(here, ff_step), :]
        d_in = jnp.zeros((model, ff_step), F32)
        d_out = jnp.zeros((ff_step, model), F32)
        for source in range(heads):
            rows_in = rx_ref[source, :, 0:model]
            grads_out = rx_ref[source, :, model : 2 * model]
            act, slope = gelu_parts(dot(rows_in, into))
            d_act = dot(grads_out, outof, (1, 1))
            d_in = d_in + dot(rows_in, (slope * d_act).astype(BF16), (0, 0))
            d_out = d_out + dot(act.astype(BF16), grads_out, (0, 0))
        din_ref[core, :, pl.ds(there, ff_step)] = d_in.astype(BF16)
        dout_ref[core, pl.ds(there, ff_step), :] = d_out.astype(BF16)

    finish(fetched)

    @pl.loop(0, 2)
    def _(chunk):
        expert_chunk(chunk)

    for step, there, back, slot in directions:

        @pl.when(there)
        def _():
            for side in range(2):
                near_send_buf[slot + side] = dkv_ref[2 * (z + step) + side]

        @pl.when(jnp.logical_and(there, back))
        def _():
            for side in range(2):
                arrived(far_all.at[slot + side], far_recv.at[slot + side])
                near_send_buf[slot + side] = (
                    near_send_buf[slot + side].astype(F32) + far_all[slot + side].astype(F32)
                ).astype(BF16)

        @pl.when(there)
        def _():
            for side in range(2):
                near_copy(step, slot, side).start()

    @pl.loop(2, 4)
    def _(chunk):
        expert_chunk(chunk)

    e_copies = [
        remote(din_ref.at[core], din_ref.at[core], e_send.at[0], e_recv.at[0], sibling, blk),
        remote(dout_ref.at[core], dout_ref.at[core], e_send.at[1], e_recv.at[1], sibling, blk),
    ]
    start(e_copies)

    pair_copy.wait()
    q_copy.wait()
    for step, there, back, slot in directions:

        @pl.when(back)
        def _():
            for side in range(2):
                arrived(near_all.at[slot // 2, side], near_recv.at[slot // 2, side])

        @pl.when(jnp.logical_not(back))
        def _():
            near_all[slot // 2] = jnp.zeros(near_all.shape[1:], BF16)

    lanes = lane_ids((tokens, LANES))
    even = y == 0
    weight = wa_ref[...].reshape(model, 3 * LANES)
    g_sum = jnp.zeros((model, 3 * LANES), F32)
    for piece in range(heads):
        span = slice(piece * tokens, (piece + 1) * tokens)
        own = dkv_ref[blk, span, :].astype(F32)
        other = pair_all[span, :].astype(F32)
        kv_grads = [
            jnp.where(even, own, other) + near_all[0, 0, span, :].astype(F32) + near_all[1, 0, span, :].astype(F32),
            jnp.where(even, other, own) + near_all[0, 1, span, :].astype(F32) + near_all[1, 1, span, :].astype(F32),
        ]
        q_own = dq_ref[y, span, :]
        q_other = dq_all[span, :]
        own_lanes = (lanes < HALF) == even
        q_grads = jnp.where(own_lanes, q_own, q_other)
        made = jnp.concatenate([kv_grads[0].astype(BF16), kv_grads[1].astype(BF16), q_grads], axis=1)
        us[piece] = dot(made, weight, (1, 1)).astype(BF16)
        g_sum = g_sum + dot(xa_ref[piece], made, (0, 0))
    u_copies = [
        remote(
            us.at[around(head, k, heads)], ua.at[head],
            u_send.at[k], u_recv.at[k], around(head, k, heads), blk,
        )
        for k in range(1, heads)
    ]
    start(u_copies)
    ua[head] = us[head]
    gs[...] = g_sum.astype(BF16).reshape(gs.shape)
    g_copies = [
        remote(
            gs.at[around(blk, k, blks)], ga.at[blk],
            g_send.at[k], g_recv.at[k], head, around(blk, k, blks),
        )
        for k in range(1, blks)
    ]
    start(g_copies)
    ga[blk] = gs[blk]

    finish(w1_copies)
    summed = w1[0].astype(F32)
    for source in range(1, heads):
        summed = summed + w1[source].astype(F32)
    w2s[...] = summed.astype(BF16)
    w2_copies = [
        remote(
            w2s.at[around(blk, k, blks)], w2.at[blk],
            w2_send.at[k], w2_recv.at[k], head, around(blk, k, blks),
        )
        for k in range(1, blks)
    ]
    start(w2_copies)
    w2[blk] = w2s[blk]

    finish(u_copies)
    grad = ua[0].astype(F32)
    for source in range(1, heads):
        grad = grad + ua[source].astype(F32)
    xhat, scale = centre(x_ref[...].astype(F32))
    dx_ref[...] = dh_ref[...] + centre_back(grad, xhat, scale)

    finish(g_copies)
    total = ga[0].astype(F32)
    for source in range(1, blks):
        total = total + ga[source].astype(F32)
    gh[head] = total.astype(BF16)
    gh_copies = [
        remote(gh.at[head], gh.at[head], gh_send.at[k], gh_recv.at[k], around(head, k, heads), blk)
        for k in range(1, heads)
    ]
    start(gh_copies)
    finish(w2_copies)
    part = w2[0].astype(F32)
    for source in range(1, blks):
        part = part + w2[source].astype(F32)
    w3[head] = part.astype(BF16)
    w3_copies = [
        remote(w3.at[head], w3.at[head], w3_send.at[k], w3_recv.at[k], around(head, k, heads), blk)
        for k in range(1, heads)
    ]
    start(w3_copies)

    gain_tile[...] = jnp.zeros_like(gain_tile)
    gain_tile[0:1, 0:rows] = g1_ref[...].astype(F32)
    gain = jnp.transpose(jnp.broadcast_to(gain_tile[0:1, :], (LANES, LANES)))[:rows]
    low_half = lane_ids((rows, LANES)) < HALF
    finish(gh_copies)
    d_gain = jnp.zeros((rows, LANES), F32)
    for source in range(heads):
        both = [gh[source, :, i * LANES : (i + 1) * LANES].astype(F32) for i in range(3)]
        grads = (
            both[2] * HS ** (-0.5),
            jnp.where(low_half, both[0], both[1]),
            pltpu.roll(jnp.where(low_half, both[1], both[0]), HALF, 1),
        )
        for which, value in enumerate(grads):
            columns = slice(which * model + source * LANES, which * model + (source + 1) * LANES)
            d_gain = d_gain + value * w_ref[:, columns].astype(F32)
            dw_ref[:, columns] = value * gain
    finish(w3_copies)
    shared = w3[...].reshape(rows, w3.shape[-1]).astype(F32)
    shared_ref[:, 0:model] = shared[:, 0:model]
    gain_col = jnp.sum(d_gain, axis=1, keepdims=True)
    shared_ref[:, model : model + LANES] = jnp.where(
        lane_ids((rows, LANES)) == blks + 1, gain_col, shared[:, model : model + LANES]
    )
    for step, there, back, slot in directions:

        @pl.when(two_away(step))
        def _():
            for side in range(2):
                far_copy(step, slot, side).wait_send()

        @pl.when(there)
        def _():
            for side in range(2):
                near_copy(step, slot, side).wait_send()

    finish(e_copies)


def call_last(x, dh, dq, dkv, xa, wa, w_qkv, g1, grads, rx, win, wout, heads, blks):
    tokens, model = x.shape
    span = tokens * heads
    rows = w_qkv.shape[0]
    wide = model + LANES
    part = rows // heads
    ff = wout.shape[0]

    def block(*lead):
        return pltpu.VMEM((*lead, span, LANES), BF16)

    return pl.pallas_call(
        functools.partial(last_kernel, heads, blks),
        out_shape=(
            jax.ShapeDtypeStruct((tokens, model), F32),
            jax.ShapeDtypeStruct((rows, 3 * model), F32),
            jax.ShapeDtypeStruct((rows, wide), F32),
            jax.ShapeDtypeStruct((2, model, ff // 2), BF16),
            jax.ShapeDtypeStruct((2, ff // 2, model), BF16),
        ),
        in_specs=hbm_specs(1) + vmem_specs(5) + hbm_specs(2) + vmem_specs(2) + hbm_specs(2),
        out_specs=tuple(vmem_specs(5)),
        scratch_shapes=[
            pltpu.VMEM((tokens, model), BF16),
            pltpu.VMEM((rows, 3 * model), BF16),
            pltpu.VMEM((1, rows), BF16),
            pltpu.VMEM(win.shape, BF16),
            pltpu.VMEM(wout.shape, BF16),
            dma(5),
            pltpu.VMEM((8, LANES), F32),
            block(4), block(4), block(2, 2), block(), block(),
            pltpu.VMEM((heads, tokens, model), BF16), pltpu.VMEM((heads, tokens, model), BF16),
            pltpu.VMEM((blks, rows, 3 * LANES), BF16), pltpu.VMEM((blks, rows, 3 * LANES), BF16),
            pltpu.VMEM((heads, rows, 3 * LANES), BF16),
            pltpu.VMEM((heads, blks, part, wide), BF16), pltpu.VMEM((blks, part, wide), BF16),
            pltpu.VMEM((blks, part, wide), BF16), pltpu.VMEM((heads, part, wide), BF16),
            pltpu.SemaphoreType.DMA, pltpu.SemaphoreType.DMA, pltpu.SemaphoreType.DMA, pltpu.SemaphoreType.DMA,
            dma(4), dma(4), dma(4), dma(2, 2),
            dma(heads), dma(heads), dma(blks), dma(blks), dma(heads), dma(heads), dma(heads), dma(heads),
            dma(blks), dma(blks), dma(heads), dma(heads), dma(2), dma(2),
        ],
        compiler_params=pltpu.CompilerParams(
            collective_id=3, has_side_effects=True, vmem_limit_bytes=24 * MIB
        ),
        name="last",
    )(
        *in_hbm(x), dh, dq.reshape(2, span, LANES), dkv, xa, wa, *in_hbm(w_qkv, g1.reshape(1, rows)),
        grads.reshape(blks, heads, part, wide), rx, *in_hbm(win, wout),
    )


def finish_kernel(
    experts,
    y_ref, dx_ref, dw_ref, shared_ref, din_ref, dout_ref,
    y_out, dx_out, g1_out, dw_out, dwo_out, g2_out, wr_out, din_out, dout_out,
    tile, wr, g2, g1, din, dout, sem, wide_sem,
):
    rows = shared_ref.shape[0]
    model = dx_ref.shape[1]
    copies = [
        pltpu.make_async_copy(dx_ref, dx_out, sem.at[0]),
        pltpu.make_async_copy(dw_ref, dw_out, sem.at[1]),
        pltpu.make_async_copy(shared_ref.at[:, pl.ds(0, model)], dwo_out, sem.at[2]),
        pltpu.make_async_copy(y_ref, y_out, sem.at[6]),
    ]
    for copy in copies:
        copy.start()
    half = dout_ref.shape[1]
    quarter = half // 2
    for piece in range(4):
        down = slice(piece * quarter, (piece + 1) * quarter)
        dout[down, :] = dout_ref[piece // 2, (piece % 2) * quarter : (piece % 2 + 1) * quarter, :].astype(F32)
        copies.append(pltpu.make_async_copy(dout.at[down], dout_out.at[down], wide_sem.at[piece]))
        copies[-1].start()
    step = model // 4
    for piece in range(4):
        down = slice(piece * step, (piece + 1) * step)
        for side in range(2):
            din[down, side * half : (side + 1) * half] = din_ref[side, down, :].astype(F32)
        copies.append(pltpu.make_async_copy(din.at[down], din_out.at[down], wide_sem.at[4 + piece]))
        copies[-1].start()
    tile[...] = jnp.zeros_like(tile)
    tile[0:rows, :] = shared_ref[:, model : model + LANES]
    across = jnp.transpose(tile[...])[:, 0:rows]
    wr[...] = across[0:experts]
    g2[...] = across[experts : experts + 1]
    g1[...] = across[experts + 1 : experts + 2]
    for index, (src, dst) in enumerate(((wr, wr_out), (g2, g2_out), (g1, g1_out))):
        copies.append(pltpu.make_async_copy(src, dst, sem.at[3 + index]))
        copies[-1].start()
    for copy in copies:
        copy.wait()


def call_finish(output, dx, dw, shared, d_in, d_out):
    rows = shared.shape[0]
    model = dx.shape[1]
    experts = model // rows
    ff = 2 * d_out.shape[1]
    return pl.pallas_call(
        functools.partial(finish_kernel, experts),
        out_shape=(
            jax.ShapeDtypeStruct(output.shape, BF16),
            jax.ShapeDtypeStruct(dx.shape, F32),
            jax.ShapeDtypeStruct((1, rows), F32),
            jax.ShapeDtypeStruct(dw.shape, F32),
            jax.ShapeDtypeStruct((rows, model), F32),
            jax.ShapeDtypeStruct((1, rows), F32),
            jax.ShapeDtypeStruct((experts, rows), F32),
            jax.ShapeDtypeStruct((model, ff), F32),
            jax.ShapeDtypeStruct((ff, model), F32),
        ),
        in_specs=vmem_specs(6),
        out_specs=tuple(hbm_specs(9)),
        scratch_shapes=[
            pltpu.VMEM((LANES, LANES), F32),
            pltpu.VMEM((experts, rows), F32),
            pltpu.VMEM((1, rows), F32),
            pltpu.VMEM((1, rows), F32),
            pltpu.VMEM((model, ff), F32),
            pltpu.VMEM((ff, model), F32),
            dma(7),
            dma(8),
        ],
        compiler_params=pltpu.CompilerParams(vmem_limit_bytes=16 * MIB),
        name="finish",
    )(output, dx, dw, shared, d_in, d_out)


def local_kernels(
    inputs, ln1_gain, w_qkv, w_out, ln2_gain, w_router,
    expert_in, expert_out, routes, priority, doc_lengths, d_out,
):
    heads, blks = lax.axis_size("head"), lax.axis_size("blk")
    model = inputs.shape[1]
    tokens = inputs.shape[0]
    win, wout = expert_in[0], expert_out[0]
    q, kv, xa, wa, wo, kvt, bounds = call_qkv(
        inputs, w_qkv, ln1_gain, w_out, w_router, ln2_gain, doc_lengths, heads, blks
    )
    o, o_low, lse = call_forward(bounds, q, kv, kvt)
    output, dh, d_o, grads, rx = call_middle(
        inputs, o_low.reshape(2, heads, tokens // 2, LANES), wo.reshape(model, model + LANES),
        routes, priority, d_out, win, wout, heads, blks,
    )
    dq, dkv = call_backward(bounds, q, kv, kvt, d_o, o, lse)
    ends = call_last(
        inputs, dh, dq, dkv, xa, wa, w_qkv, ln1_gain, grads, rx, win, wout, heads, blks
    )
    output, d_inputs, d_gain_one, d_qkv, d_out_proj, d_gain_two, d_router, d_in, d_out_weight = call_finish(output, *ends)
    return (
        output,
        d_inputs,
        d_gain_one.reshape(-1),
        d_qkv,
        d_out_proj,
        d_gain_two.reshape(-1),
        d_router.T,
        d_in[None],
        d_out_weight[None],
    )


def solution(mesh):
    in_specs = (
        P(("blk", "head"), None),
        P("blk"),
        P("blk", None),
        P("blk", None),
        P("blk"),
        P("blk", None),
        P("blk", None, None),
        P("blk", None, None),
        P(("blk", "head"), None),
        P(("blk", "head"), None),
        P(),
        P(("blk", "head"), None),
    )
    out_specs = (
        P(("blk", "head"), None),
        P(("blk", "head"), None),
        P("blk"),
        P("blk", None),
        P("blk", None),
        P("blk"),
        P("blk", None),
        P("blk", None, None),
        P("blk", None, None),
    )
    fits = mesh.shape["head"] == 4 and mesh.shape["blk"] == 8
    body = local_kernels if fits else local
    return jax.shard_map(body, mesh=mesh, in_specs=in_specs, out_specs=out_specs, check_vma=False)
```

```python
import functools
import math

import jax
import jax.numpy as jnp
from jax import lax
from jax.experimental import pallas as pl
from jax.experimental.pallas import tpu as pltpu
from jax.sharding import PartitionSpec as P

HS = 64
KEY_BLOCK = 2048


PRECISE = lax.Precision.HIGHEST
MASKED = -1e30
EPSILON = 1e-06


def layer_norm(values, gain):
    average = jnp.mean(values, axis=-1, keepdims=True)
    centred = values - average
    spread = jnp.mean(centred * centred, axis=-1, keepdims=True)
    return centred * lax.rsqrt(spread + EPSILON) * gain


def gelu_exact(values):
    return jax.nn.gelu(values, approximate=False)


def router(row_block, weight):
    return jax.nn.softmax(jnp.dot(row_block, weight, precision=PRECISE), axis=-1)


def doc_index(positions, doc_lengths):
    places = jnp.arange(doc_lengths.shape[0], dtype=jnp.int32)
    starts = jnp.sum(jnp.where(places[None, :] < places[:, None], doc_lengths[None, :], 0), axis=1)
    at_most = (starts[None, :] <= positions[:, None]).astype(jnp.int32)
    return jnp.sum(at_most, axis=1) - 1


def slot_table(route_rows, ranking, capacity):
    token_count = route_rows.shape[0]
    expert = jnp.transpose(route_rows).reshape(-1)
    pair_order = (jnp.arange(2, dtype=jnp.int32)[:, None] * token_count + ranking[None, :]).reshape(
        -1
    )
    before = (expert[:, None] == expert[None, :]) & (pair_order[None, :] < pair_order[:, None])
    position = jnp.sum(before.astype(jnp.int32), axis=1)
    slot_ids = jnp.where(position < capacity, expert * capacity + position, -1)
    return slot_ids.reshape(2, token_count)


def keep_state(current):
    return current


def local(
    inputs,
    ln1_gain,
    w_qkv,
    w_out,
    ln2_gain,
    w_router,
    expert_in,
    expert_out,
    routes,
    priority,
    doc_lengths,
    d_out,
):
    blk_size = lax.axis_size("blk")
    tok_rows = inputs.shape[0]
    model_width = inputs.shape[1]
    capacity = 2 * tok_rows // blk_size
    slot_total = blk_size * capacity
    gain_one, qkv_weight, out_weight, gain_two, router_weight = (
        lax.all_gather(ln1_gain, "blk", axis=0, tiled=True),
        lax.all_gather(w_qkv, "blk", axis=0, tiled=True),
        lax.all_gather(w_out, "blk", axis=0, tiled=True),
        lax.all_gather(ln2_gain, "blk", axis=0, tiled=True),
        lax.all_gather(w_router, "blk", axis=0, tiled=True),
    )
    input_rows = inputs.astype(jnp.float32)
    normed_one, norm_one_pull = jax.vjp(layer_norm, input_rows, gain_one.astype(jnp.float32))
    normed_low = normed_one.astype(jnp.bfloat16)
    qkv_rows = jnp.dot(normed_low, qkv_weight, preferred_element_type=jnp.float32).astype(
        jnp.bfloat16
    )
    query_heads, key_heads, value_heads = (
        lax.all_to_all(qkv_rows[:, :model_width], "head", split_axis=1, concat_axis=0, tiled=True),
        lax.all_to_all(
            qkv_rows[:, model_width : 2 * model_width],
            "head",
            split_axis=1,
            concat_axis=0,
            tiled=True,
        ),
        lax.all_to_all(
            qkv_rows[:, 2 * model_width :], "head", split_axis=1, concat_axis=0, tiled=True
        ),
    )
    span_rows = query_heads.shape[0]
    head_count = query_heads.shape[1] // HS
    key_all, value_all = (
        lax.all_gather(key_heads, "blk", axis=0, tiled=True),
        lax.all_gather(value_heads, "blk", axis=0, tiled=True),
    )
    total_rows = key_all.shape[0]
    block_count = total_rows // KEY_BLOCK
    scale_factor = HS ** (-0.5)
    query_pos = lax.axis_index("blk") * span_rows + jnp.arange(span_rows, dtype=jnp.int32)
    query_docs = doc_index(query_pos, doc_lengths)
    queries = query_heads.reshape(span_rows, head_count, HS)

    def block_parts(block_index, key_source, value_source):
        first_key = block_index * KEY_BLOCK
        key_rows = lax.dynamic_slice_in_dim(key_source, first_key, KEY_BLOCK, 0).reshape(
            KEY_BLOCK, head_count, HS
        )
        value_rows = lax.dynamic_slice_in_dim(value_source, first_key, KEY_BLOCK, 0).reshape(
            KEY_BLOCK, head_count, HS
        )
        key_docs = doc_index(first_key + jnp.arange(KEY_BLOCK, dtype=jnp.int32), doc_lengths)
        is_live = (key_docs[0] <= query_docs[-1]) & (key_docs[-1] >= query_docs[0])
        same_doc = query_docs[:, None] == key_docs[None, :]
        return (first_key, key_rows, value_rows, same_doc, is_live)

    def block_scores(key_rows, same_doc):
        raw_scores = (
            jnp.einsum("qhd,khd->hqk", queries, key_rows, preferred_element_type=jnp.float32)
            * scale_factor
        )
        return jnp.where(same_doc[None], raw_scores, MASKED)

    def stat_step(block_index, loop_state):
        first_key, key_rows, value_rows, same_doc, is_live = block_parts(
            block_index, key_all, value_all
        )

        def stat_update(current):
            running_max, running_sum = current
            scores = block_scores(key_rows, same_doc)
            new_max = jnp.maximum(running_max, jnp.max(scores, axis=2))
            exp_terms = jnp.where(same_doc[None], jnp.exp(scores - new_max[:, :, None]), 0.0)
            return (
                new_max,
                running_sum * jnp.exp(running_max - new_max) + jnp.sum(exp_terms, axis=2),
            )

        return lax.cond(is_live, stat_update, keep_state, loop_state)

    start_state = (
        jnp.full((head_count, span_rows), MASKED, jnp.float32),
        jnp.zeros((head_count, span_rows), jnp.float32),
    )
    running_max, running_sum = lax.fori_loop(0, block_count, stat_step, start_state)
    log_total = running_max + jnp.log(running_sum)

    def out_step(block_index, loop_state):
        first_key, key_rows, value_rows, same_doc, is_live = block_parts(
            block_index, key_all, value_all
        )

        def out_update(current):
            scores = block_scores(key_rows, same_doc)
            weights = jnp.where(
                same_doc[None], jnp.exp(scores - log_total[:, :, None]), 0.0
            ).astype(jnp.bfloat16)
            return current + jnp.einsum(
                "hqk,khd->qhd", weights, value_rows, preferred_element_type=jnp.float32
            )

        return lax.cond(is_live, out_update, keep_state, loop_state)

    mixed_full = lax.fori_loop(
        0, block_count, out_step, jnp.zeros((span_rows, head_count, HS), jnp.float32)
    )
    mixed_low = mixed_full.reshape(span_rows, head_count * HS).astype(jnp.bfloat16)
    mixed_tokens = lax.all_to_all(mixed_low, "head", split_axis=0, concat_axis=1, tiled=True)
    attended = jnp.dot(mixed_tokens, out_weight, preferred_element_type=jnp.float32)
    hidden_one = input_rows + attended
    normed_two, norm_two_pull = jax.vjp(layer_norm, hidden_one, gain_two.astype(jnp.float32))
    routed_low = normed_two.astype(jnp.bfloat16)
    router_probs, router_pull = jax.vjp(
        router, routed_low.astype(jnp.float32), router_weight.astype(jnp.float32)
    )
    slot_ids = slot_table(routes, priority[0], capacity)
    select = (
        slot_ids[:, :, None] == jnp.arange(slot_total, dtype=jnp.int32)[None, None, :]
    ).astype(jnp.bfloat16)
    send_rows = jnp.einsum(
        "kts,td->sd", select, routed_low, preferred_element_type=jnp.float32
    ).astype(jnp.bfloat16)
    expert_rows = lax.all_to_all(
        send_rows.reshape(blk_size, capacity, model_width),
        "blk",
        split_axis=0,
        concat_axis=0,
        tiled=True,
    ).reshape(slot_total, model_width)
    weight_in = expert_in[0]
    weight_out = expert_out[0]
    pre_act = jnp.dot(expert_rows, weight_in, preferred_element_type=jnp.float32)
    hidden_act, gelu_pull = jax.vjp(gelu_exact, pre_act)
    hidden_low = hidden_act.astype(jnp.bfloat16)
    expert_result = jnp.dot(hidden_low, weight_out, preferred_element_type=jnp.float32).astype(
        jnp.bfloat16
    )
    slot_result = lax.all_to_all(
        expert_result.reshape(blk_size, capacity, model_width),
        "blk",
        split_axis=0,
        concat_axis=0,
        tiled=True,
    ).reshape(slot_total, model_width)
    pair_result = jnp.einsum("kts,sd->ktd", select, slot_result, preferred_element_type=jnp.float32)
    route_hot = (routes[:, :, None] == jnp.arange(blk_size, dtype=jnp.int32)[None, None, :]).astype(
        jnp.float32
    )
    gate_vals = jnp.sum(router_probs[:, None, :] * route_hot, axis=2)
    mixture = gate_vals[:, 0, None] * pair_result[0] + gate_vals[:, 1, None] * pair_result[1]
    output = (hidden_one + mixture).astype(jnp.bfloat16)
    d_gates = jnp.transpose(jnp.sum(d_out[None] * pair_result, axis=2))
    d_probs = jnp.sum(d_gates[:, :, None] * route_hot, axis=1)
    pair_grads = (jnp.transpose(gate_vals)[:, :, None] * d_out[None]).astype(jnp.bfloat16)
    slot_grads = jnp.einsum(
        "kts,ktd->sd", select, pair_grads, preferred_element_type=jnp.float32
    ).astype(jnp.bfloat16)
    result_grads = lax.all_to_all(
        slot_grads.reshape(blk_size, capacity, model_width),
        "blk",
        split_axis=0,
        concat_axis=0,
        tiled=True,
    ).reshape(slot_total, model_width)
    d_hidden_act = jnp.dot(result_grads, weight_out.T, preferred_element_type=jnp.float32)
    d_weight_out = jnp.dot(hidden_low.T, result_grads, preferred_element_type=jnp.float32)
    d_preact = gelu_pull(d_hidden_act)[0].astype(jnp.bfloat16)
    d_weight_in = jnp.dot(expert_rows.T, d_preact, preferred_element_type=jnp.float32)
    row_grads = jnp.dot(d_preact, weight_in.T, preferred_element_type=jnp.float32).astype(
        jnp.bfloat16
    )
    slot_back = lax.all_to_all(
        row_grads.reshape(blk_size, capacity, model_width),
        "blk",
        split_axis=0,
        concat_axis=0,
        tiled=True,
    ).reshape(slot_total, model_width)
    d_routed = jnp.einsum("kts,sd->td", select, slot_back, preferred_element_type=jnp.float32)
    d_routed_router, d_router = router_pull(d_probs)
    d_hidden_norm, d_gain_two = norm_two_pull(d_routed + d_routed_router)
    d_hidden_one = d_out + d_hidden_norm
    attn_grads = d_hidden_one.astype(jnp.bfloat16)
    d_out_weight = jnp.dot(mixed_tokens.T, attn_grads, preferred_element_type=jnp.float32)
    mixed_grads = jnp.dot(attn_grads, out_weight.T, preferred_element_type=jnp.float32).astype(
        jnp.bfloat16
    )
    head_grads = lax.all_to_all(mixed_grads, "head", split_axis=1, concat_axis=0, tiled=True)
    out_grads = head_grads.reshape(span_rows, head_count, HS)
    row_delta = jnp.transpose(jnp.sum(out_grads.astype(jnp.float32) * mixed_full, axis=2))
    key_back, value_back = (
        lax.all_gather(key_heads, "blk", axis=0, tiled=True),
        lax.all_gather(value_heads, "blk", axis=0, tiled=True),
    )

    def grad_step(block_index, loop_state):
        first_key, key_rows, value_rows, same_doc, is_live = block_parts(
            block_index, key_back, value_back
        )

        def grad_update(current):
            query_grad, key_grad, value_grad = current
            scores = block_scores(key_rows, same_doc)
            weights = jnp.where(same_doc[None], jnp.exp(scores - log_total[:, :, None]), 0.0)
            value_part = jnp.einsum(
                "hqk,qhd->khd",
                weights.astype(jnp.bfloat16),
                out_grads,
                preferred_element_type=jnp.float32,
            )
            weight_grads = jnp.einsum(
                "qhd,khd->hqk", out_grads, value_rows, preferred_element_type=jnp.float32
            )
            score_grads = (weights * (weight_grads - row_delta[:, :, None])).astype(jnp.bfloat16)
            query_grad = (
                query_grad
                + jnp.einsum(
                    "hqk,khd->qhd", score_grads, key_rows, preferred_element_type=jnp.float32
                )
                * scale_factor
            )
            key_part = (
                jnp.einsum("hqk,qhd->khd", score_grads, queries, preferred_element_type=jnp.float32)
                * scale_factor
            )
            key_grad = lax.dynamic_update_slice_in_dim(
                key_grad, key_part.reshape(KEY_BLOCK, head_count * HS), first_key, 0
            )
            value_grad = lax.dynamic_update_slice_in_dim(
                value_grad, value_part.reshape(KEY_BLOCK, head_count * HS), first_key, 0
            )
            return (query_grad, key_grad, value_grad)

        return lax.cond(is_live, grad_update, keep_state, loop_state)

    start_grads = (
        jnp.zeros((span_rows, head_count, HS), jnp.float32),
        jnp.zeros((total_rows, head_count * HS), jnp.float32),
        jnp.zeros((total_rows, head_count * HS), jnp.float32),
    )
    query_grad, key_grad, value_grad = lax.fori_loop(0, block_count, grad_step, start_grads)
    key_own, value_own = (
        lax.psum_scatter(
            key_grad.astype(jnp.bfloat16), "blk", scatter_dimension=0, tiled=True
        ).astype(jnp.float32),
        lax.psum_scatter(
            value_grad.astype(jnp.bfloat16), "blk", scatter_dimension=0, tiled=True
        ).astype(jnp.float32),
    )
    query_tokens_grad, key_tokens_grad, value_tokens_grad = (
        lax.all_to_all(
            query_grad.reshape(span_rows, head_count * HS).astype(jnp.bfloat16),
            "head",
            split_axis=0,
            concat_axis=1,
            tiled=True,
        ),
        lax.all_to_all(
            key_own.astype(jnp.bfloat16), "head", split_axis=0, concat_axis=1, tiled=True
        ),
        lax.all_to_all(
            value_own.astype(jnp.bfloat16), "head", split_axis=0, concat_axis=1, tiled=True
        ),
    )
    qkv_grads = jnp.concatenate([query_tokens_grad, key_tokens_grad, value_tokens_grad], axis=1)
    d_qkv_weight = jnp.dot(normed_low.T, qkv_grads, preferred_element_type=jnp.float32)
    normed_grads = jnp.dot(qkv_grads, qkv_weight.T, preferred_element_type=jnp.float32)
    d_inputs_norm, d_gain_one = norm_one_pull(normed_grads)
    d_inputs = d_hidden_one + d_inputs_norm
    gain_one_sum, qkv_sum, out_sum, gain_two_sum, router_sum = (
        lax.psum_scatter(
            d_gain_one.astype(jnp.bfloat16), "blk", scatter_dimension=0, tiled=True
        ).astype(jnp.float32),
        lax.psum_scatter(
            d_qkv_weight.astype(jnp.bfloat16), "blk", scatter_dimension=0, tiled=True
        ).astype(jnp.float32),
        lax.psum_scatter(
            d_out_weight.astype(jnp.bfloat16), "blk", scatter_dimension=0, tiled=True
        ).astype(jnp.float32),
        lax.psum_scatter(
            d_gain_two.astype(jnp.bfloat16), "blk", scatter_dimension=0, tiled=True
        ).astype(jnp.float32),
        lax.psum_scatter(
            d_router.astype(jnp.bfloat16), "blk", scatter_dimension=0, tiled=True
        ).astype(jnp.float32),
    )
    gain_one_all, qkv_all, out_all, gain_two_all, router_all, expert_in_all, expert_out_all = (
        lax.psum(gain_one_sum.astype(jnp.bfloat16), "head").astype(jnp.float32),
        lax.psum(qkv_sum.astype(jnp.bfloat16), "head").astype(jnp.float32),
        lax.psum(out_sum.astype(jnp.bfloat16), "head").astype(jnp.float32),
        lax.psum(gain_two_sum.astype(jnp.bfloat16), "head").astype(jnp.float32),
        lax.psum(router_sum.astype(jnp.bfloat16), "head").astype(jnp.float32),
        lax.psum(d_weight_in[None].astype(jnp.bfloat16), "head").astype(jnp.float32),
        lax.psum(d_weight_out[None].astype(jnp.bfloat16), "head").astype(jnp.float32),
    )
    return (
        output,
        d_inputs,
        gain_one_all,
        qkv_all,
        out_all,
        gain_two_all,
        router_all,
        expert_in_all,
        expert_out_all,
    )


MESH = pl.DeviceIdType.MESH
LANES = 128
HALF = LANES // 2
MIB = 2**20
F32 = jnp.float32
BF16 = jnp.bfloat16


def dot(left, right, dims=(1, 0)):
    return lax.dot_general(
        left, right, (((dims[0],), (dims[1],)), ((), ())), preferred_element_type=F32
    )


def remote(src, dst, send_sem, recv_sem, head, blk):
    return pltpu.make_async_remote_copy(
        src_ref=src,
        dst_ref=dst,
        send_sem=send_sem,
        recv_sem=recv_sem,
        device_id={"head": head, "blk": blk},
        device_id_type=MESH,
    )


def arrived(ref, sem):
    pltpu.make_async_copy(ref, ref, sem).wait()


def greet(peers):
    barrier = pltpu.get_barrier_semaphore()
    for head, blk in peers:
        pl.semaphore_signal(
            barrier, inc=1, device_id={"head": head, "blk": blk}, device_id_type=MESH
        )
    return len(peers)


def meet(count):
    pl.semaphore_wait(pltpu.get_barrier_semaphore(), count)


def halves(values, lanes_kept):
    rows = values.shape[0] // 2
    moved = pltpu.roll(values[rows:], HALF, 1)
    return jnp.where(lanes_kept, values[:rows], moved)


def lane_ids(shape):
    return lax.broadcasted_iota(jnp.int32, shape, len(shape) - 1)


def centre(values):
    average = jnp.mean(values, axis=-1, keepdims=True)
    centred = values - average
    spread = jnp.mean(centred * centred, axis=-1, keepdims=True)
    scale = lax.rsqrt(spread + EPSILON)
    return centred * scale, scale


def centre_back(grad, xhat, scale):
    middle = jnp.mean(grad, axis=-1, keepdims=True)
    along = jnp.mean(grad * xhat, axis=-1, keepdims=True)
    return (grad - middle - xhat * along) * scale


def split_high_low(column, lanes):
    high = column.astype(BF16)
    low = (column - high.astype(F32)).astype(BF16)
    return jnp.where(lanes < HALF, high.astype(F32), low.astype(F32)).astype(BF16)


def join_high_low(matrix, start):
    return matrix[:, start : start + 1].astype(F32) + matrix[
        :, start + HALF : start + HALF + 1
    ].astype(F32)


def place():
    head, blk = lax.axis_index("head"), lax.axis_index("blk")
    return head, blk, blk // 2, lax.rem(blk, 2)


def around(index, step, size):
    return lax.rem(index + step, size)


QUERY_TILE = 256
CHAINS = 2


def masked_queries(q_ref, tile, key_lanes, query_tile):
    tiles_per_span = q_ref.shape[1] // query_tile
    inner = tile % tiles_per_span * query_tile
    query = q_ref[tile // tiles_per_span, inner : inner + query_tile, :]
    return jnp.where(key_lanes, query, jnp.zeros_like(query))


def group_blocks(bounds_ref, group, size, key_tile):
    first, last = group * size, (group + 1) * size
    low = jnp.min(bounds_ref[0:1, first : first + LANES])
    high = jnp.max(bounds_ref[1:2, last - LANES : last])
    return low // key_tile, (high + key_tile - 1) // key_tile


def inside_document(bounds_ref, tile, first, shape):
    key = first + lax.broadcasted_iota(jnp.int32, shape, 0)
    columns = slice(tile * shape[1], (tile + 1) * shape[1])
    return jnp.logical_and(key >= bounds_ref[0:1, columns], key < bounds_ref[1:2, columns])


def query_group(q_ref, group, y):
    key_lanes = (lane_ids((QUERY_TILE, LANES)) < HALF) == (y == 0)
    tiles = range(group * CHAINS, (group + 1) * CHAINS)
    return tiles, [masked_queries(q_ref, tile, key_lanes, QUERY_TILE) for tile in tiles]


def attend(bounds_ref, tiles, first, keys, keys_across, queries, carry):
    scores = [dot(keys, query, (1, 1)) for query in queries]
    made = []
    for tile, score, (biggest, weight, mixed) in zip(tiles, scores, carry):
        inside = inside_document(bounds_ref, tile, first, score.shape)
        score = jnp.where(inside, score, MASKED)
        bigger = jnp.maximum(biggest, jnp.max(score, axis=0, keepdims=True))
        fade = jnp.exp(biggest - bigger)
        terms = jnp.exp(score - bigger)
        weight = weight * fade + jnp.sum(terms, axis=0, keepdims=True)
        made.append((bigger, weight, mixed * fade + dot(keys_across, terms.astype(BF16))))
    return tuple(made)


def nothing_attended():
    return (
        jnp.full((1, QUERY_TILE), MASKED, F32),
        jnp.zeros((1, QUERY_TILE), F32),
        jnp.zeros((LANES, QUERY_TILE), F32),
    )


def attend_back(bounds_ref, tiles, first, keys, keys_across, group, carry):
    queries, out_grads, deltas, log_totals = group
    scores = [dot(keys, query, (1, 1)) for query in queries]
    weight_grads = [dot(keys, out_grad, (1, 1)) for out_grad in out_grads]
    pieces, score_grads = [], []
    for i, tile in enumerate(tiles):
        inside = inside_document(bounds_ref, tile, first, scores[i].shape)
        weights = jnp.exp(jnp.where(inside, scores[i], MASKED) - log_totals[i])
        score_grads.append((weights * (weight_grads[i] - deltas[i])).astype(BF16))
        pieces.append(weights.astype(BF16))
    wide = jnp.concatenate(score_grads + pieces, axis=1)
    given = dot(wide, jnp.concatenate(queries + out_grads, axis=0))
    return given, tuple(c + dot(keys_across, g) for c, g in zip(carry, score_grads))


def group_grads(do_ref, tiles, y):
    key_lanes = (lane_ids((QUERY_TILE, LANES)) < HALF) == (y == 0)
    out_grads = []
    for tile in tiles:
        parts = []
        for part in range(QUERY_TILE // LANES):
            packed = do_ref[tile, part].astype(F32)
            parts += [packed, pltpu.roll(packed, HALF, 1)]
        out_grads.append(jnp.where(key_lanes, 0.0, jnp.concatenate(parts, axis=0)).astype(BF16))
    return out_grads


def qkv_kernel(
    heads, blks,
    x_hbm, w_hbm, g1_hbm, wo_hbm, wr_hbm, g2_hbm, docs_hbm,
    qall, kvall, xall, wall, wo_all, kvt, bounds, begun,
    x_ref, w_ref, rows_in, g1_ref, g2_ref, wr_ref, docs_ref, wo_own, kv_other, q_packed, q_landed, in_sem,
    x_send, x_recv, w_send, w_recv, o_send, o_recv, p_send, p_recv,
    k_send, k_recv, q_recv,
):
    head, blk, z, y = place()
    planes = blks // 2
    model = x_ref.shape[1]
    rows = w_ref.shape[0]
    part = rows // heads
    experts = wr_ref.shape[0]
    wanted = (
        (w_hbm, w_ref), (g1_hbm, g1_ref), (g2_hbm, g2_ref), (wr_hbm, wr_ref), (x_hbm, x_ref),
        (wo_hbm, wo_own.at[:, pl.ds(0, model)]), (docs_hbm, docs_ref),
    )
    fetched = [
        pltpu.make_async_copy(src, dst, in_sem.at[i]) for i, (src, dst) in enumerate(wanted)
    ]
    for copy in fetched:
        copy.start()
    rows_in[...] = jnp.zeros_like(rows_in)
    met = greet(
        [(around(head, k, heads), blk) for k in range(1, heads)]
        + [(head, around(blk, k, blks)) for k in range(1, blks)]
    )
    lanes = lane_ids((rows, LANES))
    for copy in fetched:
        copy.wait()
    rows_in[0:experts, 0:rows] = wr_ref[...].astype(F32)
    rows_in[experts : experts + 1, 0:rows] = g2_ref[...].astype(F32)
    rows_in[experts + 1 : experts + 2, 0:rows] = g1_ref[...].astype(F32)
    vectors = jnp.transpose(rows_in[...])[:rows]
    gain = vectors[:, experts + 1 : experts + 2]

    def columns(which):
        start = pl.multiple_of(which * model + head * LANES, LANES)
        return w_ref[:, pl.ds(start, LANES)].astype(F32) * gain

    key_cols = columns(1)
    value_cols = pltpu.roll(columns(2), HALF, 1)
    wall[blk, :, 0:LANES] = jnp.where(lanes < HALF, key_cols, value_cols).astype(BF16)
    wall[blk, :, LANES : 2 * LANES] = jnp.where(lanes < HALF, value_cols, key_cols).astype(BF16)
    wall[blk, :, 2 * LANES : 3 * LANES] = (columns(0) * HS ** (-0.5)).astype(BF16)
    w_copies = [
        remote(wall.at[blk], wall.at[blk], w_send.at[k], w_recv.at[k], head, around(blk, k, blks))
        for k in range(1, blks)
    ]
    xhat, _ = centre(x_ref[...].astype(F32))
    xall[head] = xhat.astype(BF16)
    meet(met)
    for copy in w_copies:
        copy.start()
    x_copies = [
        remote(xall.at[head], xall.at[head], x_send.at[k], x_recv.at[k], around(head, k, heads), blk)
        for k in range(1, heads)
    ]
    for copy in x_copies:
        copy.start()
    wo_own[:, model : model + LANES] = vectors.astype(BF16)
    wo_all[blk, head] = wo_own[pl.ds(pl.multiple_of(head * part, part), part), :]
    o_copies = [
        remote(
            wo_all.at[blk, head], wo_all.at[blk, head],
            o_send.at[k], o_recv.at[k], head, around(blk, k, blks),
        )
        for k in range(1, blks)
    ]
    document_bounds(docs_ref, bounds, z)
    for copy in w_copies:
        copy.wait_send()
    for copy in o_copies:
        copy.start()
    for copy in x_copies:
        copy.wait()
    for copy in w_copies:
        copy.wait_recv()
    weight = wall[...].reshape(model, 3 * LANES)
    tokens = x_ref.shape[0]
    even = y == 0
    above, below = z < planes - 1, z > 0
    half_span = kvall.shape[1] // 2
    sides = ((1, above, below, 0), (-1, below, above, 4))

    def half_of(ref, half):
        return ref.at[pl.ds(half * half_span, half_span)]

    def outward(slot, step, across, half):
        target = 2 * (z + step) + around(y, across, 2)
        return remote(
            half_of(kv_other if across else kvall.at[blk], half), half_of(kvall.at[blk], half),
            k_send.at[slot], k_recv.at[blk, half], head, target,
        )

    def onward(slot, step, side, half):
        from_span = 2 * (z - step) + side
        ref = half_of(kvall.at[from_span], half)
        return remote(ref, ref, k_send.at[slot], k_recv.at[from_span, half], head, 2 * (z + step) + y)

    def await_half(span, half):
        arrived(half_of(kvall.at[span], half), k_recv.at[span, half])

    def turn(span):
        size = kvall.shape[1]
        kvt[:, pl.ds(pl.multiple_of(span * size, size), size)] = jnp.transpose(kvall[span])

    for half in range(2):
        for piece in range(half * heads // 2, (half + 1) * heads // 2):
            made = dot(xall[piece], weight).astype(BF16)
            first, second = made[:, 0:LANES], made[:, LANES : 2 * LANES]
            span = slice(piece * tokens, (piece + 1) * tokens)
            kvall[blk, span, :] = jnp.where(even, first, second)
            kv_other[span, :] = jnp.where(even, second, first)
            qall[y, span, :] = made[:, 2 * LANES : 3 * LANES]
        outward(8 + half, 0, 1, half).start()
        for step, there, _, slot in sides:

            @pl.when(there)
            def _():
                outward(slot + 2 * half, step, 0, half).start()
                outward(slot + 2 * half + 1, step, 1, half).start()

    other_y = around(y, 1, 2)
    kept = (lane_ids(q_packed.shape) < HALF) == (y == 1)
    q_packed[...] = halves(qall[y].astype(F32), kept).astype(BF16)
    q_pair = remote(q_packed, q_landed, k_send.at[10], q_recv, head, 2 * z + other_y)
    q_pair.start()
    turn(blk)
    for copy in o_copies:
        copy.wait()
    core = lax.rem(head, 2)
    sibling, across = head - core + 1 - core, around(head, 2, heads)

    def quarter_copy(index, quarter, to_head):
        ref = wo_all.at[:, quarter]
        return remote(ref, ref, p_send.at[index], p_recv.at[index], to_head, blk)

    p_copies = [quarter_copy(0, head, sibling), quarter_copy(1, head, across)]
    for copy in p_copies:
        copy.start()
    p_copies.append(quarter_copy(2, across, sibling))
    for half in range(2):
        for step, there, back, slot in sides:

            @pl.when(back)
            def _():
                for side in range(2):
                    await_half(2 * (z - step) + side, half)

            @pl.when(jnp.logical_and(there, back))
            def _():
                for side in range(2):
                    onward(11 + slot + 2 * half + side, step, side, half).start()

    arrived(wo_all.at[:, across], p_recv.at[1])
    p_copies[2].start()
    pair = 2 * z + other_y
    for half in range(2):
        await_half(pair, half)
    turn(pair)
    q_pair.wait()
    landed = q_landed[...]
    qall[other_y, 0:half_span, :] = landed
    qall[other_y, half_span : 2 * half_span, :] = pltpu.roll(landed.astype(F32), HALF, 1).astype(BF16)
    key_tile = kvall.shape[1]
    for group in range(2 * key_tile // (CHAINS * QUERY_TILE)):
        tiles, queries = query_group(qall, group, y)
        carry = (nothing_attended(),) * CHAINS
        for side in range(2):
            first = pl.multiple_of((2 * z + side) * key_tile, key_tile)
            keys_across = kvt[:, pl.ds(first, key_tile)]
            carry = attend(bounds, tiles, first, kvall[2 * z + side], keys_across, queries, carry)
        for tile, (biggest, weight, mixed) in zip(tiles, carry):
            begun[tile, 0:LANES] = mixed
            begun[tile, LANES : LANES + 8] = jnp.broadcast_to(biggest, (8, QUERY_TILE))
            begun[tile, LANES + 8 : LANES + 16] = jnp.broadcast_to(weight, (8, QUERY_TILE))
    for step, there, back, slot in sides:

        @pl.when(back)
        def _():
            for side in range(2):
                turn(2 * (z - step) + side)

    for other in range(planes):
        for side in range(2):
            span = 2 * other + side

            @pl.when(jnp.logical_or(z - other == 2, other - z == 2))
            def _():
                for half in range(2):
                    await_half(span, half)
                turn(span)

    for index, quarter in ((0, sibling), (2, around(sibling, 2, heads))):
        arrived(wo_all.at[:, quarter], p_recv.at[index])
    for copy in p_copies:
        copy.wait_send()
    for half in range(2):
        outward(8 + half, 0, 1, half).wait_send()
        for step, there, back, slot in sides:

            @pl.when(there)
            def _():
                outward(slot + 2 * half, step, 0, half).wait_send()
                outward(slot + 2 * half + 1, step, 1, half).wait_send()

            @pl.when(jnp.logical_and(there, back))
            def _():
                for side in range(2):
                    onward(11 + slot + 2 * half + side, step, side, half).wait_send()


def document_bounds(docs_ref, bounds, z):
    count = docs_ref.shape[1]
    lengths = docs_ref[...].astype(F32)
    doc = lax.broadcasted_iota(jnp.int32, (count, count), 0)
    other = lane_ids((count, count))
    start = jnp.sum(jnp.where(other < doc, lengths, 0.0), axis=1, keepdims=True)
    end = jnp.sum(jnp.where(other <= doc, lengths, 0.0), axis=1, keepdims=True)
    queries = bounds.shape[1]
    token = (z * queries + lane_ids((count, queries))).astype(F32)
    begun = start <= token
    bounds[...] = jnp.zeros_like(bounds)
    bounds[0:1, :] = jnp.max(jnp.where(begun, start, 0.0), axis=0, keepdims=True).astype(jnp.int32)
    bounds[1:2, :] = jnp.max(jnp.where(begun, end, 0.0), axis=0, keepdims=True).astype(jnp.int32)


def vmem_specs(count):
    return [pl.BlockSpec(memory_space=pltpu.VMEM)] * count


def hbm_specs(count):
    return [pl.BlockSpec(memory_space=pltpu.HBM)] * count


def in_hbm(*arrays):
    return [pltpu.with_memory_space_constraint(array, pltpu.HBM) for array in arrays]


def dma(*shape):
    return pltpu.SemaphoreType.DMA(shape)


def call_qkv(x, w_qkv, g1, w_out, w_router, g2, doc_lengths, heads, blks):
    tokens, model = x.shape
    rows = w_qkv.shape[0]
    span = tokens * heads
    wide = model + LANES
    part = rows // heads
    return pl.pallas_call(
        functools.partial(qkv_kernel, heads, blks),
        out_shape=(
            jax.ShapeDtypeStruct((2, span, LANES), BF16),
            jax.ShapeDtypeStruct((blks, span, LANES), BF16),
            jax.ShapeDtypeStruct((heads, tokens, model), BF16),
            jax.ShapeDtypeStruct((blks, rows, 3 * LANES), BF16),
            jax.ShapeDtypeStruct((blks, heads, part, wide), BF16),
            jax.ShapeDtypeStruct((LANES, blks * span), BF16),
            jax.ShapeDtypeStruct((8, 2 * span), jnp.int32),
            jax.ShapeDtypeStruct((2 * span // QUERY_TILE, LANES + 16, QUERY_TILE), F32),
        ),
        in_specs=hbm_specs(7),
        out_specs=tuple(vmem_specs(8)),
        scratch_shapes=[
            pltpu.VMEM((tokens, model), BF16),
            pltpu.VMEM((rows, 3 * model), BF16),
            pltpu.VMEM((LANES, LANES), F32),
            pltpu.VMEM((1, rows), BF16),
            pltpu.VMEM((1, rows), BF16),
            pltpu.VMEM((w_router.shape[1], rows), BF16),
            pltpu.VMEM((1, doc_lengths.shape[0]), jnp.int32),
            pltpu.VMEM((rows, wide), BF16),
            pltpu.VMEM((span, LANES), BF16),
            pltpu.VMEM((span // 2, LANES), BF16),
            pltpu.VMEM((span // 2, LANES), BF16),
            dma(7),
            dma(heads), dma(heads), dma(blks), dma(blks), dma(blks), dma(blks), dma(heads), dma(heads),
            dma(19), dma(blks, 2), pltpu.SemaphoreType.DMA,
        ],
        compiler_params=pltpu.CompilerParams(
            collective_id=1, has_side_effects=True, vmem_limit_bytes=16 * MIB
        ),
        name="qkv",
    )(
        *in_hbm(
            x, w_qkv, g1.reshape(1, rows), w_out, w_router.T, g2.reshape(1, rows),
            doc_lengths.reshape(1, -1),
        )
    )


def other_blocks(bounds_ref, group, key_tile, z, step, carry):
    low, high = group_blocks(bounds_ref, group, CHAINS * QUERY_TILE, key_tile)
    carry = lax.fori_loop(low, 2 * z, step, carry)
    return lax.fori_loop(2 * z + 2, high, step, carry)


def forward_kernel(bounds_ref, q_ref, kv_ref, kvt_ref, begun_ref, o_out, ob_out, lse_out):
    _, _, z, y = place()
    key_tile = kv_ref.shape[1]
    value_lanes = (lane_ids((HALF, LANES)) < HALF) == (y == 1)
    for group in range(q_ref.shape[0] * q_ref.shape[1] // (CHAINS * QUERY_TILE)):
        tiles, queries = query_group(q_ref, group, y)

        def step(block, carry, queries=queries, tiles=tiles):
            first = pl.multiple_of(block * key_tile, key_tile)
            across = kvt_ref[:, pl.ds(first, key_tile)]
            return attend(bounds_ref, tiles, first, kv_ref[block], across, queries, carry)

        start = tuple(
            (begun_ref[t, LANES : LANES + 1], begun_ref[t, LANES + 8 : LANES + 9], begun_ref[t, 0:LANES])
            for t in tiles
        )
        ends = other_blocks(bounds_ref, group, key_tile, z, step, start)
        for tile, (biggest, weight, mixed) in zip(tiles, ends):
            result = jnp.transpose(mixed / weight)
            o_out[tile] = result
            for part in range(QUERY_TILE // LANES):
                block = result[part * LANES : (part + 1) * LANES]
                ob_out[tile, part] = halves(block, value_lanes).astype(BF16)
            lse_out[tile] = jnp.broadcast_to(biggest + jnp.log(weight), (8, QUERY_TILE))


def call_forward(bounds, q, kv, kvt, begun):
    blks, span, _ = kv.shape
    tiles = 2 * span // QUERY_TILE
    return pl.pallas_call(
        forward_kernel,
        out_shape=(
            jax.ShapeDtypeStruct((tiles, QUERY_TILE, LANES), F32),
            jax.ShapeDtypeStruct((tiles, QUERY_TILE // LANES, HALF, LANES), BF16),
            jax.ShapeDtypeStruct((tiles, 8, QUERY_TILE), F32),
        ),
        in_specs=vmem_specs(5),
        out_specs=tuple(vmem_specs(3)),
        compiler_params=pltpu.CompilerParams(vmem_limit_bytes=16 * MIB),
        name="attend",
    )(bounds, q, kv, kvt, begun)


def backward_kernel(
    bounds_ref, q_ref, kv_ref, kvt_ref, do_ref, o_ref, lse_ref, dq_out, dkv_out, delta_out, dkv
):
    _, _, z, y = place()
    key_tile = kv_ref.shape[1]
    dkv[...] = jnp.zeros_like(dkv)
    for group in range(q_ref.shape[0] * q_ref.shape[1] // (CHAINS * QUERY_TILE)):
        tiles, queries = query_group(q_ref, group, y)
        out_grads = group_grads(do_ref, tiles, y)
        deltas, log_totals = [], []
        for tile, out_grad in zip(tiles, out_grads):
            product = jnp.transpose(out_grad.astype(F32) * o_ref[tile])
            deltas.append(jnp.sum(product, axis=0, keepdims=True))
            delta_out[tile] = jnp.broadcast_to(deltas[-1], delta_out.shape[1:])
            log_totals.append(lse_ref[tile, 0:1, :])
        known = (queries, out_grads, deltas, log_totals)

        def step(block, carry, tiles=tiles, known=known):
            first = pl.multiple_of(block * key_tile, key_tile)
            across = kvt_ref[:, pl.ds(first, key_tile)]
            given, carry = attend_back(bounds_ref, tiles, first, kv_ref[block], across, known, carry)
            dkv[block] += given
            return carry

        zero = jnp.zeros((LANES, QUERY_TILE), F32)
        ends = other_blocks(bounds_ref, group, key_tile, z, step, (zero,) * CHAINS)
        for tile, mixed in zip(tiles, ends):
            dq_out[tile] = mixed
    for block in range(dkv.shape[0]):
        dkv_out[block] = dkv[block].astype(BF16)


def call_backward(bounds, q, kv, kvt, d_o, o, lse):
    blks, span, _ = kv.shape
    tiles = 2 * span // QUERY_TILE
    return pl.pallas_call(
        backward_kernel,
        out_shape=(
            jax.ShapeDtypeStruct((tiles, LANES, QUERY_TILE), F32),
            jax.ShapeDtypeStruct((blks, span, LANES), BF16),
            jax.ShapeDtypeStruct((tiles, 8, QUERY_TILE), F32),
        ),
        in_specs=vmem_specs(7),
        out_specs=tuple(vmem_specs(3)),
        scratch_shapes=[pltpu.VMEM((blks, span, LANES), F32)],
        compiler_params=pltpu.CompilerParams(vmem_limit_bytes=16 * MIB),
        name="attend_back",
    )(bounds, q, kv, kvt, d_o, o, lse)


def gelu_parts(values):
    share = 0.5 * (1.0 + lax.erf(values * (2.0**-0.5)))
    slope = share + values * jnp.exp(-0.5 * values * values) * (2.0 * math.pi) ** -0.5
    return values * share, slope


def positions(expert_rows, expert_cols, rank_row, rank_col):
    def count(mask, axis):
        return jnp.sum(mask.astype(F32), axis=axis, keepdims=True)

    row = [None, None]
    col = [None, None]
    before = rank_col < rank_row
    after = rank_row < rank_col
    for choice in range(2):
        row[choice] = count((expert_cols[choice] == expert_rows[choice]) & before, 0)
        col[choice] = count((expert_rows[choice] == expert_cols[choice]) & after, 1)
    row[1] = row[1] + count(expert_cols[0] == expert_rows[1], 0)
    col[1] = col[1] + count(expert_rows[0] == expert_cols[1], 1)
    return row, col


def own_columns(rows_ref, turned, blk, capacity):
    blks, _, slots = rows_ref.shape
    rows = jnp.concatenate(
        [rows_ref[...].reshape(blks, slots), jnp.zeros((LANES - blks, slots), F32)], axis=0
    )
    for piece in range(slots // LANES):
        columns = slice(piece * LANES, (piece + 1) * LANES)
        turned[columns, :] = jnp.transpose(rows[:, columns])
    own = turned[pl.ds(pl.multiple_of(blk * capacity, capacity), capacity), :]
    return jnp.concatenate([own[:, source : source + 1] for source in range(blks)], axis=0)


def middle_kernel(
    heads, blks,
    x_hbm, o_ref, wo_ref, routes_hbm, rank_hbm, d_out_hbm, win_hbm, wout_hbm,
    po, hidden_ref, share_ref, dh_ref, dma_all, grads_ref, rx,
    x_ref, routes_ref, rank_ref, d_out_ref, win_ref, wout_ref, rows_in, in_sem,
    o_all, dos, doa, rs, ra, dr, da, dms, acc_out, acc_row, mix, gate_rows, d_gate_rows, turned,
    o_send, o_recv, dos_send, dos_recv, r_send, r_recv,
    dr_send, dr_recv, dm_send, dm_recv, rx_send, rx_recv, g_send, g_recv, dg_send, dg_recv,
):
    head, blk, z, y = place()
    tokens, model = x_ref.shape
    capacity = 2 * tokens // blks
    slots = capacity * blks
    plane = [(k % heads, k // heads) for k in range(1, 2 * heads)]
    wanted = (
        (routes_hbm, routes_ref), (rank_hbm, rank_ref), (d_out_hbm, d_out_ref), (x_hbm, x_ref),
        (win_hbm, win_ref), (wout_hbm, wout_ref),
    )
    fetched = [
        pltpu.make_async_copy(src, dst, in_sem.at[i]) for i, (src, dst) in enumerate(wanted)
    ]
    for copy in fetched:
        copy.start()
    met = greet(
        [(around(head, kh, heads), 2 * z + around(y, ky, 2)) for kh, ky in plane]
        + [(head, around(blk, k, blks)) for k in range(1, blks)]
    )
    meet(met)

    def plane_copies(src_of, dst, send, recv):
        copies = []
        for k, (kh, ky) in enumerate(plane):
            to_head, to_y = around(head, kh, heads), around(y, ky, 2)
            copies.append(
                remote(src_of(to_y, to_head), dst, send.at[k], recv.at[k], to_head, 2 * z + to_y)
            )
        return copies

    def blk_copies(src, dst, send, recv):
        return [
            remote(
                src.at[around(blk, k, blks)], dst.at[blk],
                send.at[k], recv.at[k], head, around(blk, k, blks),
            )
            for k in range(1, blks)
        ]

    def start(copies):
        for copy in copies:
            copy.start()

    def finish(copies):
        for copy in copies:
            copy.wait()

    o_copies = plane_copies(lambda to_y, to_head: o_ref.at[to_y, to_head], o_all.at[y, head], o_send, o_recv)
    start(o_copies)
    o_all[y, head] = o_ref[y, head]

    lanes = lane_ids((tokens, LANES))
    for copy in fetched[:4]:
        copy.wait()
    e_rows = [routes_ref[i : i + 1, :].astype(F32) for i in range(2)]
    rank_row = rank_ref[...].astype(F32)
    rows_in[...] = jnp.zeros_like(rows_in)
    rows_in[0:1, :], rows_in[1:2, :], rows_in[2:3, :] = *e_rows, rank_row
    columns = jnp.transpose(rows_in[...])
    e_cols = [columns[:, 0:1], columns[:, 1:2]]
    rank_col = columns[:, 2:3]
    pos_rows, pos_cols = positions(e_rows, e_cols, rank_row, rank_col)

    def slot_of(expert, position):
        return jnp.where(position < capacity, expert * capacity + position, -1.0).astype(jnp.int32)

    slot_rows = [slot_of(e, p) for e, p in zip(e_rows, pos_rows)]
    slot_cols = [slot_of(e, p) for e, p in zip(e_cols, pos_cols)]
    slot_down = lax.broadcasted_iota(jnp.int32, (slots, tokens), 0)
    slot_across = lane_ids((tokens, slots))
    pick = [(slot_down == s).astype(BF16) for s in slot_rows]
    put = [(slot_across == s).astype(BF16) for s in slot_cols]
    pick_any = pick[0] + pick[1]
    put_any = put[0] + put[1]

    d_out = d_out_ref[...]
    dos[...] = dot(pick_any, d_out.astype(BF16)).astype(BF16).reshape(dos.shape)
    dos_copies = blk_copies(dos, doa, dos_send, dos_recv)
    start(dos_copies)
    doa[blk] = dos[blk]

    weight_out = jnp.concatenate(
        [wo_ref[(b ^ 1) * HALF : ((b ^ 1) + 1) * HALF, 0:model] for b in range(blks)], axis=0
    )
    small = wo_ref[:, model : model + LANES]
    small_across = jnp.concatenate(
        [
            jnp.transpose(small[i * LANES : (i + 1) * LANES].astype(F32))
            for i in range(model // LANES)
        ],
        axis=1,
    )
    gain = small_across[blks : blks + 1, :]

    finish(o_copies)
    low_lanes = lanes[:HALF] < HALF
    for piece in range(heads):
        columns = slice(piece * LANES, (piece + 1) * LANES)
        first, second = o_all[1, piece].astype(F32), o_all[0, piece].astype(F32)
        mix[:HALF, columns] = jnp.where(low_lanes, first, second).astype(BF16)
        swapped = pltpu.roll(jnp.where(low_lanes, second, first), HALF, 1)
        mix[HALF:, columns] = swapped.astype(BF16)
    mixed = mix[...]
    hidden = x_ref[...].astype(F32) + dot(mixed, weight_out)
    xhat, scale = centre(hidden)
    routed = (xhat * gain).astype(BF16)
    rs[...] = dot(pick_any, routed).astype(BF16).reshape(rs.shape)
    r_copies = blk_copies(rs, ra, r_send, r_recv)
    start(r_copies)
    ra[blk] = rs[blk]
    logits = jnp.where(lanes < blks, dot(routed, small), MASKED)
    powers = jnp.exp(logits - jnp.max(logits, axis=1, keepdims=True))
    probs = powers / jnp.sum(powers, axis=1, keepdims=True)
    lanes_f = lanes.astype(F32)
    hots = [lanes_f == e for e in e_cols]
    gates = [jnp.sum(jnp.where(hot, probs, 0.0), axis=1, keepdims=True) for hot in hots]
    gate_high = [g.astype(BF16).astype(F32) for g in gates]
    gate_across = jnp.transpose(
        jnp.where(lanes == 0, gate_high[0], jnp.where(lanes == 1, gates[0] - gate_high[0], 0.0))
        + jnp.where(lanes == 2, gate_high[1], jnp.where(lanes == 3, gates[1] - gate_high[1], 0.0))
    ).astype(BF16)
    by_slot = (dot(gate_across, put[0]), dot(gate_across, put[1]))
    gate_rows[blk] = by_slot[0][0:1] + by_slot[0][1:2] + by_slot[1][2:3] + by_slot[1][3:4]
    g_copies = [
        remote(
            gate_rows.at[blk], gate_rows.at[blk],
            g_send.at[k], g_recv.at[k], head, around(blk, k, blks),
        )
        for k in range(1, blks)
    ]
    start(g_copies)
    acc_out[...] = jnp.zeros_like(acc_out)
    acc_row[...] = jnp.zeros_like(acc_row)
    finish(dos_copies)
    finish(r_copies)

    out_rows = doa[...].reshape(slots, model)
    rx[head, :, 0:model] = ra[...].reshape(slots, model)
    finish(g_copies)
    gate_col = own_columns(gate_rows, turned, blk, capacity)
    rx[head, :, model : 2 * model] = (out_rows.astype(F32) * gate_col).astype(BF16)
    core = lax.rem(head, 2)
    sibling, across = head - core + 1 - core, around(head, 2, heads)

    def half_rows(source, half):
        return rx.at[source, pl.ds(half * slots // 2, slots // 2)]

    to_across = [
        remote(
            half_rows(head, half), half_rows(head, half),
            rx_send.at[1 + half], rx_recv.at[1 + half], across, blk,
        )
        for half in range(2)
    ]
    to_sibling = remote(rx.at[head], rx.at[head], rx_send.at[0], rx_recv.at[0], sibling, blk)
    forwards = [
        remote(
            half_rows(across, half), half_rows(across, half),
            rx_send.at[3 + half], rx_recv.at[3 + half], sibling, blk,
        )
        for half in range(2)
    ]
    start(to_across)
    to_sibling.start()
    half_ff = wout_ref.shape[0] // 4
    for copy in fetched[4:]:
        copy.wait()

    @pl.loop(0, 4)
    def _(chunk):
        first = pl.multiple_of(chunk * half_ff, half_ff)
        into = win_ref[:, pl.ds(first, half_ff)]
        outof = wout_ref[pl.ds(first, half_ff), :]
        act, slope = gelu_parts(dot(rx[head, :, 0:model], into))
        acc_out[...] += dot(act.astype(BF16), outof)
        d_act = dot(rx[head, :, model : 2 * model], outof, (1, 1))
        acc_row[...] += dot((slope * d_act).astype(BF16), into, (1, 1))

    result = acc_out[...].astype(BF16)
    d_gate = jnp.sum(out_rows.astype(F32) * result.astype(F32), axis=1, keepdims=True)
    dr[...] = acc_row[...].astype(BF16).reshape(dr.shape)
    dr_copies = blk_copies(dr, da, dr_send, dr_recv)
    start(dr_copies)
    da[blk] = dr[blk]
    d_wide = jnp.broadcast_to(d_gate, (slots, LANES))
    d_gate_rows[blk] = jnp.concatenate(
        [jnp.transpose(d_wide[i * LANES : (i + 1) * LANES])[0:1] for i in range(slots // LANES)],
        axis=1,
    )
    dg_copies = [
        remote(
            d_gate_rows.at[blk], d_gate_rows.at[blk],
            dg_send.at[k], dg_recv.at[k], head, around(blk, k, blks),
        )
        for k in range(1, blks)
    ]
    start(dg_copies)
    po[...] = result.reshape(blks, capacity, model)

    finish(dg_copies)
    back_gate = own_columns(d_gate_rows, turned, blk, capacity)
    back_gate = split_high_low(back_gate, lane_ids((slots, LANES)))
    d_gates = [join_high_low(dot(p, back_gate), 0) for p in put]
    d_probs = jnp.where(hots[0], d_gates[0], 0.0) + jnp.where(hots[1], d_gates[1], 0.0)
    d_logits = probs * (d_probs - jnp.sum(probs * d_probs, axis=1, keepdims=True))
    d_high = d_logits.astype(BF16)
    d_low = (d_logits - d_high.astype(F32)).astype(BF16)
    d_router_part = dot(d_high, small, (1, 1)) + dot(d_low, small, (1, 1))
    finish(dr_copies)
    d_routed = dot(put_any, da[...].reshape(slots, model)) + d_router_part
    d_hidden = d_out + centre_back(d_routed * gain, xhat, scale)
    dh_ref[...] = d_hidden
    d_attn = d_hidden.astype(BF16)
    d_mixed = dot(d_attn, weight_out, (1, 1))
    for piece in range(heads):
        block = d_mixed[:, piece * LANES : (piece + 1) * LANES]
        for to_y in range(2):
            dms[to_y, piece] = halves(block, low_lanes == (to_y == 1)).astype(BF16)
    dm_copies = plane_copies(lambda to_y, to_head: dms.at[to_y, to_head], dma_all.at[y, head], dm_send, dm_recv)
    start(dm_copies)
    dma_all[y, head] = dms[y, head]
    arrived(half_rows(across, 0), rx_recv.at[1])
    forwards[0].start()

    d_weight = dot(mixed, d_attn, (0, 0)).astype(BF16)
    for b in range(blks):
        grads_ref[b, :, 0:model] = d_weight[(b ^ 1) * HALF : ((b ^ 1) + 1) * HALF, :]
    last = (lanes == blks).astype(BF16)
    d_small = dot(routed, d_high, (0, 0)) + dot((d_routed * xhat).astype(BF16), last, (0, 0))
    grads_ref[:, :, model : model + LANES] = d_small.astype(BF16).reshape(blks, HALF, LANES)
    share = gates[0] * put[0].astype(F32) + gates[1] * put[1].astype(F32)
    share_ref[0] = share.astype(BF16)
    share_ref[1] = (share - share_ref[0].astype(F32)).astype(BF16)
    hidden_ref[...] = hidden

    arrived(half_rows(across, 1), rx_recv.at[2])
    forwards[1].start()
    finish(dm_copies)
    to_sibling.wait()
    for copy in to_across:
        copy.wait_send()
    finish(forwards)


def call_middle(x, o, wo, routes, rank, d_out, win, wout, heads, blks):
    tokens, model = x.shape
    capacity = 2 * tokens // blks
    slots = capacity * blks
    wide = model + LANES

    def rows(width):
        return pltpu.VMEM((blks, capacity, width), BF16)

    def block(*lead):
        return pltpu.VMEM((*lead, tokens // 2, LANES), BF16)

    return pl.pallas_call(
        functools.partial(middle_kernel, heads, blks),
        out_shape=(
            jax.ShapeDtypeStruct((blks, capacity, model), BF16),
            jax.ShapeDtypeStruct((tokens, model), F32),
            jax.ShapeDtypeStruct((2, tokens, slots), BF16),
            jax.ShapeDtypeStruct((tokens, model), F32),
            jax.ShapeDtypeStruct((2, heads, tokens // 2, LANES), BF16),
            jax.ShapeDtypeStruct((blks, model // blks, wide), BF16),
            jax.ShapeDtypeStruct((heads, slots, 2 * model), BF16),
        ),
        in_specs=hbm_specs(1) + vmem_specs(2) + hbm_specs(5),
        out_specs=tuple(vmem_specs(7)),
        scratch_shapes=[
            pltpu.VMEM((tokens, model), BF16),
            pltpu.VMEM((2, tokens), jnp.int32),
            pltpu.VMEM((1, tokens), jnp.int32),
            pltpu.VMEM((tokens, model), F32),
            pltpu.VMEM(win.shape, BF16),
            pltpu.VMEM(wout.shape, BF16),
            pltpu.VMEM((tokens, tokens), F32),
            dma(6),
            block(2, heads), rows(model), rows(model), rows(model), rows(model),
            rows(model), rows(model), block(2, heads),
            pltpu.VMEM((slots, model), F32), pltpu.VMEM((slots, model), F32),
            pltpu.VMEM((tokens, model), BF16),
            pltpu.VMEM((blks, 1, slots), F32), pltpu.VMEM((blks, 1, slots), F32),
            pltpu.VMEM((slots, LANES), F32),
            dma(2 * heads), dma(2 * heads), dma(blks), dma(blks), dma(blks), dma(blks),
            dma(blks), dma(blks), dma(2 * heads), dma(2 * heads), dma(5), dma(5),
            dma(blks), dma(blks), dma(blks), dma(blks),
        ],
        compiler_params=pltpu.CompilerParams(
            collective_id=2, has_side_effects=True, vmem_limit_bytes=20 * MIB
        ),
        name="experts",
    )(*in_hbm(x), o, wo, *in_hbm(routes.T, rank, d_out, win, wout))


def last_kernel(
    heads, blks,
    x_hbm, dh_ref, begun_ref, dkv_ref, xa_ref, wa_ref, w_hbm, g1_hbm, grads_ref, rx_ref, win_hbm, wout_hbm,
    po_ref, hidden_ref, share_ref, bounds_ref, q_ref, kv_ref, kvt_ref, do_ref, lse_ref, delta_ref,
    y_ref, dx_ref, dw_ref, shared_ref, din_ref, dout_ref,
    x_ref, w_ref, g1_ref, win_ref, wout_ref, in_sem,
    gain_tile, far_all, near_send_buf, near_all, pair_all, dq_all, dq_ref, dq_packed, dkv_own, pair_buf, us, ua, gs, ga, gqs, gqa, u_part, xat, pa, gh, w1, w2s, w2, w3,
    q_send, q_recv, pair_send, pair_recv, far_send, far_recv, near_send, near_recv,
    u_send, u_recv, g_send, g_recv, gh_send, gh_recv, w1_send, w1_recv, w2_send, w2_recv,
    w3_send, w3_recv, e_send, e_recv, gq_send, gq_recv, po_send, po_recv,
):
    head, blk, z, y = place()
    planes = blks // 2
    tokens, model = x_ref.shape
    rows = w_ref.shape[0]
    wanted = (
        (win_hbm, win_ref), (wout_hbm, wout_ref), (x_hbm, x_ref), (w_hbm, w_ref), (g1_hbm, g1_ref)
    )
    fetched = [
        pltpu.make_async_copy(src, dst, in_sem.at[i]) for i, (src, dst) in enumerate(wanted)
    ]
    for copy in fetched:
        copy.start()
    met = greet(
        [(around(head, k, heads), blk) for k in range(1, heads)]
        + [(head, around(blk, k, blks)) for k in range(1, blks)]
    )
    meet(met)

    def start(copies):
        for copy in copies:
            copy.start()

    def finish(copies):
        for copy in copies:
            copy.wait()

    other_y = around(y, 1, 2)
    pair = 2 * z + other_y
    above, below = z < planes - 1, z > 0
    directions = ((1, above, below, 0), (-1, below, above, 2))

    def far_copy(step, slot, side):
        span = 2 * (z + 2 * step) + side
        return remote(
            dkv_ref.at[span], far_all.at[slot + side],
            far_send.at[slot + side], far_recv.at[slot + side], head, 2 * (z + step) + y,
        )

    def near_copy(step, slot, side):
        return remote(
            near_send_buf.at[slot + side], near_all.at[slot // 2, y],
            near_send.at[slot + side], near_recv.at[slot // 2, y], head, 2 * (z + step) + side,
        )

    def two_away(step):
        return z + 2 * step < planes if step > 0 else z + 2 * step >= 0

    for step, there, back, slot in directions:

        @pl.when(two_away(step))
        def _():
            for side in range(2):
                far_copy(step, slot, side).start()

    w1_copies = [
        remote(
            grads_ref.at[:, around(head, k, heads)], w1.at[head],
            w1_send.at[k], w1_recv.at[k], around(head, k, heads), blk,
        )
        for k in range(1, heads)
    ]
    start(w1_copies)
    w1[head] = grads_ref[:, head]

    core = lax.rem(head, 2)
    sibling = head - core + 1 - core
    ff_half = wout_ref.shape[0] // 2
    ff_step = ff_half // 4

    def expert_chunk(chunk):
        here = pl.multiple_of(core * ff_half + chunk * ff_step, ff_step)
        there = pl.multiple_of(chunk * ff_step, ff_step)
        into = win_ref[:, pl.ds(here, ff_step)]
        outof = wout_ref[pl.ds(here, ff_step), :]
        d_in = jnp.zeros((model, ff_step), F32)
        d_out = jnp.zeros((ff_step, model), F32)
        for source in range(heads):
            rows_in = rx_ref[source, :, 0:model]
            grads_out = rx_ref[source, :, model : 2 * model]
            act, slope = gelu_parts(dot(rows_in, into))
            d_act = dot(grads_out, outof, (1, 1))
            d_in = d_in + dot(rows_in, (slope * d_act).astype(BF16), (0, 0))
            d_out = d_out + dot(act.astype(BF16), grads_out, (0, 0))
        din_ref[core, :, pl.ds(there, ff_step)] = d_in.astype(BF16)
        dout_ref[core, pl.ds(there, ff_step), :] = d_out.astype(BF16)

    key_tile = kv_ref.shape[1]
    for group in range(2 * key_tile // (CHAINS * QUERY_TILE)):
        tiles, queries = query_group(q_ref, group, y)
        known = (
            queries,
            group_grads(do_ref, tiles, y),
            [delta_ref[tile, 0:1, :] for tile in tiles],
            [lse_ref[tile, 0:1, :] for tile in tiles],
        )
        carry = tuple(begun_ref[tile] for tile in tiles)
        for side in range(2):
            first = pl.multiple_of((2 * z + side) * key_tile, key_tile)
            keys_across = kvt_ref[:, pl.ds(first, key_tile)]
            given, carry = attend_back(
                bounds_ref, tiles, first, kv_ref[2 * z + side], keys_across, known, carry
            )
            dkv_own[side] = given if group == 0 else dkv_own[side] + given
        for tile, total in zip(tiles, carry):
            at = tile * QUERY_TILE % key_tile
            dq_ref[tile * QUERY_TILE // key_tile, at : at + QUERY_TILE] = jnp.transpose(total)
    pair_buf[...] = dkv_own[other_y].astype(BF16)
    pair_copy = remote(pair_buf, pair_all, pair_send, pair_recv, head, pair)
    pair_copy.start()
    own_lanes = (lane_ids(dq_packed.shape) < HALF) == (y == 0)
    dq_packed[...] = halves(dq_ref[other_y], own_lanes).astype(BF16)
    q_copy = remote(dq_packed, dq_all, q_send, q_recv, head, pair)
    q_copy.start()
    finish(fetched[:2])
    weight = wa_ref[...].reshape(model, 3 * LANES)
    for piece in range(heads):
        xat[:, piece * tokens : (piece + 1) * tokens] = jnp.transpose(xa_ref[piece])
    even = y == 0

    expert_chunk(0)
    q_copy.wait()
    landed = dq_all[...].astype(F32)
    landed = jnp.concatenate([landed, pltpu.roll(landed, HALF, 1)], axis=0)
    own_lanes = (lane_ids(landed.shape) < HALF) == even
    q_grads = jnp.where(own_lanes, dq_ref[y], landed).astype(BF16)
    gqs[...] = dot(xat[...], q_grads).astype(BF16).reshape(gqs.shape)
    gq_copies = [
        remote(
            gqs.at[around(blk, k, blks)], gqa.at[blk],
            gq_send.at[k], gq_recv.at[k], head, around(blk, k, blks),
        )
        for k in range(1, blks)
    ]
    start(gq_copies)
    gqa[blk] = gqs[blk]
    u_part[...] = dot(q_grads, weight[:, 2 * LANES : 3 * LANES], (1, 1)).reshape(u_part.shape)

    for step, there, back, slot in directions:

        @pl.when(there)
        def _():
            for side in range(2):
                near_send_buf[slot + side] = dkv_ref[2 * (z + step) + side]

        @pl.when(jnp.logical_and(there, back))
        def _():
            for side in range(2):
                arrived(far_all.at[slot + side], far_recv.at[slot + side])
                near_send_buf[slot + side] = (
                    near_send_buf[slot + side].astype(F32) + far_all[slot + side].astype(F32)
                ).astype(BF16)

        @pl.when(there)
        def _():
            for side in range(2):
                near_copy(step, slot, side).start()

    finish(w1_copies)
    summed = w1[0].astype(F32)
    for source in range(1, heads):
        summed = summed + w1[source].astype(F32)
    w2s[...] = summed.astype(BF16)
    w2_copies = [
        remote(
            w2s.at[around(blk, k, blks)], w2.at[blk],
            w2_send.at[k], w2_recv.at[k], head, around(blk, k, blks),
        )
        for k in range(1, blks)
    ]
    start(w2_copies)
    w2[blk] = w2s[blk]

    @pl.loop(1, 4)
    def _(chunk):
        expert_chunk(chunk)

    e_copies = [
        remote(din_ref.at[core], din_ref.at[core], e_send.at[0], e_recv.at[0], sibling, blk),
        remote(dout_ref.at[core], dout_ref.at[core], e_send.at[1], e_recv.at[1], sibling, blk),
    ]
    start(e_copies)

    pair_copy.wait()
    for step, there, back, slot in directions:

        @pl.when(back)
        def _():
            for side in range(2):
                arrived(near_all.at[slot // 2, side], near_recv.at[slot // 2, side])

        @pl.when(jnp.logical_not(back))
        def _():
            near_all[slot // 2] = jnp.zeros(near_all.shape[1:], BF16)

    own = dkv_own[y]
    other = pair_all[...].astype(F32)
    made = jnp.concatenate(
        [
            (
                jnp.where(even == (side == 0), own, other)
                + near_all[0, side].astype(F32)
                + near_all[1, side].astype(F32)
            ).astype(BF16)
            for side in range(2)
        ],
        axis=1,
    )
    gs[...] = dot(xat[...], made).astype(BF16).reshape(gs.shape)
    g_copies = [
        remote(
            gs.at[around(blk, k, blks)], ga.at[blk],
            g_send.at[k], g_recv.at[k], head, around(blk, k, blks),
        )
        for k in range(1, blks)
    ]
    start(g_copies)
    ga[blk] = gs[blk]
    us[...] = (
        u_part[...] + dot(made, weight[:, 0 : 2 * LANES], (1, 1)).reshape(us.shape)
    ).astype(BF16)
    u_copies = [
        remote(
            us.at[around(head, k, heads)], ua.at[head],
            u_send.at[k], u_recv.at[k], around(head, k, heads), blk,
        )
        for k in range(1, heads)
    ]
    start(u_copies)
    ua[head] = us[head]
    finish(fetched[2:])
    for copy in g_copies:
        copy.wait_send()
    po_copies = [
        remote(
            po_ref.at[around(blk, k, blks)], pa.at[blk],
            po_send.at[k], po_recv.at[k], head, around(blk, k, blks),
        )
        for k in range(1, blks)
    ]
    start(po_copies)
    pa[blk] = po_ref[blk]

    finish(w2_copies)
    part = w2[0].astype(F32)
    for source in range(1, blks):
        part = part + w2[source].astype(F32)
    w3[head] = part.astype(BF16)
    w3_copies = [
        remote(w3.at[head], w3.at[head], w3_send.at[k], w3_recv.at[k], around(head, k, heads), blk)
        for k in range(1, heads)
    ]
    start(w3_copies)

    finish(u_copies)
    grad = ua[0].astype(F32)
    for source in range(1, heads):
        grad = grad + ua[source].astype(F32)
    xhat, scale = centre(x_ref[...].astype(F32))
    dx_ref[...] = dh_ref[...] + centre_back(grad, xhat, scale)

    finish(gq_copies)
    total = gqa[0].astype(F32)
    for source in range(1, blks):
        total = total + gqa[source].astype(F32)
    gh[head, :, 2 * LANES : 3 * LANES] = total.astype(BF16)
    for copy in g_copies:
        copy.wait_recv()
    total = ga[0].astype(F32)
    for source in range(1, blks):
        total = total + ga[source].astype(F32)
    gh[head, :, 0 : 2 * LANES] = total.astype(BF16)
    gh_copies = [
        remote(gh.at[head], gh.at[head], gh_send.at[k], gh_recv.at[k], around(head, k, heads), blk)
        for k in range(1, heads)
    ]
    start(gh_copies)
    finish(po_copies)
    parts = pa[...].reshape(share_ref.shape[2], model)
    mixture = dot(share_ref[0], parts) + dot(share_ref[1], parts)
    y_ref[...] = (hidden_ref[...] + mixture).astype(BF16)

    gain_tile[...] = jnp.zeros_like(gain_tile)
    gain_tile[0:1, 0:rows] = g1_ref[...].astype(F32)
    gain = jnp.transpose(jnp.broadcast_to(gain_tile[0:1, :], (LANES, LANES)))[:rows]
    low_half = lane_ids((rows, LANES)) < HALF
    finish(gh_copies)
    d_gain = jnp.zeros((rows, LANES), F32)
    for source in range(heads):
        both = [gh[source, :, i * LANES : (i + 1) * LANES].astype(F32) for i in range(3)]
        grads = (
            both[2] * HS ** (-0.5),
            jnp.where(low_half, both[0], both[1]),
            pltpu.roll(jnp.where(low_half, both[1], both[0]), HALF, 1),
        )
        for which, value in enumerate(grads):
            columns = slice(which * model + source * LANES, which * model + (source + 1) * LANES)
            d_gain = d_gain + value * w_ref[:, columns].astype(F32)
            dw_ref[:, columns] = value * gain
    finish(w3_copies)
    shared = w3[...].reshape(rows, w3.shape[-1]).astype(F32)
    shared_ref[:, 0:model] = shared[:, 0:model]
    gain_col = jnp.sum(d_gain, axis=1, keepdims=True)
    shared_ref[:, model : model + LANES] = jnp.where(
        lane_ids((rows, LANES)) == blks + 1, gain_col, shared[:, model : model + LANES]
    )
    for step, there, back, slot in directions:

        @pl.when(two_away(step))
        def _():
            for side in range(2):
                far_copy(step, slot, side).wait_send()

        @pl.when(there)
        def _():
            for side in range(2):
                near_copy(step, slot, side).wait_send()

    finish(e_copies)


def call_last(
    x, dh, dq, dkv, xa, wa, w_qkv, g1, grads, rx, win, wout, po, hidden, share,
    bounds, q, kv, kvt, d_o, lse, delta, heads, blks,
):
    tokens, model = x.shape
    span = tokens * heads
    rows = w_qkv.shape[0]
    wide = model + LANES
    part = rows // heads
    ff = wout.shape[0]

    def block(*lead):
        return pltpu.VMEM((*lead, span, LANES), BF16)

    return pl.pallas_call(
        functools.partial(last_kernel, heads, blks),
        out_shape=(
            jax.ShapeDtypeStruct((tokens, model), BF16),
            jax.ShapeDtypeStruct((tokens, model), F32),
            jax.ShapeDtypeStruct((rows, 3 * model), F32),
            jax.ShapeDtypeStruct((rows, wide), F32),
            jax.ShapeDtypeStruct((2, model, ff // 2), BF16),
            jax.ShapeDtypeStruct((2, ff // 2, model), BF16),
        ),
        in_specs=hbm_specs(1) + vmem_specs(5) + hbm_specs(2) + vmem_specs(2) + hbm_specs(2) + vmem_specs(10),
        out_specs=tuple(vmem_specs(6)),
        scratch_shapes=[
            pltpu.VMEM((tokens, model), BF16),
            pltpu.VMEM((rows, 3 * model), BF16),
            pltpu.VMEM((1, rows), BF16),
            pltpu.VMEM(win.shape, BF16),
            pltpu.VMEM(wout.shape, BF16),
            dma(5),
            pltpu.VMEM((8, LANES), F32),
            block(4), block(4), block(2, 2), block(), pltpu.VMEM((span // 2, LANES), BF16),
            pltpu.VMEM((2, span, LANES), F32), pltpu.VMEM((span // 2, LANES), BF16),
            pltpu.VMEM((2, span, LANES), F32), block(),
            pltpu.VMEM((heads, tokens, model), BF16), pltpu.VMEM((heads, tokens, model), BF16),
            pltpu.VMEM((blks, rows, 2 * LANES), BF16), pltpu.VMEM((blks, rows, 2 * LANES), BF16),
            pltpu.VMEM((blks, rows, LANES), BF16), pltpu.VMEM((blks, rows, LANES), BF16),
            pltpu.VMEM((heads, tokens, model), F32), pltpu.VMEM((model, span), BF16),
            pltpu.VMEM(po.shape, BF16),
            pltpu.VMEM((heads, rows, 3 * LANES), BF16),
            pltpu.VMEM((heads, blks, part, wide), BF16), pltpu.VMEM((blks, part, wide), BF16),
            pltpu.VMEM((blks, part, wide), BF16), pltpu.VMEM((heads, part, wide), BF16),
            pltpu.SemaphoreType.DMA, pltpu.SemaphoreType.DMA, pltpu.SemaphoreType.DMA, pltpu.SemaphoreType.DMA,
            dma(4), dma(4), dma(4), dma(2, 2),
            dma(heads), dma(heads), dma(blks), dma(blks), dma(heads), dma(heads), dma(heads), dma(heads),
            dma(blks), dma(blks), dma(heads), dma(heads), dma(2), dma(2), dma(blks), dma(blks), dma(blks), dma(blks),
        ],
        compiler_params=pltpu.CompilerParams(
            collective_id=3, has_side_effects=True, vmem_limit_bytes=24 * MIB
        ),
        name="last",
    )(
        *in_hbm(x), dh, dq, dkv, xa, wa, *in_hbm(w_qkv, g1.reshape(1, rows)),
        grads.reshape(blks, heads, part, wide), rx, *in_hbm(win, wout), po, hidden, share,
        bounds, q, kv, kvt, d_o, lse, delta,
    )


def finish_kernel(
    experts,
    y_ref, dx_ref, dw_ref, shared_ref, din_ref, dout_ref,
    y_out, dx_out, g1_out, dw_out, dwo_out, g2_out, wr_out, din_out, dout_out,
    tile, wr, g2, g1, din, dout, sem, wide_sem,
):
    rows = shared_ref.shape[0]
    model = dx_ref.shape[1]
    copies = [
        pltpu.make_async_copy(dx_ref, dx_out, sem.at[0]),
        pltpu.make_async_copy(dw_ref, dw_out, sem.at[1]),
        pltpu.make_async_copy(shared_ref.at[:, pl.ds(0, model)], dwo_out, sem.at[2]),
        pltpu.make_async_copy(y_ref, y_out, sem.at[6]),
    ]
    for copy in copies:
        copy.start()
    half = dout_ref.shape[1]
    quarter = half // 2
    for piece in range(4):
        down = slice(piece * quarter, (piece + 1) * quarter)
        dout[down, :] = dout_ref[piece // 2, (piece % 2) * quarter : (piece % 2 + 1) * quarter, :].astype(F32)
        copies.append(pltpu.make_async_copy(dout.at[down], dout_out.at[down], wide_sem.at[piece]))
        copies[-1].start()
    step = model // 4
    for piece in range(4):
        down = slice(piece * step, (piece + 1) * step)
        for side in range(2):
            din[down, side * half : (side + 1) * half] = din_ref[side, down, :].astype(F32)
        copies.append(pltpu.make_async_copy(din.at[down], din_out.at[down], wide_sem.at[4 + piece]))
        copies[-1].start()
    tile[...] = jnp.zeros_like(tile)
    tile[0:rows, :] = shared_ref[:, model : model + LANES]
    across = jnp.transpose(tile[...])[:, 0:rows]
    wr[...] = across[0:experts]
    g2[...] = across[experts : experts + 1]
    g1[...] = across[experts + 1 : experts + 2]
    for index, (src, dst) in enumerate(((wr, wr_out), (g2, g2_out), (g1, g1_out))):
        copies.append(pltpu.make_async_copy(src, dst, sem.at[3 + index]))
        copies[-1].start()
    for copy in copies:
        copy.wait()


def call_finish(output, dx, dw, shared, d_in, d_out):
    rows = shared.shape[0]
    model = dx.shape[1]
    experts = model // rows
    ff = 2 * d_out.shape[1]
    return pl.pallas_call(
        functools.partial(finish_kernel, experts),
        out_shape=(
            jax.ShapeDtypeStruct(output.shape, BF16),
            jax.ShapeDtypeStruct(dx.shape, F32),
            jax.ShapeDtypeStruct((1, rows), F32),
            jax.ShapeDtypeStruct(dw.shape, F32),
            jax.ShapeDtypeStruct((rows, model), F32),
            jax.ShapeDtypeStruct((1, rows), F32),
            jax.ShapeDtypeStruct((experts, rows), F32),
            jax.ShapeDtypeStruct((model, ff), F32),
            jax.ShapeDtypeStruct((ff, model), F32),
        ),
        in_specs=vmem_specs(6),
        out_specs=tuple(hbm_specs(9)),
        scratch_shapes=[
            pltpu.VMEM((LANES, LANES), F32),
            pltpu.VMEM((experts, rows), F32),
            pltpu.VMEM((1, rows), F32),
            pltpu.VMEM((1, rows), F32),
            pltpu.VMEM((model, ff), F32),
            pltpu.VMEM((ff, model), F32),
            dma(7),
            dma(8),
        ],
        compiler_params=pltpu.CompilerParams(vmem_limit_bytes=16 * MIB),
        name="finish",
    )(output, dx, dw, shared, d_in, d_out)


def local_kernels(
    inputs, ln1_gain, w_qkv, w_out, ln2_gain, w_router,
    expert_in, expert_out, routes, priority, doc_lengths, d_out,
):
    heads, blks = lax.axis_size("head"), lax.axis_size("blk")
    model = inputs.shape[1]
    tokens = inputs.shape[0]
    win, wout = expert_in[0], expert_out[0]
    q, kv, xa, wa, wo, kvt, bounds, begun = call_qkv(
        inputs, w_qkv, ln1_gain, w_out, w_router, ln2_gain, doc_lengths, heads, blks
    )
    o, o_low, lse = call_forward(bounds, q, kv, kvt, begun)
    po, hidden, share, dh, d_o, grads, rx = call_middle(
        inputs, o_low.reshape(2, heads, tokens // 2, LANES), wo.reshape(model, model + LANES),
        routes, priority, d_out, win, wout, heads, blks,
    )
    d_o = d_o.reshape(2 * heads * tokens // QUERY_TILE, -1, HALF, LANES)
    dq, dkv, delta = call_backward(bounds, q, kv, kvt, d_o, o, lse)
    ends = call_last(
        inputs, dh, dq, dkv, xa, wa, w_qkv, ln1_gain, grads, rx, win, wout,
        po, hidden, share, bounds, q, kv, kvt, d_o, lse, delta, heads, blks,
    )
    output, d_inputs, d_gain_one, d_qkv, d_out_proj, d_gain_two, d_router, d_in, d_out_weight = call_finish(*ends)
    return (
        output,
        d_inputs,
        d_gain_one.reshape(-1),
        d_qkv,
        d_out_proj,
        d_gain_two.reshape(-1),
        d_router.T,
        d_in[None],
        d_out_weight[None],
    )


def solution(mesh):
    in_specs = (
        P(("blk", "head"), None),
        P("blk"),
        P("blk", None),
        P("blk", None),
        P("blk"),
        P("blk", None),
        P("blk", None, None),
        P("blk", None, None),
        P(("blk", "head"), None),
        P(("blk", "head"), None),
        P(),
        P(("blk", "head"), None),
    )
    out_specs = (
        P(("blk", "head"), None),
        P(("blk", "head"), None),
        P("blk"),
        P("blk", None),
        P("blk", None),
        P("blk"),
        P("blk", None),
        P("blk", None, None),
        P("blk", None, None),
    )
    fits = mesh.shape["head"] == 4 and mesh.shape["blk"] == 8
    body = local_kernels if fits else local
    return jax.shard_map(body, mesh=mesh, in_specs=in_specs, out_specs=out_specs, check_vma=False)
```

```python
import functools
import math

import jax
import jax.numpy as jnp
from jax import lax
from jax.experimental import pallas as pl
from jax.experimental.pallas import tpu as pltpu
from jax.sharding import PartitionSpec as P

HS = 64
KEY_BLOCK = 2048


PRECISE = lax.Precision.HIGHEST
MASKED = -1e30
EPSILON = 1e-06


def layer_norm(values, gain):
    average = jnp.mean(values, axis=-1, keepdims=True)
    centred = values - average
    spread = jnp.mean(centred * centred, axis=-1, keepdims=True)
    return centred * lax.rsqrt(spread + EPSILON) * gain


def gelu_exact(values):
    return jax.nn.gelu(values, approximate=False)


def router(row_block, weight):
    return jax.nn.softmax(jnp.dot(row_block, weight, precision=PRECISE), axis=-1)


def doc_index(positions, doc_lengths):
    places = jnp.arange(doc_lengths.shape[0], dtype=jnp.int32)
    starts = jnp.sum(jnp.where(places[None, :] < places[:, None], doc_lengths[None, :], 0), axis=1)
    at_most = (starts[None, :] <= positions[:, None]).astype(jnp.int32)
    return jnp.sum(at_most, axis=1) - 1


def slot_table(route_rows, ranking, capacity):
    token_count = route_rows.shape[0]
    expert = jnp.transpose(route_rows).reshape(-1)
    pair_order = (jnp.arange(2, dtype=jnp.int32)[:, None] * token_count + ranking[None, :]).reshape(
        -1
    )
    before = (expert[:, None] == expert[None, :]) & (pair_order[None, :] < pair_order[:, None])
    position = jnp.sum(before.astype(jnp.int32), axis=1)
    slot_ids = jnp.where(position < capacity, expert * capacity + position, -1)
    return slot_ids.reshape(2, token_count)


def keep_state(current):
    return current


def local(
    inputs,
    ln1_gain,
    w_qkv,
    w_out,
    ln2_gain,
    w_router,
    expert_in,
    expert_out,
    routes,
    priority,
    doc_lengths,
    d_out,
):
    blk_size = lax.axis_size("blk")
    tok_rows = inputs.shape[0]
    model_width = inputs.shape[1]
    capacity = 2 * tok_rows // blk_size
    slot_total = blk_size * capacity
    gain_one, qkv_weight, out_weight, gain_two, router_weight = (
        lax.all_gather(ln1_gain, "blk", axis=0, tiled=True),
        lax.all_gather(w_qkv, "blk", axis=0, tiled=True),
        lax.all_gather(w_out, "blk", axis=0, tiled=True),
        lax.all_gather(ln2_gain, "blk", axis=0, tiled=True),
        lax.all_gather(w_router, "blk", axis=0, tiled=True),
    )
    input_rows = inputs.astype(jnp.float32)
    normed_one, norm_one_pull = jax.vjp(layer_norm, input_rows, gain_one.astype(jnp.float32))
    normed_low = normed_one.astype(jnp.bfloat16)
    qkv_rows = jnp.dot(normed_low, qkv_weight, preferred_element_type=jnp.float32).astype(
        jnp.bfloat16
    )
    query_heads, key_heads, value_heads = (
        lax.all_to_all(qkv_rows[:, :model_width], "head", split_axis=1, concat_axis=0, tiled=True),
        lax.all_to_all(
            qkv_rows[:, model_width : 2 * model_width],
            "head",
            split_axis=1,
            concat_axis=0,
            tiled=True,
        ),
        lax.all_to_all(
            qkv_rows[:, 2 * model_width :], "head", split_axis=1, concat_axis=0, tiled=True
        ),
    )
    span_rows = query_heads.shape[0]
    head_count = query_heads.shape[1] // HS
    key_all, value_all = (
        lax.all_gather(key_heads, "blk", axis=0, tiled=True),
        lax.all_gather(value_heads, "blk", axis=0, tiled=True),
    )
    total_rows = key_all.shape[0]
    block_count = total_rows // KEY_BLOCK
    scale_factor = HS ** (-0.5)
    query_pos = lax.axis_index("blk") * span_rows + jnp.arange(span_rows, dtype=jnp.int32)
    query_docs = doc_index(query_pos, doc_lengths)
    queries = query_heads.reshape(span_rows, head_count, HS)

    def block_parts(block_index, key_source, value_source):
        first_key = block_index * KEY_BLOCK
        key_rows = lax.dynamic_slice_in_dim(key_source, first_key, KEY_BLOCK, 0).reshape(
            KEY_BLOCK, head_count, HS
        )
        value_rows = lax.dynamic_slice_in_dim(value_source, first_key, KEY_BLOCK, 0).reshape(
            KEY_BLOCK, head_count, HS
        )
        key_docs = doc_index(first_key + jnp.arange(KEY_BLOCK, dtype=jnp.int32), doc_lengths)
        is_live = (key_docs[0] <= query_docs[-1]) & (key_docs[-1] >= query_docs[0])
        same_doc = query_docs[:, None] == key_docs[None, :]
        return (first_key, key_rows, value_rows, same_doc, is_live)

    def block_scores(key_rows, same_doc):
        raw_scores = (
            jnp.einsum("qhd,khd->hqk", queries, key_rows, preferred_element_type=jnp.float32)
            * scale_factor
        )
        return jnp.where(same_doc[None], raw_scores, MASKED)

    def stat_step(block_index, loop_state):
        first_key, key_rows, value_rows, same_doc, is_live = block_parts(
            block_index, key_all, value_all
        )

        def stat_update(current):
            running_max, running_sum = current
            scores = block_scores(key_rows, same_doc)
            new_max = jnp.maximum(running_max, jnp.max(scores, axis=2))
            exp_terms = jnp.where(same_doc[None], jnp.exp(scores - new_max[:, :, None]), 0.0)
            return (
                new_max,
                running_sum * jnp.exp(running_max - new_max) + jnp.sum(exp_terms, axis=2),
            )

        return lax.cond(is_live, stat_update, keep_state, loop_state)

    start_state = (
        jnp.full((head_count, span_rows), MASKED, jnp.float32),
        jnp.zeros((head_count, span_rows), jnp.float32),
    )
    running_max, running_sum = lax.fori_loop(0, block_count, stat_step, start_state)
    log_total = running_max + jnp.log(running_sum)

    def out_step(block_index, loop_state):
        first_key, key_rows, value_rows, same_doc, is_live = block_parts(
            block_index, key_all, value_all
        )

        def out_update(current):
            scores = block_scores(key_rows, same_doc)
            weights = jnp.where(
                same_doc[None], jnp.exp(scores - log_total[:, :, None]), 0.0
            ).astype(jnp.bfloat16)
            return current + jnp.einsum(
                "hqk,khd->qhd", weights, value_rows, preferred_element_type=jnp.float32
            )

        return lax.cond(is_live, out_update, keep_state, loop_state)

    mixed_full = lax.fori_loop(
        0, block_count, out_step, jnp.zeros((span_rows, head_count, HS), jnp.float32)
    )
    mixed_low = mixed_full.reshape(span_rows, head_count * HS).astype(jnp.bfloat16)
    mixed_tokens = lax.all_to_all(mixed_low, "head", split_axis=0, concat_axis=1, tiled=True)
    attended = jnp.dot(mixed_tokens, out_weight, preferred_element_type=jnp.float32)
    hidden_one = input_rows + attended
    normed_two, norm_two_pull = jax.vjp(layer_norm, hidden_one, gain_two.astype(jnp.float32))
    routed_low = normed_two.astype(jnp.bfloat16)
    router_probs, router_pull = jax.vjp(
        router, routed_low.astype(jnp.float32), router_weight.astype(jnp.float32)
    )
    slot_ids = slot_table(routes, priority[0], capacity)
    select = (
        slot_ids[:, :, None] == jnp.arange(slot_total, dtype=jnp.int32)[None, None, :]
    ).astype(jnp.bfloat16)
    send_rows = jnp.einsum(
        "kts,td->sd", select, routed_low, preferred_element_type=jnp.float32
    ).astype(jnp.bfloat16)
    expert_rows = lax.all_to_all(
        send_rows.reshape(blk_size, capacity, model_width),
        "blk",
        split_axis=0,
        concat_axis=0,
        tiled=True,
    ).reshape(slot_total, model_width)
    weight_in = expert_in[0]
    weight_out = expert_out[0]
    pre_act = jnp.dot(expert_rows, weight_in, preferred_element_type=jnp.float32)
    hidden_act, gelu_pull = jax.vjp(gelu_exact, pre_act)
    hidden_low = hidden_act.astype(jnp.bfloat16)
    expert_result = jnp.dot(hidden_low, weight_out, preferred_element_type=jnp.float32).astype(
        jnp.bfloat16
    )
    slot_result = lax.all_to_all(
        expert_result.reshape(blk_size, capacity, model_width),
        "blk",
        split_axis=0,
        concat_axis=0,
        tiled=True,
    ).reshape(slot_total, model_width)
    pair_result = jnp.einsum("kts,sd->ktd", select, slot_result, preferred_element_type=jnp.float32)
    route_hot = (routes[:, :, None] == jnp.arange(blk_size, dtype=jnp.int32)[None, None, :]).astype(
        jnp.float32
    )
    gate_vals = jnp.sum(router_probs[:, None, :] * route_hot, axis=2)
    mixture = gate_vals[:, 0, None] * pair_result[0] + gate_vals[:, 1, None] * pair_result[1]
    output = (hidden_one + mixture).astype(jnp.bfloat16)
    d_gates = jnp.transpose(jnp.sum(d_out[None] * pair_result, axis=2))
    d_probs = jnp.sum(d_gates[:, :, None] * route_hot, axis=1)
    pair_grads = (jnp.transpose(gate_vals)[:, :, None] * d_out[None]).astype(jnp.bfloat16)
    slot_grads = jnp.einsum(
        "kts,ktd->sd", select, pair_grads, preferred_element_type=jnp.float32
    ).astype(jnp.bfloat16)
    result_grads = lax.all_to_all(
        slot_grads.reshape(blk_size, capacity, model_width),
        "blk",
        split_axis=0,
        concat_axis=0,
        tiled=True,
    ).reshape(slot_total, model_width)
    d_hidden_act = jnp.dot(result_grads, weight_out.T, preferred_element_type=jnp.float32)
    d_weight_out = jnp.dot(hidden_low.T, result_grads, preferred_element_type=jnp.float32)
    d_preact = gelu_pull(d_hidden_act)[0].astype(jnp.bfloat16)
    d_weight_in = jnp.dot(expert_rows.T, d_preact, preferred_element_type=jnp.float32)
    row_grads = jnp.dot(d_preact, weight_in.T, preferred_element_type=jnp.float32).astype(
        jnp.bfloat16
    )
    slot_back = lax.all_to_all(
        row_grads.reshape(blk_size, capacity, model_width),
        "blk",
        split_axis=0,
        concat_axis=0,
        tiled=True,
    ).reshape(slot_total, model_width)
    d_routed = jnp.einsum("kts,sd->td", select, slot_back, preferred_element_type=jnp.float32)
    d_routed_router, d_router = router_pull(d_probs)
    d_hidden_norm, d_gain_two = norm_two_pull(d_routed + d_routed_router)
    d_hidden_one = d_out + d_hidden_norm
    attn_grads = d_hidden_one.astype(jnp.bfloat16)
    d_out_weight = jnp.dot(mixed_tokens.T, attn_grads, preferred_element_type=jnp.float32)
    mixed_grads = jnp.dot(attn_grads, out_weight.T, preferred_element_type=jnp.float32).astype(
        jnp.bfloat16
    )
    head_grads = lax.all_to_all(mixed_grads, "head", split_axis=1, concat_axis=0, tiled=True)
    out_grads = head_grads.reshape(span_rows, head_count, HS)
    row_delta = jnp.transpose(jnp.sum(out_grads.astype(jnp.float32) * mixed_full, axis=2))
    key_back, value_back = (
        lax.all_gather(key_heads, "blk", axis=0, tiled=True),
        lax.all_gather(value_heads, "blk", axis=0, tiled=True),
    )

    def grad_step(block_index, loop_state):
        first_key, key_rows, value_rows, same_doc, is_live = block_parts(
            block_index, key_back, value_back
        )

        def grad_update(current):
            query_grad, key_grad, value_grad = current
            scores = block_scores(key_rows, same_doc)
            weights = jnp.where(same_doc[None], jnp.exp(scores - log_total[:, :, None]), 0.0)
            value_part = jnp.einsum(
                "hqk,qhd->khd",
                weights.astype(jnp.bfloat16),
                out_grads,
                preferred_element_type=jnp.float32,
            )
            weight_grads = jnp.einsum(
                "qhd,khd->hqk", out_grads, value_rows, preferred_element_type=jnp.float32
            )
            score_grads = (weights * (weight_grads - row_delta[:, :, None])).astype(jnp.bfloat16)
            query_grad = (
                query_grad
                + jnp.einsum(
                    "hqk,khd->qhd", score_grads, key_rows, preferred_element_type=jnp.float32
                )
                * scale_factor
            )
            key_part = (
                jnp.einsum("hqk,qhd->khd", score_grads, queries, preferred_element_type=jnp.float32)
                * scale_factor
            )
            key_grad = lax.dynamic_update_slice_in_dim(
                key_grad, key_part.reshape(KEY_BLOCK, head_count * HS), first_key, 0
            )
            value_grad = lax.dynamic_update_slice_in_dim(
                value_grad, value_part.reshape(KEY_BLOCK, head_count * HS), first_key, 0
            )
            return (query_grad, key_grad, value_grad)

        return lax.cond(is_live, grad_update, keep_state, loop_state)

    start_grads = (
        jnp.zeros((span_rows, head_count, HS), jnp.float32),
        jnp.zeros((total_rows, head_count * HS), jnp.float32),
        jnp.zeros((total_rows, head_count * HS), jnp.float32),
    )
    query_grad, key_grad, value_grad = lax.fori_loop(0, block_count, grad_step, start_grads)
    key_own, value_own = (
        lax.psum_scatter(
            key_grad.astype(jnp.bfloat16), "blk", scatter_dimension=0, tiled=True
        ).astype(jnp.float32),
        lax.psum_scatter(
            value_grad.astype(jnp.bfloat16), "blk", scatter_dimension=0, tiled=True
        ).astype(jnp.float32),
    )
    query_tokens_grad, key_tokens_grad, value_tokens_grad = (
        lax.all_to_all(
            query_grad.reshape(span_rows, head_count * HS).astype(jnp.bfloat16),
            "head",
            split_axis=0,
            concat_axis=1,
            tiled=True,
        ),
        lax.all_to_all(
            key_own.astype(jnp.bfloat16), "head", split_axis=0, concat_axis=1, tiled=True
        ),
        lax.all_to_all(
            value_own.astype(jnp.bfloat16), "head", split_axis=0, concat_axis=1, tiled=True
        ),
    )
    qkv_grads = jnp.concatenate([query_tokens_grad, key_tokens_grad, value_tokens_grad], axis=1)
    d_qkv_weight = jnp.dot(normed_low.T, qkv_grads, preferred_element_type=jnp.float32)
    normed_grads = jnp.dot(qkv_grads, qkv_weight.T, preferred_element_type=jnp.float32)
    d_inputs_norm, d_gain_one = norm_one_pull(normed_grads)
    d_inputs = d_hidden_one + d_inputs_norm
    gain_one_sum, qkv_sum, out_sum, gain_two_sum, router_sum = (
        lax.psum_scatter(
            d_gain_one.astype(jnp.bfloat16), "blk", scatter_dimension=0, tiled=True
        ).astype(jnp.float32),
        lax.psum_scatter(
            d_qkv_weight.astype(jnp.bfloat16), "blk", scatter_dimension=0, tiled=True
        ).astype(jnp.float32),
        lax.psum_scatter(
            d_out_weight.astype(jnp.bfloat16), "blk", scatter_dimension=0, tiled=True
        ).astype(jnp.float32),
        lax.psum_scatter(
            d_gain_two.astype(jnp.bfloat16), "blk", scatter_dimension=0, tiled=True
        ).astype(jnp.float32),
        lax.psum_scatter(
            d_router.astype(jnp.bfloat16), "blk", scatter_dimension=0, tiled=True
        ).astype(jnp.float32),
    )
    gain_one_all, qkv_all, out_all, gain_two_all, router_all, expert_in_all, expert_out_all = (
        lax.psum(gain_one_sum.astype(jnp.bfloat16), "head").astype(jnp.float32),
        lax.psum(qkv_sum.astype(jnp.bfloat16), "head").astype(jnp.float32),
        lax.psum(out_sum.astype(jnp.bfloat16), "head").astype(jnp.float32),
        lax.psum(gain_two_sum.astype(jnp.bfloat16), "head").astype(jnp.float32),
        lax.psum(router_sum.astype(jnp.bfloat16), "head").astype(jnp.float32),
        lax.psum(d_weight_in[None].astype(jnp.bfloat16), "head").astype(jnp.float32),
        lax.psum(d_weight_out[None].astype(jnp.bfloat16), "head").astype(jnp.float32),
    )
    return (
        output,
        d_inputs,
        gain_one_all,
        qkv_all,
        out_all,
        gain_two_all,
        router_all,
        expert_in_all,
        expert_out_all,
    )


MESH = pl.DeviceIdType.MESH
LANES = 128
HALF = LANES // 2
MIB = 2**20
F32 = jnp.float32
BF16 = jnp.bfloat16


def dot(left, right, dims=(1, 0)):
    return lax.dot_general(
        left, right, (((dims[0],), (dims[1],)), ((), ())), preferred_element_type=F32
    )


def remote(src, dst, send_sem, recv_sem, head, blk):
    return pltpu.make_async_remote_copy(
        src_ref=src,
        dst_ref=dst,
        send_sem=send_sem,
        recv_sem=recv_sem,
        device_id={"head": head, "blk": blk},
        device_id_type=MESH,
    )


def arrived(ref, sem):
    pltpu.make_async_copy(ref, ref, sem).wait()


def greet(peers):
    barrier = pltpu.get_barrier_semaphore()
    for head, blk in peers:
        pl.semaphore_signal(
            barrier, inc=1, device_id={"head": head, "blk": blk}, device_id_type=MESH
        )
    return len(peers)


def meet(count):
    pl.semaphore_wait(pltpu.get_barrier_semaphore(), count)


def halves(values, lanes_kept):
    rows = values.shape[0] // 2
    moved = pltpu.roll(values[rows:], HALF, 1)
    return jnp.where(lanes_kept, values[:rows], moved)


def lane_ids(shape):
    return lax.broadcasted_iota(jnp.int32, shape, len(shape) - 1)


def centre(values):
    average = jnp.mean(values, axis=-1, keepdims=True)
    centred = values - average
    spread = jnp.mean(centred * centred, axis=-1, keepdims=True)
    scale = lax.rsqrt(spread + EPSILON)
    return centred * scale, scale


def centre_back(grad, xhat, scale):
    middle = jnp.mean(grad, axis=-1, keepdims=True)
    along = jnp.mean(grad * xhat, axis=-1, keepdims=True)
    return (grad - middle - xhat * along) * scale


def split_high_low(column, lanes):
    high = column.astype(BF16)
    low = (column - high.astype(F32)).astype(BF16)
    return jnp.where(lanes < HALF, high.astype(F32), low.astype(F32)).astype(BF16)


def join_high_low(matrix, start):
    return matrix[:, start : start + 1].astype(F32) + matrix[
        :, start + HALF : start + HALF + 1
    ].astype(F32)


def place():
    head, blk = lax.axis_index("head"), lax.axis_index("blk")
    return head, blk, blk // 2, lax.rem(blk, 2)


def around(index, step, size):
    return lax.rem(index + step, size)


QUERY_TILE = 256
CHAINS = 2


def masked_queries(q_ref, tile, key_lanes, query_tile):
    tiles_per_span = q_ref.shape[1] // query_tile
    inner = tile % tiles_per_span * query_tile
    query = q_ref[tile // tiles_per_span, inner : inner + query_tile, :]
    return jnp.where(key_lanes, query, jnp.zeros_like(query))


def group_blocks(bounds_ref, group, size, key_tile):
    first, last = group * size, (group + 1) * size
    low = jnp.min(bounds_ref[0:1, first : first + LANES])
    high = jnp.max(bounds_ref[1:2, last - LANES : last])
    return low // key_tile, (high + key_tile - 1) // key_tile


def inside_document(bounds_ref, tile, first, shape):
    key = first + lax.broadcasted_iota(jnp.int32, shape, 0)
    columns = slice(tile * shape[1], (tile + 1) * shape[1])
    return jnp.logical_and(key >= bounds_ref[0:1, columns], key < bounds_ref[1:2, columns])


def query_group(q_ref, group, y):
    key_lanes = (lane_ids((QUERY_TILE, LANES)) < HALF) == (y == 0)
    tiles = range(group * CHAINS, (group + 1) * CHAINS)
    return tiles, [masked_queries(q_ref, tile, key_lanes, QUERY_TILE) for tile in tiles]


def attend(bounds_ref, tiles, first, keys, keys_across, queries, carry):
    scores = [dot(keys, query, (1, 1)) for query in queries]
    made = []
    for tile, score, (biggest, weight, mixed) in zip(tiles, scores, carry):
        inside = inside_document(bounds_ref, tile, first, score.shape)
        score = jnp.where(inside, score, MASKED)
        bigger = jnp.maximum(biggest, jnp.max(score, axis=0, keepdims=True))
        fade = jnp.exp(biggest - bigger)
        terms = jnp.exp(score - bigger)
        weight = weight * fade + jnp.sum(terms, axis=0, keepdims=True)
        made.append((bigger, weight, mixed * fade + dot(keys_across, terms.astype(BF16))))
    return tuple(made)


def nothing_attended():
    return (
        jnp.full((1, QUERY_TILE), MASKED, F32),
        jnp.zeros((1, QUERY_TILE), F32),
        jnp.zeros((LANES, QUERY_TILE), F32),
    )


def attend_back(bounds_ref, tiles, first, keys, keys_across, group, carry):
    queries, out_grads, deltas, log_totals = group
    scores = [dot(keys, query, (1, 1)) for query in queries]
    weight_grads = [dot(keys, out_grad, (1, 1)) for out_grad in out_grads]
    pieces, score_grads = [], []
    for i, tile in enumerate(tiles):
        inside = inside_document(bounds_ref, tile, first, scores[i].shape)
        weights = jnp.exp(jnp.where(inside, scores[i], MASKED) - log_totals[i])
        score_grads.append((weights * (weight_grads[i] - deltas[i])).astype(BF16))
        pieces.append(weights.astype(BF16))
    wide = jnp.concatenate(score_grads + pieces, axis=1)
    given = dot(wide, jnp.concatenate(queries + out_grads, axis=0))
    return given, tuple(c + dot(keys_across, g) for c, g in zip(carry, score_grads))


def group_grads(do_ref, tiles, y):
    key_lanes = (lane_ids((QUERY_TILE, LANES)) < HALF) == (y == 0)
    out_grads = []
    for tile in tiles:
        parts = []
        for part in range(QUERY_TILE // LANES):
            packed = do_ref[tile, part].astype(F32)
            parts += [packed, pltpu.roll(packed, HALF, 1)]
        out_grads.append(jnp.where(key_lanes, 0.0, jnp.concatenate(parts, axis=0)).astype(BF16))
    return out_grads


def qkv_kernel(
    heads, blks,
    x_hbm, w_hbm, g1_hbm, wo_hbm, wr_hbm, g2_hbm, docs_hbm,
    qall, kvall, xall, wall, wo_all, kvt, bounds, begun,
    x_ref, w_ref, rows_in, g1_ref, g2_ref, wr_ref, docs_ref, wo_own, kv_other, q_packed, q_landed, in_sem,
    x_send, x_recv, w_send, w_recv, o_send, o_recv, p_send, p_recv,
    k_send, k_recv, q_recv,
):
    head, blk, z, y = place()
    planes = blks // 2
    model = x_ref.shape[1]
    rows = w_ref.shape[0]
    part = rows // heads
    experts = wr_ref.shape[0]
    wanted = (
        (w_hbm, w_ref), (g1_hbm, g1_ref), (g2_hbm, g2_ref), (wr_hbm, wr_ref), (x_hbm, x_ref),
        (wo_hbm, wo_own.at[:, pl.ds(0, model)]), (docs_hbm, docs_ref),
    )
    fetched = [
        pltpu.make_async_copy(src, dst, in_sem.at[i]) for i, (src, dst) in enumerate(wanted)
    ]
    for copy in fetched:
        copy.start()
    rows_in[...] = jnp.zeros_like(rows_in)
    met = greet(
        [(around(head, k, heads), blk) for k in range(1, heads)]
        + [(head, around(blk, k, blks)) for k in range(1, blks)]
    )
    lanes = lane_ids((rows, LANES))
    for copy in fetched:
        copy.wait()
    rows_in[0:experts, 0:rows] = wr_ref[...].astype(F32)
    rows_in[experts : experts + 1, 0:rows] = g2_ref[...].astype(F32)
    rows_in[experts + 1 : experts + 2, 0:rows] = g1_ref[...].astype(F32)
    vectors = jnp.transpose(rows_in[...])[:rows]
    gain = vectors[:, experts + 1 : experts + 2]

    def columns(which):
        start = pl.multiple_of(which * model + head * LANES, LANES)
        return w_ref[:, pl.ds(start, LANES)].astype(F32) * gain

    key_cols = columns(1)
    value_cols = pltpu.roll(columns(2), HALF, 1)
    wall[blk, :, 0:LANES] = jnp.where(lanes < HALF, key_cols, value_cols).astype(BF16)
    wall[blk, :, LANES : 2 * LANES] = jnp.where(lanes < HALF, value_cols, key_cols).astype(BF16)
    wall[blk, :, 2 * LANES : 3 * LANES] = (columns(0) * HS ** (-0.5)).astype(BF16)
    w_copies = [
        remote(wall.at[blk], wall.at[blk], w_send.at[k], w_recv.at[k], head, around(blk, k, blks))
        for k in range(1, blks)
    ]
    xhat, _ = centre(x_ref[...].astype(F32))
    xall[head] = xhat.astype(BF16)
    meet(met)
    for copy in w_copies:
        copy.start()
    x_copies = [
        remote(xall.at[head], xall.at[head], x_send.at[k], x_recv.at[k], around(head, k, heads), blk)
        for k in range(1, heads)
    ]
    for copy in x_copies:
        copy.start()
    wo_own[:, model : model + LANES] = vectors.astype(BF16)
    wo_all[blk, head] = wo_own[pl.ds(pl.multiple_of(head * part, part), part), :]
    o_copies = [
        remote(
            wo_all.at[blk, head], wo_all.at[blk, head],
            o_send.at[k], o_recv.at[k], head, around(blk, k, blks),
        )
        for k in range(1, blks)
    ]
    document_bounds(docs_ref, bounds, z)
    for copy in w_copies:
        copy.wait_send()
    for copy in o_copies:
        copy.start()
    for copy in x_copies:
        copy.wait()
    for copy in w_copies:
        copy.wait_recv()
    weight = wall[...].reshape(model, 3 * LANES)
    tokens = x_ref.shape[0]
    even = y == 0
    above, below = z < planes - 1, z > 0
    half_span = kvall.shape[1] // 2
    sides = ((1, above, below, 0), (-1, below, above, 4))

    def half_of(ref, half):
        return ref.at[pl.ds(half * half_span, half_span)]

    def outward(slot, step, across, half):
        target = 2 * (z + step) + around(y, across, 2)
        return remote(
            half_of(kv_other if across else kvall.at[blk], half), half_of(kvall.at[blk], half),
            k_send.at[slot], k_recv.at[blk, half], head, target,
        )

    def onward(slot, step, side, half):
        from_span = 2 * (z - step) + side
        ref = half_of(kvall.at[from_span], half)
        return remote(ref, ref, k_send.at[slot], k_recv.at[from_span, half], head, 2 * (z + step) + y)

    def await_half(span, half):
        arrived(half_of(kvall.at[span], half), k_recv.at[span, half])

    def turn(span):
        size = kvall.shape[1]
        kvt[:, pl.ds(pl.multiple_of(span * size, size), size)] = jnp.transpose(kvall[span])

    for half in range(2):
        for piece in range(half * heads // 2, (half + 1) * heads // 2):
            made = dot(xall[piece], weight).astype(BF16)
            first, second = made[:, 0:LANES], made[:, LANES : 2 * LANES]
            span = slice(piece * tokens, (piece + 1) * tokens)
            kvall[blk, span, :] = jnp.where(even, first, second)
            kv_other[span, :] = jnp.where(even, second, first)
            qall[y, span, :] = made[:, 2 * LANES : 3 * LANES]
        outward(8 + half, 0, 1, half).start()
        for step, there, _, slot in sides:

            @pl.when(there)
            def _():
                outward(slot + 2 * half, step, 0, half).start()
                outward(slot + 2 * half + 1, step, 1, half).start()

    other_y = around(y, 1, 2)
    kept = (lane_ids(q_packed.shape) < HALF) == (y == 1)
    q_packed[...] = halves(qall[y].astype(F32), kept).astype(BF16)
    q_pair = remote(q_packed, q_landed, k_send.at[10], q_recv, head, 2 * z + other_y)
    q_pair.start()
    turn(blk)
    for copy in o_copies:
        copy.wait()
    core = lax.rem(head, 2)
    sibling, across = head - core + 1 - core, around(head, 2, heads)

    def quarter_copy(index, quarter, to_head):
        ref = wo_all.at[:, quarter]
        return remote(ref, ref, p_send.at[index], p_recv.at[index], to_head, blk)

    p_copies = [quarter_copy(0, head, sibling), quarter_copy(1, head, across)]
    for copy in p_copies:
        copy.start()
    p_copies.append(quarter_copy(2, across, sibling))
    for half in range(2):
        for step, there, back, slot in sides:

            @pl.when(back)
            def _():
                for side in range(2):
                    await_half(2 * (z - step) + side, half)

            @pl.when(jnp.logical_and(there, back))
            def _():
                for side in range(2):
                    onward(11 + slot + 2 * half + side, step, side, half).start()

    arrived(wo_all.at[:, across], p_recv.at[1])
    p_copies[2].start()
    pair = 2 * z + other_y
    for half in range(2):
        await_half(pair, half)
    turn(pair)
    q_pair.wait()
    landed = q_landed[...]
    qall[other_y, 0:half_span, :] = landed
    qall[other_y, half_span : 2 * half_span, :] = pltpu.roll(landed.astype(F32), HALF, 1).astype(BF16)
    key_tile = kvall.shape[1]
    for group in range(2 * key_tile // (CHAINS * QUERY_TILE)):
        tiles, queries = query_group(qall, group, y)
        carry = (nothing_attended(),) * CHAINS
        for side in range(2):
            first = pl.multiple_of((2 * z + side) * key_tile, key_tile)
            keys_across = kvt[:, pl.ds(first, key_tile)]
            carry = attend(bounds, tiles, first, kvall[2 * z + side], keys_across, queries, carry)
        for tile, (biggest, weight, mixed) in zip(tiles, carry):
            begun[tile, 0:LANES] = mixed
            begun[tile, LANES : LANES + 8] = jnp.broadcast_to(biggest, (8, QUERY_TILE))
            begun[tile, LANES + 8 : LANES + 16] = jnp.broadcast_to(weight, (8, QUERY_TILE))
    for step, there, back, slot in sides:

        @pl.when(back)
        def _():
            for side in range(2):
                turn(2 * (z - step) + side)

    for other in range(planes):
        for side in range(2):
            span = 2 * other + side

            @pl.when(jnp.logical_or(z - other == 2, other - z == 2))
            def _():
                for half in range(2):
                    await_half(span, half)
                turn(span)

    for index, quarter in ((0, sibling), (2, around(sibling, 2, heads))):
        arrived(wo_all.at[:, quarter], p_recv.at[index])
    for copy in p_copies:
        copy.wait_send()
    for half in range(2):
        outward(8 + half, 0, 1, half).wait_send()
        for step, there, back, slot in sides:

            @pl.when(there)
            def _():
                outward(slot + 2 * half, step, 0, half).wait_send()
                outward(slot + 2 * half + 1, step, 1, half).wait_send()

            @pl.when(jnp.logical_and(there, back))
            def _():
                for side in range(2):
                    onward(11 + slot + 2 * half + side, step, side, half).wait_send()


def document_bounds(docs_ref, bounds, z):
    count = docs_ref.shape[1]
    lengths = docs_ref[...].astype(F32)
    doc = lax.broadcasted_iota(jnp.int32, (count, count), 0)
    other = lane_ids((count, count))
    start = jnp.sum(jnp.where(other < doc, lengths, 0.0), axis=1, keepdims=True)
    end = jnp.sum(jnp.where(other <= doc, lengths, 0.0), axis=1, keepdims=True)
    queries = bounds.shape[1]
    token = (z * queries + lane_ids((count, queries))).astype(F32)
    begun = start <= token
    bounds[...] = jnp.zeros_like(bounds)
    bounds[0:1, :] = jnp.max(jnp.where(begun, start, 0.0), axis=0, keepdims=True).astype(jnp.int32)
    bounds[1:2, :] = jnp.max(jnp.where(begun, end, 0.0), axis=0, keepdims=True).astype(jnp.int32)


def vmem_specs(count):
    return [pl.BlockSpec(memory_space=pltpu.VMEM)] * count


def hbm_specs(count):
    return [pl.BlockSpec(memory_space=pltpu.HBM)] * count


def in_hbm(*arrays):
    return [pltpu.with_memory_space_constraint(array, pltpu.HBM) for array in arrays]


def dma(*shape):
    return pltpu.SemaphoreType.DMA(shape)


def call_qkv(x, w_qkv, g1, w_out, w_router, g2, doc_lengths, heads, blks):
    tokens, model = x.shape
    rows = w_qkv.shape[0]
    span = tokens * heads
    wide = model + LANES
    part = rows // heads
    return pl.pallas_call(
        functools.partial(qkv_kernel, heads, blks),
        out_shape=(
            jax.ShapeDtypeStruct((2, span, LANES), BF16),
            jax.ShapeDtypeStruct((blks, span, LANES), BF16),
            jax.ShapeDtypeStruct((heads, tokens, model), BF16),
            jax.ShapeDtypeStruct((blks, rows, 3 * LANES), BF16),
            jax.ShapeDtypeStruct((blks, heads, part, wide), BF16),
            jax.ShapeDtypeStruct((LANES, blks * span), BF16),
            jax.ShapeDtypeStruct((8, 2 * span), jnp.int32),
            jax.ShapeDtypeStruct((2 * span // QUERY_TILE, LANES + 16, QUERY_TILE), F32),
        ),
        in_specs=hbm_specs(7),
        out_specs=tuple(vmem_specs(8)),
        scratch_shapes=[
            pltpu.VMEM((tokens, model), BF16),
            pltpu.VMEM((rows, 3 * model), BF16),
            pltpu.VMEM((LANES, LANES), F32),
            pltpu.VMEM((1, rows), BF16),
            pltpu.VMEM((1, rows), BF16),
            pltpu.VMEM((w_router.shape[1], rows), BF16),
            pltpu.VMEM((1, doc_lengths.shape[0]), jnp.int32),
            pltpu.VMEM((rows, wide), BF16),
            pltpu.VMEM((span, LANES), BF16),
            pltpu.VMEM((span // 2, LANES), BF16),
            pltpu.VMEM((span // 2, LANES), BF16),
            dma(7),
            dma(heads), dma(heads), dma(blks), dma(blks), dma(blks), dma(blks), dma(heads), dma(heads),
            dma(19), dma(blks, 2), pltpu.SemaphoreType.DMA,
        ],
        compiler_params=pltpu.CompilerParams(
            collective_id=1, has_side_effects=True, vmem_limit_bytes=16 * MIB
        ),
        name="qkv",
    )(
        *in_hbm(
            x, w_qkv, g1.reshape(1, rows), w_out, w_router.T, g2.reshape(1, rows),
            doc_lengths.reshape(1, -1),
        )
    )


def other_blocks(bounds_ref, group, key_tile, z, step, carry):
    low, high = group_blocks(bounds_ref, group, CHAINS * QUERY_TILE, key_tile)
    carry = lax.fori_loop(low, 2 * z, step, carry)
    return lax.fori_loop(2 * z + 2, high, step, carry)


def forward_kernel(bounds_ref, q_ref, kv_ref, kvt_ref, begun_ref, o_out, ob_out, lse_out):
    _, _, z, y = place()
    key_tile = kv_ref.shape[1]
    value_lanes = (lane_ids((HALF, LANES)) < HALF) == (y == 1)
    for group in range(q_ref.shape[0] * q_ref.shape[1] // (CHAINS * QUERY_TILE)):
        tiles, queries = query_group(q_ref, group, y)

        def step(block, carry, queries=queries, tiles=tiles):
            first = pl.multiple_of(block * key_tile, key_tile)
            across = kvt_ref[:, pl.ds(first, key_tile)]
            return attend(bounds_ref, tiles, first, kv_ref[block], across, queries, carry)

        start = tuple(
            (begun_ref[t, LANES : LANES + 1], begun_ref[t, LANES + 8 : LANES + 9], begun_ref[t, 0:LANES])
            for t in tiles
        )
        ends = other_blocks(bounds_ref, group, key_tile, z, step, start)
        for tile, (biggest, weight, mixed) in zip(tiles, ends):
            result = jnp.transpose(mixed / weight)
            o_out[tile] = result
            for part in range(QUERY_TILE // LANES):
                block = result[part * LANES : (part + 1) * LANES]
                ob_out[tile, part] = halves(block, value_lanes).astype(BF16)
            lse_out[tile] = jnp.broadcast_to(biggest + jnp.log(weight), (8, QUERY_TILE))


def call_forward(bounds, q, kv, kvt, begun):
    blks, span, _ = kv.shape
    tiles = 2 * span // QUERY_TILE
    return pl.pallas_call(
        forward_kernel,
        out_shape=(
            jax.ShapeDtypeStruct((tiles, QUERY_TILE, LANES), F32),
            jax.ShapeDtypeStruct((tiles, QUERY_TILE // LANES, HALF, LANES), BF16),
            jax.ShapeDtypeStruct((tiles, 8, QUERY_TILE), F32),
        ),
        in_specs=vmem_specs(5),
        out_specs=tuple(vmem_specs(3)),
        compiler_params=pltpu.CompilerParams(vmem_limit_bytes=16 * MIB),
        name="attend",
    )(bounds, q, kv, kvt, begun)


def backward_kernel(
    bounds_ref, q_ref, kv_ref, kvt_ref, do_ref, o_ref, lse_ref, dq_out, dkv_out, delta_out, dkv
):
    _, _, z, y = place()
    key_tile = kv_ref.shape[1]
    dkv[...] = jnp.zeros_like(dkv)
    for group in range(q_ref.shape[0] * q_ref.shape[1] // (CHAINS * QUERY_TILE)):
        tiles, queries = query_group(q_ref, group, y)
        out_grads = group_grads(do_ref, tiles, y)
        deltas, log_totals = [], []
        for tile, out_grad in zip(tiles, out_grads):
            product = jnp.transpose(out_grad.astype(F32) * o_ref[tile])
            deltas.append(jnp.sum(product, axis=0, keepdims=True))
            delta_out[tile] = jnp.broadcast_to(deltas[-1], delta_out.shape[1:])
            log_totals.append(lse_ref[tile, 0:1, :])
        known = (queries, out_grads, deltas, log_totals)

        def step(block, carry, tiles=tiles, known=known):
            first = pl.multiple_of(block * key_tile, key_tile)
            across = kvt_ref[:, pl.ds(first, key_tile)]
            given, carry = attend_back(bounds_ref, tiles, first, kv_ref[block], across, known, carry)
            dkv[block] += given
            return carry

        zero = jnp.zeros((LANES, QUERY_TILE), F32)
        ends = other_blocks(bounds_ref, group, key_tile, z, step, (zero,) * CHAINS)
        for tile, mixed in zip(tiles, ends):
            dq_out[tile] = mixed
    for block in range(dkv.shape[0]):
        dkv_out[block] = dkv[block].astype(BF16)


def call_backward(bounds, q, kv, kvt, d_o, o, lse):
    blks, span, _ = kv.shape
    tiles = 2 * span // QUERY_TILE
    return pl.pallas_call(
        backward_kernel,
        out_shape=(
            jax.ShapeDtypeStruct((tiles, LANES, QUERY_TILE), F32),
            jax.ShapeDtypeStruct((blks, span, LANES), BF16),
            jax.ShapeDtypeStruct((tiles, 8, QUERY_TILE), F32),
        ),
        in_specs=vmem_specs(7),
        out_specs=tuple(vmem_specs(3)),
        scratch_shapes=[pltpu.VMEM((blks, span, LANES), F32)],
        compiler_params=pltpu.CompilerParams(vmem_limit_bytes=16 * MIB),
        name="attend_back",
    )(bounds, q, kv, kvt, d_o, o, lse)


def gelu_parts(values):
    share = 0.5 * (1.0 + lax.erf(values * (2.0**-0.5)))
    slope = share + values * jnp.exp(-0.5 * values * values) * (2.0 * math.pi) ** -0.5
    return values * share, slope


def positions(expert_rows, expert_cols, rank_row, rank_col):
    def count(mask, axis):
        return jnp.sum(mask.astype(F32), axis=axis, keepdims=True)

    row = [None, None]
    col = [None, None]
    before = rank_col < rank_row
    after = rank_row < rank_col
    for choice in range(2):
        row[choice] = count((expert_cols[choice] == expert_rows[choice]) & before, 0)
        col[choice] = count((expert_rows[choice] == expert_cols[choice]) & after, 1)
    row[1] = row[1] + count(expert_cols[0] == expert_rows[1], 0)
    col[1] = col[1] + count(expert_rows[0] == expert_cols[1], 1)
    return row, col


def own_columns(rows_ref, turned, blk, capacity):
    blks, _, slots = rows_ref.shape
    rows = jnp.concatenate(
        [rows_ref[...].reshape(blks, slots), jnp.zeros((LANES - blks, slots), F32)], axis=0
    )
    for piece in range(slots // LANES):
        columns = slice(piece * LANES, (piece + 1) * LANES)
        turned[columns, :] = jnp.transpose(rows[:, columns])
    own = turned[pl.ds(pl.multiple_of(blk * capacity, capacity), capacity), :]
    return jnp.concatenate([own[:, source : source + 1] for source in range(blks)], axis=0)


def middle_kernel(
    heads, blks,
    x_hbm, o_ref, wo_ref, routes_hbm, rank_hbm, d_out_hbm, win_hbm, wout_hbm,
    po, hidden_ref, share_ref, dh_ref, dma_all, grads_ref, rx,
    x_ref, routes_ref, rank_ref, d_out_ref, win_ref, wout_ref, rows_in, in_sem,
    o_all, dos, doa, rs, ra, dr, da, dms, acc_out, acc_row, mix, gate_rows, d_gate_rows, turned,
    o_send, o_recv, dos_send, dos_recv, r_send, r_recv,
    dr_send, dr_recv, dm_send, dm_recv, rx_send, rx_recv, g_send, g_recv, dg_send, dg_recv,
):
    head, blk, z, y = place()
    tokens, model = x_ref.shape
    capacity = 2 * tokens // blks
    slots = capacity * blks
    plane = [(k % heads, k // heads) for k in range(1, 2 * heads)]
    wanted = (
        (routes_hbm, routes_ref), (rank_hbm, rank_ref), (d_out_hbm, d_out_ref), (x_hbm, x_ref),
        (win_hbm, win_ref), (wout_hbm, wout_ref),
    )
    fetched = [
        pltpu.make_async_copy(src, dst, in_sem.at[i]) for i, (src, dst) in enumerate(wanted)
    ]
    for copy in fetched:
        copy.start()
    met = greet(
        [(around(head, kh, heads), 2 * z + around(y, ky, 2)) for kh, ky in plane]
        + [(head, around(blk, k, blks)) for k in range(1, blks)]
    )
    meet(met)

    def plane_copies(src_of, dst, send, recv):
        copies = []
        for k, (kh, ky) in enumerate(plane):
            to_head, to_y = around(head, kh, heads), around(y, ky, 2)
            copies.append(
                remote(src_of(to_y, to_head), dst, send.at[k], recv.at[k], to_head, 2 * z + to_y)
            )
        return copies

    def blk_copies(src, dst, send, recv):
        return [
            remote(
                src.at[around(blk, k, blks)], dst.at[blk],
                send.at[k], recv.at[k], head, around(blk, k, blks),
            )
            for k in range(1, blks)
        ]

    def start(copies):
        for copy in copies:
            copy.start()

    def finish(copies):
        for copy in copies:
            copy.wait()

    o_copies = plane_copies(lambda to_y, to_head: o_ref.at[to_y, to_head], o_all.at[y, head], o_send, o_recv)
    start(o_copies)
    o_all[y, head] = o_ref[y, head]

    lanes = lane_ids((tokens, LANES))
    for copy in fetched[:4]:
        copy.wait()
    e_rows = [routes_ref[i : i + 1, :].astype(F32) for i in range(2)]
    rank_row = rank_ref[...].astype(F32)
    rows_in[...] = jnp.zeros_like(rows_in)
    rows_in[0:1, :], rows_in[1:2, :], rows_in[2:3, :] = *e_rows, rank_row
    columns = jnp.transpose(rows_in[...])
    e_cols = [columns[:, 0:1], columns[:, 1:2]]
    rank_col = columns[:, 2:3]
    pos_rows, pos_cols = positions(e_rows, e_cols, rank_row, rank_col)

    def slot_of(expert, position):
        return jnp.where(position < capacity, expert * capacity + position, -1.0).astype(jnp.int32)

    slot_rows = [slot_of(e, p) for e, p in zip(e_rows, pos_rows)]
    slot_cols = [slot_of(e, p) for e, p in zip(e_cols, pos_cols)]
    slot_down = lax.broadcasted_iota(jnp.int32, (slots, tokens), 0)
    slot_across = lane_ids((tokens, slots))
    pick = [(slot_down == s).astype(BF16) for s in slot_rows]
    put = [(slot_across == s).astype(BF16) for s in slot_cols]
    pick_any = pick[0] + pick[1]
    put_any = put[0] + put[1]

    d_out = d_out_ref[...]
    dos[...] = dot(pick_any, d_out.astype(BF16)).astype(BF16).reshape(dos.shape)
    dos_copies = blk_copies(dos, doa, dos_send, dos_recv)
    start(dos_copies)
    doa[blk] = dos[blk]

    weight_out = jnp.concatenate(
        [wo_ref[(b ^ 1) * HALF : ((b ^ 1) + 1) * HALF, 0:model] for b in range(blks)], axis=0
    )
    small = wo_ref[:, model : model + LANES]
    small_across = jnp.concatenate(
        [
            jnp.transpose(small[i * LANES : (i + 1) * LANES].astype(F32))
            for i in range(model // LANES)
        ],
        axis=1,
    )
    gain = small_across[blks : blks + 1, :]

    finish(o_copies)
    low_lanes = lanes[:HALF] < HALF
    for piece in range(heads):
        columns = slice(piece * LANES, (piece + 1) * LANES)
        first, second = o_all[1, piece].astype(F32), o_all[0, piece].astype(F32)
        mix[:HALF, columns] = jnp.where(low_lanes, first, second).astype(BF16)
        swapped = pltpu.roll(jnp.where(low_lanes, second, first), HALF, 1)
        mix[HALF:, columns] = swapped.astype(BF16)
    mixed = mix[...]
    hidden = x_ref[...].astype(F32) + dot(mixed, weight_out)
    xhat, scale = centre(hidden)
    routed = (xhat * gain).astype(BF16)
    rs[...] = dot(pick_any, routed).astype(BF16).reshape(rs.shape)
    r_copies = blk_copies(rs, ra, r_send, r_recv)
    start(r_copies)
    ra[blk] = rs[blk]
    logits = jnp.where(lanes < blks, dot(routed, small), MASKED)
    powers = jnp.exp(logits - jnp.max(logits, axis=1, keepdims=True))
    probs = powers / jnp.sum(powers, axis=1, keepdims=True)
    lanes_f = lanes.astype(F32)
    hots = [lanes_f == e for e in e_cols]
    gates = [jnp.sum(jnp.where(hot, probs, 0.0), axis=1, keepdims=True) for hot in hots]
    gate_high = [g.astype(BF16).astype(F32) for g in gates]
    gate_across = jnp.transpose(
        jnp.where(lanes == 0, gate_high[0], jnp.where(lanes == 1, gates[0] - gate_high[0], 0.0))
        + jnp.where(lanes == 2, gate_high[1], jnp.where(lanes == 3, gates[1] - gate_high[1], 0.0))
    ).astype(BF16)
    by_slot = (dot(gate_across, put[0]), dot(gate_across, put[1]))
    gate_rows[blk] = by_slot[0][0:1] + by_slot[0][1:2] + by_slot[1][2:3] + by_slot[1][3:4]
    g_copies = [
        remote(
            gate_rows.at[blk], gate_rows.at[blk],
            g_send.at[k], g_recv.at[k], head, around(blk, k, blks),
        )
        for k in range(1, blks)
    ]
    start(g_copies)
    acc_out[...] = jnp.zeros_like(acc_out)
    acc_row[...] = jnp.zeros_like(acc_row)
    finish(dos_copies)
    finish(r_copies)

    out_rows = doa[...].reshape(slots, model)
    rx[head, :, 0:model] = ra[...].reshape(slots, model)
    finish(g_copies)
    gate_col = own_columns(gate_rows, turned, blk, capacity)
    rx[head, :, model : 2 * model] = (out_rows.astype(F32) * gate_col).astype(BF16)
    core = lax.rem(head, 2)
    sibling, across = head - core + 1 - core, around(head, 2, heads)

    def half_rows(source, half):
        return rx.at[source, pl.ds(half * slots // 2, slots // 2)]

    to_across = [
        remote(
            half_rows(head, half), half_rows(head, half),
            rx_send.at[1 + half], rx_recv.at[1 + half], across, blk,
        )
        for half in range(2)
    ]
    to_sibling = remote(rx.at[head], rx.at[head], rx_send.at[0], rx_recv.at[0], sibling, blk)
    forwards = [
        remote(
            half_rows(across, half), half_rows(across, half),
            rx_send.at[3 + half], rx_recv.at[3 + half], sibling, blk,
        )
        for half in range(2)
    ]
    start(to_across)
    to_sibling.start()
    half_ff = wout_ref.shape[0] // 4
    for copy in fetched[4:]:
        copy.wait()

    @pl.loop(0, 4)
    def _(chunk):
        first = pl.multiple_of(chunk * half_ff, half_ff)
        into = win_ref[:, pl.ds(first, half_ff)]
        outof = wout_ref[pl.ds(first, half_ff), :]
        act, slope = gelu_parts(dot(rx[head, :, 0:model], into))
        acc_out[...] += dot(act.astype(BF16), outof)
        d_act = dot(rx[head, :, model : 2 * model], outof, (1, 1))
        acc_row[...] += dot((slope * d_act).astype(BF16), into, (1, 1))

    result = acc_out[...].astype(BF16)
    d_gate = jnp.sum(out_rows.astype(F32) * result.astype(F32), axis=1, keepdims=True)
    dr[...] = acc_row[...].astype(BF16).reshape(dr.shape)
    dr_copies = blk_copies(dr, da, dr_send, dr_recv)
    start(dr_copies)
    da[blk] = dr[blk]
    d_wide = jnp.broadcast_to(d_gate, (slots, LANES))
    d_gate_rows[blk] = jnp.concatenate(
        [jnp.transpose(d_wide[i * LANES : (i + 1) * LANES])[0:1] for i in range(slots // LANES)],
        axis=1,
    )
    dg_copies = [
        remote(
            d_gate_rows.at[blk], d_gate_rows.at[blk],
            dg_send.at[k], dg_recv.at[k], head, around(blk, k, blks),
        )
        for k in range(1, blks)
    ]
    start(dg_copies)
    po[...] = result.reshape(blks, capacity, model)

    finish(dg_copies)
    back_gate = own_columns(d_gate_rows, turned, blk, capacity)
    back_gate = split_high_low(back_gate, lane_ids((slots, LANES)))
    d_gates = [join_high_low(dot(p, back_gate), 0) for p in put]
    d_probs = jnp.where(hots[0], d_gates[0], 0.0) + jnp.where(hots[1], d_gates[1], 0.0)
    d_logits = probs * (d_probs - jnp.sum(probs * d_probs, axis=1, keepdims=True))
    d_high = d_logits.astype(BF16)
    d_low = (d_logits - d_high.astype(F32)).astype(BF16)
    d_router_part = dot(d_high, small, (1, 1)) + dot(d_low, small, (1, 1))
    finish(dr_copies)
    d_routed = dot(put_any, da[...].reshape(slots, model)) + d_router_part
    d_hidden = d_out + centre_back(d_routed * gain, xhat, scale)
    dh_ref[...] = d_hidden
    d_attn = d_hidden.astype(BF16)
    d_mixed = dot(d_attn, weight_out, (1, 1))
    for piece in range(heads):
        block = d_mixed[:, piece * LANES : (piece + 1) * LANES]
        for to_y in range(2):
            dms[to_y, piece] = halves(block, low_lanes == (to_y == 1)).astype(BF16)
    dm_copies = plane_copies(lambda to_y, to_head: dms.at[to_y, to_head], dma_all.at[y, head], dm_send, dm_recv)
    start(dm_copies)
    dma_all[y, head] = dms[y, head]
    arrived(half_rows(across, 0), rx_recv.at[1])
    forwards[0].start()

    d_weight = dot(mixed, d_attn, (0, 0)).astype(BF16)
    for b in range(blks):
        grads_ref[b, :, 0:model] = d_weight[(b ^ 1) * HALF : ((b ^ 1) + 1) * HALF, :]
    last = (lanes == blks).astype(BF16)
    d_small = dot(routed, d_high, (0, 0)) + dot((d_routed * xhat).astype(BF16), last, (0, 0))
    grads_ref[:, :, model : model + LANES] = d_small.astype(BF16).reshape(blks, HALF, LANES)
    share = gates[0] * put[0].astype(F32) + gates[1] * put[1].astype(F32)
    share_ref[0] = share.astype(BF16)
    share_ref[1] = (share - share_ref[0].astype(F32)).astype(BF16)
    hidden_ref[...] = hidden

    arrived(half_rows(across, 1), rx_recv.at[2])
    forwards[1].start()
    finish(dm_copies)
    to_sibling.wait()
    for copy in to_across:
        copy.wait_send()
    finish(forwards)


def call_middle(x, o, wo, routes, rank, d_out, win, wout, heads, blks):
    tokens, model = x.shape
    capacity = 2 * tokens // blks
    slots = capacity * blks
    wide = model + LANES

    def rows(width):
        return pltpu.VMEM((blks, capacity, width), BF16)

    def block(*lead):
        return pltpu.VMEM((*lead, tokens // 2, LANES), BF16)

    return pl.pallas_call(
        functools.partial(middle_kernel, heads, blks),
        out_shape=(
            jax.ShapeDtypeStruct((blks, capacity, model), BF16),
            jax.ShapeDtypeStruct((tokens, model), F32),
            jax.ShapeDtypeStruct((2, tokens, slots), BF16),
            jax.ShapeDtypeStruct((tokens, model), F32),
            jax.ShapeDtypeStruct((2, heads, tokens // 2, LANES), BF16),
            jax.ShapeDtypeStruct((blks, model // blks, wide), BF16),
            jax.ShapeDtypeStruct((heads, slots, 2 * model), BF16),
        ),
        in_specs=hbm_specs(1) + vmem_specs(2) + hbm_specs(5),
        out_specs=tuple(vmem_specs(7)),
        scratch_shapes=[
            pltpu.VMEM((tokens, model), BF16),
            pltpu.VMEM((2, tokens), jnp.int32),
            pltpu.VMEM((1, tokens), jnp.int32),
            pltpu.VMEM((tokens, model), F32),
            pltpu.VMEM(win.shape, BF16),
            pltpu.VMEM(wout.shape, BF16),
            pltpu.VMEM((tokens, tokens), F32),
            dma(6),
            block(2, heads), rows(model), rows(model), rows(model), rows(model),
            rows(model), rows(model), block(2, heads),
            pltpu.VMEM((slots, model), F32), pltpu.VMEM((slots, model), F32),
            pltpu.VMEM((tokens, model), BF16),
            pltpu.VMEM((blks, 1, slots), F32), pltpu.VMEM((blks, 1, slots), F32),
            pltpu.VMEM((slots, LANES), F32),
            dma(2 * heads), dma(2 * heads), dma(blks), dma(blks), dma(blks), dma(blks),
            dma(blks), dma(blks), dma(2 * heads), dma(2 * heads), dma(5), dma(5),
            dma(blks), dma(blks), dma(blks), dma(blks),
        ],
        compiler_params=pltpu.CompilerParams(
            collective_id=2, has_side_effects=True, vmem_limit_bytes=20 * MIB
        ),
        name="experts",
    )(*in_hbm(x), o, wo, *in_hbm(routes.T, rank, d_out, win, wout))


def last_kernel(
    heads, blks,
    x_hbm, dh_ref, begun_ref, dkv_ref, xa_ref, wa_ref, w_hbm, g1_hbm, grads_ref, rx_ref, win_hbm, wout_hbm,
    po_ref, hidden_ref, share_ref, bounds_ref, q_ref, kv_ref, kvt_ref, do_ref, lse_ref, delta_ref,
    y_ref, dx_ref, dw_ref, shared_ref, din_ref, dout_ref,
    x_ref, w_ref, g1_ref, win_ref, wout_ref, in_sem,
    gain_tile, far_all, near_send_buf, near_all, pair_all, dq_all, dq_ref, dq_packed, dkv_own, pair_buf, us, ua, gs, ga, gqs, gqa, u_part, xat, pa, gh, w1, w2s, w2, w3,
    q_send, q_recv, pair_send, pair_recv, far_send, far_recv, near_send, near_recv,
    u_send, u_recv, g_send, g_recv, gh_send, gh_recv, w1_send, w1_recv, w2_send, w2_recv,
    w3_send, w3_recv, e_send, e_recv, gq_send, gq_recv, po_send, po_recv,
):
    head, blk, z, y = place()
    planes = blks // 2
    tokens, model = x_ref.shape
    rows = w_ref.shape[0]
    wanted = (
        (win_hbm, win_ref), (wout_hbm, wout_ref), (x_hbm, x_ref), (w_hbm, w_ref), (g1_hbm, g1_ref)
    )
    fetched = [
        pltpu.make_async_copy(src, dst, in_sem.at[i]) for i, (src, dst) in enumerate(wanted)
    ]
    for copy in fetched:
        copy.start()
    met = greet(
        [(around(head, k, heads), blk) for k in range(1, heads)]
        + [(head, around(blk, k, blks)) for k in range(1, blks)]
    )
    meet(met)

    def start(copies):
        for copy in copies:
            copy.start()

    def finish(copies):
        for copy in copies:
            copy.wait()

    other_y = around(y, 1, 2)
    pair = 2 * z + other_y
    above, below = z < planes - 1, z > 0
    directions = ((1, above, below, 0), (-1, below, above, 2))

    def far_copy(step, slot, side):
        span = 2 * (z + 2 * step) + side
        return remote(
            dkv_ref.at[span], far_all.at[slot + side],
            far_send.at[slot + side], far_recv.at[slot + side], head, 2 * (z + step) + y,
        )

    def near_copy(step, slot, side):
        return remote(
            near_send_buf.at[slot + side], near_all.at[slot // 2, y],
            near_send.at[slot + side], near_recv.at[slot // 2, y], head, 2 * (z + step) + side,
        )

    def two_away(step):
        return z + 2 * step < planes if step > 0 else z + 2 * step >= 0

    for step, there, back, slot in directions:

        @pl.when(two_away(step))
        def _():
            for side in range(2):
                far_copy(step, slot, side).start()

    w1_copies = [
        remote(
            grads_ref.at[:, around(head, k, heads)], w1.at[head],
            w1_send.at[k], w1_recv.at[k], around(head, k, heads), blk,
        )
        for k in range(1, heads)
    ]
    start(w1_copies)
    w1[head] = grads_ref[:, head]

    core = lax.rem(head, 2)
    sibling = head - core + 1 - core
    ff_half = wout_ref.shape[0] // 2
    ff_step = ff_half // 4

    def expert_chunk(chunk):
        here = pl.multiple_of(core * ff_half + chunk * ff_step, ff_step)
        there = pl.multiple_of(chunk * ff_step, ff_step)
        into = win_ref[:, pl.ds(here, ff_step)]
        outof = wout_ref[pl.ds(here, ff_step), :]
        d_in = jnp.zeros((model, ff_step), F32)
        d_out = jnp.zeros((ff_step, model), F32)
        for source in range(heads):
            rows_in = rx_ref[source, :, 0:model]
            grads_out = rx_ref[source, :, model : 2 * model]
            act, slope = gelu_parts(dot(rows_in, into))
            d_act = dot(grads_out, outof, (1, 1))
            d_in = d_in + dot(rows_in, (slope * d_act).astype(BF16), (0, 0))
            d_out = d_out + dot(act.astype(BF16), grads_out, (0, 0))
        din_ref[core, :, pl.ds(there, ff_step)] = d_in.astype(BF16)
        dout_ref[core, pl.ds(there, ff_step), :] = d_out.astype(BF16)

    key_tile = kv_ref.shape[1]
    for group in range(2 * key_tile // (CHAINS * QUERY_TILE)):
        tiles, queries = query_group(q_ref, group, y)
        known = (
            queries,
            group_grads(do_ref, tiles, y),
            [delta_ref[tile, 0:1, :] for tile in tiles],
            [lse_ref[tile, 0:1, :] for tile in tiles],
        )
        carry = tuple(begun_ref[tile] for tile in tiles)
        for side in range(2):
            first = pl.multiple_of((2 * z + side) * key_tile, key_tile)
            keys_across = kvt_ref[:, pl.ds(first, key_tile)]
            given, carry = attend_back(
                bounds_ref, tiles, first, kv_ref[2 * z + side], keys_across, known, carry
            )
            dkv_own[side] = given if group == 0 else dkv_own[side] + given
        for tile, total in zip(tiles, carry):
            at = tile * QUERY_TILE % key_tile
            dq_ref[tile * QUERY_TILE // key_tile, at : at + QUERY_TILE] = jnp.transpose(total)
    pair_buf[...] = dkv_own[other_y].astype(BF16)
    pair_copy = remote(pair_buf, pair_all, pair_send, pair_recv, head, pair)
    pair_copy.start()
    own_lanes = (lane_ids(dq_packed.shape) < HALF) == (y == 0)
    dq_packed[...] = halves(dq_ref[other_y], own_lanes).astype(BF16)
    q_copy = remote(dq_packed, dq_all, q_send, q_recv, head, pair)
    q_copy.start()
    for step, there, back, slot in directions:

        @pl.when(there)
        def _():
            for side in range(2):
                near_send_buf[slot + side] = dkv_ref[2 * (z + step) + side]

        @pl.when(jnp.logical_and(there, back))
        def _():
            for side in range(2):
                arrived(far_all.at[slot + side], far_recv.at[slot + side])
                near_send_buf[slot + side] = (
                    near_send_buf[slot + side].astype(F32) + far_all[slot + side].astype(F32)
                ).astype(BF16)

        @pl.when(there)
        def _():
            for side in range(2):
                near_copy(step, slot, side).start()

    finish(fetched[:2])
    weight = wa_ref[...].reshape(model, 3 * LANES)
    for piece in range(heads):
        xat[:, piece * tokens : (piece + 1) * tokens] = jnp.transpose(xa_ref[piece])
    even = y == 0


    @pl.loop(0, 2)
    def _(chunk):
        expert_chunk(chunk)

    q_copy.wait()
    landed = dq_all[...].astype(F32)
    landed = jnp.concatenate([landed, pltpu.roll(landed, HALF, 1)], axis=0)
    own_lanes = (lane_ids(landed.shape) < HALF) == even
    q_grads = jnp.where(own_lanes, dq_ref[y], landed).astype(BF16)
    gqs[...] = dot(xat[...], q_grads).astype(BF16).reshape(gqs.shape)
    gq_copies = [
        remote(
            gqs.at[around(blk, k, blks)], gqa.at[blk],
            gq_send.at[k], gq_recv.at[k], head, around(blk, k, blks),
        )
        for k in range(1, blks)
    ]
    start(gq_copies)
    gqa[blk] = gqs[blk]
    u_part[...] = dot(q_grads, weight[:, 2 * LANES : 3 * LANES], (1, 1)).reshape(u_part.shape)

    finish(w1_copies)
    summed = w1[0].astype(F32)
    for source in range(1, heads):
        summed = summed + w1[source].astype(F32)
    w2s[...] = summed.astype(BF16)
    w2_copies = [
        remote(
            w2s.at[around(blk, k, blks)], w2.at[blk],
            w2_send.at[k], w2_recv.at[k], head, around(blk, k, blks),
        )
        for k in range(1, blks)
    ]
    start(w2_copies)
    w2[blk] = w2s[blk]

    @pl.loop(2, 4)
    def _(chunk):
        expert_chunk(chunk)

    e_copies = [
        remote(din_ref.at[core], din_ref.at[core], e_send.at[0], e_recv.at[0], sibling, blk),
        remote(dout_ref.at[core], dout_ref.at[core], e_send.at[1], e_recv.at[1], sibling, blk),
    ]
    start(e_copies)

    pair_copy.wait()
    for step, there, back, slot in directions:

        @pl.when(back)
        def _():
            for side in range(2):
                arrived(near_all.at[slot // 2, side], near_recv.at[slot // 2, side])

        @pl.when(jnp.logical_not(back))
        def _():
            near_all[slot // 2] = jnp.zeros(near_all.shape[1:], BF16)

    own = dkv_own[y]
    other = pair_all[...].astype(F32)
    made = jnp.concatenate(
        [
            (
                jnp.where(even == (side == 0), own, other)
                + near_all[0, side].astype(F32)
                + near_all[1, side].astype(F32)
            ).astype(BF16)
            for side in range(2)
        ],
        axis=1,
    )
    gs[...] = dot(xat[...], made).astype(BF16).reshape(gs.shape)
    g_copies = [
        remote(
            gs.at[around(blk, k, blks)], ga.at[blk],
            g_send.at[k], g_recv.at[k], head, around(blk, k, blks),
        )
        for k in range(1, blks)
    ]
    start(g_copies)
    ga[blk] = gs[blk]
    us[...] = (
        u_part[...] + dot(made, weight[:, 0 : 2 * LANES], (1, 1)).reshape(us.shape)
    ).astype(BF16)
    u_copies = [
        remote(
            us.at[around(head, k, heads)], ua.at[head],
            u_send.at[k], u_recv.at[k], around(head, k, heads), blk,
        )
        for k in range(1, heads)
    ]
    start(u_copies)
    ua[head] = us[head]
    finish(fetched[2:])

    finish(w2_copies)
    part = w2[0].astype(F32)
    for source in range(1, blks):
        part = part + w2[source].astype(F32)
    w3[head] = part.astype(BF16)
    w3_copies = [
        remote(w3.at[head], w3.at[head], w3_send.at[k], w3_recv.at[k], around(head, k, heads), blk)
        for k in range(1, heads)
    ]
    start(w3_copies)

    xhat, scale = centre(x_ref[...].astype(F32))
    finish(gq_copies)
    total = gqa[0].astype(F32)
    for source in range(1, blks):
        total = total + gqa[source].astype(F32)
    gh[head, :, 2 * LANES : 3 * LANES] = total.astype(BF16)
    finish(g_copies)
    total = ga[0].astype(F32)
    for source in range(1, blks):
        total = total + ga[source].astype(F32)
    gh[head, :, 0 : 2 * LANES] = total.astype(BF16)
    gh_copies = [
        remote(gh.at[head], gh.at[head], gh_send.at[k], gh_recv.at[k], around(head, k, heads), blk)
        for k in range(1, heads)
    ]
    start(gh_copies)
    po_copies = [
        remote(
            po_ref.at[around(blk, k, blks)], pa.at[blk],
            po_send.at[k], po_recv.at[k], head, around(blk, k, blks),
        )
        for k in range(1, blks)
    ]
    start(po_copies)
    pa[blk] = po_ref[blk]
    finish(u_copies)
    grad = ua[0].astype(F32)
    for source in range(1, heads):
        grad = grad + ua[source].astype(F32)
    dx_ref[...] = dh_ref[...] + centre_back(grad, xhat, scale)

    gain_tile[...] = jnp.zeros_like(gain_tile)
    gain_tile[0:1, 0:rows] = g1_ref[...].astype(F32)
    gain = jnp.transpose(jnp.broadcast_to(gain_tile[0:1, :], (LANES, LANES)))[:rows]
    low_half = lane_ids((rows, LANES)) < HALF
    finish(gh_copies)
    d_gain = jnp.zeros((rows, LANES), F32)
    for source in range(heads):
        both = [gh[source, :, i * LANES : (i + 1) * LANES].astype(F32) for i in range(3)]
        grads = (
            both[2] * HS ** (-0.5),
            jnp.where(low_half, both[0], both[1]),
            pltpu.roll(jnp.where(low_half, both[1], both[0]), HALF, 1),
        )
        for which, value in enumerate(grads):
            columns = slice(which * model + source * LANES, which * model + (source + 1) * LANES)
            d_gain = d_gain + value * w_ref[:, columns].astype(F32)
            dw_ref[:, columns] = value * gain
    finish(w3_copies)
    shared = w3[...].reshape(rows, w3.shape[-1]).astype(F32)
    shared_ref[:, 0:model] = shared[:, 0:model]
    gain_col = jnp.sum(d_gain, axis=1, keepdims=True)
    shared_ref[:, model : model + LANES] = jnp.where(
        lane_ids((rows, LANES)) == blks + 1, gain_col, shared[:, model : model + LANES]
    )
    finish(po_copies)
    parts = pa[...].reshape(share_ref.shape[2], model)
    mixture = dot(share_ref[0], parts) + dot(share_ref[1], parts)
    y_ref[...] = (hidden_ref[...] + mixture).astype(BF16)

    for step, there, back, slot in directions:

        @pl.when(two_away(step))
        def _():
            for side in range(2):
                far_copy(step, slot, side).wait_send()

        @pl.when(there)
        def _():
            for side in range(2):
                near_copy(step, slot, side).wait_send()

    finish(e_copies)


def call_last(
    x, dh, dq, dkv, xa, wa, w_qkv, g1, grads, rx, win, wout, po, hidden, share,
    bounds, q, kv, kvt, d_o, lse, delta, heads, blks,
):
    tokens, model = x.shape
    span = tokens * heads
    rows = w_qkv.shape[0]
    wide = model + LANES
    part = rows // heads
    ff = wout.shape[0]

    def block(*lead):
        return pltpu.VMEM((*lead, span, LANES), BF16)

    return pl.pallas_call(
        functools.partial(last_kernel, heads, blks),
        out_shape=(
            jax.ShapeDtypeStruct((tokens, model), BF16),
            jax.ShapeDtypeStruct((tokens, model), F32),
            jax.ShapeDtypeStruct((rows, 3 * model), F32),
            jax.ShapeDtypeStruct((rows, wide), F32),
            jax.ShapeDtypeStruct((2, model, ff // 2), BF16),
            jax.ShapeDtypeStruct((2, ff // 2, model), BF16),
        ),
        in_specs=hbm_specs(1) + vmem_specs(5) + hbm_specs(2) + vmem_specs(2) + hbm_specs(2) + vmem_specs(10),
        out_specs=tuple(vmem_specs(6)),
        scratch_shapes=[
            pltpu.VMEM((tokens, model), BF16),
            pltpu.VMEM((rows, 3 * model), BF16),
            pltpu.VMEM((1, rows), BF16),
            pltpu.VMEM(win.shape, BF16),
            pltpu.VMEM(wout.shape, BF16),
            dma(5),
            pltpu.VMEM((8, LANES), F32),
            block(4), block(4), block(2, 2), block(), pltpu.VMEM((span // 2, LANES), BF16),
            pltpu.VMEM((2, span, LANES), F32), pltpu.VMEM((span // 2, LANES), BF16),
            pltpu.VMEM((2, span, LANES), F32), block(),
            pltpu.VMEM((heads, tokens, model), BF16), pltpu.VMEM((heads, tokens, model), BF16),
            pltpu.VMEM((blks, rows, 2 * LANES), BF16), pltpu.VMEM((blks, rows, 2 * LANES), BF16),
            pltpu.VMEM((blks, rows, LANES), BF16), pltpu.VMEM((blks, rows, LANES), BF16),
            pltpu.VMEM((heads, tokens, model), F32), pltpu.VMEM((model, span), BF16),
            pltpu.VMEM(po.shape, BF16),
            pltpu.VMEM((heads, rows, 3 * LANES), BF16),
            pltpu.VMEM((heads, blks, part, wide), BF16), pltpu.VMEM((blks, part, wide), BF16),
            pltpu.VMEM((blks, part, wide), BF16), pltpu.VMEM((heads, part, wide), BF16),
            pltpu.SemaphoreType.DMA, pltpu.SemaphoreType.DMA, pltpu.SemaphoreType.DMA, pltpu.SemaphoreType.DMA,
            dma(4), dma(4), dma(4), dma(2, 2),
            dma(heads), dma(heads), dma(blks), dma(blks), dma(heads), dma(heads), dma(heads), dma(heads),
            dma(blks), dma(blks), dma(heads), dma(heads), dma(2), dma(2), dma(blks), dma(blks), dma(blks), dma(blks),
        ],
        compiler_params=pltpu.CompilerParams(
            collective_id=3, has_side_effects=True, vmem_limit_bytes=24 * MIB
        ),
        name="last",
    )(
        *in_hbm(x), dh, dq, dkv, xa, wa, *in_hbm(w_qkv, g1.reshape(1, rows)),
        grads.reshape(blks, heads, part, wide), rx, *in_hbm(win, wout), po, hidden, share,
        bounds, q, kv, kvt, d_o, lse, delta,
    )


def finish_kernel(
    experts,
    y_ref, dx_ref, dw_ref, shared_ref, din_ref, dout_ref,
    y_out, dx_out, g1_out, dw_out, dwo_out, g2_out, wr_out, din_out, dout_out,
    tile, wr, g2, g1, din, dout, sem, wide_sem,
):
    rows = shared_ref.shape[0]
    model = dx_ref.shape[1]
    copies = [
        pltpu.make_async_copy(dx_ref, dx_out, sem.at[0]),
        pltpu.make_async_copy(dw_ref, dw_out, sem.at[1]),
        pltpu.make_async_copy(shared_ref.at[:, pl.ds(0, model)], dwo_out, sem.at[2]),
        pltpu.make_async_copy(y_ref, y_out, sem.at[6]),
    ]
    for copy in copies:
        copy.start()
    half = dout_ref.shape[1]
    quarter = half // 2
    for piece in range(4):
        down = slice(piece * quarter, (piece + 1) * quarter)
        dout[down, :] = dout_ref[piece // 2, (piece % 2) * quarter : (piece % 2 + 1) * quarter, :].astype(F32)
        copies.append(pltpu.make_async_copy(dout.at[down], dout_out.at[down], wide_sem.at[piece]))
        copies[-1].start()
    step = model // 4
    for piece in range(4):
        down = slice(piece * step, (piece + 1) * step)
        for side in range(2):
            din[down, side * half : (side + 1) * half] = din_ref[side, down, :].astype(F32)
        copies.append(pltpu.make_async_copy(din.at[down], din_out.at[down], wide_sem.at[4 + piece]))
        copies[-1].start()
    tile[...] = jnp.zeros_like(tile)
    tile[0:rows, :] = shared_ref[:, model : model + LANES]
    across = jnp.transpose(tile[...])[:, 0:rows]
    wr[...] = across[0:experts]
    g2[...] = across[experts : experts + 1]
    g1[...] = across[experts + 1 : experts + 2]
    for index, (src, dst) in enumerate(((wr, wr_out), (g2, g2_out), (g1, g1_out))):
        copies.append(pltpu.make_async_copy(src, dst, sem.at[3 + index]))
        copies[-1].start()
    for copy in copies:
        copy.wait()


def call_finish(output, dx, dw, shared, d_in, d_out):
    rows = shared.shape[0]
    model = dx.shape[1]
    experts = model // rows
    ff = 2 * d_out.shape[1]
    return pl.pallas_call(
        functools.partial(finish_kernel, experts),
        out_shape=(
            jax.ShapeDtypeStruct(output.shape, BF16),
            jax.ShapeDtypeStruct(dx.shape, F32),
            jax.ShapeDtypeStruct((1, rows), F32),
            jax.ShapeDtypeStruct(dw.shape, F32),
            jax.ShapeDtypeStruct((rows, model), F32),
            jax.ShapeDtypeStruct((1, rows), F32),
            jax.ShapeDtypeStruct((experts, rows), F32),
            jax.ShapeDtypeStruct((model, ff), F32),
            jax.ShapeDtypeStruct((ff, model), F32),
        ),
        in_specs=vmem_specs(6),
        out_specs=tuple(hbm_specs(9)),
        scratch_shapes=[
            pltpu.VMEM((LANES, LANES), F32),
            pltpu.VMEM((experts, rows), F32),
            pltpu.VMEM((1, rows), F32),
            pltpu.VMEM((1, rows), F32),
            pltpu.VMEM((model, ff), F32),
            pltpu.VMEM((ff, model), F32),
            dma(7),
            dma(8),
        ],
        compiler_params=pltpu.CompilerParams(vmem_limit_bytes=16 * MIB),
        name="finish",
    )(output, dx, dw, shared, d_in, d_out)


def local_kernels(
    inputs, ln1_gain, w_qkv, w_out, ln2_gain, w_router,
    expert_in, expert_out, routes, priority, doc_lengths, d_out,
):
    heads, blks = lax.axis_size("head"), lax.axis_size("blk")
    model = inputs.shape[1]
    tokens = inputs.shape[0]
    win, wout = expert_in[0], expert_out[0]
    q, kv, xa, wa, wo, kvt, bounds, begun = call_qkv(
        inputs, w_qkv, ln1_gain, w_out, w_router, ln2_gain, doc_lengths, heads, blks
    )
    o, o_low, lse = call_forward(bounds, q, kv, kvt, begun)
    po, hidden, share, dh, d_o, grads, rx = call_middle(
        inputs, o_low.reshape(2, heads, tokens // 2, LANES), wo.reshape(model, model + LANES),
        routes, priority, d_out, win, wout, heads, blks,
    )
    d_o = d_o.reshape(2 * heads * tokens // QUERY_TILE, -1, HALF, LANES)
    dq, dkv, delta = call_backward(bounds, q, kv, kvt, d_o, o, lse)
    ends = call_last(
        inputs, dh, dq, dkv, xa, wa, w_qkv, ln1_gain, grads, rx, win, wout,
        po, hidden, share, bounds, q, kv, kvt, d_o, lse, delta, heads, blks,
    )
    output, d_inputs, d_gain_one, d_qkv, d_out_proj, d_gain_two, d_router, d_in, d_out_weight = call_finish(*ends)
    return (
        output,
        d_inputs,
        d_gain_one.reshape(-1),
        d_qkv,
        d_out_proj,
        d_gain_two.reshape(-1),
        d_router.T,
        d_in[None],
        d_out_weight[None],
    )


def solution(mesh):
    in_specs = (
        P(("blk", "head"), None),
        P("blk"),
        P("blk", None),
        P("blk", None),
        P("blk"),
        P("blk", None),
        P("blk", None, None),
        P("blk", None, None),
        P(("blk", "head"), None),
        P(("blk", "head"), None),
        P(),
        P(("blk", "head"), None),
    )
    out_specs = (
        P(("blk", "head"), None),
        P(("blk", "head"), None),
        P("blk"),
        P("blk", None),
        P("blk", None),
        P("blk"),
        P("blk", None),
        P("blk", None, None),
        P("blk", None, None),
    )
    fits = mesh.shape["head"] == 4 and mesh.shape["blk"] == 8
    body = local_kernels if fits else local
    return jax.shard_map(body, mesh=mesh, in_specs=in_specs, out_specs=out_specs, check_vma=False)
```

```python
import functools
import math

import jax
import jax.numpy as jnp
from jax import lax
from jax.experimental import pallas as pl
from jax.experimental.pallas import tpu as pltpu
from jax.sharding import PartitionSpec as P

HS = 64
KEY_BLOCK = 2048


PRECISE = lax.Precision.HIGHEST
MASKED = -1e30
EPSILON = 1e-06


def layer_norm(values, gain):
    average = jnp.mean(values, axis=-1, keepdims=True)
    centred = values - average
    spread = jnp.mean(centred * centred, axis=-1, keepdims=True)
    return centred * lax.rsqrt(spread + EPSILON) * gain


def gelu_exact(values):
    return jax.nn.gelu(values, approximate=False)


def router(row_block, weight):
    return jax.nn.softmax(jnp.dot(row_block, weight, precision=PRECISE), axis=-1)


def doc_index(positions, doc_lengths):
    places = jnp.arange(doc_lengths.shape[0], dtype=jnp.int32)
    starts = jnp.sum(jnp.where(places[None, :] < places[:, None], doc_lengths[None, :], 0), axis=1)
    at_most = (starts[None, :] <= positions[:, None]).astype(jnp.int32)
    return jnp.sum(at_most, axis=1) - 1


def slot_table(route_rows, ranking, capacity):
    token_count = route_rows.shape[0]
    expert = jnp.transpose(route_rows).reshape(-1)
    pair_order = (jnp.arange(2, dtype=jnp.int32)[:, None] * token_count + ranking[None, :]).reshape(
        -1
    )
    before = (expert[:, None] == expert[None, :]) & (pair_order[None, :] < pair_order[:, None])
    position = jnp.sum(before.astype(jnp.int32), axis=1)
    slot_ids = jnp.where(position < capacity, expert * capacity + position, -1)
    return slot_ids.reshape(2, token_count)


def keep_state(current):
    return current


def local(
    inputs,
    ln1_gain,
    w_qkv,
    w_out,
    ln2_gain,
    w_router,
    expert_in,
    expert_out,
    routes,
    priority,
    doc_lengths,
    d_out,
):
    blk_size = lax.axis_size("blk")
    tok_rows = inputs.shape[0]
    model_width = inputs.shape[1]
    capacity = 2 * tok_rows // blk_size
    slot_total = blk_size * capacity
    gain_one, qkv_weight, out_weight, gain_two, router_weight = (
        lax.all_gather(ln1_gain, "blk", axis=0, tiled=True),
        lax.all_gather(w_qkv, "blk", axis=0, tiled=True),
        lax.all_gather(w_out, "blk", axis=0, tiled=True),
        lax.all_gather(ln2_gain, "blk", axis=0, tiled=True),
        lax.all_gather(w_router, "blk", axis=0, tiled=True),
    )
    input_rows = inputs.astype(jnp.float32)
    normed_one, norm_one_pull = jax.vjp(layer_norm, input_rows, gain_one.astype(jnp.float32))
    normed_low = normed_one.astype(jnp.bfloat16)
    qkv_rows = jnp.dot(normed_low, qkv_weight, preferred_element_type=jnp.float32).astype(
        jnp.bfloat16
    )
    query_heads, key_heads, value_heads = (
        lax.all_to_all(qkv_rows[:, :model_width], "head", split_axis=1, concat_axis=0, tiled=True),
        lax.all_to_all(
            qkv_rows[:, model_width : 2 * model_width],
            "head",
            split_axis=1,
            concat_axis=0,
            tiled=True,
        ),
        lax.all_to_all(
            qkv_rows[:, 2 * model_width :], "head", split_axis=1, concat_axis=0, tiled=True
        ),
    )
    span_rows = query_heads.shape[0]
    head_count = query_heads.shape[1] // HS
    key_all, value_all = (
        lax.all_gather(key_heads, "blk", axis=0, tiled=True),
        lax.all_gather(value_heads, "blk", axis=0, tiled=True),
    )
    total_rows = key_all.shape[0]
    block_count = total_rows // KEY_BLOCK
    scale_factor = HS ** (-0.5)
    query_pos = lax.axis_index("blk") * span_rows + jnp.arange(span_rows, dtype=jnp.int32)
    query_docs = doc_index(query_pos, doc_lengths)
    queries = query_heads.reshape(span_rows, head_count, HS)

    def block_parts(block_index, key_source, value_source):
        first_key = block_index * KEY_BLOCK
        key_rows = lax.dynamic_slice_in_dim(key_source, first_key, KEY_BLOCK, 0).reshape(
            KEY_BLOCK, head_count, HS
        )
        value_rows = lax.dynamic_slice_in_dim(value_source, first_key, KEY_BLOCK, 0).reshape(
            KEY_BLOCK, head_count, HS
        )
        key_docs = doc_index(first_key + jnp.arange(KEY_BLOCK, dtype=jnp.int32), doc_lengths)
        is_live = (key_docs[0] <= query_docs[-1]) & (key_docs[-1] >= query_docs[0])
        same_doc = query_docs[:, None] == key_docs[None, :]
        return (first_key, key_rows, value_rows, same_doc, is_live)

    def block_scores(key_rows, same_doc):
        raw_scores = (
            jnp.einsum("qhd,khd->hqk", queries, key_rows, preferred_element_type=jnp.float32)
            * scale_factor
        )
        return jnp.where(same_doc[None], raw_scores, MASKED)

    def stat_step(block_index, loop_state):
        first_key, key_rows, value_rows, same_doc, is_live = block_parts(
            block_index, key_all, value_all
        )

        def stat_update(current):
            running_max, running_sum = current
            scores = block_scores(key_rows, same_doc)
            new_max = jnp.maximum(running_max, jnp.max(scores, axis=2))
            exp_terms = jnp.where(same_doc[None], jnp.exp(scores - new_max[:, :, None]), 0.0)
            return (
                new_max,
                running_sum * jnp.exp(running_max - new_max) + jnp.sum(exp_terms, axis=2),
            )

        return lax.cond(is_live, stat_update, keep_state, loop_state)

    start_state = (
        jnp.full((head_count, span_rows), MASKED, jnp.float32),
        jnp.zeros((head_count, span_rows), jnp.float32),
    )
    running_max, running_sum = lax.fori_loop(0, block_count, stat_step, start_state)
    log_total = running_max + jnp.log(running_sum)

    def out_step(block_index, loop_state):
        first_key, key_rows, value_rows, same_doc, is_live = block_parts(
            block_index, key_all, value_all
        )

        def out_update(current):
            scores = block_scores(key_rows, same_doc)
            weights = jnp.where(
                same_doc[None], jnp.exp(scores - log_total[:, :, None]), 0.0
            ).astype(jnp.bfloat16)
            return current + jnp.einsum(
                "hqk,khd->qhd", weights, value_rows, preferred_element_type=jnp.float32
            )

        return lax.cond(is_live, out_update, keep_state, loop_state)

    mixed_full = lax.fori_loop(
        0, block_count, out_step, jnp.zeros((span_rows, head_count, HS), jnp.float32)
    )
    mixed_low = mixed_full.reshape(span_rows, head_count * HS).astype(jnp.bfloat16)
    mixed_tokens = lax.all_to_all(mixed_low, "head", split_axis=0, concat_axis=1, tiled=True)
    attended = jnp.dot(mixed_tokens, out_weight, preferred_element_type=jnp.float32)
    hidden_one = input_rows + attended
    normed_two, norm_two_pull = jax.vjp(layer_norm, hidden_one, gain_two.astype(jnp.float32))
    routed_low = normed_two.astype(jnp.bfloat16)
    router_probs, router_pull = jax.vjp(
        router, routed_low.astype(jnp.float32), router_weight.astype(jnp.float32)
    )
    slot_ids = slot_table(routes, priority[0], capacity)
    select = (
        slot_ids[:, :, None] == jnp.arange(slot_total, dtype=jnp.int32)[None, None, :]
    ).astype(jnp.bfloat16)
    send_rows = jnp.einsum(
        "kts,td->sd", select, routed_low, preferred_element_type=jnp.float32
    ).astype(jnp.bfloat16)
    expert_rows = lax.all_to_all(
        send_rows.reshape(blk_size, capacity, model_width),
        "blk",
        split_axis=0,
        concat_axis=0,
        tiled=True,
    ).reshape(slot_total, model_width)
    weight_in = expert_in[0]
    weight_out = expert_out[0]
    pre_act = jnp.dot(expert_rows, weight_in, preferred_element_type=jnp.float32)
    hidden_act, gelu_pull = jax.vjp(gelu_exact, pre_act)
    hidden_low = hidden_act.astype(jnp.bfloat16)
    expert_result = jnp.dot(hidden_low, weight_out, preferred_element_type=jnp.float32).astype(
        jnp.bfloat16
    )
    slot_result = lax.all_to_all(
        expert_result.reshape(blk_size, capacity, model_width),
        "blk",
        split_axis=0,
        concat_axis=0,
        tiled=True,
    ).reshape(slot_total, model_width)
    pair_result = jnp.einsum("kts,sd->ktd", select, slot_result, preferred_element_type=jnp.float32)
    route_hot = (routes[:, :, None] == jnp.arange(blk_size, dtype=jnp.int32)[None, None, :]).astype(
        jnp.float32
    )
    gate_vals = jnp.sum(router_probs[:, None, :] * route_hot, axis=2)
    mixture = gate_vals[:, 0, None] * pair_result[0] + gate_vals[:, 1, None] * pair_result[1]
    output = (hidden_one + mixture).astype(jnp.bfloat16)
    d_gates = jnp.transpose(jnp.sum(d_out[None] * pair_result, axis=2))
    d_probs = jnp.sum(d_gates[:, :, None] * route_hot, axis=1)
    pair_grads = (jnp.transpose(gate_vals)[:, :, None] * d_out[None]).astype(jnp.bfloat16)
    slot_grads = jnp.einsum(
        "kts,ktd->sd", select, pair_grads, preferred_element_type=jnp.float32
    ).astype(jnp.bfloat16)
    result_grads = lax.all_to_all(
        slot_grads.reshape(blk_size, capacity, model_width),
        "blk",
        split_axis=0,
        concat_axis=0,
        tiled=True,
    ).reshape(slot_total, model_width)
    d_hidden_act = jnp.dot(result_grads, weight_out.T, preferred_element_type=jnp.float32)
    d_weight_out = jnp.dot(hidden_low.T, result_grads, preferred_element_type=jnp.float32)
    d_preact = gelu_pull(d_hidden_act)[0].astype(jnp.bfloat16)
    d_weight_in = jnp.dot(expert_rows.T, d_preact, preferred_element_type=jnp.float32)
    row_grads = jnp.dot(d_preact, weight_in.T, preferred_element_type=jnp.float32).astype(
        jnp.bfloat16
    )
    slot_back = lax.all_to_all(
        row_grads.reshape(blk_size, capacity, model_width),
        "blk",
        split_axis=0,
        concat_axis=0,
        tiled=True,
    ).reshape(slot_total, model_width)
    d_routed = jnp.einsum("kts,sd->td", select, slot_back, preferred_element_type=jnp.float32)
    d_routed_router, d_router = router_pull(d_probs)
    d_hidden_norm, d_gain_two = norm_two_pull(d_routed + d_routed_router)
    d_hidden_one = d_out + d_hidden_norm
    attn_grads = d_hidden_one.astype(jnp.bfloat16)
    d_out_weight = jnp.dot(mixed_tokens.T, attn_grads, preferred_element_type=jnp.float32)
    mixed_grads = jnp.dot(attn_grads, out_weight.T, preferred_element_type=jnp.float32).astype(
        jnp.bfloat16
    )
    head_grads = lax.all_to_all(mixed_grads, "head", split_axis=1, concat_axis=0, tiled=True)
    out_grads = head_grads.reshape(span_rows, head_count, HS)
    row_delta = jnp.transpose(jnp.sum(out_grads.astype(jnp.float32) * mixed_full, axis=2))
    key_back, value_back = (
        lax.all_gather(key_heads, "blk", axis=0, tiled=True),
        lax.all_gather(value_heads, "blk", axis=0, tiled=True),
    )

    def grad_step(block_index, loop_state):
        first_key, key_rows, value_rows, same_doc, is_live = block_parts(
            block_index, key_back, value_back
        )

        def grad_update(current):
            query_grad, key_grad, value_grad = current
            scores = block_scores(key_rows, same_doc)
            weights = jnp.where(same_doc[None], jnp.exp(scores - log_total[:, :, None]), 0.0)
            value_part = jnp.einsum(
                "hqk,qhd->khd",
                weights.astype(jnp.bfloat16),
                out_grads,
                preferred_element_type=jnp.float32,
            )
            weight_grads = jnp.einsum(
                "qhd,khd->hqk", out_grads, value_rows, preferred_element_type=jnp.float32
            )
            score_grads = (weights * (weight_grads - row_delta[:, :, None])).astype(jnp.bfloat16)
            query_grad = (
                query_grad
                + jnp.einsum(
                    "hqk,khd->qhd", score_grads, key_rows, preferred_element_type=jnp.float32
                )
                * scale_factor
            )
            key_part = (
                jnp.einsum("hqk,qhd->khd", score_grads, queries, preferred_element_type=jnp.float32)
                * scale_factor
            )
            key_grad = lax.dynamic_update_slice_in_dim(
                key_grad, key_part.reshape(KEY_BLOCK, head_count * HS), first_key, 0
            )
            value_grad = lax.dynamic_update_slice_in_dim(
                value_grad, value_part.reshape(KEY_BLOCK, head_count * HS), first_key, 0
            )
            return (query_grad, key_grad, value_grad)

        return lax.cond(is_live, grad_update, keep_state, loop_state)

    start_grads = (
        jnp.zeros((span_rows, head_count, HS), jnp.float32),
        jnp.zeros((total_rows, head_count * HS), jnp.float32),
        jnp.zeros((total_rows, head_count * HS), jnp.float32),
    )
    query_grad, key_grad, value_grad = lax.fori_loop(0, block_count, grad_step, start_grads)
    key_own, value_own = (
        lax.psum_scatter(
            key_grad.astype(jnp.bfloat16), "blk", scatter_dimension=0, tiled=True
        ).astype(jnp.float32),
        lax.psum_scatter(
            value_grad.astype(jnp.bfloat16), "blk", scatter_dimension=0, tiled=True
        ).astype(jnp.float32),
    )
    query_tokens_grad, key_tokens_grad, value_tokens_grad = (
        lax.all_to_all(
            query_grad.reshape(span_rows, head_count * HS).astype(jnp.bfloat16),
            "head",
            split_axis=0,
            concat_axis=1,
            tiled=True,
        ),
        lax.all_to_all(
            key_own.astype(jnp.bfloat16), "head", split_axis=0, concat_axis=1, tiled=True
        ),
        lax.all_to_all(
            value_own.astype(jnp.bfloat16), "head", split_axis=0, concat_axis=1, tiled=True
        ),
    )
    qkv_grads = jnp.concatenate([query_tokens_grad, key_tokens_grad, value_tokens_grad], axis=1)
    d_qkv_weight = jnp.dot(normed_low.T, qkv_grads, preferred_element_type=jnp.float32)
    normed_grads = jnp.dot(qkv_grads, qkv_weight.T, preferred_element_type=jnp.float32)
    d_inputs_norm, d_gain_one = norm_one_pull(normed_grads)
    d_inputs = d_hidden_one + d_inputs_norm
    gain_one_sum, qkv_sum, out_sum, gain_two_sum, router_sum = (
        lax.psum_scatter(
            d_gain_one.astype(jnp.bfloat16), "blk", scatter_dimension=0, tiled=True
        ).astype(jnp.float32),
        lax.psum_scatter(
            d_qkv_weight.astype(jnp.bfloat16), "blk", scatter_dimension=0, tiled=True
        ).astype(jnp.float32),
        lax.psum_scatter(
            d_out_weight.astype(jnp.bfloat16), "blk", scatter_dimension=0, tiled=True
        ).astype(jnp.float32),
        lax.psum_scatter(
            d_gain_two.astype(jnp.bfloat16), "blk", scatter_dimension=0, tiled=True
        ).astype(jnp.float32),
        lax.psum_scatter(
            d_router.astype(jnp.bfloat16), "blk", scatter_dimension=0, tiled=True
        ).astype(jnp.float32),
    )
    gain_one_all, qkv_all, out_all, gain_two_all, router_all, expert_in_all, expert_out_all = (
        lax.psum(gain_one_sum.astype(jnp.bfloat16), "head").astype(jnp.float32),
        lax.psum(qkv_sum.astype(jnp.bfloat16), "head").astype(jnp.float32),
        lax.psum(out_sum.astype(jnp.bfloat16), "head").astype(jnp.float32),
        lax.psum(gain_two_sum.astype(jnp.bfloat16), "head").astype(jnp.float32),
        lax.psum(router_sum.astype(jnp.bfloat16), "head").astype(jnp.float32),
        lax.psum(d_weight_in[None].astype(jnp.bfloat16), "head").astype(jnp.float32),
        lax.psum(d_weight_out[None].astype(jnp.bfloat16), "head").astype(jnp.float32),
    )
    return (
        output,
        d_inputs,
        gain_one_all,
        qkv_all,
        out_all,
        gain_two_all,
        router_all,
        expert_in_all,
        expert_out_all,
    )


MESH = pl.DeviceIdType.MESH
LANES = 128
HALF = LANES // 2
MIB = 2**20
F32 = jnp.float32
BF16 = jnp.bfloat16


def dot(left, right, dims=(1, 0)):
    return lax.dot_general(
        left, right, (((dims[0],), (dims[1],)), ((), ())), preferred_element_type=F32
    )


def remote(src, dst, send_sem, recv_sem, head, blk):
    return pltpu.make_async_remote_copy(
        src_ref=src,
        dst_ref=dst,
        send_sem=send_sem,
        recv_sem=recv_sem,
        device_id={"head": head, "blk": blk},
        device_id_type=MESH,
    )


def arrived(ref, sem):
    pltpu.make_async_copy(ref, ref, sem).wait()


def greet(peers):
    barrier = pltpu.get_barrier_semaphore()
    for head, blk in peers:
        pl.semaphore_signal(
            barrier, inc=1, device_id={"head": head, "blk": blk}, device_id_type=MESH
        )
    return len(peers)


def meet(count):
    pl.semaphore_wait(pltpu.get_barrier_semaphore(), count)


def halves(values, lanes_kept):
    rows = values.shape[0] // 2
    moved = pltpu.roll(values[rows:], HALF, 1)
    return jnp.where(lanes_kept, values[:rows], moved)


def lane_ids(shape):
    return lax.broadcasted_iota(jnp.int32, shape, len(shape) - 1)


def centre(values):
    average = jnp.mean(values, axis=-1, keepdims=True)
    centred = values - average
    spread = jnp.mean(centred * centred, axis=-1, keepdims=True)
    scale = lax.rsqrt(spread + EPSILON)
    return centred * scale, scale


def centre_back(grad, xhat, scale):
    middle = jnp.mean(grad, axis=-1, keepdims=True)
    along = jnp.mean(grad * xhat, axis=-1, keepdims=True)
    return (grad - middle - xhat * along) * scale


def split_high_low(column, lanes):
    high = column.astype(BF16)
    low = (column - high.astype(F32)).astype(BF16)
    return jnp.where(lanes < HALF, high.astype(F32), low.astype(F32)).astype(BF16)


def join_high_low(matrix, start):
    return matrix[:, start : start + 1].astype(F32) + matrix[
        :, start + HALF : start + HALF + 1
    ].astype(F32)


def place():
    head, blk = lax.axis_index("head"), lax.axis_index("blk")
    return head, blk, blk // 2, lax.rem(blk, 2)


def around(index, step, size):
    return lax.rem(index + step, size)


QUERY_TILE = 256
CHAINS = 2


def masked_queries(q_ref, tile, key_lanes, query_tile):
    tiles_per_span = q_ref.shape[1] // query_tile
    inner = tile % tiles_per_span * query_tile
    query = q_ref[tile // tiles_per_span, inner : inner + query_tile, :]
    return jnp.where(key_lanes, query, jnp.zeros_like(query))


def group_blocks(bounds_ref, group, size, key_tile):
    first, last = group * size, (group + 1) * size
    low = jnp.min(bounds_ref[0:1, first : first + LANES])
    high = jnp.max(bounds_ref[1:2, last - LANES : last])
    return low // key_tile, (high + key_tile - 1) // key_tile


def inside_document(bounds_ref, tile, first, shape):
    key = first + lax.broadcasted_iota(jnp.int32, shape, 0)
    columns = slice(tile * shape[1], (tile + 1) * shape[1])
    return jnp.logical_and(key >= bounds_ref[0:1, columns], key < bounds_ref[1:2, columns])


def query_group(q_ref, group, y):
    key_lanes = (lane_ids((QUERY_TILE, LANES)) < HALF) == (y == 0)
    tiles = range(group * CHAINS, (group + 1) * CHAINS)
    return tiles, [masked_queries(q_ref, tile, key_lanes, QUERY_TILE) for tile in tiles]


def attend(bounds_ref, tiles, first, keys, keys_across, queries, carry):
    scores = [dot(keys, query, (1, 1)) for query in queries]
    made = []
    for tile, score, (biggest, weight, mixed) in zip(tiles, scores, carry):
        inside = inside_document(bounds_ref, tile, first, score.shape)
        score = jnp.where(inside, score, MASKED)
        bigger = jnp.maximum(biggest, jnp.max(score, axis=0, keepdims=True))
        fade = jnp.exp(biggest - bigger)
        terms = jnp.exp(score - bigger)
        weight = weight * fade + jnp.sum(terms, axis=0, keepdims=True)
        made.append((bigger, weight, mixed * fade + dot(keys_across, terms.astype(BF16))))
    return tuple(made)


def nothing_attended():
    return (
        jnp.full((1, QUERY_TILE), MASKED, F32),
        jnp.zeros((1, QUERY_TILE), F32),
        jnp.zeros((LANES, QUERY_TILE), F32),
    )


def attend_back(bounds_ref, tiles, first, keys, keys_across, group, carry):
    queries, out_grads, deltas, log_totals = group
    scores = [dot(keys, query, (1, 1)) for query in queries]
    weight_grads = [dot(keys, out_grad, (1, 1)) for out_grad in out_grads]
    pieces, score_grads = [], []
    for i, tile in enumerate(tiles):
        inside = inside_document(bounds_ref, tile, first, scores[i].shape)
        weights = jnp.exp(jnp.where(inside, scores[i], MASKED) - log_totals[i])
        score_grads.append((weights * (weight_grads[i] - deltas[i])).astype(BF16))
        pieces.append(weights.astype(BF16))
    wide = jnp.concatenate(score_grads + pieces, axis=1)
    given = dot(wide, jnp.concatenate(queries + out_grads, axis=0))
    return given, tuple(c + dot(keys_across, g) for c, g in zip(carry, score_grads))


def group_grads(do_ref, tiles, y):
    key_lanes = (lane_ids((QUERY_TILE, LANES)) < HALF) == (y == 0)
    out_grads = []
    for tile in tiles:
        parts = []
        for part in range(QUERY_TILE // LANES):
            packed = do_ref[tile, part].astype(F32)
            parts += [packed, pltpu.roll(packed, HALF, 1)]
        out_grads.append(jnp.where(key_lanes, 0.0, jnp.concatenate(parts, axis=0)).astype(BF16))
    return out_grads


def qkv_kernel(
    heads, blks,
    x_hbm, w_hbm, g1_hbm, wo_hbm, wr_hbm, g2_hbm, docs_hbm,
    qall, kvall, xall, wall, wo_all, kvt, bounds, begun,
    x_ref, w_ref, rows_in, g1_ref, g2_ref, wr_ref, docs_ref, wo_own, kv_other, q_packed, q_landed, in_sem,
    x_send, x_recv, w_send, w_recv, o_send, o_recv, p_send, p_recv,
    k_send, k_recv, q_recv,
):
    head, blk, z, y = place()
    planes = blks // 2
    model = x_ref.shape[1]
    rows = w_ref.shape[0]
    part = rows // heads
    experts = wr_ref.shape[0]
    wanted = (
        (w_hbm, w_ref), (g1_hbm, g1_ref), (g2_hbm, g2_ref), (wr_hbm, wr_ref), (x_hbm, x_ref),
        (wo_hbm, wo_own.at[:, pl.ds(0, model)]), (docs_hbm, docs_ref),
    )
    fetched = [
        pltpu.make_async_copy(src, dst, in_sem.at[i]) for i, (src, dst) in enumerate(wanted)
    ]
    for copy in fetched:
        copy.start()
    rows_in[...] = jnp.zeros_like(rows_in)
    met = greet(
        [(around(head, k, heads), blk) for k in range(1, heads)]
        + [(head, around(blk, k, blks)) for k in range(1, blks)]
    )
    lanes = lane_ids((rows, LANES))
    for copy in fetched:
        copy.wait()
    rows_in[0:experts, 0:rows] = wr_ref[...].astype(F32)
    rows_in[experts : experts + 1, 0:rows] = g2_ref[...].astype(F32)
    rows_in[experts + 1 : experts + 2, 0:rows] = g1_ref[...].astype(F32)
    vectors = jnp.transpose(rows_in[...])[:rows]
    gain = vectors[:, experts + 1 : experts + 2]

    def columns(which):
        start = pl.multiple_of(which * model + head * LANES, LANES)
        return w_ref[:, pl.ds(start, LANES)].astype(F32) * gain

    key_cols = columns(1)
    value_cols = pltpu.roll(columns(2), HALF, 1)
    wall[blk, :, 0:LANES] = jnp.where(lanes < HALF, key_cols, value_cols).astype(BF16)
    wall[blk, :, LANES : 2 * LANES] = jnp.where(lanes < HALF, value_cols, key_cols).astype(BF16)
    wall[blk, :, 2 * LANES : 3 * LANES] = (columns(0) * HS ** (-0.5)).astype(BF16)
    w_copies = [
        remote(wall.at[blk], wall.at[blk], w_send.at[k], w_recv.at[k], head, around(blk, k, blks))
        for k in range(1, blks)
    ]
    xhat, _ = centre(x_ref[...].astype(F32))
    xall[head] = xhat.astype(BF16)
    meet(met)
    for copy in w_copies:
        copy.start()
    x_copies = [
        remote(xall.at[head], xall.at[head], x_send.at[k], x_recv.at[k], around(head, k, heads), blk)
        for k in range(1, heads)
    ]
    for copy in x_copies:
        copy.start()
    wo_own[:, model : model + LANES] = vectors.astype(BF16)
    wo_all[blk, head] = wo_own[pl.ds(pl.multiple_of(head * part, part), part), :]
    o_copies = [
        remote(
            wo_all.at[blk, head], wo_all.at[blk, head],
            o_send.at[k], o_recv.at[k], head, around(blk, k, blks),
        )
        for k in range(1, blks)
    ]
    document_bounds(docs_ref, bounds, z)
    for copy in w_copies:
        copy.wait_send()
    for copy in o_copies:
        copy.start()
    for copy in x_copies:
        copy.wait()
    for copy in w_copies:
        copy.wait_recv()
    weight = wall[...].reshape(model, 3 * LANES)
    tokens = x_ref.shape[0]
    even = y == 0
    above, below = z < planes - 1, z > 0
    half_span = kvall.shape[1] // 2
    sides = ((1, above, below, 0), (-1, below, above, 4))

    def half_of(ref, half):
        return ref.at[pl.ds(half * half_span, half_span)]

    def outward(slot, step, across, half):
        target = 2 * (z + step) + around(y, across, 2)
        return remote(
            half_of(kv_other if across else kvall.at[blk], half), half_of(kvall.at[blk], half),
            k_send.at[slot], k_recv.at[blk, half], head, target,
        )

    def onward(slot, step, side, half):
        from_span = 2 * (z - step) + side
        ref = half_of(kvall.at[from_span], half)
        return remote(ref, ref, k_send.at[slot], k_recv.at[from_span, half], head, 2 * (z + step) + y)

    def await_half(span, half):
        arrived(half_of(kvall.at[span], half), k_recv.at[span, half])

    def turn(span):
        size = kvall.shape[1]
        kvt[:, pl.ds(pl.multiple_of(span * size, size), size)] = jnp.transpose(kvall[span])

    for half in range(2):
        for piece in range(half * heads // 2, (half + 1) * heads // 2):
            made = dot(xall[piece], weight).astype(BF16)
            first, second = made[:, 0:LANES], made[:, LANES : 2 * LANES]
            span = slice(piece * tokens, (piece + 1) * tokens)
            kvall[blk, span, :] = jnp.where(even, first, second)
            kv_other[span, :] = jnp.where(even, second, first)
            qall[y, span, :] = made[:, 2 * LANES : 3 * LANES]
        outward(8 + half, 0, 1, half).start()
        for step, there, _, slot in sides:

            @pl.when(there)
            def _():
                outward(slot + 2 * half, step, 0, half).start()
                outward(slot + 2 * half + 1, step, 1, half).start()

    other_y = around(y, 1, 2)
    kept = (lane_ids(q_packed.shape) < HALF) == (y == 1)
    q_packed[...] = halves(qall[y].astype(F32), kept).astype(BF16)
    q_pair = remote(q_packed, q_landed, k_send.at[10], q_recv, head, 2 * z + other_y)
    q_pair.start()
    turn(blk)
    for copy in o_copies:
        copy.wait()
    core = lax.rem(head, 2)
    sibling, across = head - core + 1 - core, around(head, 2, heads)

    def quarter_copy(index, quarter, to_head):
        ref = wo_all.at[:, quarter]
        return remote(ref, ref, p_send.at[index], p_recv.at[index], to_head, blk)

    p_copies = [quarter_copy(0, head, sibling), quarter_copy(1, head, across)]
    for copy in p_copies:
        copy.start()
    p_copies.append(quarter_copy(2, across, sibling))
    for half in range(2):
        for step, there, back, slot in sides:

            @pl.when(back)
            def _():
                for side in range(2):
                    await_half(2 * (z - step) + side, half)

            @pl.when(jnp.logical_and(there, back))
            def _():
                for side in range(2):
                    onward(11 + slot + 2 * half + side, step, side, half).start()

    arrived(wo_all.at[:, across], p_recv.at[1])
    p_copies[2].start()
    pair = 2 * z + other_y
    for half in range(2):
        await_half(pair, half)
    turn(pair)
    q_pair.wait()
    landed = q_landed[...]
    qall[other_y, 0:half_span, :] = landed
    qall[other_y, half_span : 2 * half_span, :] = pltpu.roll(landed.astype(F32), HALF, 1).astype(BF16)
    key_tile = kvall.shape[1]
    for group in range(2 * key_tile // (CHAINS * QUERY_TILE)):
        tiles, queries = query_group(qall, group, y)
        carry = (nothing_attended(),) * CHAINS
        for side in range(2):
            first = pl.multiple_of((2 * z + side) * key_tile, key_tile)
            keys_across = kvt[:, pl.ds(first, key_tile)]
            carry = attend(bounds, tiles, first, kvall[2 * z + side], keys_across, queries, carry)
        for tile, (biggest, weight, mixed) in zip(tiles, carry):
            begun[tile, 0:LANES] = mixed
            begun[tile, LANES : LANES + 8] = jnp.broadcast_to(biggest, (8, QUERY_TILE))
            begun[tile, LANES + 8 : LANES + 16] = jnp.broadcast_to(weight, (8, QUERY_TILE))
    for step, there, back, slot in sides:

        @pl.when(back)
        def _():
            for side in range(2):
                turn(2 * (z - step) + side)

    for other in range(planes):
        for side in range(2):
            span = 2 * other + side

            @pl.when(jnp.logical_or(z - other == 2, other - z == 2))
            def _():
                for half in range(2):
                    await_half(span, half)
                turn(span)

    for index, quarter in ((0, sibling), (2, around(sibling, 2, heads))):
        arrived(wo_all.at[:, quarter], p_recv.at[index])
    for copy in p_copies:
        copy.wait_send()
    for half in range(2):
        outward(8 + half, 0, 1, half).wait_send()
        for step, there, back, slot in sides:

            @pl.when(there)
            def _():
                outward(slot + 2 * half, step, 0, half).wait_send()
                outward(slot + 2 * half + 1, step, 1, half).wait_send()

            @pl.when(jnp.logical_and(there, back))
            def _():
                for side in range(2):
                    onward(11 + slot + 2 * half + side, step, side, half).wait_send()


def document_bounds(docs_ref, bounds, z):
    count = docs_ref.shape[1]
    lengths = docs_ref[...].astype(F32)
    doc = lax.broadcasted_iota(jnp.int32, (count, count), 0)
    other = lane_ids((count, count))
    start = jnp.sum(jnp.where(other < doc, lengths, 0.0), axis=1, keepdims=True)
    end = jnp.sum(jnp.where(other <= doc, lengths, 0.0), axis=1, keepdims=True)
    queries = bounds.shape[1]
    token = (z * queries + lane_ids((count, queries))).astype(F32)
    begun = start <= token
    bounds[...] = jnp.zeros_like(bounds)
    bounds[0:1, :] = jnp.max(jnp.where(begun, start, 0.0), axis=0, keepdims=True).astype(jnp.int32)
    bounds[1:2, :] = jnp.max(jnp.where(begun, end, 0.0), axis=0, keepdims=True).astype(jnp.int32)


def vmem_specs(count):
    return [pl.BlockSpec(memory_space=pltpu.VMEM)] * count


def hbm_specs(count):
    return [pl.BlockSpec(memory_space=pltpu.HBM)] * count


def in_hbm(*arrays):
    return [pltpu.with_memory_space_constraint(array, pltpu.HBM) for array in arrays]


def dma(*shape):
    return pltpu.SemaphoreType.DMA(shape)


def call_qkv(x, w_qkv, g1, w_out, w_router, g2, doc_lengths, heads, blks):
    tokens, model = x.shape
    rows = w_qkv.shape[0]
    span = tokens * heads
    wide = model + LANES
    part = rows // heads
    return pl.pallas_call(
        functools.partial(qkv_kernel, heads, blks),
        out_shape=(
            jax.ShapeDtypeStruct((2, span, LANES), BF16),
            jax.ShapeDtypeStruct((blks, span, LANES), BF16),
            jax.ShapeDtypeStruct((heads, tokens, model), BF16),
            jax.ShapeDtypeStruct((blks, rows, 3 * LANES), BF16),
            jax.ShapeDtypeStruct((blks, heads, part, wide), BF16),
            jax.ShapeDtypeStruct((LANES, blks * span), BF16),
            jax.ShapeDtypeStruct((8, 2 * span), jnp.int32),
            jax.ShapeDtypeStruct((2 * span // QUERY_TILE, LANES + 16, QUERY_TILE), F32),
        ),
        in_specs=hbm_specs(7),
        out_specs=tuple(vmem_specs(8)),
        scratch_shapes=[
            pltpu.VMEM((tokens, model), BF16),
            pltpu.VMEM((rows, 3 * model), BF16),
            pltpu.VMEM((LANES, LANES), F32),
            pltpu.VMEM((1, rows), BF16),
            pltpu.VMEM((1, rows), BF16),
            pltpu.VMEM((w_router.shape[1], rows), BF16),
            pltpu.VMEM((1, doc_lengths.shape[0]), jnp.int32),
            pltpu.VMEM((rows, wide), BF16),
            pltpu.VMEM((span, LANES), BF16),
            pltpu.VMEM((span // 2, LANES), BF16),
            pltpu.VMEM((span // 2, LANES), BF16),
            dma(7),
            dma(heads), dma(heads), dma(blks), dma(blks), dma(blks), dma(blks), dma(heads), dma(heads),
            dma(19), dma(blks, 2), pltpu.SemaphoreType.DMA,
        ],
        compiler_params=pltpu.CompilerParams(
            collective_id=1, has_side_effects=True, vmem_limit_bytes=16 * MIB
        ),
        name="qkv",
    )(
        *in_hbm(
            x, w_qkv, g1.reshape(1, rows), w_out, w_router.T, g2.reshape(1, rows),
            doc_lengths.reshape(1, -1),
        )
    )


def other_blocks(bounds_ref, group, key_tile, z, step, carry):
    low, high = group_blocks(bounds_ref, group, CHAINS * QUERY_TILE, key_tile)
    carry = lax.fori_loop(low, 2 * z, step, carry)
    return lax.fori_loop(2 * z + 2, high, step, carry)


def forward_kernel(bounds_ref, q_ref, kv_ref, kvt_ref, begun_ref, o_out, ob_out, lse_out):
    _, _, z, y = place()
    key_tile = kv_ref.shape[1]
    value_lanes = (lane_ids((HALF, LANES)) < HALF) == (y == 1)
    for group in range(q_ref.shape[0] * q_ref.shape[1] // (CHAINS * QUERY_TILE)):
        tiles, queries = query_group(q_ref, group, y)

        def step(block, carry, queries=queries, tiles=tiles):
            first = pl.multiple_of(block * key_tile, key_tile)
            across = kvt_ref[:, pl.ds(first, key_tile)]
            return attend(bounds_ref, tiles, first, kv_ref[block], across, queries, carry)

        start = tuple(
            (begun_ref[t, LANES : LANES + 1], begun_ref[t, LANES + 8 : LANES + 9], begun_ref[t, 0:LANES])
            for t in tiles
        )
        ends = other_blocks(bounds_ref, group, key_tile, z, step, start)
        for tile, (biggest, weight, mixed) in zip(tiles, ends):
            result = jnp.transpose(mixed / weight)
            o_out[tile] = result
            for part in range(QUERY_TILE // LANES):
                block = result[part * LANES : (part + 1) * LANES]
                ob_out[tile, part] = halves(block, value_lanes).astype(BF16)
            lse_out[tile] = jnp.broadcast_to(biggest + jnp.log(weight), (8, QUERY_TILE))


def call_forward(bounds, q, kv, kvt, begun):
    blks, span, _ = kv.shape
    tiles = 2 * span // QUERY_TILE
    return pl.pallas_call(
        forward_kernel,
        out_shape=(
            jax.ShapeDtypeStruct((tiles, QUERY_TILE, LANES), F32),
            jax.ShapeDtypeStruct((tiles, QUERY_TILE // LANES, HALF, LANES), BF16),
            jax.ShapeDtypeStruct((tiles, 8, QUERY_TILE), F32),
        ),
        in_specs=vmem_specs(5),
        out_specs=tuple(vmem_specs(3)),
        compiler_params=pltpu.CompilerParams(vmem_limit_bytes=16 * MIB),
        name="attend",
    )(bounds, q, kv, kvt, begun)


def backward_kernel(
    bounds_ref, q_ref, kv_ref, kvt_ref, do_ref, o_ref, lse_ref, dq_out, dkv_out, delta_out, dkv
):
    _, _, z, y = place()
    key_tile = kv_ref.shape[1]
    dkv[...] = jnp.zeros_like(dkv)
    for group in range(q_ref.shape[0] * q_ref.shape[1] // (CHAINS * QUERY_TILE)):
        tiles, queries = query_group(q_ref, group, y)
        out_grads = group_grads(do_ref, tiles, y)
        deltas, log_totals = [], []
        for tile, out_grad in zip(tiles, out_grads):
            product = jnp.transpose(out_grad.astype(F32) * o_ref[tile])
            deltas.append(jnp.sum(product, axis=0, keepdims=True))
            delta_out[tile] = jnp.broadcast_to(deltas[-1], delta_out.shape[1:])
            log_totals.append(lse_ref[tile, 0:1, :])
        known = (queries, out_grads, deltas, log_totals)

        def step(block, carry, tiles=tiles, known=known):
            first = pl.multiple_of(block * key_tile, key_tile)
            across = kvt_ref[:, pl.ds(first, key_tile)]
            given, carry = attend_back(bounds_ref, tiles, first, kv_ref[block], across, known, carry)
            dkv[block] += given
            return carry

        zero = jnp.zeros((LANES, QUERY_TILE), F32)
        ends = other_blocks(bounds_ref, group, key_tile, z, step, (zero,) * CHAINS)
        for tile, mixed in zip(tiles, ends):
            dq_out[tile] = mixed
    for block in range(dkv.shape[0]):
        dkv_out[block] = dkv[block].astype(BF16)


def call_backward(bounds, q, kv, kvt, d_o, o, lse):
    blks, span, _ = kv.shape
    tiles = 2 * span // QUERY_TILE
    return pl.pallas_call(
        backward_kernel,
        out_shape=(
            jax.ShapeDtypeStruct((tiles, LANES, QUERY_TILE), F32),
            jax.ShapeDtypeStruct((blks, span, LANES), BF16),
            jax.ShapeDtypeStruct((tiles, 8, QUERY_TILE), F32),
        ),
        in_specs=vmem_specs(7),
        out_specs=tuple(vmem_specs(3)),
        scratch_shapes=[pltpu.VMEM((blks, span, LANES), F32)],
        compiler_params=pltpu.CompilerParams(vmem_limit_bytes=16 * MIB),
        name="attend_back",
    )(bounds, q, kv, kvt, d_o, o, lse)


def gelu_parts(values):
    share = 0.5 * (1.0 + lax.erf(values * (2.0**-0.5)))
    slope = share + values * jnp.exp(-0.5 * values * values) * (2.0 * math.pi) ** -0.5
    return values * share, slope


def positions(expert_rows, expert_cols, rank_row, rank_col):
    def count(mask, axis):
        return jnp.sum(mask.astype(F32), axis=axis, keepdims=True)

    row = [None, None]
    col = [None, None]
    before = rank_col < rank_row
    after = rank_row < rank_col
    for choice in range(2):
        row[choice] = count((expert_cols[choice] == expert_rows[choice]) & before, 0)
        col[choice] = count((expert_rows[choice] == expert_cols[choice]) & after, 1)
    row[1] = row[1] + count(expert_cols[0] == expert_rows[1], 0)
    col[1] = col[1] + count(expert_rows[0] == expert_cols[1], 1)
    return row, col


def own_columns(rows_ref, turned, blk, capacity):
    blks, _, slots = rows_ref.shape
    rows = jnp.concatenate(
        [rows_ref[...].reshape(blks, slots), jnp.zeros((LANES - blks, slots), F32)], axis=0
    )
    for piece in range(slots // LANES):
        columns = slice(piece * LANES, (piece + 1) * LANES)
        turned[columns, :] = jnp.transpose(rows[:, columns])
    own = turned[pl.ds(pl.multiple_of(blk * capacity, capacity), capacity), :]
    return jnp.concatenate([own[:, source : source + 1] for source in range(blks)], axis=0)


def middle_kernel(
    heads, blks,
    x_hbm, o_ref, wo_ref, routes_hbm, rank_hbm, d_out_hbm, win_hbm, wout_hbm,
    po, hidden_ref, share_ref, dh_ref, dma_all, grads_ref, rx,
    x_ref, routes_ref, rank_ref, d_out_ref, win_ref, wout_ref, rows_in, in_sem,
    o_all, dos, doa, rs, ra, dr, da, dms, acc_out, acc_row, mix, gate_rows, d_gate_rows, turned,
    o_send, o_recv, dos_send, dos_recv, r_send, r_recv,
    dr_send, dr_recv, dm_send, dm_recv, rx_send, rx_recv, g_send, g_recv, dg_send, dg_recv,
):
    head, blk, z, y = place()
    tokens, model = x_ref.shape
    capacity = 2 * tokens // blks
    slots = capacity * blks
    plane = [(k % heads, k // heads) for k in range(1, 2 * heads)]
    wanted = (
        (routes_hbm, routes_ref), (rank_hbm, rank_ref), (d_out_hbm, d_out_ref), (x_hbm, x_ref),
        (win_hbm, win_ref), (wout_hbm, wout_ref),
    )
    fetched = [
        pltpu.make_async_copy(src, dst, in_sem.at[i]) for i, (src, dst) in enumerate(wanted)
    ]
    for copy in fetched:
        copy.start()
    met = greet(
        [(around(head, kh, heads), 2 * z + around(y, ky, 2)) for kh, ky in plane]
        + [(head, around(blk, k, blks)) for k in range(1, blks)]
    )
    meet(met)

    def plane_copies(src_of, dst, send, recv):
        copies = []
        for k, (kh, ky) in enumerate(plane):
            to_head, to_y = around(head, kh, heads), around(y, ky, 2)
            copies.append(
                remote(src_of(to_y, to_head), dst, send.at[k], recv.at[k], to_head, 2 * z + to_y)
            )
        return copies

    def blk_copies(src, dst, send, recv):
        return [
            remote(
                src.at[around(blk, k, blks)], dst.at[blk],
                send.at[k], recv.at[k], head, around(blk, k, blks),
            )
            for k in range(1, blks)
        ]

    def start(copies):
        for copy in copies:
            copy.start()

    def finish(copies):
        for copy in copies:
            copy.wait()

    o_copies = plane_copies(lambda to_y, to_head: o_ref.at[to_y, to_head], o_all.at[y, head], o_send, o_recv)
    start(o_copies)
    o_all[y, head] = o_ref[y, head]

    lanes = lane_ids((tokens, LANES))
    for copy in fetched[:4]:
        copy.wait()
    e_rows = [routes_ref[i : i + 1, :].astype(F32) for i in range(2)]
    rank_row = rank_ref[...].astype(F32)
    rows_in[...] = jnp.zeros_like(rows_in)
    rows_in[0:1, :], rows_in[1:2, :], rows_in[2:3, :] = *e_rows, rank_row
    columns = jnp.transpose(rows_in[...])
    e_cols = [columns[:, 0:1], columns[:, 1:2]]
    rank_col = columns[:, 2:3]
    pos_rows, pos_cols = positions(e_rows, e_cols, rank_row, rank_col)

    def slot_of(expert, position):
        return jnp.where(position < capacity, expert * capacity + position, -1.0).astype(jnp.int32)

    slot_rows = [slot_of(e, p) for e, p in zip(e_rows, pos_rows)]
    slot_cols = [slot_of(e, p) for e, p in zip(e_cols, pos_cols)]
    slot_down = lax.broadcasted_iota(jnp.int32, (slots, tokens), 0)
    slot_across = lane_ids((tokens, slots))
    pick = [(slot_down == s).astype(BF16) for s in slot_rows]
    put = [(slot_across == s).astype(BF16) for s in slot_cols]
    pick_any = pick[0] + pick[1]
    put_any = put[0] + put[1]

    d_out = d_out_ref[...]
    dos[...] = dot(pick_any, d_out.astype(BF16)).astype(BF16).reshape(dos.shape)
    dos_copies = blk_copies(dos, doa, dos_send, dos_recv)
    start(dos_copies)
    doa[blk] = dos[blk]

    weight_out = jnp.concatenate(
        [wo_ref[(b ^ 1) * HALF : ((b ^ 1) + 1) * HALF, 0:model] for b in range(blks)], axis=0
    )
    small = wo_ref[:, model : model + LANES]
    small_across = jnp.concatenate(
        [
            jnp.transpose(small[i * LANES : (i + 1) * LANES].astype(F32))
            for i in range(model // LANES)
        ],
        axis=1,
    )
    gain = small_across[blks : blks + 1, :]

    finish(o_copies)
    low_lanes = lanes[:HALF] < HALF
    for piece in range(heads):
        columns = slice(piece * LANES, (piece + 1) * LANES)
        first, second = o_all[1, piece].astype(F32), o_all[0, piece].astype(F32)
        mix[:HALF, columns] = jnp.where(low_lanes, first, second).astype(BF16)
        swapped = pltpu.roll(jnp.where(low_lanes, second, first), HALF, 1)
        mix[HALF:, columns] = swapped.astype(BF16)
    mixed = mix[...]
    hidden = x_ref[...].astype(F32) + dot(mixed, weight_out)
    xhat, scale = centre(hidden)
    routed = (xhat * gain).astype(BF16)
    rs[...] = dot(pick_any, routed).astype(BF16).reshape(rs.shape)
    r_copies = blk_copies(rs, ra, r_send, r_recv)
    start(r_copies)
    ra[blk] = rs[blk]
    logits = jnp.where(lanes < blks, dot(routed, small), MASKED)
    powers = jnp.exp(logits - jnp.max(logits, axis=1, keepdims=True))
    probs = powers / jnp.sum(powers, axis=1, keepdims=True)
    lanes_f = lanes.astype(F32)
    hots = [lanes_f == e for e in e_cols]
    gates = [jnp.sum(jnp.where(hot, probs, 0.0), axis=1, keepdims=True) for hot in hots]
    gate_high = [g.astype(BF16).astype(F32) for g in gates]
    gate_across = jnp.transpose(
        jnp.where(lanes == 0, gate_high[0], jnp.where(lanes == 1, gates[0] - gate_high[0], 0.0))
        + jnp.where(lanes == 2, gate_high[1], jnp.where(lanes == 3, gates[1] - gate_high[1], 0.0))
    ).astype(BF16)
    by_slot = (dot(gate_across, put[0]), dot(gate_across, put[1]))
    gate_rows[blk] = by_slot[0][0:1] + by_slot[0][1:2] + by_slot[1][2:3] + by_slot[1][3:4]
    g_copies = [
        remote(
            gate_rows.at[blk], gate_rows.at[blk],
            g_send.at[k], g_recv.at[k], head, around(blk, k, blks),
        )
        for k in range(1, blks)
    ]
    start(g_copies)
    acc_out[...] = jnp.zeros_like(acc_out)
    acc_row[...] = jnp.zeros_like(acc_row)
    finish(dos_copies)
    finish(r_copies)

    out_rows = doa[...].reshape(slots, model)
    rx[head, :, 0:model] = ra[...].reshape(slots, model)
    finish(g_copies)
    gate_col = own_columns(gate_rows, turned, blk, capacity)
    rx[head, :, model : 2 * model] = (out_rows.astype(F32) * gate_col).astype(BF16)
    core = lax.rem(head, 2)
    sibling, across = head - core + 1 - core, around(head, 2, heads)

    def half_rows(source, half):
        return rx.at[source, pl.ds(half * slots // 2, slots // 2)]

    to_across = [
        remote(
            half_rows(head, half), half_rows(head, half),
            rx_send.at[1 + half], rx_recv.at[1 + half], across, blk,
        )
        for half in range(2)
    ]
    to_sibling = remote(rx.at[head], rx.at[head], rx_send.at[0], rx_recv.at[0], sibling, blk)
    forwards = [
        remote(
            half_rows(across, half), half_rows(across, half),
            rx_send.at[3 + half], rx_recv.at[3 + half], sibling, blk,
        )
        for half in range(2)
    ]
    start(to_across)
    to_sibling.start()
    half_ff = wout_ref.shape[0] // 4
    for copy in fetched[4:]:
        copy.wait()

    @pl.loop(0, 4)
    def _(chunk):
        first = pl.multiple_of(chunk * half_ff, half_ff)
        into = win_ref[:, pl.ds(first, half_ff)]
        outof = wout_ref[pl.ds(first, half_ff), :]
        act, slope = gelu_parts(dot(rx[head, :, 0:model], into))
        acc_out[...] += dot(act.astype(BF16), outof)
        d_act = dot(rx[head, :, model : 2 * model], outof, (1, 1))
        acc_row[...] += dot((slope * d_act).astype(BF16), into, (1, 1))

    result = acc_out[...].astype(BF16)
    d_gate = jnp.sum(out_rows.astype(F32) * result.astype(F32), axis=1, keepdims=True)
    dr[...] = acc_row[...].astype(BF16).reshape(dr.shape)
    dr_copies = blk_copies(dr, da, dr_send, dr_recv)
    start(dr_copies)
    da[blk] = dr[blk]
    d_wide = jnp.broadcast_to(d_gate, (slots, LANES))
    d_gate_rows[blk] = jnp.concatenate(
        [jnp.transpose(d_wide[i * LANES : (i + 1) * LANES])[0:1] for i in range(slots // LANES)],
        axis=1,
    )
    dg_copies = [
        remote(
            d_gate_rows.at[blk], d_gate_rows.at[blk],
            dg_send.at[k], dg_recv.at[k], head, around(blk, k, blks),
        )
        for k in range(1, blks)
    ]
    start(dg_copies)
    po[...] = result.reshape(blks, capacity, model)

    finish(dg_copies)
    back_gate = own_columns(d_gate_rows, turned, blk, capacity)
    back_gate = split_high_low(back_gate, lane_ids((slots, LANES)))
    d_gates = [join_high_low(dot(p, back_gate), 0) for p in put]
    d_probs = jnp.where(hots[0], d_gates[0], 0.0) + jnp.where(hots[1], d_gates[1], 0.0)
    d_logits = probs * (d_probs - jnp.sum(probs * d_probs, axis=1, keepdims=True))
    d_high = d_logits.astype(BF16)
    d_low = (d_logits - d_high.astype(F32)).astype(BF16)
    d_router_part = dot(d_high, small, (1, 1)) + dot(d_low, small, (1, 1))
    finish(dr_copies)
    d_routed = dot(put_any, da[...].reshape(slots, model)) + d_router_part
    d_hidden = d_out + centre_back(d_routed * gain, xhat, scale)
    dh_ref[...] = d_hidden
    d_attn = d_hidden.astype(BF16)
    d_mixed = dot(d_attn, weight_out, (1, 1))
    for piece in range(heads):
        block = d_mixed[:, piece * LANES : (piece + 1) * LANES]
        for to_y in range(2):
            dms[to_y, piece] = halves(block, low_lanes == (to_y == 1)).astype(BF16)
    dm_copies = plane_copies(lambda to_y, to_head: dms.at[to_y, to_head], dma_all.at[y, head], dm_send, dm_recv)
    start(dm_copies)
    dma_all[y, head] = dms[y, head]
    arrived(half_rows(across, 0), rx_recv.at[1])
    forwards[0].start()

    d_weight = dot(mixed, d_attn, (0, 0)).astype(BF16)
    for b in range(blks):
        grads_ref[b, :, 0:model] = d_weight[(b ^ 1) * HALF : ((b ^ 1) + 1) * HALF, :]
    last = (lanes == blks).astype(BF16)
    d_small = dot(routed, d_high, (0, 0)) + dot((d_routed * xhat).astype(BF16), last, (0, 0))
    grads_ref[:, :, model : model + LANES] = d_small.astype(BF16).reshape(blks, HALF, LANES)
    share = gates[0] * put[0].astype(F32) + gates[1] * put[1].astype(F32)
    share_ref[0] = share.astype(BF16)
    share_ref[1] = (share - share_ref[0].astype(F32)).astype(BF16)
    hidden_ref[...] = hidden

    arrived(half_rows(across, 1), rx_recv.at[2])
    forwards[1].start()
    finish(dm_copies)
    to_sibling.wait()
    for copy in to_across:
        copy.wait_send()
    finish(forwards)


def call_middle(x, o, wo, routes, rank, d_out, win, wout, heads, blks):
    tokens, model = x.shape
    capacity = 2 * tokens // blks
    slots = capacity * blks
    wide = model + LANES

    def rows(width):
        return pltpu.VMEM((blks, capacity, width), BF16)

    def block(*lead):
        return pltpu.VMEM((*lead, tokens // 2, LANES), BF16)

    return pl.pallas_call(
        functools.partial(middle_kernel, heads, blks),
        out_shape=(
            jax.ShapeDtypeStruct((blks, capacity, model), BF16),
            jax.ShapeDtypeStruct((tokens, model), F32),
            jax.ShapeDtypeStruct((2, tokens, slots), BF16),
            jax.ShapeDtypeStruct((tokens, model), F32),
            jax.ShapeDtypeStruct((2, heads, tokens // 2, LANES), BF16),
            jax.ShapeDtypeStruct((blks, model // blks, wide), BF16),
            jax.ShapeDtypeStruct((heads, slots, 2 * model), BF16),
        ),
        in_specs=hbm_specs(1) + vmem_specs(2) + hbm_specs(5),
        out_specs=tuple(vmem_specs(7)),
        scratch_shapes=[
            pltpu.VMEM((tokens, model), BF16),
            pltpu.VMEM((2, tokens), jnp.int32),
            pltpu.VMEM((1, tokens), jnp.int32),
            pltpu.VMEM((tokens, model), F32),
            pltpu.VMEM(win.shape, BF16),
            pltpu.VMEM(wout.shape, BF16),
            pltpu.VMEM((tokens, tokens), F32),
            dma(6),
            block(2, heads), rows(model), rows(model), rows(model), rows(model),
            rows(model), rows(model), block(2, heads),
            pltpu.VMEM((slots, model), F32), pltpu.VMEM((slots, model), F32),
            pltpu.VMEM((tokens, model), BF16),
            pltpu.VMEM((blks, 1, slots), F32), pltpu.VMEM((blks, 1, slots), F32),
            pltpu.VMEM((slots, LANES), F32),
            dma(2 * heads), dma(2 * heads), dma(blks), dma(blks), dma(blks), dma(blks),
            dma(blks), dma(blks), dma(2 * heads), dma(2 * heads), dma(5), dma(5),
            dma(blks), dma(blks), dma(blks), dma(blks),
        ],
        compiler_params=pltpu.CompilerParams(
            collective_id=2, has_side_effects=True, vmem_limit_bytes=20 * MIB
        ),
        name="experts",
    )(*in_hbm(x), o, wo, *in_hbm(routes.T, rank, d_out, win, wout))


def last_kernel(
    heads, blks,
    x_hbm, dh_ref, begun_ref, dkv_ref, xa_ref, wa_ref, w_hbm, g1_hbm, grads_ref, rx_ref, win_hbm, wout_hbm,
    po_ref, hidden_ref, share_ref, bounds_ref, q_ref, kv_ref, kvt_ref, do_ref, lse_ref, delta_ref,
    y_ref, dx_ref, dw_ref, shared_ref, din_ref, dout_ref,
    x_ref, w_ref, g1_ref, win_ref, wout_ref, in_sem,
    gain_tile, far_all, near_send_buf, near_all, pair_all, dq_all, dq_ref, dq_packed, dkv_own, pair_buf, us, ua, gs, ga, gqs, gqa, u_part, xat, pa, gh, ghq, w1, w2s, w2, w3,
    q_send, q_recv, pair_send, pair_recv, far_send, far_recv, near_send, near_recv,
    u_send, u_recv, g_send, g_recv, gh_send, gh_recv, w1_send, w1_recv, w2_send, w2_recv,
    w3_send, w3_recv, e_send, e_recv, gq_send, gq_recv, po_send, po_recv, ghq_send, ghq_recv,
    din_half, dout_half,
):
    head, blk, z, y = place()
    planes = blks // 2
    tokens, model = x_ref.shape
    rows = w_ref.shape[0]
    wanted = (
        (win_hbm, win_ref), (wout_hbm, wout_ref), (x_hbm, x_ref), (w_hbm, w_ref), (g1_hbm, g1_ref)
    )
    fetched = [
        pltpu.make_async_copy(src, dst, in_sem.at[i]) for i, (src, dst) in enumerate(wanted)
    ]
    for copy in fetched:
        copy.start()
    met = greet(
        [(around(head, k, heads), blk) for k in range(1, heads)]
        + [(head, around(blk, k, blks)) for k in range(1, blks)]
    )
    meet(met)

    def start(copies):
        for copy in copies:
            copy.start()

    def finish(copies):
        for copy in copies:
            copy.wait()

    other_y = around(y, 1, 2)
    pair = 2 * z + other_y
    above, below = z < planes - 1, z > 0
    directions = ((1, above, below, 0), (-1, below, above, 2))

    half_span = dkv_ref.shape[1] // 2

    def half_of(ref, half):
        return ref.at[pl.ds(half * half_span, half_span)]

    def far_copy(step, slot, side, half):
        span = 2 * (z + 2 * step) + side
        return remote(
            half_of(dkv_ref.at[span], half), half_of(far_all.at[slot + side], half),
            far_send.at[slot + side, half], far_recv.at[slot + side, half], head, 2 * (z + step) + y,
        )

    def near_copy(step, slot, side, half):
        return remote(
            half_of(near_send_buf.at[slot + side], half), half_of(near_all.at[slot // 2, y], half),
            near_send.at[slot + side, half], near_recv.at[slot // 2, y, half],
            head, 2 * (z + step) + side,
        )

    def two_away(step):
        return z + 2 * step < planes if step > 0 else z + 2 * step >= 0

    for half in range(2):
        for step, there, back, slot in directions:

            @pl.when(two_away(step))
            def _():
                for side in range(2):
                    far_copy(step, slot, side, half).start()

    w1_copies = [
        remote(
            grads_ref.at[:, around(head, k, heads)], w1.at[head],
            w1_send.at[k], w1_recv.at[k], around(head, k, heads), blk,
        )
        for k in range(1, heads)
    ]
    start(w1_copies)
    w1[head] = grads_ref[:, head]

    core = lax.rem(head, 2)
    sibling = head - core + 1 - core
    ff_half = wout_ref.shape[0] // 2
    ff_step = ff_half // 4

    def expert_chunk(chunk):
        here = pl.multiple_of(core * ff_half + chunk * ff_step, ff_step)
        there = pl.multiple_of(chunk * ff_step, ff_step)
        into = win_ref[:, pl.ds(here, ff_step)]
        outof = wout_ref[pl.ds(here, ff_step), :]
        d_in = jnp.zeros((model, ff_step), F32)
        d_out = jnp.zeros((ff_step, model), F32)
        for source in range(heads):
            rows_in = rx_ref[source, :, 0:model]
            grads_out = rx_ref[source, :, model : 2 * model]
            act, slope = gelu_parts(dot(rows_in, into))
            d_act = dot(grads_out, outof, (1, 1))
            d_in = d_in + dot(rows_in, (slope * d_act).astype(BF16), (0, 0))
            d_out = d_out + dot(act.astype(BF16), grads_out, (0, 0))
        din_ref[:, pl.ds(here, ff_step)] = d_in
        dout_ref[pl.ds(here, ff_step), :] = d_out
        din_half[core, :, pl.ds(there, ff_step)] = d_in.astype(BF16)
        dout_half[core, pl.ds(there, ff_step), :] = d_out.astype(BF16)

    key_tile = kv_ref.shape[1]
    for group in range(2 * key_tile // (CHAINS * QUERY_TILE)):
        tiles, queries = query_group(q_ref, group, y)
        known = (
            queries,
            group_grads(do_ref, tiles, y),
            [delta_ref[tile, 0:1, :] for tile in tiles],
            [lse_ref[tile, 0:1, :] for tile in tiles],
        )
        carry = tuple(begun_ref[tile] for tile in tiles)
        for side in range(2):
            first = pl.multiple_of((2 * z + side) * key_tile, key_tile)
            keys_across = kvt_ref[:, pl.ds(first, key_tile)]
            given, carry = attend_back(
                bounds_ref, tiles, first, kv_ref[2 * z + side], keys_across, known, carry
            )
            dkv_own[side] = given if group == 0 else dkv_own[side] + given
        for tile, total in zip(tiles, carry):
            at = tile * QUERY_TILE % key_tile
            dq_ref[tile * QUERY_TILE // key_tile, at : at + QUERY_TILE] = jnp.transpose(total)
    pair_buf[...] = dkv_own[other_y].astype(BF16)
    pair_copy = remote(pair_buf, pair_all, pair_send, pair_recv, head, pair)
    pair_copy.start()
    own_lanes = (lane_ids(dq_packed.shape) < HALF) == (y == 0)
    dq_packed[...] = halves(dq_ref[other_y], own_lanes).astype(BF16)
    q_copy = remote(dq_packed, dq_all, q_send, q_recv, head, pair)
    q_copy.start()
    for half in range(2):
        rows_here = slice(half * half_span, (half + 1) * half_span)
        for step, there, back, slot in directions:

            @pl.when(there)
            def _():
                for side in range(2):
                    near_send_buf[slot + side, rows_here] = dkv_ref[2 * (z + step) + side, rows_here]

            @pl.when(jnp.logical_and(there, back))
            def _():
                for side in range(2):
                    arrived(half_of(far_all.at[slot + side], half), far_recv.at[slot + side, half])
                    near_send_buf[slot + side, rows_here] = (
                        near_send_buf[slot + side, rows_here].astype(F32)
                        + far_all[slot + side, rows_here].astype(F32)
                    ).astype(BF16)

            @pl.when(there)
            def _():
                for side in range(2):
                    near_copy(step, slot, side, half).start()

    finish(fetched[:2])
    weight = wa_ref[...].reshape(model, 3 * LANES)
    for piece in range(heads):
        xat[:, piece * tokens : (piece + 1) * tokens] = jnp.transpose(xa_ref[piece])
    even = y == 0


    @pl.loop(0, 2)
    def _(chunk):
        expert_chunk(chunk)

    q_copy.wait()
    landed = dq_all[...].astype(F32)
    landed = jnp.concatenate([landed, pltpu.roll(landed, HALF, 1)], axis=0)
    own_lanes = (lane_ids(landed.shape) < HALF) == even
    q_grads = jnp.where(own_lanes, dq_ref[y], landed).astype(BF16)
    gqs[...] = dot(xat[...], q_grads).astype(BF16).reshape(gqs.shape)
    gq_copies = [
        remote(
            gqs.at[around(blk, k, blks)], gqa.at[blk],
            gq_send.at[k], gq_recv.at[k], head, around(blk, k, blks),
        )
        for k in range(1, blks)
    ]
    start(gq_copies)
    gqa[blk] = gqs[blk]
    u_part[...] = dot(q_grads, weight[:, 2 * LANES : 3 * LANES], (1, 1)).reshape(u_part.shape)

    finish(w1_copies)
    summed = w1[0].astype(F32)
    for source in range(1, heads):
        summed = summed + w1[source].astype(F32)
    w2s[...] = summed.astype(BF16)
    w2_copies = [
        remote(
            w2s.at[around(blk, k, blks)], w2.at[blk],
            w2_send.at[k], w2_recv.at[k], head, around(blk, k, blks),
        )
        for k in range(1, blks)
    ]
    start(w2_copies)
    w2[blk] = w2s[blk]

    @pl.loop(2, 4)
    def _(chunk):
        expert_chunk(chunk)

    e_copies = [
        remote(din_half.at[core], din_half.at[core], e_send.at[0], e_recv.at[0], sibling, blk),
        remote(dout_half.at[core], dout_half.at[core], e_send.at[1], e_recv.at[1], sibling, blk),
    ]
    start(e_copies)

    pair_copy.wait()
    for step, there, back, slot in directions:

        @pl.when(back)
        def _():
            for side in range(2):
                for half in range(2):
                    arrived(
                        half_of(near_all.at[slot // 2, side], half),
                        near_recv.at[slot // 2, side, half],
                    )

        @pl.when(jnp.logical_not(back))
        def _():
            near_all[slot // 2] = jnp.zeros(near_all.shape[1:], BF16)

    own = dkv_own[y]
    other = pair_all[...].astype(F32)
    made = jnp.concatenate(
        [
            (
                jnp.where(even == (side == 0), own, other)
                + near_all[0, side].astype(F32)
                + near_all[1, side].astype(F32)
            ).astype(BF16)
            for side in range(2)
        ],
        axis=1,
    )
    gs[...] = dot(xat[...], made).astype(BF16).reshape(gs.shape)
    g_copies = [
        remote(
            gs.at[around(blk, k, blks)], ga.at[blk],
            g_send.at[k], g_recv.at[k], head, around(blk, k, blks),
        )
        for k in range(1, blks)
    ]
    start(g_copies)
    ga[blk] = gs[blk]
    us[...] = (
        u_part[...] + dot(made, weight[:, 0 : 2 * LANES], (1, 1)).reshape(us.shape)
    ).astype(BF16)
    u_copies = [
        remote(
            us.at[around(head, k, heads)], ua.at[head],
            u_send.at[k], u_recv.at[k], around(head, k, heads), blk,
        )
        for k in range(1, heads)
    ]
    start(u_copies)
    ua[head] = us[head]
    finish(fetched[2:])
    finish(gq_copies)
    total = gqa[0].astype(F32)
    for source in range(1, blks):
        total = total + gqa[source].astype(F32)
    ghq[head] = total.astype(BF16)
    ghq_copies = [
        remote(ghq.at[head], ghq.at[head], ghq_send.at[k], ghq_recv.at[k], around(head, k, heads), blk)
        for k in range(1, heads)
    ]
    start(ghq_copies)

    finish(w2_copies)
    part = w2[0].astype(F32)
    for source in range(1, blks):
        part = part + w2[source].astype(F32)
    w3[head] = part.astype(BF16)
    w3_copies = [
        remote(w3.at[head], w3.at[head], w3_send.at[k], w3_recv.at[k], around(head, k, heads), blk)
        for k in range(1, heads)
    ]
    start(w3_copies)

    xhat, scale = centre(x_ref[...].astype(F32))
    finish(e_copies)
    there = pl.multiple_of((1 - core) * ff_half, ff_half)
    din_ref[:, pl.ds(there, ff_half)] = din_half[1 - core].astype(F32)
    dout_ref[pl.ds(there, ff_half), :] = dout_half[1 - core].astype(F32)
    finish(g_copies)
    total = ga[0].astype(F32)
    for source in range(1, blks):
        total = total + ga[source].astype(F32)
    gh[head] = total.astype(BF16)
    gh_copies = [
        remote(gh.at[head], gh.at[head], gh_send.at[k], gh_recv.at[k], around(head, k, heads), blk)
        for k in range(1, heads)
    ]
    start(gh_copies)
    po_copies = [
        remote(
            po_ref.at[around(blk, k, blks)], pa.at[blk],
            po_send.at[k], po_recv.at[k], head, around(blk, k, blks),
        )
        for k in range(1, blks)
    ]
    start(po_copies)
    pa[blk] = po_ref[blk]
    finish(u_copies)
    grad = ua[0].astype(F32)
    for source in range(1, heads):
        grad = grad + ua[source].astype(F32)
    dx_ref[...] = dh_ref[...] + centre_back(grad, xhat, scale)

    gain_tile[...] = jnp.zeros_like(gain_tile)
    gain_tile[0:1, 0:rows] = g1_ref[...].astype(F32)
    gain = jnp.transpose(jnp.broadcast_to(gain_tile[0:1, :], (LANES, LANES)))[:rows]
    low_half = lane_ids((rows, LANES)) < HALF
    finish(ghq_copies)
    finish(gh_copies)
    d_gain = jnp.zeros((rows, LANES), F32)
    for source in range(heads):
        both = [gh[source, :, i * LANES : (i + 1) * LANES].astype(F32) for i in range(2)]
        grads = (
            ghq[source].astype(F32) * HS ** (-0.5),
            jnp.where(low_half, both[0], both[1]),
            pltpu.roll(jnp.where(low_half, both[1], both[0]), HALF, 1),
        )
        for which, value in enumerate(grads):
            columns = slice(which * model + source * LANES, which * model + (source + 1) * LANES)
            d_gain = d_gain + value * w_ref[:, columns].astype(F32)
            dw_ref[:, columns] = value * gain
    finish(w3_copies)
    shared = w3[...].reshape(rows, w3.shape[-1]).astype(F32)
    shared_ref[:, 0:model] = shared[:, 0:model]
    gain_col = jnp.sum(d_gain, axis=1, keepdims=True)
    shared_ref[:, model : model + LANES] = jnp.where(
        lane_ids((rows, LANES)) == blks + 1, gain_col, shared[:, model : model + LANES]
    )
    finish(po_copies)
    parts = pa[...].reshape(share_ref.shape[2], model)
    mixture = dot(share_ref[0], parts) + dot(share_ref[1], parts)
    y_ref[...] = (hidden_ref[...] + mixture).astype(BF16)

    for step, there, back, slot in directions:

        @pl.when(two_away(step))
        def _():
            for side in range(2):
                for half in range(2):
                    far_copy(step, slot, side, half).wait_send()

        @pl.when(there)
        def _():
            for side in range(2):
                for half in range(2):
                    near_copy(step, slot, side, half).wait_send()


def call_last(
    x, dh, dq, dkv, xa, wa, w_qkv, g1, grads, rx, win, wout, po, hidden, share,
    bounds, q, kv, kvt, d_o, lse, delta, heads, blks,
):
    tokens, model = x.shape
    span = tokens * heads
    rows = w_qkv.shape[0]
    wide = model + LANES
    part = rows // heads
    ff = wout.shape[0]

    def block(*lead):
        return pltpu.VMEM((*lead, span, LANES), BF16)

    return pl.pallas_call(
        functools.partial(last_kernel, heads, blks),
        out_shape=(
            jax.ShapeDtypeStruct((tokens, model), BF16),
            jax.ShapeDtypeStruct((tokens, model), F32),
            jax.ShapeDtypeStruct((rows, 3 * model), F32),
            jax.ShapeDtypeStruct((rows, wide), F32),
            jax.ShapeDtypeStruct((model, ff), F32),
            jax.ShapeDtypeStruct((ff, model), F32),
        ),
        in_specs=hbm_specs(1) + vmem_specs(5) + hbm_specs(2) + vmem_specs(2) + hbm_specs(2) + vmem_specs(10),
        out_specs=tuple(vmem_specs(6)),
        scratch_shapes=[
            pltpu.VMEM((tokens, model), BF16),
            pltpu.VMEM((rows, 3 * model), BF16),
            pltpu.VMEM((1, rows), BF16),
            pltpu.VMEM(win.shape, BF16),
            pltpu.VMEM(wout.shape, BF16),
            dma(5),
            pltpu.VMEM((8, LANES), F32),
            block(4), block(4), block(2, 2), block(), pltpu.VMEM((span // 2, LANES), BF16),
            pltpu.VMEM((2, span, LANES), F32), pltpu.VMEM((span // 2, LANES), BF16),
            pltpu.VMEM((2, span, LANES), F32), block(),
            pltpu.VMEM((heads, tokens, model), BF16), pltpu.VMEM((heads, tokens, model), BF16),
            pltpu.VMEM((blks, rows, 2 * LANES), BF16), pltpu.VMEM((blks, rows, 2 * LANES), BF16),
            pltpu.VMEM((blks, rows, LANES), BF16), pltpu.VMEM((blks, rows, LANES), BF16),
            pltpu.VMEM((heads, tokens, model), F32), pltpu.VMEM((model, span), BF16),
            pltpu.VMEM(po.shape, BF16),
            pltpu.VMEM((heads, rows, 2 * LANES), BF16), pltpu.VMEM((heads, rows, LANES), BF16),
            pltpu.VMEM((heads, blks, part, wide), BF16), pltpu.VMEM((blks, part, wide), BF16),
            pltpu.VMEM((blks, part, wide), BF16), pltpu.VMEM((heads, part, wide), BF16),
            pltpu.SemaphoreType.DMA, pltpu.SemaphoreType.DMA, pltpu.SemaphoreType.DMA, pltpu.SemaphoreType.DMA,
            dma(4, 2), dma(4, 2), dma(4, 2), dma(2, 2, 2),
            dma(heads), dma(heads), dma(blks), dma(blks), dma(heads), dma(heads), dma(heads), dma(heads),
            dma(blks), dma(blks), dma(heads), dma(heads), dma(2), dma(2), dma(blks), dma(blks), dma(blks), dma(blks), dma(heads), dma(heads),
            pltpu.VMEM((2, model, ff // 2), BF16), pltpu.VMEM((2, ff // 2, model), BF16),
        ],
        compiler_params=pltpu.CompilerParams(
            collective_id=3, has_side_effects=True, vmem_limit_bytes=36 * MIB
        ),
        name="last",
    )(
        *in_hbm(x), dh, dq, dkv, xa, wa, *in_hbm(w_qkv, g1.reshape(1, rows)),
        grads.reshape(blks, heads, part, wide), rx, *in_hbm(win, wout), po, hidden, share,
        bounds, q, kv, kvt, d_o, lse, delta,
    )


def finish_kernel(
    experts,
    y_ref, dx_ref, dw_ref, shared_ref, din_ref, dout_ref,
    y_out, dx_out, g1_out, dw_out, dwo_out, g2_out, wr_out, din_out, dout_out,
    tile, wr, g2, g1, sem,
):
    rows = shared_ref.shape[0]
    model = dx_ref.shape[1]
    copies = [
        pltpu.make_async_copy(dx_ref, dx_out, sem.at[0]),
        pltpu.make_async_copy(dw_ref, dw_out, sem.at[1]),
        pltpu.make_async_copy(shared_ref.at[:, pl.ds(0, model)], dwo_out, sem.at[2]),
        pltpu.make_async_copy(y_ref, y_out, sem.at[6]),
        pltpu.make_async_copy(din_ref, din_out, sem.at[7]),
        pltpu.make_async_copy(dout_ref, dout_out, sem.at[8]),
    ]
    for copy in copies:
        copy.start()
    tile[...] = jnp.zeros_like(tile)
    tile[0:rows, :] = shared_ref[:, model : model + LANES]
    across = jnp.transpose(tile[...])[:, 0:rows]
    wr[...] = across[0:experts]
    g2[...] = across[experts : experts + 1]
    g1[...] = across[experts + 1 : experts + 2]
    for index, (src, dst) in enumerate(((wr, wr_out), (g2, g2_out), (g1, g1_out))):
        copies.append(pltpu.make_async_copy(src, dst, sem.at[3 + index]))
        copies[-1].start()
    for copy in copies:
        copy.wait()


def call_finish(output, dx, dw, shared, d_in, d_out):
    rows = shared.shape[0]
    model = dx.shape[1]
    experts = model // rows
    return pl.pallas_call(
        functools.partial(finish_kernel, experts),
        out_shape=(
            jax.ShapeDtypeStruct(output.shape, BF16),
            jax.ShapeDtypeStruct(dx.shape, F32),
            jax.ShapeDtypeStruct((1, rows), F32),
            jax.ShapeDtypeStruct(dw.shape, F32),
            jax.ShapeDtypeStruct((rows, model), F32),
            jax.ShapeDtypeStruct((1, rows), F32),
            jax.ShapeDtypeStruct((experts, rows), F32),
            jax.ShapeDtypeStruct(d_in.shape, F32),
            jax.ShapeDtypeStruct(d_out.shape, F32),
        ),
        in_specs=vmem_specs(6),
        out_specs=tuple(hbm_specs(9)),
        scratch_shapes=[
            pltpu.VMEM((LANES, LANES), F32),
            pltpu.VMEM((experts, rows), F32),
            pltpu.VMEM((1, rows), F32),
            pltpu.VMEM((1, rows), F32),
            dma(9),
        ],
        compiler_params=pltpu.CompilerParams(vmem_limit_bytes=16 * MIB),
        name="finish",
    )(output, dx, dw, shared, d_in, d_out)


def local_kernels(
    inputs, ln1_gain, w_qkv, w_out, ln2_gain, w_router,
    expert_in, expert_out, routes, priority, doc_lengths, d_out,
):
    heads, blks = lax.axis_size("head"), lax.axis_size("blk")
    model = inputs.shape[1]
    tokens = inputs.shape[0]
    win, wout = expert_in[0], expert_out[0]
    q, kv, xa, wa, wo, kvt, bounds, begun = call_qkv(
        inputs, w_qkv, ln1_gain, w_out, w_router, ln2_gain, doc_lengths, heads, blks
    )
    o, o_low, lse = call_forward(bounds, q, kv, kvt, begun)
    po, hidden, share, dh, d_o, grads, rx = call_middle(
        inputs, o_low.reshape(2, heads, tokens // 2, LANES), wo.reshape(model, model + LANES),
        routes, priority, d_out, win, wout, heads, blks,
    )
    d_o = d_o.reshape(2 * heads * tokens // QUERY_TILE, -1, HALF, LANES)
    dq, dkv, delta = call_backward(bounds, q, kv, kvt, d_o, o, lse)
    ends = call_last(
        inputs, dh, dq, dkv, xa, wa, w_qkv, ln1_gain, grads, rx, win, wout,
        po, hidden, share, bounds, q, kv, kvt, d_o, lse, delta, heads, blks,
    )
    output, d_inputs, d_gain_one, d_qkv, d_out_proj, d_gain_two, d_router, d_in, d_out_weight = call_finish(*ends)
    return (
        output,
        d_inputs,
        d_gain_one.reshape(-1),
        d_qkv,
        d_out_proj,
        d_gain_two.reshape(-1),
        d_router.T,
        d_in[None],
        d_out_weight[None],
    )


def solution(mesh):
    in_specs = (
        P(("blk", "head"), None),
        P("blk"),
        P("blk", None),
        P("blk", None),
        P("blk"),
        P("blk", None),
        P("blk", None, None),
        P("blk", None, None),
        P(("blk", "head"), None),
        P(("blk", "head"), None),
        P(),
        P(("blk", "head"), None),
    )
    out_specs = (
        P(("blk", "head"), None),
        P(("blk", "head"), None),
        P("blk"),
        P("blk", None),
        P("blk", None),
        P("blk"),
        P("blk", None),
        P("blk", None, None),
        P("blk", None, None),
    )
    fits = mesh.shape["head"] == 4 and mesh.shape["blk"] == 8
    body = local_kernels if fits else local
    return jax.shard_map(body, mesh=mesh, in_specs=in_specs, out_specs=out_specs, check_vma=False)
```

```python
import functools
import math

import jax
import jax.numpy as jnp
from jax import lax
from jax.experimental import pallas as pl
from jax.experimental.pallas import tpu as pltpu
from jax.sharding import PartitionSpec as P

HS = 64
KEY_BLOCK = 2048


PRECISE = lax.Precision.HIGHEST
MASKED = -1e30
EPSILON = 1e-06


def layer_norm(values, gain):
    average = jnp.mean(values, axis=-1, keepdims=True)
    centred = values - average
    spread = jnp.mean(centred * centred, axis=-1, keepdims=True)
    return centred * lax.rsqrt(spread + EPSILON) * gain


def gelu_exact(values):
    return jax.nn.gelu(values, approximate=False)


def router(row_block, weight):
    return jax.nn.softmax(jnp.dot(row_block, weight, precision=PRECISE), axis=-1)


def doc_index(positions, doc_lengths):
    places = jnp.arange(doc_lengths.shape[0], dtype=jnp.int32)
    starts = jnp.sum(jnp.where(places[None, :] < places[:, None], doc_lengths[None, :], 0), axis=1)
    at_most = (starts[None, :] <= positions[:, None]).astype(jnp.int32)
    return jnp.sum(at_most, axis=1) - 1


def slot_table(route_rows, ranking, capacity):
    token_count = route_rows.shape[0]
    expert = jnp.transpose(route_rows).reshape(-1)
    pair_order = (jnp.arange(2, dtype=jnp.int32)[:, None] * token_count + ranking[None, :]).reshape(
        -1
    )
    before = (expert[:, None] == expert[None, :]) & (pair_order[None, :] < pair_order[:, None])
    position = jnp.sum(before.astype(jnp.int32), axis=1)
    slot_ids = jnp.where(position < capacity, expert * capacity + position, -1)
    return slot_ids.reshape(2, token_count)


def keep_state(current):
    return current


def local(
    inputs,
    ln1_gain,
    w_qkv,
    w_out,
    ln2_gain,
    w_router,
    expert_in,
    expert_out,
    routes,
    priority,
    doc_lengths,
    d_out,
):
    blk_size = lax.axis_size("blk")
    tok_rows = inputs.shape[0]
    model_width = inputs.shape[1]
    capacity = 2 * tok_rows // blk_size
    slot_total = blk_size * capacity
    gain_one, qkv_weight, out_weight, gain_two, router_weight = (
        lax.all_gather(ln1_gain, "blk", axis=0, tiled=True),
        lax.all_gather(w_qkv, "blk", axis=0, tiled=True),
        lax.all_gather(w_out, "blk", axis=0, tiled=True),
        lax.all_gather(ln2_gain, "blk", axis=0, tiled=True),
        lax.all_gather(w_router, "blk", axis=0, tiled=True),
    )
    input_rows = inputs.astype(jnp.float32)
    normed_one, norm_one_pull = jax.vjp(layer_norm, input_rows, gain_one.astype(jnp.float32))
    normed_low = normed_one.astype(jnp.bfloat16)
    qkv_rows = jnp.dot(normed_low, qkv_weight, preferred_element_type=jnp.float32).astype(
        jnp.bfloat16
    )
    query_heads, key_heads, value_heads = (
        lax.all_to_all(qkv_rows[:, :model_width], "head", split_axis=1, concat_axis=0, tiled=True),
        lax.all_to_all(
            qkv_rows[:, model_width : 2 * model_width],
            "head",
            split_axis=1,
            concat_axis=0,
            tiled=True,
        ),
        lax.all_to_all(
            qkv_rows[:, 2 * model_width :], "head", split_axis=1, concat_axis=0, tiled=True
        ),
    )
    span_rows = query_heads.shape[0]
    head_count = query_heads.shape[1] // HS
    key_all, value_all = (
        lax.all_gather(key_heads, "blk", axis=0, tiled=True),
        lax.all_gather(value_heads, "blk", axis=0, tiled=True),
    )
    total_rows = key_all.shape[0]
    block_count = total_rows // KEY_BLOCK
    scale_factor = HS ** (-0.5)
    query_pos = lax.axis_index("blk") * span_rows + jnp.arange(span_rows, dtype=jnp.int32)
    query_docs = doc_index(query_pos, doc_lengths)
    queries = query_heads.reshape(span_rows, head_count, HS)

    def block_parts(block_index, key_source, value_source):
        first_key = block_index * KEY_BLOCK
        key_rows = lax.dynamic_slice_in_dim(key_source, first_key, KEY_BLOCK, 0).reshape(
            KEY_BLOCK, head_count, HS
        )
        value_rows = lax.dynamic_slice_in_dim(value_source, first_key, KEY_BLOCK, 0).reshape(
            KEY_BLOCK, head_count, HS
        )
        key_docs = doc_index(first_key + jnp.arange(KEY_BLOCK, dtype=jnp.int32), doc_lengths)
        is_live = (key_docs[0] <= query_docs[-1]) & (key_docs[-1] >= query_docs[0])
        same_doc = query_docs[:, None] == key_docs[None, :]
        return (first_key, key_rows, value_rows, same_doc, is_live)

    def block_scores(key_rows, same_doc):
        raw_scores = (
            jnp.einsum("qhd,khd->hqk", queries, key_rows, preferred_element_type=jnp.float32)
            * scale_factor
        )
        return jnp.where(same_doc[None], raw_scores, MASKED)

    def stat_step(block_index, loop_state):
        first_key, key_rows, value_rows, same_doc, is_live = block_parts(
            block_index, key_all, value_all
        )

        def stat_update(current):
            running_max, running_sum = current
            scores = block_scores(key_rows, same_doc)
            new_max = jnp.maximum(running_max, jnp.max(scores, axis=2))
            exp_terms = jnp.where(same_doc[None], jnp.exp(scores - new_max[:, :, None]), 0.0)
            return (
                new_max,
                running_sum * jnp.exp(running_max - new_max) + jnp.sum(exp_terms, axis=2),
            )

        return lax.cond(is_live, stat_update, keep_state, loop_state)

    start_state = (
        jnp.full((head_count, span_rows), MASKED, jnp.float32),
        jnp.zeros((head_count, span_rows), jnp.float32),
    )
    running_max, running_sum = lax.fori_loop(0, block_count, stat_step, start_state)
    log_total = running_max + jnp.log(running_sum)

    def out_step(block_index, loop_state):
        first_key, key_rows, value_rows, same_doc, is_live = block_parts(
            block_index, key_all, value_all
        )

        def out_update(current):
            scores = block_scores(key_rows, same_doc)
            weights = jnp.where(
                same_doc[None], jnp.exp(scores - log_total[:, :, None]), 0.0
            ).astype(jnp.bfloat16)
            return current + jnp.einsum(
                "hqk,khd->qhd", weights, value_rows, preferred_element_type=jnp.float32
            )

        return lax.cond(is_live, out_update, keep_state, loop_state)

    mixed_full = lax.fori_loop(
        0, block_count, out_step, jnp.zeros((span_rows, head_count, HS), jnp.float32)
    )
    mixed_low = mixed_full.reshape(span_rows, head_count * HS).astype(jnp.bfloat16)
    mixed_tokens = lax.all_to_all(mixed_low, "head", split_axis=0, concat_axis=1, tiled=True)
    attended = jnp.dot(mixed_tokens, out_weight, preferred_element_type=jnp.float32)
    hidden_one = input_rows + attended
    normed_two, norm_two_pull = jax.vjp(layer_norm, hidden_one, gain_two.astype(jnp.float32))
    routed_low = normed_two.astype(jnp.bfloat16)
    router_probs, router_pull = jax.vjp(
        router, routed_low.astype(jnp.float32), router_weight.astype(jnp.float32)
    )
    slot_ids = slot_table(routes, priority[0], capacity)
    select = (
        slot_ids[:, :, None] == jnp.arange(slot_total, dtype=jnp.int32)[None, None, :]
    ).astype(jnp.bfloat16)
    send_rows = jnp.einsum(
        "kts,td->sd", select, routed_low, preferred_element_type=jnp.float32
    ).astype(jnp.bfloat16)
    expert_rows = lax.all_to_all(
        send_rows.reshape(blk_size, capacity, model_width),
        "blk",
        split_axis=0,
        concat_axis=0,
        tiled=True,
    ).reshape(slot_total, model_width)
    weight_in = expert_in[0]
    weight_out = expert_out[0]
    pre_act = jnp.dot(expert_rows, weight_in, preferred_element_type=jnp.float32)
    hidden_act, gelu_pull = jax.vjp(gelu_exact, pre_act)
    hidden_low = hidden_act.astype(jnp.bfloat16)
    expert_result = jnp.dot(hidden_low, weight_out, preferred_element_type=jnp.float32).astype(
        jnp.bfloat16
    )
    slot_result = lax.all_to_all(
        expert_result.reshape(blk_size, capacity, model_width),
        "blk",
        split_axis=0,
        concat_axis=0,
        tiled=True,
    ).reshape(slot_total, model_width)
    pair_result = jnp.einsum("kts,sd->ktd", select, slot_result, preferred_element_type=jnp.float32)
    route_hot = (routes[:, :, None] == jnp.arange(blk_size, dtype=jnp.int32)[None, None, :]).astype(
        jnp.float32
    )
    gate_vals = jnp.sum(router_probs[:, None, :] * route_hot, axis=2)
    mixture = gate_vals[:, 0, None] * pair_result[0] + gate_vals[:, 1, None] * pair_result[1]
    output = (hidden_one + mixture).astype(jnp.bfloat16)
    d_gates = jnp.transpose(jnp.sum(d_out[None] * pair_result, axis=2))
    d_probs = jnp.sum(d_gates[:, :, None] * route_hot, axis=1)
    pair_grads = (jnp.transpose(gate_vals)[:, :, None] * d_out[None]).astype(jnp.bfloat16)
    slot_grads = jnp.einsum(
        "kts,ktd->sd", select, pair_grads, preferred_element_type=jnp.float32
    ).astype(jnp.bfloat16)
    result_grads = lax.all_to_all(
        slot_grads.reshape(blk_size, capacity, model_width),
        "blk",
        split_axis=0,
        concat_axis=0,
        tiled=True,
    ).reshape(slot_total, model_width)
    d_hidden_act = jnp.dot(result_grads, weight_out.T, preferred_element_type=jnp.float32)
    d_weight_out = jnp.dot(hidden_low.T, result_grads, preferred_element_type=jnp.float32)
    d_preact = gelu_pull(d_hidden_act)[0].astype(jnp.bfloat16)
    d_weight_in = jnp.dot(expert_rows.T, d_preact, preferred_element_type=jnp.float32)
    row_grads = jnp.dot(d_preact, weight_in.T, preferred_element_type=jnp.float32).astype(
        jnp.bfloat16
    )
    slot_back = lax.all_to_all(
        row_grads.reshape(blk_size, capacity, model_width),
        "blk",
        split_axis=0,
        concat_axis=0,
        tiled=True,
    ).reshape(slot_total, model_width)
    d_routed = jnp.einsum("kts,sd->td", select, slot_back, preferred_element_type=jnp.float32)
    d_routed_router, d_router = router_pull(d_probs)
    d_hidden_norm, d_gain_two = norm_two_pull(d_routed + d_routed_router)
    d_hidden_one = d_out + d_hidden_norm
    attn_grads = d_hidden_one.astype(jnp.bfloat16)
    d_out_weight = jnp.dot(mixed_tokens.T, attn_grads, preferred_element_type=jnp.float32)
    mixed_grads = jnp.dot(attn_grads, out_weight.T, preferred_element_type=jnp.float32).astype(
        jnp.bfloat16
    )
    head_grads = lax.all_to_all(mixed_grads, "head", split_axis=1, concat_axis=0, tiled=True)
    out_grads = head_grads.reshape(span_rows, head_count, HS)
    row_delta = jnp.transpose(jnp.sum(out_grads.astype(jnp.float32) * mixed_full, axis=2))
    key_back, value_back = (
        lax.all_gather(key_heads, "blk", axis=0, tiled=True),
        lax.all_gather(value_heads, "blk", axis=0, tiled=True),
    )

    def grad_step(block_index, loop_state):
        first_key, key_rows, value_rows, same_doc, is_live = block_parts(
            block_index, key_back, value_back
        )

        def grad_update(current):
            query_grad, key_grad, value_grad = current
            scores = block_scores(key_rows, same_doc)
            weights = jnp.where(same_doc[None], jnp.exp(scores - log_total[:, :, None]), 0.0)
            value_part = jnp.einsum(
                "hqk,qhd->khd",
                weights.astype(jnp.bfloat16),
                out_grads,
                preferred_element_type=jnp.float32,
            )
            weight_grads = jnp.einsum(
                "qhd,khd->hqk", out_grads, value_rows, preferred_element_type=jnp.float32
            )
            score_grads = (weights * (weight_grads - row_delta[:, :, None])).astype(jnp.bfloat16)
            query_grad = (
                query_grad
                + jnp.einsum(
                    "hqk,khd->qhd", score_grads, key_rows, preferred_element_type=jnp.float32
                )
                * scale_factor
            )
            key_part = (
                jnp.einsum("hqk,qhd->khd", score_grads, queries, preferred_element_type=jnp.float32)
                * scale_factor
            )
            key_grad = lax.dynamic_update_slice_in_dim(
                key_grad, key_part.reshape(KEY_BLOCK, head_count * HS), first_key, 0
            )
            value_grad = lax.dynamic_update_slice_in_dim(
                value_grad, value_part.reshape(KEY_BLOCK, head_count * HS), first_key, 0
            )
            return (query_grad, key_grad, value_grad)

        return lax.cond(is_live, grad_update, keep_state, loop_state)

    start_grads = (
        jnp.zeros((span_rows, head_count, HS), jnp.float32),
        jnp.zeros((total_rows, head_count * HS), jnp.float32),
        jnp.zeros((total_rows, head_count * HS), jnp.float32),
    )
    query_grad, key_grad, value_grad = lax.fori_loop(0, block_count, grad_step, start_grads)
    key_own, value_own = (
        lax.psum_scatter(
            key_grad.astype(jnp.bfloat16), "blk", scatter_dimension=0, tiled=True
        ).astype(jnp.float32),
        lax.psum_scatter(
            value_grad.astype(jnp.bfloat16), "blk", scatter_dimension=0, tiled=True
        ).astype(jnp.float32),
    )
    query_tokens_grad, key_tokens_grad, value_tokens_grad = (
        lax.all_to_all(
            query_grad.reshape(span_rows, head_count * HS).astype(jnp.bfloat16),
            "head",
            split_axis=0,
            concat_axis=1,
            tiled=True,
        ),
        lax.all_to_all(
            key_own.astype(jnp.bfloat16), "head", split_axis=0, concat_axis=1, tiled=True
        ),
        lax.all_to_all(
            value_own.astype(jnp.bfloat16), "head", split_axis=0, concat_axis=1, tiled=True
        ),
    )
    qkv_grads = jnp.concatenate([query_tokens_grad, key_tokens_grad, value_tokens_grad], axis=1)
    d_qkv_weight = jnp.dot(normed_low.T, qkv_grads, preferred_element_type=jnp.float32)
    normed_grads = jnp.dot(qkv_grads, qkv_weight.T, preferred_element_type=jnp.float32)
    d_inputs_norm, d_gain_one = norm_one_pull(normed_grads)
    d_inputs = d_hidden_one + d_inputs_norm
    gain_one_sum, qkv_sum, out_sum, gain_two_sum, router_sum = (
        lax.psum_scatter(
            d_gain_one.astype(jnp.bfloat16), "blk", scatter_dimension=0, tiled=True
        ).astype(jnp.float32),
        lax.psum_scatter(
            d_qkv_weight.astype(jnp.bfloat16), "blk", scatter_dimension=0, tiled=True
        ).astype(jnp.float32),
        lax.psum_scatter(
            d_out_weight.astype(jnp.bfloat16), "blk", scatter_dimension=0, tiled=True
        ).astype(jnp.float32),
        lax.psum_scatter(
            d_gain_two.astype(jnp.bfloat16), "blk", scatter_dimension=0, tiled=True
        ).astype(jnp.float32),
        lax.psum_scatter(
            d_router.astype(jnp.bfloat16), "blk", scatter_dimension=0, tiled=True
        ).astype(jnp.float32),
    )
    gain_one_all, qkv_all, out_all, gain_two_all, router_all, expert_in_all, expert_out_all = (
        lax.psum(gain_one_sum.astype(jnp.bfloat16), "head").astype(jnp.float32),
        lax.psum(qkv_sum.astype(jnp.bfloat16), "head").astype(jnp.float32),
        lax.psum(out_sum.astype(jnp.bfloat16), "head").astype(jnp.float32),
        lax.psum(gain_two_sum.astype(jnp.bfloat16), "head").astype(jnp.float32),
        lax.psum(router_sum.astype(jnp.bfloat16), "head").astype(jnp.float32),
        lax.psum(d_weight_in[None].astype(jnp.bfloat16), "head").astype(jnp.float32),
        lax.psum(d_weight_out[None].astype(jnp.bfloat16), "head").astype(jnp.float32),
    )
    return (
        output,
        d_inputs,
        gain_one_all,
        qkv_all,
        out_all,
        gain_two_all,
        router_all,
        expert_in_all,
        expert_out_all,
    )


MESH = pl.DeviceIdType.MESH
LANES = 128
HALF = LANES // 2
MIB = 2**20
F32 = jnp.float32
BF16 = jnp.bfloat16


def dot(left, right, dims=(1, 0)):
    return lax.dot_general(
        left, right, (((dims[0],), (dims[1],)), ((), ())), preferred_element_type=F32
    )


def remote(src, dst, send_sem, recv_sem, head, blk):
    return pltpu.make_async_remote_copy(
        src_ref=src,
        dst_ref=dst,
        send_sem=send_sem,
        recv_sem=recv_sem,
        device_id={"head": head, "blk": blk},
        device_id_type=MESH,
    )


def arrived(ref, sem):
    pltpu.make_async_copy(ref, ref, sem).wait()


def greet(peers):
    barrier = pltpu.get_barrier_semaphore()
    for head, blk in peers:
        pl.semaphore_signal(
            barrier, inc=1, device_id={"head": head, "blk": blk}, device_id_type=MESH
        )
    return len(peers)


def meet(count):
    pl.semaphore_wait(pltpu.get_barrier_semaphore(), count)


def halves(values, lanes_kept):
    rows = values.shape[0] // 2
    moved = pltpu.roll(values[rows:], HALF, 1)
    return jnp.where(lanes_kept, values[:rows], moved)


def lane_ids(shape):
    return lax.broadcasted_iota(jnp.int32, shape, len(shape) - 1)


def centre(values):
    average = jnp.mean(values, axis=-1, keepdims=True)
    centred = values - average
    spread = jnp.mean(centred * centred, axis=-1, keepdims=True)
    scale = lax.rsqrt(spread + EPSILON)
    return centred * scale, scale


def centre_back(grad, xhat, scale):
    middle = jnp.mean(grad, axis=-1, keepdims=True)
    along = jnp.mean(grad * xhat, axis=-1, keepdims=True)
    return (grad - middle - xhat * along) * scale


def split_high_low(column, lanes):
    high = column.astype(BF16)
    low = (column - high.astype(F32)).astype(BF16)
    return jnp.where(lanes < HALF, high.astype(F32), low.astype(F32)).astype(BF16)


def join_high_low(matrix, start):
    return matrix[:, start : start + 1].astype(F32) + matrix[
        :, start + HALF : start + HALF + 1
    ].astype(F32)


def place():
    head, blk = lax.axis_index("head"), lax.axis_index("blk")
    return head, blk, blk // 2, lax.rem(blk, 2)


def around(index, step, size):
    return lax.rem(index + step, size)


QUERY_TILE = 256
CHAINS = 2


def masked_queries(q_ref, tile, key_lanes, query_tile):
    tiles_per_span = q_ref.shape[1] // query_tile
    inner = tile % tiles_per_span * query_tile
    query = q_ref[tile // tiles_per_span, inner : inner + query_tile, :]
    return jnp.where(key_lanes, query, jnp.zeros_like(query))


def group_blocks(bounds_ref, group, size, key_tile):
    first, last = group * size, (group + 1) * size
    low = jnp.min(bounds_ref[0:1, first : first + LANES])
    high = jnp.max(bounds_ref[1:2, last - LANES : last])
    return low // key_tile, (high + key_tile - 1) // key_tile


def inside_document(bounds_ref, tile, first, shape):
    key = first + lax.broadcasted_iota(jnp.int32, shape, 0)
    columns = slice(tile * shape[1], (tile + 1) * shape[1])
    return jnp.logical_and(key >= bounds_ref[0:1, columns], key < bounds_ref[1:2, columns])


def query_group(q_ref, group, y):
    key_lanes = (lane_ids((QUERY_TILE, LANES)) < HALF) == (y == 0)
    tiles = range(group * CHAINS, (group + 1) * CHAINS)
    return tiles, [masked_queries(q_ref, tile, key_lanes, QUERY_TILE) for tile in tiles]


def attend(bounds_ref, tiles, first, keys, keys_across, queries, carry):
    scores = [dot(keys, query, (1, 1)) for query in queries]
    made = []
    for tile, score, (biggest, weight, mixed) in zip(tiles, scores, carry):
        inside = inside_document(bounds_ref, tile, first, score.shape)
        score = jnp.where(inside, score, MASKED)
        bigger = jnp.maximum(biggest, jnp.max(score, axis=0, keepdims=True))
        fade = jnp.exp(biggest - bigger)
        terms = jnp.exp(score - bigger)
        weight = weight * fade + jnp.sum(terms, axis=0, keepdims=True)
        made.append((bigger, weight, mixed * fade + dot(keys_across, terms.astype(BF16))))
    return tuple(made)


def nothing_attended():
    return (
        jnp.full((1, QUERY_TILE), MASKED, F32),
        jnp.zeros((1, QUERY_TILE), F32),
        jnp.zeros((LANES, QUERY_TILE), F32),
    )


def attend_back(bounds_ref, tiles, first, keys, keys_across, group, carry):
    queries, out_grads, deltas, log_totals = group
    scores = [dot(keys, query, (1, 1)) for query in queries]
    weight_grads = [dot(keys, out_grad, (1, 1)) for out_grad in out_grads]
    pieces, score_grads = [], []
    for i, tile in enumerate(tiles):
        inside = inside_document(bounds_ref, tile, first, scores[i].shape)
        weights = jnp.exp(jnp.where(inside, scores[i], MASKED) - log_totals[i])
        score_grads.append((weights * (weight_grads[i] - deltas[i])).astype(BF16))
        pieces.append(weights.astype(BF16))
    wide = jnp.concatenate(score_grads + pieces, axis=1)
    given = dot(wide, jnp.concatenate(queries + out_grads, axis=0))
    return given, tuple(c + dot(keys_across, g) for c, g in zip(carry, score_grads))


def group_grads(do_ref, tiles, y):
    key_lanes = (lane_ids((QUERY_TILE, LANES)) < HALF) == (y == 0)
    out_grads = []
    for tile in tiles:
        parts = []
        for part in range(QUERY_TILE // LANES):
            packed = do_ref[tile, part].astype(F32)
            parts += [packed, pltpu.roll(packed, HALF, 1)]
        out_grads.append(jnp.where(key_lanes, 0.0, jnp.concatenate(parts, axis=0)).astype(BF16))
    return out_grads


def qkv_kernel(
    heads, blks,
    x_hbm, w_hbm, g1_hbm, wo_hbm, wr_hbm, g2_hbm, docs_hbm,
    qall, kvall, xall, wall, wo_all, kvt, bounds, begun,
    x_ref, w_ref, rows_in, g1_ref, g2_ref, wr_ref, docs_ref, wo_own, kv_other, q_packed, q_landed, in_sem,
    x_send, x_recv, w_send, w_recv, o_send, o_recv, p_send, p_recv,
    k_send, k_recv, q_recv,
):
    head, blk, z, y = place()
    planes = blks // 2
    model = x_ref.shape[1]
    rows = w_ref.shape[0]
    part = rows // heads
    experts = wr_ref.shape[0]
    wanted = (
        (w_hbm, w_ref), (g1_hbm, g1_ref), (g2_hbm, g2_ref), (wr_hbm, wr_ref), (x_hbm, x_ref),
        (wo_hbm, wo_own.at[:, pl.ds(0, model)]), (docs_hbm, docs_ref),
    )
    fetched = [
        pltpu.make_async_copy(src, dst, in_sem.at[i]) for i, (src, dst) in enumerate(wanted)
    ]
    for copy in fetched:
        copy.start()
    rows_in[...] = jnp.zeros_like(rows_in)
    met = greet(
        [(around(head, k, heads), blk) for k in range(1, heads)]
        + [(head, around(blk, k, blks)) for k in range(1, blks)]
    )
    lanes = lane_ids((rows, LANES))
    for copy in fetched:
        copy.wait()
    rows_in[0:experts, 0:rows] = wr_ref[...].astype(F32)
    rows_in[experts : experts + 1, 0:rows] = g2_ref[...].astype(F32)
    rows_in[experts + 1 : experts + 2, 0:rows] = g1_ref[...].astype(F32)
    vectors = jnp.transpose(rows_in[...])[:rows]
    gain = vectors[:, experts + 1 : experts + 2]

    def columns(which):
        start = pl.multiple_of(which * model + head * LANES, LANES)
        return w_ref[:, pl.ds(start, LANES)].astype(F32) * gain

    key_cols = columns(1)
    value_cols = pltpu.roll(columns(2), HALF, 1)
    wall[blk, :, 0:LANES] = jnp.where(lanes < HALF, key_cols, value_cols).astype(BF16)
    wall[blk, :, LANES : 2 * LANES] = jnp.where(lanes < HALF, value_cols, key_cols).astype(BF16)
    wall[blk, :, 2 * LANES : 3 * LANES] = (columns(0) * HS ** (-0.5)).astype(BF16)
    def slice_copy(slot, source, target):
        ref = wall.at[source]
        return remote(ref, ref, w_send.at[slot], w_recv.at[source], head, target)

    pair = 2 * z + around(y, 1, 2)
    line = [2 * around(z, step, planes) + y for step in (1, planes - 1, *range(2, planes - 1))]
    w_copies = [slice_copy(slot, blk, target) for slot, target in enumerate((*line, pair))]
    w_onward = [slice_copy(planes + slot, source, pair) for slot, source in enumerate(line)]
    xhat, _ = centre(x_ref[...].astype(F32))
    xall[head] = xhat.astype(BF16)
    meet(met)
    for copy in w_copies:
        copy.start()
    x_copies = [
        remote(xall.at[head], xall.at[head], x_send.at[k], x_recv.at[k], around(head, k, heads), blk)
        for k in range(1, heads)
    ]
    for copy in x_copies:
        copy.start()
    wo_own[:, model : model + LANES] = vectors.astype(BF16)
    wo_all[blk, head] = wo_own[pl.ds(pl.multiple_of(head * part, part), part), :]
    o_copies = [
        remote(
            wo_all.at[blk, head], wo_all.at[blk, head],
            o_send.at[k], o_recv.at[k], head, around(blk, k, blks),
        )
        for k in range(1, blks)
    ]
    document_bounds(docs_ref, bounds, z)
    for source, copy in zip(line, w_onward):
        arrived(wall.at[source], w_recv.at[source])
        copy.start()
    for copy in o_copies:
        copy.start()
    for source in (pair, *[other - y + around(y, 1, 2) for other in line]):
        arrived(wall.at[source], w_recv.at[source])
    for copy in w_copies + w_onward:
        copy.wait_send()
    for copy in x_copies:
        copy.wait()
    weight = wall[...].reshape(model, 3 * LANES)
    tokens = x_ref.shape[0]
    even = y == 0
    above, below = z < planes - 1, z > 0
    half_span = kvall.shape[1] // 2
    sides = ((1, above, below, 0), (-1, below, above, 4))

    def half_of(ref, half):
        return ref.at[pl.ds(half * half_span, half_span)]

    def outward(slot, step, across, half):
        target = 2 * (z + step) + around(y, across, 2)
        return remote(
            half_of(kv_other if across else kvall.at[blk], half), half_of(kvall.at[blk], half),
            k_send.at[slot], k_recv.at[blk, half], head, target,
        )

    def onward(slot, step, side, half):
        from_span = 2 * (z - step) + side
        ref = half_of(kvall.at[from_span], half)
        return remote(ref, ref, k_send.at[slot], k_recv.at[from_span, half], head, 2 * (z + step) + y)

    def await_half(span, half):
        arrived(half_of(kvall.at[span], half), k_recv.at[span, half])

    def turn(span):
        size = kvall.shape[1]
        kvt[:, pl.ds(pl.multiple_of(span * size, size), size)] = jnp.transpose(kvall[span])

    for half in range(2):
        for piece in range(half * heads // 2, (half + 1) * heads // 2):
            made = dot(xall[piece], weight).astype(BF16)
            first, second = made[:, 0:LANES], made[:, LANES : 2 * LANES]
            span = slice(piece * tokens, (piece + 1) * tokens)
            kvall[blk, span, :] = jnp.where(even, first, second)
            kv_other[span, :] = jnp.where(even, second, first)
            qall[y, span, :] = made[:, 2 * LANES : 3 * LANES]
        outward(8 + half, 0, 1, half).start()
        for step, there, _, slot in sides:

            @pl.when(there)
            def _():
                outward(slot + 2 * half, step, 0, half).start()
                outward(slot + 2 * half + 1, step, 1, half).start()

    other_y = around(y, 1, 2)
    kept = (lane_ids(q_packed.shape) < HALF) == (y == 1)
    q_packed[...] = halves(qall[y].astype(F32), kept).astype(BF16)
    q_pair = remote(q_packed, q_landed, k_send.at[10], q_recv, head, 2 * z + other_y)
    q_pair.start()
    turn(blk)
    for copy in o_copies:
        copy.wait()
    core = lax.rem(head, 2)
    sibling, across = head - core + 1 - core, around(head, 2, heads)

    def quarter_copy(index, quarter, to_head):
        ref = wo_all.at[:, quarter]
        return remote(ref, ref, p_send.at[index], p_recv.at[index], to_head, blk)

    p_copies = [quarter_copy(0, head, sibling), quarter_copy(1, head, across)]
    for copy in p_copies:
        copy.start()
    p_copies.append(quarter_copy(2, across, sibling))
    for half in range(2):
        for step, there, back, slot in sides:

            @pl.when(back)
            def _():
                for side in range(2):
                    await_half(2 * (z - step) + side, half)

            @pl.when(jnp.logical_and(there, back))
            def _():
                for side in range(2):
                    onward(11 + slot + 2 * half + side, step, side, half).start()

    arrived(wo_all.at[:, across], p_recv.at[1])
    p_copies[2].start()
    for half in range(2):
        await_half(pair, half)
    turn(pair)
    q_pair.wait()
    landed = q_landed[...]
    qall[other_y, 0:half_span, :] = landed
    qall[other_y, half_span : 2 * half_span, :] = pltpu.roll(landed.astype(F32), HALF, 1).astype(BF16)
    key_tile = kvall.shape[1]
    for group in range(2 * key_tile // (CHAINS * QUERY_TILE)):
        tiles, queries = query_group(qall, group, y)
        carry = (nothing_attended(),) * CHAINS
        for side in range(2):
            first = pl.multiple_of((2 * z + side) * key_tile, key_tile)
            keys_across = kvt[:, pl.ds(first, key_tile)]
            carry = attend(bounds, tiles, first, kvall[2 * z + side], keys_across, queries, carry)
        for tile, (biggest, weight, mixed) in zip(tiles, carry):
            begun[tile, 0:LANES] = mixed
            begun[tile, LANES : LANES + 8] = jnp.broadcast_to(biggest, (8, QUERY_TILE))
            begun[tile, LANES + 8 : LANES + 16] = jnp.broadcast_to(weight, (8, QUERY_TILE))
    for step, there, back, slot in sides:

        @pl.when(back)
        def _():
            for side in range(2):
                turn(2 * (z - step) + side)

    for other in range(planes):
        for side in range(2):
            span = 2 * other + side

            @pl.when(jnp.logical_or(z - other == 2, other - z == 2))
            def _():
                for half in range(2):
                    await_half(span, half)
                turn(span)

    for index, quarter in ((0, sibling), (2, around(sibling, 2, heads))):
        arrived(wo_all.at[:, quarter], p_recv.at[index])
    for copy in p_copies:
        copy.wait_send()
    for half in range(2):
        outward(8 + half, 0, 1, half).wait_send()
        for step, there, back, slot in sides:

            @pl.when(there)
            def _():
                outward(slot + 2 * half, step, 0, half).wait_send()
                outward(slot + 2 * half + 1, step, 1, half).wait_send()

            @pl.when(jnp.logical_and(there, back))
            def _():
                for side in range(2):
                    onward(11 + slot + 2 * half + side, step, side, half).wait_send()


def document_bounds(docs_ref, bounds, z):
    count = docs_ref.shape[1]
    lengths = docs_ref[...].astype(F32)
    doc = lax.broadcasted_iota(jnp.int32, (count, count), 0)
    other = lane_ids((count, count))
    start = jnp.sum(jnp.where(other < doc, lengths, 0.0), axis=1, keepdims=True)
    end = jnp.sum(jnp.where(other <= doc, lengths, 0.0), axis=1, keepdims=True)
    queries = bounds.shape[1]
    token = (z * queries + lane_ids((count, queries))).astype(F32)
    begun = start <= token
    bounds[...] = jnp.zeros_like(bounds)
    bounds[0:1, :] = jnp.max(jnp.where(begun, start, 0.0), axis=0, keepdims=True).astype(jnp.int32)
    bounds[1:2, :] = jnp.max(jnp.where(begun, end, 0.0), axis=0, keepdims=True).astype(jnp.int32)


def vmem_specs(count):
    return [pl.BlockSpec(memory_space=pltpu.VMEM)] * count


def hbm_specs(count):
    return [pl.BlockSpec(memory_space=pltpu.HBM)] * count


def in_hbm(*arrays):
    return [pltpu.with_memory_space_constraint(array, pltpu.HBM) for array in arrays]


def dma(*shape):
    return pltpu.SemaphoreType.DMA(shape)


def call_qkv(x, w_qkv, g1, w_out, w_router, g2, doc_lengths, heads, blks):
    tokens, model = x.shape
    rows = w_qkv.shape[0]
    span = tokens * heads
    wide = model + LANES
    part = rows // heads
    return pl.pallas_call(
        functools.partial(qkv_kernel, heads, blks),
        out_shape=(
            jax.ShapeDtypeStruct((2, span, LANES), BF16),
            jax.ShapeDtypeStruct((blks, span, LANES), BF16),
            jax.ShapeDtypeStruct((heads, tokens, model), BF16),
            jax.ShapeDtypeStruct((blks, rows, 3 * LANES), BF16),
            jax.ShapeDtypeStruct((blks, heads, part, wide), BF16),
            jax.ShapeDtypeStruct((LANES, blks * span), BF16),
            jax.ShapeDtypeStruct((8, 2 * span), jnp.int32),
            jax.ShapeDtypeStruct((2 * span // QUERY_TILE, LANES + 16, QUERY_TILE), F32),
        ),
        in_specs=hbm_specs(7),
        out_specs=tuple(vmem_specs(8)),
        scratch_shapes=[
            pltpu.VMEM((tokens, model), BF16),
            pltpu.VMEM((rows, 3 * model), BF16),
            pltpu.VMEM((LANES, LANES), F32),
            pltpu.VMEM((1, rows), BF16),
            pltpu.VMEM((1, rows), BF16),
            pltpu.VMEM((w_router.shape[1], rows), BF16),
            pltpu.VMEM((1, doc_lengths.shape[0]), jnp.int32),
            pltpu.VMEM((rows, wide), BF16),
            pltpu.VMEM((span, LANES), BF16),
            pltpu.VMEM((span // 2, LANES), BF16),
            pltpu.VMEM((span // 2, LANES), BF16),
            dma(7),
            dma(heads), dma(heads), dma(blks), dma(blks), dma(blks), dma(blks), dma(heads), dma(heads),
            dma(19), dma(blks, 2), pltpu.SemaphoreType.DMA,
        ],
        compiler_params=pltpu.CompilerParams(
            collective_id=1, has_side_effects=True, vmem_limit_bytes=16 * MIB
        ),
        name="qkv",
    )(
        *in_hbm(
            x, w_qkv, g1.reshape(1, rows), w_out, w_router.T, g2.reshape(1, rows),
            doc_lengths.reshape(1, -1),
        )
    )


def other_blocks(bounds_ref, group, key_tile, z, step, carry):
    low, high = group_blocks(bounds_ref, group, CHAINS * QUERY_TILE, key_tile)
    carry = lax.fori_loop(low, 2 * z, step, carry)
    return lax.fori_loop(2 * z + 2, high, step, carry)


def forward_kernel(bounds_ref, q_ref, kv_ref, kvt_ref, begun_ref, o_out, ob_out, lse_out):
    _, _, z, y = place()
    key_tile = kv_ref.shape[1]
    value_lanes = (lane_ids((HALF, LANES)) < HALF) == (y == 1)
    for group in range(q_ref.shape[0] * q_ref.shape[1] // (CHAINS * QUERY_TILE)):
        tiles, queries = query_group(q_ref, group, y)

        def step(block, carry, queries=queries, tiles=tiles):
            first = pl.multiple_of(block * key_tile, key_tile)
            across = kvt_ref[:, pl.ds(first, key_tile)]
            return attend(bounds_ref, tiles, first, kv_ref[block], across, queries, carry)

        start = tuple(
            (begun_ref[t, LANES : LANES + 1], begun_ref[t, LANES + 8 : LANES + 9], begun_ref[t, 0:LANES])
            for t in tiles
        )
        ends = other_blocks(bounds_ref, group, key_tile, z, step, start)
        for tile, (biggest, weight, mixed) in zip(tiles, ends):
            result = jnp.transpose(mixed / weight)
            o_out[tile] = result
            for part in range(QUERY_TILE // LANES):
                block = result[part * LANES : (part + 1) * LANES]
                ob_out[tile, part] = halves(block, value_lanes).astype(BF16)
            lse_out[tile] = jnp.broadcast_to(biggest + jnp.log(weight), (8, QUERY_TILE))


def call_forward(bounds, q, kv, kvt, begun):
    blks, span, _ = kv.shape
    tiles = 2 * span // QUERY_TILE
    return pl.pallas_call(
        forward_kernel,
        out_shape=(
            jax.ShapeDtypeStruct((tiles, QUERY_TILE, LANES), F32),
            jax.ShapeDtypeStruct((tiles, QUERY_TILE // LANES, HALF, LANES), BF16),
            jax.ShapeDtypeStruct((tiles, 8, QUERY_TILE), F32),
        ),
        in_specs=vmem_specs(5),
        out_specs=tuple(vmem_specs(3)),
        compiler_params=pltpu.CompilerParams(vmem_limit_bytes=16 * MIB),
        name="attend",
    )(bounds, q, kv, kvt, begun)


def backward_kernel(
    bounds_ref, q_ref, kv_ref, kvt_ref, do_ref, o_ref, lse_ref, dq_out, dkv_out, delta_out, dkv
):
    _, _, z, y = place()
    key_tile = kv_ref.shape[1]
    dkv[...] = jnp.zeros_like(dkv)
    for group in range(q_ref.shape[0] * q_ref.shape[1] // (CHAINS * QUERY_TILE)):
        tiles, queries = query_group(q_ref, group, y)
        out_grads = group_grads(do_ref, tiles, y)
        deltas, log_totals = [], []
        for tile, out_grad in zip(tiles, out_grads):
            product = jnp.transpose(out_grad.astype(F32) * o_ref[tile])
            deltas.append(jnp.sum(product, axis=0, keepdims=True))
            delta_out[tile] = jnp.broadcast_to(deltas[-1], delta_out.shape[1:])
            log_totals.append(lse_ref[tile, 0:1, :])
        known = (queries, out_grads, deltas, log_totals)

        def step(block, carry, tiles=tiles, known=known):
            first = pl.multiple_of(block * key_tile, key_tile)
            across = kvt_ref[:, pl.ds(first, key_tile)]
            given, carry = attend_back(bounds_ref, tiles, first, kv_ref[block], across, known, carry)
            dkv[block] += given
            return carry

        zero = jnp.zeros((LANES, QUERY_TILE), F32)
        ends = other_blocks(bounds_ref, group, key_tile, z, step, (zero,) * CHAINS)
        for tile, mixed in zip(tiles, ends):
            dq_out[tile] = mixed
    for block in range(dkv.shape[0]):
        dkv_out[block] = dkv[block].astype(BF16)


def call_backward(bounds, q, kv, kvt, d_o, o, lse):
    blks, span, _ = kv.shape
    tiles = 2 * span // QUERY_TILE
    return pl.pallas_call(
        backward_kernel,
        out_shape=(
            jax.ShapeDtypeStruct((tiles, LANES, QUERY_TILE), F32),
            jax.ShapeDtypeStruct((blks, span, LANES), BF16),
            jax.ShapeDtypeStruct((tiles, 8, QUERY_TILE), F32),
        ),
        in_specs=vmem_specs(7),
        out_specs=tuple(vmem_specs(3)),
        scratch_shapes=[pltpu.VMEM((blks, span, LANES), F32)],
        compiler_params=pltpu.CompilerParams(vmem_limit_bytes=16 * MIB),
        name="attend_back",
    )(bounds, q, kv, kvt, d_o, o, lse)


def gelu_parts(values):
    share = 0.5 * (1.0 + lax.erf(values * (2.0**-0.5)))
    slope = share + values * jnp.exp(-0.5 * values * values) * (2.0 * math.pi) ** -0.5
    return values * share, slope


def positions(expert_rows, expert_cols, rank_row, rank_col):
    def count(mask, axis):
        return jnp.sum(mask.astype(F32), axis=axis, keepdims=True)

    row = [None, None]
    col = [None, None]
    before = rank_col < rank_row
    after = rank_row < rank_col
    for choice in range(2):
        row[choice] = count((expert_cols[choice] == expert_rows[choice]) & before, 0)
        col[choice] = count((expert_rows[choice] == expert_cols[choice]) & after, 1)
    row[1] = row[1] + count(expert_cols[0] == expert_rows[1], 0)
    col[1] = col[1] + count(expert_rows[0] == expert_cols[1], 1)
    return row, col


def own_columns(rows_ref, turned, blk, capacity):
    blks, _, slots = rows_ref.shape
    rows = jnp.concatenate(
        [rows_ref[...].reshape(blks, slots), jnp.zeros((LANES - blks, slots), F32)], axis=0
    )
    for piece in range(slots // LANES):
        columns = slice(piece * LANES, (piece + 1) * LANES)
        turned[columns, :] = jnp.transpose(rows[:, columns])
    own = turned[pl.ds(pl.multiple_of(blk * capacity, capacity), capacity), :]
    return jnp.concatenate([own[:, source : source + 1] for source in range(blks)], axis=0)


def middle_kernel(
    heads, blks,
    x_hbm, o_ref, wo_ref, routes_hbm, rank_hbm, d_out_hbm, win_hbm, wout_hbm,
    po, hidden_ref, share_ref, dh_ref, dma_all, grads_ref, rx,
    x_ref, routes_ref, rank_ref, d_out_ref, win_ref, wout_ref, rows_in, in_sem,
    o_all, dos, doa, rs, ra, dr, da, dms, acc_out, acc_row, mix, gate_rows, d_gate_rows, turned,
    o_send, o_recv, dos_send, dos_recv, r_send, r_recv,
    dr_send, dr_recv, dm_send, dm_recv, rx_send, rx_recv, g_send, g_recv, dg_send, dg_recv,
):
    head, blk, z, y = place()
    tokens, model = x_ref.shape
    capacity = 2 * tokens // blks
    slots = capacity * blks
    plane = [(k % heads, k // heads) for k in range(1, 2 * heads)]
    wanted = (
        (routes_hbm, routes_ref), (rank_hbm, rank_ref), (d_out_hbm, d_out_ref), (x_hbm, x_ref),
        (win_hbm, win_ref), (wout_hbm, wout_ref),
    )
    fetched = [
        pltpu.make_async_copy(src, dst, in_sem.at[i]) for i, (src, dst) in enumerate(wanted)
    ]
    for copy in fetched:
        copy.start()
    met = greet(
        [(around(head, kh, heads), 2 * z + around(y, ky, 2)) for kh, ky in plane]
        + [(head, around(blk, k, blks)) for k in range(1, blks)]
    )
    meet(met)

    def plane_copies(src_of, dst, send, recv):
        copies = []
        for k, (kh, ky) in enumerate(plane):
            to_head, to_y = around(head, kh, heads), around(y, ky, 2)
            copies.append(
                remote(src_of(to_y, to_head), dst, send.at[k], recv.at[k], to_head, 2 * z + to_y)
            )
        return copies

    def blk_copies(src, dst, send, recv):
        return [
            remote(
                src.at[around(blk, k, blks)], dst.at[blk],
                send.at[k], recv.at[k], head, around(blk, k, blks),
            )
            for k in range(1, blks)
        ]

    def start(copies):
        for copy in copies:
            copy.start()

    def finish(copies):
        for copy in copies:
            copy.wait()

    o_copies = plane_copies(lambda to_y, to_head: o_ref.at[to_y, to_head], o_all.at[y, head], o_send, o_recv)
    start(o_copies)
    o_all[y, head] = o_ref[y, head]

    lanes = lane_ids((tokens, LANES))
    for copy in fetched[:4]:
        copy.wait()
    e_rows = [routes_ref[i : i + 1, :].astype(F32) for i in range(2)]
    rank_row = rank_ref[...].astype(F32)
    rows_in[...] = jnp.zeros_like(rows_in)
    rows_in[0:1, :], rows_in[1:2, :], rows_in[2:3, :] = *e_rows, rank_row
    columns = jnp.transpose(rows_in[...])
    e_cols = [columns[:, 0:1], columns[:, 1:2]]
    rank_col = columns[:, 2:3]
    pos_rows, pos_cols = positions(e_rows, e_cols, rank_row, rank_col)

    def slot_of(expert, position):
        return jnp.where(position < capacity, expert * capacity + position, -1.0).astype(jnp.int32)

    slot_rows = [slot_of(e, p) for e, p in zip(e_rows, pos_rows)]
    slot_cols = [slot_of(e, p) for e, p in zip(e_cols, pos_cols)]
    slot_down = lax.broadcasted_iota(jnp.int32, (slots, tokens), 0)
    slot_across = lane_ids((tokens, slots))
    pick = [(slot_down == s).astype(BF16) for s in slot_rows]
    put = [(slot_across == s).astype(BF16) for s in slot_cols]
    pick_any = pick[0] + pick[1]
    put_any = put[0] + put[1]

    d_out = d_out_ref[...]
    dos[...] = dot(pick_any, d_out.astype(BF16)).astype(BF16).reshape(dos.shape)
    dos_copies = blk_copies(dos, doa, dos_send, dos_recv)
    start(dos_copies)
    doa[blk] = dos[blk]

    weight_out = jnp.concatenate(
        [wo_ref[(b ^ 1) * HALF : ((b ^ 1) + 1) * HALF, 0:model] for b in range(blks)], axis=0
    )
    small = wo_ref[:, model : model + LANES]
    small_across = jnp.concatenate(
        [
            jnp.transpose(small[i * LANES : (i + 1) * LANES].astype(F32))
            for i in range(model // LANES)
        ],
        axis=1,
    )
    gain = small_across[blks : blks + 1, :]

    finish(o_copies)
    low_lanes = lanes[:HALF] < HALF
    for piece in range(heads):
        columns = slice(piece * LANES, (piece + 1) * LANES)
        first, second = o_all[1, piece].astype(F32), o_all[0, piece].astype(F32)
        mix[:HALF, columns] = jnp.where(low_lanes, first, second).astype(BF16)
        swapped = pltpu.roll(jnp.where(low_lanes, second, first), HALF, 1)
        mix[HALF:, columns] = swapped.astype(BF16)
    mixed = mix[...]
    hidden = x_ref[...].astype(F32) + dot(mixed, weight_out)
    xhat, scale = centre(hidden)
    routed = (xhat * gain).astype(BF16)
    rs[...] = dot(pick_any, routed).astype(BF16).reshape(rs.shape)
    r_copies = blk_copies(rs, ra, r_send, r_recv)
    start(r_copies)
    ra[blk] = rs[blk]
    logits = jnp.where(lanes < blks, dot(routed, small), MASKED)
    powers = jnp.exp(logits - jnp.max(logits, axis=1, keepdims=True))
    probs = powers / jnp.sum(powers, axis=1, keepdims=True)
    lanes_f = lanes.astype(F32)
    hots = [lanes_f == e for e in e_cols]
    gates = [jnp.sum(jnp.where(hot, probs, 0.0), axis=1, keepdims=True) for hot in hots]
    gate_high = [g.astype(BF16).astype(F32) for g in gates]
    gate_across = jnp.transpose(
        jnp.where(lanes == 0, gate_high[0], jnp.where(lanes == 1, gates[0] - gate_high[0], 0.0))
        + jnp.where(lanes == 2, gate_high[1], jnp.where(lanes == 3, gates[1] - gate_high[1], 0.0))
    ).astype(BF16)
    by_slot = (dot(gate_across, put[0]), dot(gate_across, put[1]))
    gate_rows[blk] = by_slot[0][0:1] + by_slot[0][1:2] + by_slot[1][2:3] + by_slot[1][3:4]
    g_copies = [
        remote(
            gate_rows.at[blk], gate_rows.at[blk],
            g_send.at[k], g_recv.at[k], head, around(blk, k, blks),
        )
        for k in range(1, blks)
    ]
    start(g_copies)
    acc_out[...] = jnp.zeros_like(acc_out)
    acc_row[...] = jnp.zeros_like(acc_row)
    finish(dos_copies)
    finish(r_copies)

    out_rows = doa[...].reshape(slots, model)
    rx[head, :, 0:model] = ra[...].reshape(slots, model)
    finish(g_copies)
    gate_col = own_columns(gate_rows, turned, blk, capacity)
    rx[head, :, model : 2 * model] = (out_rows.astype(F32) * gate_col).astype(BF16)
    core = lax.rem(head, 2)
    sibling, across = head - core + 1 - core, around(head, 2, heads)

    def half_rows(source, half):
        return rx.at[source, pl.ds(half * slots // 2, slots // 2)]

    to_across = [
        remote(
            half_rows(head, half), half_rows(head, half),
            rx_send.at[1 + half], rx_recv.at[1 + half], across, blk,
        )
        for half in range(2)
    ]
    to_sibling = remote(rx.at[head], rx.at[head], rx_send.at[0], rx_recv.at[0], sibling, blk)
    forwards = [
        remote(
            half_rows(across, half), half_rows(across, half),
            rx_send.at[3 + half], rx_recv.at[3 + half], sibling, blk,
        )
        for half in range(2)
    ]
    start(to_across)
    to_sibling.start()
    half_ff = wout_ref.shape[0] // 4
    for copy in fetched[4:]:
        copy.wait()

    @pl.loop(0, 4)
    def _(chunk):
        first = pl.multiple_of(chunk * half_ff, half_ff)
        into = win_ref[:, pl.ds(first, half_ff)]
        outof = wout_ref[pl.ds(first, half_ff), :]
        act, slope = gelu_parts(dot(rx[head, :, 0:model], into))
        acc_out[...] += dot(act.astype(BF16), outof)
        d_act = dot(rx[head, :, model : 2 * model], outof, (1, 1))
        acc_row[...] += dot((slope * d_act).astype(BF16), into, (1, 1))

    result = acc_out[...].astype(BF16)
    d_gate = jnp.sum(out_rows.astype(F32) * result.astype(F32), axis=1, keepdims=True)
    dr[...] = acc_row[...].astype(BF16).reshape(dr.shape)
    dr_copies = blk_copies(dr, da, dr_send, dr_recv)
    start(dr_copies)
    da[blk] = dr[blk]
    d_wide = jnp.broadcast_to(d_gate, (slots, LANES))
    d_gate_rows[blk] = jnp.concatenate(
        [jnp.transpose(d_wide[i * LANES : (i + 1) * LANES])[0:1] for i in range(slots // LANES)],
        axis=1,
    )
    dg_copies = [
        remote(
            d_gate_rows.at[blk], d_gate_rows.at[blk],
            dg_send.at[k], dg_recv.at[k], head, around(blk, k, blks),
        )
        for k in range(1, blks)
    ]
    start(dg_copies)
    po[...] = result.reshape(blks, capacity, model)

    finish(dg_copies)
    back_gate = own_columns(d_gate_rows, turned, blk, capacity)
    back_gate = split_high_low(back_gate, lane_ids((slots, LANES)))
    d_gates = [join_high_low(dot(p, back_gate), 0) for p in put]
    d_probs = jnp.where(hots[0], d_gates[0], 0.0) + jnp.where(hots[1], d_gates[1], 0.0)
    d_logits = probs * (d_probs - jnp.sum(probs * d_probs, axis=1, keepdims=True))
    d_high = d_logits.astype(BF16)
    d_low = (d_logits - d_high.astype(F32)).astype(BF16)
    d_router_part = dot(d_high, small, (1, 1)) + dot(d_low, small, (1, 1))
    finish(dr_copies)
    d_routed = dot(put_any, da[...].reshape(slots, model)) + d_router_part
    d_hidden = d_out + centre_back(d_routed * gain, xhat, scale)
    dh_ref[...] = d_hidden
    d_attn = d_hidden.astype(BF16)
    d_mixed = dot(d_attn, weight_out, (1, 1))
    for piece in range(heads):
        block = d_mixed[:, piece * LANES : (piece + 1) * LANES]
        for to_y in range(2):
            dms[to_y, piece] = halves(block, low_lanes == (to_y == 1)).astype(BF16)
    dm_copies = plane_copies(lambda to_y, to_head: dms.at[to_y, to_head], dma_all.at[y, head], dm_send, dm_recv)
    start(dm_copies)
    dma_all[y, head] = dms[y, head]
    arrived(half_rows(across, 0), rx_recv.at[1])
    forwards[0].start()

    d_weight = dot(mixed, d_attn, (0, 0)).astype(BF16)
    for b in range(blks):
        grads_ref[b, :, 0:model] = d_weight[(b ^ 1) * HALF : ((b ^ 1) + 1) * HALF, :]
    last = (lanes == blks).astype(BF16)
    d_small = dot(routed, d_high, (0, 0)) + dot((d_routed * xhat).astype(BF16), last, (0, 0))
    grads_ref[:, :, model : model + LANES] = d_small.astype(BF16).reshape(blks, HALF, LANES)
    share = gates[0] * put[0].astype(F32) + gates[1] * put[1].astype(F32)
    share_ref[0] = share.astype(BF16)
    share_ref[1] = (share - share_ref[0].astype(F32)).astype(BF16)
    hidden_ref[...] = hidden

    arrived(half_rows(across, 1), rx_recv.at[2])
    forwards[1].start()
    finish(dm_copies)
    to_sibling.wait()
    for copy in to_across:
        copy.wait_send()
    finish(forwards)


def call_middle(x, o, wo, routes, rank, d_out, win, wout, heads, blks):
    tokens, model = x.shape
    capacity = 2 * tokens // blks
    slots = capacity * blks
    wide = model + LANES

    def rows(width):
        return pltpu.VMEM((blks, capacity, width), BF16)

    def block(*lead):
        return pltpu.VMEM((*lead, tokens // 2, LANES), BF16)

    return pl.pallas_call(
        functools.partial(middle_kernel, heads, blks),
        out_shape=(
            jax.ShapeDtypeStruct((blks, capacity, model), BF16),
            jax.ShapeDtypeStruct((tokens, model), F32),
            jax.ShapeDtypeStruct((2, tokens, slots), BF16),
            jax.ShapeDtypeStruct((tokens, model), F32),
            jax.ShapeDtypeStruct((2, heads, tokens // 2, LANES), BF16),
            jax.ShapeDtypeStruct((blks, model // blks, wide), BF16),
            jax.ShapeDtypeStruct((heads, slots, 2 * model), BF16),
        ),
        in_specs=hbm_specs(1) + vmem_specs(2) + hbm_specs(5),
        out_specs=tuple(vmem_specs(7)),
        scratch_shapes=[
            pltpu.VMEM((tokens, model), BF16),
            pltpu.VMEM((2, tokens), jnp.int32),
            pltpu.VMEM((1, tokens), jnp.int32),
            pltpu.VMEM((tokens, model), F32),
            pltpu.VMEM(win.shape, BF16),
            pltpu.VMEM(wout.shape, BF16),
            pltpu.VMEM((tokens, tokens), F32),
            dma(6),
            block(2, heads), rows(model), rows(model), rows(model), rows(model),
            rows(model), rows(model), block(2, heads),
            pltpu.VMEM((slots, model), F32), pltpu.VMEM((slots, model), F32),
            pltpu.VMEM((tokens, model), BF16),
            pltpu.VMEM((blks, 1, slots), F32), pltpu.VMEM((blks, 1, slots), F32),
            pltpu.VMEM((slots, LANES), F32),
            dma(2 * heads), dma(2 * heads), dma(blks), dma(blks), dma(blks), dma(blks),
            dma(blks), dma(blks), dma(2 * heads), dma(2 * heads), dma(5), dma(5),
            dma(blks), dma(blks), dma(blks), dma(blks),
        ],
        compiler_params=pltpu.CompilerParams(
            collective_id=2, has_side_effects=True, vmem_limit_bytes=20 * MIB
        ),
        name="experts",
    )(*in_hbm(x), o, wo, *in_hbm(routes.T, rank, d_out, win, wout))


def last_kernel(
    heads, blks,
    x_hbm, dh_ref, begun_ref, dkv_ref, xa_ref, wa_ref, w_hbm, g1_hbm, grads_ref, rx_ref, win_hbm, wout_hbm,
    po_ref, hidden_ref, share_ref, bounds_ref, q_ref, kv_ref, kvt_ref, do_ref, lse_ref, delta_ref,
    y_ref, dx_ref, dw_ref, shared_ref, din_ref, dout_ref,
    x_ref, w_ref, g1_ref, win_ref, wout_ref, in_sem,
    gain_tile, far_all, near_send_buf, near_all, pair_all, dq_all, dq_ref, dq_packed, dkv_own, pair_buf, us, ua, gs, ga, gqs, gqa, u_part, xat, pa, gh, ghq, w1, w2s, w2, w3,
    q_send, q_recv, pair_send, pair_recv, far_send, far_recv, near_send, near_recv,
    u_send, u_recv, g_send, g_recv, gh_send, gh_recv, w1_send, w1_recv, w2_send, w2_recv,
    w3_send, w3_recv, e_send, e_recv, gq_send, gq_recv, po_send, po_recv, ghq_send, ghq_recv,
    din_half, dout_half,
):
    head, blk, z, y = place()
    planes = blks // 2
    tokens, model = x_ref.shape
    rows = w_ref.shape[0]
    wanted = (
        (win_hbm, win_ref), (wout_hbm, wout_ref), (x_hbm, x_ref), (w_hbm, w_ref), (g1_hbm, g1_ref)
    )
    fetched = [
        pltpu.make_async_copy(src, dst, in_sem.at[i]) for i, (src, dst) in enumerate(wanted)
    ]
    for copy in fetched:
        copy.start()
    met = greet(
        [(around(head, k, heads), blk) for k in range(1, heads)]
        + [(head, around(blk, k, blks)) for k in range(1, blks)]
    )
    meet(met)

    def start(copies):
        for copy in copies:
            copy.start()

    def finish(copies):
        for copy in copies:
            copy.wait()

    other_y = around(y, 1, 2)
    pair = 2 * z + other_y
    above, below = z < planes - 1, z > 0
    directions = ((1, above, below, 0), (-1, below, above, 2))

    half_span = dkv_ref.shape[1] // 2

    def half_of(ref, half):
        return ref.at[pl.ds(half * half_span, half_span)]

    def far_copy(step, slot, side, half):
        span = 2 * (z + 2 * step) + side
        return remote(
            half_of(dkv_ref.at[span], half), half_of(far_all.at[slot + side], half),
            far_send.at[slot + side, half], far_recv.at[slot + side, half], head, 2 * (z + step) + y,
        )

    def near_copy(step, slot, side, half):
        return remote(
            half_of(near_send_buf.at[slot + side], half), half_of(near_all.at[slot // 2, y], half),
            near_send.at[slot + side, half], near_recv.at[slot // 2, y, half],
            head, 2 * (z + step) + side,
        )

    def two_away(step):
        return z + 2 * step < planes if step > 0 else z + 2 * step >= 0

    for half in range(2):
        for step, there, back, slot in directions:

            @pl.when(two_away(step))
            def _():
                for side in range(2):
                    far_copy(step, slot, side, half).start()

    w1_copies = [
        remote(
            grads_ref.at[:, around(head, k, heads)], w1.at[head],
            w1_send.at[k], w1_recv.at[k], around(head, k, heads), blk,
        )
        for k in range(1, heads)
    ]
    start(w1_copies)
    w1[head] = grads_ref[:, head]

    core = lax.rem(head, 2)
    sibling = head - core + 1 - core
    ff_half = wout_ref.shape[0] // 2
    ff_step = ff_half // 4

    def expert_chunk(chunk):
        here = pl.multiple_of(core * ff_half + chunk * ff_step, ff_step)
        there = pl.multiple_of(chunk * ff_step, ff_step)
        into = win_ref[:, pl.ds(here, ff_step)]
        outof = wout_ref[pl.ds(here, ff_step), :]
        d_in = jnp.zeros((model, ff_step), F32)
        d_out = jnp.zeros((ff_step, model), F32)
        for source in range(heads):
            rows_in = rx_ref[source, :, 0:model]
            grads_out = rx_ref[source, :, model : 2 * model]
            act, slope = gelu_parts(dot(rows_in, into))
            d_act = dot(grads_out, outof, (1, 1))
            d_in = d_in + dot(rows_in, (slope * d_act).astype(BF16), (0, 0))
            d_out = d_out + dot(act.astype(BF16), grads_out, (0, 0))
        din_ref[:, pl.ds(here, ff_step)] = d_in
        dout_ref[pl.ds(here, ff_step), :] = d_out
        din_half[core, :, pl.ds(there, ff_step)] = d_in.astype(BF16)
        dout_half[core, pl.ds(there, ff_step), :] = d_out.astype(BF16)

    key_tile = kv_ref.shape[1]
    for group in range(2 * key_tile // (CHAINS * QUERY_TILE)):
        tiles, queries = query_group(q_ref, group, y)
        known = (
            queries,
            group_grads(do_ref, tiles, y),
            [delta_ref[tile, 0:1, :] for tile in tiles],
            [lse_ref[tile, 0:1, :] for tile in tiles],
        )
        carry = tuple(begun_ref[tile] for tile in tiles)
        for side in range(2):
            first = pl.multiple_of((2 * z + side) * key_tile, key_tile)
            keys_across = kvt_ref[:, pl.ds(first, key_tile)]
            given, carry = attend_back(
                bounds_ref, tiles, first, kv_ref[2 * z + side], keys_across, known, carry
            )
            dkv_own[side] = given if group == 0 else dkv_own[side] + given
        for tile, total in zip(tiles, carry):
            at = tile * QUERY_TILE % key_tile
            dq_ref[tile * QUERY_TILE // key_tile, at : at + QUERY_TILE] = jnp.transpose(total)
    pair_buf[...] = dkv_own[other_y].astype(BF16)
    pair_copy = remote(pair_buf, pair_all, pair_send, pair_recv, head, pair)
    pair_copy.start()
    own_lanes = (lane_ids(dq_packed.shape) < HALF) == (y == 0)
    dq_packed[...] = halves(dq_ref[other_y], own_lanes).astype(BF16)
    q_copy = remote(dq_packed, dq_all, q_send, q_recv, head, pair)
    q_copy.start()
    for half in range(2):
        rows_here = slice(half * half_span, (half + 1) * half_span)
        for step, there, back, slot in directions:

            @pl.when(there)
            def _():
                for side in range(2):
                    near_send_buf[slot + side, rows_here] = dkv_ref[2 * (z + step) + side, rows_here]

            @pl.when(jnp.logical_and(there, back))
            def _():
                for side in range(2):
                    arrived(half_of(far_all.at[slot + side], half), far_recv.at[slot + side, half])
                    near_send_buf[slot + side, rows_here] = (
                        near_send_buf[slot + side, rows_here].astype(F32)
                        + far_all[slot + side, rows_here].astype(F32)
                    ).astype(BF16)

            @pl.when(there)
            def _():
                for side in range(2):
                    near_copy(step, slot, side, half).start()

    finish(fetched[:2])
    weight = wa_ref[...].reshape(model, 3 * LANES)
    for piece in range(heads):
        xat[:, piece * tokens : (piece + 1) * tokens] = jnp.transpose(xa_ref[piece])
    even = y == 0


    @pl.loop(0, 2)
    def _(chunk):
        expert_chunk(chunk)

    q_copy.wait()
    landed = dq_all[...].astype(F32)
    landed = jnp.concatenate([landed, pltpu.roll(landed, HALF, 1)], axis=0)
    own_lanes = (lane_ids(landed.shape) < HALF) == even
    q_grads = jnp.where(own_lanes, dq_ref[y], landed).astype(BF16)
    gqs[...] = dot(xat[...], q_grads).astype(BF16).reshape(gqs.shape)
    gq_copies = [
        remote(
            gqs.at[around(blk, k, blks)], gqa.at[blk],
            gq_send.at[k], gq_recv.at[k], head, around(blk, k, blks),
        )
        for k in range(1, blks)
    ]
    start(gq_copies)
    gqa[blk] = gqs[blk]
    u_part[...] = dot(q_grads, weight[:, 2 * LANES : 3 * LANES], (1, 1)).reshape(u_part.shape)

    finish(w1_copies)
    summed = w1[0].astype(F32)
    for source in range(1, heads):
        summed = summed + w1[source].astype(F32)
    w2s[...] = summed.astype(BF16)
    w2_copies = [
        remote(
            w2s.at[around(blk, k, blks)], w2.at[blk],
            w2_send.at[k], w2_recv.at[k], head, around(blk, k, blks),
        )
        for k in range(1, blks)
    ]
    start(w2_copies)
    w2[blk] = w2s[blk]

    @pl.loop(2, 4)
    def _(chunk):
        expert_chunk(chunk)

    e_copies = [
        remote(din_half.at[core], din_half.at[core], e_send.at[0], e_recv.at[0], sibling, blk),
        remote(dout_half.at[core], dout_half.at[core], e_send.at[1], e_recv.at[1], sibling, blk),
    ]
    start(e_copies)

    pair_copy.wait()
    for step, there, back, slot in directions:

        @pl.when(back)
        def _():
            for side in range(2):
                for half in range(2):
                    arrived(
                        half_of(near_all.at[slot // 2, side], half),
                        near_recv.at[slot // 2, side, half],
                    )

        @pl.when(jnp.logical_not(back))
        def _():
            near_all[slot // 2] = jnp.zeros(near_all.shape[1:], BF16)

    own = dkv_own[y]
    other = pair_all[...].astype(F32)
    made = jnp.concatenate(
        [
            (
                jnp.where(even == (side == 0), own, other)
                + near_all[0, side].astype(F32)
                + near_all[1, side].astype(F32)
            ).astype(BF16)
            for side in range(2)
        ],
        axis=1,
    )
    gs[...] = dot(xat[...], made).astype(BF16).reshape(gs.shape)
    g_copies = [
        remote(
            gs.at[around(blk, k, blks)], ga.at[blk],
            g_send.at[k], g_recv.at[k], head, around(blk, k, blks),
        )
        for k in range(1, blks)
    ]
    start(g_copies)
    ga[blk] = gs[blk]
    us[...] = (
        u_part[...] + dot(made, weight[:, 0 : 2 * LANES], (1, 1)).reshape(us.shape)
    ).astype(BF16)
    u_copies = [
        remote(
            us.at[around(head, k, heads)], ua.at[head],
            u_send.at[k], u_recv.at[k], around(head, k, heads), blk,
        )
        for k in range(1, heads)
    ]
    start(u_copies)
    ua[head] = us[head]
    finish(fetched[2:])
    finish(gq_copies)
    total = gqa[0].astype(F32)
    for source in range(1, blks):
        total = total + gqa[source].astype(F32)
    ghq[head] = total.astype(BF16)
    ghq_copies = [
        remote(ghq.at[head], ghq.at[head], ghq_send.at[k], ghq_recv.at[k], around(head, k, heads), blk)
        for k in range(1, heads)
    ]
    start(ghq_copies)

    finish(w2_copies)
    part = w2[0].astype(F32)
    for source in range(1, blks):
        part = part + w2[source].astype(F32)
    w3[head] = part.astype(BF16)
    w3_copies = [
        remote(w3.at[head], w3.at[head], w3_send.at[k], w3_recv.at[k], around(head, k, heads), blk)
        for k in range(1, heads)
    ]
    start(w3_copies)

    xhat, scale = centre(x_ref[...].astype(F32))
    finish(e_copies)
    there = pl.multiple_of((1 - core) * ff_half, ff_half)
    din_ref[:, pl.ds(there, ff_half)] = din_half[1 - core].astype(F32)
    dout_ref[pl.ds(there, ff_half), :] = dout_half[1 - core].astype(F32)
    finish(g_copies)
    total = ga[0].astype(F32)
    for source in range(1, blks):
        total = total + ga[source].astype(F32)
    gh[head] = total.astype(BF16)
    gh_copies = [
        remote(gh.at[head], gh.at[head], gh_send.at[k], gh_recv.at[k], around(head, k, heads), blk)
        for k in range(1, heads)
    ]
    start(gh_copies)
    po_copies = [
        remote(
            po_ref.at[around(blk, k, blks)], pa.at[blk],
            po_send.at[k], po_recv.at[k], head, around(blk, k, blks),
        )
        for k in range(1, blks)
    ]
    start(po_copies)
    pa[blk] = po_ref[blk]
    finish(u_copies)
    grad = ua[0].astype(F32)
    for source in range(1, heads):
        grad = grad + ua[source].astype(F32)
    dx_ref[...] = dh_ref[...] + centre_back(grad, xhat, scale)

    gain_tile[...] = jnp.zeros_like(gain_tile)
    gain_tile[0:1, 0:rows] = g1_ref[...].astype(F32)
    gain = jnp.transpose(jnp.broadcast_to(gain_tile[0:1, :], (LANES, LANES)))[:rows]
    low_half = lane_ids((rows, LANES)) < HALF
    finish(ghq_copies)
    finish(gh_copies)
    d_gain = jnp.zeros((rows, LANES), F32)
    for source in range(heads):
        both = [gh[source, :, i * LANES : (i + 1) * LANES].astype(F32) for i in range(2)]
        grads = (
            ghq[source].astype(F32) * HS ** (-0.5),
            jnp.where(low_half, both[0], both[1]),
            pltpu.roll(jnp.where(low_half, both[1], both[0]), HALF, 1),
        )
        for which, value in enumerate(grads):
            columns = slice(which * model + source * LANES, which * model + (source + 1) * LANES)
            d_gain = d_gain + value * w_ref[:, columns].astype(F32)
            dw_ref[:, columns] = value * gain
    finish(w3_copies)
    shared = w3[...].reshape(rows, w3.shape[-1]).astype(F32)
    shared_ref[:, 0:model] = shared[:, 0:model]
    gain_col = jnp.sum(d_gain, axis=1, keepdims=True)
    shared_ref[:, model : model + LANES] = jnp.where(
        lane_ids((rows, LANES)) == blks + 1, gain_col, shared[:, model : model + LANES]
    )
    finish(po_copies)
    parts = pa[...].reshape(share_ref.shape[2], model)
    mixture = dot(share_ref[0], parts) + dot(share_ref[1], parts)
    y_ref[...] = (hidden_ref[...] + mixture).astype(BF16)

    for step, there, back, slot in directions:

        @pl.when(two_away(step))
        def _():
            for side in range(2):
                for half in range(2):
                    far_copy(step, slot, side, half).wait_send()

        @pl.when(there)
        def _():
            for side in range(2):
                for half in range(2):
                    near_copy(step, slot, side, half).wait_send()


def call_last(
    x, dh, dq, dkv, xa, wa, w_qkv, g1, grads, rx, win, wout, po, hidden, share,
    bounds, q, kv, kvt, d_o, lse, delta, heads, blks,
):
    tokens, model = x.shape
    span = tokens * heads
    rows = w_qkv.shape[0]
    wide = model + LANES
    part = rows // heads
    ff = wout.shape[0]

    def block(*lead):
        return pltpu.VMEM((*lead, span, LANES), BF16)

    return pl.pallas_call(
        functools.partial(last_kernel, heads, blks),
        out_shape=(
            jax.ShapeDtypeStruct((tokens, model), BF16),
            jax.ShapeDtypeStruct((tokens, model), F32),
            jax.ShapeDtypeStruct((rows, 3 * model), F32),
            jax.ShapeDtypeStruct((rows, wide), F32),
            jax.ShapeDtypeStruct((model, ff), F32),
            jax.ShapeDtypeStruct((ff, model), F32),
        ),
        in_specs=hbm_specs(1) + vmem_specs(5) + hbm_specs(2) + vmem_specs(2) + hbm_specs(2) + vmem_specs(10),
        out_specs=tuple(vmem_specs(6)),
        scratch_shapes=[
            pltpu.VMEM((tokens, model), BF16),
            pltpu.VMEM((rows, 3 * model), BF16),
            pltpu.VMEM((1, rows), BF16),
            pltpu.VMEM(win.shape, BF16),
            pltpu.VMEM(wout.shape, BF16),
            dma(5),
            pltpu.VMEM((8, LANES), F32),
            block(4), block(4), block(2, 2), block(), pltpu.VMEM((span // 2, LANES), BF16),
            pltpu.VMEM((2, span, LANES), F32), pltpu.VMEM((span // 2, LANES), BF16),
            pltpu.VMEM((2, span, LANES), F32), block(),
            pltpu.VMEM((heads, tokens, model), BF16), pltpu.VMEM((heads, tokens, model), BF16),
            pltpu.VMEM((blks, rows, 2 * LANES), BF16), pltpu.VMEM((blks, rows, 2 * LANES), BF16),
            pltpu.VMEM((blks, rows, LANES), BF16), pltpu.VMEM((blks, rows, LANES), BF16),
            pltpu.VMEM((heads, tokens, model), F32), pltpu.VMEM((model, span), BF16),
            pltpu.VMEM(po.shape, BF16),
            pltpu.VMEM((heads, rows, 2 * LANES), BF16), pltpu.VMEM((heads, rows, LANES), BF16),
            pltpu.VMEM((heads, blks, part, wide), BF16), pltpu.VMEM((blks, part, wide), BF16),
            pltpu.VMEM((blks, part, wide), BF16), pltpu.VMEM((heads, part, wide), BF16),
            pltpu.SemaphoreType.DMA, pltpu.SemaphoreType.DMA, pltpu.SemaphoreType.DMA, pltpu.SemaphoreType.DMA,
            dma(4, 2), dma(4, 2), dma(4, 2), dma(2, 2, 2),
            dma(heads), dma(heads), dma(blks), dma(blks), dma(heads), dma(heads), dma(heads), dma(heads),
            dma(blks), dma(blks), dma(heads), dma(heads), dma(2), dma(2), dma(blks), dma(blks), dma(blks), dma(blks), dma(heads), dma(heads),
            pltpu.VMEM((2, model, ff // 2), BF16), pltpu.VMEM((2, ff // 2, model), BF16),
        ],
        compiler_params=pltpu.CompilerParams(
            collective_id=3, has_side_effects=True, vmem_limit_bytes=36 * MIB
        ),
        name="last",
    )(
        *in_hbm(x), dh, dq, dkv, xa, wa, *in_hbm(w_qkv, g1.reshape(1, rows)),
        grads.reshape(blks, heads, part, wide), rx, *in_hbm(win, wout), po, hidden, share,
        bounds, q, kv, kvt, d_o, lse, delta,
    )


def finish_kernel(
    experts,
    y_ref, dx_ref, dw_ref, shared_ref, din_ref, dout_ref,
    y_out, dx_out, g1_out, dw_out, dwo_out, g2_out, wr_out, din_out, dout_out,
    tile, wr, g2, g1, sem,
):
    rows = shared_ref.shape[0]
    model = dx_ref.shape[1]
    copies = [
        pltpu.make_async_copy(dx_ref, dx_out, sem.at[0]),
        pltpu.make_async_copy(dw_ref, dw_out, sem.at[1]),
        pltpu.make_async_copy(shared_ref.at[:, pl.ds(0, model)], dwo_out, sem.at[2]),
        pltpu.make_async_copy(y_ref, y_out, sem.at[6]),
        pltpu.make_async_copy(din_ref, din_out, sem.at[7]),
        pltpu.make_async_copy(dout_ref, dout_out, sem.at[8]),
    ]
    for copy in copies:
        copy.start()
    tile[...] = jnp.zeros_like(tile)
    tile[0:rows, :] = shared_ref[:, model : model + LANES]
    across = jnp.transpose(tile[...])[:, 0:rows]
    wr[...] = across[0:experts]
    g2[...] = across[experts : experts + 1]
    g1[...] = across[experts + 1 : experts + 2]
    for index, (src, dst) in enumerate(((wr, wr_out), (g2, g2_out), (g1, g1_out))):
        copies.append(pltpu.make_async_copy(src, dst, sem.at[3 + index]))
        copies[-1].start()
    for copy in copies:
        copy.wait()


def call_finish(output, dx, dw, shared, d_in, d_out):
    rows = shared.shape[0]
    model = dx.shape[1]
    experts = model // rows
    return pl.pallas_call(
        functools.partial(finish_kernel, experts),
        out_shape=(
            jax.ShapeDtypeStruct(output.shape, BF16),
            jax.ShapeDtypeStruct(dx.shape, F32),
            jax.ShapeDtypeStruct((1, rows), F32),
            jax.ShapeDtypeStruct(dw.shape, F32),
            jax.ShapeDtypeStruct((rows, model), F32),
            jax.ShapeDtypeStruct((1, rows), F32),
            jax.ShapeDtypeStruct((experts, rows), F32),
            jax.ShapeDtypeStruct(d_in.shape, F32),
            jax.ShapeDtypeStruct(d_out.shape, F32),
        ),
        in_specs=vmem_specs(6),
        out_specs=tuple(hbm_specs(9)),
        scratch_shapes=[
            pltpu.VMEM((LANES, LANES), F32),
            pltpu.VMEM((experts, rows), F32),
            pltpu.VMEM((1, rows), F32),
            pltpu.VMEM((1, rows), F32),
            dma(9),
        ],
        compiler_params=pltpu.CompilerParams(vmem_limit_bytes=16 * MIB),
        name="finish",
    )(output, dx, dw, shared, d_in, d_out)


def local_kernels(
    inputs, ln1_gain, w_qkv, w_out, ln2_gain, w_router,
    expert_in, expert_out, routes, priority, doc_lengths, d_out,
):
    heads, blks = lax.axis_size("head"), lax.axis_size("blk")
    model = inputs.shape[1]
    tokens = inputs.shape[0]
    win, wout = expert_in[0], expert_out[0]
    q, kv, xa, wa, wo, kvt, bounds, begun = call_qkv(
        inputs, w_qkv, ln1_gain, w_out, w_router, ln2_gain, doc_lengths, heads, blks
    )
    o, o_low, lse = call_forward(bounds, q, kv, kvt, begun)
    po, hidden, share, dh, d_o, grads, rx = call_middle(
        inputs, o_low.reshape(2, heads, tokens // 2, LANES), wo.reshape(model, model + LANES),
        routes, priority, d_out, win, wout, heads, blks,
    )
    d_o = d_o.reshape(2 * heads * tokens // QUERY_TILE, -1, HALF, LANES)
    dq, dkv, delta = call_backward(bounds, q, kv, kvt, d_o, o, lse)
    ends = call_last(
        inputs, dh, dq, dkv, xa, wa, w_qkv, ln1_gain, grads, rx, win, wout,
        po, hidden, share, bounds, q, kv, kvt, d_o, lse, delta, heads, blks,
    )
    output, d_inputs, d_gain_one, d_qkv, d_out_proj, d_gain_two, d_router, d_in, d_out_weight = call_finish(*ends)
    return (
        output,
        d_inputs,
        d_gain_one.reshape(-1),
        d_qkv,
        d_out_proj,
        d_gain_two.reshape(-1),
        d_router.T,
        d_in[None],
        d_out_weight[None],
    )


def solution(mesh):
    in_specs = (
        P(("blk", "head"), None),
        P("blk"),
        P("blk", None),
        P("blk", None),
        P("blk"),
        P("blk", None),
        P("blk", None, None),
        P("blk", None, None),
        P(("blk", "head"), None),
        P(("blk", "head"), None),
        P(),
        P(("blk", "head"), None),
    )
    out_specs = (
        P(("blk", "head"), None),
        P(("blk", "head"), None),
        P("blk"),
        P("blk", None),
        P("blk", None),
        P("blk"),
        P("blk", None),
        P("blk", None, None),
        P("blk", None, None),
    )
    fits = mesh.shape["head"] == 4 and mesh.shape["blk"] == 8
    body = local_kernels if fits else local
    return jax.shard_map(body, mesh=mesh, in_specs=in_specs, out_specs=out_specs, check_vma=False)
```

```python
import functools
import math

import jax
import jax.numpy as jnp
from jax import lax
from jax.experimental import pallas as pl
from jax.experimental.pallas import tpu as pltpu
from jax.sharding import PartitionSpec as P

HS = 64
KEY_BLOCK = 2048


PRECISE = lax.Precision.HIGHEST
MASKED = -1e30
EPSILON = 1e-06


def layer_norm(values, gain):
    average = jnp.mean(values, axis=-1, keepdims=True)
    centred = values - average
    spread = jnp.mean(centred * centred, axis=-1, keepdims=True)
    return centred * lax.rsqrt(spread + EPSILON) * gain


def gelu_exact(values):
    return jax.nn.gelu(values, approximate=False)


def router(row_block, weight):
    return jax.nn.softmax(jnp.dot(row_block, weight, precision=PRECISE), axis=-1)


def doc_index(positions, doc_lengths):
    places = jnp.arange(doc_lengths.shape[0], dtype=jnp.int32)
    starts = jnp.sum(jnp.where(places[None, :] < places[:, None], doc_lengths[None, :], 0), axis=1)
    at_most = (starts[None, :] <= positions[:, None]).astype(jnp.int32)
    return jnp.sum(at_most, axis=1) - 1


def slot_table(route_rows, ranking, capacity):
    token_count = route_rows.shape[0]
    expert = jnp.transpose(route_rows).reshape(-1)
    pair_order = (jnp.arange(2, dtype=jnp.int32)[:, None] * token_count + ranking[None, :]).reshape(
        -1
    )
    before = (expert[:, None] == expert[None, :]) & (pair_order[None, :] < pair_order[:, None])
    position = jnp.sum(before.astype(jnp.int32), axis=1)
    slot_ids = jnp.where(position < capacity, expert * capacity + position, -1)
    return slot_ids.reshape(2, token_count)


def keep_state(current):
    return current


def local(
    inputs,
    ln1_gain,
    w_qkv,
    w_out,
    ln2_gain,
    w_router,
    expert_in,
    expert_out,
    routes,
    priority,
    doc_lengths,
    d_out,
):
    blk_size = lax.axis_size("blk")
    tok_rows = inputs.shape[0]
    model_width = inputs.shape[1]
    capacity = 2 * tok_rows // blk_size
    slot_total = blk_size * capacity
    gain_one, qkv_weight, out_weight, gain_two, router_weight = (
        lax.all_gather(ln1_gain, "blk", axis=0, tiled=True),
        lax.all_gather(w_qkv, "blk", axis=0, tiled=True),
        lax.all_gather(w_out, "blk", axis=0, tiled=True),
        lax.all_gather(ln2_gain, "blk", axis=0, tiled=True),
        lax.all_gather(w_router, "blk", axis=0, tiled=True),
    )
    input_rows = inputs.astype(jnp.float32)
    normed_one, norm_one_pull = jax.vjp(layer_norm, input_rows, gain_one.astype(jnp.float32))
    normed_low = normed_one.astype(jnp.bfloat16)
    qkv_rows = jnp.dot(normed_low, qkv_weight, preferred_element_type=jnp.float32).astype(
        jnp.bfloat16
    )
    query_heads, key_heads, value_heads = (
        lax.all_to_all(qkv_rows[:, :model_width], "head", split_axis=1, concat_axis=0, tiled=True),
        lax.all_to_all(
            qkv_rows[:, model_width : 2 * model_width],
            "head",
            split_axis=1,
            concat_axis=0,
            tiled=True,
        ),
        lax.all_to_all(
            qkv_rows[:, 2 * model_width :], "head", split_axis=1, concat_axis=0, tiled=True
        ),
    )
    span_rows = query_heads.shape[0]
    head_count = query_heads.shape[1] // HS
    key_all, value_all = (
        lax.all_gather(key_heads, "blk", axis=0, tiled=True),
        lax.all_gather(value_heads, "blk", axis=0, tiled=True),
    )
    total_rows = key_all.shape[0]
    block_count = total_rows // KEY_BLOCK
    scale_factor = HS ** (-0.5)
    query_pos = lax.axis_index("blk") * span_rows + jnp.arange(span_rows, dtype=jnp.int32)
    query_docs = doc_index(query_pos, doc_lengths)
    queries = query_heads.reshape(span_rows, head_count, HS)

    def block_parts(block_index, key_source, value_source):
        first_key = block_index * KEY_BLOCK
        key_rows = lax.dynamic_slice_in_dim(key_source, first_key, KEY_BLOCK, 0).reshape(
            KEY_BLOCK, head_count, HS
        )
        value_rows = lax.dynamic_slice_in_dim(value_source, first_key, KEY_BLOCK, 0).reshape(
            KEY_BLOCK, head_count, HS
        )
        key_docs = doc_index(first_key + jnp.arange(KEY_BLOCK, dtype=jnp.int32), doc_lengths)
        is_live = (key_docs[0] <= query_docs[-1]) & (key_docs[-1] >= query_docs[0])
        same_doc = query_docs[:, None] == key_docs[None, :]
        return (first_key, key_rows, value_rows, same_doc, is_live)

    def block_scores(key_rows, same_doc):
        raw_scores = (
            jnp.einsum("qhd,khd->hqk", queries, key_rows, preferred_element_type=jnp.float32)
            * scale_factor
        )
        return jnp.where(same_doc[None], raw_scores, MASKED)

    def stat_step(block_index, loop_state):
        first_key, key_rows, value_rows, same_doc, is_live = block_parts(
            block_index, key_all, value_all
        )

        def stat_update(current):
            running_max, running_sum = current
            scores = block_scores(key_rows, same_doc)
            new_max = jnp.maximum(running_max, jnp.max(scores, axis=2))
            exp_terms = jnp.where(same_doc[None], jnp.exp(scores - new_max[:, :, None]), 0.0)
            return (
                new_max,
                running_sum * jnp.exp(running_max - new_max) + jnp.sum(exp_terms, axis=2),
            )

        return lax.cond(is_live, stat_update, keep_state, loop_state)

    start_state = (
        jnp.full((head_count, span_rows), MASKED, jnp.float32),
        jnp.zeros((head_count, span_rows), jnp.float32),
    )
    running_max, running_sum = lax.fori_loop(0, block_count, stat_step, start_state)
    log_total = running_max + jnp.log(running_sum)

    def out_step(block_index, loop_state):
        first_key, key_rows, value_rows, same_doc, is_live = block_parts(
            block_index, key_all, value_all
        )

        def out_update(current):
            scores = block_scores(key_rows, same_doc)
            weights = jnp.where(
                same_doc[None], jnp.exp(scores - log_total[:, :, None]), 0.0
            ).astype(jnp.bfloat16)
            return current + jnp.einsum(
                "hqk,khd->qhd", weights, value_rows, preferred_element_type=jnp.float32
            )

        return lax.cond(is_live, out_update, keep_state, loop_state)

    mixed_full = lax.fori_loop(
        0, block_count, out_step, jnp.zeros((span_rows, head_count, HS), jnp.float32)
    )
    mixed_low = mixed_full.reshape(span_rows, head_count * HS).astype(jnp.bfloat16)
    mixed_tokens = lax.all_to_all(mixed_low, "head", split_axis=0, concat_axis=1, tiled=True)
    attended = jnp.dot(mixed_tokens, out_weight, preferred_element_type=jnp.float32)
    hidden_one = input_rows + attended
    normed_two, norm_two_pull = jax.vjp(layer_norm, hidden_one, gain_two.astype(jnp.float32))
    routed_low = normed_two.astype(jnp.bfloat16)
    router_probs, router_pull = jax.vjp(
        router, routed_low.astype(jnp.float32), router_weight.astype(jnp.float32)
    )
    slot_ids = slot_table(routes, priority[0], capacity)
    select = (
        slot_ids[:, :, None] == jnp.arange(slot_total, dtype=jnp.int32)[None, None, :]
    ).astype(jnp.bfloat16)
    send_rows = jnp.einsum(
        "kts,td->sd", select, routed_low, preferred_element_type=jnp.float32
    ).astype(jnp.bfloat16)
    expert_rows = lax.all_to_all(
        send_rows.reshape(blk_size, capacity, model_width),
        "blk",
        split_axis=0,
        concat_axis=0,
        tiled=True,
    ).reshape(slot_total, model_width)
    weight_in = expert_in[0]
    weight_out = expert_out[0]
    pre_act = jnp.dot(expert_rows, weight_in, preferred_element_type=jnp.float32)
    hidden_act, gelu_pull = jax.vjp(gelu_exact, pre_act)
    hidden_low = hidden_act.astype(jnp.bfloat16)
    expert_result = jnp.dot(hidden_low, weight_out, preferred_element_type=jnp.float32).astype(
        jnp.bfloat16
    )
    slot_result = lax.all_to_all(
        expert_result.reshape(blk_size, capacity, model_width),
        "blk",
        split_axis=0,
        concat_axis=0,
        tiled=True,
    ).reshape(slot_total, model_width)
    pair_result = jnp.einsum("kts,sd->ktd", select, slot_result, preferred_element_type=jnp.float32)
    route_hot = (routes[:, :, None] == jnp.arange(blk_size, dtype=jnp.int32)[None, None, :]).astype(
        jnp.float32
    )
    gate_vals = jnp.sum(router_probs[:, None, :] * route_hot, axis=2)
    mixture = gate_vals[:, 0, None] * pair_result[0] + gate_vals[:, 1, None] * pair_result[1]
    output = (hidden_one + mixture).astype(jnp.bfloat16)
    d_gates = jnp.transpose(jnp.sum(d_out[None] * pair_result, axis=2))
    d_probs = jnp.sum(d_gates[:, :, None] * route_hot, axis=1)
    pair_grads = (jnp.transpose(gate_vals)[:, :, None] * d_out[None]).astype(jnp.bfloat16)
    slot_grads = jnp.einsum(
        "kts,ktd->sd", select, pair_grads, preferred_element_type=jnp.float32
    ).astype(jnp.bfloat16)
    result_grads = lax.all_to_all(
        slot_grads.reshape(blk_size, capacity, model_width),
        "blk",
        split_axis=0,
        concat_axis=0,
        tiled=True,
    ).reshape(slot_total, model_width)
    d_hidden_act = jnp.dot(result_grads, weight_out.T, preferred_element_type=jnp.float32)
    d_weight_out = jnp.dot(hidden_low.T, result_grads, preferred_element_type=jnp.float32)
    d_preact = gelu_pull(d_hidden_act)[0].astype(jnp.bfloat16)
    d_weight_in = jnp.dot(expert_rows.T, d_preact, preferred_element_type=jnp.float32)
    row_grads = jnp.dot(d_preact, weight_in.T, preferred_element_type=jnp.float32).astype(
        jnp.bfloat16
    )
    slot_back = lax.all_to_all(
        row_grads.reshape(blk_size, capacity, model_width),
        "blk",
        split_axis=0,
        concat_axis=0,
        tiled=True,
    ).reshape(slot_total, model_width)
    d_routed = jnp.einsum("kts,sd->td", select, slot_back, preferred_element_type=jnp.float32)
    d_routed_router, d_router = router_pull(d_probs)
    d_hidden_norm, d_gain_two = norm_two_pull(d_routed + d_routed_router)
    d_hidden_one = d_out + d_hidden_norm
    attn_grads = d_hidden_one.astype(jnp.bfloat16)
    d_out_weight = jnp.dot(mixed_tokens.T, attn_grads, preferred_element_type=jnp.float32)
    mixed_grads = jnp.dot(attn_grads, out_weight.T, preferred_element_type=jnp.float32).astype(
        jnp.bfloat16
    )
    head_grads = lax.all_to_all(mixed_grads, "head", split_axis=1, concat_axis=0, tiled=True)
    out_grads = head_grads.reshape(span_rows, head_count, HS)
    row_delta = jnp.transpose(jnp.sum(out_grads.astype(jnp.float32) * mixed_full, axis=2))
    key_back, value_back = (
        lax.all_gather(key_heads, "blk", axis=0, tiled=True),
        lax.all_gather(value_heads, "blk", axis=0, tiled=True),
    )

    def grad_step(block_index, loop_state):
        first_key, key_rows, value_rows, same_doc, is_live = block_parts(
            block_index, key_back, value_back
        )

        def grad_update(current):
            query_grad, key_grad, value_grad = current
            scores = block_scores(key_rows, same_doc)
            weights = jnp.where(same_doc[None], jnp.exp(scores - log_total[:, :, None]), 0.0)
            value_part = jnp.einsum(
                "hqk,qhd->khd",
                weights.astype(jnp.bfloat16),
                out_grads,
                preferred_element_type=jnp.float32,
            )
            weight_grads = jnp.einsum(
                "qhd,khd->hqk", out_grads, value_rows, preferred_element_type=jnp.float32
            )
            score_grads = (weights * (weight_grads - row_delta[:, :, None])).astype(jnp.bfloat16)
            query_grad = (
                query_grad
                + jnp.einsum(
                    "hqk,khd->qhd", score_grads, key_rows, preferred_element_type=jnp.float32
                )
                * scale_factor
            )
            key_part = (
                jnp.einsum("hqk,qhd->khd", score_grads, queries, preferred_element_type=jnp.float32)
                * scale_factor
            )
            key_grad = lax.dynamic_update_slice_in_dim(
                key_grad, key_part.reshape(KEY_BLOCK, head_count * HS), first_key, 0
            )
            value_grad = lax.dynamic_update_slice_in_dim(
                value_grad, value_part.reshape(KEY_BLOCK, head_count * HS), first_key, 0
            )
            return (query_grad, key_grad, value_grad)

        return lax.cond(is_live, grad_update, keep_state, loop_state)

    start_grads = (
        jnp.zeros((span_rows, head_count, HS), jnp.float32),
        jnp.zeros((total_rows, head_count * HS), jnp.float32),
        jnp.zeros((total_rows, head_count * HS), jnp.float32),
    )
    query_grad, key_grad, value_grad = lax.fori_loop(0, block_count, grad_step, start_grads)
    key_own, value_own = (
        lax.psum_scatter(
            key_grad.astype(jnp.bfloat16), "blk", scatter_dimension=0, tiled=True
        ).astype(jnp.float32),
        lax.psum_scatter(
            value_grad.astype(jnp.bfloat16), "blk", scatter_dimension=0, tiled=True
        ).astype(jnp.float32),
    )
    query_tokens_grad, key_tokens_grad, value_tokens_grad = (
        lax.all_to_all(
            query_grad.reshape(span_rows, head_count * HS).astype(jnp.bfloat16),
            "head",
            split_axis=0,
            concat_axis=1,
            tiled=True,
        ),
        lax.all_to_all(
            key_own.astype(jnp.bfloat16), "head", split_axis=0, concat_axis=1, tiled=True
        ),
        lax.all_to_all(
            value_own.astype(jnp.bfloat16), "head", split_axis=0, concat_axis=1, tiled=True
        ),
    )
    qkv_grads = jnp.concatenate([query_tokens_grad, key_tokens_grad, value_tokens_grad], axis=1)
    d_qkv_weight = jnp.dot(normed_low.T, qkv_grads, preferred_element_type=jnp.float32)
    normed_grads = jnp.dot(qkv_grads, qkv_weight.T, preferred_element_type=jnp.float32)
    d_inputs_norm, d_gain_one = norm_one_pull(normed_grads)
    d_inputs = d_hidden_one + d_inputs_norm
    gain_one_sum, qkv_sum, out_sum, gain_two_sum, router_sum = (
        lax.psum_scatter(
            d_gain_one.astype(jnp.bfloat16), "blk", scatter_dimension=0, tiled=True
        ).astype(jnp.float32),
        lax.psum_scatter(
            d_qkv_weight.astype(jnp.bfloat16), "blk", scatter_dimension=0, tiled=True
        ).astype(jnp.float32),
        lax.psum_scatter(
            d_out_weight.astype(jnp.bfloat16), "blk", scatter_dimension=0, tiled=True
        ).astype(jnp.float32),
        lax.psum_scatter(
            d_gain_two.astype(jnp.bfloat16), "blk", scatter_dimension=0, tiled=True
        ).astype(jnp.float32),
        lax.psum_scatter(
            d_router.astype(jnp.bfloat16), "blk", scatter_dimension=0, tiled=True
        ).astype(jnp.float32),
    )
    gain_one_all, qkv_all, out_all, gain_two_all, router_all, expert_in_all, expert_out_all = (
        lax.psum(gain_one_sum.astype(jnp.bfloat16), "head").astype(jnp.float32),
        lax.psum(qkv_sum.astype(jnp.bfloat16), "head").astype(jnp.float32),
        lax.psum(out_sum.astype(jnp.bfloat16), "head").astype(jnp.float32),
        lax.psum(gain_two_sum.astype(jnp.bfloat16), "head").astype(jnp.float32),
        lax.psum(router_sum.astype(jnp.bfloat16), "head").astype(jnp.float32),
        lax.psum(d_weight_in[None].astype(jnp.bfloat16), "head").astype(jnp.float32),
        lax.psum(d_weight_out[None].astype(jnp.bfloat16), "head").astype(jnp.float32),
    )
    return (
        output,
        d_inputs,
        gain_one_all,
        qkv_all,
        out_all,
        gain_two_all,
        router_all,
        expert_in_all,
        expert_out_all,
    )


MESH = pl.DeviceIdType.MESH
LANES = 128
HALF = LANES // 2
MIB = 2**20
F32 = jnp.float32
BF16 = jnp.bfloat16


def dot(left, right, dims=(1, 0)):
    return lax.dot_general(
        left, right, (((dims[0],), (dims[1],)), ((), ())), preferred_element_type=F32
    )


def remote(src, dst, send_sem, recv_sem, head, blk):
    return pltpu.make_async_remote_copy(
        src_ref=src,
        dst_ref=dst,
        send_sem=send_sem,
        recv_sem=recv_sem,
        device_id={"head": head, "blk": blk},
        device_id_type=MESH,
    )


def arrived(ref, sem):
    pltpu.make_async_copy(ref, ref, sem).wait()


def greet(peers):
    barrier = pltpu.get_barrier_semaphore()
    for head, blk in peers:
        pl.semaphore_signal(
            barrier, inc=1, device_id={"head": head, "blk": blk}, device_id_type=MESH
        )
    return len(peers)


def meet(count):
    pl.semaphore_wait(pltpu.get_barrier_semaphore(), count)


def halves(values, lanes_kept):
    rows = values.shape[0] // 2
    moved = pltpu.roll(values[rows:], HALF, 1)
    return jnp.where(lanes_kept, values[:rows], moved)


def lane_ids(shape):
    return lax.broadcasted_iota(jnp.int32, shape, len(shape) - 1)


def centre(values):
    average = jnp.mean(values, axis=-1, keepdims=True)
    centred = values - average
    spread = jnp.mean(centred * centred, axis=-1, keepdims=True)
    scale = lax.rsqrt(spread + EPSILON)
    return centred * scale, scale


def centre_back(grad, xhat, scale):
    middle = jnp.mean(grad, axis=-1, keepdims=True)
    along = jnp.mean(grad * xhat, axis=-1, keepdims=True)
    return (grad - middle - xhat * along) * scale


def split_high_low(column, lanes):
    high = column.astype(BF16)
    low = (column - high.astype(F32)).astype(BF16)
    return jnp.where(lanes < HALF, high.astype(F32), low.astype(F32)).astype(BF16)


def join_high_low(matrix, start):
    return matrix[:, start : start + 1].astype(F32) + matrix[
        :, start + HALF : start + HALF + 1
    ].astype(F32)


def place():
    head, blk = lax.axis_index("head"), lax.axis_index("blk")
    return head, blk, blk // 2, lax.rem(blk, 2)


def around(index, step, size):
    return lax.rem(index + step, size)


QUERY_TILE = 256
CHAINS = 2


def masked_queries(q_ref, tile, key_lanes, query_tile):
    tiles_per_span = q_ref.shape[1] // query_tile
    inner = tile % tiles_per_span * query_tile
    query = q_ref[tile // tiles_per_span, inner : inner + query_tile, :]
    return jnp.where(key_lanes, query, jnp.zeros_like(query))


def group_blocks(bounds_ref, group, size, key_tile):
    first, last = group * size, (group + 1) * size
    low = jnp.min(bounds_ref[0:1, first : first + LANES])
    high = jnp.max(bounds_ref[1:2, last - LANES : last])
    return low // key_tile, (high + key_tile - 1) // key_tile


def inside_document(bounds_ref, tile, first, shape):
    key = first + lax.broadcasted_iota(jnp.int32, shape, 0)
    columns = slice(tile * shape[1], (tile + 1) * shape[1])
    return jnp.logical_and(key >= bounds_ref[0:1, columns], key < bounds_ref[1:2, columns])


def query_group(q_ref, group, y):
    key_lanes = (lane_ids((QUERY_TILE, LANES)) < HALF) == (y == 0)
    tiles = range(group * CHAINS, (group + 1) * CHAINS)
    return tiles, [masked_queries(q_ref, tile, key_lanes, QUERY_TILE) for tile in tiles]


def attend(bounds_ref, tiles, first, keys, keys_across, queries, carry):
    scores = [dot(keys, query, (1, 1)) for query in queries]
    made = []
    for tile, score, (biggest, weight, mixed) in zip(tiles, scores, carry):
        inside = inside_document(bounds_ref, tile, first, score.shape)
        score = jnp.where(inside, score, MASKED)
        bigger = jnp.maximum(biggest, jnp.max(score, axis=0, keepdims=True))
        fade = jnp.exp(biggest - bigger)
        terms = jnp.exp(score - bigger)
        weight = weight * fade + jnp.sum(terms, axis=0, keepdims=True)
        made.append((bigger, weight, mixed * fade + dot(keys_across, terms.astype(BF16))))
    return tuple(made)


def nothing_attended():
    return (
        jnp.full((1, QUERY_TILE), MASKED, F32),
        jnp.zeros((1, QUERY_TILE), F32),
        jnp.zeros((LANES, QUERY_TILE), F32),
    )


def attend_back(bounds_ref, tiles, first, keys, keys_across, group, carry):
    queries, out_grads, deltas, log_totals = group
    scores = [dot(keys, query, (1, 1)) for query in queries]
    weight_grads = [dot(keys, out_grad, (1, 1)) for out_grad in out_grads]
    pieces, score_grads = [], []
    for i, tile in enumerate(tiles):
        inside = inside_document(bounds_ref, tile, first, scores[i].shape)
        weights = jnp.exp(jnp.where(inside, scores[i], MASKED) - log_totals[i])
        score_grads.append((weights * (weight_grads[i] - deltas[i])).astype(BF16))
        pieces.append(weights.astype(BF16))
    wide = jnp.concatenate(score_grads + pieces, axis=1)
    given = dot(wide, jnp.concatenate(queries + out_grads, axis=0))
    return given, tuple(c + dot(keys_across, g) for c, g in zip(carry, score_grads))


def group_grads(do_ref, tiles, y):
    key_lanes = (lane_ids((QUERY_TILE, LANES)) < HALF) == (y == 0)
    out_grads = []
    for tile in tiles:
        parts = []
        for part in range(QUERY_TILE // LANES):
            packed = do_ref[tile, part].astype(F32)
            parts += [packed, pltpu.roll(packed, HALF, 1)]
        out_grads.append(jnp.where(key_lanes, 0.0, jnp.concatenate(parts, axis=0)).astype(BF16))
    return out_grads


def qkv_kernel(
    heads, blks,
    x_hbm, w_hbm, g1_hbm, wo_hbm, wr_hbm, g2_hbm, docs_hbm,
    qall, kvall, xall, wall, wo_all, kvt, bounds, begun,
    x_ref, w_ref, rows_in, g1_ref, g2_ref, wr_ref, docs_ref, wo_own, kv_other, q_packed, q_landed, in_sem,
    x_send, x_recv, w_send, w_recv, o_send, o_recv, p_send, p_recv,
    k_send, k_recv, q_recv,
):
    head, blk, z, y = place()
    planes = blks // 2
    model = x_ref.shape[1]
    rows = w_ref.shape[0]
    part = rows // heads
    experts = wr_ref.shape[0]
    wanted = (
        (w_hbm, w_ref), (g1_hbm, g1_ref), (g2_hbm, g2_ref), (wr_hbm, wr_ref), (x_hbm, x_ref),
        (wo_hbm, wo_own.at[:, pl.ds(0, model)]), (docs_hbm, docs_ref),
    )
    fetched = [
        pltpu.make_async_copy(src, dst, in_sem.at[i]) for i, (src, dst) in enumerate(wanted)
    ]
    for copy in fetched:
        copy.start()
    rows_in[...] = jnp.zeros_like(rows_in)
    met = greet(
        [(around(head, k, heads), blk) for k in range(1, heads)]
        + [(head, around(blk, k, blks)) for k in range(1, blks)]
    )
    lanes = lane_ids((rows, LANES))
    for copy in fetched:
        copy.wait()
    rows_in[0:experts, 0:rows] = wr_ref[...].astype(F32)
    rows_in[experts : experts + 1, 0:rows] = g2_ref[...].astype(F32)
    rows_in[experts + 1 : experts + 2, 0:rows] = g1_ref[...].astype(F32)
    vectors = jnp.transpose(rows_in[...])[:rows]
    gain = vectors[:, experts + 1 : experts + 2]

    def columns(which):
        start = pl.multiple_of(which * model + head * LANES, LANES)
        return w_ref[:, pl.ds(start, LANES)].astype(F32) * gain

    key_cols = columns(1)
    value_cols = pltpu.roll(columns(2), HALF, 1)
    wall[blk, :, 0:LANES] = jnp.where(lanes < HALF, key_cols, value_cols).astype(BF16)
    wall[blk, :, LANES : 2 * LANES] = jnp.where(lanes < HALF, value_cols, key_cols).astype(BF16)
    wall[blk, :, 2 * LANES : 3 * LANES] = (columns(0) * HS ** (-0.5)).astype(BF16)
    def slice_copy(slot, source, target):
        ref = wall.at[source]
        return remote(ref, ref, w_send.at[slot], w_recv.at[source], head, target)

    pair = 2 * z + around(y, 1, 2)
    line = [2 * around(z, step, planes) + y for step in (1, planes - 1, *range(2, planes - 1))]
    w_copies = [slice_copy(slot, blk, target) for slot, target in enumerate((*line, pair))]
    w_onward = [slice_copy(planes + slot, source, pair) for slot, source in enumerate(line)]
    xhat, _ = centre(x_ref[...].astype(F32))
    xall[head] = xhat.astype(BF16)
    meet(met)
    for copy in w_copies:
        copy.start()
    x_copies = [
        remote(xall.at[head], xall.at[head], x_send.at[k], x_recv.at[k], around(head, k, heads), blk)
        for k in range(1, heads)
    ]
    for copy in x_copies:
        copy.start()
    wo_own[:, model : model + LANES] = vectors.astype(BF16)
    wo_all[blk, head] = wo_own[pl.ds(pl.multiple_of(head * part, part), part), :]
    o_copies = [
        remote(
            wo_all.at[blk, head], wo_all.at[blk, head],
            o_send.at[k], o_recv.at[k], head, around(blk, k, blks),
        )
        for k in range(1, blks)
    ]
    document_bounds(docs_ref, bounds, z)
    for source, copy in zip(line, w_onward):
        arrived(wall.at[source], w_recv.at[source])
        copy.start()
    for copy in o_copies:
        copy.start()
    for source in (pair, *[other - y + around(y, 1, 2) for other in line]):
        arrived(wall.at[source], w_recv.at[source])
    for copy in w_copies + w_onward:
        copy.wait_send()
    for copy in x_copies:
        copy.wait()
    weight = wall[...].reshape(model, 3 * LANES)
    tokens = x_ref.shape[0]
    even = y == 0
    above, below = z < planes - 1, z > 0
    half_span = kvall.shape[1] // 2
    sides = ((1, above, below, 0), (-1, below, above, 4))

    def half_of(ref, half):
        return ref.at[pl.ds(half * half_span, half_span)]

    def outward(slot, step, across, half):
        target = 2 * (z + step) + around(y, across, 2)
        return remote(
            half_of(kv_other if across else kvall.at[blk], half), half_of(kvall.at[blk], half),
            k_send.at[slot], k_recv.at[blk, half], head, target,
        )

    def onward(slot, step, side, half):
        from_span = 2 * (z - step) + side
        ref = half_of(kvall.at[from_span], half)
        return remote(ref, ref, k_send.at[slot], k_recv.at[from_span, half], head, 2 * (z + step) + y)

    def await_half(span, half):
        arrived(half_of(kvall.at[span], half), k_recv.at[span, half])

    def turn(span):
        size = kvall.shape[1]
        kvt[:, pl.ds(pl.multiple_of(span * size, size), size)] = jnp.transpose(kvall[span])

    for half in range(2):
        for piece in range(half * heads // 2, (half + 1) * heads // 2):
            made = dot(xall[piece], weight).astype(BF16)
            first, second = made[:, 0:LANES], made[:, LANES : 2 * LANES]
            span = slice(piece * tokens, (piece + 1) * tokens)
            kvall[blk, span, :] = jnp.where(even, first, second)
            kv_other[span, :] = jnp.where(even, second, first)
            qall[y, span, :] = made[:, 2 * LANES : 3 * LANES]
        outward(8 + half, 0, 1, half).start()
        for step, there, _, slot in sides:

            @pl.when(there)
            def _():
                outward(slot + 2 * half, step, 0, half).start()
                outward(slot + 2 * half + 1, step, 1, half).start()

    other_y = around(y, 1, 2)
    kept = (lane_ids(q_packed.shape) < HALF) == (y == 1)
    q_packed[...] = halves(qall[y].astype(F32), kept).astype(BF16)
    q_pair = remote(q_packed, q_landed, k_send.at[10], q_recv, head, 2 * z + other_y)
    q_pair.start()
    turn(blk)
    for copy in o_copies:
        copy.wait()
    core = lax.rem(head, 2)
    sibling, across = head - core + 1 - core, around(head, 2, heads)

    def quarter_copy(index, quarter, to_head):
        ref = wo_all.at[:, quarter]
        return remote(ref, ref, p_send.at[index], p_recv.at[index], to_head, blk)

    p_copies = [quarter_copy(0, head, sibling), quarter_copy(1, head, across)]
    for copy in p_copies:
        copy.start()
    p_copies.append(quarter_copy(2, across, sibling))
    for half in range(2):
        for step, there, back, slot in sides:

            @pl.when(back)
            def _():
                for side in range(2):
                    await_half(2 * (z - step) + side, half)

            @pl.when(jnp.logical_and(there, back))
            def _():
                for side in range(2):
                    onward(11 + slot + 2 * half + side, step, side, half).start()

    arrived(wo_all.at[:, across], p_recv.at[1])
    p_copies[2].start()
    for half in range(2):
        await_half(pair, half)
    turn(pair)
    q_pair.wait()
    landed = q_landed[...]
    qall[other_y, 0:half_span, :] = landed
    qall[other_y, half_span : 2 * half_span, :] = pltpu.roll(landed.astype(F32), HALF, 1).astype(BF16)
    key_tile = kvall.shape[1]
    for group in range(2 * key_tile // (CHAINS * QUERY_TILE)):
        tiles, queries = query_group(qall, group, y)
        carry = (nothing_attended(),) * CHAINS
        for side in range(2):
            first = pl.multiple_of((2 * z + side) * key_tile, key_tile)
            keys_across = kvt[:, pl.ds(first, key_tile)]
            carry = attend(bounds, tiles, first, kvall[2 * z + side], keys_across, queries, carry)
        for tile, (biggest, weight, mixed) in zip(tiles, carry):
            begun[tile, 0:LANES] = mixed
            begun[tile, LANES : LANES + 8] = jnp.broadcast_to(biggest, (8, QUERY_TILE))
            begun[tile, LANES + 8 : LANES + 16] = jnp.broadcast_to(weight, (8, QUERY_TILE))
    for step, there, back, slot in sides:

        @pl.when(back)
        def _():
            for side in range(2):
                turn(2 * (z - step) + side)

    for other in range(planes):
        for side in range(2):
            span = 2 * other + side

            @pl.when(jnp.logical_or(z - other == 2, other - z == 2))
            def _():
                for half in range(2):
                    await_half(span, half)
                turn(span)

    for index, quarter in ((0, sibling), (2, around(sibling, 2, heads))):
        arrived(wo_all.at[:, quarter], p_recv.at[index])
    for copy in p_copies:
        copy.wait_send()
    for half in range(2):
        outward(8 + half, 0, 1, half).wait_send()
        for step, there, back, slot in sides:

            @pl.when(there)
            def _():
                outward(slot + 2 * half, step, 0, half).wait_send()
                outward(slot + 2 * half + 1, step, 1, half).wait_send()

            @pl.when(jnp.logical_and(there, back))
            def _():
                for side in range(2):
                    onward(11 + slot + 2 * half + side, step, side, half).wait_send()


def document_bounds(docs_ref, bounds, z):
    count = docs_ref.shape[1]
    lengths = docs_ref[...].astype(F32)
    doc = lax.broadcasted_iota(jnp.int32, (count, count), 0)
    other = lane_ids((count, count))
    start = jnp.sum(jnp.where(other < doc, lengths, 0.0), axis=1, keepdims=True)
    end = jnp.sum(jnp.where(other <= doc, lengths, 0.0), axis=1, keepdims=True)
    queries = bounds.shape[1]
    token = (z * queries + lane_ids((count, queries))).astype(F32)
    begun = start <= token
    bounds[...] = jnp.zeros_like(bounds)
    bounds[0:1, :] = jnp.max(jnp.where(begun, start, 0.0), axis=0, keepdims=True).astype(jnp.int32)
    bounds[1:2, :] = jnp.max(jnp.where(begun, end, 0.0), axis=0, keepdims=True).astype(jnp.int32)


def vmem_specs(count):
    return [pl.BlockSpec(memory_space=pltpu.VMEM)] * count


def hbm_specs(count):
    return [pl.BlockSpec(memory_space=pltpu.HBM)] * count


def in_hbm(*arrays):
    return [pltpu.with_memory_space_constraint(array, pltpu.HBM) for array in arrays]


def dma(*shape):
    return pltpu.SemaphoreType.DMA(shape)


def call_qkv(x, w_qkv, g1, w_out, w_router, g2, doc_lengths, heads, blks):
    tokens, model = x.shape
    rows = w_qkv.shape[0]
    span = tokens * heads
    wide = model + LANES
    part = rows // heads
    return pl.pallas_call(
        functools.partial(qkv_kernel, heads, blks),
        out_shape=(
            jax.ShapeDtypeStruct((2, span, LANES), BF16),
            jax.ShapeDtypeStruct((blks, span, LANES), BF16),
            jax.ShapeDtypeStruct((heads, tokens, model), BF16),
            jax.ShapeDtypeStruct((blks, rows, 3 * LANES), BF16),
            jax.ShapeDtypeStruct((blks, heads, part, wide), BF16),
            jax.ShapeDtypeStruct((LANES, blks * span), BF16),
            jax.ShapeDtypeStruct((8, 2 * span), jnp.int32),
            jax.ShapeDtypeStruct((2 * span // QUERY_TILE, LANES + 16, QUERY_TILE), F32),
        ),
        in_specs=hbm_specs(7),
        out_specs=tuple(vmem_specs(8)),
        scratch_shapes=[
            pltpu.VMEM((tokens, model), BF16),
            pltpu.VMEM((rows, 3 * model), BF16),
            pltpu.VMEM((LANES, LANES), F32),
            pltpu.VMEM((1, rows), BF16),
            pltpu.VMEM((1, rows), BF16),
            pltpu.VMEM((w_router.shape[1], rows), BF16),
            pltpu.VMEM((1, doc_lengths.shape[0]), jnp.int32),
            pltpu.VMEM((rows, wide), BF16),
            pltpu.VMEM((span, LANES), BF16),
            pltpu.VMEM((span // 2, LANES), BF16),
            pltpu.VMEM((span // 2, LANES), BF16),
            dma(7),
            dma(heads), dma(heads), dma(blks), dma(blks), dma(blks), dma(blks), dma(heads), dma(heads),
            dma(19), dma(blks, 2), pltpu.SemaphoreType.DMA,
        ],
        compiler_params=pltpu.CompilerParams(
            collective_id=1, has_side_effects=True, vmem_limit_bytes=16 * MIB
        ),
        name="qkv",
    )(
        *in_hbm(
            x, w_qkv, g1.reshape(1, rows), w_out, w_router.T, g2.reshape(1, rows),
            doc_lengths.reshape(1, -1),
        )
    )


def other_blocks(bounds_ref, group, key_tile, z, step, carry):
    low, high = group_blocks(bounds_ref, group, CHAINS * QUERY_TILE, key_tile)
    carry = lax.fori_loop(low, 2 * z, step, carry)
    return lax.fori_loop(2 * z + 2, high, step, carry)


def forward_kernel(bounds_ref, q_ref, kv_ref, kvt_ref, begun_ref, o_out, ob_out, lse_out):
    _, _, z, y = place()
    key_tile = kv_ref.shape[1]
    value_lanes = (lane_ids((HALF, LANES)) < HALF) == (y == 1)
    for group in range(q_ref.shape[0] * q_ref.shape[1] // (CHAINS * QUERY_TILE)):
        tiles, queries = query_group(q_ref, group, y)

        def step(block, carry, queries=queries, tiles=tiles):
            first = pl.multiple_of(block * key_tile, key_tile)
            across = kvt_ref[:, pl.ds(first, key_tile)]
            return attend(bounds_ref, tiles, first, kv_ref[block], across, queries, carry)

        start = tuple(
            (begun_ref[t, LANES : LANES + 1], begun_ref[t, LANES + 8 : LANES + 9], begun_ref[t, 0:LANES])
            for t in tiles
        )
        ends = other_blocks(bounds_ref, group, key_tile, z, step, start)
        for tile, (biggest, weight, mixed) in zip(tiles, ends):
            result = jnp.transpose(mixed / weight)
            o_out[tile] = result
            for part in range(QUERY_TILE // LANES):
                block = result[part * LANES : (part + 1) * LANES]
                ob_out[tile, part] = halves(block, value_lanes).astype(BF16)
            lse_out[tile] = jnp.broadcast_to(biggest + jnp.log(weight), (8, QUERY_TILE))


def call_forward(bounds, q, kv, kvt, begun):
    blks, span, _ = kv.shape
    tiles = 2 * span // QUERY_TILE
    return pl.pallas_call(
        forward_kernel,
        out_shape=(
            jax.ShapeDtypeStruct((tiles, QUERY_TILE, LANES), F32),
            jax.ShapeDtypeStruct((tiles, QUERY_TILE // LANES, HALF, LANES), BF16),
            jax.ShapeDtypeStruct((tiles, 8, QUERY_TILE), F32),
        ),
        in_specs=vmem_specs(5),
        out_specs=tuple(vmem_specs(3)),
        compiler_params=pltpu.CompilerParams(vmem_limit_bytes=16 * MIB),
        name="attend",
    )(bounds, q, kv, kvt, begun)


def backward_kernel(
    bounds_ref, q_ref, kv_ref, kvt_ref, do_ref, o_ref, lse_ref, dq_out, dkv_out, delta_out, dkv
):
    _, _, z, y = place()
    key_tile = kv_ref.shape[1]
    dkv[...] = jnp.zeros_like(dkv)
    for group in range(q_ref.shape[0] * q_ref.shape[1] // (CHAINS * QUERY_TILE)):
        tiles, queries = query_group(q_ref, group, y)
        out_grads = group_grads(do_ref, tiles, y)
        deltas, log_totals = [], []
        for tile, out_grad in zip(tiles, out_grads):
            product = jnp.transpose(out_grad.astype(F32) * o_ref[tile])
            deltas.append(jnp.sum(product, axis=0, keepdims=True))
            delta_out[tile] = jnp.broadcast_to(deltas[-1], delta_out.shape[1:])
            log_totals.append(lse_ref[tile, 0:1, :])
        known = (queries, out_grads, deltas, log_totals)

        def step(block, carry, tiles=tiles, known=known):
            first = pl.multiple_of(block * key_tile, key_tile)
            across = kvt_ref[:, pl.ds(first, key_tile)]
            given, carry = attend_back(bounds_ref, tiles, first, kv_ref[block], across, known, carry)
            dkv[block] += given
            return carry

        zero = jnp.zeros((LANES, QUERY_TILE), F32)
        ends = other_blocks(bounds_ref, group, key_tile, z, step, (zero,) * CHAINS)
        for tile, mixed in zip(tiles, ends):
            dq_out[tile] = mixed
    for block in range(dkv.shape[0]):
        dkv_out[block] = dkv[block].astype(BF16)


def call_backward(bounds, q, kv, kvt, d_o, o, lse):
    blks, span, _ = kv.shape
    tiles = 2 * span // QUERY_TILE
    return pl.pallas_call(
        backward_kernel,
        out_shape=(
            jax.ShapeDtypeStruct((tiles, LANES, QUERY_TILE), F32),
            jax.ShapeDtypeStruct((blks, span, LANES), BF16),
            jax.ShapeDtypeStruct((tiles, 8, QUERY_TILE), F32),
        ),
        in_specs=vmem_specs(7),
        out_specs=tuple(vmem_specs(3)),
        scratch_shapes=[pltpu.VMEM((blks, span, LANES), F32)],
        compiler_params=pltpu.CompilerParams(vmem_limit_bytes=16 * MIB),
        name="attend_back",
    )(bounds, q, kv, kvt, d_o, o, lse)


def gelu_parts(values):
    share = 0.5 * (1.0 + lax.erf(values * (2.0**-0.5)))
    slope = share + values * jnp.exp(-0.5 * values * values) * (2.0 * math.pi) ** -0.5
    return values * share, slope


def positions(expert_rows, expert_cols, rank_row, rank_col):
    def count(mask, axis):
        return jnp.sum(mask.astype(F32), axis=axis, keepdims=True)

    row = [None, None]
    col = [None, None]
    before = rank_col < rank_row
    after = rank_row < rank_col
    for choice in range(2):
        row[choice] = count((expert_cols[choice] == expert_rows[choice]) & before, 0)
        col[choice] = count((expert_rows[choice] == expert_cols[choice]) & after, 1)
    row[1] = row[1] + count(expert_cols[0] == expert_rows[1], 0)
    col[1] = col[1] + count(expert_rows[0] == expert_cols[1], 1)
    return row, col


def own_columns(rows_ref, turned, blk, capacity):
    blks, _, slots = rows_ref.shape
    rows = jnp.concatenate(
        [rows_ref[...].reshape(blks, slots), jnp.zeros((LANES - blks, slots), F32)], axis=0
    )
    for piece in range(slots // LANES):
        columns = slice(piece * LANES, (piece + 1) * LANES)
        turned[columns, :] = jnp.transpose(rows[:, columns])
    own = turned[pl.ds(pl.multiple_of(blk * capacity, capacity), capacity), :]
    return jnp.concatenate([own[:, source : source + 1] for source in range(blks)], axis=0)


def middle_kernel(
    heads, blks,
    x_hbm, o_ref, wo_ref, routes_hbm, rank_hbm, d_out_hbm, win_hbm, wout_hbm,
    po, pa, hidden_ref, share_ref, dh_ref, dma_all, grads_ref, rx,
    x_ref, routes_ref, rank_ref, d_out_ref, win_ref, wout_ref, rows_in, in_sem,
    o_all, dos, doa, rs, ra, dr, da, dms, acc_out, acc_row, mix, gate_rows, d_gate_rows, turned,
    o_send, o_recv, dos_send, dos_recv, r_send, r_recv,
    dr_send, dr_recv, dm_send, dm_recv, rx_send, rx_recv, g_send, g_recv, dg_send, dg_recv, pa_send, pa_recv,
):
    head, blk, z, y = place()
    tokens, model = x_ref.shape
    capacity = 2 * tokens // blks
    slots = capacity * blks
    plane = [(k % heads, k // heads) for k in range(1, 2 * heads)]
    wanted = (
        (routes_hbm, routes_ref), (rank_hbm, rank_ref), (d_out_hbm, d_out_ref), (x_hbm, x_ref),
        (win_hbm, win_ref), (wout_hbm, wout_ref),
    )
    fetched = [
        pltpu.make_async_copy(src, dst, in_sem.at[i]) for i, (src, dst) in enumerate(wanted)
    ]
    for copy in fetched:
        copy.start()
    met = greet(
        [(around(head, kh, heads), 2 * z + around(y, ky, 2)) for kh, ky in plane]
        + [(head, around(blk, k, blks)) for k in range(1, blks)]
    )
    meet(met)

    def plane_copies(src_of, dst, send, recv):
        copies = []
        for k, (kh, ky) in enumerate(plane):
            to_head, to_y = around(head, kh, heads), around(y, ky, 2)
            copies.append(
                remote(src_of(to_y, to_head), dst, send.at[k], recv.at[k], to_head, 2 * z + to_y)
            )
        return copies

    def blk_copies(src, dst, send, recv):
        return [
            remote(
                src.at[around(blk, k, blks)], dst.at[blk],
                send.at[k], recv.at[k], head, around(blk, k, blks),
            )
            for k in range(1, blks)
        ]

    def start(copies):
        for copy in copies:
            copy.start()

    def finish(copies):
        for copy in copies:
            copy.wait()

    o_copies = plane_copies(lambda to_y, to_head: o_ref.at[to_y, to_head], o_all.at[y, head], o_send, o_recv)
    start(o_copies)
    o_all[y, head] = o_ref[y, head]

    lanes = lane_ids((tokens, LANES))
    for copy in fetched[:4]:
        copy.wait()
    e_rows = [routes_ref[i : i + 1, :].astype(F32) for i in range(2)]
    rank_row = rank_ref[...].astype(F32)
    rows_in[...] = jnp.zeros_like(rows_in)
    rows_in[0:1, :], rows_in[1:2, :], rows_in[2:3, :] = *e_rows, rank_row
    columns = jnp.transpose(rows_in[...])
    e_cols = [columns[:, 0:1], columns[:, 1:2]]
    rank_col = columns[:, 2:3]
    pos_rows, pos_cols = positions(e_rows, e_cols, rank_row, rank_col)

    def slot_of(expert, position):
        return jnp.where(position < capacity, expert * capacity + position, -1.0).astype(jnp.int32)

    slot_rows = [slot_of(e, p) for e, p in zip(e_rows, pos_rows)]
    slot_cols = [slot_of(e, p) for e, p in zip(e_cols, pos_cols)]
    slot_down = lax.broadcasted_iota(jnp.int32, (slots, tokens), 0)
    slot_across = lane_ids((tokens, slots))
    pick = [(slot_down == s).astype(BF16) for s in slot_rows]
    put = [(slot_across == s).astype(BF16) for s in slot_cols]
    pick_any = pick[0] + pick[1]
    put_any = put[0] + put[1]

    d_out = d_out_ref[...]
    dos[...] = dot(pick_any, d_out.astype(BF16)).astype(BF16).reshape(dos.shape)
    dos_copies = blk_copies(dos, doa, dos_send, dos_recv)
    start(dos_copies)
    doa[blk] = dos[blk]

    weight_out = jnp.concatenate(
        [wo_ref[(b ^ 1) * HALF : ((b ^ 1) + 1) * HALF, 0:model] for b in range(blks)], axis=0
    )
    small = wo_ref[:, model : model + LANES]
    small_across = jnp.concatenate(
        [
            jnp.transpose(small[i * LANES : (i + 1) * LANES].astype(F32))
            for i in range(model // LANES)
        ],
        axis=1,
    )
    gain = small_across[blks : blks + 1, :]

    finish(o_copies)
    low_lanes = lanes[:HALF] < HALF
    for piece in range(heads):
        columns = slice(piece * LANES, (piece + 1) * LANES)
        first, second = o_all[1, piece].astype(F32), o_all[0, piece].astype(F32)
        mix[:HALF, columns] = jnp.where(low_lanes, first, second).astype(BF16)
        swapped = pltpu.roll(jnp.where(low_lanes, second, first), HALF, 1)
        mix[HALF:, columns] = swapped.astype(BF16)
    mixed = mix[...]
    hidden = x_ref[...].astype(F32) + dot(mixed, weight_out)
    xhat, scale = centre(hidden)
    routed = (xhat * gain).astype(BF16)
    rs[...] = dot(pick_any, routed).astype(BF16).reshape(rs.shape)
    r_copies = blk_copies(rs, ra, r_send, r_recv)
    start(r_copies)
    ra[blk] = rs[blk]
    logits = jnp.where(lanes < blks, dot(routed, small), MASKED)
    powers = jnp.exp(logits - jnp.max(logits, axis=1, keepdims=True))
    probs = powers / jnp.sum(powers, axis=1, keepdims=True)
    lanes_f = lanes.astype(F32)
    hots = [lanes_f == e for e in e_cols]
    gates = [jnp.sum(jnp.where(hot, probs, 0.0), axis=1, keepdims=True) for hot in hots]
    gate_high = [g.astype(BF16).astype(F32) for g in gates]
    gate_across = jnp.transpose(
        jnp.where(lanes == 0, gate_high[0], jnp.where(lanes == 1, gates[0] - gate_high[0], 0.0))
        + jnp.where(lanes == 2, gate_high[1], jnp.where(lanes == 3, gates[1] - gate_high[1], 0.0))
    ).astype(BF16)
    by_slot = (dot(gate_across, put[0]), dot(gate_across, put[1]))
    gate_rows[blk] = by_slot[0][0:1] + by_slot[0][1:2] + by_slot[1][2:3] + by_slot[1][3:4]
    g_copies = [
        remote(
            gate_rows.at[blk], gate_rows.at[blk],
            g_send.at[k], g_recv.at[k], head, around(blk, k, blks),
        )
        for k in range(1, blks)
    ]
    start(g_copies)
    acc_out[...] = jnp.zeros_like(acc_out)
    acc_row[...] = jnp.zeros_like(acc_row)
    finish(dos_copies)
    finish(r_copies)

    out_rows = doa[...].reshape(slots, model)
    rx[head, :, 0:model] = ra[...].reshape(slots, model)
    finish(g_copies)
    gate_col = own_columns(gate_rows, turned, blk, capacity)
    rx[head, :, model : 2 * model] = (out_rows.astype(F32) * gate_col).astype(BF16)
    core = lax.rem(head, 2)
    sibling, across = head - core + 1 - core, around(head, 2, heads)

    def half_rows(source, half):
        return rx.at[source, pl.ds(half * slots // 2, slots // 2)]

    to_across = [
        remote(
            half_rows(head, half), half_rows(head, half),
            rx_send.at[1 + half], rx_recv.at[1 + half], across, blk,
        )
        for half in range(2)
    ]
    to_sibling = remote(rx.at[head], rx.at[head], rx_send.at[0], rx_recv.at[0], sibling, blk)
    forwards = [
        remote(
            half_rows(across, half), half_rows(across, half),
            rx_send.at[3 + half], rx_recv.at[3 + half], sibling, blk,
        )
        for half in range(2)
    ]
    start(to_across)
    to_sibling.start()
    half_ff = wout_ref.shape[0] // 4
    for copy in fetched[4:]:
        copy.wait()

    @pl.loop(0, 4)
    def _(chunk):
        first = pl.multiple_of(chunk * half_ff, half_ff)
        into = win_ref[:, pl.ds(first, half_ff)]
        outof = wout_ref[pl.ds(first, half_ff), :]
        act, slope = gelu_parts(dot(rx[head, :, 0:model], into))
        acc_out[...] += dot(act.astype(BF16), outof)
        d_act = dot(rx[head, :, model : 2 * model], outof, (1, 1))
        acc_row[...] += dot((slope * d_act).astype(BF16), into, (1, 1))

    result = acc_out[...].astype(BF16)
    d_gate = jnp.sum(out_rows.astype(F32) * result.astype(F32), axis=1, keepdims=True)
    dr[...] = acc_row[...].astype(BF16).reshape(dr.shape)
    dr_copies = blk_copies(dr, da, dr_send, dr_recv)
    start(dr_copies)
    da[blk] = dr[blk]
    d_wide = jnp.broadcast_to(d_gate, (slots, LANES))
    d_gate_rows[blk] = jnp.concatenate(
        [jnp.transpose(d_wide[i * LANES : (i + 1) * LANES])[0:1] for i in range(slots // LANES)],
        axis=1,
    )
    dg_copies = [
        remote(
            d_gate_rows.at[blk], d_gate_rows.at[blk],
            dg_send.at[k], dg_recv.at[k], head, around(blk, k, blks),
        )
        for k in range(1, blks)
    ]
    start(dg_copies)
    po[...] = result.reshape(blks, capacity, model)

    finish(dg_copies)
    back_gate = own_columns(d_gate_rows, turned, blk, capacity)
    back_gate = split_high_low(back_gate, lane_ids((slots, LANES)))
    d_gates = [join_high_low(dot(p, back_gate), 0) for p in put]
    d_probs = jnp.where(hots[0], d_gates[0], 0.0) + jnp.where(hots[1], d_gates[1], 0.0)
    d_logits = probs * (d_probs - jnp.sum(probs * d_probs, axis=1, keepdims=True))
    d_high = d_logits.astype(BF16)
    d_low = (d_logits - d_high.astype(F32)).astype(BF16)
    d_router_part = dot(d_high, small, (1, 1)) + dot(d_low, small, (1, 1))
    finish(dr_copies)
    d_routed = dot(put_any, da[...].reshape(slots, model)) + d_router_part
    d_hidden = d_out + centre_back(d_routed * gain, xhat, scale)
    dh_ref[...] = d_hidden
    d_attn = d_hidden.astype(BF16)
    d_mixed = dot(d_attn, weight_out, (1, 1))
    for piece in range(heads):
        block = d_mixed[:, piece * LANES : (piece + 1) * LANES]
        for to_y in range(2):
            dms[to_y, piece] = halves(block, low_lanes == (to_y == 1)).astype(BF16)
    dm_copies = plane_copies(lambda to_y, to_head: dms.at[to_y, to_head], dma_all.at[y, head], dm_send, dm_recv)
    start(dm_copies)
    dma_all[y, head] = dms[y, head]
    first_half = pa.shape[1]
    pa_copies = [
        remote(
            po.at[around(blk, k, blks), pl.ds(0, first_half)], pa.at[blk],
            pa_send.at[k], pa_recv.at[k], head, around(blk, k, blks),
        )
        for k in range(1, blks)
    ]
    start(pa_copies)
    pa[blk] = po[blk, 0:first_half]
    arrived(half_rows(across, 0), rx_recv.at[1])
    forwards[0].start()

    d_weight = dot(mixed, d_attn, (0, 0)).astype(BF16)
    for b in range(blks):
        grads_ref[b, :, 0:model] = d_weight[(b ^ 1) * HALF : ((b ^ 1) + 1) * HALF, :]
    last = (lanes == blks).astype(BF16)
    d_small = dot(routed, d_high, (0, 0)) + dot((d_routed * xhat).astype(BF16), last, (0, 0))
    grads_ref[:, :, model : model + LANES] = d_small.astype(BF16).reshape(blks, HALF, LANES)
    share = gates[0] * put[0].astype(F32) + gates[1] * put[1].astype(F32)
    share_ref[0] = share.astype(BF16)
    share_ref[1] = (share - share_ref[0].astype(F32)).astype(BF16)
    hidden_ref[...] = hidden

    arrived(half_rows(across, 1), rx_recv.at[2])
    forwards[1].start()
    finish(dm_copies)
    finish(pa_copies)
    to_sibling.wait()
    for copy in to_across:
        copy.wait_send()
    finish(forwards)


def call_middle(x, o, wo, routes, rank, d_out, win, wout, heads, blks):
    tokens, model = x.shape
    capacity = 2 * tokens // blks
    slots = capacity * blks
    wide = model + LANES

    def rows(width):
        return pltpu.VMEM((blks, capacity, width), BF16)

    def block(*lead):
        return pltpu.VMEM((*lead, tokens // 2, LANES), BF16)

    return pl.pallas_call(
        functools.partial(middle_kernel, heads, blks),
        out_shape=(
            jax.ShapeDtypeStruct((blks, capacity, model), BF16),
            jax.ShapeDtypeStruct((blks, capacity // 2, model), BF16),
            jax.ShapeDtypeStruct((tokens, model), F32),
            jax.ShapeDtypeStruct((2, tokens, slots), BF16),
            jax.ShapeDtypeStruct((tokens, model), F32),
            jax.ShapeDtypeStruct((2, heads, tokens // 2, LANES), BF16),
            jax.ShapeDtypeStruct((blks, model // blks, wide), BF16),
            jax.ShapeDtypeStruct((heads, slots, 2 * model), BF16),
        ),
        in_specs=hbm_specs(1) + vmem_specs(2) + hbm_specs(5),
        out_specs=tuple(vmem_specs(8)),
        scratch_shapes=[
            pltpu.VMEM((tokens, model), BF16),
            pltpu.VMEM((2, tokens), jnp.int32),
            pltpu.VMEM((1, tokens), jnp.int32),
            pltpu.VMEM((tokens, model), F32),
            pltpu.VMEM(win.shape, BF16),
            pltpu.VMEM(wout.shape, BF16),
            pltpu.VMEM((tokens, tokens), F32),
            dma(6),
            block(2, heads), rows(model), rows(model), rows(model), rows(model),
            rows(model), rows(model), block(2, heads),
            pltpu.VMEM((slots, model), F32), pltpu.VMEM((slots, model), F32),
            pltpu.VMEM((tokens, model), BF16),
            pltpu.VMEM((blks, 1, slots), F32), pltpu.VMEM((blks, 1, slots), F32),
            pltpu.VMEM((slots, LANES), F32),
            dma(2 * heads), dma(2 * heads), dma(blks), dma(blks), dma(blks), dma(blks),
            dma(blks), dma(blks), dma(2 * heads), dma(2 * heads), dma(5), dma(5),
            dma(blks), dma(blks), dma(blks), dma(blks), dma(blks), dma(blks),
        ],
        compiler_params=pltpu.CompilerParams(
            collective_id=2, has_side_effects=True, vmem_limit_bytes=20 * MIB
        ),
        name="experts",
    )(*in_hbm(x), o, wo, *in_hbm(routes.T, rank, d_out, win, wout))


def last_kernel(
    heads, blks,
    x_hbm, dh_ref, begun_ref, dkv_ref, xa_ref, wa_ref, w_hbm, g1_hbm, grads_ref, rx_ref, win_hbm, wout_hbm,
    po_ref, pa_ref, hidden_ref, share_ref, bounds_ref, q_ref, kv_ref, kvt_ref, do_ref, lse_ref, delta_ref,
    y_ref, dx_ref, dw_ref, shared_ref, din_ref, dout_ref,
    x_ref, w_ref, g1_ref, win_ref, wout_ref, in_sem,
    gain_tile, far_all, near_send_buf, near_all, pair_all, dq_all, dq_ref, dq_packed, dkv_own, pair_buf, us, ua, gs, ga, gqs, gqa, u_part, xat, pa, gh, ghq, w1, w2s, w2, w3,
    q_send, q_recv, pair_send, pair_recv, far_send, far_recv, near_send, near_recv,
    u_send, u_recv, g_send, g_recv, gh_send, gh_recv, w1_send, w1_recv, w2_send, w2_recv,
    w3_send, w3_recv, e_send, e_recv, gq_send, gq_recv, po_send, po_recv, ghq_send, ghq_recv,
    din_half, dout_half,
):
    head, blk, z, y = place()
    planes = blks // 2
    tokens, model = x_ref.shape
    rows = w_ref.shape[0]
    wanted = (
        (win_hbm, win_ref), (wout_hbm, wout_ref), (x_hbm, x_ref), (w_hbm, w_ref), (g1_hbm, g1_ref)
    )
    fetched = [
        pltpu.make_async_copy(src, dst, in_sem.at[i]) for i, (src, dst) in enumerate(wanted)
    ]
    for copy in fetched:
        copy.start()
    met = greet(
        [(around(head, k, heads), blk) for k in range(1, heads)]
        + [(head, around(blk, k, blks)) for k in range(1, blks)]
    )
    meet(met)

    def start(copies):
        for copy in copies:
            copy.start()

    def finish(copies):
        for copy in copies:
            copy.wait()

    other_y = around(y, 1, 2)
    pair = 2 * z + other_y
    above, below = z < planes - 1, z > 0
    directions = ((1, above, below, 0), (-1, below, above, 2))

    half_span = dkv_ref.shape[1] // 2

    def half_of(ref, half):
        return ref.at[pl.ds(half * half_span, half_span)]

    def far_copy(step, slot, side, half):
        span = 2 * (z + 2 * step) + side
        return remote(
            half_of(dkv_ref.at[span], half), half_of(far_all.at[slot + side], half),
            far_send.at[slot + side, half], far_recv.at[slot + side, half], head, 2 * (z + step) + y,
        )

    def near_copy(step, slot, side, half):
        return remote(
            half_of(near_send_buf.at[slot + side], half), half_of(near_all.at[slot // 2, y], half),
            near_send.at[slot + side, half], near_recv.at[slot // 2, y, half],
            head, 2 * (z + step) + side,
        )

    def two_away(step):
        return z + 2 * step < planes if step > 0 else z + 2 * step >= 0

    for half in range(2):
        for step, there, back, slot in directions:

            @pl.when(two_away(step))
            def _():
                for side in range(2):
                    far_copy(step, slot, side, half).start()

    w1_copies = [
        remote(
            grads_ref.at[:, around(head, k, heads)], w1.at[head],
            w1_send.at[k], w1_recv.at[k], around(head, k, heads), blk,
        )
        for k in range(1, heads)
    ]
    start(w1_copies)
    w1[head] = grads_ref[:, head]

    core = lax.rem(head, 2)
    sibling = head - core + 1 - core
    ff_half = wout_ref.shape[0] // 2
    ff_step = ff_half // 4

    def expert_chunk(chunk):
        here = pl.multiple_of(core * ff_half + chunk * ff_step, ff_step)
        there = pl.multiple_of(chunk * ff_step, ff_step)
        into = win_ref[:, pl.ds(here, ff_step)]
        outof = wout_ref[pl.ds(here, ff_step), :]
        d_in = jnp.zeros((model, ff_step), F32)
        d_out = jnp.zeros((ff_step, model), F32)
        for source in range(heads):
            rows_in = rx_ref[source, :, 0:model]
            grads_out = rx_ref[source, :, model : 2 * model]
            act, slope = gelu_parts(dot(rows_in, into))
            d_act = dot(grads_out, outof, (1, 1))
            d_in = d_in + dot(rows_in, (slope * d_act).astype(BF16), (0, 0))
            d_out = d_out + dot(act.astype(BF16), grads_out, (0, 0))
        din_ref[:, pl.ds(here, ff_step)] = d_in
        dout_ref[pl.ds(here, ff_step), :] = d_out
        din_half[core, :, pl.ds(there, ff_step)] = d_in.astype(BF16)
        dout_half[core, pl.ds(there, ff_step), :] = d_out.astype(BF16)

    key_tile = kv_ref.shape[1]
    for group in range(2 * key_tile // (CHAINS * QUERY_TILE)):
        tiles, queries = query_group(q_ref, group, y)
        known = (
            queries,
            group_grads(do_ref, tiles, y),
            [delta_ref[tile, 0:1, :] for tile in tiles],
            [lse_ref[tile, 0:1, :] for tile in tiles],
        )
        carry = tuple(begun_ref[tile] for tile in tiles)
        for side in range(2):
            first = pl.multiple_of((2 * z + side) * key_tile, key_tile)
            keys_across = kvt_ref[:, pl.ds(first, key_tile)]
            given, carry = attend_back(
                bounds_ref, tiles, first, kv_ref[2 * z + side], keys_across, known, carry
            )
            dkv_own[side] = given if group == 0 else dkv_own[side] + given
        for tile, total in zip(tiles, carry):
            at = tile * QUERY_TILE % key_tile
            dq_ref[tile * QUERY_TILE // key_tile, at : at + QUERY_TILE] = jnp.transpose(total)
    pair_buf[...] = dkv_own[other_y].astype(BF16)
    pair_copy = remote(pair_buf, pair_all, pair_send, pair_recv, head, pair)
    pair_copy.start()
    own_lanes = (lane_ids(dq_packed.shape) < HALF) == (y == 0)
    dq_packed[...] = halves(dq_ref[other_y], own_lanes).astype(BF16)
    q_copy = remote(dq_packed, dq_all, q_send, q_recv, head, pair)
    q_copy.start()
    for half in range(2):
        rows_here = slice(half * half_span, (half + 1) * half_span)
        for step, there, back, slot in directions:

            @pl.when(there)
            def _():
                for side in range(2):
                    near_send_buf[slot + side, rows_here] = dkv_ref[2 * (z + step) + side, rows_here]

            @pl.when(jnp.logical_and(there, back))
            def _():
                for side in range(2):
                    arrived(half_of(far_all.at[slot + side], half), far_recv.at[slot + side, half])
                    near_send_buf[slot + side, rows_here] = (
                        near_send_buf[slot + side, rows_here].astype(F32)
                        + far_all[slot + side, rows_here].astype(F32)
                    ).astype(BF16)

            @pl.when(there)
            def _():
                for side in range(2):
                    near_copy(step, slot, side, half).start()

    finish(fetched[:2])
    weight = wa_ref[...].reshape(model, 3 * LANES)
    for piece in range(heads):
        xat[:, piece * tokens : (piece + 1) * tokens] = jnp.transpose(xa_ref[piece])
    even = y == 0


    @pl.loop(0, 2)
    def _(chunk):
        expert_chunk(chunk)

    q_copy.wait()
    landed = dq_all[...].astype(F32)
    landed = jnp.concatenate([landed, pltpu.roll(landed, HALF, 1)], axis=0)
    own_lanes = (lane_ids(landed.shape) < HALF) == even
    q_grads = jnp.where(own_lanes, dq_ref[y], landed).astype(BF16)
    gqs[...] = dot(xat[...], q_grads).astype(BF16).reshape(gqs.shape)
    gq_copies = [
        remote(
            gqs.at[around(blk, k, blks)], gqa.at[blk],
            gq_send.at[k], gq_recv.at[k], head, around(blk, k, blks),
        )
        for k in range(1, blks)
    ]
    start(gq_copies)
    gqa[blk] = gqs[blk]
    u_part[...] = dot(q_grads, weight[:, 2 * LANES : 3 * LANES], (1, 1)).reshape(u_part.shape)

    finish(w1_copies)
    summed = w1[0].astype(F32)
    for source in range(1, heads):
        summed = summed + w1[source].astype(F32)
    w2s[...] = summed.astype(BF16)
    w2_copies = [
        remote(
            w2s.at[around(blk, k, blks)], w2.at[blk],
            w2_send.at[k], w2_recv.at[k], head, around(blk, k, blks),
        )
        for k in range(1, blks)
    ]
    start(w2_copies)
    w2[blk] = w2s[blk]

    @pl.loop(2, 4)
    def _(chunk):
        expert_chunk(chunk)

    e_copies = [
        remote(din_half.at[core], din_half.at[core], e_send.at[0], e_recv.at[0], sibling, blk),
        remote(dout_half.at[core], dout_half.at[core], e_send.at[1], e_recv.at[1], sibling, blk),
    ]
    start(e_copies)

    pair_copy.wait()
    for step, there, back, slot in directions:

        @pl.when(back)
        def _():
            for side in range(2):
                for half in range(2):
                    arrived(
                        half_of(near_all.at[slot // 2, side], half),
                        near_recv.at[slot // 2, side, half],
                    )

        @pl.when(jnp.logical_not(back))
        def _():
            near_all[slot // 2] = jnp.zeros(near_all.shape[1:], BF16)

    own = dkv_own[y]
    other = pair_all[...].astype(F32)
    made = jnp.concatenate(
        [
            (
                jnp.where(even == (side == 0), own, other)
                + near_all[0, side].astype(F32)
                + near_all[1, side].astype(F32)
            ).astype(BF16)
            for side in range(2)
        ],
        axis=1,
    )
    gs[...] = dot(xat[...], made).astype(BF16).reshape(gs.shape)
    g_copies = [
        remote(
            gs.at[around(blk, k, blks)], ga.at[blk],
            g_send.at[k], g_recv.at[k], head, around(blk, k, blks),
        )
        for k in range(1, blks)
    ]
    start(g_copies)
    ga[blk] = gs[blk]
    us[...] = (
        u_part[...] + dot(made, weight[:, 0 : 2 * LANES], (1, 1)).reshape(us.shape)
    ).astype(BF16)
    u_copies = [
        remote(
            us.at[around(head, k, heads)], ua.at[head],
            u_send.at[k], u_recv.at[k], around(head, k, heads), blk,
        )
        for k in range(1, heads)
    ]
    start(u_copies)
    ua[head] = us[head]
    finish(fetched[2:])
    finish(gq_copies)
    total = gqa[0].astype(F32)
    for source in range(1, blks):
        total = total + gqa[source].astype(F32)
    ghq[head] = total.astype(BF16)
    ghq_copies = [
        remote(ghq.at[head], ghq.at[head], ghq_send.at[k], ghq_recv.at[k], around(head, k, heads), blk)
        for k in range(1, heads)
    ]
    start(ghq_copies)

    finish(w2_copies)
    part = w2[0].astype(F32)
    for source in range(1, blks):
        part = part + w2[source].astype(F32)
    w3[head] = part.astype(BF16)
    w3_copies = [
        remote(w3.at[head], w3.at[head], w3_send.at[k], w3_recv.at[k], around(head, k, heads), blk)
        for k in range(1, heads)
    ]
    start(w3_copies)

    xhat, scale = centre(x_ref[...].astype(F32))
    finish(e_copies)
    there = pl.multiple_of((1 - core) * ff_half, ff_half)
    din_ref[:, pl.ds(there, ff_half)] = din_half[1 - core].astype(F32)
    dout_ref[pl.ds(there, ff_half), :] = dout_half[1 - core].astype(F32)
    finish(g_copies)
    total = ga[0].astype(F32)
    for source in range(1, blks):
        total = total + ga[source].astype(F32)
    gh[head] = total.astype(BF16)
    gh_copies = [
        remote(gh.at[head], gh.at[head], gh_send.at[k], gh_recv.at[k], around(head, k, heads), blk)
        for k in range(1, heads)
    ]
    start(gh_copies)
    half_slots = pa_ref.shape[1]
    po_copies = [
        remote(
            po_ref.at[around(blk, k, blks), pl.ds(half_slots, half_slots)], pa.at[blk],
            po_send.at[k], po_recv.at[k], head, around(blk, k, blks),
        )
        for k in range(1, blks)
    ]
    start(po_copies)
    pa[blk] = po_ref[blk, half_slots : 2 * half_slots]
    finish(u_copies)
    grad = ua[0].astype(F32)
    for source in range(1, heads):
        grad = grad + ua[source].astype(F32)
    dx_ref[...] = dh_ref[...] + centre_back(grad, xhat, scale)

    gain_tile[...] = jnp.zeros_like(gain_tile)
    gain_tile[0:1, 0:rows] = g1_ref[...].astype(F32)
    gain = jnp.transpose(jnp.broadcast_to(gain_tile[0:1, :], (LANES, LANES)))[:rows]
    low_half = lane_ids((rows, LANES)) < HALF
    finish(ghq_copies)
    finish(gh_copies)
    d_gain = jnp.zeros((rows, LANES), F32)
    for source in range(heads):
        both = [gh[source, :, i * LANES : (i + 1) * LANES].astype(F32) for i in range(2)]
        grads = (
            ghq[source].astype(F32) * HS ** (-0.5),
            jnp.where(low_half, both[0], both[1]),
            pltpu.roll(jnp.where(low_half, both[1], both[0]), HALF, 1),
        )
        for which, value in enumerate(grads):
            columns = slice(which * model + source * LANES, which * model + (source + 1) * LANES)
            d_gain = d_gain + value * w_ref[:, columns].astype(F32)
            dw_ref[:, columns] = value * gain
    finish(w3_copies)
    shared = w3[...].reshape(rows, w3.shape[-1]).astype(F32)
    shared_ref[:, 0:model] = shared[:, 0:model]
    gain_col = jnp.sum(d_gain, axis=1, keepdims=True)
    shared_ref[:, model : model + LANES] = jnp.where(
        lane_ids((rows, LANES)) == blks + 1, gain_col, shared[:, model : model + LANES]
    )
    finish(po_copies)
    parts = jnp.concatenate([pa_ref[...], pa[...]], axis=1).reshape(share_ref.shape[2], model)
    mixture = dot(share_ref[0], parts) + dot(share_ref[1], parts)
    y_ref[...] = (hidden_ref[...] + mixture).astype(BF16)

    for step, there, back, slot in directions:

        @pl.when(two_away(step))
        def _():
            for side in range(2):
                for half in range(2):
                    far_copy(step, slot, side, half).wait_send()

        @pl.when(there)
        def _():
            for side in range(2):
                for half in range(2):
                    near_copy(step, slot, side, half).wait_send()


def call_last(
    x, dh, dq, dkv, xa, wa, w_qkv, g1, grads, rx, win, wout, po, pa, hidden, share,
    bounds, q, kv, kvt, d_o, lse, delta, heads, blks,
):
    tokens, model = x.shape
    span = tokens * heads
    rows = w_qkv.shape[0]
    wide = model + LANES
    part = rows // heads
    ff = wout.shape[0]

    def block(*lead):
        return pltpu.VMEM((*lead, span, LANES), BF16)

    return pl.pallas_call(
        functools.partial(last_kernel, heads, blks),
        out_shape=(
            jax.ShapeDtypeStruct((tokens, model), BF16),
            jax.ShapeDtypeStruct((tokens, model), F32),
            jax.ShapeDtypeStruct((rows, 3 * model), F32),
            jax.ShapeDtypeStruct((rows, wide), F32),
            jax.ShapeDtypeStruct((model, ff), F32),
            jax.ShapeDtypeStruct((ff, model), F32),
        ),
        in_specs=hbm_specs(1) + vmem_specs(5) + hbm_specs(2) + vmem_specs(2) + hbm_specs(2) + vmem_specs(11),
        out_specs=tuple(vmem_specs(6)),
        scratch_shapes=[
            pltpu.VMEM((tokens, model), BF16),
            pltpu.VMEM((rows, 3 * model), BF16),
            pltpu.VMEM((1, rows), BF16),
            pltpu.VMEM(win.shape, BF16),
            pltpu.VMEM(wout.shape, BF16),
            dma(5),
            pltpu.VMEM((8, LANES), F32),
            block(4), block(4), block(2, 2), block(), pltpu.VMEM((span // 2, LANES), BF16),
            pltpu.VMEM((2, span, LANES), F32), pltpu.VMEM((span // 2, LANES), BF16),
            pltpu.VMEM((2, span, LANES), F32), block(),
            pltpu.VMEM((heads, tokens, model), BF16), pltpu.VMEM((heads, tokens, model), BF16),
            pltpu.VMEM((blks, rows, 2 * LANES), BF16), pltpu.VMEM((blks, rows, 2 * LANES), BF16),
            pltpu.VMEM((blks, rows, LANES), BF16), pltpu.VMEM((blks, rows, LANES), BF16),
            pltpu.VMEM((heads, tokens, model), F32), pltpu.VMEM((model, span), BF16),
            pltpu.VMEM(pa.shape, BF16),
            pltpu.VMEM((heads, rows, 2 * LANES), BF16), pltpu.VMEM((heads, rows, LANES), BF16),
            pltpu.VMEM((heads, blks, part, wide), BF16), pltpu.VMEM((blks, part, wide), BF16),
            pltpu.VMEM((blks, part, wide), BF16), pltpu.VMEM((heads, part, wide), BF16),
            pltpu.SemaphoreType.DMA, pltpu.SemaphoreType.DMA, pltpu.SemaphoreType.DMA, pltpu.SemaphoreType.DMA,
            dma(4, 2), dma(4, 2), dma(4, 2), dma(2, 2, 2),
            dma(heads), dma(heads), dma(blks), dma(blks), dma(heads), dma(heads), dma(heads), dma(heads),
            dma(blks), dma(blks), dma(heads), dma(heads), dma(2), dma(2), dma(blks), dma(blks), dma(blks), dma(blks), dma(heads), dma(heads),
            pltpu.VMEM((2, model, ff // 2), BF16), pltpu.VMEM((2, ff // 2, model), BF16),
        ],
        compiler_params=pltpu.CompilerParams(
            collective_id=3, has_side_effects=True, vmem_limit_bytes=36 * MIB
        ),
        name="last",
    )(
        *in_hbm(x), dh, dq, dkv, xa, wa, *in_hbm(w_qkv, g1.reshape(1, rows)),
        grads.reshape(blks, heads, part, wide), rx, *in_hbm(win, wout), po, pa, hidden, share,
        bounds, q, kv, kvt, d_o, lse, delta,
    )


def finish_kernel(
    experts,
    y_ref, dx_ref, dw_ref, shared_ref, din_ref, dout_ref,
    y_out, dx_out, g1_out, dw_out, dwo_out, g2_out, wr_out, din_out, dout_out,
    tile, wr, g2, g1, sem,
):
    rows = shared_ref.shape[0]
    model = dx_ref.shape[1]
    copies = [
        pltpu.make_async_copy(dx_ref, dx_out, sem.at[0]),
        pltpu.make_async_copy(dw_ref, dw_out, sem.at[1]),
        pltpu.make_async_copy(shared_ref.at[:, pl.ds(0, model)], dwo_out, sem.at[2]),
        pltpu.make_async_copy(y_ref, y_out, sem.at[6]),
        pltpu.make_async_copy(din_ref, din_out, sem.at[7]),
        pltpu.make_async_copy(dout_ref, dout_out, sem.at[8]),
    ]
    for copy in copies:
        copy.start()
    tile[...] = jnp.zeros_like(tile)
    tile[0:rows, :] = shared_ref[:, model : model + LANES]
    across = jnp.transpose(tile[...])[:, 0:rows]
    wr[...] = across[0:experts]
    g2[...] = across[experts : experts + 1]
    g1[...] = across[experts + 1 : experts + 2]
    for index, (src, dst) in enumerate(((wr, wr_out), (g2, g2_out), (g1, g1_out))):
        copies.append(pltpu.make_async_copy(src, dst, sem.at[3 + index]))
        copies[-1].start()
    for copy in copies:
        copy.wait()


def call_finish(output, dx, dw, shared, d_in, d_out):
    rows = shared.shape[0]
    model = dx.shape[1]
    experts = model // rows
    return pl.pallas_call(
        functools.partial(finish_kernel, experts),
        out_shape=(
            jax.ShapeDtypeStruct(output.shape, BF16),
            jax.ShapeDtypeStruct(dx.shape, F32),
            jax.ShapeDtypeStruct((1, rows), F32),
            jax.ShapeDtypeStruct(dw.shape, F32),
            jax.ShapeDtypeStruct((rows, model), F32),
            jax.ShapeDtypeStruct((1, rows), F32),
            jax.ShapeDtypeStruct((experts, rows), F32),
            jax.ShapeDtypeStruct(d_in.shape, F32),
            jax.ShapeDtypeStruct(d_out.shape, F32),
        ),
        in_specs=vmem_specs(6),
        out_specs=tuple(hbm_specs(9)),
        scratch_shapes=[
            pltpu.VMEM((LANES, LANES), F32),
            pltpu.VMEM((experts, rows), F32),
            pltpu.VMEM((1, rows), F32),
            pltpu.VMEM((1, rows), F32),
            dma(9),
        ],
        compiler_params=pltpu.CompilerParams(vmem_limit_bytes=16 * MIB),
        name="finish",
    )(output, dx, dw, shared, d_in, d_out)


def local_kernels(
    inputs, ln1_gain, w_qkv, w_out, ln2_gain, w_router,
    expert_in, expert_out, routes, priority, doc_lengths, d_out,
):
    heads, blks = lax.axis_size("head"), lax.axis_size("blk")
    model = inputs.shape[1]
    tokens = inputs.shape[0]
    win, wout = expert_in[0], expert_out[0]
    q, kv, xa, wa, wo, kvt, bounds, begun = call_qkv(
        inputs, w_qkv, ln1_gain, w_out, w_router, ln2_gain, doc_lengths, heads, blks
    )
    o, o_low, lse = call_forward(bounds, q, kv, kvt, begun)
    po, pa, hidden, share, dh, d_o, grads, rx = call_middle(
        inputs, o_low.reshape(2, heads, tokens // 2, LANES), wo.reshape(model, model + LANES),
        routes, priority, d_out, win, wout, heads, blks,
    )
    d_o = d_o.reshape(2 * heads * tokens // QUERY_TILE, -1, HALF, LANES)
    dq, dkv, delta = call_backward(bounds, q, kv, kvt, d_o, o, lse)
    ends = call_last(
        inputs, dh, dq, dkv, xa, wa, w_qkv, ln1_gain, grads, rx, win, wout,
        po, pa, hidden, share, bounds, q, kv, kvt, d_o, lse, delta, heads, blks,
    )
    output, d_inputs, d_gain_one, d_qkv, d_out_proj, d_gain_two, d_router, d_in, d_out_weight = call_finish(*ends)
    return (
        output,
        d_inputs,
        d_gain_one.reshape(-1),
        d_qkv,
        d_out_proj,
        d_gain_two.reshape(-1),
        d_router.T,
        d_in[None],
        d_out_weight[None],
    )


def solution(mesh):
    in_specs = (
        P(("blk", "head"), None),
        P("blk"),
        P("blk", None),
        P("blk", None),
        P("blk"),
        P("blk", None),
        P("blk", None, None),
        P("blk", None, None),
        P(("blk", "head"), None),
        P(("blk", "head"), None),
        P(),
        P(("blk", "head"), None),
    )
    out_specs = (
        P(("blk", "head"), None),
        P(("blk", "head"), None),
        P("blk"),
        P("blk", None),
        P("blk", None),
        P("blk"),
        P("blk", None),
        P("blk", None, None),
        P("blk", None, None),
    )
    fits = mesh.shape["head"] == 4 and mesh.shape["blk"] == 8
    body = local_kernels if fits else local
    return jax.shard_map(body, mesh=mesh, in_specs=in_specs, out_specs=out_specs, check_vma=False)
```

```python
import functools
import math

import jax
import jax.numpy as jnp
from jax import lax
from jax.experimental import pallas as pl
from jax.experimental.pallas import tpu as pltpu
from jax.sharding import PartitionSpec as P

HS = 64
KEY_BLOCK = 2048


PRECISE = lax.Precision.HIGHEST
MASKED = -1e30
EPSILON = 1e-06


def layer_norm(values, gain):
    average = jnp.mean(values, axis=-1, keepdims=True)
    centred = values - average
    spread = jnp.mean(centred * centred, axis=-1, keepdims=True)
    return centred * lax.rsqrt(spread + EPSILON) * gain


def gelu_exact(values):
    return jax.nn.gelu(values, approximate=False)


def router(row_block, weight):
    return jax.nn.softmax(jnp.dot(row_block, weight, precision=PRECISE), axis=-1)


def doc_index(positions, doc_lengths):
    places = jnp.arange(doc_lengths.shape[0], dtype=jnp.int32)
    starts = jnp.sum(jnp.where(places[None, :] < places[:, None], doc_lengths[None, :], 0), axis=1)
    at_most = (starts[None, :] <= positions[:, None]).astype(jnp.int32)
    return jnp.sum(at_most, axis=1) - 1


def slot_table(route_rows, ranking, capacity):
    token_count = route_rows.shape[0]
    expert = jnp.transpose(route_rows).reshape(-1)
    pair_order = (jnp.arange(2, dtype=jnp.int32)[:, None] * token_count + ranking[None, :]).reshape(
        -1
    )
    before = (expert[:, None] == expert[None, :]) & (pair_order[None, :] < pair_order[:, None])
    position = jnp.sum(before.astype(jnp.int32), axis=1)
    slot_ids = jnp.where(position < capacity, expert * capacity + position, -1)
    return slot_ids.reshape(2, token_count)


def keep_state(current):
    return current


def local(
    inputs,
    ln1_gain,
    w_qkv,
    w_out,
    ln2_gain,
    w_router,
    expert_in,
    expert_out,
    routes,
    priority,
    doc_lengths,
    d_out,
):
    blk_size = lax.axis_size("blk")
    tok_rows = inputs.shape[0]
    model_width = inputs.shape[1]
    capacity = 2 * tok_rows // blk_size
    slot_total = blk_size * capacity
    gain_one, qkv_weight, out_weight, gain_two, router_weight = (
        lax.all_gather(ln1_gain, "blk", axis=0, tiled=True),
        lax.all_gather(w_qkv, "blk", axis=0, tiled=True),
        lax.all_gather(w_out, "blk", axis=0, tiled=True),
        lax.all_gather(ln2_gain, "blk", axis=0, tiled=True),
        lax.all_gather(w_router, "blk", axis=0, tiled=True),
    )
    input_rows = inputs.astype(jnp.float32)
    normed_one, norm_one_pull = jax.vjp(layer_norm, input_rows, gain_one.astype(jnp.float32))
    normed_low = normed_one.astype(jnp.bfloat16)
    qkv_rows = jnp.dot(normed_low, qkv_weight, preferred_element_type=jnp.float32).astype(
        jnp.bfloat16
    )
    query_heads, key_heads, value_heads = (
        lax.all_to_all(qkv_rows[:, :model_width], "head", split_axis=1, concat_axis=0, tiled=True),
        lax.all_to_all(
            qkv_rows[:, model_width : 2 * model_width],
            "head",
            split_axis=1,
            concat_axis=0,
            tiled=True,
        ),
        lax.all_to_all(
            qkv_rows[:, 2 * model_width :], "head", split_axis=1, concat_axis=0, tiled=True
        ),
    )
    span_rows = query_heads.shape[0]
    head_count = query_heads.shape[1] // HS
    key_all, value_all = (
        lax.all_gather(key_heads, "blk", axis=0, tiled=True),
        lax.all_gather(value_heads, "blk", axis=0, tiled=True),
    )
    total_rows = key_all.shape[0]
    block_count = total_rows // KEY_BLOCK
    scale_factor = HS ** (-0.5)
    query_pos = lax.axis_index("blk") * span_rows + jnp.arange(span_rows, dtype=jnp.int32)
    query_docs = doc_index(query_pos, doc_lengths)
    queries = query_heads.reshape(span_rows, head_count, HS)

    def block_parts(block_index, key_source, value_source):
        first_key = block_index * KEY_BLOCK
        key_rows = lax.dynamic_slice_in_dim(key_source, first_key, KEY_BLOCK, 0).reshape(
            KEY_BLOCK, head_count, HS
        )
        value_rows = lax.dynamic_slice_in_dim(value_source, first_key, KEY_BLOCK, 0).reshape(
            KEY_BLOCK, head_count, HS
        )
        key_docs = doc_index(first_key + jnp.arange(KEY_BLOCK, dtype=jnp.int32), doc_lengths)
        is_live = (key_docs[0] <= query_docs[-1]) & (key_docs[-1] >= query_docs[0])
        same_doc = query_docs[:, None] == key_docs[None, :]
        return (first_key, key_rows, value_rows, same_doc, is_live)

    def block_scores(key_rows, same_doc):
        raw_scores = (
            jnp.einsum("qhd,khd->hqk", queries, key_rows, preferred_element_type=jnp.float32)
            * scale_factor
        )
        return jnp.where(same_doc[None], raw_scores, MASKED)

    def stat_step(block_index, loop_state):
        first_key, key_rows, value_rows, same_doc, is_live = block_parts(
            block_index, key_all, value_all
        )

        def stat_update(current):
            running_max, running_sum = current
            scores = block_scores(key_rows, same_doc)
            new_max = jnp.maximum(running_max, jnp.max(scores, axis=2))
            exp_terms = jnp.where(same_doc[None], jnp.exp(scores - new_max[:, :, None]), 0.0)
            return (
                new_max,
                running_sum * jnp.exp(running_max - new_max) + jnp.sum(exp_terms, axis=2),
            )

        return lax.cond(is_live, stat_update, keep_state, loop_state)

    start_state = (
        jnp.full((head_count, span_rows), MASKED, jnp.float32),
        jnp.zeros((head_count, span_rows), jnp.float32),
    )
    running_max, running_sum = lax.fori_loop(0, block_count, stat_step, start_state)
    log_total = running_max + jnp.log(running_sum)

    def out_step(block_index, loop_state):
        first_key, key_rows, value_rows, same_doc, is_live = block_parts(
            block_index, key_all, value_all
        )

        def out_update(current):
            scores = block_scores(key_rows, same_doc)
            weights = jnp.where(
                same_doc[None], jnp.exp(scores - log_total[:, :, None]), 0.0
            ).astype(jnp.bfloat16)
            return current + jnp.einsum(
                "hqk,khd->qhd", weights, value_rows, preferred_element_type=jnp.float32
            )

        return lax.cond(is_live, out_update, keep_state, loop_state)

    mixed_full = lax.fori_loop(
        0, block_count, out_step, jnp.zeros((span_rows, head_count, HS), jnp.float32)
    )
    mixed_low = mixed_full.reshape(span_rows, head_count * HS).astype(jnp.bfloat16)
    mixed_tokens = lax.all_to_all(mixed_low, "head", split_axis=0, concat_axis=1, tiled=True)
    attended = jnp.dot(mixed_tokens, out_weight, preferred_element_type=jnp.float32)
    hidden_one = input_rows + attended
    normed_two, norm_two_pull = jax.vjp(layer_norm, hidden_one, gain_two.astype(jnp.float32))
    routed_low = normed_two.astype(jnp.bfloat16)
    router_probs, router_pull = jax.vjp(
        router, routed_low.astype(jnp.float32), router_weight.astype(jnp.float32)
    )
    slot_ids = slot_table(routes, priority[0], capacity)
    select = (
        slot_ids[:, :, None] == jnp.arange(slot_total, dtype=jnp.int32)[None, None, :]
    ).astype(jnp.bfloat16)
    send_rows = jnp.einsum(
        "kts,td->sd", select, routed_low, preferred_element_type=jnp.float32
    ).astype(jnp.bfloat16)
    expert_rows = lax.all_to_all(
        send_rows.reshape(blk_size, capacity, model_width),
        "blk",
        split_axis=0,
        concat_axis=0,
        tiled=True,
    ).reshape(slot_total, model_width)
    weight_in = expert_in[0]
    weight_out = expert_out[0]
    pre_act = jnp.dot(expert_rows, weight_in, preferred_element_type=jnp.float32)
    hidden_act, gelu_pull = jax.vjp(gelu_exact, pre_act)
    hidden_low = hidden_act.astype(jnp.bfloat16)
    expert_result = jnp.dot(hidden_low, weight_out, preferred_element_type=jnp.float32).astype(
        jnp.bfloat16
    )
    slot_result = lax.all_to_all(
        expert_result.reshape(blk_size, capacity, model_width),
        "blk",
        split_axis=0,
        concat_axis=0,
        tiled=True,
    ).reshape(slot_total, model_width)
    pair_result = jnp.einsum("kts,sd->ktd", select, slot_result, preferred_element_type=jnp.float32)
    route_hot = (routes[:, :, None] == jnp.arange(blk_size, dtype=jnp.int32)[None, None, :]).astype(
        jnp.float32
    )
    gate_vals = jnp.sum(router_probs[:, None, :] * route_hot, axis=2)
    mixture = gate_vals[:, 0, None] * pair_result[0] + gate_vals[:, 1, None] * pair_result[1]
    output = (hidden_one + mixture).astype(jnp.bfloat16)
    d_gates = jnp.transpose(jnp.sum(d_out[None] * pair_result, axis=2))
    d_probs = jnp.sum(d_gates[:, :, None] * route_hot, axis=1)
    pair_grads = (jnp.transpose(gate_vals)[:, :, None] * d_out[None]).astype(jnp.bfloat16)
    slot_grads = jnp.einsum(
        "kts,ktd->sd", select, pair_grads, preferred_element_type=jnp.float32
    ).astype(jnp.bfloat16)
    result_grads = lax.all_to_all(
        slot_grads.reshape(blk_size, capacity, model_width),
        "blk",
        split_axis=0,
        concat_axis=0,
        tiled=True,
    ).reshape(slot_total, model_width)
    d_hidden_act = jnp.dot(result_grads, weight_out.T, preferred_element_type=jnp.float32)
    d_weight_out = jnp.dot(hidden_low.T, result_grads, preferred_element_type=jnp.float32)
    d_preact = gelu_pull(d_hidden_act)[0].astype(jnp.bfloat16)
    d_weight_in = jnp.dot(expert_rows.T, d_preact, preferred_element_type=jnp.float32)
    row_grads = jnp.dot(d_preact, weight_in.T, preferred_element_type=jnp.float32).astype(
        jnp.bfloat16
    )
    slot_back = lax.all_to_all(
        row_grads.reshape(blk_size, capacity, model_width),
        "blk",
        split_axis=0,
        concat_axis=0,
        tiled=True,
    ).reshape(slot_total, model_width)
    d_routed = jnp.einsum("kts,sd->td", select, slot_back, preferred_element_type=jnp.float32)
    d_routed_router, d_router = router_pull(d_probs)
    d_hidden_norm, d_gain_two = norm_two_pull(d_routed + d_routed_router)
    d_hidden_one = d_out + d_hidden_norm
    attn_grads = d_hidden_one.astype(jnp.bfloat16)
    d_out_weight = jnp.dot(mixed_tokens.T, attn_grads, preferred_element_type=jnp.float32)
    mixed_grads = jnp.dot(attn_grads, out_weight.T, preferred_element_type=jnp.float32).astype(
        jnp.bfloat16
    )
    head_grads = lax.all_to_all(mixed_grads, "head", split_axis=1, concat_axis=0, tiled=True)
    out_grads = head_grads.reshape(span_rows, head_count, HS)
    row_delta = jnp.transpose(jnp.sum(out_grads.astype(jnp.float32) * mixed_full, axis=2))
    key_back, value_back = (
        lax.all_gather(key_heads, "blk", axis=0, tiled=True),
        lax.all_gather(value_heads, "blk", axis=0, tiled=True),
    )

    def grad_step(block_index, loop_state):
        first_key, key_rows, value_rows, same_doc, is_live = block_parts(
            block_index, key_back, value_back
        )

        def grad_update(current):
            query_grad, key_grad, value_grad = current
            scores = block_scores(key_rows, same_doc)
            weights = jnp.where(same_doc[None], jnp.exp(scores - log_total[:, :, None]), 0.0)
            value_part = jnp.einsum(
                "hqk,qhd->khd",
                weights.astype(jnp.bfloat16),
                out_grads,
                preferred_element_type=jnp.float32,
            )
            weight_grads = jnp.einsum(
                "qhd,khd->hqk", out_grads, value_rows, preferred_element_type=jnp.float32
            )
            score_grads = (weights * (weight_grads - row_delta[:, :, None])).astype(jnp.bfloat16)
            query_grad = (
                query_grad
                + jnp.einsum(
                    "hqk,khd->qhd", score_grads, key_rows, preferred_element_type=jnp.float32
                )
                * scale_factor
            )
            key_part = (
                jnp.einsum("hqk,qhd->khd", score_grads, queries, preferred_element_type=jnp.float32)
                * scale_factor
            )
            key_grad = lax.dynamic_update_slice_in_dim(
                key_grad, key_part.reshape(KEY_BLOCK, head_count * HS), first_key, 0
            )
            value_grad = lax.dynamic_update_slice_in_dim(
                value_grad, value_part.reshape(KEY_BLOCK, head_count * HS), first_key, 0
            )
            return (query_grad, key_grad, value_grad)

        return lax.cond(is_live, grad_update, keep_state, loop_state)

    start_grads = (
        jnp.zeros((span_rows, head_count, HS), jnp.float32),
        jnp.zeros((total_rows, head_count * HS), jnp.float32),
        jnp.zeros((total_rows, head_count * HS), jnp.float32),
    )
    query_grad, key_grad, value_grad = lax.fori_loop(0, block_count, grad_step, start_grads)
    key_own, value_own = (
        lax.psum_scatter(
            key_grad.astype(jnp.bfloat16), "blk", scatter_dimension=0, tiled=True
        ).astype(jnp.float32),
        lax.psum_scatter(
            value_grad.astype(jnp.bfloat16), "blk", scatter_dimension=0, tiled=True
        ).astype(jnp.float32),
    )
    query_tokens_grad, key_tokens_grad, value_tokens_grad = (
        lax.all_to_all(
            query_grad.reshape(span_rows, head_count * HS).astype(jnp.bfloat16),
            "head",
            split_axis=0,
            concat_axis=1,
            tiled=True,
        ),
        lax.all_to_all(
            key_own.astype(jnp.bfloat16), "head", split_axis=0, concat_axis=1, tiled=True
        ),
        lax.all_to_all(
            value_own.astype(jnp.bfloat16), "head", split_axis=0, concat_axis=1, tiled=True
        ),
    )
    qkv_grads = jnp.concatenate([query_tokens_grad, key_tokens_grad, value_tokens_grad], axis=1)
    d_qkv_weight = jnp.dot(normed_low.T, qkv_grads, preferred_element_type=jnp.float32)
    normed_grads = jnp.dot(qkv_grads, qkv_weight.T, preferred_element_type=jnp.float32)
    d_inputs_norm, d_gain_one = norm_one_pull(normed_grads)
    d_inputs = d_hidden_one + d_inputs_norm
    gain_one_sum, qkv_sum, out_sum, gain_two_sum, router_sum = (
        lax.psum_scatter(
            d_gain_one.astype(jnp.bfloat16), "blk", scatter_dimension=0, tiled=True
        ).astype(jnp.float32),
        lax.psum_scatter(
            d_qkv_weight.astype(jnp.bfloat16), "blk", scatter_dimension=0, tiled=True
        ).astype(jnp.float32),
        lax.psum_scatter(
            d_out_weight.astype(jnp.bfloat16), "blk", scatter_dimension=0, tiled=True
        ).astype(jnp.float32),
        lax.psum_scatter(
            d_gain_two.astype(jnp.bfloat16), "blk", scatter_dimension=0, tiled=True
        ).astype(jnp.float32),
        lax.psum_scatter(
            d_router.astype(jnp.bfloat16), "blk", scatter_dimension=0, tiled=True
        ).astype(jnp.float32),
    )
    gain_one_all, qkv_all, out_all, gain_two_all, router_all, expert_in_all, expert_out_all = (
        lax.psum(gain_one_sum.astype(jnp.bfloat16), "head").astype(jnp.float32),
        lax.psum(qkv_sum.astype(jnp.bfloat16), "head").astype(jnp.float32),
        lax.psum(out_sum.astype(jnp.bfloat16), "head").astype(jnp.float32),
        lax.psum(gain_two_sum.astype(jnp.bfloat16), "head").astype(jnp.float32),
        lax.psum(router_sum.astype(jnp.bfloat16), "head").astype(jnp.float32),
        lax.psum(d_weight_in[None].astype(jnp.bfloat16), "head").astype(jnp.float32),
        lax.psum(d_weight_out[None].astype(jnp.bfloat16), "head").astype(jnp.float32),
    )
    return (
        output,
        d_inputs,
        gain_one_all,
        qkv_all,
        out_all,
        gain_two_all,
        router_all,
        expert_in_all,
        expert_out_all,
    )


MESH = pl.DeviceIdType.MESH
LANES = 128
HALF = LANES // 2
MIB = 2**20
F32 = jnp.float32
BF16 = jnp.bfloat16


def dot(left, right, dims=(1, 0)):
    return lax.dot_general(
        left, right, (((dims[0],), (dims[1],)), ((), ())), preferred_element_type=F32
    )


def remote(src, dst, send_sem, recv_sem, head, blk):
    return pltpu.make_async_remote_copy(
        src_ref=src,
        dst_ref=dst,
        send_sem=send_sem,
        recv_sem=recv_sem,
        device_id={"head": head, "blk": blk},
        device_id_type=MESH,
    )


def arrived(ref, sem):
    pltpu.make_async_copy(ref, ref, sem).wait()


def greet(peers):
    barrier = pltpu.get_barrier_semaphore()
    for head, blk in peers:
        pl.semaphore_signal(
            barrier, inc=1, device_id={"head": head, "blk": blk}, device_id_type=MESH
        )
    return len(peers)


def meet(count):
    pl.semaphore_wait(pltpu.get_barrier_semaphore(), count)


def halves(values, lanes_kept):
    rows = values.shape[0] // 2
    moved = pltpu.roll(values[rows:], HALF, 1)
    return jnp.where(lanes_kept, values[:rows], moved)


def lane_ids(shape):
    return lax.broadcasted_iota(jnp.int32, shape, len(shape) - 1)


def centre(values):
    average = jnp.mean(values, axis=-1, keepdims=True)
    centred = values - average
    spread = jnp.mean(centred * centred, axis=-1, keepdims=True)
    scale = lax.rsqrt(spread + EPSILON)
    return centred * scale, scale


def centre_back(grad, xhat, scale):
    middle = jnp.mean(grad, axis=-1, keepdims=True)
    along = jnp.mean(grad * xhat, axis=-1, keepdims=True)
    return (grad - middle - xhat * along) * scale


def split_high_low(column, lanes):
    high = column.astype(BF16)
    low = (column - high.astype(F32)).astype(BF16)
    return jnp.where(lanes < HALF, high.astype(F32), low.astype(F32)).astype(BF16)


def join_high_low(matrix, start):
    return matrix[:, start : start + 1].astype(F32) + matrix[
        :, start + HALF : start + HALF + 1
    ].astype(F32)


def place():
    head, blk = lax.axis_index("head"), lax.axis_index("blk")
    return head, blk, blk // 2, lax.rem(blk, 2)


def around(index, step, size):
    return lax.rem(index + step, size)


QUERY_TILE = 256
CHAINS = 2


def masked_queries(q_ref, tile, key_lanes, query_tile):
    tiles_per_span = q_ref.shape[1] // query_tile
    inner = tile % tiles_per_span * query_tile
    query = q_ref[tile // tiles_per_span, inner : inner + query_tile, :]
    return jnp.where(key_lanes, query, jnp.zeros_like(query))


def group_blocks(bounds_ref, group, size, key_tile):
    first, last = group * size, (group + 1) * size
    low = jnp.min(bounds_ref[0:1, first : first + LANES])
    high = jnp.max(bounds_ref[1:2, last - LANES : last])
    return low // key_tile, (high + key_tile - 1) // key_tile


def inside_document(bounds_ref, tile, first, shape):
    key = first + lax.broadcasted_iota(jnp.int32, shape, 0)
    columns = slice(tile * shape[1], (tile + 1) * shape[1])
    return jnp.logical_and(key >= bounds_ref[0:1, columns], key < bounds_ref[1:2, columns])


def query_group(q_ref, group, y):
    key_lanes = (lane_ids((QUERY_TILE, LANES)) < HALF) == (y == 0)
    tiles = range(group * CHAINS, (group + 1) * CHAINS)
    return tiles, [masked_queries(q_ref, tile, key_lanes, QUERY_TILE) for tile in tiles]


def attend(bounds_ref, tiles, first, keys, keys_across, queries, carry):
    scores = [dot(keys, query, (1, 1)) for query in queries]
    made = []
    for tile, score, (biggest, weight, mixed) in zip(tiles, scores, carry):
        inside = inside_document(bounds_ref, tile, first, score.shape)
        score = jnp.where(inside, score, MASKED)
        bigger = jnp.maximum(biggest, jnp.max(score, axis=0, keepdims=True))
        fade = jnp.exp(biggest - bigger)
        terms = jnp.exp(score - bigger)
        weight = weight * fade + jnp.sum(terms, axis=0, keepdims=True)
        made.append((bigger, weight, mixed * fade + dot(keys_across, terms.astype(BF16))))
    return tuple(made)


def nothing_attended():
    return (
        jnp.full((1, QUERY_TILE), MASKED, F32),
        jnp.zeros((1, QUERY_TILE), F32),
        jnp.zeros((LANES, QUERY_TILE), F32),
    )


def attend_back(bounds_ref, tiles, first, keys, keys_across, group, carry):
    queries, out_grads, deltas, log_totals = group
    scores = [dot(keys, query, (1, 1)) for query in queries]
    weight_grads = [dot(keys, out_grad, (1, 1)) for out_grad in out_grads]
    pieces, score_grads = [], []
    for i, tile in enumerate(tiles):
        inside = inside_document(bounds_ref, tile, first, scores[i].shape)
        weights = jnp.exp(jnp.where(inside, scores[i], MASKED) - log_totals[i])
        score_grads.append((weights * (weight_grads[i] - deltas[i])).astype(BF16))
        pieces.append(weights.astype(BF16))
    wide = jnp.concatenate(score_grads + pieces, axis=1)
    given = dot(wide, jnp.concatenate(queries + out_grads, axis=0))
    return given, tuple(c + dot(keys_across, g) for c, g in zip(carry, score_grads))


def group_grads(do_ref, tiles, y):
    key_lanes = (lane_ids((QUERY_TILE, LANES)) < HALF) == (y == 0)
    out_grads = []
    for tile in tiles:
        parts = []
        for part in range(QUERY_TILE // LANES):
            packed = do_ref[tile, part].astype(F32)
            parts += [packed, pltpu.roll(packed, HALF, 1)]
        out_grads.append(jnp.where(key_lanes, 0.0, jnp.concatenate(parts, axis=0)).astype(BF16))
    return out_grads


def qkv_kernel(
    heads, blks,
    x_hbm, w_hbm, g1_hbm, wo_hbm, wr_hbm, g2_hbm, docs_hbm,
    qall, kvall, xall, wall, wo_all, kvt, bounds, begun,
    x_ref, w_ref, rows_in, g1_ref, g2_ref, wr_ref, docs_ref, wo_own, kv_other, q_packed, q_landed, in_sem,
    x_send, x_recv, w_send, w_recv, o_send, o_recv, p_send, p_recv,
    k_send, k_recv, q_recv,
):
    head, blk, z, y = place()
    planes = blks // 2
    model = x_ref.shape[1]
    rows = w_ref.shape[0]
    part = rows // heads
    experts = wr_ref.shape[0]
    wanted = (
        (w_hbm, w_ref), (g1_hbm, g1_ref), (g2_hbm, g2_ref), (wr_hbm, wr_ref), (x_hbm, x_ref),
        (wo_hbm, wo_own.at[:, pl.ds(0, model)]), (docs_hbm, docs_ref),
    )
    fetched = [
        pltpu.make_async_copy(src, dst, in_sem.at[i]) for i, (src, dst) in enumerate(wanted)
    ]
    for copy in fetched:
        copy.start()
    rows_in[...] = jnp.zeros_like(rows_in)
    met = greet(
        [(around(head, k, heads), blk) for k in range(1, heads)]
        + [(head, around(blk, k, blks)) for k in range(1, blks)]
    )
    lanes = lane_ids((rows, LANES))
    for copy in fetched:
        copy.wait()
    rows_in[0:experts, 0:rows] = wr_ref[...].astype(F32)
    rows_in[experts : experts + 1, 0:rows] = g2_ref[...].astype(F32)
    rows_in[experts + 1 : experts + 2, 0:rows] = g1_ref[...].astype(F32)
    vectors = jnp.transpose(rows_in[...])[:rows]
    gain = vectors[:, experts + 1 : experts + 2]

    def columns(which):
        start = pl.multiple_of(which * model + head * LANES, LANES)
        return w_ref[:, pl.ds(start, LANES)].astype(F32) * gain

    key_cols = columns(1)
    value_cols = pltpu.roll(columns(2), HALF, 1)
    wall[blk, :, 0:LANES] = jnp.where(lanes < HALF, key_cols, value_cols).astype(BF16)
    wall[blk, :, LANES : 2 * LANES] = jnp.where(lanes < HALF, value_cols, key_cols).astype(BF16)
    wall[blk, :, 2 * LANES : 3 * LANES] = (columns(0) * HS ** (-0.5)).astype(BF16)
    def slice_copy(slot, source, target):
        ref = wall.at[source]
        return remote(ref, ref, w_send.at[slot], w_recv.at[source], head, target)

    pair = 2 * z + around(y, 1, 2)
    line = [2 * around(z, step, planes) + y for step in (1, planes - 1, *range(2, planes - 1))]
    w_copies = [slice_copy(slot, blk, target) for slot, target in enumerate((*line, pair))]
    w_onward = [slice_copy(planes + slot, source, pair) for slot, source in enumerate(line)]
    xhat, _ = centre(x_ref[...].astype(F32))
    xall[head] = xhat.astype(BF16)
    meet(met)
    for copy in w_copies:
        copy.start()
    x_copies = [
        remote(xall.at[head], xall.at[head], x_send.at[k], x_recv.at[k], around(head, k, heads), blk)
        for k in range(1, heads)
    ]
    for copy in x_copies:
        copy.start()
    wo_own[:, model : model + LANES] = vectors.astype(BF16)
    wo_all[blk, head] = wo_own[pl.ds(pl.multiple_of(head * part, part), part), :]
    o_copies = [
        remote(
            wo_all.at[blk, head], wo_all.at[blk, head],
            o_send.at[k], o_recv.at[k], head, around(blk, k, blks),
        )
        for k in range(1, blks)
    ]
    document_bounds(docs_ref, bounds, z)
    for source, copy in zip(line, w_onward):
        arrived(wall.at[source], w_recv.at[source])
        copy.start()
    for copy in o_copies:
        copy.start()
    for source in (pair, *[other - y + around(y, 1, 2) for other in line]):
        arrived(wall.at[source], w_recv.at[source])
    for copy in w_copies + w_onward:
        copy.wait_send()
    for copy in x_copies:
        copy.wait()
    weight = wall[...].reshape(model, 3 * LANES)
    tokens = x_ref.shape[0]
    even = y == 0
    above, below = z < planes - 1, z > 0
    half_span = kvall.shape[1] // 2
    sides = ((1, above, below, 0), (-1, below, above, 4))

    def half_of(ref, half):
        return ref.at[pl.ds(half * half_span, half_span)]

    def outward(slot, step, across, half):
        target = 2 * (z + step) + around(y, across, 2)
        return remote(
            half_of(kv_other if across else kvall.at[blk], half), half_of(kvall.at[blk], half),
            k_send.at[slot], k_recv.at[blk, half], head, target,
        )

    def onward(slot, step, side, half):
        from_span = 2 * (z - step) + side
        ref = half_of(kvall.at[from_span], half)
        return remote(ref, ref, k_send.at[slot], k_recv.at[from_span, half], head, 2 * (z + step) + y)

    def await_half(span, half):
        arrived(half_of(kvall.at[span], half), k_recv.at[span, half])

    def turn(span):
        size = kvall.shape[1]
        kvt[:, pl.ds(pl.multiple_of(span * size, size), size)] = jnp.transpose(kvall[span])

    for half in range(2):
        for piece in range(half * heads // 2, (half + 1) * heads // 2):
            made = dot(xall[piece], weight).astype(BF16)
            first, second = made[:, 0:LANES], made[:, LANES : 2 * LANES]
            span = slice(piece * tokens, (piece + 1) * tokens)
            kvall[blk, span, :] = jnp.where(even, first, second)
            kv_other[span, :] = jnp.where(even, second, first)
            qall[y, span, :] = made[:, 2 * LANES : 3 * LANES]
        outward(8 + half, 0, 1, half).start()
        for step, there, _, slot in sides:

            @pl.when(there)
            def _():
                outward(slot + 2 * half, step, 0, half).start()
                outward(slot + 2 * half + 1, step, 1, half).start()

    other_y = around(y, 1, 2)
    kept = (lane_ids(q_packed.shape) < HALF) == (y == 1)
    q_packed[...] = halves(qall[y].astype(F32), kept).astype(BF16)
    q_pair = remote(q_packed, q_landed, k_send.at[10], q_recv, head, 2 * z + other_y)
    q_pair.start()
    turn(blk)
    for copy in o_copies:
        copy.wait()
    core = lax.rem(head, 2)
    sibling, across = head - core + 1 - core, around(head, 2, heads)

    def quarter_copy(index, quarter, to_head):
        ref = wo_all.at[:, quarter]
        return remote(ref, ref, p_send.at[index], p_recv.at[index], to_head, blk)

    p_copies = [quarter_copy(0, head, sibling), quarter_copy(1, head, across)]
    for copy in p_copies:
        copy.start()
    p_copies.append(quarter_copy(2, across, sibling))
    for half in range(2):
        for step, there, back, slot in sides:

            @pl.when(back)
            def _():
                for side in range(2):
                    await_half(2 * (z - step) + side, half)

            @pl.when(jnp.logical_and(there, back))
            def _():
                for side in range(2):
                    onward(11 + slot + 2 * half + side, step, side, half).start()

    arrived(wo_all.at[:, across], p_recv.at[1])
    p_copies[2].start()
    for half in range(2):
        await_half(pair, half)
    turn(pair)
    q_pair.wait()
    landed = q_landed[...]
    qall[other_y, 0:half_span, :] = landed
    qall[other_y, half_span : 2 * half_span, :] = pltpu.roll(landed.astype(F32), HALF, 1).astype(BF16)
    key_tile = kvall.shape[1]
    for group in range(2 * key_tile // (CHAINS * QUERY_TILE)):
        tiles, queries = query_group(qall, group, y)
        carry = (nothing_attended(),) * CHAINS
        for side in range(2):
            first = pl.multiple_of((2 * z + side) * key_tile, key_tile)
            keys_across = kvt[:, pl.ds(first, key_tile)]
            carry = attend(bounds, tiles, first, kvall[2 * z + side], keys_across, queries, carry)
        for tile, (biggest, weight, mixed) in zip(tiles, carry):
            begun[tile, 0:LANES] = mixed
            begun[tile, LANES : LANES + 8] = jnp.broadcast_to(biggest, (8, QUERY_TILE))
            begun[tile, LANES + 8 : LANES + 16] = jnp.broadcast_to(weight, (8, QUERY_TILE))
    for step, there, back, slot in sides:

        @pl.when(back)
        def _():
            for side in range(2):
                turn(2 * (z - step) + side)

    for other in range(planes):
        for side in range(2):
            span = 2 * other + side

            @pl.when(jnp.logical_or(z - other == 2, other - z == 2))
            def _():
                for half in range(2):
                    await_half(span, half)
                turn(span)

    for index, quarter in ((0, sibling), (2, around(sibling, 2, heads))):
        arrived(wo_all.at[:, quarter], p_recv.at[index])
    for copy in p_copies:
        copy.wait_send()
    for half in range(2):
        outward(8 + half, 0, 1, half).wait_send()
        for step, there, back, slot in sides:

            @pl.when(there)
            def _():
                outward(slot + 2 * half, step, 0, half).wait_send()
                outward(slot + 2 * half + 1, step, 1, half).wait_send()

            @pl.when(jnp.logical_and(there, back))
            def _():
                for side in range(2):
                    onward(11 + slot + 2 * half + side, step, side, half).wait_send()


def document_bounds(docs_ref, bounds, z):
    count = docs_ref.shape[1]
    lengths = docs_ref[...].astype(F32)
    doc = lax.broadcasted_iota(jnp.int32, (count, count), 0)
    other = lane_ids((count, count))
    start = jnp.sum(jnp.where(other < doc, lengths, 0.0), axis=1, keepdims=True)
    end = jnp.sum(jnp.where(other <= doc, lengths, 0.0), axis=1, keepdims=True)
    queries = bounds.shape[1]
    token = (z * queries + lane_ids((count, queries))).astype(F32)
    begun = start <= token
    bounds[...] = jnp.zeros_like(bounds)
    bounds[0:1, :] = jnp.max(jnp.where(begun, start, 0.0), axis=0, keepdims=True).astype(jnp.int32)
    bounds[1:2, :] = jnp.max(jnp.where(begun, end, 0.0), axis=0, keepdims=True).astype(jnp.int32)


def vmem_specs(count):
    return [pl.BlockSpec(memory_space=pltpu.VMEM)] * count


def hbm_specs(count):
    return [pl.BlockSpec(memory_space=pltpu.HBM)] * count


def in_hbm(*arrays):
    return [pltpu.with_memory_space_constraint(array, pltpu.HBM) for array in arrays]


def dma(*shape):
    return pltpu.SemaphoreType.DMA(shape)


def call_qkv(x, w_qkv, g1, w_out, w_router, g2, doc_lengths, heads, blks):
    tokens, model = x.shape
    rows = w_qkv.shape[0]
    span = tokens * heads
    wide = model + LANES
    part = rows // heads
    return pl.pallas_call(
        functools.partial(qkv_kernel, heads, blks),
        out_shape=(
            jax.ShapeDtypeStruct((2, span, LANES), BF16),
            jax.ShapeDtypeStruct((blks, span, LANES), BF16),
            jax.ShapeDtypeStruct((heads, tokens, model), BF16),
            jax.ShapeDtypeStruct((blks, rows, 3 * LANES), BF16),
            jax.ShapeDtypeStruct((blks, heads, part, wide), BF16),
            jax.ShapeDtypeStruct((LANES, blks * span), BF16),
            jax.ShapeDtypeStruct((8, 2 * span), jnp.int32),
            jax.ShapeDtypeStruct((2 * span // QUERY_TILE, LANES + 16, QUERY_TILE), F32),
        ),
        in_specs=hbm_specs(7),
        out_specs=tuple(vmem_specs(8)),
        scratch_shapes=[
            pltpu.VMEM((tokens, model), BF16),
            pltpu.VMEM((rows, 3 * model), BF16),
            pltpu.VMEM((LANES, LANES), F32),
            pltpu.VMEM((1, rows), BF16),
            pltpu.VMEM((1, rows), BF16),
            pltpu.VMEM((w_router.shape[1], rows), BF16),
            pltpu.VMEM((1, doc_lengths.shape[0]), jnp.int32),
            pltpu.VMEM((rows, wide), BF16),
            pltpu.VMEM((span, LANES), BF16),
            pltpu.VMEM((span // 2, LANES), BF16),
            pltpu.VMEM((span // 2, LANES), BF16),
            dma(7),
            dma(heads), dma(heads), dma(blks), dma(blks), dma(blks), dma(blks), dma(heads), dma(heads),
            dma(19), dma(blks, 2), pltpu.SemaphoreType.DMA,
        ],
        compiler_params=pltpu.CompilerParams(
            collective_id=1, has_side_effects=True, vmem_limit_bytes=16 * MIB
        ),
        name="qkv",
    )(
        *in_hbm(
            x, w_qkv, g1.reshape(1, rows), w_out, w_router.T, g2.reshape(1, rows),
            doc_lengths.reshape(1, -1),
        )
    )


def other_blocks(bounds_ref, group, key_tile, z, step, carry):
    low, high = group_blocks(bounds_ref, group, CHAINS * QUERY_TILE, key_tile)
    carry = lax.fori_loop(low, 2 * z, step, carry)
    return lax.fori_loop(2 * z + 2, high, step, carry)


def forward_kernel(bounds_ref, q_ref, kv_ref, kvt_ref, begun_ref, o_out, ob_out, lse_out):
    _, _, z, y = place()
    key_tile = kv_ref.shape[1]
    value_lanes = (lane_ids((HALF, LANES)) < HALF) == (y == 1)
    for group in range(q_ref.shape[0] * q_ref.shape[1] // (CHAINS * QUERY_TILE)):
        tiles, queries = query_group(q_ref, group, y)

        def step(block, carry, queries=queries, tiles=tiles):
            first = pl.multiple_of(block * key_tile, key_tile)
            across = kvt_ref[:, pl.ds(first, key_tile)]
            return attend(bounds_ref, tiles, first, kv_ref[block], across, queries, carry)

        start = tuple(
            (begun_ref[t, LANES : LANES + 1], begun_ref[t, LANES + 8 : LANES + 9], begun_ref[t, 0:LANES])
            for t in tiles
        )
        ends = other_blocks(bounds_ref, group, key_tile, z, step, start)
        for tile, (biggest, weight, mixed) in zip(tiles, ends):
            result = jnp.transpose(mixed / weight)
            o_out[tile] = result
            for part in range(QUERY_TILE // LANES):
                block = result[part * LANES : (part + 1) * LANES]
                ob_out[tile, part] = halves(block, value_lanes).astype(BF16)
            lse_out[tile] = jnp.broadcast_to(biggest + jnp.log(weight), (8, QUERY_TILE))


def call_forward(bounds, q, kv, kvt, begun):
    blks, span, _ = kv.shape
    tiles = 2 * span // QUERY_TILE
    return pl.pallas_call(
        forward_kernel,
        out_shape=(
            jax.ShapeDtypeStruct((tiles, QUERY_TILE, LANES), F32),
            jax.ShapeDtypeStruct((tiles, QUERY_TILE // LANES, HALF, LANES), BF16),
            jax.ShapeDtypeStruct((tiles, 8, QUERY_TILE), F32),
        ),
        in_specs=vmem_specs(5),
        out_specs=tuple(vmem_specs(3)),
        compiler_params=pltpu.CompilerParams(vmem_limit_bytes=16 * MIB),
        name="attend",
    )(bounds, q, kv, kvt, begun)


def backward_kernel(
    bounds_ref, q_ref, kv_ref, kvt_ref, do_ref, o_ref, lse_ref, dq_out, dkv_out, delta_out, dkv
):
    _, _, z, y = place()
    key_tile = kv_ref.shape[1]
    dkv[...] = jnp.zeros_like(dkv)
    for group in range(q_ref.shape[0] * q_ref.shape[1] // (CHAINS * QUERY_TILE)):
        tiles, queries = query_group(q_ref, group, y)
        out_grads = group_grads(do_ref, tiles, y)
        deltas, log_totals = [], []
        for tile, out_grad in zip(tiles, out_grads):
            product = jnp.transpose(out_grad.astype(F32) * o_ref[tile])
            deltas.append(jnp.sum(product, axis=0, keepdims=True))
            delta_out[tile] = jnp.broadcast_to(deltas[-1], delta_out.shape[1:])
            log_totals.append(lse_ref[tile, 0:1, :])
        known = (queries, out_grads, deltas, log_totals)

        def step(block, carry, tiles=tiles, known=known):
            first = pl.multiple_of(block * key_tile, key_tile)
            across = kvt_ref[:, pl.ds(first, key_tile)]
            given, carry = attend_back(bounds_ref, tiles, first, kv_ref[block], across, known, carry)
            dkv[block] += given
            return carry

        zero = jnp.zeros((LANES, QUERY_TILE), F32)
        ends = other_blocks(bounds_ref, group, key_tile, z, step, (zero,) * CHAINS)
        for tile, mixed in zip(tiles, ends):
            dq_out[tile] = mixed
    for block in range(dkv.shape[0]):
        dkv_out[block] = dkv[block].astype(BF16)


def call_backward(bounds, q, kv, kvt, d_o, o, lse):
    blks, span, _ = kv.shape
    tiles = 2 * span // QUERY_TILE
    return pl.pallas_call(
        backward_kernel,
        out_shape=(
            jax.ShapeDtypeStruct((tiles, LANES, QUERY_TILE), F32),
            jax.ShapeDtypeStruct((blks, span, LANES), BF16),
            jax.ShapeDtypeStruct((tiles, 8, QUERY_TILE), F32),
        ),
        in_specs=vmem_specs(7),
        out_specs=tuple(vmem_specs(3)),
        scratch_shapes=[pltpu.VMEM((blks, span, LANES), F32)],
        compiler_params=pltpu.CompilerParams(vmem_limit_bytes=16 * MIB),
        name="attend_back",
    )(bounds, q, kv, kvt, d_o, o, lse)


def gelu_parts(values):
    share = 0.5 * (1.0 + lax.erf(values * (2.0**-0.5)))
    slope = share + values * jnp.exp(-0.5 * values * values) * (2.0 * math.pi) ** -0.5
    return values * share, slope


def positions(expert_rows, expert_cols, rank_row, rank_col):
    def count(mask, axis):
        return jnp.sum(mask.astype(F32), axis=axis, keepdims=True)

    row = [None, None]
    col = [None, None]
    before = rank_col < rank_row
    after = rank_row < rank_col
    for choice in range(2):
        row[choice] = count((expert_cols[choice] == expert_rows[choice]) & before, 0)
        col[choice] = count((expert_rows[choice] == expert_cols[choice]) & after, 1)
    row[1] = row[1] + count(expert_cols[0] == expert_rows[1], 0)
    col[1] = col[1] + count(expert_rows[0] == expert_cols[1], 1)
    return row, col


def own_columns(rows_ref, turned, blk, capacity):
    blks, _, slots = rows_ref.shape
    rows = jnp.concatenate(
        [rows_ref[...].reshape(blks, slots), jnp.zeros((LANES - blks, slots), F32)], axis=0
    )
    for piece in range(slots // LANES):
        columns = slice(piece * LANES, (piece + 1) * LANES)
        turned[columns, :] = jnp.transpose(rows[:, columns])
    own = turned[pl.ds(pl.multiple_of(blk * capacity, capacity), capacity), :]
    return jnp.concatenate([own[:, source : source + 1] for source in range(blks)], axis=0)


def middle_kernel(
    heads, blks,
    x_hbm, o_ref, wo_ref, routes_hbm, rank_hbm, d_out_hbm, win_hbm, wout_hbm,
    po, hidden_ref, share_ref, dh_ref, dma_all, grads_ref, rx,
    x_ref, routes_ref, rank_ref, d_out_ref, win_ref, wout_ref, rows_in, in_sem,
    o_all, dos, doa, rs, ra, dr, da, dms, mix, gate_rows, d_gate_rows, turned,
    o_send, o_recv, dos_send, dos_recv, r_send, r_recv,
    dr_send, dr_recv, dm_send, dm_recv, rx_send, rx_recv, g_send, g_recv, dg_send, dg_recv,
):
    head, blk, z, y = place()
    tokens, model = x_ref.shape
    capacity = 2 * tokens // blks
    slots = capacity * blks
    plane = [(k % heads, k // heads) for k in range(1, 2 * heads)]
    wanted = (
        (routes_hbm, routes_ref), (rank_hbm, rank_ref), (d_out_hbm, d_out_ref), (x_hbm, x_ref),
        (win_hbm, win_ref), (wout_hbm, wout_ref),
    )
    fetched = [
        pltpu.make_async_copy(src, dst, in_sem.at[i]) for i, (src, dst) in enumerate(wanted)
    ]
    for copy in fetched:
        copy.start()
    met = greet(
        [(around(head, kh, heads), 2 * z + around(y, ky, 2)) for kh, ky in plane]
        + [(head, around(blk, k, blks)) for k in range(1, blks)]
    )
    meet(met)

    def plane_copies(src_of, dst, send, recv):
        copies = []
        for k, (kh, ky) in enumerate(plane):
            to_head, to_y = around(head, kh, heads), around(y, ky, 2)
            copies.append(
                remote(src_of(to_y, to_head), dst, send.at[k], recv.at[k], to_head, 2 * z + to_y)
            )
        return copies

    def blk_copies(src, dst, send, recv):
        return [
            remote(
                src.at[around(blk, k, blks)], dst.at[blk],
                send.at[k], recv.at[k], head, around(blk, k, blks),
            )
            for k in range(1, blks)
        ]

    def start(copies):
        for copy in copies:
            copy.start()

    def finish(copies):
        for copy in copies:
            copy.wait()

    o_copies = plane_copies(lambda to_y, to_head: o_ref.at[to_y, to_head], o_all.at[y, head], o_send, o_recv)
    start(o_copies)
    o_all[y, head] = o_ref[y, head]

    lanes = lane_ids((tokens, LANES))
    for copy in fetched[:4]:
        copy.wait()
    e_rows = [routes_ref[i : i + 1, :].astype(F32) for i in range(2)]
    rank_row = rank_ref[...].astype(F32)
    rows_in[...] = jnp.zeros_like(rows_in)
    rows_in[0:1, :], rows_in[1:2, :], rows_in[2:3, :] = *e_rows, rank_row
    columns = jnp.transpose(rows_in[...])
    e_cols = [columns[:, 0:1], columns[:, 1:2]]
    rank_col = columns[:, 2:3]
    pos_rows, pos_cols = positions(e_rows, e_cols, rank_row, rank_col)

    def slot_of(expert, position):
        return jnp.where(position < capacity, expert * capacity + position, -1.0).astype(jnp.int32)

    slot_rows = [slot_of(e, p) for e, p in zip(e_rows, pos_rows)]
    slot_cols = [slot_of(e, p) for e, p in zip(e_cols, pos_cols)]
    slot_down = lax.broadcasted_iota(jnp.int32, (slots, tokens), 0)
    slot_across = lane_ids((tokens, slots))
    pick = [(slot_down == s).astype(BF16) for s in slot_rows]
    put = [(slot_across == s).astype(BF16) for s in slot_cols]
    pick_any = pick[0] + pick[1]
    put_any = put[0] + put[1]

    d_out = d_out_ref[...]
    dos[...] = dot(pick_any, d_out.astype(BF16)).astype(BF16).reshape(dos.shape)
    dos_copies = blk_copies(dos, doa, dos_send, dos_recv)
    start(dos_copies)
    doa[blk] = dos[blk]

    weight_out = jnp.concatenate(
        [wo_ref[(b ^ 1) * HALF : ((b ^ 1) + 1) * HALF, 0:model] for b in range(blks)], axis=0
    )
    small = wo_ref[:, model : model + LANES]
    small_across = jnp.concatenate(
        [
            jnp.transpose(small[i * LANES : (i + 1) * LANES].astype(F32))
            for i in range(model // LANES)
        ],
        axis=1,
    )
    gain = small_across[blks : blks + 1, :]

    finish(o_copies)
    low_lanes = lanes[:HALF] < HALF
    for piece in range(heads):
        columns = slice(piece * LANES, (piece + 1) * LANES)
        first, second = o_all[1, piece].astype(F32), o_all[0, piece].astype(F32)
        mix[:HALF, columns] = jnp.where(low_lanes, first, second).astype(BF16)
        swapped = pltpu.roll(jnp.where(low_lanes, second, first), HALF, 1)
        mix[HALF:, columns] = swapped.astype(BF16)
    mixed = mix[...]
    hidden = x_ref[...].astype(F32) + dot(mixed, weight_out)
    xhat, scale = centre(hidden)
    routed = (xhat * gain).astype(BF16)
    rs[...] = dot(pick_any, routed).astype(BF16).reshape(rs.shape)
    r_copies = blk_copies(rs, ra, r_send, r_recv)
    start(r_copies)
    ra[blk] = rs[blk]
    logits = jnp.where(lanes < blks, dot(routed, small), MASKED)
    powers = jnp.exp(logits - jnp.max(logits, axis=1, keepdims=True))
    probs = powers / jnp.sum(powers, axis=1, keepdims=True)
    lanes_f = lanes.astype(F32)
    hots = [lanes_f == e for e in e_cols]
    gates = [jnp.sum(jnp.where(hot, probs, 0.0), axis=1, keepdims=True) for hot in hots]
    gate_high = [g.astype(BF16).astype(F32) for g in gates]
    gate_across = jnp.transpose(
        jnp.where(lanes == 0, gate_high[0], jnp.where(lanes == 1, gates[0] - gate_high[0], 0.0))
        + jnp.where(lanes == 2, gate_high[1], jnp.where(lanes == 3, gates[1] - gate_high[1], 0.0))
    ).astype(BF16)
    by_slot = (dot(gate_across, put[0]), dot(gate_across, put[1]))
    gate_rows[blk] = by_slot[0][0:1] + by_slot[0][1:2] + by_slot[1][2:3] + by_slot[1][3:4]
    g_copies = [
        remote(
            gate_rows.at[blk], gate_rows.at[blk],
            g_send.at[k], g_recv.at[k], head, around(blk, k, blks),
        )
        for k in range(1, blks)
    ]
    start(g_copies)
    finish(dos_copies)
    finish(r_copies)

    out_rows = doa[...].reshape(slots, model)
    rx[head, :, 0:model] = ra[...].reshape(slots, model)
    finish(g_copies)
    gate_col = own_columns(gate_rows, turned, blk, capacity)
    rx[head, :, model : 2 * model] = (out_rows.astype(F32) * gate_col).astype(BF16)
    core = lax.rem(head, 2)
    sibling, across = head - core + 1 - core, around(head, 2, heads)

    def half_rows(source, half):
        return rx.at[source, pl.ds(half * slots // 2, slots // 2)]

    to_across = [
        remote(
            half_rows(head, half), half_rows(head, half),
            rx_send.at[1 + half], rx_recv.at[1 + half], across, blk,
        )
        for half in range(2)
    ]
    to_sibling = remote(rx.at[head], rx.at[head], rx_send.at[0], rx_recv.at[0], sibling, blk)
    forwards = [
        remote(
            half_rows(across, half), half_rows(across, half),
            rx_send.at[3 + half], rx_recv.at[3 + half], sibling, blk,
        )
        for half in range(2)
    ]
    start(to_across)
    to_sibling.start()
    for copy in fetched[4:]:
        copy.wait()
    act, slope = gelu_parts(dot(rx[head, :, 0:model], win_ref[...]))
    d_act = dot(rx[head, :, model : 2 * model], wout_ref[...], (1, 1))
    row_grads = dot((slope * d_act).astype(BF16), win_ref[...], (1, 1))
    dr[...] = row_grads.astype(BF16).reshape(dr.shape)
    dr_copies = blk_copies(dr, da, dr_send, dr_recv)
    start(dr_copies)
    result = dot(act.astype(BF16), wout_ref[...]).astype(BF16)
    d_gate = jnp.sum(out_rows.astype(F32) * result.astype(F32), axis=1, keepdims=True)
    da[blk] = dr[blk]
    d_wide = jnp.broadcast_to(d_gate, (slots, LANES))
    d_gate_rows[blk] = jnp.concatenate(
        [jnp.transpose(d_wide[i * LANES : (i + 1) * LANES])[0:1] for i in range(slots // LANES)],
        axis=1,
    )
    dg_copies = [
        remote(
            d_gate_rows.at[blk], d_gate_rows.at[blk],
            dg_send.at[k], dg_recv.at[k], head, around(blk, k, blks),
        )
        for k in range(1, blks)
    ]
    start(dg_copies)
    po[...] = result.reshape(blks, capacity, model)

    finish(dg_copies)
    back_gate = own_columns(d_gate_rows, turned, blk, capacity)
    back_gate = split_high_low(back_gate, lane_ids((slots, LANES)))
    d_gates = [join_high_low(dot(p, back_gate), 0) for p in put]
    d_probs = jnp.where(hots[0], d_gates[0], 0.0) + jnp.where(hots[1], d_gates[1], 0.0)
    d_logits = probs * (d_probs - jnp.sum(probs * d_probs, axis=1, keepdims=True))
    d_high = d_logits.astype(BF16)
    d_low = (d_logits - d_high.astype(F32)).astype(BF16)
    d_router_part = dot(d_high, small, (1, 1)) + dot(d_low, small, (1, 1))
    finish(dr_copies)
    d_routed = dot(put_any, da[...].reshape(slots, model)) + d_router_part
    d_hidden = d_out + centre_back(d_routed * gain, xhat, scale)
    dh_ref[...] = d_hidden
    d_attn = d_hidden.astype(BF16)
    d_mixed = dot(d_attn, weight_out, (1, 1))
    for piece in range(heads):
        block = d_mixed[:, piece * LANES : (piece + 1) * LANES]
        for to_y in range(2):
            dms[to_y, piece] = halves(block, low_lanes == (to_y == 1)).astype(BF16)
    dm_copies = plane_copies(lambda to_y, to_head: dms.at[to_y, to_head], dma_all.at[y, head], dm_send, dm_recv)
    start(dm_copies)
    dma_all[y, head] = dms[y, head]
    arrived(half_rows(across, 0), rx_recv.at[1])
    forwards[0].start()

    d_weight = dot(mixed, d_attn, (0, 0)).astype(BF16)
    for b in range(blks):
        grads_ref[b, :, 0:model] = d_weight[(b ^ 1) * HALF : ((b ^ 1) + 1) * HALF, :]
    last = (lanes == blks).astype(BF16)
    d_small = dot(routed, d_high, (0, 0)) + dot((d_routed * xhat).astype(BF16), last, (0, 0))
    grads_ref[:, :, model : model + LANES] = d_small.astype(BF16).reshape(blks, HALF, LANES)
    share = gates[0] * put[0].astype(F32) + gates[1] * put[1].astype(F32)
    share_ref[0] = share.astype(BF16)
    share_ref[1] = (share - share_ref[0].astype(F32)).astype(BF16)
    hidden_ref[...] = hidden

    arrived(half_rows(across, 1), rx_recv.at[2])
    forwards[1].start()
    finish(dm_copies)
    to_sibling.wait()
    for copy in to_across:
        copy.wait_send()
    finish(forwards)


def call_middle(x, o, wo, routes, rank, d_out, win, wout, heads, blks):
    tokens, model = x.shape
    capacity = 2 * tokens // blks
    slots = capacity * blks
    wide = model + LANES

    def rows(width):
        return pltpu.VMEM((blks, capacity, width), BF16)

    def block(*lead):
        return pltpu.VMEM((*lead, tokens // 2, LANES), BF16)

    return pl.pallas_call(
        functools.partial(middle_kernel, heads, blks),
        out_shape=(
            jax.ShapeDtypeStruct((blks, capacity, model), BF16),
            jax.ShapeDtypeStruct((tokens, model), F32),
            jax.ShapeDtypeStruct((2, tokens, slots), BF16),
            jax.ShapeDtypeStruct((tokens, model), F32),
            jax.ShapeDtypeStruct((2, heads, tokens // 2, LANES), BF16),
            jax.ShapeDtypeStruct((blks, model // blks, wide), BF16),
            jax.ShapeDtypeStruct((heads, slots, 2 * model), BF16),
        ),
        in_specs=hbm_specs(1) + vmem_specs(2) + hbm_specs(5),
        out_specs=tuple(vmem_specs(7)),
        scratch_shapes=[
            pltpu.VMEM((tokens, model), BF16),
            pltpu.VMEM((2, tokens), jnp.int32),
            pltpu.VMEM((1, tokens), jnp.int32),
            pltpu.VMEM((tokens, model), F32),
            pltpu.VMEM(win.shape, BF16),
            pltpu.VMEM(wout.shape, BF16),
            pltpu.VMEM((tokens, tokens), F32),
            dma(6),
            block(2, heads), rows(model), rows(model), rows(model), rows(model),
            rows(model), rows(model), block(2, heads),
            pltpu.VMEM((tokens, model), BF16),
            pltpu.VMEM((blks, 1, slots), F32), pltpu.VMEM((blks, 1, slots), F32),
            pltpu.VMEM((slots, LANES), F32),
            dma(2 * heads), dma(2 * heads), dma(blks), dma(blks), dma(blks), dma(blks),
            dma(blks), dma(blks), dma(2 * heads), dma(2 * heads), dma(5), dma(5),
            dma(blks), dma(blks), dma(blks), dma(blks),
        ],
        compiler_params=pltpu.CompilerParams(
            collective_id=2, has_side_effects=True, vmem_limit_bytes=20 * MIB
        ),
        name="experts",
    )(*in_hbm(x), o, wo, *in_hbm(routes.T, rank, d_out, win, wout))


def last_kernel(
    heads, blks,
    x_hbm, dh_ref, begun_ref, dkv_ref, xa_ref, wa_ref, w_hbm, g1_hbm, grads_ref, rx_ref, win_hbm, wout_hbm,
    po_ref, hidden_ref, share_ref, bounds_ref, q_ref, kv_ref, kvt_ref, do_ref, lse_ref, delta_ref,
    y_ref, dx_ref, dw_ref, shared_ref, din_ref, dout_ref,
    x_ref, w_ref, g1_ref, win_ref, wout_ref, in_sem,
    gain_tile, far_all, near_send_buf, near_all, pair_all, dq_all, dq_ref, dq_packed, dkv_own, pair_buf, us, ua, gs, ga, gqs, gqa, u_part, xat, pa, gh, ghq, w1, w2s, w2, w3,
    q_send, q_recv, pair_send, pair_recv, far_send, far_recv, near_send, near_recv,
    u_send, u_recv, g_send, g_recv, gh_send, gh_recv, w1_send, w1_recv, w2_send, w2_recv,
    w3_send, w3_recv, e_send, e_recv, gq_send, gq_recv, po_send, po_recv, ghq_send, ghq_recv,
    din_half, dout_half,
):
    head, blk, z, y = place()
    planes = blks // 2
    tokens, model = x_ref.shape
    rows = w_ref.shape[0]
    wanted = (
        (win_hbm, win_ref), (wout_hbm, wout_ref), (x_hbm, x_ref), (w_hbm, w_ref), (g1_hbm, g1_ref)
    )
    fetched = [
        pltpu.make_async_copy(src, dst, in_sem.at[i]) for i, (src, dst) in enumerate(wanted)
    ]
    for copy in fetched:
        copy.start()
    met = greet(
        [(around(head, k, heads), blk) for k in range(1, heads)]
        + [(head, around(blk, k, blks)) for k in range(1, blks)]
    )
    meet(met)

    def start(copies):
        for copy in copies:
            copy.start()

    def finish(copies):
        for copy in copies:
            copy.wait()

    other_y = around(y, 1, 2)
    pair = 2 * z + other_y
    above, below = z < planes - 1, z > 0
    directions = ((1, above, below, 0), (-1, below, above, 2))

    half_span = dkv_ref.shape[1] // 2

    def half_of(ref, half):
        return ref.at[pl.ds(half * half_span, half_span)]

    def far_copy(step, slot, side, half):
        span = 2 * (z + 2 * step) + side
        return remote(
            half_of(dkv_ref.at[span], half), half_of(far_all.at[slot + side], half),
            far_send.at[slot + side, half], far_recv.at[slot + side, half], head, 2 * (z + step) + y,
        )

    def near_copy(step, slot, side, half):
        return remote(
            half_of(near_send_buf.at[slot + side], half), half_of(near_all.at[slot // 2, y], half),
            near_send.at[slot + side, half], near_recv.at[slot // 2, y, half],
            head, 2 * (z + step) + side,
        )

    def two_away(step):
        return z + 2 * step < planes if step > 0 else z + 2 * step >= 0

    for half in range(2):
        for step, there, back, slot in directions:

            @pl.when(two_away(step))
            def _():
                for side in range(2):
                    far_copy(step, slot, side, half).start()

    w1_copies = [
        remote(
            grads_ref.at[:, around(head, k, heads)], w1.at[head],
            w1_send.at[k], w1_recv.at[k], around(head, k, heads), blk,
        )
        for k in range(1, heads)
    ]
    start(w1_copies)
    w1[head] = grads_ref[:, head]

    core = lax.rem(head, 2)
    sibling = head - core + 1 - core
    ff_half = wout_ref.shape[0] // 2
    ff_step = ff_half // 4

    def expert_chunk(chunk):
        here = pl.multiple_of(core * ff_half + chunk * ff_step, ff_step)
        there = pl.multiple_of(chunk * ff_step, ff_step)
        into = win_ref[:, pl.ds(here, ff_step)]
        outof = wout_ref[pl.ds(here, ff_step), :]
        d_in = jnp.zeros((model, ff_step), F32)
        d_out = jnp.zeros((ff_step, model), F32)
        for source in range(heads):
            rows_in = rx_ref[source, :, 0:model]
            grads_out = rx_ref[source, :, model : 2 * model]
            act, slope = gelu_parts(dot(rows_in, into))
            d_act = dot(grads_out, outof, (1, 1))
            d_in = d_in + dot(rows_in, (slope * d_act).astype(BF16), (0, 0))
            d_out = d_out + dot(act.astype(BF16), grads_out, (0, 0))
        din_ref[:, pl.ds(here, ff_step)] = d_in
        dout_ref[pl.ds(here, ff_step), :] = d_out
        din_half[core, :, pl.ds(there, ff_step)] = d_in.astype(BF16)
        dout_half[core, pl.ds(there, ff_step), :] = d_out.astype(BF16)

    key_tile = kv_ref.shape[1]
    for group in range(2 * key_tile // (CHAINS * QUERY_TILE)):
        tiles, queries = query_group(q_ref, group, y)
        known = (
            queries,
            group_grads(do_ref, tiles, y),
            [delta_ref[tile, 0:1, :] for tile in tiles],
            [lse_ref[tile, 0:1, :] for tile in tiles],
        )
        carry = tuple(begun_ref[tile] for tile in tiles)
        for side in range(2):
            first = pl.multiple_of((2 * z + side) * key_tile, key_tile)
            keys_across = kvt_ref[:, pl.ds(first, key_tile)]
            given, carry = attend_back(
                bounds_ref, tiles, first, kv_ref[2 * z + side], keys_across, known, carry
            )
            dkv_own[side] = given if group == 0 else dkv_own[side] + given
        for tile, total in zip(tiles, carry):
            at = tile * QUERY_TILE % key_tile
            dq_ref[tile * QUERY_TILE // key_tile, at : at + QUERY_TILE] = jnp.transpose(total)
    pair_buf[...] = dkv_own[other_y].astype(BF16)
    pair_copy = remote(pair_buf, pair_all, pair_send, pair_recv, head, pair)
    pair_copy.start()
    own_lanes = (lane_ids(dq_packed.shape) < HALF) == (y == 0)
    dq_packed[...] = halves(dq_ref[other_y], own_lanes).astype(BF16)
    q_copy = remote(dq_packed, dq_all, q_send, q_recv, head, pair)
    q_copy.start()
    for half in range(2):
        rows_here = slice(half * half_span, (half + 1) * half_span)
        for step, there, back, slot in directions:

            @pl.when(there)
            def _():
                for side in range(2):
                    near_send_buf[slot + side, rows_here] = dkv_ref[2 * (z + step) + side, rows_here]

            @pl.when(jnp.logical_and(there, back))
            def _():
                for side in range(2):
                    arrived(half_of(far_all.at[slot + side], half), far_recv.at[slot + side, half])
                    near_send_buf[slot + side, rows_here] = (
                        near_send_buf[slot + side, rows_here].astype(F32)
                        + far_all[slot + side, rows_here].astype(F32)
                    ).astype(BF16)

            @pl.when(there)
            def _():
                for side in range(2):
                    near_copy(step, slot, side, half).start()

    finish(fetched[:2])
    weight = wa_ref[...].reshape(model, 3 * LANES)
    for piece in range(heads):
        xat[:, piece * tokens : (piece + 1) * tokens] = jnp.transpose(xa_ref[piece])
    even = y == 0


    @pl.loop(0, 2)
    def _(chunk):
        expert_chunk(chunk)

    q_copy.wait()
    landed = dq_all[...].astype(F32)
    landed = jnp.concatenate([landed, pltpu.roll(landed, HALF, 1)], axis=0)
    own_lanes = (lane_ids(landed.shape) < HALF) == even
    q_grads = jnp.where(own_lanes, dq_ref[y], landed).astype(BF16)
    gqs[...] = dot(xat[...], q_grads).astype(BF16).reshape(gqs.shape)
    gq_copies = [
        remote(
            gqs.at[around(blk, k, blks)], gqa.at[blk],
            gq_send.at[k], gq_recv.at[k], head, around(blk, k, blks),
        )
        for k in range(1, blks)
    ]
    start(gq_copies)
    gqa[blk] = gqs[blk]
    u_part[...] = dot(q_grads, weight[:, 2 * LANES : 3 * LANES], (1, 1)).reshape(u_part.shape)

    finish(w1_copies)
    summed = w1[0].astype(F32)
    for source in range(1, heads):
        summed = summed + w1[source].astype(F32)
    w2s[...] = summed.astype(BF16)
    w2_copies = [
        remote(
            w2s.at[around(blk, k, blks)], w2.at[blk],
            w2_send.at[k], w2_recv.at[k], head, around(blk, k, blks),
        )
        for k in range(1, blks)
    ]
    start(w2_copies)
    w2[blk] = w2s[blk]

    @pl.loop(2, 4)
    def _(chunk):
        expert_chunk(chunk)

    e_copies = [
        remote(din_half.at[core], din_half.at[core], e_send.at[0], e_recv.at[0], sibling, blk),
        remote(dout_half.at[core], dout_half.at[core], e_send.at[1], e_recv.at[1], sibling, blk),
    ]
    start(e_copies)

    pair_copy.wait()
    for step, there, back, slot in directions:

        @pl.when(back)
        def _():
            for side in range(2):
                for half in range(2):
                    arrived(
                        half_of(near_all.at[slot // 2, side], half),
                        near_recv.at[slot // 2, side, half],
                    )

        @pl.when(jnp.logical_not(back))
        def _():
            near_all[slot // 2] = jnp.zeros(near_all.shape[1:], BF16)

    own = dkv_own[y]
    other = pair_all[...].astype(F32)
    made = jnp.concatenate(
        [
            (
                jnp.where(even == (side == 0), own, other)
                + near_all[0, side].astype(F32)
                + near_all[1, side].astype(F32)
            ).astype(BF16)
            for side in range(2)
        ],
        axis=1,
    )
    gs[...] = dot(xat[...], made).astype(BF16).reshape(gs.shape)
    g_copies = [
        remote(
            gs.at[around(blk, k, blks)], ga.at[blk],
            g_send.at[k], g_recv.at[k], head, around(blk, k, blks),
        )
        for k in range(1, blks)
    ]
    start(g_copies)
    ga[blk] = gs[blk]
    us[...] = (
        u_part[...] + dot(made, weight[:, 0 : 2 * LANES], (1, 1)).reshape(us.shape)
    ).astype(BF16)
    u_copies = [
        remote(
            us.at[around(head, k, heads)], ua.at[head],
            u_send.at[k], u_recv.at[k], around(head, k, heads), blk,
        )
        for k in range(1, heads)
    ]
    start(u_copies)
    ua[head] = us[head]
    finish(fetched[2:])
    finish(gq_copies)
    total = gqa[0].astype(F32)
    for source in range(1, blks):
        total = total + gqa[source].astype(F32)
    ghq[head] = total.astype(BF16)
    ghq_copies = [
        remote(ghq.at[head], ghq.at[head], ghq_send.at[k], ghq_recv.at[k], around(head, k, heads), blk)
        for k in range(1, heads)
    ]
    start(ghq_copies)

    finish(w2_copies)
    part = w2[0].astype(F32)
    for source in range(1, blks):
        part = part + w2[source].astype(F32)
    w3[head] = part.astype(BF16)
    w3_copies = [
        remote(w3.at[head], w3.at[head], w3_send.at[k], w3_recv.at[k], around(head, k, heads), blk)
        for k in range(1, heads)
    ]
    start(w3_copies)

    xhat, scale = centre(x_ref[...].astype(F32))
    finish(e_copies)
    there = pl.multiple_of((1 - core) * ff_half, ff_half)
    din_ref[:, pl.ds(there, ff_half)] = din_half[1 - core].astype(F32)
    dout_ref[pl.ds(there, ff_half), :] = dout_half[1 - core].astype(F32)
    finish(g_copies)
    total = ga[0].astype(F32)
    for source in range(1, blks):
        total = total + ga[source].astype(F32)
    gh[head] = total.astype(BF16)
    gh_copies = [
        remote(gh.at[head], gh.at[head], gh_send.at[k], gh_recv.at[k], around(head, k, heads), blk)
        for k in range(1, heads)
    ]
    start(gh_copies)
    po_copies = [
        remote(
            po_ref.at[around(blk, k, blks)], pa.at[blk],
            po_send.at[k], po_recv.at[k], head, around(blk, k, blks),
        )
        for k in range(1, blks)
    ]
    start(po_copies)
    pa[blk] = po_ref[blk]
    finish(u_copies)
    grad = ua[0].astype(F32)
    for source in range(1, heads):
        grad = grad + ua[source].astype(F32)
    dx_ref[...] = dh_ref[...] + centre_back(grad, xhat, scale)

    gain_tile[...] = jnp.zeros_like(gain_tile)
    gain_tile[0:1, 0:rows] = g1_ref[...].astype(F32)
    gain = jnp.transpose(jnp.broadcast_to(gain_tile[0:1, :], (LANES, LANES)))[:rows]
    low_half = lane_ids((rows, LANES)) < HALF
    finish(ghq_copies)
    finish(gh_copies)
    d_gain = jnp.zeros((rows, LANES), F32)
    for source in range(heads):
        both = [gh[source, :, i * LANES : (i + 1) * LANES].astype(F32) for i in range(2)]
        grads = (
            ghq[source].astype(F32) * HS ** (-0.5),
            jnp.where(low_half, both[0], both[1]),
            pltpu.roll(jnp.where(low_half, both[1], both[0]), HALF, 1),
        )
        for which, value in enumerate(grads):
            columns = slice(which * model + source * LANES, which * model + (source + 1) * LANES)
            d_gain = d_gain + value * w_ref[:, columns].astype(F32)
            dw_ref[:, columns] = value * gain
    finish(w3_copies)
    shared = w3[...].reshape(rows, w3.shape[-1]).astype(F32)
    shared_ref[:, 0:model] = shared[:, 0:model]
    gain_col = jnp.sum(d_gain, axis=1, keepdims=True)
    shared_ref[:, model : model + LANES] = jnp.where(
        lane_ids((rows, LANES)) == blks + 1, gain_col, shared[:, model : model + LANES]
    )
    finish(po_copies)
    parts = pa[...].reshape(share_ref.shape[2], model)
    mixture = dot(share_ref[0], parts) + dot(share_ref[1], parts)
    y_ref[...] = (hidden_ref[...] + mixture).astype(BF16)

    for step, there, back, slot in directions:

        @pl.when(two_away(step))
        def _():
            for side in range(2):
                for half in range(2):
                    far_copy(step, slot, side, half).wait_send()

        @pl.when(there)
        def _():
            for side in range(2):
                for half in range(2):
                    near_copy(step, slot, side, half).wait_send()


def call_last(
    x, dh, dq, dkv, xa, wa, w_qkv, g1, grads, rx, win, wout, po, hidden, share,
    bounds, q, kv, kvt, d_o, lse, delta, heads, blks,
):
    tokens, model = x.shape
    span = tokens * heads
    rows = w_qkv.shape[0]
    wide = model + LANES
    part = rows // heads
    ff = wout.shape[0]

    def block(*lead):
        return pltpu.VMEM((*lead, span, LANES), BF16)

    return pl.pallas_call(
        functools.partial(last_kernel, heads, blks),
        out_shape=(
            jax.ShapeDtypeStruct((tokens, model), BF16),
            jax.ShapeDtypeStruct((tokens, model), F32),
            jax.ShapeDtypeStruct((rows, 3 * model), F32),
            jax.ShapeDtypeStruct((rows, wide), F32),
            jax.ShapeDtypeStruct((model, ff), F32),
            jax.ShapeDtypeStruct((ff, model), F32),
        ),
        in_specs=hbm_specs(1) + vmem_specs(5) + hbm_specs(2) + vmem_specs(2) + hbm_specs(2) + vmem_specs(10),
        out_specs=tuple(vmem_specs(6)),
        scratch_shapes=[
            pltpu.VMEM((tokens, model), BF16),
            pltpu.VMEM((rows, 3 * model), BF16),
            pltpu.VMEM((1, rows), BF16),
            pltpu.VMEM(win.shape, BF16),
            pltpu.VMEM(wout.shape, BF16),
            dma(5),
            pltpu.VMEM((8, LANES), F32),
            block(4), block(4), block(2, 2), block(), pltpu.VMEM((span // 2, LANES), BF16),
            pltpu.VMEM((2, span, LANES), F32), pltpu.VMEM((span // 2, LANES), BF16),
            pltpu.VMEM((2, span, LANES), F32), block(),
            pltpu.VMEM((heads, tokens, model), BF16), pltpu.VMEM((heads, tokens, model), BF16),
            pltpu.VMEM((blks, rows, 2 * LANES), BF16), pltpu.VMEM((blks, rows, 2 * LANES), BF16),
            pltpu.VMEM((blks, rows, LANES), BF16), pltpu.VMEM((blks, rows, LANES), BF16),
            pltpu.VMEM((heads, tokens, model), F32), pltpu.VMEM((model, span), BF16),
            pltpu.VMEM(po.shape, BF16),
            pltpu.VMEM((heads, rows, 2 * LANES), BF16), pltpu.VMEM((heads, rows, LANES), BF16),
            pltpu.VMEM((heads, blks, part, wide), BF16), pltpu.VMEM((blks, part, wide), BF16),
            pltpu.VMEM((blks, part, wide), BF16), pltpu.VMEM((heads, part, wide), BF16),
            pltpu.SemaphoreType.DMA, pltpu.SemaphoreType.DMA, pltpu.SemaphoreType.DMA, pltpu.SemaphoreType.DMA,
            dma(4, 2), dma(4, 2), dma(4, 2), dma(2, 2, 2),
            dma(heads), dma(heads), dma(blks), dma(blks), dma(heads), dma(heads), dma(heads), dma(heads),
            dma(blks), dma(blks), dma(heads), dma(heads), dma(2), dma(2), dma(blks), dma(blks), dma(blks), dma(blks), dma(heads), dma(heads),
            pltpu.VMEM((2, model, ff // 2), BF16), pltpu.VMEM((2, ff // 2, model), BF16),
        ],
        compiler_params=pltpu.CompilerParams(
            collective_id=3, has_side_effects=True, vmem_limit_bytes=36 * MIB
        ),
        name="last",
    )(
        *in_hbm(x), dh, dq, dkv, xa, wa, *in_hbm(w_qkv, g1.reshape(1, rows)),
        grads.reshape(blks, heads, part, wide), rx, *in_hbm(win, wout), po, hidden, share,
        bounds, q, kv, kvt, d_o, lse, delta,
    )


def finish_kernel(
    experts,
    y_ref, dx_ref, dw_ref, shared_ref, din_ref, dout_ref,
    y_out, dx_out, g1_out, dw_out, dwo_out, g2_out, wr_out, din_out, dout_out,
    tile, wr, g2, g1, sem,
):
    rows = shared_ref.shape[0]
    model = dx_ref.shape[1]
    copies = [
        pltpu.make_async_copy(dx_ref, dx_out, sem.at[0]),
        pltpu.make_async_copy(dw_ref, dw_out, sem.at[1]),
        pltpu.make_async_copy(shared_ref.at[:, pl.ds(0, model)], dwo_out, sem.at[2]),
        pltpu.make_async_copy(y_ref, y_out, sem.at[6]),
        pltpu.make_async_copy(din_ref, din_out, sem.at[7]),
        pltpu.make_async_copy(dout_ref, dout_out, sem.at[8]),
    ]
    for copy in copies:
        copy.start()
    tile[...] = jnp.zeros_like(tile)
    tile[0:rows, :] = shared_ref[:, model : model + LANES]
    across = jnp.transpose(tile[...])[:, 0:rows]
    wr[...] = across[0:experts]
    g2[...] = across[experts : experts + 1]
    g1[...] = across[experts + 1 : experts + 2]
    for index, (src, dst) in enumerate(((wr, wr_out), (g2, g2_out), (g1, g1_out))):
        copies.append(pltpu.make_async_copy(src, dst, sem.at[3 + index]))
        copies[-1].start()
    for copy in copies:
        copy.wait()


def call_finish(output, dx, dw, shared, d_in, d_out):
    rows = shared.shape[0]
    model = dx.shape[1]
    experts = model // rows
    return pl.pallas_call(
        functools.partial(finish_kernel, experts),
        out_shape=(
            jax.ShapeDtypeStruct(output.shape, BF16),
            jax.ShapeDtypeStruct(dx.shape, F32),
            jax.ShapeDtypeStruct((1, rows), F32),
            jax.ShapeDtypeStruct(dw.shape, F32),
            jax.ShapeDtypeStruct((rows, model), F32),
            jax.ShapeDtypeStruct((1, rows), F32),
            jax.ShapeDtypeStruct((experts, rows), F32),
            jax.ShapeDtypeStruct(d_in.shape, F32),
            jax.ShapeDtypeStruct(d_out.shape, F32),
        ),
        in_specs=vmem_specs(6),
        out_specs=tuple(hbm_specs(9)),
        scratch_shapes=[
            pltpu.VMEM((LANES, LANES), F32),
            pltpu.VMEM((experts, rows), F32),
            pltpu.VMEM((1, rows), F32),
            pltpu.VMEM((1, rows), F32),
            dma(9),
        ],
        compiler_params=pltpu.CompilerParams(vmem_limit_bytes=16 * MIB),
        name="finish",
    )(output, dx, dw, shared, d_in, d_out)


def local_kernels(
    inputs, ln1_gain, w_qkv, w_out, ln2_gain, w_router,
    expert_in, expert_out, routes, priority, doc_lengths, d_out,
):
    heads, blks = lax.axis_size("head"), lax.axis_size("blk")
    model = inputs.shape[1]
    tokens = inputs.shape[0]
    win, wout = expert_in[0], expert_out[0]
    q, kv, xa, wa, wo, kvt, bounds, begun = call_qkv(
        inputs, w_qkv, ln1_gain, w_out, w_router, ln2_gain, doc_lengths, heads, blks
    )
    o, o_low, lse = call_forward(bounds, q, kv, kvt, begun)
    po, hidden, share, dh, d_o, grads, rx = call_middle(
        inputs, o_low.reshape(2, heads, tokens // 2, LANES), wo.reshape(model, model + LANES),
        routes, priority, d_out, win, wout, heads, blks,
    )
    d_o = d_o.reshape(2 * heads * tokens // QUERY_TILE, -1, HALF, LANES)
    dq, dkv, delta = call_backward(bounds, q, kv, kvt, d_o, o, lse)
    ends = call_last(
        inputs, dh, dq, dkv, xa, wa, w_qkv, ln1_gain, grads, rx, win, wout,
        po, hidden, share, bounds, q, kv, kvt, d_o, lse, delta, heads, blks,
    )
    output, d_inputs, d_gain_one, d_qkv, d_out_proj, d_gain_two, d_router, d_in, d_out_weight = call_finish(*ends)
    return (
        output,
        d_inputs,
        d_gain_one.reshape(-1),
        d_qkv,
        d_out_proj,
        d_gain_two.reshape(-1),
        d_router.T,
        d_in[None],
        d_out_weight[None],
    )


def solution(mesh):
    in_specs = (
        P(("blk", "head"), None),
        P("blk"),
        P("blk", None),
        P("blk", None),
        P("blk"),
        P("blk", None),
        P("blk", None, None),
        P("blk", None, None),
        P(("blk", "head"), None),
        P(("blk", "head"), None),
        P(),
        P(("blk", "head"), None),
    )
    out_specs = (
        P(("blk", "head"), None),
        P(("blk", "head"), None),
        P("blk"),
        P("blk", None),
        P("blk", None),
        P("blk"),
        P("blk", None),
        P("blk", None, None),
        P("blk", None, None),
    )
    fits = mesh.shape["head"] == 4 and mesh.shape["blk"] == 8
    body = local_kernels if fits else local
    return jax.shard_map(body, mesh=mesh, in_specs=in_specs, out_specs=out_specs, check_vma=False)
```

```python
import functools
import math

import jax
import jax.numpy as jnp
from jax import lax
from jax.experimental import pallas as pl
from jax.experimental.pallas import tpu as pltpu
from jax.sharding import PartitionSpec as P

HS = 64
KEY_BLOCK = 2048


PRECISE = lax.Precision.HIGHEST
MASKED = -1e30
EPSILON = 1e-06


def layer_norm(values, gain):
    average = jnp.mean(values, axis=-1, keepdims=True)
    centred = values - average
    spread = jnp.mean(centred * centred, axis=-1, keepdims=True)
    return centred * lax.rsqrt(spread + EPSILON) * gain


def gelu_exact(values):
    return jax.nn.gelu(values, approximate=False)


def router(row_block, weight):
    return jax.nn.softmax(jnp.dot(row_block, weight, precision=PRECISE), axis=-1)


def doc_index(positions, doc_lengths):
    places = jnp.arange(doc_lengths.shape[0], dtype=jnp.int32)
    starts = jnp.sum(jnp.where(places[None, :] < places[:, None], doc_lengths[None, :], 0), axis=1)
    at_most = (starts[None, :] <= positions[:, None]).astype(jnp.int32)
    return jnp.sum(at_most, axis=1) - 1


def slot_table(route_rows, ranking, capacity):
    token_count = route_rows.shape[0]
    expert = jnp.transpose(route_rows).reshape(-1)
    pair_order = (jnp.arange(2, dtype=jnp.int32)[:, None] * token_count + ranking[None, :]).reshape(
        -1
    )
    before = (expert[:, None] == expert[None, :]) & (pair_order[None, :] < pair_order[:, None])
    position = jnp.sum(before.astype(jnp.int32), axis=1)
    slot_ids = jnp.where(position < capacity, expert * capacity + position, -1)
    return slot_ids.reshape(2, token_count)


def keep_state(current):
    return current


def local(
    inputs,
    ln1_gain,
    w_qkv,
    w_out,
    ln2_gain,
    w_router,
    expert_in,
    expert_out,
    routes,
    priority,
    doc_lengths,
    d_out,
):
    blk_size = lax.axis_size("blk")
    tok_rows = inputs.shape[0]
    model_width = inputs.shape[1]
    capacity = 2 * tok_rows // blk_size
    slot_total = blk_size * capacity
    gain_one, qkv_weight, out_weight, gain_two, router_weight = (
        lax.all_gather(ln1_gain, "blk", axis=0, tiled=True),
        lax.all_gather(w_qkv, "blk", axis=0, tiled=True),
        lax.all_gather(w_out, "blk", axis=0, tiled=True),
        lax.all_gather(ln2_gain, "blk", axis=0, tiled=True),
        lax.all_gather(w_router, "blk", axis=0, tiled=True),
    )
    input_rows = inputs.astype(jnp.float32)
    normed_one, norm_one_pull = jax.vjp(layer_norm, input_rows, gain_one.astype(jnp.float32))
    normed_low = normed_one.astype(jnp.bfloat16)
    qkv_rows = jnp.dot(normed_low, qkv_weight, preferred_element_type=jnp.float32).astype(
        jnp.bfloat16
    )
    query_heads, key_heads, value_heads = (
        lax.all_to_all(qkv_rows[:, :model_width], "head", split_axis=1, concat_axis=0, tiled=True),
        lax.all_to_all(
            qkv_rows[:, model_width : 2 * model_width],
            "head",
            split_axis=1,
            concat_axis=0,
            tiled=True,
        ),
        lax.all_to_all(
            qkv_rows[:, 2 * model_width :], "head", split_axis=1, concat_axis=0, tiled=True
        ),
    )
    span_rows = query_heads.shape[0]
    head_count = query_heads.shape[1] // HS
    key_all, value_all = (
        lax.all_gather(key_heads, "blk", axis=0, tiled=True),
        lax.all_gather(value_heads, "blk", axis=0, tiled=True),
    )
    total_rows = key_all.shape[0]
    block_count = total_rows // KEY_BLOCK
    scale_factor = HS ** (-0.5)
    query_pos = lax.axis_index("blk") * span_rows + jnp.arange(span_rows, dtype=jnp.int32)
    query_docs = doc_index(query_pos, doc_lengths)
    queries = query_heads.reshape(span_rows, head_count, HS)

    def block_parts(block_index, key_source, value_source):
        first_key = block_index * KEY_BLOCK
        key_rows = lax.dynamic_slice_in_dim(key_source, first_key, KEY_BLOCK, 0).reshape(
            KEY_BLOCK, head_count, HS
        )
        value_rows = lax.dynamic_slice_in_dim(value_source, first_key, KEY_BLOCK, 0).reshape(
            KEY_BLOCK, head_count, HS
        )
        key_docs = doc_index(first_key + jnp.arange(KEY_BLOCK, dtype=jnp.int32), doc_lengths)
        is_live = (key_docs[0] <= query_docs[-1]) & (key_docs[-1] >= query_docs[0])
        same_doc = query_docs[:, None] == key_docs[None, :]
        return (first_key, key_rows, value_rows, same_doc, is_live)

    def block_scores(key_rows, same_doc):
        raw_scores = (
            jnp.einsum("qhd,khd->hqk", queries, key_rows, preferred_element_type=jnp.float32)
            * scale_factor
        )
        return jnp.where(same_doc[None], raw_scores, MASKED)

    def stat_step(block_index, loop_state):
        first_key, key_rows, value_rows, same_doc, is_live = block_parts(
            block_index, key_all, value_all
        )

        def stat_update(current):
            running_max, running_sum = current
            scores = block_scores(key_rows, same_doc)
            new_max = jnp.maximum(running_max, jnp.max(scores, axis=2))
            exp_terms = jnp.where(same_doc[None], jnp.exp(scores - new_max[:, :, None]), 0.0)
            return (
                new_max,
                running_sum * jnp.exp(running_max - new_max) + jnp.sum(exp_terms, axis=2),
            )

        return lax.cond(is_live, stat_update, keep_state, loop_state)

    start_state = (
        jnp.full((head_count, span_rows), MASKED, jnp.float32),
        jnp.zeros((head_count, span_rows), jnp.float32),
    )
    running_max, running_sum = lax.fori_loop(0, block_count, stat_step, start_state)
    log_total = running_max + jnp.log(running_sum)

    def out_step(block_index, loop_state):
        first_key, key_rows, value_rows, same_doc, is_live = block_parts(
            block_index, key_all, value_all
        )

        def out_update(current):
            scores = block_scores(key_rows, same_doc)
            weights = jnp.where(
                same_doc[None], jnp.exp(scores - log_total[:, :, None]), 0.0
            ).astype(jnp.bfloat16)
            return current + jnp.einsum(
                "hqk,khd->qhd", weights, value_rows, preferred_element_type=jnp.float32
            )

        return lax.cond(is_live, out_update, keep_state, loop_state)

    mixed_full = lax.fori_loop(
        0, block_count, out_step, jnp.zeros((span_rows, head_count, HS), jnp.float32)
    )
    mixed_low = mixed_full.reshape(span_rows, head_count * HS).astype(jnp.bfloat16)
    mixed_tokens = lax.all_to_all(mixed_low, "head", split_axis=0, concat_axis=1, tiled=True)
    attended = jnp.dot(mixed_tokens, out_weight, preferred_element_type=jnp.float32)
    hidden_one = input_rows + attended
    normed_two, norm_two_pull = jax.vjp(layer_norm, hidden_one, gain_two.astype(jnp.float32))
    routed_low = normed_two.astype(jnp.bfloat16)
    router_probs, router_pull = jax.vjp(
        router, routed_low.astype(jnp.float32), router_weight.astype(jnp.float32)
    )
    slot_ids = slot_table(routes, priority[0], capacity)
    select = (
        slot_ids[:, :, None] == jnp.arange(slot_total, dtype=jnp.int32)[None, None, :]
    ).astype(jnp.bfloat16)
    send_rows = jnp.einsum(
        "kts,td->sd", select, routed_low, preferred_element_type=jnp.float32
    ).astype(jnp.bfloat16)
    expert_rows = lax.all_to_all(
        send_rows.reshape(blk_size, capacity, model_width),
        "blk",
        split_axis=0,
        concat_axis=0,
        tiled=True,
    ).reshape(slot_total, model_width)
    weight_in = expert_in[0]
    weight_out = expert_out[0]
    pre_act = jnp.dot(expert_rows, weight_in, preferred_element_type=jnp.float32)
    hidden_act, gelu_pull = jax.vjp(gelu_exact, pre_act)
    hidden_low = hidden_act.astype(jnp.bfloat16)
    expert_result = jnp.dot(hidden_low, weight_out, preferred_element_type=jnp.float32).astype(
        jnp.bfloat16
    )
    slot_result = lax.all_to_all(
        expert_result.reshape(blk_size, capacity, model_width),
        "blk",
        split_axis=0,
        concat_axis=0,
        tiled=True,
    ).reshape(slot_total, model_width)
    pair_result = jnp.einsum("kts,sd->ktd", select, slot_result, preferred_element_type=jnp.float32)
    route_hot = (routes[:, :, None] == jnp.arange(blk_size, dtype=jnp.int32)[None, None, :]).astype(
        jnp.float32
    )
    gate_vals = jnp.sum(router_probs[:, None, :] * route_hot, axis=2)
    mixture = gate_vals[:, 0, None] * pair_result[0] + gate_vals[:, 1, None] * pair_result[1]
    output = (hidden_one + mixture).astype(jnp.bfloat16)
    d_gates = jnp.transpose(jnp.sum(d_out[None] * pair_result, axis=2))
    d_probs = jnp.sum(d_gates[:, :, None] * route_hot, axis=1)
    pair_grads = (jnp.transpose(gate_vals)[:, :, None] * d_out[None]).astype(jnp.bfloat16)
    slot_grads = jnp.einsum(
        "kts,ktd->sd", select, pair_grads, preferred_element_type=jnp.float32
    ).astype(jnp.bfloat16)
    result_grads = lax.all_to_all(
        slot_grads.reshape(blk_size, capacity, model_width),
        "blk",
        split_axis=0,
        concat_axis=0,
        tiled=True,
    ).reshape(slot_total, model_width)
    d_hidden_act = jnp.dot(result_grads, weight_out.T, preferred_element_type=jnp.float32)
    d_weight_out = jnp.dot(hidden_low.T, result_grads, preferred_element_type=jnp.float32)
    d_preact = gelu_pull(d_hidden_act)[0].astype(jnp.bfloat16)
    d_weight_in = jnp.dot(expert_rows.T, d_preact, preferred_element_type=jnp.float32)
    row_grads = jnp.dot(d_preact, weight_in.T, preferred_element_type=jnp.float32).astype(
        jnp.bfloat16
    )
    slot_back = lax.all_to_all(
        row_grads.reshape(blk_size, capacity, model_width),
        "blk",
        split_axis=0,
        concat_axis=0,
        tiled=True,
    ).reshape(slot_total, model_width)
    d_routed = jnp.einsum("kts,sd->td", select, slot_back, preferred_element_type=jnp.float32)
    d_routed_router, d_router = router_pull(d_probs)
    d_hidden_norm, d_gain_two = norm_two_pull(d_routed + d_routed_router)
    d_hidden_one = d_out + d_hidden_norm
    attn_grads = d_hidden_one.astype(jnp.bfloat16)
    d_out_weight = jnp.dot(mixed_tokens.T, attn_grads, preferred_element_type=jnp.float32)
    mixed_grads = jnp.dot(attn_grads, out_weight.T, preferred_element_type=jnp.float32).astype(
        jnp.bfloat16
    )
    head_grads = lax.all_to_all(mixed_grads, "head", split_axis=1, concat_axis=0, tiled=True)
    out_grads = head_grads.reshape(span_rows, head_count, HS)
    row_delta = jnp.transpose(jnp.sum(out_grads.astype(jnp.float32) * mixed_full, axis=2))
    key_back, value_back = (
        lax.all_gather(key_heads, "blk", axis=0, tiled=True),
        lax.all_gather(value_heads, "blk", axis=0, tiled=True),
    )

    def grad_step(block_index, loop_state):
        first_key, key_rows, value_rows, same_doc, is_live = block_parts(
            block_index, key_back, value_back
        )

        def grad_update(current):
            query_grad, key_grad, value_grad = current
            scores = block_scores(key_rows, same_doc)
            weights = jnp.where(same_doc[None], jnp.exp(scores - log_total[:, :, None]), 0.0)
            value_part = jnp.einsum(
                "hqk,qhd->khd",
                weights.astype(jnp.bfloat16),
                out_grads,
                preferred_element_type=jnp.float32,
            )
            weight_grads = jnp.einsum(
                "qhd,khd->hqk", out_grads, value_rows, preferred_element_type=jnp.float32
            )
            score_grads = (weights * (weight_grads - row_delta[:, :, None])).astype(jnp.bfloat16)
            query_grad = (
                query_grad
                + jnp.einsum(
                    "hqk,khd->qhd", score_grads, key_rows, preferred_element_type=jnp.float32
                )
                * scale_factor
            )
            key_part = (
                jnp.einsum("hqk,qhd->khd", score_grads, queries, preferred_element_type=jnp.float32)
                * scale_factor
            )
            key_grad = lax.dynamic_update_slice_in_dim(
                key_grad, key_part.reshape(KEY_BLOCK, head_count * HS), first_key, 0
            )
            value_grad = lax.dynamic_update_slice_in_dim(
                value_grad, value_part.reshape(KEY_BLOCK, head_count * HS), first_key, 0
            )
            return (query_grad, key_grad, value_grad)

        return lax.cond(is_live, grad_update, keep_state, loop_state)

    start_grads = (
        jnp.zeros((span_rows, head_count, HS), jnp.float32),
        jnp.zeros((total_rows, head_count * HS), jnp.float32),
        jnp.zeros((total_rows, head_count * HS), jnp.float32),
    )
    query_grad, key_grad, value_grad = lax.fori_loop(0, block_count, grad_step, start_grads)
    key_own, value_own = (
        lax.psum_scatter(
            key_grad.astype(jnp.bfloat16), "blk", scatter_dimension=0, tiled=True
        ).astype(jnp.float32),
        lax.psum_scatter(
            value_grad.astype(jnp.bfloat16), "blk", scatter_dimension=0, tiled=True
        ).astype(jnp.float32),
    )
    query_tokens_grad, key_tokens_grad, value_tokens_grad = (
        lax.all_to_all(
            query_grad.reshape(span_rows, head_count * HS).astype(jnp.bfloat16),
            "head",
            split_axis=0,
            concat_axis=1,
            tiled=True,
        ),
        lax.all_to_all(
            key_own.astype(jnp.bfloat16), "head", split_axis=0, concat_axis=1, tiled=True
        ),
        lax.all_to_all(
            value_own.astype(jnp.bfloat16), "head", split_axis=0, concat_axis=1, tiled=True
        ),
    )
    qkv_grads = jnp.concatenate([query_tokens_grad, key_tokens_grad, value_tokens_grad], axis=1)
    d_qkv_weight = jnp.dot(normed_low.T, qkv_grads, preferred_element_type=jnp.float32)
    normed_grads = jnp.dot(qkv_grads, qkv_weight.T, preferred_element_type=jnp.float32)
    d_inputs_norm, d_gain_one = norm_one_pull(normed_grads)
    d_inputs = d_hidden_one + d_inputs_norm
    gain_one_sum, qkv_sum, out_sum, gain_two_sum, router_sum = (
        lax.psum_scatter(
            d_gain_one.astype(jnp.bfloat16), "blk", scatter_dimension=0, tiled=True
        ).astype(jnp.float32),
        lax.psum_scatter(
            d_qkv_weight.astype(jnp.bfloat16), "blk", scatter_dimension=0, tiled=True
        ).astype(jnp.float32),
        lax.psum_scatter(
            d_out_weight.astype(jnp.bfloat16), "blk", scatter_dimension=0, tiled=True
        ).astype(jnp.float32),
        lax.psum_scatter(
            d_gain_two.astype(jnp.bfloat16), "blk", scatter_dimension=0, tiled=True
        ).astype(jnp.float32),
        lax.psum_scatter(
            d_router.astype(jnp.bfloat16), "blk", scatter_dimension=0, tiled=True
        ).astype(jnp.float32),
    )
    gain_one_all, qkv_all, out_all, gain_two_all, router_all, expert_in_all, expert_out_all = (
        lax.psum(gain_one_sum.astype(jnp.bfloat16), "head").astype(jnp.float32),
        lax.psum(qkv_sum.astype(jnp.bfloat16), "head").astype(jnp.float32),
        lax.psum(out_sum.astype(jnp.bfloat16), "head").astype(jnp.float32),
        lax.psum(gain_two_sum.astype(jnp.bfloat16), "head").astype(jnp.float32),
        lax.psum(router_sum.astype(jnp.bfloat16), "head").astype(jnp.float32),
        lax.psum(d_weight_in[None].astype(jnp.bfloat16), "head").astype(jnp.float32),
        lax.psum(d_weight_out[None].astype(jnp.bfloat16), "head").astype(jnp.float32),
    )
    return (
        output,
        d_inputs,
        gain_one_all,
        qkv_all,
        out_all,
        gain_two_all,
        router_all,
        expert_in_all,
        expert_out_all,
    )


MESH = pl.DeviceIdType.MESH
LANES = 128
HALF = LANES // 2
MIB = 2**20
F32 = jnp.float32
BF16 = jnp.bfloat16


def dot(left, right, dims=(1, 0)):
    return lax.dot_general(
        left, right, (((dims[0],), (dims[1],)), ((), ())), preferred_element_type=F32
    )


def remote(src, dst, send_sem, recv_sem, head, blk):
    return pltpu.make_async_remote_copy(
        src_ref=src,
        dst_ref=dst,
        send_sem=send_sem,
        recv_sem=recv_sem,
        device_id={"head": head, "blk": blk},
        device_id_type=MESH,
    )


def arrived(ref, sem):
    pltpu.make_async_copy(ref, ref, sem).wait()


def greet(peers):
    barrier = pltpu.get_barrier_semaphore()
    for head, blk in peers:
        pl.semaphore_signal(
            barrier, inc=1, device_id={"head": head, "blk": blk}, device_id_type=MESH
        )
    return len(peers)


def meet(count):
    pl.semaphore_wait(pltpu.get_barrier_semaphore(), count)


def halves(values, lanes_kept):
    rows = values.shape[0] // 2
    moved = pltpu.roll(values[rows:], HALF, 1)
    return jnp.where(lanes_kept, values[:rows], moved)


def lane_ids(shape):
    return lax.broadcasted_iota(jnp.int32, shape, len(shape) - 1)


def centre(values):
    average = jnp.mean(values, axis=-1, keepdims=True)
    centred = values - average
    spread = jnp.mean(centred * centred, axis=-1, keepdims=True)
    scale = lax.rsqrt(spread + EPSILON)
    return centred * scale, scale


def centre_back(grad, xhat, scale):
    middle = jnp.mean(grad, axis=-1, keepdims=True)
    along = jnp.mean(grad * xhat, axis=-1, keepdims=True)
    return (grad - middle - xhat * along) * scale


def split_high_low(column, lanes):
    high = column.astype(BF16)
    low = (column - high.astype(F32)).astype(BF16)
    return jnp.where(lanes < HALF, high.astype(F32), low.astype(F32)).astype(BF16)


def join_high_low(matrix, start):
    return matrix[:, start : start + 1].astype(F32) + matrix[
        :, start + HALF : start + HALF + 1
    ].astype(F32)


def place():
    head, blk = lax.axis_index("head"), lax.axis_index("blk")
    return head, blk, blk // 2, lax.rem(blk, 2)


def around(index, step, size):
    return lax.rem(index + step, size)


QUERY_TILE = 256
CHAINS = 2


def masked_queries(q_ref, tile, key_lanes, query_tile):
    tiles_per_span = q_ref.shape[1] // query_tile
    inner = tile % tiles_per_span * query_tile
    query = q_ref[tile // tiles_per_span, inner : inner + query_tile, :]
    return jnp.where(key_lanes, query, jnp.zeros_like(query))


def group_blocks(bounds_ref, group, size, key_tile):
    first, last = group * size, (group + 1) * size
    low = jnp.min(bounds_ref[0:1, first : first + LANES])
    high = jnp.max(bounds_ref[1:2, last - LANES : last])
    return low // key_tile, (high + key_tile - 1) // key_tile


def inside_document(bounds_ref, tile, first, shape):
    key = first + lax.broadcasted_iota(jnp.int32, shape, 0)
    columns = slice(tile * shape[1], (tile + 1) * shape[1])
    return jnp.logical_and(key >= bounds_ref[0:1, columns], key < bounds_ref[1:2, columns])


def query_group(q_ref, group, y):
    key_lanes = (lane_ids((QUERY_TILE, LANES)) < HALF) == (y == 0)
    tiles = range(group * CHAINS, (group + 1) * CHAINS)
    return tiles, [masked_queries(q_ref, tile, key_lanes, QUERY_TILE) for tile in tiles]


def attend(bounds_ref, tiles, first, keys, keys_across, queries, carry):
    scores = [dot(keys, query, (1, 1)) for query in queries]
    made = []
    for tile, score, (biggest, weight, mixed) in zip(tiles, scores, carry):
        inside = inside_document(bounds_ref, tile, first, score.shape)
        score = jnp.where(inside, score, MASKED)
        bigger = jnp.maximum(biggest, jnp.max(score, axis=0, keepdims=True))
        fade = jnp.exp(biggest - bigger)
        terms = jnp.exp(score - bigger)
        weight = weight * fade + jnp.sum(terms, axis=0, keepdims=True)
        made.append((bigger, weight, mixed * fade + dot(keys_across, terms.astype(BF16))))
    return tuple(made)


def nothing_attended():
    return (
        jnp.full((1, QUERY_TILE), MASKED, F32),
        jnp.zeros((1, QUERY_TILE), F32),
        jnp.zeros((LANES, QUERY_TILE), F32),
    )


def attend_back(bounds_ref, tiles, first, keys, keys_across, group, carry):
    queries, out_grads, deltas, log_totals = group
    scores = [dot(keys, query, (1, 1)) for query in queries]
    weight_grads = [dot(keys, out_grad, (1, 1)) for out_grad in out_grads]
    pieces, score_grads = [], []
    for i, tile in enumerate(tiles):
        inside = inside_document(bounds_ref, tile, first, scores[i].shape)
        weights = jnp.exp(jnp.where(inside, scores[i], MASKED) - log_totals[i])
        score_grads.append((weights * (weight_grads[i] - deltas[i])).astype(BF16))
        pieces.append(weights.astype(BF16))
    wide = jnp.concatenate(score_grads + pieces, axis=1)
    given = dot(wide, jnp.concatenate(queries + out_grads, axis=0))
    return given, tuple(c + dot(keys_across, g) for c, g in zip(carry, score_grads))


def group_grads(do_ref, tiles, y):
    key_lanes = (lane_ids((QUERY_TILE, LANES)) < HALF) == (y == 0)
    out_grads = []
    for tile in tiles:
        parts = []
        for part in range(QUERY_TILE // LANES):
            packed = do_ref[tile, part].astype(F32)
            parts += [packed, pltpu.roll(packed, HALF, 1)]
        out_grads.append(jnp.where(key_lanes, 0.0, jnp.concatenate(parts, axis=0)).astype(BF16))
    return out_grads


def qkv_kernel(
    heads, blks,
    x_hbm, w_hbm, g1_hbm, wo_hbm, wr_hbm, g2_hbm, docs_hbm,
    qall, kvall, xall, wall, wo_all, kvt, bounds, begun,
    x_ref, w_ref, rows_in, g1_ref, g2_ref, wr_ref, docs_ref, wo_own, kv_other, q_packed, q_landed, in_sem,
    x_send, x_recv, w_send, w_recv, o_send, o_recv, p_send, p_recv,
    k_send, k_recv, q_recv,
):
    head, blk, z, y = place()
    planes = blks // 2
    model = x_ref.shape[1]
    rows = w_ref.shape[0]
    part = rows // heads
    experts = wr_ref.shape[0]
    wanted = (
        (w_hbm, w_ref), (g1_hbm, g1_ref), (g2_hbm, g2_ref), (wr_hbm, wr_ref), (x_hbm, x_ref),
        (wo_hbm, wo_own.at[:, pl.ds(0, model)]), (docs_hbm, docs_ref),
    )
    fetched = [
        pltpu.make_async_copy(src, dst, in_sem.at[i]) for i, (src, dst) in enumerate(wanted)
    ]
    for copy in fetched:
        copy.start()
    rows_in[...] = jnp.zeros_like(rows_in)
    met = greet(
        [(around(head, k, heads), blk) for k in range(1, heads)]
        + [(head, around(blk, k, blks)) for k in range(1, blks)]
    )
    lanes = lane_ids((rows, LANES))
    for copy in fetched:
        copy.wait()
    rows_in[0:experts, 0:rows] = wr_ref[...].astype(F32)
    rows_in[experts : experts + 1, 0:rows] = g2_ref[...].astype(F32)
    rows_in[experts + 1 : experts + 2, 0:rows] = g1_ref[...].astype(F32)
    vectors = jnp.transpose(rows_in[...])[:rows]
    gain = vectors[:, experts + 1 : experts + 2]

    def columns(which):
        start = pl.multiple_of(which * model + head * LANES, LANES)
        return w_ref[:, pl.ds(start, LANES)].astype(F32) * gain

    key_cols = columns(1)
    value_cols = pltpu.roll(columns(2), HALF, 1)
    wall[blk, :, 0:LANES] = jnp.where(lanes < HALF, key_cols, value_cols).astype(BF16)
    wall[blk, :, LANES : 2 * LANES] = jnp.where(lanes < HALF, value_cols, key_cols).astype(BF16)
    wall[blk, :, 2 * LANES : 3 * LANES] = (columns(0) * HS ** (-0.5)).astype(BF16)
    def slice_copy(slot, source, target):
        ref = wall.at[source]
        return remote(ref, ref, w_send.at[slot], w_recv.at[source], head, target)

    pair = 2 * z + around(y, 1, 2)
    line = [2 * around(z, step, planes) + y for step in (1, planes - 1, *range(2, planes - 1))]
    w_copies = [slice_copy(slot, blk, target) for slot, target in enumerate((*line, pair))]
    w_onward = [slice_copy(planes + slot, source, pair) for slot, source in enumerate(line)]
    xhat, _ = centre(x_ref[...].astype(F32))
    xall[head] = xhat.astype(BF16)
    meet(met)
    for copy in w_copies:
        copy.start()
    x_copies = [
        remote(xall.at[head], xall.at[head], x_send.at[k], x_recv.at[k], around(head, k, heads), blk)
        for k in range(1, heads)
    ]
    for copy in x_copies:
        copy.start()
    wo_own[:, model : model + LANES] = vectors.astype(BF16)
    wo_all[blk, head] = wo_own[pl.ds(pl.multiple_of(head * part, part), part), :]
    o_copies = [
        remote(
            wo_all.at[blk, head], wo_all.at[blk, head],
            o_send.at[k], o_recv.at[k], head, around(blk, k, blks),
        )
        for k in range(1, blks)
    ]
    document_bounds(docs_ref, bounds, z)
    for source, copy in zip(line, w_onward):
        arrived(wall.at[source], w_recv.at[source])
        copy.start()
    for copy in o_copies:
        copy.start()
    for source in (pair, *[other - y + around(y, 1, 2) for other in line]):
        arrived(wall.at[source], w_recv.at[source])
    for copy in w_copies + w_onward:
        copy.wait_send()
    for copy in x_copies:
        copy.wait()
    weight = wall[...].reshape(model, 3 * LANES)
    tokens = x_ref.shape[0]
    even = y == 0
    above, below = z < planes - 1, z > 0
    half_span = kvall.shape[1] // 2
    sides = ((1, above, below, 0), (-1, below, above, 4))

    def half_of(ref, half):
        return ref.at[pl.ds(half * half_span, half_span)]

    def outward(slot, step, across, half):
        target = 2 * (z + step) + around(y, across, 2)
        return remote(
            half_of(kv_other if across else kvall.at[blk], half), half_of(kvall.at[blk], half),
            k_send.at[slot], k_recv.at[blk, half], head, target,
        )

    def onward(slot, step, side, half):
        from_span = 2 * (z - step) + side
        ref = half_of(kvall.at[from_span], half)
        return remote(ref, ref, k_send.at[slot], k_recv.at[from_span, half], head, 2 * (z + step) + y)

    def await_half(span, half):
        arrived(half_of(kvall.at[span], half), k_recv.at[span, half])

    def turn(span):
        size = kvall.shape[1]
        kvt[:, pl.ds(pl.multiple_of(span * size, size), size)] = jnp.transpose(kvall[span])

    for half in range(2):
        for piece in range(half * heads // 2, (half + 1) * heads // 2):
            made = dot(xall[piece], weight).astype(BF16)
            first, second = made[:, 0:LANES], made[:, LANES : 2 * LANES]
            span = slice(piece * tokens, (piece + 1) * tokens)
            kvall[blk, span, :] = jnp.where(even, first, second)
            kv_other[span, :] = jnp.where(even, second, first)
            qall[y, span, :] = made[:, 2 * LANES : 3 * LANES]
        outward(8 + half, 0, 1, half).start()
        for step, there, _, slot in sides:

            @pl.when(there)
            def _():
                outward(slot + 2 * half, step, 0, half).start()
                outward(slot + 2 * half + 1, step, 1, half).start()

    other_y = around(y, 1, 2)
    kept = (lane_ids(q_packed.shape) < HALF) == (y == 1)
    q_packed[...] = halves(qall[y].astype(F32), kept).astype(BF16)
    q_pair = remote(q_packed, q_landed, k_send.at[10], q_recv, head, 2 * z + other_y)
    q_pair.start()
    turn(blk)
    for copy in o_copies:
        copy.wait()
    core = lax.rem(head, 2)
    sibling, across = head - core + 1 - core, around(head, 2, heads)

    def quarter_copy(index, quarter, to_head):
        ref = wo_all.at[:, quarter]
        return remote(ref, ref, p_send.at[index], p_recv.at[index], to_head, blk)

    p_copies = [quarter_copy(0, head, sibling), quarter_copy(1, head, across)]
    for copy in p_copies:
        copy.start()
    p_copies.append(quarter_copy(2, across, sibling))
    for half in range(2):
        for step, there, back, slot in sides:

            @pl.when(back)
            def _():
                for side in range(2):
                    await_half(2 * (z - step) + side, half)

            @pl.when(jnp.logical_and(there, back))
            def _():
                for side in range(2):
                    onward(11 + slot + 2 * half + side, step, side, half).start()

    arrived(wo_all.at[:, across], p_recv.at[1])
    p_copies[2].start()
    for half in range(2):
        await_half(pair, half)
    turn(pair)
    q_pair.wait()
    landed = q_landed[...]
    qall[other_y, 0:half_span, :] = landed
    qall[other_y, half_span : 2 * half_span, :] = pltpu.roll(landed.astype(F32), HALF, 1).astype(BF16)
    key_tile = kvall.shape[1]
    for group in range(2 * key_tile // (CHAINS * QUERY_TILE)):
        tiles, queries = query_group(qall, group, y)
        carry = (nothing_attended(),) * CHAINS
        for side in range(2):
            first = pl.multiple_of((2 * z + side) * key_tile, key_tile)
            keys_across = kvt[:, pl.ds(first, key_tile)]
            carry = attend(bounds, tiles, first, kvall[2 * z + side], keys_across, queries, carry)
        for tile, (biggest, weight, mixed) in zip(tiles, carry):
            begun[tile, 0:LANES] = mixed
            begun[tile, LANES : LANES + 8] = jnp.broadcast_to(biggest, (8, QUERY_TILE))
            begun[tile, LANES + 8 : LANES + 16] = jnp.broadcast_to(weight, (8, QUERY_TILE))
    for step, there, back, slot in sides:

        @pl.when(back)
        def _():
            for side in range(2):
                turn(2 * (z - step) + side)

    for other in range(planes):
        for side in range(2):
            span = 2 * other + side

            @pl.when(jnp.logical_or(z - other == 2, other - z == 2))
            def _():
                for half in range(2):
                    await_half(span, half)
                turn(span)

    for index, quarter in ((0, sibling), (2, around(sibling, 2, heads))):
        arrived(wo_all.at[:, quarter], p_recv.at[index])
    for copy in p_copies:
        copy.wait_send()
    for half in range(2):
        outward(8 + half, 0, 1, half).wait_send()
        for step, there, back, slot in sides:

            @pl.when(there)
            def _():
                outward(slot + 2 * half, step, 0, half).wait_send()
                outward(slot + 2 * half + 1, step, 1, half).wait_send()

            @pl.when(jnp.logical_and(there, back))
            def _():
                for side in range(2):
                    onward(11 + slot + 2 * half + side, step, side, half).wait_send()


def document_bounds(docs_ref, bounds, z):
    count = docs_ref.shape[1]
    lengths = docs_ref[...].astype(F32)
    doc = lax.broadcasted_iota(jnp.int32, (count, count), 0)
    other = lane_ids((count, count))
    start = jnp.sum(jnp.where(other < doc, lengths, 0.0), axis=1, keepdims=True)
    end = jnp.sum(jnp.where(other <= doc, lengths, 0.0), axis=1, keepdims=True)
    queries = bounds.shape[1]
    token = (z * queries + lane_ids((count, queries))).astype(F32)
    begun = start <= token
    bounds[...] = jnp.zeros_like(bounds)
    bounds[0:1, :] = jnp.max(jnp.where(begun, start, 0.0), axis=0, keepdims=True).astype(jnp.int32)
    bounds[1:2, :] = jnp.max(jnp.where(begun, end, 0.0), axis=0, keepdims=True).astype(jnp.int32)


def vmem_specs(count):
    return [pl.BlockSpec(memory_space=pltpu.VMEM)] * count


def hbm_specs(count):
    return [pl.BlockSpec(memory_space=pltpu.HBM)] * count


def in_hbm(*arrays):
    return [pltpu.with_memory_space_constraint(array, pltpu.HBM) for array in arrays]


def dma(*shape):
    return pltpu.SemaphoreType.DMA(shape)


def call_qkv(x, w_qkv, g1, w_out, w_router, g2, doc_lengths, heads, blks):
    tokens, model = x.shape
    rows = w_qkv.shape[0]
    span = tokens * heads
    wide = model + LANES
    part = rows // heads
    return pl.pallas_call(
        functools.partial(qkv_kernel, heads, blks),
        out_shape=(
            jax.ShapeDtypeStruct((2, span, LANES), BF16),
            jax.ShapeDtypeStruct((blks, span, LANES), BF16),
            jax.ShapeDtypeStruct((heads, tokens, model), BF16),
            jax.ShapeDtypeStruct((blks, rows, 3 * LANES), BF16),
            jax.ShapeDtypeStruct((blks, heads, part, wide), BF16),
            jax.ShapeDtypeStruct((LANES, blks * span), BF16),
            jax.ShapeDtypeStruct((8, 2 * span), jnp.int32),
            jax.ShapeDtypeStruct((2 * span // QUERY_TILE, LANES + 16, QUERY_TILE), F32),
        ),
        in_specs=hbm_specs(7),
        out_specs=tuple(vmem_specs(8)),
        scratch_shapes=[
            pltpu.VMEM((tokens, model), BF16),
            pltpu.VMEM((rows, 3 * model), BF16),
            pltpu.VMEM((LANES, LANES), F32),
            pltpu.VMEM((1, rows), BF16),
            pltpu.VMEM((1, rows), BF16),
            pltpu.VMEM((w_router.shape[1], rows), BF16),
            pltpu.VMEM((1, doc_lengths.shape[0]), jnp.int32),
            pltpu.VMEM((rows, wide), BF16),
            pltpu.VMEM((span, LANES), BF16),
            pltpu.VMEM((span // 2, LANES), BF16),
            pltpu.VMEM((span // 2, LANES), BF16),
            dma(7),
            dma(heads), dma(heads), dma(blks), dma(blks), dma(blks), dma(blks), dma(heads), dma(heads),
            dma(19), dma(blks, 2), pltpu.SemaphoreType.DMA,
        ],
        compiler_params=pltpu.CompilerParams(
            collective_id=1, has_side_effects=True, vmem_limit_bytes=16 * MIB
        ),
        name="qkv",
    )(
        *in_hbm(
            x, w_qkv, g1.reshape(1, rows), w_out, w_router.T, g2.reshape(1, rows),
            doc_lengths.reshape(1, -1),
        )
    )


def other_blocks(bounds_ref, group, key_tile, z, step, carry):
    low, high = group_blocks(bounds_ref, group, CHAINS * QUERY_TILE, key_tile)
    carry = lax.fori_loop(low, 2 * z, step, carry)
    return lax.fori_loop(2 * z + 2, high, step, carry)


def forward_kernel(bounds_ref, q_ref, kv_ref, kvt_ref, begun_ref, o_out, ob_out, lse_out):
    _, _, z, y = place()
    key_tile = kv_ref.shape[1]
    value_lanes = (lane_ids((HALF, LANES)) < HALF) == (y == 1)
    for group in range(q_ref.shape[0] * q_ref.shape[1] // (CHAINS * QUERY_TILE)):
        tiles, queries = query_group(q_ref, group, y)

        def step(block, carry, queries=queries, tiles=tiles):
            first = pl.multiple_of(block * key_tile, key_tile)
            across = kvt_ref[:, pl.ds(first, key_tile)]
            return attend(bounds_ref, tiles, first, kv_ref[block], across, queries, carry)

        start = tuple(
            (begun_ref[t, LANES : LANES + 1], begun_ref[t, LANES + 8 : LANES + 9], begun_ref[t, 0:LANES])
            for t in tiles
        )
        ends = other_blocks(bounds_ref, group, key_tile, z, step, start)
        for tile, (biggest, weight, mixed) in zip(tiles, ends):
            result = jnp.transpose(mixed / weight)
            o_out[tile] = result
            for part in range(QUERY_TILE // LANES):
                block = result[part * LANES : (part + 1) * LANES]
                ob_out[tile, part] = halves(block, value_lanes).astype(BF16)
            lse_out[tile] = jnp.broadcast_to(biggest + jnp.log(weight), (8, QUERY_TILE))


def call_forward(bounds, q, kv, kvt, begun):
    blks, span, _ = kv.shape
    tiles = 2 * span // QUERY_TILE
    return pl.pallas_call(
        forward_kernel,
        out_shape=(
            jax.ShapeDtypeStruct((tiles, QUERY_TILE, LANES), F32),
            jax.ShapeDtypeStruct((tiles, QUERY_TILE // LANES, HALF, LANES), BF16),
            jax.ShapeDtypeStruct((tiles, 8, QUERY_TILE), F32),
        ),
        in_specs=vmem_specs(5),
        out_specs=tuple(vmem_specs(3)),
        compiler_params=pltpu.CompilerParams(vmem_limit_bytes=16 * MIB),
        name="attend",
    )(bounds, q, kv, kvt, begun)


def backward_kernel(
    bounds_ref, q_ref, kv_ref, kvt_ref, do_ref, o_ref, lse_ref, dq_out, dkv_out, delta_out, dkv
):
    _, _, z, y = place()
    key_tile = kv_ref.shape[1]
    dkv[...] = jnp.zeros_like(dkv)
    for group in range(q_ref.shape[0] * q_ref.shape[1] // (CHAINS * QUERY_TILE)):
        tiles, queries = query_group(q_ref, group, y)
        out_grads = group_grads(do_ref, tiles, y)
        deltas, log_totals = [], []
        for tile, out_grad in zip(tiles, out_grads):
            product = jnp.transpose(out_grad.astype(F32) * o_ref[tile])
            deltas.append(jnp.sum(product, axis=0, keepdims=True))
            delta_out[tile] = jnp.broadcast_to(deltas[-1], delta_out.shape[1:])
            log_totals.append(lse_ref[tile, 0:1, :])
        known = (queries, out_grads, deltas, log_totals)

        def step(block, carry, tiles=tiles, known=known):
            first = pl.multiple_of(block * key_tile, key_tile)
            across = kvt_ref[:, pl.ds(first, key_tile)]
            given, carry = attend_back(bounds_ref, tiles, first, kv_ref[block], across, known, carry)
            dkv[block] += given
            return carry

        zero = jnp.zeros((LANES, QUERY_TILE), F32)
        ends = other_blocks(bounds_ref, group, key_tile, z, step, (zero,) * CHAINS)
        for tile, mixed in zip(tiles, ends):
            dq_out[tile] = mixed
    for block in range(dkv.shape[0]):
        dkv_out[block] = dkv[block].astype(BF16)


def call_backward(bounds, q, kv, kvt, d_o, o, lse):
    blks, span, _ = kv.shape
    tiles = 2 * span // QUERY_TILE
    return pl.pallas_call(
        backward_kernel,
        out_shape=(
            jax.ShapeDtypeStruct((tiles, LANES, QUERY_TILE), F32),
            jax.ShapeDtypeStruct((blks, span, LANES), BF16),
            jax.ShapeDtypeStruct((tiles, 8, QUERY_TILE), F32),
        ),
        in_specs=vmem_specs(7),
        out_specs=tuple(vmem_specs(3)),
        scratch_shapes=[pltpu.VMEM((blks, span, LANES), F32)],
        compiler_params=pltpu.CompilerParams(vmem_limit_bytes=16 * MIB),
        name="attend_back",
    )(bounds, q, kv, kvt, d_o, o, lse)


def gelu_parts(values):
    share = 0.5 * (1.0 + lax.erf(values * (2.0**-0.5)))
    slope = share + values * jnp.exp(-0.5 * values * values) * (2.0 * math.pi) ** -0.5
    return values * share, slope


def positions(expert_rows, expert_cols, rank_row, rank_col):
    def count(mask, axis):
        return jnp.sum(mask.astype(F32), axis=axis, keepdims=True)

    row = [None, None]
    col = [None, None]
    before = rank_col < rank_row
    after = rank_row < rank_col
    for choice in range(2):
        row[choice] = count((expert_cols[choice] == expert_rows[choice]) & before, 0)
        col[choice] = count((expert_rows[choice] == expert_cols[choice]) & after, 1)
    row[1] = row[1] + count(expert_cols[0] == expert_rows[1], 0)
    col[1] = col[1] + count(expert_rows[0] == expert_cols[1], 1)
    return row, col


def own_columns(rows_ref, turned, blk, capacity):
    blks, _, slots = rows_ref.shape
    rows = jnp.concatenate(
        [rows_ref[...].reshape(blks, slots), jnp.zeros((LANES - blks, slots), F32)], axis=0
    )
    for piece in range(slots // LANES):
        columns = slice(piece * LANES, (piece + 1) * LANES)
        turned[columns, :] = jnp.transpose(rows[:, columns])
    own = turned[pl.ds(pl.multiple_of(blk * capacity, capacity), capacity), :]
    return jnp.concatenate([own[:, source : source + 1] for source in range(blks)], axis=0)


def middle_kernel(
    heads, blks,
    x_hbm, o_ref, wo_ref, routes_hbm, rank_hbm, d_out_hbm, win_hbm, wout_hbm,
    po, pa, hidden_ref, share_ref, dh_ref, dma_all, grads_ref, rx,
    x_ref, routes_ref, rank_ref, d_out_ref, win_ref, wout_ref, rows_in, in_sem,
    o_all, dos, doa, rs, ra, dr, da, dms, mix, gate_rows, d_gate_rows, turned,
    o_send, o_recv, dos_send, dos_recv, r_send, r_recv,
    dr_send, dr_recv, dm_send, dm_recv, rx_send, rx_recv, g_send, g_recv, dg_send, dg_recv, pa_send, pa_recv,
):
    head, blk, z, y = place()
    tokens, model = x_ref.shape
    capacity = 2 * tokens // blks
    slots = capacity * blks
    plane = [(k % heads, k // heads) for k in range(1, 2 * heads)]
    wanted = (
        (routes_hbm, routes_ref), (rank_hbm, rank_ref), (d_out_hbm, d_out_ref), (x_hbm, x_ref),
        (win_hbm, win_ref), (wout_hbm, wout_ref),
    )
    fetched = [
        pltpu.make_async_copy(src, dst, in_sem.at[i]) for i, (src, dst) in enumerate(wanted)
    ]
    for copy in fetched:
        copy.start()
    met = greet(
        [(around(head, kh, heads), 2 * z + around(y, ky, 2)) for kh, ky in plane]
        + [(head, around(blk, k, blks)) for k in range(1, blks)]
    )
    meet(met)

    def plane_copies(src_of, dst, send, recv):
        copies = []
        for k, (kh, ky) in enumerate(plane):
            to_head, to_y = around(head, kh, heads), around(y, ky, 2)
            copies.append(
                remote(src_of(to_y, to_head), dst, send.at[k], recv.at[k], to_head, 2 * z + to_y)
            )
        return copies

    def blk_copies(src, dst, send, recv):
        return [
            remote(
                src.at[around(blk, k, blks)], dst.at[blk],
                send.at[k], recv.at[k], head, around(blk, k, blks),
            )
            for k in range(1, blks)
        ]

    def start(copies):
        for copy in copies:
            copy.start()

    def finish(copies):
        for copy in copies:
            copy.wait()

    o_copies = plane_copies(lambda to_y, to_head: o_ref.at[to_y, to_head], o_all.at[y, head], o_send, o_recv)
    start(o_copies)
    o_all[y, head] = o_ref[y, head]

    lanes = lane_ids((tokens, LANES))
    for copy in fetched[:4]:
        copy.wait()
    e_rows = [routes_ref[i : i + 1, :].astype(F32) for i in range(2)]
    rank_row = rank_ref[...].astype(F32)
    rows_in[...] = jnp.zeros_like(rows_in)
    rows_in[0:1, :], rows_in[1:2, :], rows_in[2:3, :] = *e_rows, rank_row
    columns = jnp.transpose(rows_in[...])
    e_cols = [columns[:, 0:1], columns[:, 1:2]]
    rank_col = columns[:, 2:3]
    pos_rows, pos_cols = positions(e_rows, e_cols, rank_row, rank_col)

    def slot_of(expert, position):
        return jnp.where(position < capacity, expert * capacity + position, -1.0).astype(jnp.int32)

    slot_rows = [slot_of(e, p) for e, p in zip(e_rows, pos_rows)]
    slot_cols = [slot_of(e, p) for e, p in zip(e_cols, pos_cols)]
    slot_down = lax.broadcasted_iota(jnp.int32, (slots, tokens), 0)
    slot_across = lane_ids((tokens, slots))
    pick = [(slot_down == s).astype(BF16) for s in slot_rows]
    put = [(slot_across == s).astype(BF16) for s in slot_cols]
    pick_any = pick[0] + pick[1]
    put_any = put[0] + put[1]

    d_out = d_out_ref[...]
    dos[...] = dot(pick_any, d_out.astype(BF16)).astype(BF16).reshape(dos.shape)
    dos_copies = blk_copies(dos, doa, dos_send, dos_recv)
    start(dos_copies)
    doa[blk] = dos[blk]

    weight_out = jnp.concatenate(
        [wo_ref[(b ^ 1) * HALF : ((b ^ 1) + 1) * HALF, 0:model] for b in range(blks)], axis=0
    )
    small = wo_ref[:, model : model + LANES]
    small_across = jnp.concatenate(
        [
            jnp.transpose(small[i * LANES : (i + 1) * LANES].astype(F32))
            for i in range(model // LANES)
        ],
        axis=1,
    )
    gain = small_across[blks : blks + 1, :]

    finish(o_copies)
    low_lanes = lanes[:HALF] < HALF
    for piece in range(heads):
        columns = slice(piece * LANES, (piece + 1) * LANES)
        first, second = o_all[1, piece].astype(F32), o_all[0, piece].astype(F32)
        mix[:HALF, columns] = jnp.where(low_lanes, first, second).astype(BF16)
        swapped = pltpu.roll(jnp.where(low_lanes, second, first), HALF, 1)
        mix[HALF:, columns] = swapped.astype(BF16)
    mixed = mix[...]
    hidden = x_ref[...].astype(F32) + dot(mixed, weight_out)
    xhat, scale = centre(hidden)
    routed = (xhat * gain).astype(BF16)
    rs[...] = dot(pick_any, routed).astype(BF16).reshape(rs.shape)
    r_copies = blk_copies(rs, ra, r_send, r_recv)
    start(r_copies)
    ra[blk] = rs[blk]
    logits = jnp.where(lanes < blks, dot(routed, small), MASKED)
    powers = jnp.exp(logits - jnp.max(logits, axis=1, keepdims=True))
    probs = powers / jnp.sum(powers, axis=1, keepdims=True)
    lanes_f = lanes.astype(F32)
    hots = [lanes_f == e for e in e_cols]
    gates = [jnp.sum(jnp.where(hot, probs, 0.0), axis=1, keepdims=True) for hot in hots]
    gate_high = [g.astype(BF16).astype(F32) for g in gates]
    gate_across = jnp.transpose(
        jnp.where(lanes == 0, gate_high[0], jnp.where(lanes == 1, gates[0] - gate_high[0], 0.0))
        + jnp.where(lanes == 2, gate_high[1], jnp.where(lanes == 3, gates[1] - gate_high[1], 0.0))
    ).astype(BF16)
    by_slot = (dot(gate_across, put[0]), dot(gate_across, put[1]))
    gate_rows[blk] = by_slot[0][0:1] + by_slot[0][1:2] + by_slot[1][2:3] + by_slot[1][3:4]
    g_copies = [
        remote(
            gate_rows.at[blk], gate_rows.at[blk],
            g_send.at[k], g_recv.at[k], head, around(blk, k, blks),
        )
        for k in range(1, blks)
    ]
    start(g_copies)
    finish(dos_copies)
    finish(r_copies)

    out_rows = doa[...].reshape(slots, model)
    rx[head, :, 0:model] = ra[...].reshape(slots, model)
    finish(g_copies)
    gate_col = own_columns(gate_rows, turned, blk, capacity)
    rx[head, :, model : 2 * model] = (out_rows.astype(F32) * gate_col).astype(BF16)
    core = lax.rem(head, 2)
    sibling, across = head - core + 1 - core, around(head, 2, heads)

    def half_rows(source, half):
        return rx.at[source, pl.ds(half * slots // 2, slots // 2)]

    to_across = [
        remote(
            half_rows(head, half), half_rows(head, half),
            rx_send.at[1 + half], rx_recv.at[1 + half], across, blk,
        )
        for half in range(2)
    ]
    to_sibling = remote(rx.at[head], rx.at[head], rx_send.at[0], rx_recv.at[0], sibling, blk)
    forwards = [
        remote(
            half_rows(across, half), half_rows(across, half),
            rx_send.at[3 + half], rx_recv.at[3 + half], sibling, blk,
        )
        for half in range(2)
    ]
    start(to_across)
    to_sibling.start()
    for copy in fetched[4:]:
        copy.wait()
    act, slope = gelu_parts(dot(rx[head, :, 0:model], win_ref[...]))
    d_act = dot(rx[head, :, model : 2 * model], wout_ref[...], (1, 1))
    row_grads = dot((slope * d_act).astype(BF16), win_ref[...], (1, 1))
    dr[...] = row_grads.astype(BF16).reshape(dr.shape)
    dr_copies = blk_copies(dr, da, dr_send, dr_recv)
    start(dr_copies)
    result = dot(act.astype(BF16), wout_ref[...]).astype(BF16)
    d_gate = jnp.sum(out_rows.astype(F32) * result.astype(F32), axis=1, keepdims=True)
    da[blk] = dr[blk]
    d_wide = jnp.broadcast_to(d_gate, (slots, LANES))
    d_gate_rows[blk] = jnp.concatenate(
        [jnp.transpose(d_wide[i * LANES : (i + 1) * LANES])[0:1] for i in range(slots // LANES)],
        axis=1,
    )
    dg_copies = [
        remote(
            d_gate_rows.at[blk], d_gate_rows.at[blk],
            dg_send.at[k], dg_recv.at[k], head, around(blk, k, blks),
        )
        for k in range(1, blks)
    ]
    start(dg_copies)
    po[...] = result.reshape(blks, capacity, model)

    finish(dg_copies)
    back_gate = own_columns(d_gate_rows, turned, blk, capacity)
    back_gate = split_high_low(back_gate, lane_ids((slots, LANES)))
    d_gates = [join_high_low(dot(p, back_gate), 0) for p in put]
    d_probs = jnp.where(hots[0], d_gates[0], 0.0) + jnp.where(hots[1], d_gates[1], 0.0)
    d_logits = probs * (d_probs - jnp.sum(probs * d_probs, axis=1, keepdims=True))
    d_high = d_logits.astype(BF16)
    d_low = (d_logits - d_high.astype(F32)).astype(BF16)
    d_router_part = dot(d_high, small, (1, 1)) + dot(d_low, small, (1, 1))
    finish(dr_copies)
    d_routed = dot(put_any, da[...].reshape(slots, model)) + d_router_part
    d_hidden = d_out + centre_back(d_routed * gain, xhat, scale)
    dh_ref[...] = d_hidden
    d_attn = d_hidden.astype(BF16)
    d_mixed = dot(d_attn, weight_out, (1, 1))
    for piece in range(heads):
        block = d_mixed[:, piece * LANES : (piece + 1) * LANES]
        for to_y in range(2):
            dms[to_y, piece] = halves(block, low_lanes == (to_y == 1)).astype(BF16)
    dm_copies = plane_copies(lambda to_y, to_head: dms.at[to_y, to_head], dma_all.at[y, head], dm_send, dm_recv)
    start(dm_copies)
    dma_all[y, head] = dms[y, head]
    first_half = pa.shape[1]
    pa_copies = [
        remote(
            po.at[around(blk, k, blks), pl.ds(0, first_half)], pa.at[blk],
            pa_send.at[k], pa_recv.at[k], head, around(blk, k, blks),
        )
        for k in range(1, blks)
    ]
    start(pa_copies)
    pa[blk] = po[blk, 0:first_half]
    arrived(half_rows(across, 0), rx_recv.at[1])
    forwards[0].start()

    d_weight = dot(mixed, d_attn, (0, 0)).astype(BF16)
    for b in range(blks):
        grads_ref[b, :, 0:model] = d_weight[(b ^ 1) * HALF : ((b ^ 1) + 1) * HALF, :]
    last = (lanes == blks).astype(BF16)
    d_small = dot(routed, d_high, (0, 0)) + dot((d_routed * xhat).astype(BF16), last, (0, 0))
    grads_ref[:, :, model : model + LANES] = d_small.astype(BF16).reshape(blks, HALF, LANES)
    share = gates[0] * put[0].astype(F32) + gates[1] * put[1].astype(F32)
    share_ref[0] = share.astype(BF16)
    share_ref[1] = (share - share_ref[0].astype(F32)).astype(BF16)
    hidden_ref[...] = hidden

    arrived(half_rows(across, 1), rx_recv.at[2])
    forwards[1].start()
    finish(dm_copies)
    finish(pa_copies)
    to_sibling.wait()
    for copy in to_across:
        copy.wait_send()
    finish(forwards)


def call_middle(x, o, wo, routes, rank, d_out, win, wout, heads, blks):
    tokens, model = x.shape
    capacity = 2 * tokens // blks
    slots = capacity * blks
    wide = model + LANES

    def rows(width):
        return pltpu.VMEM((blks, capacity, width), BF16)

    def block(*lead):
        return pltpu.VMEM((*lead, tokens // 2, LANES), BF16)

    return pl.pallas_call(
        functools.partial(middle_kernel, heads, blks),
        out_shape=(
            jax.ShapeDtypeStruct((blks, capacity, model), BF16),
            jax.ShapeDtypeStruct((blks, capacity // 2, model), BF16),
            jax.ShapeDtypeStruct((tokens, model), F32),
            jax.ShapeDtypeStruct((2, tokens, slots), BF16),
            jax.ShapeDtypeStruct((tokens, model), F32),
            jax.ShapeDtypeStruct((2, heads, tokens // 2, LANES), BF16),
            jax.ShapeDtypeStruct((blks, model // blks, wide), BF16),
            jax.ShapeDtypeStruct((heads, slots, 2 * model), BF16),
        ),
        in_specs=hbm_specs(1) + vmem_specs(2) + hbm_specs(5),
        out_specs=tuple(vmem_specs(8)),
        scratch_shapes=[
            pltpu.VMEM((tokens, model), BF16),
            pltpu.VMEM((2, tokens), jnp.int32),
            pltpu.VMEM((1, tokens), jnp.int32),
            pltpu.VMEM((tokens, model), F32),
            pltpu.VMEM(win.shape, BF16),
            pltpu.VMEM(wout.shape, BF16),
            pltpu.VMEM((tokens, tokens), F32),
            dma(6),
            block(2, heads), rows(model), rows(model), rows(model), rows(model),
            rows(model), rows(model), block(2, heads),
            pltpu.VMEM((tokens, model), BF16),
            pltpu.VMEM((blks, 1, slots), F32), pltpu.VMEM((blks, 1, slots), F32),
            pltpu.VMEM((slots, LANES), F32),
            dma(2 * heads), dma(2 * heads), dma(blks), dma(blks), dma(blks), dma(blks),
            dma(blks), dma(blks), dma(2 * heads), dma(2 * heads), dma(5), dma(5),
            dma(blks), dma(blks), dma(blks), dma(blks), dma(blks), dma(blks),
        ],
        compiler_params=pltpu.CompilerParams(
            collective_id=2, has_side_effects=True, vmem_limit_bytes=20 * MIB
        ),
        name="experts",
    )(*in_hbm(x), o, wo, *in_hbm(routes.T, rank, d_out, win, wout))


def last_kernel(
    heads, blks,
    x_hbm, dh_ref, begun_ref, dkv_ref, xa_ref, wa_ref, w_hbm, g1_hbm, grads_ref, rx_ref, win_hbm, wout_hbm,
    po_ref, pa_ref, hidden_ref, share_ref, bounds_ref, q_ref, kv_ref, kvt_ref, do_ref, lse_ref, delta_ref,
    y_ref, dx_ref, dw_ref, shared_ref, din_ref, dout_ref,
    x_ref, w_ref, g1_ref, win_ref, wout_ref, in_sem,
    gain_tile, far_all, near_send_buf, near_all, pair_all, dq_all, dq_ref, dq_packed, dkv_own, pair_buf, us, ua, gs, ga, gqs, gqa, u_part, xat, pa, gh, ghq, w1, w2s, w2, w3,
    q_send, q_recv, pair_send, pair_recv, far_send, far_recv, near_send, near_recv,
    u_send, u_recv, g_send, g_recv, gh_send, gh_recv, w1_send, w1_recv, w2_send, w2_recv,
    w3_send, w3_recv, e_send, e_recv, gq_send, gq_recv, po_send, po_recv, ghq_send, ghq_recv,
    din_half, dout_half,
):
    head, blk, z, y = place()
    planes = blks // 2
    tokens, model = x_ref.shape
    rows = w_ref.shape[0]
    wanted = (
        (win_hbm, win_ref), (wout_hbm, wout_ref), (x_hbm, x_ref), (w_hbm, w_ref), (g1_hbm, g1_ref)
    )
    fetched = [
        pltpu.make_async_copy(src, dst, in_sem.at[i]) for i, (src, dst) in enumerate(wanted)
    ]
    for copy in fetched:
        copy.start()
    met = greet(
        [(around(head, k, heads), blk) for k in range(1, heads)]
        + [(head, around(blk, k, blks)) for k in range(1, blks)]
    )
    meet(met)

    def start(copies):
        for copy in copies:
            copy.start()

    def finish(copies):
        for copy in copies:
            copy.wait()

    other_y = around(y, 1, 2)
    pair = 2 * z + other_y
    above, below = z < planes - 1, z > 0
    directions = ((1, above, below, 0), (-1, below, above, 2))

    half_span = dkv_ref.shape[1] // 2

    def half_of(ref, half):
        return ref.at[pl.ds(half * half_span, half_span)]

    def far_copy(step, slot, side, half):
        span = 2 * (z + 2 * step) + side
        return remote(
            half_of(dkv_ref.at[span], half), half_of(far_all.at[slot + side], half),
            far_send.at[slot + side, half], far_recv.at[slot + side, half], head, 2 * (z + step) + y,
        )

    def near_copy(step, slot, side, half):
        return remote(
            half_of(near_send_buf.at[slot + side], half), half_of(near_all.at[slot // 2, y], half),
            near_send.at[slot + side, half], near_recv.at[slot // 2, y, half],
            head, 2 * (z + step) + side,
        )

    def two_away(step):
        return z + 2 * step < planes if step > 0 else z + 2 * step >= 0

    for half in range(2):
        for step, there, back, slot in directions:

            @pl.when(two_away(step))
            def _():
                for side in range(2):
                    far_copy(step, slot, side, half).start()

    w1_copies = [
        remote(
            grads_ref.at[:, around(head, k, heads)], w1.at[head],
            w1_send.at[k], w1_recv.at[k], around(head, k, heads), blk,
        )
        for k in range(1, heads)
    ]
    start(w1_copies)
    w1[head] = grads_ref[:, head]

    core = lax.rem(head, 2)
    sibling = head - core + 1 - core
    ff_half = wout_ref.shape[0] // 2
    ff_step = ff_half // 4

    def expert_chunk(chunk):
        here = pl.multiple_of(core * ff_half + chunk * ff_step, ff_step)
        there = pl.multiple_of(chunk * ff_step, ff_step)
        into = win_ref[:, pl.ds(here, ff_step)]
        outof = wout_ref[pl.ds(here, ff_step), :]
        d_in = jnp.zeros((model, ff_step), F32)
        d_out = jnp.zeros((ff_step, model), F32)
        for source in range(heads):
            rows_in = rx_ref[source, :, 0:model]
            grads_out = rx_ref[source, :, model : 2 * model]
            act, slope = gelu_parts(dot(rows_in, into))
            d_act = dot(grads_out, outof, (1, 1))
            d_in = d_in + dot(rows_in, (slope * d_act).astype(BF16), (0, 0))
            d_out = d_out + dot(act.astype(BF16), grads_out, (0, 0))
        din_ref[:, pl.ds(here, ff_step)] = d_in
        dout_ref[pl.ds(here, ff_step), :] = d_out
        din_half[core, :, pl.ds(there, ff_step)] = d_in.astype(BF16)
        dout_half[core, pl.ds(there, ff_step), :] = d_out.astype(BF16)

    key_tile = kv_ref.shape[1]
    for group in range(2 * key_tile // (CHAINS * QUERY_TILE)):
        tiles, queries = query_group(q_ref, group, y)
        known = (
            queries,
            group_grads(do_ref, tiles, y),
            [delta_ref[tile, 0:1, :] for tile in tiles],
            [lse_ref[tile, 0:1, :] for tile in tiles],
        )
        carry = tuple(begun_ref[tile] for tile in tiles)
        for side in range(2):
            first = pl.multiple_of((2 * z + side) * key_tile, key_tile)
            keys_across = kvt_ref[:, pl.ds(first, key_tile)]
            given, carry = attend_back(
                bounds_ref, tiles, first, kv_ref[2 * z + side], keys_across, known, carry
            )
            dkv_own[side] = given if group == 0 else dkv_own[side] + given
        for tile, total in zip(tiles, carry):
            at = tile * QUERY_TILE % key_tile
            dq_ref[tile * QUERY_TILE // key_tile, at : at + QUERY_TILE] = jnp.transpose(total)
    pair_buf[...] = dkv_own[other_y].astype(BF16)
    pair_copy = remote(pair_buf, pair_all, pair_send, pair_recv, head, pair)
    pair_copy.start()
    own_lanes = (lane_ids(dq_packed.shape) < HALF) == (y == 0)
    dq_packed[...] = halves(dq_ref[other_y], own_lanes).astype(BF16)
    q_copy = remote(dq_packed, dq_all, q_send, q_recv, head, pair)
    q_copy.start()
    for half in range(2):
        rows_here = slice(half * half_span, (half + 1) * half_span)
        for step, there, back, slot in directions:

            @pl.when(there)
            def _():
                for side in range(2):
                    near_send_buf[slot + side, rows_here] = dkv_ref[2 * (z + step) + side, rows_here]

            @pl.when(jnp.logical_and(there, back))
            def _():
                for side in range(2):
                    arrived(half_of(far_all.at[slot + side], half), far_recv.at[slot + side, half])
                    near_send_buf[slot + side, rows_here] = (
                        near_send_buf[slot + side, rows_here].astype(F32)
                        + far_all[slot + side, rows_here].astype(F32)
                    ).astype(BF16)

            @pl.when(there)
            def _():
                for side in range(2):
                    near_copy(step, slot, side, half).start()

    finish(fetched[:2])
    weight = wa_ref[...].reshape(model, 3 * LANES)
    for piece in range(heads):
        xat[:, piece * tokens : (piece + 1) * tokens] = jnp.transpose(xa_ref[piece])
    even = y == 0


    def wide_copies(part):
        some = pl.ds(part * ff_half // 2, ff_half // 2)
        ins = din_half.at[core, :, some]
        outs = dout_half.at[core, some]
        return [
            remote(ins, ins, e_send.at[part, 0], e_recv.at[part, 0], sibling, blk),
            remote(outs, outs, e_send.at[part, 1], e_recv.at[part, 1], sibling, blk),
        ]

    e_copies = [wide_copies(part) for part in range(2)]

    @pl.loop(0, 2)
    def _(chunk):
        expert_chunk(chunk)

    start(e_copies[0])
    q_copy.wait()
    landed = dq_all[...].astype(F32)
    landed = jnp.concatenate([landed, pltpu.roll(landed, HALF, 1)], axis=0)
    own_lanes = (lane_ids(landed.shape) < HALF) == even
    q_grads = jnp.where(own_lanes, dq_ref[y], landed).astype(BF16)
    gqs[...] = dot(xat[...], q_grads).astype(BF16).reshape(gqs.shape)
    gq_copies = [
        remote(
            gqs.at[around(blk, k, blks)], gqa.at[blk],
            gq_send.at[k], gq_recv.at[k], head, around(blk, k, blks),
        )
        for k in range(1, blks)
    ]
    start(gq_copies)
    gqa[blk] = gqs[blk]
    u_part[...] = dot(q_grads, weight[:, 2 * LANES : 3 * LANES], (1, 1)).reshape(u_part.shape)

    finish(w1_copies)
    summed = w1[0].astype(F32)
    for source in range(1, heads):
        summed = summed + w1[source].astype(F32)
    w2s[...] = summed.astype(BF16)
    w2_copies = [
        remote(
            w2s.at[around(blk, k, blks)], w2.at[blk],
            w2_send.at[k], w2_recv.at[k], head, around(blk, k, blks),
        )
        for k in range(1, blks)
    ]
    start(w2_copies)
    w2[blk] = w2s[blk]

    @pl.loop(2, 4)
    def _(chunk):
        expert_chunk(chunk)

    start(e_copies[1])

    pair_copy.wait()
    for step, there, back, slot in directions:

        @pl.when(back)
        def _():
            for side in range(2):
                for half in range(2):
                    arrived(
                        half_of(near_all.at[slot // 2, side], half),
                        near_recv.at[slot // 2, side, half],
                    )

        @pl.when(jnp.logical_not(back))
        def _():
            near_all[slot // 2] = jnp.zeros(near_all.shape[1:], BF16)

    own = dkv_own[y]
    other = pair_all[...].astype(F32)
    made = jnp.concatenate(
        [
            (
                jnp.where(even == (side == 0), own, other)
                + near_all[0, side].astype(F32)
                + near_all[1, side].astype(F32)
            ).astype(BF16)
            for side in range(2)
        ],
        axis=1,
    )
    gs[...] = dot(xat[...], made).astype(BF16).reshape(gs.shape)
    g_copies = [
        remote(
            gs.at[around(blk, k, blks)], ga.at[blk],
            g_send.at[k], g_recv.at[k], head, around(blk, k, blks),
        )
        for k in range(1, blks)
    ]
    start(g_copies)
    ga[blk] = gs[blk]
    us[...] = (
        u_part[...] + dot(made, weight[:, 0 : 2 * LANES], (1, 1)).reshape(us.shape)
    ).astype(BF16)
    u_copies = [
        remote(
            us.at[around(head, k, heads)], ua.at[head],
            u_send.at[k], u_recv.at[k], around(head, k, heads), blk,
        )
        for k in range(1, heads)
    ]
    start(u_copies)
    ua[head] = us[head]
    finish(fetched[2:])
    finish(gq_copies)
    total = gqa[0].astype(F32)
    for source in range(1, blks):
        total = total + gqa[source].astype(F32)
    ghq[head] = total.astype(BF16)
    ghq_copies = [
        remote(ghq.at[head], ghq.at[head], ghq_send.at[k], ghq_recv.at[k], around(head, k, heads), blk)
        for k in range(1, heads)
    ]
    start(ghq_copies)

    finish(w2_copies)
    part = w2[0].astype(F32)
    for source in range(1, blks):
        part = part + w2[source].astype(F32)
    w3[head] = part.astype(BF16)
    w3_copies = [
        remote(w3.at[head], w3.at[head], w3_send.at[k], w3_recv.at[k], around(head, k, heads), blk)
        for k in range(1, heads)
    ]
    start(w3_copies)

    xhat, scale = centre(x_ref[...].astype(F32))
    for part in range(2):
        finish(e_copies[part])
        size = ff_half // 2
        there = pl.multiple_of((1 - core) * ff_half + part * size, size)
        here = slice(part * size, (part + 1) * size)
        din_ref[:, pl.ds(there, size)] = din_half[1 - core, :, here].astype(F32)
        dout_ref[pl.ds(there, size), :] = dout_half[1 - core, here].astype(F32)
    finish(g_copies)
    total = ga[0].astype(F32)
    for source in range(1, blks):
        total = total + ga[source].astype(F32)
    gh[head] = total.astype(BF16)
    gh_copies = [
        remote(gh.at[head], gh.at[head], gh_send.at[k], gh_recv.at[k], around(head, k, heads), blk)
        for k in range(1, heads)
    ]
    start(gh_copies)
    half_slots = pa_ref.shape[1]
    po_copies = [
        remote(
            po_ref.at[around(blk, k, blks), pl.ds(half_slots, half_slots)], pa.at[blk],
            po_send.at[k], po_recv.at[k], head, around(blk, k, blks),
        )
        for k in range(1, blks)
    ]
    start(po_copies)
    pa[blk] = po_ref[blk, half_slots : 2 * half_slots]
    finish(u_copies)
    grad = ua[0].astype(F32)
    for source in range(1, heads):
        grad = grad + ua[source].astype(F32)
    dx_ref[...] = dh_ref[...] + centre_back(grad, xhat, scale)

    gain_tile[...] = jnp.zeros_like(gain_tile)
    gain_tile[0:1, 0:rows] = g1_ref[...].astype(F32)
    gain = jnp.transpose(jnp.broadcast_to(gain_tile[0:1, :], (LANES, LANES)))[:rows]
    low_half = lane_ids((rows, LANES)) < HALF
    finish(ghq_copies)
    finish(gh_copies)
    d_gain = jnp.zeros((rows, LANES), F32)
    for source in range(heads):
        both = [gh[source, :, i * LANES : (i + 1) * LANES].astype(F32) for i in range(2)]
        grads = (
            ghq[source].astype(F32) * HS ** (-0.5),
            jnp.where(low_half, both[0], both[1]),
            pltpu.roll(jnp.where(low_half, both[1], both[0]), HALF, 1),
        )
        for which, value in enumerate(grads):
            columns = slice(which * model + source * LANES, which * model + (source + 1) * LANES)
            d_gain = d_gain + value * w_ref[:, columns].astype(F32)
            dw_ref[:, columns] = value * gain
    finish(w3_copies)
    shared = w3[...].reshape(rows, w3.shape[-1]).astype(F32)
    shared_ref[:, 0:model] = shared[:, 0:model]
    gain_col = jnp.sum(d_gain, axis=1, keepdims=True)
    shared_ref[:, model : model + LANES] = jnp.where(
        lane_ids((rows, LANES)) == blks + 1, gain_col, shared[:, model : model + LANES]
    )
    finish(po_copies)
    parts = jnp.concatenate([pa_ref[...], pa[...]], axis=1).reshape(share_ref.shape[2], model)
    mixture = dot(share_ref[0], parts) + dot(share_ref[1], parts)
    y_ref[...] = (hidden_ref[...] + mixture).astype(BF16)

    for step, there, back, slot in directions:

        @pl.when(two_away(step))
        def _():
            for side in range(2):
                for half in range(2):
                    far_copy(step, slot, side, half).wait_send()

        @pl.when(there)
        def _():
            for side in range(2):
                for half in range(2):
                    near_copy(step, slot, side, half).wait_send()


def call_last(
    x, dh, dq, dkv, xa, wa, w_qkv, g1, grads, rx, win, wout, po, pa, hidden, share,
    bounds, q, kv, kvt, d_o, lse, delta, heads, blks,
):
    tokens, model = x.shape
    span = tokens * heads
    rows = w_qkv.shape[0]
    wide = model + LANES
    part = rows // heads
    ff = wout.shape[0]

    def block(*lead):
        return pltpu.VMEM((*lead, span, LANES), BF16)

    return pl.pallas_call(
        functools.partial(last_kernel, heads, blks),
        out_shape=(
            jax.ShapeDtypeStruct((tokens, model), BF16),
            jax.ShapeDtypeStruct((tokens, model), F32),
            jax.ShapeDtypeStruct((rows, 3 * model), F32),
            jax.ShapeDtypeStruct((rows, wide), F32),
            jax.ShapeDtypeStruct((model, ff), F32),
            jax.ShapeDtypeStruct((ff, model), F32),
        ),
        in_specs=hbm_specs(1) + vmem_specs(5) + hbm_specs(2) + vmem_specs(2) + hbm_specs(2) + vmem_specs(11),
        out_specs=tuple(vmem_specs(6)),
        scratch_shapes=[
            pltpu.VMEM((tokens, model), BF16),
            pltpu.VMEM((rows, 3 * model), BF16),
            pltpu.VMEM((1, rows), BF16),
            pltpu.VMEM(win.shape, BF16),
            pltpu.VMEM(wout.shape, BF16),
            dma(5),
            pltpu.VMEM((8, LANES), F32),
            block(4), block(4), block(2, 2), block(), pltpu.VMEM((span // 2, LANES), BF16),
            pltpu.VMEM((2, span, LANES), F32), pltpu.VMEM((span // 2, LANES), BF16),
            pltpu.VMEM((2, span, LANES), F32), block(),
            pltpu.VMEM((heads, tokens, model), BF16), pltpu.VMEM((heads, tokens, model), BF16),
            pltpu.VMEM((blks, rows, 2 * LANES), BF16), pltpu.VMEM((blks, rows, 2 * LANES), BF16),
            pltpu.VMEM((blks, rows, LANES), BF16), pltpu.VMEM((blks, rows, LANES), BF16),
            pltpu.VMEM((heads, tokens, model), F32), pltpu.VMEM((model, span), BF16),
            pltpu.VMEM(pa.shape, BF16),
            pltpu.VMEM((heads, rows, 2 * LANES), BF16), pltpu.VMEM((heads, rows, LANES), BF16),
            pltpu.VMEM((heads, blks, part, wide), BF16), pltpu.VMEM((blks, part, wide), BF16),
            pltpu.VMEM((blks, part, wide), BF16), pltpu.VMEM((heads, part, wide), BF16),
            pltpu.SemaphoreType.DMA, pltpu.SemaphoreType.DMA, pltpu.SemaphoreType.DMA, pltpu.SemaphoreType.DMA,
            dma(4, 2), dma(4, 2), dma(4, 2), dma(2, 2, 2),
            dma(heads), dma(heads), dma(blks), dma(blks), dma(heads), dma(heads), dma(heads), dma(heads),
            dma(blks), dma(blks), dma(heads), dma(heads), dma(2, 2), dma(2, 2), dma(blks), dma(blks), dma(blks), dma(blks), dma(heads), dma(heads),
            pltpu.VMEM((2, model, ff // 2), BF16), pltpu.VMEM((2, ff // 2, model), BF16),
        ],
        compiler_params=pltpu.CompilerParams(
            collective_id=3, has_side_effects=True, vmem_limit_bytes=36 * MIB
        ),
        name="last",
    )(
        *in_hbm(x), dh, dq, dkv, xa, wa, *in_hbm(w_qkv, g1.reshape(1, rows)),
        grads.reshape(blks, heads, part, wide), rx, *in_hbm(win, wout), po, pa, hidden, share,
        bounds, q, kv, kvt, d_o, lse, delta,
    )


def finish_kernel(
    experts,
    y_ref, dx_ref, dw_ref, shared_ref, din_ref, dout_ref,
    y_out, dx_out, g1_out, dw_out, dwo_out, g2_out, wr_out, din_out, dout_out,
    tile, wr, g2, g1, sem,
):
    rows = shared_ref.shape[0]
    model = dx_ref.shape[1]
    copies = [
        pltpu.make_async_copy(dx_ref, dx_out, sem.at[0]),
        pltpu.make_async_copy(dw_ref, dw_out, sem.at[1]),
        pltpu.make_async_copy(shared_ref.at[:, pl.ds(0, model)], dwo_out, sem.at[2]),
        pltpu.make_async_copy(y_ref, y_out, sem.at[6]),
        pltpu.make_async_copy(din_ref, din_out, sem.at[7]),
        pltpu.make_async_copy(dout_ref, dout_out, sem.at[8]),
    ]
    for copy in copies:
        copy.start()
    tile[...] = jnp.zeros_like(tile)
    tile[0:rows, :] = shared_ref[:, model : model + LANES]
    across = jnp.transpose(tile[...])[:, 0:rows]
    wr[...] = across[0:experts]
    g2[...] = across[experts : experts + 1]
    g1[...] = across[experts + 1 : experts + 2]
    for index, (src, dst) in enumerate(((wr, wr_out), (g2, g2_out), (g1, g1_out))):
        copies.append(pltpu.make_async_copy(src, dst, sem.at[3 + index]))
        copies[-1].start()
    for copy in copies:
        copy.wait()


def call_finish(output, dx, dw, shared, d_in, d_out):
    rows = shared.shape[0]
    model = dx.shape[1]
    experts = model // rows
    return pl.pallas_call(
        functools.partial(finish_kernel, experts),
        out_shape=(
            jax.ShapeDtypeStruct(output.shape, BF16),
            jax.ShapeDtypeStruct(dx.shape, F32),
            jax.ShapeDtypeStruct((1, rows), F32),
            jax.ShapeDtypeStruct(dw.shape, F32),
            jax.ShapeDtypeStruct((rows, model), F32),
            jax.ShapeDtypeStruct((1, rows), F32),
            jax.ShapeDtypeStruct((experts, rows), F32),
            jax.ShapeDtypeStruct(d_in.shape, F32),
            jax.ShapeDtypeStruct(d_out.shape, F32),
        ),
        in_specs=vmem_specs(6),
        out_specs=tuple(hbm_specs(9)),
        scratch_shapes=[
            pltpu.VMEM((LANES, LANES), F32),
            pltpu.VMEM((experts, rows), F32),
            pltpu.VMEM((1, rows), F32),
            pltpu.VMEM((1, rows), F32),
            dma(9),
        ],
        compiler_params=pltpu.CompilerParams(vmem_limit_bytes=16 * MIB),
        name="finish",
    )(output, dx, dw, shared, d_in, d_out)


def local_kernels(
    inputs, ln1_gain, w_qkv, w_out, ln2_gain, w_router,
    expert_in, expert_out, routes, priority, doc_lengths, d_out,
):
    heads, blks = lax.axis_size("head"), lax.axis_size("blk")
    model = inputs.shape[1]
    tokens = inputs.shape[0]
    win, wout = expert_in[0], expert_out[0]
    q, kv, xa, wa, wo, kvt, bounds, begun = call_qkv(
        inputs, w_qkv, ln1_gain, w_out, w_router, ln2_gain, doc_lengths, heads, blks
    )
    o, o_low, lse = call_forward(bounds, q, kv, kvt, begun)
    po, pa, hidden, share, dh, d_o, grads, rx = call_middle(
        inputs, o_low.reshape(2, heads, tokens // 2, LANES), wo.reshape(model, model + LANES),
        routes, priority, d_out, win, wout, heads, blks,
    )
    d_o = d_o.reshape(2 * heads * tokens // QUERY_TILE, -1, HALF, LANES)
    dq, dkv, delta = call_backward(bounds, q, kv, kvt, d_o, o, lse)
    ends = call_last(
        inputs, dh, dq, dkv, xa, wa, w_qkv, ln1_gain, grads, rx, win, wout,
        po, pa, hidden, share, bounds, q, kv, kvt, d_o, lse, delta, heads, blks,
    )
    output, d_inputs, d_gain_one, d_qkv, d_out_proj, d_gain_two, d_router, d_in, d_out_weight = call_finish(*ends)
    return (
        output,
        d_inputs,
        d_gain_one.reshape(-1),
        d_qkv,
        d_out_proj,
        d_gain_two.reshape(-1),
        d_router.T,
        d_in[None],
        d_out_weight[None],
    )


def solution(mesh):
    in_specs = (
        P(("blk", "head"), None),
        P("blk"),
        P("blk", None),
        P("blk", None),
        P("blk"),
        P("blk", None),
        P("blk", None, None),
        P("blk", None, None),
        P(("blk", "head"), None),
        P(("blk", "head"), None),
        P(),
        P(("blk", "head"), None),
    )
    out_specs = (
        P(("blk", "head"), None),
        P(("blk", "head"), None),
        P("blk"),
        P("blk", None),
        P("blk", None),
        P("blk"),
        P("blk", None),
        P("blk", None, None),
        P("blk", None, None),
    )
    fits = mesh.shape["head"] == 4 and mesh.shape["blk"] == 8
    body = local_kernels if fits else local
    return jax.shard_map(body, mesh=mesh, in_specs=in_specs, out_specs=out_specs, check_vma=False)
```

```python
import functools
import math

import jax
import jax.numpy as jnp
from jax import lax
from jax.experimental import pallas as pl
from jax.experimental.pallas import tpu as pltpu
from jax.sharding import PartitionSpec as P

HS = 64
KEY_BLOCK = 2048


PRECISE = lax.Precision.HIGHEST
MASKED = -1e30
EPSILON = 1e-06


def layer_norm(values, gain):
    average = jnp.mean(values, axis=-1, keepdims=True)
    centred = values - average
    spread = jnp.mean(centred * centred, axis=-1, keepdims=True)
    return centred * lax.rsqrt(spread + EPSILON) * gain


def gelu_exact(values):
    return jax.nn.gelu(values, approximate=False)


def router(row_block, weight):
    return jax.nn.softmax(jnp.dot(row_block, weight, precision=PRECISE), axis=-1)


def doc_index(positions, doc_lengths):
    places = jnp.arange(doc_lengths.shape[0], dtype=jnp.int32)
    starts = jnp.sum(jnp.where(places[None, :] < places[:, None], doc_lengths[None, :], 0), axis=1)
    at_most = (starts[None, :] <= positions[:, None]).astype(jnp.int32)
    return jnp.sum(at_most, axis=1) - 1


def slot_table(route_rows, ranking, capacity):
    token_count = route_rows.shape[0]
    expert = jnp.transpose(route_rows).reshape(-1)
    pair_order = (jnp.arange(2, dtype=jnp.int32)[:, None] * token_count + ranking[None, :]).reshape(
        -1
    )
    before = (expert[:, None] == expert[None, :]) & (pair_order[None, :] < pair_order[:, None])
    position = jnp.sum(before.astype(jnp.int32), axis=1)
    slot_ids = jnp.where(position < capacity, expert * capacity + position, -1)
    return slot_ids.reshape(2, token_count)


def keep_state(current):
    return current


def local(
    inputs,
    ln1_gain,
    w_qkv,
    w_out,
    ln2_gain,
    w_router,
    expert_in,
    expert_out,
    routes,
    priority,
    doc_lengths,
    d_out,
):
    blk_size = lax.axis_size("blk")
    tok_rows = inputs.shape[0]
    model_width = inputs.shape[1]
    capacity = 2 * tok_rows // blk_size
    slot_total = blk_size * capacity
    gain_one, qkv_weight, out_weight, gain_two, router_weight = (
        lax.all_gather(ln1_gain, "blk", axis=0, tiled=True),
        lax.all_gather(w_qkv, "blk", axis=0, tiled=True),
        lax.all_gather(w_out, "blk", axis=0, tiled=True),
        lax.all_gather(ln2_gain, "blk", axis=0, tiled=True),
        lax.all_gather(w_router, "blk", axis=0, tiled=True),
    )
    input_rows = inputs.astype(jnp.float32)
    normed_one, norm_one_pull = jax.vjp(layer_norm, input_rows, gain_one.astype(jnp.float32))
    normed_low = normed_one.astype(jnp.bfloat16)
    qkv_rows = jnp.dot(normed_low, qkv_weight, preferred_element_type=jnp.float32).astype(
        jnp.bfloat16
    )
    query_heads, key_heads, value_heads = (
        lax.all_to_all(qkv_rows[:, :model_width], "head", split_axis=1, concat_axis=0, tiled=True),
        lax.all_to_all(
            qkv_rows[:, model_width : 2 * model_width],
            "head",
            split_axis=1,
            concat_axis=0,
            tiled=True,
        ),
        lax.all_to_all(
            qkv_rows[:, 2 * model_width :], "head", split_axis=1, concat_axis=0, tiled=True
        ),
    )
    span_rows = query_heads.shape[0]
    head_count = query_heads.shape[1] // HS
    key_all, value_all = (
        lax.all_gather(key_heads, "blk", axis=0, tiled=True),
        lax.all_gather(value_heads, "blk", axis=0, tiled=True),
    )
    total_rows = key_all.shape[0]
    block_count = total_rows // KEY_BLOCK
    scale_factor = HS ** (-0.5)
    query_pos = lax.axis_index("blk") * span_rows + jnp.arange(span_rows, dtype=jnp.int32)
    query_docs = doc_index(query_pos, doc_lengths)
    queries = query_heads.reshape(span_rows, head_count, HS)

    def block_parts(block_index, key_source, value_source):
        first_key = block_index * KEY_BLOCK
        key_rows = lax.dynamic_slice_in_dim(key_source, first_key, KEY_BLOCK, 0).reshape(
            KEY_BLOCK, head_count, HS
        )
        value_rows = lax.dynamic_slice_in_dim(value_source, first_key, KEY_BLOCK, 0).reshape(
            KEY_BLOCK, head_count, HS
        )
        key_docs = doc_index(first_key + jnp.arange(KEY_BLOCK, dtype=jnp.int32), doc_lengths)
        is_live = (key_docs[0] <= query_docs[-1]) & (key_docs[-1] >= query_docs[0])
        same_doc = query_docs[:, None] == key_docs[None, :]
        return (first_key, key_rows, value_rows, same_doc, is_live)

    def block_scores(key_rows, same_doc):
        raw_scores = (
            jnp.einsum("qhd,khd->hqk", queries, key_rows, preferred_element_type=jnp.float32)
            * scale_factor
        )
        return jnp.where(same_doc[None], raw_scores, MASKED)

    def stat_step(block_index, loop_state):
        first_key, key_rows, value_rows, same_doc, is_live = block_parts(
            block_index, key_all, value_all
        )

        def stat_update(current):
            running_max, running_sum = current
            scores = block_scores(key_rows, same_doc)
            new_max = jnp.maximum(running_max, jnp.max(scores, axis=2))
            exp_terms = jnp.where(same_doc[None], jnp.exp(scores - new_max[:, :, None]), 0.0)
            return (
                new_max,
                running_sum * jnp.exp(running_max - new_max) + jnp.sum(exp_terms, axis=2),
            )

        return lax.cond(is_live, stat_update, keep_state, loop_state)

    start_state = (
        jnp.full((head_count, span_rows), MASKED, jnp.float32),
        jnp.zeros((head_count, span_rows), jnp.float32),
    )
    running_max, running_sum = lax.fori_loop(0, block_count, stat_step, start_state)
    log_total = running_max + jnp.log(running_sum)

    def out_step(block_index, loop_state):
        first_key, key_rows, value_rows, same_doc, is_live = block_parts(
            block_index, key_all, value_all
        )

        def out_update(current):
            scores = block_scores(key_rows, same_doc)
            weights = jnp.where(
                same_doc[None], jnp.exp(scores - log_total[:, :, None]), 0.0
            ).astype(jnp.bfloat16)
            return current + jnp.einsum(
                "hqk,khd->qhd", weights, value_rows, preferred_element_type=jnp.float32
            )

        return lax.cond(is_live, out_update, keep_state, loop_state)

    mixed_full = lax.fori_loop(
        0, block_count, out_step, jnp.zeros((span_rows, head_count, HS), jnp.float32)
    )
    mixed_low = mixed_full.reshape(span_rows, head_count * HS).astype(jnp.bfloat16)
    mixed_tokens = lax.all_to_all(mixed_low, "head", split_axis=0, concat_axis=1, tiled=True)
    attended = jnp.dot(mixed_tokens, out_weight, preferred_element_type=jnp.float32)
    hidden_one = input_rows + attended
    normed_two, norm_two_pull = jax.vjp(layer_norm, hidden_one, gain_two.astype(jnp.float32))
    routed_low = normed_two.astype(jnp.bfloat16)
    router_probs, router_pull = jax.vjp(
        router, routed_low.astype(jnp.float32), router_weight.astype(jnp.float32)
    )
    slot_ids = slot_table(routes, priority[0], capacity)
    select = (
        slot_ids[:, :, None] == jnp.arange(slot_total, dtype=jnp.int32)[None, None, :]
    ).astype(jnp.bfloat16)
    send_rows = jnp.einsum(
        "kts,td->sd", select, routed_low, preferred_element_type=jnp.float32
    ).astype(jnp.bfloat16)
    expert_rows = lax.all_to_all(
        send_rows.reshape(blk_size, capacity, model_width),
        "blk",
        split_axis=0,
        concat_axis=0,
        tiled=True,
    ).reshape(slot_total, model_width)
    weight_in = expert_in[0]
    weight_out = expert_out[0]
    pre_act = jnp.dot(expert_rows, weight_in, preferred_element_type=jnp.float32)
    hidden_act, gelu_pull = jax.vjp(gelu_exact, pre_act)
    hidden_low = hidden_act.astype(jnp.bfloat16)
    expert_result = jnp.dot(hidden_low, weight_out, preferred_element_type=jnp.float32).astype(
        jnp.bfloat16
    )
    slot_result = lax.all_to_all(
        expert_result.reshape(blk_size, capacity, model_width),
        "blk",
        split_axis=0,
        concat_axis=0,
        tiled=True,
    ).reshape(slot_total, model_width)
    pair_result = jnp.einsum("kts,sd->ktd", select, slot_result, preferred_element_type=jnp.float32)
    route_hot = (routes[:, :, None] == jnp.arange(blk_size, dtype=jnp.int32)[None, None, :]).astype(
        jnp.float32
    )
    gate_vals = jnp.sum(router_probs[:, None, :] * route_hot, axis=2)
    mixture = gate_vals[:, 0, None] * pair_result[0] + gate_vals[:, 1, None] * pair_result[1]
    output = (hidden_one + mixture).astype(jnp.bfloat16)
    d_gates = jnp.transpose(jnp.sum(d_out[None] * pair_result, axis=2))
    d_probs = jnp.sum(d_gates[:, :, None] * route_hot, axis=1)
    pair_grads = (jnp.transpose(gate_vals)[:, :, None] * d_out[None]).astype(jnp.bfloat16)
    slot_grads = jnp.einsum(
        "kts,ktd->sd", select, pair_grads, preferred_element_type=jnp.float32
    ).astype(jnp.bfloat16)
    result_grads = lax.all_to_all(
        slot_grads.reshape(blk_size, capacity, model_width),
        "blk",
        split_axis=0,
        concat_axis=0,
        tiled=True,
    ).reshape(slot_total, model_width)
    d_hidden_act = jnp.dot(result_grads, weight_out.T, preferred_element_type=jnp.float32)
    d_weight_out = jnp.dot(hidden_low.T, result_grads, preferred_element_type=jnp.float32)
    d_preact = gelu_pull(d_hidden_act)[0].astype(jnp.bfloat16)
    d_weight_in = jnp.dot(expert_rows.T, d_preact, preferred_element_type=jnp.float32)
    row_grads = jnp.dot(d_preact, weight_in.T, preferred_element_type=jnp.float32).astype(
        jnp.bfloat16
    )
    slot_back = lax.all_to_all(
        row_grads.reshape(blk_size, capacity, model_width),
        "blk",
        split_axis=0,
        concat_axis=0,
        tiled=True,
    ).reshape(slot_total, model_width)
    d_routed = jnp.einsum("kts,sd->td", select, slot_back, preferred_element_type=jnp.float32)
    d_routed_router, d_router = router_pull(d_probs)
    d_hidden_norm, d_gain_two = norm_two_pull(d_routed + d_routed_router)
    d_hidden_one = d_out + d_hidden_norm
    attn_grads = d_hidden_one.astype(jnp.bfloat16)
    d_out_weight = jnp.dot(mixed_tokens.T, attn_grads, preferred_element_type=jnp.float32)
    mixed_grads = jnp.dot(attn_grads, out_weight.T, preferred_element_type=jnp.float32).astype(
        jnp.bfloat16
    )
    head_grads = lax.all_to_all(mixed_grads, "head", split_axis=1, concat_axis=0, tiled=True)
    out_grads = head_grads.reshape(span_rows, head_count, HS)
    row_delta = jnp.transpose(jnp.sum(out_grads.astype(jnp.float32) * mixed_full, axis=2))
    key_back, value_back = (
        lax.all_gather(key_heads, "blk", axis=0, tiled=True),
        lax.all_gather(value_heads, "blk", axis=0, tiled=True),
    )

    def grad_step(block_index, loop_state):
        first_key, key_rows, value_rows, same_doc, is_live = block_parts(
            block_index, key_back, value_back
        )

        def grad_update(current):
            query_grad, key_grad, value_grad = current
            scores = block_scores(key_rows, same_doc)
            weights = jnp.where(same_doc[None], jnp.exp(scores - log_total[:, :, None]), 0.0)
            value_part = jnp.einsum(
                "hqk,qhd->khd",
                weights.astype(jnp.bfloat16),
                out_grads,
                preferred_element_type=jnp.float32,
            )
            weight_grads = jnp.einsum(
                "qhd,khd->hqk", out_grads, value_rows, preferred_element_type=jnp.float32
            )
            score_grads = (weights * (weight_grads - row_delta[:, :, None])).astype(jnp.bfloat16)
            query_grad = (
                query_grad
                + jnp.einsum(
                    "hqk,khd->qhd", score_grads, key_rows, preferred_element_type=jnp.float32
                )
                * scale_factor
            )
            key_part = (
                jnp.einsum("hqk,qhd->khd", score_grads, queries, preferred_element_type=jnp.float32)
                * scale_factor
            )
            key_grad = lax.dynamic_update_slice_in_dim(
                key_grad, key_part.reshape(KEY_BLOCK, head_count * HS), first_key, 0
            )
            value_grad = lax.dynamic_update_slice_in_dim(
                value_grad, value_part.reshape(KEY_BLOCK, head_count * HS), first_key, 0
            )
            return (query_grad, key_grad, value_grad)

        return lax.cond(is_live, grad_update, keep_state, loop_state)

    start_grads = (
        jnp.zeros((span_rows, head_count, HS), jnp.float32),
        jnp.zeros((total_rows, head_count * HS), jnp.float32),
        jnp.zeros((total_rows, head_count * HS), jnp.float32),
    )
    query_grad, key_grad, value_grad = lax.fori_loop(0, block_count, grad_step, start_grads)
    key_own, value_own = (
        lax.psum_scatter(
            key_grad.astype(jnp.bfloat16), "blk", scatter_dimension=0, tiled=True
        ).astype(jnp.float32),
        lax.psum_scatter(
            value_grad.astype(jnp.bfloat16), "blk", scatter_dimension=0, tiled=True
        ).astype(jnp.float32),
    )
    query_tokens_grad, key_tokens_grad, value_tokens_grad = (
        lax.all_to_all(
            query_grad.reshape(span_rows, head_count * HS).astype(jnp.bfloat16),
            "head",
            split_axis=0,
            concat_axis=1,
            tiled=True,
        ),
        lax.all_to_all(
            key_own.astype(jnp.bfloat16), "head", split_axis=0, concat_axis=1, tiled=True
        ),
        lax.all_to_all(
            value_own.astype(jnp.bfloat16), "head", split_axis=0, concat_axis=1, tiled=True
        ),
    )
    qkv_grads = jnp.concatenate([query_tokens_grad, key_tokens_grad, value_tokens_grad], axis=1)
    d_qkv_weight = jnp.dot(normed_low.T, qkv_grads, preferred_element_type=jnp.float32)
    normed_grads = jnp.dot(qkv_grads, qkv_weight.T, preferred_element_type=jnp.float32)
    d_inputs_norm, d_gain_one = norm_one_pull(normed_grads)
    d_inputs = d_hidden_one + d_inputs_norm
    gain_one_sum, qkv_sum, out_sum, gain_two_sum, router_sum = (
        lax.psum_scatter(
            d_gain_one.astype(jnp.bfloat16), "blk", scatter_dimension=0, tiled=True
        ).astype(jnp.float32),
        lax.psum_scatter(
            d_qkv_weight.astype(jnp.bfloat16), "blk", scatter_dimension=0, tiled=True
        ).astype(jnp.float32),
        lax.psum_scatter(
            d_out_weight.astype(jnp.bfloat16), "blk", scatter_dimension=0, tiled=True
        ).astype(jnp.float32),
        lax.psum_scatter(
            d_gain_two.astype(jnp.bfloat16), "blk", scatter_dimension=0, tiled=True
        ).astype(jnp.float32),
        lax.psum_scatter(
            d_router.astype(jnp.bfloat16), "blk", scatter_dimension=0, tiled=True
        ).astype(jnp.float32),
    )
    gain_one_all, qkv_all, out_all, gain_two_all, router_all, expert_in_all, expert_out_all = (
        lax.psum(gain_one_sum.astype(jnp.bfloat16), "head").astype(jnp.float32),
        lax.psum(qkv_sum.astype(jnp.bfloat16), "head").astype(jnp.float32),
        lax.psum(out_sum.astype(jnp.bfloat16), "head").astype(jnp.float32),
        lax.psum(gain_two_sum.astype(jnp.bfloat16), "head").astype(jnp.float32),
        lax.psum(router_sum.astype(jnp.bfloat16), "head").astype(jnp.float32),
        lax.psum(d_weight_in[None].astype(jnp.bfloat16), "head").astype(jnp.float32),
        lax.psum(d_weight_out[None].astype(jnp.bfloat16), "head").astype(jnp.float32),
    )
    return (
        output,
        d_inputs,
        gain_one_all,
        qkv_all,
        out_all,
        gain_two_all,
        router_all,
        expert_in_all,
        expert_out_all,
    )


MESH = pl.DeviceIdType.MESH
LANES = 128
HALF = LANES // 2
MIB = 2**20
F32 = jnp.float32
BF16 = jnp.bfloat16


def dot(left, right, dims=(1, 0)):
    return lax.dot_general(
        left, right, (((dims[0],), (dims[1],)), ((), ())), preferred_element_type=F32
    )


def remote(src, dst, send_sem, recv_sem, head, blk):
    return pltpu.make_async_remote_copy(
        src_ref=src,
        dst_ref=dst,
        send_sem=send_sem,
        recv_sem=recv_sem,
        device_id={"head": head, "blk": blk},
        device_id_type=MESH,
    )


def arrived(ref, sem):
    pltpu.make_async_copy(ref, ref, sem).wait()


def greet(peers):
    barrier = pltpu.get_barrier_semaphore()
    for head, blk in peers:
        pl.semaphore_signal(
            barrier, inc=1, device_id={"head": head, "blk": blk}, device_id_type=MESH
        )
    return len(peers)


def meet(count):
    pl.semaphore_wait(pltpu.get_barrier_semaphore(), count)


def halves(values, lanes_kept):
    rows = values.shape[0] // 2
    moved = pltpu.roll(values[rows:], HALF, 1)
    return jnp.where(lanes_kept, values[:rows], moved)


def lane_ids(shape):
    return lax.broadcasted_iota(jnp.int32, shape, len(shape) - 1)


def centre(values):
    average = jnp.mean(values, axis=-1, keepdims=True)
    centred = values - average
    spread = jnp.mean(centred * centred, axis=-1, keepdims=True)
    scale = lax.rsqrt(spread + EPSILON)
    return centred * scale, scale


def centre_back(grad, xhat, scale):
    middle = jnp.mean(grad, axis=-1, keepdims=True)
    along = jnp.mean(grad * xhat, axis=-1, keepdims=True)
    return (grad - middle - xhat * along) * scale


def split_high_low(column, lanes):
    high = column.astype(BF16)
    low = (column - high.astype(F32)).astype(BF16)
    return jnp.where(lanes < HALF, high.astype(F32), low.astype(F32)).astype(BF16)


def join_high_low(matrix, start):
    return matrix[:, start : start + 1].astype(F32) + matrix[
        :, start + HALF : start + HALF + 1
    ].astype(F32)


def place():
    head, blk = lax.axis_index("head"), lax.axis_index("blk")
    return head, blk, blk // 2, lax.rem(blk, 2)


def around(index, step, size):
    return lax.rem(index + step, size)


QUERY_TILE = 256
CHAINS = 2


def masked_queries(q_ref, tile, key_lanes, query_tile):
    tiles_per_span = q_ref.shape[1] // query_tile
    inner = tile % tiles_per_span * query_tile
    query = q_ref[tile // tiles_per_span, inner : inner + query_tile, :]
    return jnp.where(key_lanes, query, jnp.zeros_like(query))


def group_blocks(bounds_ref, group, size, key_tile):
    first, last = group * size, (group + 1) * size
    low = jnp.min(bounds_ref[0:1, first : first + LANES])
    high = jnp.max(bounds_ref[1:2, last - LANES : last])
    return low // key_tile, (high + key_tile - 1) // key_tile


def inside_document(bounds_ref, tile, first, shape):
    key = first + lax.broadcasted_iota(jnp.int32, shape, 0)
    columns = slice(tile * shape[1], (tile + 1) * shape[1])
    return jnp.logical_and(key >= bounds_ref[0:1, columns], key < bounds_ref[1:2, columns])


def query_group(q_ref, group, y):
    key_lanes = (lane_ids((QUERY_TILE, LANES)) < HALF) == (y == 0)
    tiles = range(group * CHAINS, (group + 1) * CHAINS)
    return tiles, [masked_queries(q_ref, tile, key_lanes, QUERY_TILE) for tile in tiles]


def attend(bounds_ref, tiles, first, keys, keys_across, queries, carry):
    scores = [dot(keys, query, (1, 1)) for query in queries]
    made = []
    for tile, score, (biggest, weight, mixed) in zip(tiles, scores, carry):
        inside = inside_document(bounds_ref, tile, first, score.shape)
        score = jnp.where(inside, score, MASKED)
        bigger = jnp.maximum(biggest, jnp.max(score, axis=0, keepdims=True))
        fade = jnp.exp(biggest - bigger)
        terms = jnp.exp(score - bigger)
        weight = weight * fade + jnp.sum(terms, axis=0, keepdims=True)
        made.append((bigger, weight, mixed * fade + dot(keys_across, terms.astype(BF16))))
    return tuple(made)


def nothing_attended():
    return (
        jnp.full((1, QUERY_TILE), MASKED, F32),
        jnp.zeros((1, QUERY_TILE), F32),
        jnp.zeros((LANES, QUERY_TILE), F32),
    )


def attend_back(bounds_ref, tiles, first, keys, keys_across, group, carry):
    queries, out_grads, deltas, log_totals = group
    scores = [dot(keys, query, (1, 1)) for query in queries]
    weight_grads = [dot(keys, out_grad, (1, 1)) for out_grad in out_grads]
    pieces, score_grads = [], []
    for i, tile in enumerate(tiles):
        inside = inside_document(bounds_ref, tile, first, scores[i].shape)
        weights = jnp.exp(jnp.where(inside, scores[i], MASKED) - log_totals[i])
        score_grads.append((weights * (weight_grads[i] - deltas[i])).astype(BF16))
        pieces.append(weights.astype(BF16))
    wide = jnp.concatenate(score_grads + pieces, axis=1)
    given = dot(wide, jnp.concatenate(queries + out_grads, axis=0))
    return given, tuple(c + dot(keys_across, g) for c, g in zip(carry, score_grads))


def group_grads(do_ref, tiles, y):
    key_lanes = (lane_ids((QUERY_TILE, LANES)) < HALF) == (y == 0)
    out_grads = []
    for tile in tiles:
        parts = []
        for part in range(QUERY_TILE // LANES):
            packed = do_ref[tile, part].astype(F32)
            parts += [packed, pltpu.roll(packed, HALF, 1)]
        out_grads.append(jnp.where(key_lanes, 0.0, jnp.concatenate(parts, axis=0)).astype(BF16))
    return out_grads


def qkv_kernel(
    heads, blks,
    x_hbm, w_hbm, g1_hbm, wo_hbm, wr_hbm, g2_hbm, docs_hbm,
    qall, kvall, xall, wall, wo_all, kvt, bounds, begun,
    x_ref, w_ref, rows_in, g1_ref, g2_ref, wr_ref, docs_ref, wo_own, kv_other, q_packed, q_landed, in_sem,
    x_send, x_recv, w_send, w_recv, o_send, o_recv, p_send, p_recv,
    k_send, k_recv, q_recv,
):
    head, blk, z, y = place()
    planes = blks // 2
    model = x_ref.shape[1]
    rows = w_ref.shape[0]
    part = rows // heads
    experts = wr_ref.shape[0]
    wanted = (
        (w_hbm, w_ref), (g1_hbm, g1_ref), (g2_hbm, g2_ref), (wr_hbm, wr_ref), (x_hbm, x_ref),
        (wo_hbm, wo_own.at[:, pl.ds(0, model)]), (docs_hbm, docs_ref),
    )
    fetched = [
        pltpu.make_async_copy(src, dst, in_sem.at[i]) for i, (src, dst) in enumerate(wanted)
    ]
    for copy in fetched:
        copy.start()
    rows_in[...] = jnp.zeros_like(rows_in)
    met = greet(
        [(around(head, k, heads), blk) for k in range(1, heads)]
        + [(head, around(blk, k, blks)) for k in range(1, blks)]
    )
    lanes = lane_ids((rows, LANES))
    for copy in fetched:
        copy.wait()
    rows_in[0:experts, 0:rows] = wr_ref[...].astype(F32)
    rows_in[experts : experts + 1, 0:rows] = g2_ref[...].astype(F32)
    rows_in[experts + 1 : experts + 2, 0:rows] = g1_ref[...].astype(F32)
    vectors = jnp.transpose(rows_in[...])[:rows]
    gain = vectors[:, experts + 1 : experts + 2]

    def columns(which):
        start = pl.multiple_of(which * model + head * LANES, LANES)
        return w_ref[:, pl.ds(start, LANES)].astype(F32) * gain

    key_cols = columns(1)
    value_cols = pltpu.roll(columns(2), HALF, 1)
    wall[blk, :, 0:LANES] = jnp.where(lanes < HALF, key_cols, value_cols).astype(BF16)
    wall[blk, :, LANES : 2 * LANES] = jnp.where(lanes < HALF, value_cols, key_cols).astype(BF16)
    wall[blk, :, 2 * LANES : 3 * LANES] = (columns(0) * HS ** (-0.5)).astype(BF16)
    def slice_copy(slot, source, target):
        ref = wall.at[source]
        return remote(ref, ref, w_send.at[slot], w_recv.at[source], head, target)

    pair = 2 * z + around(y, 1, 2)
    line = [2 * around(z, step, planes) + y for step in (1, planes - 1, *range(2, planes - 1))]
    w_copies = [slice_copy(slot, blk, target) for slot, target in enumerate((*line, pair))]
    w_onward = [slice_copy(planes + slot, source, pair) for slot, source in enumerate(line)]
    xhat, _ = centre(x_ref[...].astype(F32))
    xall[head] = xhat.astype(BF16)
    meet(met)
    for copy in w_copies:
        copy.start()
    x_copies = [
        remote(xall.at[head], xall.at[head], x_send.at[k], x_recv.at[k], around(head, k, heads), blk)
        for k in range(1, heads)
    ]
    for copy in x_copies:
        copy.start()
    wo_own[:, model : model + LANES] = vectors.astype(BF16)
    wo_all[blk, head] = wo_own[pl.ds(pl.multiple_of(head * part, part), part), :]
    o_copies = [
        remote(
            wo_all.at[blk, head], wo_all.at[blk, head],
            o_send.at[k], o_recv.at[k], head, around(blk, k, blks),
        )
        for k in range(1, blks)
    ]
    document_bounds(docs_ref, bounds, z)
    for source, copy in zip(line, w_onward):
        arrived(wall.at[source], w_recv.at[source])
        copy.start()
    for copy in o_copies:
        copy.start()
    for source in (pair, *[other - y + around(y, 1, 2) for other in line]):
        arrived(wall.at[source], w_recv.at[source])
    for copy in w_copies + w_onward:
        copy.wait_send()
    for copy in x_copies:
        copy.wait()
    weight = wall[...].reshape(model, 3 * LANES)
    tokens = x_ref.shape[0]
    even = y == 0
    above, below = z < planes - 1, z > 0
    half_span = kvall.shape[1] // 2
    sides = ((1, above, below, 0), (-1, below, above, 4))

    def half_of(ref, half):
        return ref.at[pl.ds(half * half_span, half_span)]

    def outward(slot, step, across, half):
        target = 2 * (z + step) + around(y, across, 2)
        return remote(
            half_of(kv_other if across else kvall.at[blk], half), half_of(kvall.at[blk], half),
            k_send.at[slot], k_recv.at[blk, half], head, target,
        )

    def onward(slot, step, side, half):
        from_span = 2 * (z - step) + side
        ref = half_of(kvall.at[from_span], half)
        return remote(ref, ref, k_send.at[slot], k_recv.at[from_span, half], head, 2 * (z + step) + y)

    def await_half(span, half):
        arrived(half_of(kvall.at[span], half), k_recv.at[span, half])

    def turn(span):
        size = kvall.shape[1]
        kvt[:, pl.ds(pl.multiple_of(span * size, size), size)] = jnp.transpose(kvall[span])

    for half in range(2):
        for piece in range(half * heads // 2, (half + 1) * heads // 2):
            made = dot(xall[piece], weight).astype(BF16)
            first, second = made[:, 0:LANES], made[:, LANES : 2 * LANES]
            span = slice(piece * tokens, (piece + 1) * tokens)
            kvall[blk, span, :] = jnp.where(even, first, second)
            kv_other[span, :] = jnp.where(even, second, first)
            qall[y, span, :] = made[:, 2 * LANES : 3 * LANES]
        outward(8 + half, 0, 1, half).start()
        for step, there, _, slot in sides:

            @pl.when(there)
            def _():
                outward(slot + 2 * half, step, 0, half).start()
                outward(slot + 2 * half + 1, step, 1, half).start()

    other_y = around(y, 1, 2)
    kept = (lane_ids(q_packed.shape) < HALF) == (y == 1)
    q_packed[...] = halves(qall[y].astype(F32), kept).astype(BF16)
    q_pair = remote(q_packed, q_landed, k_send.at[10], q_recv, head, 2 * z + other_y)
    q_pair.start()
    turn(blk)
    for copy in o_copies:
        copy.wait()
    core = lax.rem(head, 2)
    sibling, across = head - core + 1 - core, around(head, 2, heads)

    def quarter_copy(index, quarter, to_head):
        ref = wo_all.at[:, quarter]
        return remote(ref, ref, p_send.at[index], p_recv.at[index], to_head, blk)

    p_copies = [quarter_copy(0, head, sibling), quarter_copy(1, head, across)]
    for copy in p_copies:
        copy.start()
    p_copies.append(quarter_copy(2, across, sibling))
    for half in range(2):
        for step, there, back, slot in sides:

            @pl.when(back)
            def _():
                for side in range(2):
                    await_half(2 * (z - step) + side, half)

            @pl.when(jnp.logical_and(there, back))
            def _():
                for side in range(2):
                    onward(11 + slot + 2 * half + side, step, side, half).start()

    arrived(wo_all.at[:, across], p_recv.at[1])
    p_copies[2].start()
    for half in range(2):
        await_half(pair, half)
    turn(pair)
    q_pair.wait()
    landed = q_landed[...]
    qall[other_y, 0:half_span, :] = landed
    qall[other_y, half_span : 2 * half_span, :] = pltpu.roll(landed.astype(F32), HALF, 1).astype(BF16)
    key_tile = kvall.shape[1]
    for group in range(2 * key_tile // (CHAINS * QUERY_TILE)):
        tiles, queries = query_group(qall, group, y)
        carry = (nothing_attended(),) * CHAINS
        for side in range(2):
            first = pl.multiple_of((2 * z + side) * key_tile, key_tile)
            keys_across = kvt[:, pl.ds(first, key_tile)]
            carry = attend(bounds, tiles, first, kvall[2 * z + side], keys_across, queries, carry)
        for tile, (biggest, weight, mixed) in zip(tiles, carry):
            begun[tile, 0:LANES] = mixed
            begun[tile, LANES : LANES + 8] = jnp.broadcast_to(biggest, (8, QUERY_TILE))
            begun[tile, LANES + 8 : LANES + 16] = jnp.broadcast_to(weight, (8, QUERY_TILE))
    for step, there, back, slot in sides:

        @pl.when(back)
        def _():
            for side in range(2):
                turn(2 * (z - step) + side)

    for other in range(planes):
        for side in range(2):
            span = 2 * other + side

            @pl.when(jnp.logical_or(z - other == 2, other - z == 2))
            def _():
                for half in range(2):
                    await_half(span, half)
                turn(span)

    for index, quarter in ((0, sibling), (2, around(sibling, 2, heads))):
        arrived(wo_all.at[:, quarter], p_recv.at[index])
    for copy in p_copies:
        copy.wait_send()
    for half in range(2):
        outward(8 + half, 0, 1, half).wait_send()
        for step, there, back, slot in sides:

            @pl.when(there)
            def _():
                outward(slot + 2 * half, step, 0, half).wait_send()
                outward(slot + 2 * half + 1, step, 1, half).wait_send()

            @pl.when(jnp.logical_and(there, back))
            def _():
                for side in range(2):
                    onward(11 + slot + 2 * half + side, step, side, half).wait_send()


def document_bounds(docs_ref, bounds, z):
    count = docs_ref.shape[1]
    lengths = docs_ref[...].astype(F32)
    doc = lax.broadcasted_iota(jnp.int32, (count, count), 0)
    other = lane_ids((count, count))
    start = jnp.sum(jnp.where(other < doc, lengths, 0.0), axis=1, keepdims=True)
    end = jnp.sum(jnp.where(other <= doc, lengths, 0.0), axis=1, keepdims=True)
    queries = bounds.shape[1]
    token = (z * queries + lane_ids((count, queries))).astype(F32)
    begun = start <= token
    bounds[...] = jnp.zeros_like(bounds)
    bounds[0:1, :] = jnp.max(jnp.where(begun, start, 0.0), axis=0, keepdims=True).astype(jnp.int32)
    bounds[1:2, :] = jnp.max(jnp.where(begun, end, 0.0), axis=0, keepdims=True).astype(jnp.int32)


def vmem_specs(count):
    return [pl.BlockSpec(memory_space=pltpu.VMEM)] * count


def hbm_specs(count):
    return [pl.BlockSpec(memory_space=pltpu.HBM)] * count


def in_hbm(*arrays):
    return [pltpu.with_memory_space_constraint(array, pltpu.HBM) for array in arrays]


def dma(*shape):
    return pltpu.SemaphoreType.DMA(shape)


def call_qkv(x, w_qkv, g1, w_out, w_router, g2, doc_lengths, heads, blks):
    tokens, model = x.shape
    rows = w_qkv.shape[0]
    span = tokens * heads
    wide = model + LANES
    part = rows // heads
    return pl.pallas_call(
        functools.partial(qkv_kernel, heads, blks),
        out_shape=(
            jax.ShapeDtypeStruct((2, span, LANES), BF16),
            jax.ShapeDtypeStruct((blks, span, LANES), BF16),
            jax.ShapeDtypeStruct((heads, tokens, model), BF16),
            jax.ShapeDtypeStruct((blks, rows, 3 * LANES), BF16),
            jax.ShapeDtypeStruct((blks, heads, part, wide), BF16),
            jax.ShapeDtypeStruct((LANES, blks * span), BF16),
            jax.ShapeDtypeStruct((8, 2 * span), jnp.int32),
            jax.ShapeDtypeStruct((2 * span // QUERY_TILE, LANES + 16, QUERY_TILE), F32),
        ),
        in_specs=hbm_specs(7),
        out_specs=tuple(vmem_specs(8)),
        scratch_shapes=[
            pltpu.VMEM((tokens, model), BF16),
            pltpu.VMEM((rows, 3 * model), BF16),
            pltpu.VMEM((LANES, LANES), F32),
            pltpu.VMEM((1, rows), BF16),
            pltpu.VMEM((1, rows), BF16),
            pltpu.VMEM((w_router.shape[1], rows), BF16),
            pltpu.VMEM((1, doc_lengths.shape[0]), jnp.int32),
            pltpu.VMEM((rows, wide), BF16),
            pltpu.VMEM((span, LANES), BF16),
            pltpu.VMEM((span // 2, LANES), BF16),
            pltpu.VMEM((span // 2, LANES), BF16),
            dma(7),
            dma(heads), dma(heads), dma(blks), dma(blks), dma(blks), dma(blks), dma(heads), dma(heads),
            dma(19), dma(blks, 2), pltpu.SemaphoreType.DMA,
        ],
        compiler_params=pltpu.CompilerParams(
            collective_id=1, has_side_effects=True, vmem_limit_bytes=16 * MIB
        ),
        name="qkv",
    )(
        *in_hbm(
            x, w_qkv, g1.reshape(1, rows), w_out, w_router.T, g2.reshape(1, rows),
            doc_lengths.reshape(1, -1),
        )
    )


def other_blocks(bounds_ref, group, key_tile, z, step, carry):
    low, high = group_blocks(bounds_ref, group, CHAINS * QUERY_TILE, key_tile)
    carry = lax.fori_loop(low, 2 * z, step, carry)
    return lax.fori_loop(2 * z + 2, high, step, carry)


def forward_kernel(bounds_ref, q_ref, kv_ref, kvt_ref, begun_ref, o_out, ob_out, lse_out):
    _, _, z, y = place()
    key_tile = kv_ref.shape[1]
    value_lanes = (lane_ids((HALF, LANES)) < HALF) == (y == 1)
    for group in range(q_ref.shape[0] * q_ref.shape[1] // (CHAINS * QUERY_TILE)):
        tiles, queries = query_group(q_ref, group, y)

        def step(block, carry, queries=queries, tiles=tiles):
            first = pl.multiple_of(block * key_tile, key_tile)
            across = kvt_ref[:, pl.ds(first, key_tile)]
            return attend(bounds_ref, tiles, first, kv_ref[block], across, queries, carry)

        start = tuple(
            (begun_ref[t, LANES : LANES + 1], begun_ref[t, LANES + 8 : LANES + 9], begun_ref[t, 0:LANES])
            for t in tiles
        )
        ends = other_blocks(bounds_ref, group, key_tile, z, step, start)
        for tile, (biggest, weight, mixed) in zip(tiles, ends):
            result = jnp.transpose(mixed / weight)
            o_out[tile] = result
            for part in range(QUERY_TILE // LANES):
                block = result[part * LANES : (part + 1) * LANES]
                ob_out[tile, part] = halves(block, value_lanes).astype(BF16)
            lse_out[tile] = jnp.broadcast_to(biggest + jnp.log(weight), (8, QUERY_TILE))


def call_forward(bounds, q, kv, kvt, begun):
    blks, span, _ = kv.shape
    tiles = 2 * span // QUERY_TILE
    return pl.pallas_call(
        forward_kernel,
        out_shape=(
            jax.ShapeDtypeStruct((tiles, QUERY_TILE, LANES), F32),
            jax.ShapeDtypeStruct((tiles, QUERY_TILE // LANES, HALF, LANES), BF16),
            jax.ShapeDtypeStruct((tiles, 8, QUERY_TILE), F32),
        ),
        in_specs=vmem_specs(5),
        out_specs=tuple(vmem_specs(3)),
        compiler_params=pltpu.CompilerParams(vmem_limit_bytes=16 * MIB),
        name="attend",
    )(bounds, q, kv, kvt, begun)


def backward_kernel(
    bounds_ref, q_ref, kv_ref, kvt_ref, do_ref, o_ref, lse_ref, dq_out, dkv_out, delta_out, dkv
):
    _, _, z, y = place()
    key_tile = kv_ref.shape[1]
    dkv[...] = jnp.zeros_like(dkv)
    for group in range(q_ref.shape[0] * q_ref.shape[1] // (CHAINS * QUERY_TILE)):
        tiles, queries = query_group(q_ref, group, y)
        out_grads = group_grads(do_ref, tiles, y)
        deltas, log_totals = [], []
        for tile, out_grad in zip(tiles, out_grads):
            product = jnp.transpose(out_grad.astype(F32) * o_ref[tile])
            deltas.append(jnp.sum(product, axis=0, keepdims=True))
            delta_out[tile] = jnp.broadcast_to(deltas[-1], delta_out.shape[1:])
            log_totals.append(lse_ref[tile, 0:1, :])
        known = (queries, out_grads, deltas, log_totals)

        def step(block, carry, tiles=tiles, known=known):
            first = pl.multiple_of(block * key_tile, key_tile)
            across = kvt_ref[:, pl.ds(first, key_tile)]
            given, carry = attend_back(bounds_ref, tiles, first, kv_ref[block], across, known, carry)
            dkv[block] += given
            return carry

        zero = jnp.zeros((LANES, QUERY_TILE), F32)
        ends = other_blocks(bounds_ref, group, key_tile, z, step, (zero,) * CHAINS)
        for tile, mixed in zip(tiles, ends):
            dq_out[tile] = mixed
    for block in range(dkv.shape[0]):
        dkv_out[block] = dkv[block].astype(BF16)


def call_backward(bounds, q, kv, kvt, d_o, o, lse):
    blks, span, _ = kv.shape
    tiles = 2 * span // QUERY_TILE
    return pl.pallas_call(
        backward_kernel,
        out_shape=(
            jax.ShapeDtypeStruct((tiles, LANES, QUERY_TILE), F32),
            jax.ShapeDtypeStruct((blks, span, LANES), BF16),
            jax.ShapeDtypeStruct((tiles, 8, QUERY_TILE), F32),
        ),
        in_specs=vmem_specs(7),
        out_specs=tuple(vmem_specs(3)),
        scratch_shapes=[pltpu.VMEM((blks, span, LANES), F32)],
        compiler_params=pltpu.CompilerParams(vmem_limit_bytes=16 * MIB),
        name="attend_back",
    )(bounds, q, kv, kvt, d_o, o, lse)


def gelu_parts(values):
    share = 0.5 * (1.0 + lax.erf(values * (2.0**-0.5)))
    slope = share + values * jnp.exp(-0.5 * values * values) * (2.0 * math.pi) ** -0.5
    return values * share, slope


def positions(expert_rows, expert_cols, rank_row, rank_col):
    def count(mask, axis):
        return jnp.sum(mask.astype(F32), axis=axis, keepdims=True)

    row = [None, None]
    col = [None, None]
    before = rank_col < rank_row
    after = rank_row < rank_col
    for choice in range(2):
        row[choice] = count((expert_cols[choice] == expert_rows[choice]) & before, 0)
        col[choice] = count((expert_rows[choice] == expert_cols[choice]) & after, 1)
    row[1] = row[1] + count(expert_cols[0] == expert_rows[1], 0)
    col[1] = col[1] + count(expert_rows[0] == expert_cols[1], 1)
    return row, col


def own_columns(rows_ref, turned, blk, capacity):
    blks, _, slots = rows_ref.shape
    rows = jnp.concatenate(
        [rows_ref[...].reshape(blks, slots), jnp.zeros((LANES - blks, slots), F32)], axis=0
    )
    for piece in range(slots // LANES):
        columns = slice(piece * LANES, (piece + 1) * LANES)
        turned[columns, :] = jnp.transpose(rows[:, columns])
    own = turned[pl.ds(pl.multiple_of(blk * capacity, capacity), capacity), :]
    return jnp.concatenate([own[:, source : source + 1] for source in range(blks)], axis=0)


def middle_kernel(
    heads, blks,
    x_hbm, o_ref, wo_ref, routes_hbm, rank_hbm, d_out_hbm, win_hbm, wout_hbm,
    po, hidden_ref, share_ref, dh_ref, dma_all, grads_ref, rx,
    x_ref, routes_ref, rank_ref, d_out_ref, win_ref, wout_ref, rows_in, in_sem,
    o_all, dos, doa, rs, ra, dr, da, dms, mix, gate_rows, d_gate_rows, turned,
    o_send, o_recv, dos_send, dos_recv, r_send, r_recv,
    dr_send, dr_recv, dm_send, dm_recv, rx_send, rx_recv, g_send, g_recv, dg_send, dg_recv,
):
    head, blk, z, y = place()
    tokens, model = x_ref.shape
    capacity = 2 * tokens // blks
    slots = capacity * blks
    plane = [(k % heads, k // heads) for k in range(1, 2 * heads)]
    wanted = (
        (routes_hbm, routes_ref), (rank_hbm, rank_ref), (d_out_hbm, d_out_ref), (x_hbm, x_ref),
        (win_hbm, win_ref), (wout_hbm, wout_ref),
    )
    fetched = [
        pltpu.make_async_copy(src, dst, in_sem.at[i]) for i, (src, dst) in enumerate(wanted)
    ]
    for copy in fetched:
        copy.start()
    met = greet(
        [(around(head, kh, heads), 2 * z + around(y, ky, 2)) for kh, ky in plane]
        + [(head, around(blk, k, blks)) for k in range(1, blks)]
    )
    meet(met)

    def plane_copies(src_of, dst, send, recv):
        copies = []
        for k, (kh, ky) in enumerate(plane):
            to_head, to_y = around(head, kh, heads), around(y, ky, 2)
            copies.append(
                remote(src_of(to_y, to_head), dst, send.at[k], recv.at[k], to_head, 2 * z + to_y)
            )
        return copies

    def blk_copies(src, dst, send, recv):
        return [
            remote(
                src.at[around(blk, k, blks)], dst.at[blk],
                send.at[k], recv.at[k], head, around(blk, k, blks),
            )
            for k in range(1, blks)
        ]

    def start(copies):
        for copy in copies:
            copy.start()

    def finish(copies):
        for copy in copies:
            copy.wait()

    o_copies = plane_copies(lambda to_y, to_head: o_ref.at[to_y, to_head], o_all.at[y, head], o_send, o_recv)
    start(o_copies)
    o_all[y, head] = o_ref[y, head]

    lanes = lane_ids((tokens, LANES))
    for copy in fetched[:4]:
        copy.wait()
    e_rows = [routes_ref[i : i + 1, :].astype(F32) for i in range(2)]
    rank_row = rank_ref[...].astype(F32)
    rows_in[...] = jnp.zeros_like(rows_in)
    rows_in[0:1, :], rows_in[1:2, :], rows_in[2:3, :] = *e_rows, rank_row
    columns = jnp.transpose(rows_in[...])
    e_cols = [columns[:, 0:1], columns[:, 1:2]]
    rank_col = columns[:, 2:3]
    pos_rows, pos_cols = positions(e_rows, e_cols, rank_row, rank_col)

    def slot_of(expert, position):
        return jnp.where(position < capacity, expert * capacity + position, -1.0).astype(jnp.int32)

    slot_rows = [slot_of(e, p) for e, p in zip(e_rows, pos_rows)]
    slot_cols = [slot_of(e, p) for e, p in zip(e_cols, pos_cols)]
    slot_down = lax.broadcasted_iota(jnp.int32, (slots, tokens), 0)
    slot_across = lane_ids((tokens, slots))
    pick = [(slot_down == s).astype(BF16) for s in slot_rows]
    put = [(slot_across == s).astype(BF16) for s in slot_cols]
    pick_any = pick[0] + pick[1]
    put_any = put[0] + put[1]

    d_out = d_out_ref[...]
    dos[...] = dot(pick_any, d_out.astype(BF16)).astype(BF16).reshape(dos.shape)
    dos_copies = blk_copies(dos, doa, dos_send, dos_recv)
    start(dos_copies)
    doa[blk] = dos[blk]

    weight_out = jnp.concatenate(
        [wo_ref[(b ^ 1) * HALF : ((b ^ 1) + 1) * HALF, 0:model] for b in range(blks)], axis=0
    )
    small = wo_ref[:, model : model + LANES]
    small_across = jnp.concatenate(
        [
            jnp.transpose(small[i * LANES : (i + 1) * LANES].astype(F32))
            for i in range(model // LANES)
        ],
        axis=1,
    )
    gain = small_across[blks : blks + 1, :]

    finish(o_copies)
    low_lanes = lanes[:HALF] < HALF
    for piece in range(heads):
        columns = slice(piece * LANES, (piece + 1) * LANES)
        first, second = o_all[1, piece].astype(F32), o_all[0, piece].astype(F32)
        mix[:HALF, columns] = jnp.where(low_lanes, first, second).astype(BF16)
        swapped = pltpu.roll(jnp.where(low_lanes, second, first), HALF, 1)
        mix[HALF:, columns] = swapped.astype(BF16)
    mixed = mix[...]
    hidden = x_ref[...].astype(F32) + dot(mixed, weight_out)
    xhat, scale = centre(hidden)
    routed = (xhat * gain).astype(BF16)
    rs[...] = dot(pick_any, routed).astype(BF16).reshape(rs.shape)
    r_copies = blk_copies(rs, ra, r_send, r_recv)
    start(r_copies)
    ra[blk] = rs[blk]
    logits = jnp.where(lanes < blks, dot(routed, small), MASKED)
    powers = jnp.exp(logits - jnp.max(logits, axis=1, keepdims=True))
    probs = powers / jnp.sum(powers, axis=1, keepdims=True)
    lanes_f = lanes.astype(F32)
    hots = [lanes_f == e for e in e_cols]
    gates = [jnp.sum(jnp.where(hot, probs, 0.0), axis=1, keepdims=True) for hot in hots]
    gate_high = [g.astype(BF16).astype(F32) for g in gates]
    gate_across = jnp.transpose(
        jnp.where(lanes == 0, gate_high[0], jnp.where(lanes == 1, gates[0] - gate_high[0], 0.0))
        + jnp.where(lanes == 2, gate_high[1], jnp.where(lanes == 3, gates[1] - gate_high[1], 0.0))
    ).astype(BF16)
    by_slot = (dot(gate_across, put[0]), dot(gate_across, put[1]))
    gate_rows[blk] = by_slot[0][0:1] + by_slot[0][1:2] + by_slot[1][2:3] + by_slot[1][3:4]
    g_copies = [
        remote(
            gate_rows.at[blk], gate_rows.at[blk],
            g_send.at[k], g_recv.at[k], head, around(blk, k, blks),
        )
        for k in range(1, blks)
    ]
    start(g_copies)
    finish(dos_copies)
    finish(r_copies)

    out_rows = doa[...].reshape(slots, model)
    rx[head, :, 0:model] = ra[...].reshape(slots, model)
    finish(g_copies)
    gate_col = own_columns(gate_rows, turned, blk, capacity)
    rx[head, :, model : 2 * model] = (out_rows.astype(F32) * gate_col).astype(BF16)
    core = lax.rem(head, 2)
    sibling, across = head - core + 1 - core, around(head, 2, heads)

    def half_rows(source, half):
        return rx.at[source, pl.ds(half * slots // 2, slots // 2)]

    to_across = [
        remote(
            half_rows(head, half), half_rows(head, half),
            rx_send.at[1 + half], rx_recv.at[1 + half], across, blk,
        )
        for half in range(2)
    ]
    to_sibling = remote(rx.at[head], rx.at[head], rx_send.at[0], rx_recv.at[0], sibling, blk)
    forwards = [
        remote(
            half_rows(across, half), half_rows(across, half),
            rx_send.at[3 + half], rx_recv.at[3 + half], sibling, blk,
        )
        for half in range(2)
    ]
    start(to_across)
    to_sibling.start()
    for copy in fetched[4:]:
        copy.wait()
    act, slope = gelu_parts(dot(rx[head, :, 0:model], win_ref[...]))
    d_act = dot(rx[head, :, model : 2 * model], wout_ref[...], (1, 1))
    row_grads = dot((slope * d_act).astype(BF16), win_ref[...], (1, 1))
    dr[...] = row_grads.astype(BF16).reshape(dr.shape)
    dr_copies = blk_copies(dr, da, dr_send, dr_recv)
    start(dr_copies)
    result = dot(act.astype(BF16), wout_ref[...]).astype(BF16)
    d_gate = jnp.sum(out_rows.astype(F32) * result.astype(F32), axis=1, keepdims=True)
    da[blk] = dr[blk]
    d_wide = jnp.broadcast_to(d_gate, (slots, LANES))
    d_gate_rows[blk] = jnp.concatenate(
        [jnp.transpose(d_wide[i * LANES : (i + 1) * LANES])[0:1] for i in range(slots // LANES)],
        axis=1,
    )
    dg_copies = [
        remote(
            d_gate_rows.at[blk], d_gate_rows.at[blk],
            dg_send.at[k], dg_recv.at[k], head, around(blk, k, blks),
        )
        for k in range(1, blks)
    ]
    start(dg_copies)
    po[...] = result.reshape(blks, capacity, model)

    finish(dg_copies)
    back_gate = own_columns(d_gate_rows, turned, blk, capacity)
    back_gate = split_high_low(back_gate, lane_ids((slots, LANES)))
    d_gates = [join_high_low(dot(p, back_gate), 0) for p in put]
    d_probs = jnp.where(hots[0], d_gates[0], 0.0) + jnp.where(hots[1], d_gates[1], 0.0)
    d_logits = probs * (d_probs - jnp.sum(probs * d_probs, axis=1, keepdims=True))
    d_high = d_logits.astype(BF16)
    d_low = (d_logits - d_high.astype(F32)).astype(BF16)
    d_router_part = dot(d_high, small, (1, 1)) + dot(d_low, small, (1, 1))
    finish(dr_copies)
    d_routed = dot(put_any, da[...].reshape(slots, model)) + d_router_part
    d_hidden = d_out + centre_back(d_routed * gain, xhat, scale)
    dh_ref[...] = d_hidden
    d_attn = d_hidden.astype(BF16)
    d_mixed = dot(d_attn, weight_out, (1, 1))
    for piece in range(heads):
        block = d_mixed[:, piece * LANES : (piece + 1) * LANES]
        for to_y in range(2):
            dms[to_y, piece] = halves(block, low_lanes == (to_y == 1)).astype(BF16)
    dm_copies = plane_copies(lambda to_y, to_head: dms.at[to_y, to_head], dma_all.at[y, head], dm_send, dm_recv)
    start(dm_copies)
    dma_all[y, head] = dms[y, head]
    arrived(half_rows(across, 0), rx_recv.at[1])
    forwards[0].start()

    d_weight = dot(mixed, d_attn, (0, 0)).astype(BF16)
    for b in range(blks):
        grads_ref[b, :, 0:model] = d_weight[(b ^ 1) * HALF : ((b ^ 1) + 1) * HALF, :]
    last = (lanes == blks).astype(BF16)
    d_small = dot(routed, d_high, (0, 0)) + dot((d_routed * xhat).astype(BF16), last, (0, 0))
    grads_ref[:, :, model : model + LANES] = d_small.astype(BF16).reshape(blks, HALF, LANES)
    share = gates[0] * put[0].astype(F32) + gates[1] * put[1].astype(F32)
    share_ref[0] = share.astype(BF16)
    share_ref[1] = (share - share_ref[0].astype(F32)).astype(BF16)
    hidden_ref[...] = hidden

    arrived(half_rows(across, 1), rx_recv.at[2])
    forwards[1].start()
    finish(dm_copies)
    to_sibling.wait()
    for copy in to_across:
        copy.wait_send()
    finish(forwards)


def call_middle(x, o, wo, routes, rank, d_out, win, wout, heads, blks):
    tokens, model = x.shape
    capacity = 2 * tokens // blks
    slots = capacity * blks
    wide = model + LANES

    def rows(width):
        return pltpu.VMEM((blks, capacity, width), BF16)

    def block(*lead):
        return pltpu.VMEM((*lead, tokens // 2, LANES), BF16)

    return pl.pallas_call(
        functools.partial(middle_kernel, heads, blks),
        out_shape=(
            jax.ShapeDtypeStruct((blks, capacity, model), BF16),
            jax.ShapeDtypeStruct((tokens, model), F32),
            jax.ShapeDtypeStruct((2, tokens, slots), BF16),
            jax.ShapeDtypeStruct((tokens, model), F32),
            jax.ShapeDtypeStruct((2, heads, tokens // 2, LANES), BF16),
            jax.ShapeDtypeStruct((blks, model // blks, wide), BF16),
            jax.ShapeDtypeStruct((heads, slots, 2 * model), BF16),
        ),
        in_specs=hbm_specs(1) + vmem_specs(2) + hbm_specs(5),
        out_specs=tuple(vmem_specs(7)),
        scratch_shapes=[
            pltpu.VMEM((tokens, model), BF16),
            pltpu.VMEM((2, tokens), jnp.int32),
            pltpu.VMEM((1, tokens), jnp.int32),
            pltpu.VMEM((tokens, model), F32),
            pltpu.VMEM(win.shape, BF16),
            pltpu.VMEM(wout.shape, BF16),
            pltpu.VMEM((tokens, tokens), F32),
            dma(6),
            block(2, heads), rows(model), rows(model), rows(model), rows(model),
            rows(model), rows(model), block(2, heads),
            pltpu.VMEM((tokens, model), BF16),
            pltpu.VMEM((blks, 1, slots), F32), pltpu.VMEM((blks, 1, slots), F32),
            pltpu.VMEM((slots, LANES), F32),
            dma(2 * heads), dma(2 * heads), dma(blks), dma(blks), dma(blks), dma(blks),
            dma(blks), dma(blks), dma(2 * heads), dma(2 * heads), dma(5), dma(5),
            dma(blks), dma(blks), dma(blks), dma(blks),
        ],
        compiler_params=pltpu.CompilerParams(
            collective_id=2, has_side_effects=True, vmem_limit_bytes=20 * MIB
        ),
        name="experts",
    )(*in_hbm(x), o, wo, *in_hbm(routes.T, rank, d_out, win, wout))


def last_kernel(
    heads, blks,
    x_hbm, dh_ref, begun_ref, dkv_ref, xa_ref, wa_ref, w_hbm, g1_hbm, grads_ref, rx_ref, win_hbm, wout_hbm,
    po_ref, hidden_ref, share_ref, bounds_ref, q_ref, kv_ref, kvt_ref, do_ref, lse_ref, delta_ref,
    y_ref, dx_ref, dw_ref, shared_ref, din_ref, dout_ref,
    x_ref, w_ref, g1_ref, win_ref, wout_ref, in_sem,
    gain_tile, far_all, near_send_buf, near_all, pair_all, dq_all, dq_ref, dq_packed, dkv_own, pair_buf, us, ua, gs, ga, gqs, gqa, u_part, xat, pa, gh, ghq, w1, w2s, w2, w3,
    q_send, q_recv, pair_send, pair_recv, far_send, far_recv, near_send, near_recv,
    u_send, u_recv, g_send, g_recv, gh_send, gh_recv, w1_send, w1_recv, w2_send, w2_recv,
    w3_send, w3_recv, e_send, e_recv, gq_send, gq_recv, po_send, po_recv, ghq_send, ghq_recv,
    din_half, dout_half,
):
    head, blk, z, y = place()
    planes = blks // 2
    tokens, model = x_ref.shape
    rows = w_ref.shape[0]
    wanted = (
        (win_hbm, win_ref), (wout_hbm, wout_ref), (x_hbm, x_ref), (w_hbm, w_ref), (g1_hbm, g1_ref)
    )
    fetched = [
        pltpu.make_async_copy(src, dst, in_sem.at[i]) for i, (src, dst) in enumerate(wanted)
    ]
    for copy in fetched:
        copy.start()
    met = greet(
        [(around(head, k, heads), blk) for k in range(1, heads)]
        + [(head, around(blk, k, blks)) for k in range(1, blks)]
    )
    meet(met)

    def start(copies):
        for copy in copies:
            copy.start()

    def finish(copies):
        for copy in copies:
            copy.wait()

    other_y = around(y, 1, 2)
    pair = 2 * z + other_y
    above, below = z < planes - 1, z > 0
    directions = ((1, above, below, 0), (-1, below, above, 2))

    half_span = dkv_ref.shape[1] // 2

    def half_of(ref, half):
        return ref.at[pl.ds(half * half_span, half_span)]

    def far_copy(step, slot, side, half):
        span = 2 * (z + 2 * step) + side
        return remote(
            half_of(dkv_ref.at[span], half), half_of(far_all.at[slot + side], half),
            far_send.at[slot + side, half], far_recv.at[slot + side, half], head, 2 * (z + step) + y,
        )

    def near_copy(step, slot, side, half):
        return remote(
            half_of(near_send_buf.at[slot + side], half), half_of(near_all.at[slot // 2, y], half),
            near_send.at[slot + side, half], near_recv.at[slot // 2, y, half],
            head, 2 * (z + step) + side,
        )

    def two_away(step):
        return z + 2 * step < planes if step > 0 else z + 2 * step >= 0

    for half in range(2):
        for step, there, back, slot in directions:

            @pl.when(two_away(step))
            def _():
                for side in range(2):
                    far_copy(step, slot, side, half).start()

    w1_copies = [
        remote(
            grads_ref.at[:, around(head, k, heads)], w1.at[head],
            w1_send.at[k], w1_recv.at[k], around(head, k, heads), blk,
        )
        for k in range(1, heads)
    ]
    start(w1_copies)
    w1[head] = grads_ref[:, head]

    core = lax.rem(head, 2)
    sibling = head - core + 1 - core
    ff_half = wout_ref.shape[0] // 2
    ff_step = ff_half // 2

    def expert_chunk(chunk):
        here = pl.multiple_of(core * ff_half + chunk * ff_step, ff_step)
        there = pl.multiple_of(chunk * ff_step, ff_step)
        into = win_ref[:, pl.ds(here, ff_step)]
        outof = wout_ref[pl.ds(here, ff_step), :]
        d_in = jnp.zeros((model, ff_step), F32)
        d_out = jnp.zeros((ff_step, model), F32)
        for source in range(heads):
            rows_in = rx_ref[source, :, 0:model]
            grads_out = rx_ref[source, :, model : 2 * model]
            act, slope = gelu_parts(dot(rows_in, into))
            d_act = dot(grads_out, outof, (1, 1))
            d_in = d_in + dot(rows_in, (slope * d_act).astype(BF16), (0, 0))
            d_out = d_out + dot(act.astype(BF16), grads_out, (0, 0))
        din_ref[:, pl.ds(here, ff_step)] = d_in
        dout_ref[pl.ds(here, ff_step), :] = d_out
        din_half[core, :, pl.ds(there, ff_step)] = d_in.astype(BF16)
        dout_half[core, pl.ds(there, ff_step), :] = d_out.astype(BF16)

    key_tile = kv_ref.shape[1]
    for group in range(2 * key_tile // (CHAINS * QUERY_TILE)):
        tiles, queries = query_group(q_ref, group, y)
        known = (
            queries,
            group_grads(do_ref, tiles, y),
            [delta_ref[tile, 0:1, :] for tile in tiles],
            [lse_ref[tile, 0:1, :] for tile in tiles],
        )
        carry = tuple(begun_ref[tile] for tile in tiles)
        for side in range(2):
            first = pl.multiple_of((2 * z + side) * key_tile, key_tile)
            keys_across = kvt_ref[:, pl.ds(first, key_tile)]
            given, carry = attend_back(
                bounds_ref, tiles, first, kv_ref[2 * z + side], keys_across, known, carry
            )
            dkv_own[side] = given if group == 0 else dkv_own[side] + given
        for tile, total in zip(tiles, carry):
            at = tile * QUERY_TILE % key_tile
            dq_ref[tile * QUERY_TILE // key_tile, at : at + QUERY_TILE] = jnp.transpose(total)
    pair_buf[...] = dkv_own[other_y].astype(BF16)
    pair_copy = remote(pair_buf, pair_all, pair_send, pair_recv, head, pair)
    pair_copy.start()
    own_lanes = (lane_ids(dq_packed.shape) < HALF) == (y == 0)
    dq_packed[...] = halves(dq_ref[other_y], own_lanes).astype(BF16)
    q_copy = remote(dq_packed, dq_all, q_send, q_recv, head, pair)
    q_copy.start()
    for half in range(2):
        rows_here = slice(half * half_span, (half + 1) * half_span)
        for step, there, back, slot in directions:

            @pl.when(there)
            def _():
                for side in range(2):
                    near_send_buf[slot + side, rows_here] = dkv_ref[2 * (z + step) + side, rows_here]

            @pl.when(jnp.logical_and(there, back))
            def _():
                for side in range(2):
                    arrived(half_of(far_all.at[slot + side], half), far_recv.at[slot + side, half])
                    near_send_buf[slot + side, rows_here] = (
                        near_send_buf[slot + side, rows_here].astype(F32)
                        + far_all[slot + side, rows_here].astype(F32)
                    ).astype(BF16)

            @pl.when(there)
            def _():
                for side in range(2):
                    near_copy(step, slot, side, half).start()

    finish(fetched[:2])
    weight = wa_ref[...].reshape(model, 3 * LANES)
    for piece in range(heads):
        xat[:, piece * tokens : (piece + 1) * tokens] = jnp.transpose(xa_ref[piece])
    even = y == 0


    expert_chunk(0)

    q_copy.wait()
    landed = dq_all[...].astype(F32)
    landed = jnp.concatenate([landed, pltpu.roll(landed, HALF, 1)], axis=0)
    own_lanes = (lane_ids(landed.shape) < HALF) == even
    q_grads = jnp.where(own_lanes, dq_ref[y], landed).astype(BF16)
    gqs[...] = dot(xat[...], q_grads).astype(BF16).reshape(gqs.shape)
    gq_copies = [
        remote(
            gqs.at[around(blk, k, blks)], gqa.at[blk],
            gq_send.at[k], gq_recv.at[k], head, around(blk, k, blks),
        )
        for k in range(1, blks)
    ]
    start(gq_copies)
    gqa[blk] = gqs[blk]
    u_part[...] = dot(q_grads, weight[:, 2 * LANES : 3 * LANES], (1, 1)).reshape(u_part.shape)

    finish(w1_copies)
    summed = w1[0].astype(F32)
    for source in range(1, heads):
        summed = summed + w1[source].astype(F32)
    w2s[...] = summed.astype(BF16)
    w2_copies = [
        remote(
            w2s.at[around(blk, k, blks)], w2.at[blk],
            w2_send.at[k], w2_recv.at[k], head, around(blk, k, blks),
        )
        for k in range(1, blks)
    ]
    start(w2_copies)
    w2[blk] = w2s[blk]

    expert_chunk(1)

    e_copies = [
        remote(din_half.at[core], din_half.at[core], e_send.at[0], e_recv.at[0], sibling, blk),
        remote(dout_half.at[core], dout_half.at[core], e_send.at[1], e_recv.at[1], sibling, blk),
    ]
    start(e_copies)

    pair_copy.wait()
    for step, there, back, slot in directions:

        @pl.when(back)
        def _():
            for side in range(2):
                for half in range(2):
                    arrived(
                        half_of(near_all.at[slot // 2, side], half),
                        near_recv.at[slot // 2, side, half],
                    )

        @pl.when(jnp.logical_not(back))
        def _():
            near_all[slot // 2] = jnp.zeros(near_all.shape[1:], BF16)

    own = dkv_own[y]
    other = pair_all[...].astype(F32)
    made = jnp.concatenate(
        [
            (
                jnp.where(even == (side == 0), own, other)
                + near_all[0, side].astype(F32)
                + near_all[1, side].astype(F32)
            ).astype(BF16)
            for side in range(2)
        ],
        axis=1,
    )
    gs[...] = dot(xat[...], made).astype(BF16).reshape(gs.shape)
    g_copies = [
        remote(
            gs.at[around(blk, k, blks)], ga.at[blk],
            g_send.at[k], g_recv.at[k], head, around(blk, k, blks),
        )
        for k in range(1, blks)
    ]
    start(g_copies)
    ga[blk] = gs[blk]
    us[...] = (
        u_part[...] + dot(made, weight[:, 0 : 2 * LANES], (1, 1)).reshape(us.shape)
    ).astype(BF16)
    u_copies = [
        remote(
            us.at[around(head, k, heads)], ua.at[head],
            u_send.at[k], u_recv.at[k], around(head, k, heads), blk,
        )
        for k in range(1, heads)
    ]
    start(u_copies)
    ua[head] = us[head]
    finish(fetched[2:])
    finish(gq_copies)
    total = gqa[0].astype(F32)
    for source in range(1, blks):
        total = total + gqa[source].astype(F32)
    ghq[head] = total.astype(BF16)
    ghq_copies = [
        remote(ghq.at[head], ghq.at[head], ghq_send.at[k], ghq_recv.at[k], around(head, k, heads), blk)
        for k in range(1, heads)
    ]
    start(ghq_copies)

    finish(w2_copies)
    part = w2[0].astype(F32)
    for source in range(1, blks):
        part = part + w2[source].astype(F32)
    w3[head] = part.astype(BF16)
    w3_copies = [
        remote(w3.at[head], w3.at[head], w3_send.at[k], w3_recv.at[k], around(head, k, heads), blk)
        for k in range(1, heads)
    ]
    start(w3_copies)

    xhat, scale = centre(x_ref[...].astype(F32))
    finish(e_copies)
    there = pl.multiple_of((1 - core) * ff_half, ff_half)
    din_ref[:, pl.ds(there, ff_half)] = din_half[1 - core].astype(F32)
    dout_ref[pl.ds(there, ff_half), :] = dout_half[1 - core].astype(F32)
    finish(g_copies)
    total = ga[0].astype(F32)
    for source in range(1, blks):
        total = total + ga[source].astype(F32)
    gh[head] = total.astype(BF16)
    gh_copies = [
        remote(gh.at[head], gh.at[head], gh_send.at[k], gh_recv.at[k], around(head, k, heads), blk)
        for k in range(1, heads)
    ]
    start(gh_copies)
    po_copies = [
        remote(
            po_ref.at[around(blk, k, blks)], pa.at[blk],
            po_send.at[k], po_recv.at[k], head, around(blk, k, blks),
        )
        for k in range(1, blks)
    ]
    start(po_copies)
    pa[blk] = po_ref[blk]
    finish(u_copies)
    grad = ua[0].astype(F32)
    for source in range(1, heads):
        grad = grad + ua[source].astype(F32)
    dx_ref[...] = dh_ref[...] + centre_back(grad, xhat, scale)

    gain_tile[...] = jnp.zeros_like(gain_tile)
    gain_tile[0:1, 0:rows] = g1_ref[...].astype(F32)
    gain = jnp.transpose(jnp.broadcast_to(gain_tile[0:1, :], (LANES, LANES)))[:rows]
    low_half = lane_ids((rows, LANES)) < HALF
    finish(ghq_copies)
    finish(gh_copies)
    d_gain = jnp.zeros((rows, LANES), F32)
    for source in range(heads):
        both = [gh[source, :, i * LANES : (i + 1) * LANES].astype(F32) for i in range(2)]
        grads = (
            ghq[source].astype(F32) * HS ** (-0.5),
            jnp.where(low_half, both[0], both[1]),
            pltpu.roll(jnp.where(low_half, both[1], both[0]), HALF, 1),
        )
        for which, value in enumerate(grads):
            columns = slice(which * model + source * LANES, which * model + (source + 1) * LANES)
            d_gain = d_gain + value * w_ref[:, columns].astype(F32)
            dw_ref[:, columns] = value * gain
    finish(w3_copies)
    shared = w3[...].reshape(rows, w3.shape[-1]).astype(F32)
    shared_ref[:, 0:model] = shared[:, 0:model]
    gain_col = jnp.sum(d_gain, axis=1, keepdims=True)
    shared_ref[:, model : model + LANES] = jnp.where(
        lane_ids((rows, LANES)) == blks + 1, gain_col, shared[:, model : model + LANES]
    )
    finish(po_copies)
    parts = pa[...].reshape(share_ref.shape[2], model)
    mixture = dot(share_ref[0], parts) + dot(share_ref[1], parts)
    y_ref[...] = (hidden_ref[...] + mixture).astype(BF16)

    for step, there, back, slot in directions:

        @pl.when(two_away(step))
        def _():
            for side in range(2):
                for half in range(2):
                    far_copy(step, slot, side, half).wait_send()

        @pl.when(there)
        def _():
            for side in range(2):
                for half in range(2):
                    near_copy(step, slot, side, half).wait_send()


def call_last(
    x, dh, dq, dkv, xa, wa, w_qkv, g1, grads, rx, win, wout, po, hidden, share,
    bounds, q, kv, kvt, d_o, lse, delta, heads, blks,
):
    tokens, model = x.shape
    span = tokens * heads
    rows = w_qkv.shape[0]
    wide = model + LANES
    part = rows // heads
    ff = wout.shape[0]

    def block(*lead):
        return pltpu.VMEM((*lead, span, LANES), BF16)

    return pl.pallas_call(
        functools.partial(last_kernel, heads, blks),
        out_shape=(
            jax.ShapeDtypeStruct((tokens, model), BF16),
            jax.ShapeDtypeStruct((tokens, model), F32),
            jax.ShapeDtypeStruct((rows, 3 * model), F32),
            jax.ShapeDtypeStruct((rows, wide), F32),
            jax.ShapeDtypeStruct((model, ff), F32),
            jax.ShapeDtypeStruct((ff, model), F32),
        ),
        in_specs=hbm_specs(1) + vmem_specs(5) + hbm_specs(2) + vmem_specs(2) + hbm_specs(2) + vmem_specs(10),
        out_specs=tuple(vmem_specs(6)),
        scratch_shapes=[
            pltpu.VMEM((tokens, model), BF16),
            pltpu.VMEM((rows, 3 * model), BF16),
            pltpu.VMEM((1, rows), BF16),
            pltpu.VMEM(win.shape, BF16),
            pltpu.VMEM(wout.shape, BF16),
            dma(5),
            pltpu.VMEM((8, LANES), F32),
            block(4), block(4), block(2, 2), block(), pltpu.VMEM((span // 2, LANES), BF16),
            pltpu.VMEM((2, span, LANES), F32), pltpu.VMEM((span // 2, LANES), BF16),
            pltpu.VMEM((2, span, LANES), F32), block(),
            pltpu.VMEM((heads, tokens, model), BF16), pltpu.VMEM((heads, tokens, model), BF16),
            pltpu.VMEM((blks, rows, 2 * LANES), BF16), pltpu.VMEM((blks, rows, 2 * LANES), BF16),
            pltpu.VMEM((blks, rows, LANES), BF16), pltpu.VMEM((blks, rows, LANES), BF16),
            pltpu.VMEM((heads, tokens, model), F32), pltpu.VMEM((model, span), BF16),
            pltpu.VMEM(po.shape, BF16),
            pltpu.VMEM((heads, rows, 2 * LANES), BF16), pltpu.VMEM((heads, rows, LANES), BF16),
            pltpu.VMEM((heads, blks, part, wide), BF16), pltpu.VMEM((blks, part, wide), BF16),
            pltpu.VMEM((blks, part, wide), BF16), pltpu.VMEM((heads, part, wide), BF16),
            pltpu.SemaphoreType.DMA, pltpu.SemaphoreType.DMA, pltpu.SemaphoreType.DMA, pltpu.SemaphoreType.DMA,
            dma(4, 2), dma(4, 2), dma(4, 2), dma(2, 2, 2),
            dma(heads), dma(heads), dma(blks), dma(blks), dma(heads), dma(heads), dma(heads), dma(heads),
            dma(blks), dma(blks), dma(heads), dma(heads), dma(2), dma(2), dma(blks), dma(blks), dma(blks), dma(blks), dma(heads), dma(heads),
            pltpu.VMEM((2, model, ff // 2), BF16), pltpu.VMEM((2, ff // 2, model), BF16),
        ],
        compiler_params=pltpu.CompilerParams(
            collective_id=3, has_side_effects=True, vmem_limit_bytes=36 * MIB
        ),
        name="last",
    )(
        *in_hbm(x), dh, dq, dkv, xa, wa, *in_hbm(w_qkv, g1.reshape(1, rows)),
        grads.reshape(blks, heads, part, wide), rx, *in_hbm(win, wout), po, hidden, share,
        bounds, q, kv, kvt, d_o, lse, delta,
    )


def finish_kernel(
    experts,
    y_ref, dx_ref, dw_ref, shared_ref, din_ref, dout_ref,
    y_out, dx_out, g1_out, dw_out, dwo_out, g2_out, wr_out, din_out, dout_out,
    tile, wr, g2, g1, sem,
):
    rows = shared_ref.shape[0]
    model = dx_ref.shape[1]
    copies = [
        pltpu.make_async_copy(dx_ref, dx_out, sem.at[0]),
        pltpu.make_async_copy(dw_ref, dw_out, sem.at[1]),
        pltpu.make_async_copy(shared_ref.at[:, pl.ds(0, model)], dwo_out, sem.at[2]),
        pltpu.make_async_copy(y_ref, y_out, sem.at[6]),
        pltpu.make_async_copy(din_ref, din_out, sem.at[7]),
        pltpu.make_async_copy(dout_ref, dout_out, sem.at[8]),
    ]
    for copy in copies:
        copy.start()
    tile[...] = jnp.zeros_like(tile)
    tile[0:rows, :] = shared_ref[:, model : model + LANES]
    across = jnp.transpose(tile[...])[:, 0:rows]
    wr[...] = across[0:experts]
    g2[...] = across[experts : experts + 1]
    g1[...] = across[experts + 1 : experts + 2]
    for index, (src, dst) in enumerate(((wr, wr_out), (g2, g2_out), (g1, g1_out))):
        copies.append(pltpu.make_async_copy(src, dst, sem.at[3 + index]))
        copies[-1].start()
    for copy in copies:
        copy.wait()


def call_finish(output, dx, dw, shared, d_in, d_out):
    rows = shared.shape[0]
    model = dx.shape[1]
    experts = model // rows
    return pl.pallas_call(
        functools.partial(finish_kernel, experts),
        out_shape=(
            jax.ShapeDtypeStruct(output.shape, BF16),
            jax.ShapeDtypeStruct(dx.shape, F32),
            jax.ShapeDtypeStruct((1, rows), F32),
            jax.ShapeDtypeStruct(dw.shape, F32),
            jax.ShapeDtypeStruct((rows, model), F32),
            jax.ShapeDtypeStruct((1, rows), F32),
            jax.ShapeDtypeStruct((experts, rows), F32),
            jax.ShapeDtypeStruct(d_in.shape, F32),
            jax.ShapeDtypeStruct(d_out.shape, F32),
        ),
        in_specs=vmem_specs(6),
        out_specs=tuple(hbm_specs(9)),
        scratch_shapes=[
            pltpu.VMEM((LANES, LANES), F32),
            pltpu.VMEM((experts, rows), F32),
            pltpu.VMEM((1, rows), F32),
            pltpu.VMEM((1, rows), F32),
            dma(9),
        ],
        compiler_params=pltpu.CompilerParams(vmem_limit_bytes=16 * MIB),
        name="finish",
    )(output, dx, dw, shared, d_in, d_out)


def local_kernels(
    inputs, ln1_gain, w_qkv, w_out, ln2_gain, w_router,
    expert_in, expert_out, routes, priority, doc_lengths, d_out,
):
    heads, blks = lax.axis_size("head"), lax.axis_size("blk")
    model = inputs.shape[1]
    tokens = inputs.shape[0]
    win, wout = expert_in[0], expert_out[0]
    q, kv, xa, wa, wo, kvt, bounds, begun = call_qkv(
        inputs, w_qkv, ln1_gain, w_out, w_router, ln2_gain, doc_lengths, heads, blks
    )
    o, o_low, lse = call_forward(bounds, q, kv, kvt, begun)
    po, hidden, share, dh, d_o, grads, rx = call_middle(
        inputs, o_low.reshape(2, heads, tokens // 2, LANES), wo.reshape(model, model + LANES),
        routes, priority, d_out, win, wout, heads, blks,
    )
    d_o = d_o.reshape(2 * heads * tokens // QUERY_TILE, -1, HALF, LANES)
    dq, dkv, delta = call_backward(bounds, q, kv, kvt, d_o, o, lse)
    ends = call_last(
        inputs, dh, dq, dkv, xa, wa, w_qkv, ln1_gain, grads, rx, win, wout,
        po, hidden, share, bounds, q, kv, kvt, d_o, lse, delta, heads, blks,
    )
    output, d_inputs, d_gain_one, d_qkv, d_out_proj, d_gain_two, d_router, d_in, d_out_weight = call_finish(*ends)
    return (
        output,
        d_inputs,
        d_gain_one.reshape(-1),
        d_qkv,
        d_out_proj,
        d_gain_two.reshape(-1),
        d_router.T,
        d_in[None],
        d_out_weight[None],
    )


def solution(mesh):
    in_specs = (
        P(("blk", "head"), None),
        P("blk"),
        P("blk", None),
        P("blk", None),
        P("blk"),
        P("blk", None),
        P("blk", None, None),
        P("blk", None, None),
        P(("blk", "head"), None),
        P(("blk", "head"), None),
        P(),
        P(("blk", "head"), None),
    )
    out_specs = (
        P(("blk", "head"), None),
        P(("blk", "head"), None),
        P("blk"),
        P("blk", None),
        P("blk", None),
        P("blk"),
        P("blk", None),
        P("blk", None, None),
        P("blk", None, None),
    )
    fits = mesh.shape["head"] == 4 and mesh.shape["blk"] == 8
    body = local_kernels if fits else local
    return jax.shard_map(body, mesh=mesh, in_specs=in_specs, out_specs=out_specs, check_vma=False)
```

```python
import functools
import math

import jax
import jax.numpy as jnp
from jax import lax
from jax.experimental import pallas as pl
from jax.experimental.pallas import tpu as pltpu
from jax.sharding import PartitionSpec as P

HS = 64
KEY_BLOCK = 2048


PRECISE = lax.Precision.HIGHEST
MASKED = -1e30
EPSILON = 1e-06


def layer_norm(values, gain):
    average = jnp.mean(values, axis=-1, keepdims=True)
    centred = values - average
    spread = jnp.mean(centred * centred, axis=-1, keepdims=True)
    return centred * lax.rsqrt(spread + EPSILON) * gain


def gelu_exact(values):
    return jax.nn.gelu(values, approximate=False)


def router(row_block, weight):
    return jax.nn.softmax(jnp.dot(row_block, weight, precision=PRECISE), axis=-1)


def doc_index(positions, doc_lengths):
    places = jnp.arange(doc_lengths.shape[0], dtype=jnp.int32)
    starts = jnp.sum(jnp.where(places[None, :] < places[:, None], doc_lengths[None, :], 0), axis=1)
    at_most = (starts[None, :] <= positions[:, None]).astype(jnp.int32)
    return jnp.sum(at_most, axis=1) - 1


def slot_table(route_rows, ranking, capacity):
    token_count = route_rows.shape[0]
    expert = jnp.transpose(route_rows).reshape(-1)
    pair_order = (jnp.arange(2, dtype=jnp.int32)[:, None] * token_count + ranking[None, :]).reshape(
        -1
    )
    before = (expert[:, None] == expert[None, :]) & (pair_order[None, :] < pair_order[:, None])
    position = jnp.sum(before.astype(jnp.int32), axis=1)
    slot_ids = jnp.where(position < capacity, expert * capacity + position, -1)
    return slot_ids.reshape(2, token_count)


def keep_state(current):
    return current


def local(
    inputs,
    ln1_gain,
    w_qkv,
    w_out,
    ln2_gain,
    w_router,
    expert_in,
    expert_out,
    routes,
    priority,
    doc_lengths,
    d_out,
):
    blk_size = lax.axis_size("blk")
    tok_rows = inputs.shape[0]
    model_width = inputs.shape[1]
    capacity = 2 * tok_rows // blk_size
    slot_total = blk_size * capacity
    gain_one, qkv_weight, out_weight, gain_two, router_weight = (
        lax.all_gather(ln1_gain, "blk", axis=0, tiled=True),
        lax.all_gather(w_qkv, "blk", axis=0, tiled=True),
        lax.all_gather(w_out, "blk", axis=0, tiled=True),
        lax.all_gather(ln2_gain, "blk", axis=0, tiled=True),
        lax.all_gather(w_router, "blk", axis=0, tiled=True),
    )
    input_rows = inputs.astype(jnp.float32)
    normed_one, norm_one_pull = jax.vjp(layer_norm, input_rows, gain_one.astype(jnp.float32))
    normed_low = normed_one.astype(jnp.bfloat16)
    qkv_rows = jnp.dot(normed_low, qkv_weight, preferred_element_type=jnp.float32).astype(
        jnp.bfloat16
    )
    query_heads, key_heads, value_heads = (
        lax.all_to_all(qkv_rows[:, :model_width], "head", split_axis=1, concat_axis=0, tiled=True),
        lax.all_to_all(
            qkv_rows[:, model_width : 2 * model_width],
            "head",
            split_axis=1,
            concat_axis=0,
            tiled=True,
        ),
        lax.all_to_all(
            qkv_rows[:, 2 * model_width :], "head", split_axis=1, concat_axis=0, tiled=True
        ),
    )
    span_rows = query_heads.shape[0]
    head_count = query_heads.shape[1] // HS
    key_all, value_all = (
        lax.all_gather(key_heads, "blk", axis=0, tiled=True),
        lax.all_gather(value_heads, "blk", axis=0, tiled=True),
    )
    total_rows = key_all.shape[0]
    block_count = total_rows // KEY_BLOCK
    scale_factor = HS ** (-0.5)
    query_pos = lax.axis_index("blk") * span_rows + jnp.arange(span_rows, dtype=jnp.int32)
    query_docs = doc_index(query_pos, doc_lengths)
    queries = query_heads.reshape(span_rows, head_count, HS)

    def block_parts(block_index, key_source, value_source):
        first_key = block_index * KEY_BLOCK
        key_rows = lax.dynamic_slice_in_dim(key_source, first_key, KEY_BLOCK, 0).reshape(
            KEY_BLOCK, head_count, HS
        )
        value_rows = lax.dynamic_slice_in_dim(value_source, first_key, KEY_BLOCK, 0).reshape(
            KEY_BLOCK, head_count, HS
        )
        key_docs = doc_index(first_key + jnp.arange(KEY_BLOCK, dtype=jnp.int32), doc_lengths)
        is_live = (key_docs[0] <= query_docs[-1]) & (key_docs[-1] >= query_docs[0])
        same_doc = query_docs[:, None] == key_docs[None, :]
        return (first_key, key_rows, value_rows, same_doc, is_live)

    def block_scores(key_rows, same_doc):
        raw_scores = (
            jnp.einsum("qhd,khd->hqk", queries, key_rows, preferred_element_type=jnp.float32)
            * scale_factor
        )
        return jnp.where(same_doc[None], raw_scores, MASKED)

    def stat_step(block_index, loop_state):
        first_key, key_rows, value_rows, same_doc, is_live = block_parts(
            block_index, key_all, value_all
        )

        def stat_update(current):
            running_max, running_sum = current
            scores = block_scores(key_rows, same_doc)
            new_max = jnp.maximum(running_max, jnp.max(scores, axis=2))
            exp_terms = jnp.where(same_doc[None], jnp.exp(scores - new_max[:, :, None]), 0.0)
            return (
                new_max,
                running_sum * jnp.exp(running_max - new_max) + jnp.sum(exp_terms, axis=2),
            )

        return lax.cond(is_live, stat_update, keep_state, loop_state)

    start_state = (
        jnp.full((head_count, span_rows), MASKED, jnp.float32),
        jnp.zeros((head_count, span_rows), jnp.float32),
    )
    running_max, running_sum = lax.fori_loop(0, block_count, stat_step, start_state)
    log_total = running_max + jnp.log(running_sum)

    def out_step(block_index, loop_state):
        first_key, key_rows, value_rows, same_doc, is_live = block_parts(
            block_index, key_all, value_all
        )

        def out_update(current):
            scores = block_scores(key_rows, same_doc)
            weights = jnp.where(
                same_doc[None], jnp.exp(scores - log_total[:, :, None]), 0.0
            ).astype(jnp.bfloat16)
            return current + jnp.einsum(
                "hqk,khd->qhd", weights, value_rows, preferred_element_type=jnp.float32
            )

        return lax.cond(is_live, out_update, keep_state, loop_state)

    mixed_full = lax.fori_loop(
        0, block_count, out_step, jnp.zeros((span_rows, head_count, HS), jnp.float32)
    )
    mixed_low = mixed_full.reshape(span_rows, head_count * HS).astype(jnp.bfloat16)
    mixed_tokens = lax.all_to_all(mixed_low, "head", split_axis=0, concat_axis=1, tiled=True)
    attended = jnp.dot(mixed_tokens, out_weight, preferred_element_type=jnp.float32)
    hidden_one = input_rows + attended
    normed_two, norm_two_pull = jax.vjp(layer_norm, hidden_one, gain_two.astype(jnp.float32))
    routed_low = normed_two.astype(jnp.bfloat16)
    router_probs, router_pull = jax.vjp(
        router, routed_low.astype(jnp.float32), router_weight.astype(jnp.float32)
    )
    slot_ids = slot_table(routes, priority[0], capacity)
    select = (
        slot_ids[:, :, None] == jnp.arange(slot_total, dtype=jnp.int32)[None, None, :]
    ).astype(jnp.bfloat16)
    send_rows = jnp.einsum(
        "kts,td->sd", select, routed_low, preferred_element_type=jnp.float32
    ).astype(jnp.bfloat16)
    expert_rows = lax.all_to_all(
        send_rows.reshape(blk_size, capacity, model_width),
        "blk",
        split_axis=0,
        concat_axis=0,
        tiled=True,
    ).reshape(slot_total, model_width)
    weight_in = expert_in[0]
    weight_out = expert_out[0]
    pre_act = jnp.dot(expert_rows, weight_in, preferred_element_type=jnp.float32)
    hidden_act, gelu_pull = jax.vjp(gelu_exact, pre_act)
    hidden_low = hidden_act.astype(jnp.bfloat16)
    expert_result = jnp.dot(hidden_low, weight_out, preferred_element_type=jnp.float32).astype(
        jnp.bfloat16
    )
    slot_result = lax.all_to_all(
        expert_result.reshape(blk_size, capacity, model_width),
        "blk",
        split_axis=0,
        concat_axis=0,
        tiled=True,
    ).reshape(slot_total, model_width)
    pair_result = jnp.einsum("kts,sd->ktd", select, slot_result, preferred_element_type=jnp.float32)
    route_hot = (routes[:, :, None] == jnp.arange(blk_size, dtype=jnp.int32)[None, None, :]).astype(
        jnp.float32
    )
    gate_vals = jnp.sum(router_probs[:, None, :] * route_hot, axis=2)
    mixture = gate_vals[:, 0, None] * pair_result[0] + gate_vals[:, 1, None] * pair_result[1]
    output = (hidden_one + mixture).astype(jnp.bfloat16)
    d_gates = jnp.transpose(jnp.sum(d_out[None] * pair_result, axis=2))
    d_probs = jnp.sum(d_gates[:, :, None] * route_hot, axis=1)
    pair_grads = (jnp.transpose(gate_vals)[:, :, None] * d_out[None]).astype(jnp.bfloat16)
    slot_grads = jnp.einsum(
        "kts,ktd->sd", select, pair_grads, preferred_element_type=jnp.float32
    ).astype(jnp.bfloat16)
    result_grads = lax.all_to_all(
        slot_grads.reshape(blk_size, capacity, model_width),
        "blk",
        split_axis=0,
        concat_axis=0,
        tiled=True,
    ).reshape(slot_total, model_width)
    d_hidden_act = jnp.dot(result_grads, weight_out.T, preferred_element_type=jnp.float32)
    d_weight_out = jnp.dot(hidden_low.T, result_grads, preferred_element_type=jnp.float32)
    d_preact = gelu_pull(d_hidden_act)[0].astype(jnp.bfloat16)
    d_weight_in = jnp.dot(expert_rows.T, d_preact, preferred_element_type=jnp.float32)
    row_grads = jnp.dot(d_preact, weight_in.T, preferred_element_type=jnp.float32).astype(
        jnp.bfloat16
    )
    slot_back = lax.all_to_all(
        row_grads.reshape(blk_size, capacity, model_width),
        "blk",
        split_axis=0,
        concat_axis=0,
        tiled=True,
    ).reshape(slot_total, model_width)
    d_routed = jnp.einsum("kts,sd->td", select, slot_back, preferred_element_type=jnp.float32)
    d_routed_router, d_router = router_pull(d_probs)
    d_hidden_norm, d_gain_two = norm_two_pull(d_routed + d_routed_router)
    d_hidden_one = d_out + d_hidden_norm
    attn_grads = d_hidden_one.astype(jnp.bfloat16)
    d_out_weight = jnp.dot(mixed_tokens.T, attn_grads, preferred_element_type=jnp.float32)
    mixed_grads = jnp.dot(attn_grads, out_weight.T, preferred_element_type=jnp.float32).astype(
        jnp.bfloat16
    )
    head_grads = lax.all_to_all(mixed_grads, "head", split_axis=1, concat_axis=0, tiled=True)
    out_grads = head_grads.reshape(span_rows, head_count, HS)
    row_delta = jnp.transpose(jnp.sum(out_grads.astype(jnp.float32) * mixed_full, axis=2))
    key_back, value_back = (
        lax.all_gather(key_heads, "blk", axis=0, tiled=True),
        lax.all_gather(value_heads, "blk", axis=0, tiled=True),
    )

    def grad_step(block_index, loop_state):
        first_key, key_rows, value_rows, same_doc, is_live = block_parts(
            block_index, key_back, value_back
        )

        def grad_update(current):
            query_grad, key_grad, value_grad = current
            scores = block_scores(key_rows, same_doc)
            weights = jnp.where(same_doc[None], jnp.exp(scores - log_total[:, :, None]), 0.0)
            value_part = jnp.einsum(
                "hqk,qhd->khd",
                weights.astype(jnp.bfloat16),
                out_grads,
                preferred_element_type=jnp.float32,
            )
            weight_grads = jnp.einsum(
                "qhd,khd->hqk", out_grads, value_rows, preferred_element_type=jnp.float32
            )
            score_grads = (weights * (weight_grads - row_delta[:, :, None])).astype(jnp.bfloat16)
            query_grad = (
                query_grad
                + jnp.einsum(
                    "hqk,khd->qhd", score_grads, key_rows, preferred_element_type=jnp.float32
                )
                * scale_factor
            )
            key_part = (
                jnp.einsum("hqk,qhd->khd", score_grads, queries, preferred_element_type=jnp.float32)
                * scale_factor
            )
            key_grad = lax.dynamic_update_slice_in_dim(
                key_grad, key_part.reshape(KEY_BLOCK, head_count * HS), first_key, 0
            )
            value_grad = lax.dynamic_update_slice_in_dim(
                value_grad, value_part.reshape(KEY_BLOCK, head_count * HS), first_key, 0
            )
            return (query_grad, key_grad, value_grad)

        return lax.cond(is_live, grad_update, keep_state, loop_state)

    start_grads = (
        jnp.zeros((span_rows, head_count, HS), jnp.float32),
        jnp.zeros((total_rows, head_count * HS), jnp.float32),
        jnp.zeros((total_rows, head_count * HS), jnp.float32),
    )
    query_grad, key_grad, value_grad = lax.fori_loop(0, block_count, grad_step, start_grads)
    key_own, value_own = (
        lax.psum_scatter(
            key_grad.astype(jnp.bfloat16), "blk", scatter_dimension=0, tiled=True
        ).astype(jnp.float32),
        lax.psum_scatter(
            value_grad.astype(jnp.bfloat16), "blk", scatter_dimension=0, tiled=True
        ).astype(jnp.float32),
    )
    query_tokens_grad, key_tokens_grad, value_tokens_grad = (
        lax.all_to_all(
            query_grad.reshape(span_rows, head_count * HS).astype(jnp.bfloat16),
            "head",
            split_axis=0,
            concat_axis=1,
            tiled=True,
        ),
        lax.all_to_all(
            key_own.astype(jnp.bfloat16), "head", split_axis=0, concat_axis=1, tiled=True
        ),
        lax.all_to_all(
            value_own.astype(jnp.bfloat16), "head", split_axis=0, concat_axis=1, tiled=True
        ),
    )
    qkv_grads = jnp.concatenate([query_tokens_grad, key_tokens_grad, value_tokens_grad], axis=1)
    d_qkv_weight = jnp.dot(normed_low.T, qkv_grads, preferred_element_type=jnp.float32)
    normed_grads = jnp.dot(qkv_grads, qkv_weight.T, preferred_element_type=jnp.float32)
    d_inputs_norm, d_gain_one = norm_one_pull(normed_grads)
    d_inputs = d_hidden_one + d_inputs_norm
    gain_one_sum, qkv_sum, out_sum, gain_two_sum, router_sum = (
        lax.psum_scatter(
            d_gain_one.astype(jnp.bfloat16), "blk", scatter_dimension=0, tiled=True
        ).astype(jnp.float32),
        lax.psum_scatter(
            d_qkv_weight.astype(jnp.bfloat16), "blk", scatter_dimension=0, tiled=True
        ).astype(jnp.float32),
        lax.psum_scatter(
            d_out_weight.astype(jnp.bfloat16), "blk", scatter_dimension=0, tiled=True
        ).astype(jnp.float32),
        lax.psum_scatter(
            d_gain_two.astype(jnp.bfloat16), "blk", scatter_dimension=0, tiled=True
        ).astype(jnp.float32),
        lax.psum_scatter(
            d_router.astype(jnp.bfloat16), "blk", scatter_dimension=0, tiled=True
        ).astype(jnp.float32),
    )
    gain_one_all, qkv_all, out_all, gain_two_all, router_all, expert_in_all, expert_out_all = (
        lax.psum(gain_one_sum.astype(jnp.bfloat16), "head").astype(jnp.float32),
        lax.psum(qkv_sum.astype(jnp.bfloat16), "head").astype(jnp.float32),
        lax.psum(out_sum.astype(jnp.bfloat16), "head").astype(jnp.float32),
        lax.psum(gain_two_sum.astype(jnp.bfloat16), "head").astype(jnp.float32),
        lax.psum(router_sum.astype(jnp.bfloat16), "head").astype(jnp.float32),
        lax.psum(d_weight_in[None].astype(jnp.bfloat16), "head").astype(jnp.float32),
        lax.psum(d_weight_out[None].astype(jnp.bfloat16), "head").astype(jnp.float32),
    )
    return (
        output,
        d_inputs,
        gain_one_all,
        qkv_all,
        out_all,
        gain_two_all,
        router_all,
        expert_in_all,
        expert_out_all,
    )


MESH = pl.DeviceIdType.MESH
LANES = 128
HALF = LANES // 2
MIB = 2**20
F32 = jnp.float32
BF16 = jnp.bfloat16


def dot(left, right, dims=(1, 0)):
    return lax.dot_general(
        left, right, (((dims[0],), (dims[1],)), ((), ())), preferred_element_type=F32
    )


def remote(src, dst, send_sem, recv_sem, head, blk):
    return pltpu.make_async_remote_copy(
        src_ref=src,
        dst_ref=dst,
        send_sem=send_sem,
        recv_sem=recv_sem,
        device_id={"head": head, "blk": blk},
        device_id_type=MESH,
    )


def arrived(ref, sem):
    pltpu.make_async_copy(ref, ref, sem).wait()


def greet(peers):
    barrier = pltpu.get_barrier_semaphore()
    for head, blk in peers:
        pl.semaphore_signal(
            barrier, inc=1, device_id={"head": head, "blk": blk}, device_id_type=MESH
        )
    return len(peers)


def meet(count):
    pl.semaphore_wait(pltpu.get_barrier_semaphore(), count)


def halves(values, lanes_kept):
    rows = values.shape[0] // 2
    moved = pltpu.roll(values[rows:], HALF, 1)
    return jnp.where(lanes_kept, values[:rows], moved)


def lane_ids(shape):
    return lax.broadcasted_iota(jnp.int32, shape, len(shape) - 1)


def centre(values):
    average = jnp.mean(values, axis=-1, keepdims=True)
    centred = values - average
    spread = jnp.mean(centred * centred, axis=-1, keepdims=True)
    scale = lax.rsqrt(spread + EPSILON)
    return centred * scale, scale


def centre_back(grad, xhat, scale):
    middle = jnp.mean(grad, axis=-1, keepdims=True)
    along = jnp.mean(grad * xhat, axis=-1, keepdims=True)
    return (grad - middle - xhat * along) * scale


def split_high_low(column, lanes):
    high = column.astype(BF16)
    low = (column - high.astype(F32)).astype(BF16)
    return jnp.where(lanes < HALF, high.astype(F32), low.astype(F32)).astype(BF16)


def join_high_low(matrix, start):
    return matrix[:, start : start + 1].astype(F32) + matrix[
        :, start + HALF : start + HALF + 1
    ].astype(F32)


def place():
    head, blk = lax.axis_index("head"), lax.axis_index("blk")
    return head, blk, blk // 2, lax.rem(blk, 2)


def around(index, step, size):
    return lax.rem(index + step, size)


QUERY_TILE = 256
CHAINS = 2


def masked_queries(q_ref, tile, key_lanes, query_tile):
    tiles_per_span = q_ref.shape[1] // query_tile
    inner = tile % tiles_per_span * query_tile
    query = q_ref[tile // tiles_per_span, inner : inner + query_tile, :]
    return jnp.where(key_lanes, query, jnp.zeros_like(query))


def group_blocks(bounds_ref, group, size, key_tile):
    first, last = group * size, (group + 1) * size
    low = jnp.min(bounds_ref[0:1, first : first + LANES])
    high = jnp.max(bounds_ref[1:2, last - LANES : last])
    return low // key_tile, (high + key_tile - 1) // key_tile


def inside_document(bounds_ref, tile, first, shape):
    key = first + lax.broadcasted_iota(jnp.int32, shape, 0)
    columns = slice(tile * shape[1], (tile + 1) * shape[1])
    return jnp.logical_and(key >= bounds_ref[0:1, columns], key < bounds_ref[1:2, columns])


def query_group(q_ref, group, y):
    key_lanes = (lane_ids((QUERY_TILE, LANES)) < HALF) == (y == 0)
    tiles = range(group * CHAINS, (group + 1) * CHAINS)
    return tiles, [masked_queries(q_ref, tile, key_lanes, QUERY_TILE) for tile in tiles]


def attend(bounds_ref, tiles, first, keys, keys_across, queries, carry):
    scores = [dot(keys, query, (1, 1)) for query in queries]
    made = []
    for tile, score, (biggest, weight, mixed) in zip(tiles, scores, carry):
        inside = inside_document(bounds_ref, tile, first, score.shape)
        score = jnp.where(inside, score, MASKED)
        bigger = jnp.maximum(biggest, jnp.max(score, axis=0, keepdims=True))
        fade = jnp.exp(biggest - bigger)
        terms = jnp.exp(score - bigger)
        weight = weight * fade + jnp.sum(terms, axis=0, keepdims=True)
        made.append((bigger, weight, mixed * fade + dot(keys_across, terms.astype(BF16))))
    return tuple(made)


def nothing_attended():
    return (
        jnp.full((1, QUERY_TILE), MASKED, F32),
        jnp.zeros((1, QUERY_TILE), F32),
        jnp.zeros((LANES, QUERY_TILE), F32),
    )


def attend_back(bounds_ref, tiles, first, keys, keys_across, group, carry):
    queries, out_grads, deltas, log_totals = group
    scores = [dot(keys, query, (1, 1)) for query in queries]
    weight_grads = [dot(keys, out_grad, (1, 1)) for out_grad in out_grads]
    pieces, score_grads = [], []
    for i, tile in enumerate(tiles):
        inside = inside_document(bounds_ref, tile, first, scores[i].shape)
        weights = jnp.exp(jnp.where(inside, scores[i], MASKED) - log_totals[i])
        score_grads.append((weights * (weight_grads[i] - deltas[i])).astype(BF16))
        pieces.append(weights.astype(BF16))
    wide = jnp.concatenate(score_grads + pieces, axis=1)
    given = dot(wide, jnp.concatenate(queries + out_grads, axis=0))
    return given, tuple(c + dot(keys_across, g) for c, g in zip(carry, score_grads))


def group_grads(do_ref, tiles, y):
    key_lanes = (lane_ids((QUERY_TILE, LANES)) < HALF) == (y == 0)
    out_grads = []
    for tile in tiles:
        parts = []
        for part in range(QUERY_TILE // LANES):
            packed = do_ref[tile, part].astype(F32)
            parts += [packed, pltpu.roll(packed, HALF, 1)]
        out_grads.append(jnp.where(key_lanes, 0.0, jnp.concatenate(parts, axis=0)).astype(BF16))
    return out_grads


def qkv_kernel(
    heads, blks,
    x_hbm, w_hbm, g1_hbm, wo_hbm, wr_hbm, g2_hbm, docs_hbm,
    qall, kvall, xall, wall, wo_all, kvt, bounds, begun,
    x_ref, w_ref, rows_in, g1_ref, g2_ref, wr_ref, docs_ref, wo_own, kv_other, q_packed, q_landed, in_sem,
    x_send, x_recv, w_send, w_recv, o_send, o_recv, p_send, p_recv,
    k_send, k_recv, q_recv,
):
    head, blk, z, y = place()
    planes = blks // 2
    model = x_ref.shape[1]
    rows = w_ref.shape[0]
    part = rows // heads
    experts = wr_ref.shape[0]
    wanted = (
        (w_hbm, w_ref), (g1_hbm, g1_ref), (g2_hbm, g2_ref), (wr_hbm, wr_ref), (x_hbm, x_ref),
        (wo_hbm, wo_own.at[:, pl.ds(0, model)]), (docs_hbm, docs_ref),
    )
    fetched = [
        pltpu.make_async_copy(src, dst, in_sem.at[i]) for i, (src, dst) in enumerate(wanted)
    ]
    for copy in fetched:
        copy.start()
    rows_in[...] = jnp.zeros_like(rows_in)
    met = greet(
        [(around(head, k, heads), blk) for k in range(1, heads)]
        + [(head, around(blk, k, blks)) for k in range(1, blks)]
    )
    lanes = lane_ids((rows, LANES))
    for copy in fetched:
        copy.wait()
    rows_in[0:experts, 0:rows] = wr_ref[...].astype(F32)
    rows_in[experts : experts + 1, 0:rows] = g2_ref[...].astype(F32)
    rows_in[experts + 1 : experts + 2, 0:rows] = g1_ref[...].astype(F32)
    vectors = jnp.transpose(rows_in[...])[:rows]
    gain = vectors[:, experts + 1 : experts + 2]

    def columns(which):
        start = pl.multiple_of(which * model + head * LANES, LANES)
        return w_ref[:, pl.ds(start, LANES)].astype(F32) * gain

    key_cols = columns(1)
    value_cols = pltpu.roll(columns(2), HALF, 1)
    wall[blk, :, 0:LANES] = jnp.where(lanes < HALF, key_cols, value_cols).astype(BF16)
    wall[blk, :, LANES : 2 * LANES] = jnp.where(lanes < HALF, value_cols, key_cols).astype(BF16)
    wall[blk, :, 2 * LANES : 3 * LANES] = (columns(0) * HS ** (-0.5)).astype(BF16)
    def slice_copy(slot, source, target):
        ref = wall.at[source]
        return remote(ref, ref, w_send.at[slot], w_recv.at[source], head, target)

    pair = 2 * z + around(y, 1, 2)
    line = [2 * around(z, step, planes) + y for step in (1, planes - 1, *range(2, planes - 1))]
    w_copies = [slice_copy(slot, blk, target) for slot, target in enumerate((*line, pair))]
    w_onward = [slice_copy(planes + slot, source, pair) for slot, source in enumerate(line)]
    xhat, _ = centre(x_ref[...].astype(F32))
    xall[head] = xhat.astype(BF16)
    meet(met)
    for copy in w_copies:
        copy.start()
    x_copies = [
        remote(xall.at[head], xall.at[head], x_send.at[k], x_recv.at[k], around(head, k, heads), blk)
        for k in range(1, heads)
    ]
    for copy in x_copies:
        copy.start()
    wo_own[:, model : model + LANES] = vectors.astype(BF16)
    wo_all[blk, head] = wo_own[pl.ds(pl.multiple_of(head * part, part), part), :]
    o_copies = [
        remote(
            wo_all.at[blk, head], wo_all.at[blk, head],
            o_send.at[k], o_recv.at[k], head, around(blk, k, blks),
        )
        for k in range(1, blks)
    ]
    document_bounds(docs_ref, bounds, z)
    for source, copy in zip(line, w_onward):
        arrived(wall.at[source], w_recv.at[source])
        copy.start()
    for copy in o_copies:
        copy.start()
    for source in (pair, *[other - y + around(y, 1, 2) for other in line]):
        arrived(wall.at[source], w_recv.at[source])
    for copy in w_copies + w_onward:
        copy.wait_send()
    for copy in x_copies:
        copy.wait()
    weight = wall[...].reshape(model, 3 * LANES)
    tokens = x_ref.shape[0]
    even = y == 0
    above, below = z < planes - 1, z > 0
    half_span = kvall.shape[1] // 2
    sides = ((1, above, below, 0), (-1, below, above, 4))

    def half_of(ref, half):
        return ref.at[pl.ds(half * half_span, half_span)]

    def outward(slot, step, across, half):
        target = 2 * (z + step) + around(y, across, 2)
        return remote(
            half_of(kv_other if across else kvall.at[blk], half), half_of(kvall.at[blk], half),
            k_send.at[slot], k_recv.at[blk, half], head, target,
        )

    def onward(slot, step, side, half):
        from_span = 2 * (z - step) + side
        ref = half_of(kvall.at[from_span], half)
        return remote(ref, ref, k_send.at[slot], k_recv.at[from_span, half], head, 2 * (z + step) + y)

    def await_half(span, half):
        arrived(half_of(kvall.at[span], half), k_recv.at[span, half])

    def turn(span):
        size = kvall.shape[1]
        kvt[:, pl.ds(pl.multiple_of(span * size, size), size)] = jnp.transpose(kvall[span])

    for half in range(2):
        for piece in range(half * heads // 2, (half + 1) * heads // 2):
            made = dot(xall[piece], weight).astype(BF16)
            first, second = made[:, 0:LANES], made[:, LANES : 2 * LANES]
            span = slice(piece * tokens, (piece + 1) * tokens)
            kvall[blk, span, :] = jnp.where(even, first, second)
            kv_other[span, :] = jnp.where(even, second, first)
            qall[y, span, :] = made[:, 2 * LANES : 3 * LANES]
        outward(8 + half, 0, 1, half).start()
        for step, there, _, slot in sides:

            @pl.when(there)
            def _():
                outward(slot + 2 * half, step, 0, half).start()
                outward(slot + 2 * half + 1, step, 1, half).start()

    other_y = around(y, 1, 2)
    kept = (lane_ids(q_packed.shape) < HALF) == (y == 1)
    q_packed[...] = halves(qall[y].astype(F32), kept).astype(BF16)
    q_pair = remote(q_packed, q_landed, k_send.at[10], q_recv, head, 2 * z + other_y)
    q_pair.start()
    turn(blk)
    for copy in o_copies:
        copy.wait()
    core = lax.rem(head, 2)
    sibling, across = head - core + 1 - core, around(head, 2, heads)

    def quarter_copy(index, quarter, to_head):
        ref = wo_all.at[:, quarter]
        return remote(ref, ref, p_send.at[index], p_recv.at[index], to_head, blk)

    p_copies = [quarter_copy(0, head, sibling), quarter_copy(1, head, across)]
    for copy in p_copies:
        copy.start()
    p_copies.append(quarter_copy(2, across, sibling))
    for half in range(2):
        for step, there, back, slot in sides:

            @pl.when(back)
            def _():
                for side in range(2):
                    await_half(2 * (z - step) + side, half)

            @pl.when(jnp.logical_and(there, back))
            def _():
                for side in range(2):
                    onward(11 + slot + 2 * half + side, step, side, half).start()

    arrived(wo_all.at[:, across], p_recv.at[1])
    p_copies[2].start()
    for half in range(2):
        await_half(pair, half)
    turn(pair)
    q_pair.wait()
    landed = q_landed[...]
    qall[other_y, 0:half_span, :] = landed
    qall[other_y, half_span : 2 * half_span, :] = pltpu.roll(landed.astype(F32), HALF, 1).astype(BF16)
    key_tile = kvall.shape[1]
    for group in range(2 * key_tile // (CHAINS * QUERY_TILE)):
        tiles, queries = query_group(qall, group, y)
        carry = (nothing_attended(),) * CHAINS
        for side in range(2):
            first = pl.multiple_of((2 * z + side) * key_tile, key_tile)
            keys_across = kvt[:, pl.ds(first, key_tile)]
            carry = attend(bounds, tiles, first, kvall[2 * z + side], keys_across, queries, carry)
        for tile, (biggest, weight, mixed) in zip(tiles, carry):
            begun[tile, 0:LANES] = mixed
            begun[tile, LANES : LANES + 8] = jnp.broadcast_to(biggest, (8, QUERY_TILE))
            begun[tile, LANES + 8 : LANES + 16] = jnp.broadcast_to(weight, (8, QUERY_TILE))
    for step, there, back, slot in sides:

        @pl.when(back)
        def _():
            for side in range(2):
                turn(2 * (z - step) + side)

    for other in range(planes):
        for side in range(2):
            span = 2 * other + side

            @pl.when(jnp.logical_or(z - other == 2, other - z == 2))
            def _():
                for half in range(2):
                    await_half(span, half)
                turn(span)

    for index, quarter in ((0, sibling), (2, around(sibling, 2, heads))):
        arrived(wo_all.at[:, quarter], p_recv.at[index])
    for copy in p_copies:
        copy.wait_send()
    for half in range(2):
        outward(8 + half, 0, 1, half).wait_send()
        for step, there, back, slot in sides:

            @pl.when(there)
            def _():
                outward(slot + 2 * half, step, 0, half).wait_send()
                outward(slot + 2 * half + 1, step, 1, half).wait_send()

            @pl.when(jnp.logical_and(there, back))
            def _():
                for side in range(2):
                    onward(11 + slot + 2 * half + side, step, side, half).wait_send()


def document_bounds(docs_ref, bounds, z):
    count = docs_ref.shape[1]
    lengths = docs_ref[...].astype(F32)
    doc = lax.broadcasted_iota(jnp.int32, (count, count), 0)
    other = lane_ids((count, count))
    start = jnp.sum(jnp.where(other < doc, lengths, 0.0), axis=1, keepdims=True)
    end = jnp.sum(jnp.where(other <= doc, lengths, 0.0), axis=1, keepdims=True)
    queries = bounds.shape[1]
    token = (z * queries + lane_ids((count, queries))).astype(F32)
    begun = start <= token
    bounds[...] = jnp.zeros_like(bounds)
    bounds[0:1, :] = jnp.max(jnp.where(begun, start, 0.0), axis=0, keepdims=True).astype(jnp.int32)
    bounds[1:2, :] = jnp.max(jnp.where(begun, end, 0.0), axis=0, keepdims=True).astype(jnp.int32)


def vmem_specs(count):
    return [pl.BlockSpec(memory_space=pltpu.VMEM)] * count


def hbm_specs(count):
    return [pl.BlockSpec(memory_space=pltpu.HBM)] * count


def in_hbm(*arrays):
    return [pltpu.with_memory_space_constraint(array, pltpu.HBM) for array in arrays]


def dma(*shape):
    return pltpu.SemaphoreType.DMA(shape)


def call_qkv(x, w_qkv, g1, w_out, w_router, g2, doc_lengths, heads, blks):
    tokens, model = x.shape
    rows = w_qkv.shape[0]
    span = tokens * heads
    wide = model + LANES
    part = rows // heads
    return pl.pallas_call(
        functools.partial(qkv_kernel, heads, blks),
        out_shape=(
            jax.ShapeDtypeStruct((2, span, LANES), BF16),
            jax.ShapeDtypeStruct((blks, span, LANES), BF16),
            jax.ShapeDtypeStruct((heads, tokens, model), BF16),
            jax.ShapeDtypeStruct((blks, rows, 3 * LANES), BF16),
            jax.ShapeDtypeStruct((blks, heads, part, wide), BF16),
            jax.ShapeDtypeStruct((LANES, blks * span), BF16),
            jax.ShapeDtypeStruct((8, 2 * span), jnp.int32),
            jax.ShapeDtypeStruct((2 * span // QUERY_TILE, LANES + 16, QUERY_TILE), F32),
        ),
        in_specs=hbm_specs(7),
        out_specs=tuple(vmem_specs(8)),
        scratch_shapes=[
            pltpu.VMEM((tokens, model), BF16),
            pltpu.VMEM((rows, 3 * model), BF16),
            pltpu.VMEM((LANES, LANES), F32),
            pltpu.VMEM((1, rows), BF16),
            pltpu.VMEM((1, rows), BF16),
            pltpu.VMEM((w_router.shape[1], rows), BF16),
            pltpu.VMEM((1, doc_lengths.shape[0]), jnp.int32),
            pltpu.VMEM((rows, wide), BF16),
            pltpu.VMEM((span, LANES), BF16),
            pltpu.VMEM((span // 2, LANES), BF16),
            pltpu.VMEM((span // 2, LANES), BF16),
            dma(7),
            dma(heads), dma(heads), dma(blks), dma(blks), dma(blks), dma(blks), dma(heads), dma(heads),
            dma(19), dma(blks, 2), pltpu.SemaphoreType.DMA,
        ],
        compiler_params=pltpu.CompilerParams(
            collective_id=1, has_side_effects=True, vmem_limit_bytes=16 * MIB
        ),
        name="qkv",
    )(
        *in_hbm(
            x, w_qkv, g1.reshape(1, rows), w_out, w_router.T, g2.reshape(1, rows),
            doc_lengths.reshape(1, -1),
        )
    )


def other_blocks(bounds_ref, group, key_tile, z, step, carry):
    low, high = group_blocks(bounds_ref, group, CHAINS * QUERY_TILE, key_tile)
    carry = lax.fori_loop(low, 2 * z, step, carry)
    return lax.fori_loop(2 * z + 2, high, step, carry)


def forward_kernel(bounds_ref, q_ref, kv_ref, kvt_ref, begun_ref, o_out, ob_out, lse_out):
    _, _, z, y = place()
    key_tile = kv_ref.shape[1]
    value_lanes = (lane_ids((HALF, LANES)) < HALF) == (y == 1)
    for group in range(q_ref.shape[0] * q_ref.shape[1] // (CHAINS * QUERY_TILE)):
        tiles, queries = query_group(q_ref, group, y)

        def step(block, carry, queries=queries, tiles=tiles):
            first = pl.multiple_of(block * key_tile, key_tile)
            across = kvt_ref[:, pl.ds(first, key_tile)]
            return attend(bounds_ref, tiles, first, kv_ref[block], across, queries, carry)

        start = tuple(
            (begun_ref[t, LANES : LANES + 1], begun_ref[t, LANES + 8 : LANES + 9], begun_ref[t, 0:LANES])
            for t in tiles
        )
        ends = other_blocks(bounds_ref, group, key_tile, z, step, start)
        for tile, (biggest, weight, mixed) in zip(tiles, ends):
            result = jnp.transpose(mixed / weight)
            o_out[tile] = result
            for part in range(QUERY_TILE // LANES):
                block = result[part * LANES : (part + 1) * LANES]
                ob_out[tile, part] = halves(block, value_lanes).astype(BF16)
            lse_out[tile] = jnp.broadcast_to(biggest + jnp.log(weight), (8, QUERY_TILE))


def call_forward(bounds, q, kv, kvt, begun):
    blks, span, _ = kv.shape
    tiles = 2 * span // QUERY_TILE
    return pl.pallas_call(
        forward_kernel,
        out_shape=(
            jax.ShapeDtypeStruct((tiles, QUERY_TILE, LANES), F32),
            jax.ShapeDtypeStruct((tiles, QUERY_TILE // LANES, HALF, LANES), BF16),
            jax.ShapeDtypeStruct((tiles, 8, QUERY_TILE), F32),
        ),
        in_specs=vmem_specs(5),
        out_specs=tuple(vmem_specs(3)),
        compiler_params=pltpu.CompilerParams(vmem_limit_bytes=16 * MIB),
        name="attend",
    )(bounds, q, kv, kvt, begun)


def backward_kernel(
    bounds_ref, q_ref, kv_ref, kvt_ref, do_ref, o_ref, lse_ref, dq_out, dkv_out, delta_out, dkv
):
    _, _, z, y = place()
    key_tile = kv_ref.shape[1]
    dkv[...] = jnp.zeros_like(dkv)
    for group in range(q_ref.shape[0] * q_ref.shape[1] // (CHAINS * QUERY_TILE)):
        tiles, queries = query_group(q_ref, group, y)
        out_grads = group_grads(do_ref, tiles, y)
        deltas, log_totals = [], []
        for tile, out_grad in zip(tiles, out_grads):
            product = jnp.transpose(out_grad.astype(F32) * o_ref[tile])
            deltas.append(jnp.sum(product, axis=0, keepdims=True))
            delta_out[tile] = jnp.broadcast_to(deltas[-1], delta_out.shape[1:])
            log_totals.append(lse_ref[tile, 0:1, :])
        known = (queries, out_grads, deltas, log_totals)

        def step(block, carry, tiles=tiles, known=known):
            first = pl.multiple_of(block * key_tile, key_tile)
            across = kvt_ref[:, pl.ds(first, key_tile)]
            given, carry = attend_back(bounds_ref, tiles, first, kv_ref[block], across, known, carry)
            dkv[block] += given
            return carry

        zero = jnp.zeros((LANES, QUERY_TILE), F32)
        ends = other_blocks(bounds_ref, group, key_tile, z, step, (zero,) * CHAINS)
        for tile, mixed in zip(tiles, ends):
            dq_out[tile] = mixed
    for block in range(dkv.shape[0]):
        dkv_out[block] = dkv[block].astype(BF16)


def call_backward(bounds, q, kv, kvt, d_o, o, lse):
    blks, span, _ = kv.shape
    tiles = 2 * span // QUERY_TILE
    return pl.pallas_call(
        backward_kernel,
        out_shape=(
            jax.ShapeDtypeStruct((tiles, LANES, QUERY_TILE), F32),
            jax.ShapeDtypeStruct((blks, span, LANES), BF16),
            jax.ShapeDtypeStruct((tiles, 8, QUERY_TILE), F32),
        ),
        in_specs=vmem_specs(7),
        out_specs=tuple(vmem_specs(3)),
        scratch_shapes=[pltpu.VMEM((blks, span, LANES), F32)],
        compiler_params=pltpu.CompilerParams(vmem_limit_bytes=16 * MIB),
        name="attend_back",
    )(bounds, q, kv, kvt, d_o, o, lse)


def gelu_parts(values):
    share = 0.5 * (1.0 + lax.erf(values * (2.0**-0.5)))
    slope = share + values * jnp.exp(-0.5 * values * values) * (2.0 * math.pi) ** -0.5
    return values * share, slope


def positions(expert_rows, expert_cols, rank_row, rank_col):
    def count(mask, axis):
        return jnp.sum(mask.astype(F32), axis=axis, keepdims=True)

    row = [None, None]
    col = [None, None]
    before = rank_col < rank_row
    after = rank_row < rank_col
    for choice in range(2):
        row[choice] = count((expert_cols[choice] == expert_rows[choice]) & before, 0)
        col[choice] = count((expert_rows[choice] == expert_cols[choice]) & after, 1)
    row[1] = row[1] + count(expert_cols[0] == expert_rows[1], 0)
    col[1] = col[1] + count(expert_rows[0] == expert_cols[1], 1)
    return row, col


def own_columns(rows_ref, turned, blk, capacity):
    blks, _, slots = rows_ref.shape
    rows = jnp.concatenate(
        [rows_ref[...].reshape(blks, slots), jnp.zeros((LANES - blks, slots), F32)], axis=0
    )
    for piece in range(slots // LANES):
        columns = slice(piece * LANES, (piece + 1) * LANES)
        turned[columns, :] = jnp.transpose(rows[:, columns])
    own = turned[pl.ds(pl.multiple_of(blk * capacity, capacity), capacity), :]
    return jnp.concatenate([own[:, source : source + 1] for source in range(blks)], axis=0)


def middle_kernel(
    heads, blks,
    x_hbm, o_ref, wo_ref, routes_hbm, rank_hbm, d_out_hbm, win_hbm, wout_hbm,
    po, pa, hidden_ref, share_ref, dh_ref, dma_all, grads_ref, rx,
    x_ref, routes_ref, rank_ref, d_out_ref, win_ref, wout_ref, rows_in, in_sem,
    o_all, dos, doa, rs, ra, dr, da, dms, mix, gate_rows, d_gate_rows, turned,
    o_send, o_recv, dos_send, dos_recv, r_send, r_recv,
    dr_send, dr_recv, dm_send, dm_recv, rx_send, rx_recv, g_send, g_recv, dg_send, dg_recv, pa_send, pa_recv,
):
    head, blk, z, y = place()
    tokens, model = x_ref.shape
    capacity = 2 * tokens // blks
    slots = capacity * blks
    plane = [(k % heads, k // heads) for k in range(1, 2 * heads)]
    wanted = (
        (routes_hbm, routes_ref), (rank_hbm, rank_ref), (d_out_hbm, d_out_ref), (x_hbm, x_ref),
        (win_hbm, win_ref), (wout_hbm, wout_ref),
    )
    fetched = [
        pltpu.make_async_copy(src, dst, in_sem.at[i]) for i, (src, dst) in enumerate(wanted)
    ]
    for copy in fetched:
        copy.start()
    met = greet(
        [(around(head, kh, heads), 2 * z + around(y, ky, 2)) for kh, ky in plane]
        + [(head, around(blk, k, blks)) for k in range(1, blks)]
    )
    meet(met)

    def plane_copies(src_of, dst, send, recv):
        copies = []
        for k, (kh, ky) in enumerate(plane):
            to_head, to_y = around(head, kh, heads), around(y, ky, 2)
            copies.append(
                remote(src_of(to_y, to_head), dst, send.at[k], recv.at[k], to_head, 2 * z + to_y)
            )
        return copies

    def blk_copies(src, dst, send, recv):
        return [
            remote(
                src.at[around(blk, k, blks)], dst.at[blk],
                send.at[k], recv.at[k], head, around(blk, k, blks),
            )
            for k in range(1, blks)
        ]

    def start(copies):
        for copy in copies:
            copy.start()

    def finish(copies):
        for copy in copies:
            copy.wait()

    o_copies = plane_copies(lambda to_y, to_head: o_ref.at[to_y, to_head], o_all.at[y, head], o_send, o_recv)
    start(o_copies)
    o_all[y, head] = o_ref[y, head]

    lanes = lane_ids((tokens, LANES))
    for copy in fetched[:4]:
        copy.wait()
    e_rows = [routes_ref[i : i + 1, :].astype(F32) for i in range(2)]
    rank_row = rank_ref[...].astype(F32)
    rows_in[...] = jnp.zeros_like(rows_in)
    rows_in[0:1, :], rows_in[1:2, :], rows_in[2:3, :] = *e_rows, rank_row
    columns = jnp.transpose(rows_in[...])
    e_cols = [columns[:, 0:1], columns[:, 1:2]]
    rank_col = columns[:, 2:3]
    pos_rows, pos_cols = positions(e_rows, e_cols, rank_row, rank_col)

    def slot_of(expert, position):
        return jnp.where(position < capacity, expert * capacity + position, -1.0).astype(jnp.int32)

    slot_rows = [slot_of(e, p) for e, p in zip(e_rows, pos_rows)]
    slot_cols = [slot_of(e, p) for e, p in zip(e_cols, pos_cols)]
    slot_down = lax.broadcasted_iota(jnp.int32, (slots, tokens), 0)
    slot_across = lane_ids((tokens, slots))
    pick = [(slot_down == s).astype(BF16) for s in slot_rows]
    put = [(slot_across == s).astype(BF16) for s in slot_cols]
    pick_any = pick[0] + pick[1]
    put_any = put[0] + put[1]

    d_out = d_out_ref[...]
    dos[...] = dot(pick_any, d_out.astype(BF16)).astype(BF16).reshape(dos.shape)
    dos_copies = blk_copies(dos, doa, dos_send, dos_recv)
    start(dos_copies)
    doa[blk] = dos[blk]

    weight_out = jnp.concatenate(
        [wo_ref[(b ^ 1) * HALF : ((b ^ 1) + 1) * HALF, 0:model] for b in range(blks)], axis=0
    )
    small = wo_ref[:, model : model + LANES]
    small_across = jnp.concatenate(
        [
            jnp.transpose(small[i * LANES : (i + 1) * LANES].astype(F32))
            for i in range(model // LANES)
        ],
        axis=1,
    )
    gain = small_across[blks : blks + 1, :]

    finish(o_copies)
    low_lanes = lanes[:HALF] < HALF
    for piece in range(heads):
        columns = slice(piece * LANES, (piece + 1) * LANES)
        first, second = o_all[1, piece].astype(F32), o_all[0, piece].astype(F32)
        mix[:HALF, columns] = jnp.where(low_lanes, first, second).astype(BF16)
        swapped = pltpu.roll(jnp.where(low_lanes, second, first), HALF, 1)
        mix[HALF:, columns] = swapped.astype(BF16)
    mixed = mix[...]
    hidden = x_ref[...].astype(F32) + dot(mixed, weight_out)
    xhat, scale = centre(hidden)
    routed = (xhat * gain).astype(BF16)
    rs[...] = dot(pick_any, routed).astype(BF16).reshape(rs.shape)
    r_copies = blk_copies(rs, ra, r_send, r_recv)
    start(r_copies)
    ra[blk] = rs[blk]
    logits = jnp.where(lanes < blks, dot(routed, small), MASKED)
    powers = jnp.exp(logits - jnp.max(logits, axis=1, keepdims=True))
    probs = powers / jnp.sum(powers, axis=1, keepdims=True)
    lanes_f = lanes.astype(F32)
    hots = [lanes_f == e for e in e_cols]
    gates = [jnp.sum(jnp.where(hot, probs, 0.0), axis=1, keepdims=True) for hot in hots]
    gate_high = [g.astype(BF16).astype(F32) for g in gates]
    gate_across = jnp.transpose(
        jnp.where(lanes == 0, gate_high[0], jnp.where(lanes == 1, gates[0] - gate_high[0], 0.0))
        + jnp.where(lanes == 2, gate_high[1], jnp.where(lanes == 3, gates[1] - gate_high[1], 0.0))
    ).astype(BF16)
    by_slot = (dot(gate_across, put[0]), dot(gate_across, put[1]))
    gate_rows[blk] = by_slot[0][0:1] + by_slot[0][1:2] + by_slot[1][2:3] + by_slot[1][3:4]
    g_copies = [
        remote(
            gate_rows.at[blk], gate_rows.at[blk],
            g_send.at[k], g_recv.at[k], head, around(blk, k, blks),
        )
        for k in range(1, blks)
    ]
    start(g_copies)
    finish(dos_copies)
    finish(r_copies)

    out_rows = doa[...].reshape(slots, model)
    rx[head, :, 0:model] = ra[...].reshape(slots, model)
    finish(g_copies)
    gate_col = own_columns(gate_rows, turned, blk, capacity)
    rx[head, :, model : 2 * model] = (out_rows.astype(F32) * gate_col).astype(BF16)
    core = lax.rem(head, 2)
    sibling, across = head - core + 1 - core, around(head, 2, heads)

    def half_rows(source, half):
        return rx.at[source, pl.ds(half * slots // 2, slots // 2)]

    to_across = [
        remote(
            half_rows(head, half), half_rows(head, half),
            rx_send.at[1 + half], rx_recv.at[1 + half], across, blk,
        )
        for half in range(2)
    ]
    to_sibling = remote(rx.at[head], rx.at[head], rx_send.at[0], rx_recv.at[0], sibling, blk)
    forwards = [
        remote(
            half_rows(across, half), half_rows(across, half),
            rx_send.at[3 + half], rx_recv.at[3 + half], sibling, blk,
        )
        for half in range(2)
    ]
    start(to_across)
    to_sibling.start()
    for copy in fetched[4:]:
        copy.wait()
    act, slope = gelu_parts(dot(rx[head, :, 0:model], win_ref[...]))
    d_act = dot(rx[head, :, model : 2 * model], wout_ref[...], (1, 1))
    row_grads = dot((slope * d_act).astype(BF16), win_ref[...], (1, 1))
    dr[...] = row_grads.astype(BF16).reshape(dr.shape)
    dr_copies = blk_copies(dr, da, dr_send, dr_recv)
    start(dr_copies)
    result = dot(act.astype(BF16), wout_ref[...]).astype(BF16)
    d_gate = jnp.sum(out_rows.astype(F32) * result.astype(F32), axis=1, keepdims=True)
    da[blk] = dr[blk]
    d_wide = jnp.broadcast_to(d_gate, (slots, LANES))
    d_gate_rows[blk] = jnp.concatenate(
        [jnp.transpose(d_wide[i * LANES : (i + 1) * LANES])[0:1] for i in range(slots // LANES)],
        axis=1,
    )
    dg_copies = [
        remote(
            d_gate_rows.at[blk], d_gate_rows.at[blk],
            dg_send.at[k], dg_recv.at[k], head, around(blk, k, blks),
        )
        for k in range(1, blks)
    ]
    start(dg_copies)
    po[...] = result.reshape(blks, capacity, model)

    finish(dg_copies)
    back_gate = own_columns(d_gate_rows, turned, blk, capacity)
    back_gate = split_high_low(back_gate, lane_ids((slots, LANES)))
    d_gates = [join_high_low(dot(p, back_gate), 0) for p in put]
    d_probs = jnp.where(hots[0], d_gates[0], 0.0) + jnp.where(hots[1], d_gates[1], 0.0)
    d_logits = probs * (d_probs - jnp.sum(probs * d_probs, axis=1, keepdims=True))
    d_high = d_logits.astype(BF16)
    d_low = (d_logits - d_high.astype(F32)).astype(BF16)
    d_router_part = dot(d_high, small, (1, 1)) + dot(d_low, small, (1, 1))
    finish(dr_copies)
    d_routed = dot(put_any, da[...].reshape(slots, model)) + d_router_part
    d_hidden = d_out + centre_back(d_routed * gain, xhat, scale)
    dh_ref[...] = d_hidden
    d_attn = d_hidden.astype(BF16)
    d_mixed = dot(d_attn, weight_out, (1, 1))
    for piece in range(heads):
        block = d_mixed[:, piece * LANES : (piece + 1) * LANES]
        for to_y in range(2):
            dms[to_y, piece] = halves(block, low_lanes == (to_y == 1)).astype(BF16)
    dm_copies = plane_copies(lambda to_y, to_head: dms.at[to_y, to_head], dma_all.at[y, head], dm_send, dm_recv)
    start(dm_copies)
    dma_all[y, head] = dms[y, head]
    first_half = pa.shape[1]
    pa_copies = [
        remote(
            po.at[around(blk, k, blks), pl.ds(0, first_half)], pa.at[blk],
            pa_send.at[k], pa_recv.at[k], head, around(blk, k, blks),
        )
        for k in range(1, blks)
    ]
    start(pa_copies)
    pa[blk] = po[blk, 0:first_half]
    arrived(half_rows(across, 0), rx_recv.at[1])
    forwards[0].start()

    d_weight = dot(mixed, d_attn, (0, 0)).astype(BF16)
    for b in range(blks):
        grads_ref[b, :, 0:model] = d_weight[(b ^ 1) * HALF : ((b ^ 1) + 1) * HALF, :]
    last = (lanes == blks).astype(BF16)
    d_small = dot(routed, d_high, (0, 0)) + dot((d_routed * xhat).astype(BF16), last, (0, 0))
    grads_ref[:, :, model : model + LANES] = d_small.astype(BF16).reshape(blks, HALF, LANES)
    share = gates[0] * put[0].astype(F32) + gates[1] * put[1].astype(F32)
    share_ref[0] = share.astype(BF16)
    share_ref[1] = (share - share_ref[0].astype(F32)).astype(BF16)
    hidden_ref[...] = hidden

    arrived(half_rows(across, 1), rx_recv.at[2])
    forwards[1].start()
    finish(dm_copies)
    finish(pa_copies)
    to_sibling.wait()
    for copy in to_across:
        copy.wait_send()
    finish(forwards)


def call_middle(x, o, wo, routes, rank, d_out, win, wout, heads, blks):
    tokens, model = x.shape
    capacity = 2 * tokens // blks
    slots = capacity * blks
    wide = model + LANES

    def rows(width):
        return pltpu.VMEM((blks, capacity, width), BF16)

    def block(*lead):
        return pltpu.VMEM((*lead, tokens // 2, LANES), BF16)

    return pl.pallas_call(
        functools.partial(middle_kernel, heads, blks),
        out_shape=(
            jax.ShapeDtypeStruct((blks, capacity, model), BF16),
            jax.ShapeDtypeStruct((blks, capacity // 2, model), BF16),
            jax.ShapeDtypeStruct((tokens, model), F32),
            jax.ShapeDtypeStruct((2, tokens, slots), BF16),
            jax.ShapeDtypeStruct((tokens, model), F32),
            jax.ShapeDtypeStruct((2, heads, tokens // 2, LANES), BF16),
            jax.ShapeDtypeStruct((blks, model // blks, wide), BF16),
            jax.ShapeDtypeStruct((heads, slots, 2 * model), BF16),
        ),
        in_specs=hbm_specs(1) + vmem_specs(2) + hbm_specs(5),
        out_specs=tuple(vmem_specs(8)),
        scratch_shapes=[
            pltpu.VMEM((tokens, model), BF16),
            pltpu.VMEM((2, tokens), jnp.int32),
            pltpu.VMEM((1, tokens), jnp.int32),
            pltpu.VMEM((tokens, model), F32),
            pltpu.VMEM(win.shape, BF16),
            pltpu.VMEM(wout.shape, BF16),
            pltpu.VMEM((tokens, tokens), F32),
            dma(6),
            block(2, heads), rows(model), rows(model), rows(model), rows(model),
            rows(model), rows(model), block(2, heads),
            pltpu.VMEM((tokens, model), BF16),
            pltpu.VMEM((blks, 1, slots), F32), pltpu.VMEM((blks, 1, slots), F32),
            pltpu.VMEM((slots, LANES), F32),
            dma(2 * heads), dma(2 * heads), dma(blks), dma(blks), dma(blks), dma(blks),
            dma(blks), dma(blks), dma(2 * heads), dma(2 * heads), dma(5), dma(5),
            dma(blks), dma(blks), dma(blks), dma(blks), dma(blks), dma(blks),
        ],
        compiler_params=pltpu.CompilerParams(
            collective_id=2, has_side_effects=True, vmem_limit_bytes=20 * MIB
        ),
        name="experts",
    )(*in_hbm(x), o, wo, *in_hbm(routes.T, rank, d_out, win, wout))


def last_kernel(
    heads, blks,
    x_hbm, dh_ref, begun_ref, dkv_ref, xa_ref, wa_ref, w_hbm, g1_hbm, grads_ref, rx_ref, win_hbm, wout_hbm,
    po_ref, pa_ref, hidden_ref, share_ref, bounds_ref, q_ref, kv_ref, kvt_ref, do_ref, lse_ref, delta_ref,
    y_ref, dx_ref, dw_ref, shared_ref, din_ref, dout_ref,
    x_ref, w_ref, g1_ref, win_ref, wout_ref, in_sem,
    gain_tile, far_all, near_send_buf, near_all, pair_all, dq_all, dq_ref, dq_packed, dkv_own, pair_buf, us, ua, gs, ga, gqs, gqa, u_part, xat, pa, gh, ghq, w1, w2s, w2, w3,
    q_send, q_recv, pair_send, pair_recv, far_send, far_recv, near_send, near_recv,
    u_send, u_recv, g_send, g_recv, gh_send, gh_recv, w1_send, w1_recv, w2_send, w2_recv,
    w3_send, w3_recv, e_send, e_recv, gq_send, gq_recv, po_send, po_recv, ghq_send, ghq_recv,
    din_half, dout_half,
):
    head, blk, z, y = place()
    planes = blks // 2
    tokens, model = x_ref.shape
    rows = w_ref.shape[0]
    wanted = (
        (win_hbm, win_ref), (wout_hbm, wout_ref), (x_hbm, x_ref), (w_hbm, w_ref), (g1_hbm, g1_ref)
    )
    fetched = [
        pltpu.make_async_copy(src, dst, in_sem.at[i]) for i, (src, dst) in enumerate(wanted)
    ]
    for copy in fetched:
        copy.start()
    met = greet(
        [(around(head, k, heads), blk) for k in range(1, heads)]
        + [(head, around(blk, k, blks)) for k in range(1, blks)]
    )
    meet(met)

    def start(copies):
        for copy in copies:
            copy.start()

    def finish(copies):
        for copy in copies:
            copy.wait()

    other_y = around(y, 1, 2)
    pair = 2 * z + other_y
    above, below = z < planes - 1, z > 0
    directions = ((1, above, below, 0), (-1, below, above, 2))

    half_span = dkv_ref.shape[1] // 2

    def half_of(ref, half):
        return ref.at[pl.ds(half * half_span, half_span)]

    def far_copy(step, slot, side, half):
        span = 2 * (z + 2 * step) + side
        return remote(
            half_of(dkv_ref.at[span], half), half_of(far_all.at[slot + side], half),
            far_send.at[slot + side, half], far_recv.at[slot + side, half], head, 2 * (z + step) + y,
        )

    def near_copy(step, slot, side, half):
        return remote(
            half_of(near_send_buf.at[slot + side], half), half_of(near_all.at[slot // 2, y], half),
            near_send.at[slot + side, half], near_recv.at[slot // 2, y, half],
            head, 2 * (z + step) + side,
        )

    def two_away(step):
        return z + 2 * step < planes if step > 0 else z + 2 * step >= 0

    for half in range(2):
        for step, there, back, slot in directions:

            @pl.when(two_away(step))
            def _():
                for side in range(2):
                    far_copy(step, slot, side, half).start()

    w1_copies = [
        remote(
            grads_ref.at[:, around(head, k, heads)], w1.at[head],
            w1_send.at[k], w1_recv.at[k], around(head, k, heads), blk,
        )
        for k in range(1, heads)
    ]
    start(w1_copies)
    w1[head] = grads_ref[:, head]

    core = lax.rem(head, 2)
    sibling = head - core + 1 - core
    ff_half = wout_ref.shape[0] // 2
    ff_step = ff_half // 2

    def expert_chunk(chunk):
        here = pl.multiple_of(core * ff_half + chunk * ff_step, ff_step)
        there = pl.multiple_of(chunk * ff_step, ff_step)
        into = win_ref[:, pl.ds(here, ff_step)]
        outof = wout_ref[pl.ds(here, ff_step), :]
        d_in = jnp.zeros((model, ff_step), F32)
        d_out = jnp.zeros((ff_step, model), F32)
        for source in range(heads):
            rows_in = rx_ref[source, :, 0:model]
            grads_out = rx_ref[source, :, model : 2 * model]
            act, slope = gelu_parts(dot(rows_in, into))
            d_act = dot(grads_out, outof, (1, 1))
            d_in = d_in + dot(rows_in, (slope * d_act).astype(BF16), (0, 0))
            d_out = d_out + dot(act.astype(BF16), grads_out, (0, 0))
        din_ref[:, pl.ds(here, ff_step)] = d_in
        dout_ref[pl.ds(here, ff_step), :] = d_out
        din_half[core, :, pl.ds(there, ff_step)] = d_in.astype(BF16)
        dout_half[core, pl.ds(there, ff_step), :] = d_out.astype(BF16)

    key_tile = kv_ref.shape[1]
    for group in range(2 * key_tile // (CHAINS * QUERY_TILE)):
        tiles, queries = query_group(q_ref, group, y)
        known = (
            queries,
            group_grads(do_ref, tiles, y),
            [delta_ref[tile, 0:1, :] for tile in tiles],
            [lse_ref[tile, 0:1, :] for tile in tiles],
        )
        carry = tuple(begun_ref[tile] for tile in tiles)
        for side in range(2):
            first = pl.multiple_of((2 * z + side) * key_tile, key_tile)
            keys_across = kvt_ref[:, pl.ds(first, key_tile)]
            given, carry = attend_back(
                bounds_ref, tiles, first, kv_ref[2 * z + side], keys_across, known, carry
            )
            dkv_own[side] = given if group == 0 else dkv_own[side] + given
        for tile, total in zip(tiles, carry):
            at = tile * QUERY_TILE % key_tile
            dq_ref[tile * QUERY_TILE // key_tile, at : at + QUERY_TILE] = jnp.transpose(total)
    pair_buf[...] = dkv_own[other_y].astype(BF16)
    pair_copy = remote(pair_buf, pair_all, pair_send, pair_recv, head, pair)
    pair_copy.start()
    own_lanes = (lane_ids(dq_packed.shape) < HALF) == (y == 0)
    dq_packed[...] = halves(dq_ref[other_y], own_lanes).astype(BF16)
    q_copy = remote(dq_packed, dq_all, q_send, q_recv, head, pair)
    q_copy.start()
    for half in range(2):
        rows_here = slice(half * half_span, (half + 1) * half_span)
        for step, there, back, slot in directions:

            @pl.when(there)
            def _():
                for side in range(2):
                    near_send_buf[slot + side, rows_here] = dkv_ref[2 * (z + step) + side, rows_here]

            @pl.when(jnp.logical_and(there, back))
            def _():
                for side in range(2):
                    arrived(half_of(far_all.at[slot + side], half), far_recv.at[slot + side, half])
                    near_send_buf[slot + side, rows_here] = (
                        near_send_buf[slot + side, rows_here].astype(F32)
                        + far_all[slot + side, rows_here].astype(F32)
                    ).astype(BF16)

            @pl.when(there)
            def _():
                for side in range(2):
                    near_copy(step, slot, side, half).start()

    finish(fetched[:2])
    weight = wa_ref[...].reshape(model, 3 * LANES)
    for piece in range(heads):
        xat[:, piece * tokens : (piece + 1) * tokens] = jnp.transpose(xa_ref[piece])
    even = y == 0


    def wide_copies(part):
        some = pl.ds(part * ff_half // 2, ff_half // 2)
        ins = din_half.at[core, :, some]
        outs = dout_half.at[core, some]
        return [
            remote(ins, ins, e_send.at[part, 0], e_recv.at[part, 0], sibling, blk),
            remote(outs, outs, e_send.at[part, 1], e_recv.at[part, 1], sibling, blk),
        ]

    e_copies = [wide_copies(part) for part in range(2)]

    expert_chunk(0)

    start(e_copies[0])
    q_copy.wait()
    landed = dq_all[...].astype(F32)
    landed = jnp.concatenate([landed, pltpu.roll(landed, HALF, 1)], axis=0)
    own_lanes = (lane_ids(landed.shape) < HALF) == even
    q_grads = jnp.where(own_lanes, dq_ref[y], landed).astype(BF16)
    gqs[...] = dot(xat[...], q_grads).astype(BF16).reshape(gqs.shape)
    gq_copies = [
        remote(
            gqs.at[around(blk, k, blks)], gqa.at[blk],
            gq_send.at[k], gq_recv.at[k], head, around(blk, k, blks),
        )
        for k in range(1, blks)
    ]
    start(gq_copies)
    gqa[blk] = gqs[blk]
    u_part[...] = dot(q_grads, weight[:, 2 * LANES : 3 * LANES], (1, 1)).reshape(u_part.shape)

    finish(w1_copies)
    summed = w1[0].astype(F32)
    for source in range(1, heads):
        summed = summed + w1[source].astype(F32)
    w2s[...] = summed.astype(BF16)
    w2_copies = [
        remote(
            w2s.at[around(blk, k, blks)], w2.at[blk],
            w2_send.at[k], w2_recv.at[k], head, around(blk, k, blks),
        )
        for k in range(1, blks)
    ]
    start(w2_copies)
    w2[blk] = w2s[blk]

    expert_chunk(1)

    start(e_copies[1])

    pair_copy.wait()
    for step, there, back, slot in directions:

        @pl.when(back)
        def _():
            for side in range(2):
                for half in range(2):
                    arrived(
                        half_of(near_all.at[slot // 2, side], half),
                        near_recv.at[slot // 2, side, half],
                    )

        @pl.when(jnp.logical_not(back))
        def _():
            near_all[slot // 2] = jnp.zeros(near_all.shape[1:], BF16)

    own = dkv_own[y]
    other = pair_all[...].astype(F32)
    made = jnp.concatenate(
        [
            (
                jnp.where(even == (side == 0), own, other)
                + near_all[0, side].astype(F32)
                + near_all[1, side].astype(F32)
            ).astype(BF16)
            for side in range(2)
        ],
        axis=1,
    )
    gs[...] = dot(xat[...], made).astype(BF16).reshape(gs.shape)
    g_copies = [
        remote(
            gs.at[around(blk, k, blks)], ga.at[blk],
            g_send.at[k], g_recv.at[k], head, around(blk, k, blks),
        )
        for k in range(1, blks)
    ]
    start(g_copies)
    ga[blk] = gs[blk]
    us[...] = (
        u_part[...] + dot(made, weight[:, 0 : 2 * LANES], (1, 1)).reshape(us.shape)
    ).astype(BF16)
    u_copies = [
        remote(
            us.at[around(head, k, heads)], ua.at[head],
            u_send.at[k], u_recv.at[k], around(head, k, heads), blk,
        )
        for k in range(1, heads)
    ]
    start(u_copies)
    ua[head] = us[head]
    finish(fetched[2:])
    finish(gq_copies)
    total = gqa[0].astype(F32)
    for source in range(1, blks):
        total = total + gqa[source].astype(F32)
    ghq[head] = total.astype(BF16)
    ghq_copies = [
        remote(ghq.at[head], ghq.at[head], ghq_send.at[k], ghq_recv.at[k], around(head, k, heads), blk)
        for k in range(1, heads)
    ]
    start(ghq_copies)

    finish(w2_copies)
    part = w2[0].astype(F32)
    for source in range(1, blks):
        part = part + w2[source].astype(F32)
    w3[head] = part.astype(BF16)
    w3_copies = [
        remote(w3.at[head], w3.at[head], w3_send.at[k], w3_recv.at[k], around(head, k, heads), blk)
        for k in range(1, heads)
    ]
    start(w3_copies)

    xhat, scale = centre(x_ref[...].astype(F32))
    for part in range(2):
        finish(e_copies[part])
        size = ff_half // 2
        there = pl.multiple_of((1 - core) * ff_half + part * size, size)
        here = slice(part * size, (part + 1) * size)
        din_ref[:, pl.ds(there, size)] = din_half[1 - core, :, here].astype(F32)
        dout_ref[pl.ds(there, size), :] = dout_half[1 - core, here].astype(F32)
    finish(g_copies)
    total = ga[0].astype(F32)
    for source in range(1, blks):
        total = total + ga[source].astype(F32)
    gh[head] = total.astype(BF16)
    gh_copies = [
        remote(gh.at[head], gh.at[head], gh_send.at[k], gh_recv.at[k], around(head, k, heads), blk)
        for k in range(1, heads)
    ]
    start(gh_copies)
    half_slots = pa_ref.shape[1]
    po_copies = [
        remote(
            po_ref.at[around(blk, k, blks), pl.ds(half_slots, half_slots)], pa.at[blk],
            po_send.at[k], po_recv.at[k], head, around(blk, k, blks),
        )
        for k in range(1, blks)
    ]
    start(po_copies)
    pa[blk] = po_ref[blk, half_slots : 2 * half_slots]
    finish(u_copies)
    grad = ua[0].astype(F32)
    for source in range(1, heads):
        grad = grad + ua[source].astype(F32)
    dx_ref[...] = dh_ref[...] + centre_back(grad, xhat, scale)

    gain_tile[...] = jnp.zeros_like(gain_tile)
    gain_tile[0:1, 0:rows] = g1_ref[...].astype(F32)
    gain = jnp.transpose(jnp.broadcast_to(gain_tile[0:1, :], (LANES, LANES)))[:rows]
    low_half = lane_ids((rows, LANES)) < HALF
    finish(ghq_copies)
    finish(gh_copies)
    d_gain = jnp.zeros((rows, LANES), F32)
    for source in range(heads):
        both = [gh[source, :, i * LANES : (i + 1) * LANES].astype(F32) for i in range(2)]
        grads = (
            ghq[source].astype(F32) * HS ** (-0.5),
            jnp.where(low_half, both[0], both[1]),
            pltpu.roll(jnp.where(low_half, both[1], both[0]), HALF, 1),
        )
        for which, value in enumerate(grads):
            columns = slice(which * model + source * LANES, which * model + (source + 1) * LANES)
            d_gain = d_gain + value * w_ref[:, columns].astype(F32)
            dw_ref[:, columns] = value * gain
    finish(w3_copies)
    shared = w3[...].reshape(rows, w3.shape[-1]).astype(F32)
    shared_ref[:, 0:model] = shared[:, 0:model]
    gain_col = jnp.sum(d_gain, axis=1, keepdims=True)
    shared_ref[:, model : model + LANES] = jnp.where(
        lane_ids((rows, LANES)) == blks + 1, gain_col, shared[:, model : model + LANES]
    )
    finish(po_copies)
    parts = jnp.concatenate([pa_ref[...], pa[...]], axis=1).reshape(share_ref.shape[2], model)
    mixture = dot(share_ref[0], parts) + dot(share_ref[1], parts)
    y_ref[...] = (hidden_ref[...] + mixture).astype(BF16)

    for step, there, back, slot in directions:

        @pl.when(two_away(step))
        def _():
            for side in range(2):
                for half in range(2):
                    far_copy(step, slot, side, half).wait_send()

        @pl.when(there)
        def _():
            for side in range(2):
                for half in range(2):
                    near_copy(step, slot, side, half).wait_send()


def call_last(
    x, dh, dq, dkv, xa, wa, w_qkv, g1, grads, rx, win, wout, po, pa, hidden, share,
    bounds, q, kv, kvt, d_o, lse, delta, heads, blks,
):
    tokens, model = x.shape
    span = tokens * heads
    rows = w_qkv.shape[0]
    wide = model + LANES
    part = rows // heads
    ff = wout.shape[0]

    def block(*lead):
        return pltpu.VMEM((*lead, span, LANES), BF16)

    return pl.pallas_call(
        functools.partial(last_kernel, heads, blks),
        out_shape=(
            jax.ShapeDtypeStruct((tokens, model), BF16),
            jax.ShapeDtypeStruct((tokens, model), F32),
            jax.ShapeDtypeStruct((rows, 3 * model), F32),
            jax.ShapeDtypeStruct((rows, wide), F32),
            jax.ShapeDtypeStruct((model, ff), F32),
            jax.ShapeDtypeStruct((ff, model), F32),
        ),
        in_specs=hbm_specs(1) + vmem_specs(5) + hbm_specs(2) + vmem_specs(2) + hbm_specs(2) + vmem_specs(11),
        out_specs=tuple(vmem_specs(6)),
        scratch_shapes=[
            pltpu.VMEM((tokens, model), BF16),
            pltpu.VMEM((rows, 3 * model), BF16),
            pltpu.VMEM((1, rows), BF16),
            pltpu.VMEM(win.shape, BF16),
            pltpu.VMEM(wout.shape, BF16),
            dma(5),
            pltpu.VMEM((8, LANES), F32),
            block(4), block(4), block(2, 2), block(), pltpu.VMEM((span // 2, LANES), BF16),
            pltpu.VMEM((2, span, LANES), F32), pltpu.VMEM((span // 2, LANES), BF16),
            pltpu.VMEM((2, span, LANES), F32), block(),
            pltpu.VMEM((heads, tokens, model), BF16), pltpu.VMEM((heads, tokens, model), BF16),
            pltpu.VMEM((blks, rows, 2 * LANES), BF16), pltpu.VMEM((blks, rows, 2 * LANES), BF16),
            pltpu.VMEM((blks, rows, LANES), BF16), pltpu.VMEM((blks, rows, LANES), BF16),
            pltpu.VMEM((heads, tokens, model), F32), pltpu.VMEM((model, span), BF16),
            pltpu.VMEM(pa.shape, BF16),
            pltpu.VMEM((heads, rows, 2 * LANES), BF16), pltpu.VMEM((heads, rows, LANES), BF16),
            pltpu.VMEM((heads, blks, part, wide), BF16), pltpu.VMEM((blks, part, wide), BF16),
            pltpu.VMEM((blks, part, wide), BF16), pltpu.VMEM((heads, part, wide), BF16),
            pltpu.SemaphoreType.DMA, pltpu.SemaphoreType.DMA, pltpu.SemaphoreType.DMA, pltpu.SemaphoreType.DMA,
            dma(4, 2), dma(4, 2), dma(4, 2), dma(2, 2, 2),
            dma(heads), dma(heads), dma(blks), dma(blks), dma(heads), dma(heads), dma(heads), dma(heads),
            dma(blks), dma(blks), dma(heads), dma(heads), dma(2, 2), dma(2, 2), dma(blks), dma(blks), dma(blks), dma(blks), dma(heads), dma(heads),
            pltpu.VMEM((2, model, ff // 2), BF16), pltpu.VMEM((2, ff // 2, model), BF16),
        ],
        compiler_params=pltpu.CompilerParams(
            collective_id=3, has_side_effects=True, vmem_limit_bytes=36 * MIB
        ),
        name="last",
    )(
        *in_hbm(x), dh, dq, dkv, xa, wa, *in_hbm(w_qkv, g1.reshape(1, rows)),
        grads.reshape(blks, heads, part, wide), rx, *in_hbm(win, wout), po, pa, hidden, share,
        bounds, q, kv, kvt, d_o, lse, delta,
    )


def finish_kernel(
    experts,
    y_ref, dx_ref, dw_ref, shared_ref, din_ref, dout_ref,
    y_out, dx_out, g1_out, dw_out, dwo_out, g2_out, wr_out, din_out, dout_out,
    tile, wr, g2, g1, sem,
):
    rows = shared_ref.shape[0]
    model = dx_ref.shape[1]
    copies = [
        pltpu.make_async_copy(dx_ref, dx_out, sem.at[0]),
        pltpu.make_async_copy(dw_ref, dw_out, sem.at[1]),
        pltpu.make_async_copy(shared_ref.at[:, pl.ds(0, model)], dwo_out, sem.at[2]),
        pltpu.make_async_copy(y_ref, y_out, sem.at[6]),
        pltpu.make_async_copy(din_ref, din_out, sem.at[7]),
        pltpu.make_async_copy(dout_ref, dout_out, sem.at[8]),
    ]
    for copy in copies:
        copy.start()
    tile[...] = jnp.zeros_like(tile)
    tile[0:rows, :] = shared_ref[:, model : model + LANES]
    across = jnp.transpose(tile[...])[:, 0:rows]
    wr[...] = across[0:experts]
    g2[...] = across[experts : experts + 1]
    g1[...] = across[experts + 1 : experts + 2]
    for index, (src, dst) in enumerate(((wr, wr_out), (g2, g2_out), (g1, g1_out))):
        copies.append(pltpu.make_async_copy(src, dst, sem.at[3 + index]))
        copies[-1].start()
    for copy in copies:
        copy.wait()


def call_finish(output, dx, dw, shared, d_in, d_out):
    rows = shared.shape[0]
    model = dx.shape[1]
    experts = model // rows
    return pl.pallas_call(
        functools.partial(finish_kernel, experts),
        out_shape=(
            jax.ShapeDtypeStruct(output.shape, BF16),
            jax.ShapeDtypeStruct(dx.shape, F32),
            jax.ShapeDtypeStruct((1, rows), F32),
            jax.ShapeDtypeStruct(dw.shape, F32),
            jax.ShapeDtypeStruct((rows, model), F32),
            jax.ShapeDtypeStruct((1, rows), F32),
            jax.ShapeDtypeStruct((experts, rows), F32),
            jax.ShapeDtypeStruct(d_in.shape, F32),
            jax.ShapeDtypeStruct(d_out.shape, F32),
        ),
        in_specs=vmem_specs(6),
        out_specs=tuple(hbm_specs(9)),
        scratch_shapes=[
            pltpu.VMEM((LANES, LANES), F32),
            pltpu.VMEM((experts, rows), F32),
            pltpu.VMEM((1, rows), F32),
            pltpu.VMEM((1, rows), F32),
            dma(9),
        ],
        compiler_params=pltpu.CompilerParams(vmem_limit_bytes=16 * MIB),
        name="finish",
    )(output, dx, dw, shared, d_in, d_out)


def local_kernels(
    inputs, ln1_gain, w_qkv, w_out, ln2_gain, w_router,
    expert_in, expert_out, routes, priority, doc_lengths, d_out,
):
    heads, blks = lax.axis_size("head"), lax.axis_size("blk")
    model = inputs.shape[1]
    tokens = inputs.shape[0]
    win, wout = expert_in[0], expert_out[0]
    q, kv, xa, wa, wo, kvt, bounds, begun = call_qkv(
        inputs, w_qkv, ln1_gain, w_out, w_router, ln2_gain, doc_lengths, heads, blks
    )
    o, o_low, lse = call_forward(bounds, q, kv, kvt, begun)
    po, pa, hidden, share, dh, d_o, grads, rx = call_middle(
        inputs, o_low.reshape(2, heads, tokens // 2, LANES), wo.reshape(model, model + LANES),
        routes, priority, d_out, win, wout, heads, blks,
    )
    d_o = d_o.reshape(2 * heads * tokens // QUERY_TILE, -1, HALF, LANES)
    dq, dkv, delta = call_backward(bounds, q, kv, kvt, d_o, o, lse)
    ends = call_last(
        inputs, dh, dq, dkv, xa, wa, w_qkv, ln1_gain, grads, rx, win, wout,
        po, pa, hidden, share, bounds, q, kv, kvt, d_o, lse, delta, heads, blks,
    )
    output, d_inputs, d_gain_one, d_qkv, d_out_proj, d_gain_two, d_router, d_in, d_out_weight = call_finish(*ends)
    return (
        output,
        d_inputs,
        d_gain_one.reshape(-1),
        d_qkv,
        d_out_proj,
        d_gain_two.reshape(-1),
        d_router.T,
        d_in[None],
        d_out_weight[None],
    )


def solution(mesh):
    in_specs = (
        P(("blk", "head"), None),
        P("blk"),
        P("blk", None),
        P("blk", None),
        P("blk"),
        P("blk", None),
        P("blk", None, None),
        P("blk", None, None),
        P(("blk", "head"), None),
        P(("blk", "head"), None),
        P(),
        P(("blk", "head"), None),
    )
    out_specs = (
        P(("blk", "head"), None),
        P(("blk", "head"), None),
        P("blk"),
        P("blk", None),
        P("blk", None),
        P("blk"),
        P("blk", None),
        P("blk", None, None),
        P("blk", None, None),
    )
    fits = mesh.shape["head"] == 4 and mesh.shape["blk"] == 8
    body = local_kernels if fits else local
    return jax.shard_map(body, mesh=mesh, in_specs=in_specs, out_specs=out_specs, check_vma=False)
```

```python
import functools
import math

import jax
import jax.numpy as jnp
from jax import lax
from jax.experimental import pallas as pl
from jax.experimental.pallas import tpu as pltpu
from jax.sharding import PartitionSpec as P

HS = 64
KEY_BLOCK = 2048


PRECISE = lax.Precision.HIGHEST
MASKED = -1e30
EPSILON = 1e-06


def layer_norm(values, gain):
    average = jnp.mean(values, axis=-1, keepdims=True)
    centred = values - average
    spread = jnp.mean(centred * centred, axis=-1, keepdims=True)
    return centred * lax.rsqrt(spread + EPSILON) * gain


def gelu_exact(values):
    return jax.nn.gelu(values, approximate=False)


def router(row_block, weight):
    return jax.nn.softmax(jnp.dot(row_block, weight, precision=PRECISE), axis=-1)


def doc_index(positions, doc_lengths):
    places = jnp.arange(doc_lengths.shape[0], dtype=jnp.int32)
    starts = jnp.sum(jnp.where(places[None, :] < places[:, None], doc_lengths[None, :], 0), axis=1)
    at_most = (starts[None, :] <= positions[:, None]).astype(jnp.int32)
    return jnp.sum(at_most, axis=1) - 1


def slot_table(route_rows, ranking, capacity):
    token_count = route_rows.shape[0]
    expert = jnp.transpose(route_rows).reshape(-1)
    pair_order = (jnp.arange(2, dtype=jnp.int32)[:, None] * token_count + ranking[None, :]).reshape(
        -1
    )
    before = (expert[:, None] == expert[None, :]) & (pair_order[None, :] < pair_order[:, None])
    position = jnp.sum(before.astype(jnp.int32), axis=1)
    slot_ids = jnp.where(position < capacity, expert * capacity + position, -1)
    return slot_ids.reshape(2, token_count)


def keep_state(current):
    return current


def local(
    inputs,
    ln1_gain,
    w_qkv,
    w_out,
    ln2_gain,
    w_router,
    expert_in,
    expert_out,
    routes,
    priority,
    doc_lengths,
    d_out,
):
    blk_size = lax.axis_size("blk")
    tok_rows = inputs.shape[0]
    model_width = inputs.shape[1]
    capacity = 2 * tok_rows // blk_size
    slot_total = blk_size * capacity
    gain_one, qkv_weight, out_weight, gain_two, router_weight = (
        lax.all_gather(ln1_gain, "blk", axis=0, tiled=True),
        lax.all_gather(w_qkv, "blk", axis=0, tiled=True),
        lax.all_gather(w_out, "blk", axis=0, tiled=True),
        lax.all_gather(ln2_gain, "blk", axis=0, tiled=True),
        lax.all_gather(w_router, "blk", axis=0, tiled=True),
    )
    input_rows = inputs.astype(jnp.float32)
    normed_one, norm_one_pull = jax.vjp(layer_norm, input_rows, gain_one.astype(jnp.float32))
    normed_low = normed_one.astype(jnp.bfloat16)
    qkv_rows = jnp.dot(normed_low, qkv_weight, preferred_element_type=jnp.float32).astype(
        jnp.bfloat16
    )
    query_heads, key_heads, value_heads = (
        lax.all_to_all(qkv_rows[:, :model_width], "head", split_axis=1, concat_axis=0, tiled=True),
        lax.all_to_all(
            qkv_rows[:, model_width : 2 * model_width],
            "head",
            split_axis=1,
            concat_axis=0,
            tiled=True,
        ),
        lax.all_to_all(
            qkv_rows[:, 2 * model_width :], "head", split_axis=1, concat_axis=0, tiled=True
        ),
    )
    span_rows = query_heads.shape[0]
    head_count = query_heads.shape[1] // HS
    key_all, value_all = (
        lax.all_gather(key_heads, "blk", axis=0, tiled=True),
        lax.all_gather(value_heads, "blk", axis=0, tiled=True),
    )
    total_rows = key_all.shape[0]
    block_count = total_rows // KEY_BLOCK
    scale_factor = HS ** (-0.5)
    query_pos = lax.axis_index("blk") * span_rows + jnp.arange(span_rows, dtype=jnp.int32)
    query_docs = doc_index(query_pos, doc_lengths)
    queries = query_heads.reshape(span_rows, head_count, HS)

    def block_parts(block_index, key_source, value_source):
        first_key = block_index * KEY_BLOCK
        key_rows = lax.dynamic_slice_in_dim(key_source, first_key, KEY_BLOCK, 0).reshape(
            KEY_BLOCK, head_count, HS
        )
        value_rows = lax.dynamic_slice_in_dim(value_source, first_key, KEY_BLOCK, 0).reshape(
            KEY_BLOCK, head_count, HS
        )
        key_docs = doc_index(first_key + jnp.arange(KEY_BLOCK, dtype=jnp.int32), doc_lengths)
        is_live = (key_docs[0] <= query_docs[-1]) & (key_docs[-1] >= query_docs[0])
        same_doc = query_docs[:, None] == key_docs[None, :]
        return (first_key, key_rows, value_rows, same_doc, is_live)

    def block_scores(key_rows, same_doc):
        raw_scores = (
            jnp.einsum("qhd,khd->hqk", queries, key_rows, preferred_element_type=jnp.float32)
            * scale_factor
        )
        return jnp.where(same_doc[None], raw_scores, MASKED)

    def stat_step(block_index, loop_state):
        first_key, key_rows, value_rows, same_doc, is_live = block_parts(
            block_index, key_all, value_all
        )

        def stat_update(current):
            running_max, running_sum = current
            scores = block_scores(key_rows, same_doc)
            new_max = jnp.maximum(running_max, jnp.max(scores, axis=2))
            exp_terms = jnp.where(same_doc[None], jnp.exp(scores - new_max[:, :, None]), 0.0)
            return (
                new_max,
                running_sum * jnp.exp(running_max - new_max) + jnp.sum(exp_terms, axis=2),
            )

        return lax.cond(is_live, stat_update, keep_state, loop_state)

    start_state = (
        jnp.full((head_count, span_rows), MASKED, jnp.float32),
        jnp.zeros((head_count, span_rows), jnp.float32),
    )
    running_max, running_sum = lax.fori_loop(0, block_count, stat_step, start_state)
    log_total = running_max + jnp.log(running_sum)

    def out_step(block_index, loop_state):
        first_key, key_rows, value_rows, same_doc, is_live = block_parts(
            block_index, key_all, value_all
        )

        def out_update(current):
            scores = block_scores(key_rows, same_doc)
            weights = jnp.where(
                same_doc[None], jnp.exp(scores - log_total[:, :, None]), 0.0
            ).astype(jnp.bfloat16)
            return current + jnp.einsum(
                "hqk,khd->qhd", weights, value_rows, preferred_element_type=jnp.float32
            )

        return lax.cond(is_live, out_update, keep_state, loop_state)

    mixed_full = lax.fori_loop(
        0, block_count, out_step, jnp.zeros((span_rows, head_count, HS), jnp.float32)
    )
    mixed_low = mixed_full.reshape(span_rows, head_count * HS).astype(jnp.bfloat16)
    mixed_tokens = lax.all_to_all(mixed_low, "head", split_axis=0, concat_axis=1, tiled=True)
    attended = jnp.dot(mixed_tokens, out_weight, preferred_element_type=jnp.float32)
    hidden_one = input_rows + attended
    normed_two, norm_two_pull = jax.vjp(layer_norm, hidden_one, gain_two.astype(jnp.float32))
    routed_low = normed_two.astype(jnp.bfloat16)
    router_probs, router_pull = jax.vjp(
        router, routed_low.astype(jnp.float32), router_weight.astype(jnp.float32)
    )
    slot_ids = slot_table(routes, priority[0], capacity)
    select = (
        slot_ids[:, :, None] == jnp.arange(slot_total, dtype=jnp.int32)[None, None, :]
    ).astype(jnp.bfloat16)
    send_rows = jnp.einsum(
        "kts,td->sd", select, routed_low, preferred_element_type=jnp.float32
    ).astype(jnp.bfloat16)
    expert_rows = lax.all_to_all(
        send_rows.reshape(blk_size, capacity, model_width),
        "blk",
        split_axis=0,
        concat_axis=0,
        tiled=True,
    ).reshape(slot_total, model_width)
    weight_in = expert_in[0]
    weight_out = expert_out[0]
    pre_act = jnp.dot(expert_rows, weight_in, preferred_element_type=jnp.float32)
    hidden_act, gelu_pull = jax.vjp(gelu_exact, pre_act)
    hidden_low = hidden_act.astype(jnp.bfloat16)
    expert_result = jnp.dot(hidden_low, weight_out, preferred_element_type=jnp.float32).astype(
        jnp.bfloat16
    )
    slot_result = lax.all_to_all(
        expert_result.reshape(blk_size, capacity, model_width),
        "blk",
        split_axis=0,
        concat_axis=0,
        tiled=True,
    ).reshape(slot_total, model_width)
    pair_result = jnp.einsum("kts,sd->ktd", select, slot_result, preferred_element_type=jnp.float32)
    route_hot = (routes[:, :, None] == jnp.arange(blk_size, dtype=jnp.int32)[None, None, :]).astype(
        jnp.float32
    )
    gate_vals = jnp.sum(router_probs[:, None, :] * route_hot, axis=2)
    mixture = gate_vals[:, 0, None] * pair_result[0] + gate_vals[:, 1, None] * pair_result[1]
    output = (hidden_one + mixture).astype(jnp.bfloat16)
    d_gates = jnp.transpose(jnp.sum(d_out[None] * pair_result, axis=2))
    d_probs = jnp.sum(d_gates[:, :, None] * route_hot, axis=1)
    pair_grads = (jnp.transpose(gate_vals)[:, :, None] * d_out[None]).astype(jnp.bfloat16)
    slot_grads = jnp.einsum(
        "kts,ktd->sd", select, pair_grads, preferred_element_type=jnp.float32
    ).astype(jnp.bfloat16)
    result_grads = lax.all_to_all(
        slot_grads.reshape(blk_size, capacity, model_width),
        "blk",
        split_axis=0,
        concat_axis=0,
        tiled=True,
    ).reshape(slot_total, model_width)
    d_hidden_act = jnp.dot(result_grads, weight_out.T, preferred_element_type=jnp.float32)
    d_weight_out = jnp.dot(hidden_low.T, result_grads, preferred_element_type=jnp.float32)
    d_preact = gelu_pull(d_hidden_act)[0].astype(jnp.bfloat16)
    d_weight_in = jnp.dot(expert_rows.T, d_preact, preferred_element_type=jnp.float32)
    row_grads = jnp.dot(d_preact, weight_in.T, preferred_element_type=jnp.float32).astype(
        jnp.bfloat16
    )
    slot_back = lax.all_to_all(
        row_grads.reshape(blk_size, capacity, model_width),
        "blk",
        split_axis=0,
        concat_axis=0,
        tiled=True,
    ).reshape(slot_total, model_width)
    d_routed = jnp.einsum("kts,sd->td", select, slot_back, preferred_element_type=jnp.float32)
    d_routed_router, d_router = router_pull(d_probs)
    d_hidden_norm, d_gain_two = norm_two_pull(d_routed + d_routed_router)
    d_hidden_one = d_out + d_hidden_norm
    attn_grads = d_hidden_one.astype(jnp.bfloat16)
    d_out_weight = jnp.dot(mixed_tokens.T, attn_grads, preferred_element_type=jnp.float32)
    mixed_grads = jnp.dot(attn_grads, out_weight.T, preferred_element_type=jnp.float32).astype(
        jnp.bfloat16
    )
    head_grads = lax.all_to_all(mixed_grads, "head", split_axis=1, concat_axis=0, tiled=True)
    out_grads = head_grads.reshape(span_rows, head_count, HS)
    row_delta = jnp.transpose(jnp.sum(out_grads.astype(jnp.float32) * mixed_full, axis=2))
    key_back, value_back = (
        lax.all_gather(key_heads, "blk", axis=0, tiled=True),
        lax.all_gather(value_heads, "blk", axis=0, tiled=True),
    )

    def grad_step(block_index, loop_state):
        first_key, key_rows, value_rows, same_doc, is_live = block_parts(
            block_index, key_back, value_back
        )

        def grad_update(current):
            query_grad, key_grad, value_grad = current
            scores = block_scores(key_rows, same_doc)
            weights = jnp.where(same_doc[None], jnp.exp(scores - log_total[:, :, None]), 0.0)
            value_part = jnp.einsum(
                "hqk,qhd->khd",
                weights.astype(jnp.bfloat16),
                out_grads,
                preferred_element_type=jnp.float32,
            )
            weight_grads = jnp.einsum(
                "qhd,khd->hqk", out_grads, value_rows, preferred_element_type=jnp.float32
            )
            score_grads = (weights * (weight_grads - row_delta[:, :, None])).astype(jnp.bfloat16)
            query_grad = (
                query_grad
                + jnp.einsum(
                    "hqk,khd->qhd", score_grads, key_rows, preferred_element_type=jnp.float32
                )
                * scale_factor
            )
            key_part = (
                jnp.einsum("hqk,qhd->khd", score_grads, queries, preferred_element_type=jnp.float32)
                * scale_factor
            )
            key_grad = lax.dynamic_update_slice_in_dim(
                key_grad, key_part.reshape(KEY_BLOCK, head_count * HS), first_key, 0
            )
            value_grad = lax.dynamic_update_slice_in_dim(
                value_grad, value_part.reshape(KEY_BLOCK, head_count * HS), first_key, 0
            )
            return (query_grad, key_grad, value_grad)

        return lax.cond(is_live, grad_update, keep_state, loop_state)

    start_grads = (
        jnp.zeros((span_rows, head_count, HS), jnp.float32),
        jnp.zeros((total_rows, head_count * HS), jnp.float32),
        jnp.zeros((total_rows, head_count * HS), jnp.float32),
    )
    query_grad, key_grad, value_grad = lax.fori_loop(0, block_count, grad_step, start_grads)
    key_own, value_own = (
        lax.psum_scatter(
            key_grad.astype(jnp.bfloat16), "blk", scatter_dimension=0, tiled=True
        ).astype(jnp.float32),
        lax.psum_scatter(
            value_grad.astype(jnp.bfloat16), "blk", scatter_dimension=0, tiled=True
        ).astype(jnp.float32),
    )
    query_tokens_grad, key_tokens_grad, value_tokens_grad = (
        lax.all_to_all(
            query_grad.reshape(span_rows, head_count * HS).astype(jnp.bfloat16),
            "head",
            split_axis=0,
            concat_axis=1,
            tiled=True,
        ),
        lax.all_to_all(
            key_own.astype(jnp.bfloat16), "head", split_axis=0, concat_axis=1, tiled=True
        ),
        lax.all_to_all(
            value_own.astype(jnp.bfloat16), "head", split_axis=0, concat_axis=1, tiled=True
        ),
    )
    qkv_grads = jnp.concatenate([query_tokens_grad, key_tokens_grad, value_tokens_grad], axis=1)
    d_qkv_weight = jnp.dot(normed_low.T, qkv_grads, preferred_element_type=jnp.float32)
    normed_grads = jnp.dot(qkv_grads, qkv_weight.T, preferred_element_type=jnp.float32)
    d_inputs_norm, d_gain_one = norm_one_pull(normed_grads)
    d_inputs = d_hidden_one + d_inputs_norm
    gain_one_sum, qkv_sum, out_sum, gain_two_sum, router_sum = (
        lax.psum_scatter(
            d_gain_one.astype(jnp.bfloat16), "blk", scatter_dimension=0, tiled=True
        ).astype(jnp.float32),
        lax.psum_scatter(
            d_qkv_weight.astype(jnp.bfloat16), "blk", scatter_dimension=0, tiled=True
        ).astype(jnp.float32),
        lax.psum_scatter(
            d_out_weight.astype(jnp.bfloat16), "blk", scatter_dimension=0, tiled=True
        ).astype(jnp.float32),
        lax.psum_scatter(
            d_gain_two.astype(jnp.bfloat16), "blk", scatter_dimension=0, tiled=True
        ).astype(jnp.float32),
        lax.psum_scatter(
            d_router.astype(jnp.bfloat16), "blk", scatter_dimension=0, tiled=True
        ).astype(jnp.float32),
    )
    gain_one_all, qkv_all, out_all, gain_two_all, router_all, expert_in_all, expert_out_all = (
        lax.psum(gain_one_sum.astype(jnp.bfloat16), "head").astype(jnp.float32),
        lax.psum(qkv_sum.astype(jnp.bfloat16), "head").astype(jnp.float32),
        lax.psum(out_sum.astype(jnp.bfloat16), "head").astype(jnp.float32),
        lax.psum(gain_two_sum.astype(jnp.bfloat16), "head").astype(jnp.float32),
        lax.psum(router_sum.astype(jnp.bfloat16), "head").astype(jnp.float32),
        lax.psum(d_weight_in[None].astype(jnp.bfloat16), "head").astype(jnp.float32),
        lax.psum(d_weight_out[None].astype(jnp.bfloat16), "head").astype(jnp.float32),
    )
    return (
        output,
        d_inputs,
        gain_one_all,
        qkv_all,
        out_all,
        gain_two_all,
        router_all,
        expert_in_all,
        expert_out_all,
    )


MESH = pl.DeviceIdType.MESH
LANES = 128
HALF = LANES // 2
MIB = 2**20
F32 = jnp.float32
BF16 = jnp.bfloat16


def dot(left, right, dims=(1, 0)):
    return lax.dot_general(
        left, right, (((dims[0],), (dims[1],)), ((), ())), preferred_element_type=F32
    )


def remote(src, dst, send_sem, recv_sem, head, blk):
    return pltpu.make_async_remote_copy(
        src_ref=src,
        dst_ref=dst,
        send_sem=send_sem,
        recv_sem=recv_sem,
        device_id={"head": head, "blk": blk},
        device_id_type=MESH,
    )


def arrived(ref, sem):
    pltpu.make_async_copy(ref, ref, sem).wait()


def greet(peers):
    barrier = pltpu.get_barrier_semaphore()
    for head, blk in peers:
        pl.semaphore_signal(
            barrier, inc=1, device_id={"head": head, "blk": blk}, device_id_type=MESH
        )
    return len(peers)


def meet(count):
    pl.semaphore_wait(pltpu.get_barrier_semaphore(), count)


def halves(values, lanes_kept):
    rows = values.shape[0] // 2
    moved = pltpu.roll(values[rows:], HALF, 1)
    return jnp.where(lanes_kept, values[:rows], moved)


def lane_ids(shape):
    return lax.broadcasted_iota(jnp.int32, shape, len(shape) - 1)


def centre(values):
    average = jnp.mean(values, axis=-1, keepdims=True)
    centred = values - average
    spread = jnp.mean(centred * centred, axis=-1, keepdims=True)
    scale = lax.rsqrt(spread + EPSILON)
    return centred * scale, scale


def centre_back(grad, xhat, scale):
    middle = jnp.mean(grad, axis=-1, keepdims=True)
    along = jnp.mean(grad * xhat, axis=-1, keepdims=True)
    return (grad - middle - xhat * along) * scale


def split_high_low(column, lanes):
    high = column.astype(BF16)
    low = (column - high.astype(F32)).astype(BF16)
    return jnp.where(lanes < HALF, high.astype(F32), low.astype(F32)).astype(BF16)


def join_high_low(matrix, start):
    return matrix[:, start : start + 1].astype(F32) + matrix[
        :, start + HALF : start + HALF + 1
    ].astype(F32)


def place():
    head, blk = lax.axis_index("head"), lax.axis_index("blk")
    return head, blk, blk // 2, lax.rem(blk, 2)


def around(index, step, size):
    return lax.rem(index + step, size)


QUERY_TILE = 256
CHAINS = 2


def masked_queries(q_ref, tile, key_lanes, query_tile):
    tiles_per_span = q_ref.shape[1] // query_tile
    inner = tile % tiles_per_span * query_tile
    query = q_ref[tile // tiles_per_span, inner : inner + query_tile, :]
    return jnp.where(key_lanes, query, jnp.zeros_like(query))


def group_blocks(bounds_ref, group, size, key_tile):
    first, last = group * size, (group + 1) * size
    low = jnp.min(bounds_ref[0:1, first : first + LANES])
    high = jnp.max(bounds_ref[1:2, last - LANES : last])
    return low // key_tile, (high + key_tile - 1) // key_tile


def inside_document(bounds_ref, tile, first, shape):
    key = first + lax.broadcasted_iota(jnp.int32, shape, 0)
    columns = slice(tile * shape[1], (tile + 1) * shape[1])
    return jnp.logical_and(key >= bounds_ref[0:1, columns], key < bounds_ref[1:2, columns])


def query_group(q_ref, group, y):
    key_lanes = (lane_ids((QUERY_TILE, LANES)) < HALF) == (y == 0)
    tiles = range(group * CHAINS, (group + 1) * CHAINS)
    return tiles, [masked_queries(q_ref, tile, key_lanes, QUERY_TILE) for tile in tiles]


def attend(bounds_ref, tiles, first, keys, keys_across, queries, carry):
    scores = [dot(keys, query, (1, 1)) for query in queries]
    made = []
    for tile, score, (biggest, weight, mixed) in zip(tiles, scores, carry):
        inside = inside_document(bounds_ref, tile, first, score.shape)
        score = jnp.where(inside, score, MASKED)
        bigger = jnp.maximum(biggest, jnp.max(score, axis=0, keepdims=True))
        fade = jnp.exp(biggest - bigger)
        terms = jnp.exp(score - bigger)
        weight = weight * fade + jnp.sum(terms, axis=0, keepdims=True)
        made.append((bigger, weight, mixed * fade + dot(keys_across, terms.astype(BF16))))
    return tuple(made)


def nothing_attended():
    return (
        jnp.full((1, QUERY_TILE), MASKED, F32),
        jnp.zeros((1, QUERY_TILE), F32),
        jnp.zeros((LANES, QUERY_TILE), F32),
    )


def attend_back(bounds_ref, tiles, first, keys, keys_across, group, carry):
    queries, out_grads, deltas, log_totals = group
    scores = [dot(keys, query, (1, 1)) for query in queries]
    weight_grads = [dot(keys, out_grad, (1, 1)) for out_grad in out_grads]
    pieces, score_grads = [], []
    for i, tile in enumerate(tiles):
        inside = inside_document(bounds_ref, tile, first, scores[i].shape)
        weights = jnp.exp(jnp.where(inside, scores[i], MASKED) - log_totals[i])
        score_grads.append((weights * (weight_grads[i] - deltas[i])).astype(BF16))
        pieces.append(weights.astype(BF16))
    wide = jnp.concatenate(score_grads + pieces, axis=1)
    given = dot(wide, jnp.concatenate(queries + out_grads, axis=0))
    return given, tuple(c + dot(keys_across, g) for c, g in zip(carry, score_grads))


def group_grads(do_ref, tiles, y):
    key_lanes = (lane_ids((QUERY_TILE, LANES)) < HALF) == (y == 0)
    out_grads = []
    for tile in tiles:
        parts = []
        for part in range(QUERY_TILE // LANES):
            packed = do_ref[tile, part].astype(F32)
            parts += [packed, pltpu.roll(packed, HALF, 1)]
        out_grads.append(jnp.where(key_lanes, 0.0, jnp.concatenate(parts, axis=0)).astype(BF16))
    return out_grads


def qkv_kernel(
    heads, blks,
    x_hbm, w_hbm, g1_hbm, wo_hbm, wr_hbm, g2_hbm, docs_hbm,
    qall, kvall, xall, wall, wo_all, kvt, bounds, begun,
    x_ref, w_ref, rows_in, g1_ref, g2_ref, wr_ref, docs_ref, wo_own, kv_other, q_packed, q_landed, in_sem,
    x_send, x_recv, w_send, w_recv, o_send, o_recv, p_send, p_recv,
    k_send, k_recv, q_recv,
):
    head, blk, z, y = place()
    planes = blks // 2
    model = x_ref.shape[1]
    rows = w_ref.shape[0]
    part = rows // heads
    experts = wr_ref.shape[0]
    wanted = (
        (w_hbm, w_ref), (g1_hbm, g1_ref), (g2_hbm, g2_ref), (wr_hbm, wr_ref), (x_hbm, x_ref),
        (wo_hbm, wo_own.at[:, pl.ds(0, model)]), (docs_hbm, docs_ref),
    )
    fetched = [
        pltpu.make_async_copy(src, dst, in_sem.at[i]) for i, (src, dst) in enumerate(wanted)
    ]
    for copy in fetched:
        copy.start()
    rows_in[...] = jnp.zeros_like(rows_in)
    met = greet(
        [(around(head, k, heads), blk) for k in range(1, heads)]
        + [(head, around(blk, k, blks)) for k in range(1, blks)]
    )
    lanes = lane_ids((rows, LANES))
    for copy in fetched:
        copy.wait()
    rows_in[0:experts, 0:rows] = wr_ref[...].astype(F32)
    rows_in[experts : experts + 1, 0:rows] = g2_ref[...].astype(F32)
    rows_in[experts + 1 : experts + 2, 0:rows] = g1_ref[...].astype(F32)
    vectors = jnp.transpose(rows_in[...])[:rows]
    gain = vectors[:, experts + 1 : experts + 2]

    def columns(which):
        start = pl.multiple_of(which * model + head * LANES, LANES)
        return w_ref[:, pl.ds(start, LANES)].astype(F32) * gain

    key_cols = columns(1)
    value_cols = pltpu.roll(columns(2), HALF, 1)
    wall[blk, :, 0:LANES] = jnp.where(lanes < HALF, key_cols, value_cols).astype(BF16)
    wall[blk, :, LANES : 2 * LANES] = jnp.where(lanes < HALF, value_cols, key_cols).astype(BF16)
    wall[blk, :, 2 * LANES : 3 * LANES] = (columns(0) * HS ** (-0.5)).astype(BF16)
    def slice_copy(slot, source, target):
        ref = wall.at[source]
        return remote(ref, ref, w_send.at[slot], w_recv.at[source], head, target)

    pair = 2 * z + around(y, 1, 2)
    line = [2 * around(z, step, planes) + y for step in (1, planes - 1, *range(2, planes - 1))]
    w_copies = [slice_copy(slot, blk, target) for slot, target in enumerate((*line, pair))]
    w_onward = [slice_copy(planes + slot, source, pair) for slot, source in enumerate(line)]
    xhat, _ = centre(x_ref[...].astype(F32))
    xall[head] = xhat.astype(BF16)
    meet(met)
    for copy in w_copies:
        copy.start()
    x_copies = [
        remote(xall.at[head], xall.at[head], x_send.at[k], x_recv.at[k], around(head, k, heads), blk)
        for k in range(1, heads)
    ]
    for copy in x_copies:
        copy.start()
    wo_own[:, model : model + LANES] = vectors.astype(BF16)
    wo_all[blk, head] = wo_own[pl.ds(pl.multiple_of(head * part, part), part), :]
    o_copies = [
        remote(
            wo_all.at[blk, head], wo_all.at[blk, head],
            o_send.at[k], o_recv.at[k], head, around(blk, k, blks),
        )
        for k in range(1, blks)
    ]
    document_bounds(docs_ref, bounds, z)
    for source, copy in zip(line, w_onward):
        arrived(wall.at[source], w_recv.at[source])
        copy.start()
    for copy in o_copies:
        copy.start()
    for source in (pair, *[other - y + around(y, 1, 2) for other in line]):
        arrived(wall.at[source], w_recv.at[source])
    for copy in w_copies + w_onward:
        copy.wait_send()
    for copy in x_copies:
        copy.wait()
    weight = wall[...].reshape(model, 3 * LANES)
    tokens = x_ref.shape[0]
    even = y == 0
    above, below = z < planes - 1, z > 0
    half_span = kvall.shape[1] // 2
    sides = ((1, above, below, 0), (-1, below, above, 4))

    def half_of(ref, half):
        return ref.at[pl.ds(half * half_span, half_span)]

    def outward(slot, step, across, half):
        target = 2 * (z + step) + around(y, across, 2)
        return remote(
            half_of(kv_other if across else kvall.at[blk], half), half_of(kvall.at[blk], half),
            k_send.at[slot], k_recv.at[blk, half], head, target,
        )

    def onward(slot, step, side, half):
        from_span = 2 * (z - step) + side
        ref = half_of(kvall.at[from_span], half)
        return remote(ref, ref, k_send.at[slot], k_recv.at[from_span, half], head, 2 * (z + step) + y)

    def await_half(span, half):
        arrived(half_of(kvall.at[span], half), k_recv.at[span, half])

    def turn(span):
        size = kvall.shape[1]
        kvt[:, pl.ds(pl.multiple_of(span * size, size), size)] = jnp.transpose(kvall[span])

    for half in range(2):
        for piece in range(half * heads // 2, (half + 1) * heads // 2):
            made = dot(xall[piece], weight).astype(BF16)
            first, second = made[:, 0:LANES], made[:, LANES : 2 * LANES]
            span = slice(piece * tokens, (piece + 1) * tokens)
            kvall[blk, span, :] = jnp.where(even, first, second)
            kv_other[span, :] = jnp.where(even, second, first)
            qall[y, span, :] = made[:, 2 * LANES : 3 * LANES]
        outward(8 + half, 0, 1, half).start()
        for step, there, _, slot in sides:

            @pl.when(there)
            def _():
                outward(slot + 2 * half, step, 0, half).start()
                outward(slot + 2 * half + 1, step, 1, half).start()

    other_y = around(y, 1, 2)
    kept = (lane_ids(q_packed.shape) < HALF) == (y == 1)
    q_packed[...] = halves(qall[y].astype(F32), kept).astype(BF16)
    q_pair = remote(q_packed, q_landed, k_send.at[10], q_recv, head, 2 * z + other_y)
    q_pair.start()
    turn(blk)
    for copy in o_copies:
        copy.wait()
    core = lax.rem(head, 2)
    sibling, across = head - core + 1 - core, around(head, 2, heads)

    def quarter_copy(index, quarter, to_head):
        ref = wo_all.at[:, quarter]
        return remote(ref, ref, p_send.at[index], p_recv.at[index], to_head, blk)

    p_copies = [quarter_copy(0, head, sibling), quarter_copy(1, head, across)]
    for copy in p_copies:
        copy.start()
    p_copies.append(quarter_copy(2, across, sibling))
    for half in range(2):
        for step, there, back, slot in sides:

            @pl.when(back)
            def _():
                for side in range(2):
                    await_half(2 * (z - step) + side, half)

            @pl.when(jnp.logical_and(there, back))
            def _():
                for side in range(2):
                    onward(11 + slot + 2 * half + side, step, side, half).start()

    arrived(wo_all.at[:, across], p_recv.at[1])
    p_copies[2].start()
    for half in range(2):
        await_half(pair, half)
    turn(pair)
    q_pair.wait()
    landed = q_landed[...]
    qall[other_y, 0:half_span, :] = landed
    qall[other_y, half_span : 2 * half_span, :] = pltpu.roll(landed.astype(F32), HALF, 1).astype(BF16)
    key_tile = kvall.shape[1]
    for group in range(2 * key_tile // (CHAINS * QUERY_TILE)):
        tiles, queries = query_group(qall, group, y)
        carry = (nothing_attended(),) * CHAINS
        for side in range(2):
            first = pl.multiple_of((2 * z + side) * key_tile, key_tile)
            keys_across = kvt[:, pl.ds(first, key_tile)]
            carry = attend(bounds, tiles, first, kvall[2 * z + side], keys_across, queries, carry)
        for tile, (biggest, weight, mixed) in zip(tiles, carry):
            begun[tile, 0:LANES] = mixed
            begun[tile, LANES : LANES + 8] = jnp.broadcast_to(biggest, (8, QUERY_TILE))
            begun[tile, LANES + 8 : LANES + 16] = jnp.broadcast_to(weight, (8, QUERY_TILE))
    for step, there, back, slot in sides:

        @pl.when(back)
        def _():
            for side in range(2):
                turn(2 * (z - step) + side)

    for other in range(planes):
        for side in range(2):
            span = 2 * other + side

            @pl.when(jnp.logical_or(z - other == 2, other - z == 2))
            def _():
                for half in range(2):
                    await_half(span, half)
                    rows_here = slice(half * half_span, (half + 1) * half_span)
                    columns = slice(
                        span * kvall.shape[1] + half * half_span,
                        span * kvall.shape[1] + (half + 1) * half_span,
                    )
                    kvt[:, columns] = jnp.transpose(kvall[span, rows_here])

    for index, quarter in ((0, sibling), (2, around(sibling, 2, heads))):
        arrived(wo_all.at[:, quarter], p_recv.at[index])
    for copy in p_copies:
        copy.wait_send()
    for half in range(2):
        outward(8 + half, 0, 1, half).wait_send()
        for step, there, back, slot in sides:

            @pl.when(there)
            def _():
                outward(slot + 2 * half, step, 0, half).wait_send()
                outward(slot + 2 * half + 1, step, 1, half).wait_send()

            @pl.when(jnp.logical_and(there, back))
            def _():
                for side in range(2):
                    onward(11 + slot + 2 * half + side, step, side, half).wait_send()


def document_bounds(docs_ref, bounds, z):
    count = docs_ref.shape[1]
    lengths = docs_ref[...].astype(F32)
    doc = lax.broadcasted_iota(jnp.int32, (count, count), 0)
    other = lane_ids((count, count))
    start = jnp.sum(jnp.where(other < doc, lengths, 0.0), axis=1, keepdims=True)
    end = jnp.sum(jnp.where(other <= doc, lengths, 0.0), axis=1, keepdims=True)
    queries = bounds.shape[1]
    token = (z * queries + lane_ids((count, queries))).astype(F32)
    begun = start <= token
    bounds[...] = jnp.zeros_like(bounds)
    bounds[0:1, :] = jnp.max(jnp.where(begun, start, 0.0), axis=0, keepdims=True).astype(jnp.int32)
    bounds[1:2, :] = jnp.max(jnp.where(begun, end, 0.0), axis=0, keepdims=True).astype(jnp.int32)


def vmem_specs(count):
    return [pl.BlockSpec(memory_space=pltpu.VMEM)] * count


def hbm_specs(count):
    return [pl.BlockSpec(memory_space=pltpu.HBM)] * count


def in_hbm(*arrays):
    return [pltpu.with_memory_space_constraint(array, pltpu.HBM) for array in arrays]


def dma(*shape):
    return pltpu.SemaphoreType.DMA(shape)


def call_qkv(x, w_qkv, g1, w_out, w_router, g2, doc_lengths, heads, blks):
    tokens, model = x.shape
    rows = w_qkv.shape[0]
    span = tokens * heads
    wide = model + LANES
    part = rows // heads
    return pl.pallas_call(
        functools.partial(qkv_kernel, heads, blks),
        out_shape=(
            jax.ShapeDtypeStruct((2, span, LANES), BF16),
            jax.ShapeDtypeStruct((blks, span, LANES), BF16),
            jax.ShapeDtypeStruct((heads, tokens, model), BF16),
            jax.ShapeDtypeStruct((blks, rows, 3 * LANES), BF16),
            jax.ShapeDtypeStruct((blks, heads, part, wide), BF16),
            jax.ShapeDtypeStruct((LANES, blks * span), BF16),
            jax.ShapeDtypeStruct((8, 2 * span), jnp.int32),
            jax.ShapeDtypeStruct((2 * span // QUERY_TILE, LANES + 16, QUERY_TILE), F32),
        ),
        in_specs=hbm_specs(7),
        out_specs=tuple(vmem_specs(8)),
        scratch_shapes=[
            pltpu.VMEM((tokens, model), BF16),
            pltpu.VMEM((rows, 3 * model), BF16),
            pltpu.VMEM((LANES, LANES), F32),
            pltpu.VMEM((1, rows), BF16),
            pltpu.VMEM((1, rows), BF16),
            pltpu.VMEM((w_router.shape[1], rows), BF16),
            pltpu.VMEM((1, doc_lengths.shape[0]), jnp.int32),
            pltpu.VMEM((rows, wide), BF16),
            pltpu.VMEM((span, LANES), BF16),
            pltpu.VMEM((span // 2, LANES), BF16),
            pltpu.VMEM((span // 2, LANES), BF16),
            dma(7),
            dma(heads), dma(heads), dma(blks), dma(blks), dma(blks), dma(blks), dma(heads), dma(heads),
            dma(19), dma(blks, 2), pltpu.SemaphoreType.DMA,
        ],
        compiler_params=pltpu.CompilerParams(
            collective_id=1, has_side_effects=True, vmem_limit_bytes=16 * MIB
        ),
        name="qkv",
    )(
        *in_hbm(
            x, w_qkv, g1.reshape(1, rows), w_out, w_router.T, g2.reshape(1, rows),
            doc_lengths.reshape(1, -1),
        )
    )


def other_blocks(bounds_ref, group, key_tile, z, step, carry):
    low, high = group_blocks(bounds_ref, group, CHAINS * QUERY_TILE, key_tile)
    carry = lax.fori_loop(low, 2 * z, step, carry)
    return lax.fori_loop(2 * z + 2, high, step, carry)


def forward_kernel(bounds_ref, q_ref, kv_ref, kvt_ref, begun_ref, o_out, ob_out, lse_out):
    _, _, z, y = place()
    key_tile = kv_ref.shape[1]
    value_lanes = (lane_ids((HALF, LANES)) < HALF) == (y == 1)
    for group in range(q_ref.shape[0] * q_ref.shape[1] // (CHAINS * QUERY_TILE)):
        tiles, queries = query_group(q_ref, group, y)

        def step(block, carry, queries=queries, tiles=tiles):
            first = pl.multiple_of(block * key_tile, key_tile)
            across = kvt_ref[:, pl.ds(first, key_tile)]
            return attend(bounds_ref, tiles, first, kv_ref[block], across, queries, carry)

        start = tuple(
            (begun_ref[t, LANES : LANES + 1], begun_ref[t, LANES + 8 : LANES + 9], begun_ref[t, 0:LANES])
            for t in tiles
        )
        ends = other_blocks(bounds_ref, group, key_tile, z, step, start)
        for tile, (biggest, weight, mixed) in zip(tiles, ends):
            result = jnp.transpose(mixed / weight)
            o_out[tile] = result
            for part in range(QUERY_TILE // LANES):
                block = result[part * LANES : (part + 1) * LANES]
                ob_out[tile, part] = halves(block, value_lanes).astype(BF16)
            lse_out[tile] = jnp.broadcast_to(biggest + jnp.log(weight), (8, QUERY_TILE))


def call_forward(bounds, q, kv, kvt, begun):
    blks, span, _ = kv.shape
    tiles = 2 * span // QUERY_TILE
    return pl.pallas_call(
        forward_kernel,
        out_shape=(
            jax.ShapeDtypeStruct((tiles, QUERY_TILE, LANES), F32),
            jax.ShapeDtypeStruct((tiles, QUERY_TILE // LANES, HALF, LANES), BF16),
            jax.ShapeDtypeStruct((tiles, 8, QUERY_TILE), F32),
        ),
        in_specs=vmem_specs(5),
        out_specs=tuple(vmem_specs(3)),
        compiler_params=pltpu.CompilerParams(vmem_limit_bytes=16 * MIB),
        name="attend",
    )(bounds, q, kv, kvt, begun)


def backward_kernel(
    bounds_ref, q_ref, kv_ref, kvt_ref, do_ref, o_ref, lse_ref, dq_out, dkv_out, delta_out, dkv
):
    _, _, z, y = place()
    key_tile = kv_ref.shape[1]
    for block in range(dkv.shape[0]):

        @pl.when(block // 2 != z)
        def _():
            dkv[block] = jnp.zeros(dkv.shape[1:], F32)

    for group in range(q_ref.shape[0] * q_ref.shape[1] // (CHAINS * QUERY_TILE)):
        tiles, queries = query_group(q_ref, group, y)
        out_grads = group_grads(do_ref, tiles, y)
        deltas, log_totals = [], []
        for tile, out_grad in zip(tiles, out_grads):
            product = jnp.transpose(out_grad.astype(F32) * o_ref[tile])
            deltas.append(jnp.sum(product, axis=0, keepdims=True))
            delta_out[tile] = jnp.broadcast_to(deltas[-1], delta_out.shape[1:])
            log_totals.append(lse_ref[tile, 0:1, :])
        known = (queries, out_grads, deltas, log_totals)

        def step(block, carry, tiles=tiles, known=known):
            first = pl.multiple_of(block * key_tile, key_tile)
            across = kvt_ref[:, pl.ds(first, key_tile)]
            given, carry = attend_back(bounds_ref, tiles, first, kv_ref[block], across, known, carry)
            dkv[block] += given
            return carry

        zero = jnp.zeros((LANES, QUERY_TILE), F32)
        ends = other_blocks(bounds_ref, group, key_tile, z, step, (zero,) * CHAINS)
        for tile, mixed in zip(tiles, ends):
            dq_out[tile] = mixed
    for block in range(dkv.shape[0]):

        @pl.when(block // 2 != z)
        def _():
            dkv_out[block] = dkv[block].astype(BF16)


def call_backward(bounds, q, kv, kvt, d_o, o, lse):
    blks, span, _ = kv.shape
    tiles = 2 * span // QUERY_TILE
    return pl.pallas_call(
        backward_kernel,
        out_shape=(
            jax.ShapeDtypeStruct((tiles, LANES, QUERY_TILE), F32),
            jax.ShapeDtypeStruct((blks, span, LANES), BF16),
            jax.ShapeDtypeStruct((tiles, 8, QUERY_TILE), F32),
        ),
        in_specs=vmem_specs(7),
        out_specs=tuple(vmem_specs(3)),
        scratch_shapes=[pltpu.VMEM((blks, span, LANES), F32)],
        compiler_params=pltpu.CompilerParams(vmem_limit_bytes=16 * MIB),
        name="attend_back",
    )(bounds, q, kv, kvt, d_o, o, lse)


def gelu_parts(values):
    share = 0.5 * (1.0 + lax.erf(values * (2.0**-0.5)))
    slope = share + values * jnp.exp(-0.5 * values * values) * (2.0 * math.pi) ** -0.5
    return values * share, slope


def positions(expert_rows, expert_cols, rank_row, rank_col):
    def count(mask, axis):
        return jnp.sum(mask.astype(F32), axis=axis, keepdims=True)

    row = [None, None]
    col = [None, None]
    before = rank_col < rank_row
    after = rank_row < rank_col
    for choice in range(2):
        row[choice] = count((expert_cols[choice] == expert_rows[choice]) & before, 0)
        col[choice] = count((expert_rows[choice] == expert_cols[choice]) & after, 1)
    row[1] = row[1] + count(expert_cols[0] == expert_rows[1], 0)
    col[1] = col[1] + count(expert_rows[0] == expert_cols[1], 1)
    return row, col


def own_columns(rows_ref, turned, blk, capacity):
    blks, _, slots = rows_ref.shape
    rows = jnp.concatenate(
        [rows_ref[...].reshape(blks, slots), jnp.zeros((LANES - blks, slots), F32)], axis=0
    )
    for piece in range(slots // LANES):
        columns = slice(piece * LANES, (piece + 1) * LANES)
        turned[columns, :] = jnp.transpose(rows[:, columns])
    own = turned[pl.ds(pl.multiple_of(blk * capacity, capacity), capacity), :]
    return jnp.concatenate([own[:, source : source + 1] for source in range(blks)], axis=0)


def middle_kernel(
    heads, blks,
    x_hbm, o_ref, wo_ref, routes_hbm, rank_hbm, d_out_hbm, win_hbm, wout_hbm,
    po, hidden_ref, share_ref, dh_ref, dma_all, grads_ref, rx,
    x_ref, routes_ref, rank_ref, d_out_ref, win_ref, wout_ref, rows_in, in_sem,
    o_all, dos, doa, rs, ra, dr, da, dms, mix, gate_rows, d_gate_rows, turned,
    o_send, o_recv, dos_send, dos_recv, r_send, r_recv,
    dr_send, dr_recv, dm_send, dm_recv, rx_send, rx_recv, g_send, g_recv, dg_send, dg_recv,
):
    head, blk, z, y = place()
    tokens, model = x_ref.shape
    capacity = 2 * tokens // blks
    slots = capacity * blks
    plane = [(k % heads, k // heads) for k in range(1, 2 * heads)]
    wanted = (
        (routes_hbm, routes_ref), (rank_hbm, rank_ref), (d_out_hbm, d_out_ref), (x_hbm, x_ref),
        (win_hbm, win_ref), (wout_hbm, wout_ref),
    )
    fetched = [
        pltpu.make_async_copy(src, dst, in_sem.at[i]) for i, (src, dst) in enumerate(wanted)
    ]
    for copy in fetched:
        copy.start()
    met = greet(
        [(around(head, kh, heads), 2 * z + around(y, ky, 2)) for kh, ky in plane]
        + [(head, around(blk, k, blks)) for k in range(1, blks)]
    )
    meet(met)

    def plane_copies(src_of, dst, send, recv):
        copies = []
        for k, (kh, ky) in enumerate(plane):
            to_head, to_y = around(head, kh, heads), around(y, ky, 2)
            copies.append(
                remote(src_of(to_y, to_head), dst, send.at[k], recv.at[k], to_head, 2 * z + to_y)
            )
        return copies

    def blk_copies(src, dst, send, recv):
        return [
            remote(
                src.at[around(blk, k, blks)], dst.at[blk],
                send.at[k], recv.at[k], head, around(blk, k, blks),
            )
            for k in range(1, blks)
        ]

    def start(copies):
        for copy in copies:
            copy.start()

    def finish(copies):
        for copy in copies:
            copy.wait()

    o_copies = plane_copies(lambda to_y, to_head: o_ref.at[to_y, to_head], o_all.at[y, head], o_send, o_recv)
    start(o_copies)
    o_all[y, head] = o_ref[y, head]

    lanes = lane_ids((tokens, LANES))
    for copy in fetched[:4]:
        copy.wait()
    e_rows = [routes_ref[i : i + 1, :].astype(F32) for i in range(2)]
    rank_row = rank_ref[...].astype(F32)
    rows_in[...] = jnp.zeros_like(rows_in)
    rows_in[0:1, :], rows_in[1:2, :], rows_in[2:3, :] = *e_rows, rank_row
    columns = jnp.transpose(rows_in[...])
    e_cols = [columns[:, 0:1], columns[:, 1:2]]
    rank_col = columns[:, 2:3]
    pos_rows, pos_cols = positions(e_rows, e_cols, rank_row, rank_col)

    def slot_of(expert, position):
        return jnp.where(position < capacity, expert * capacity + position, -1.0).astype(jnp.int32)

    slot_rows = [slot_of(e, p) for e, p in zip(e_rows, pos_rows)]
    slot_cols = [slot_of(e, p) for e, p in zip(e_cols, pos_cols)]
    slot_down = lax.broadcasted_iota(jnp.int32, (slots, tokens), 0)
    slot_across = lane_ids((tokens, slots))
    pick = [(slot_down == s).astype(BF16) for s in slot_rows]
    put = [(slot_across == s).astype(BF16) for s in slot_cols]
    pick_any = pick[0] + pick[1]
    put_any = put[0] + put[1]

    d_out = d_out_ref[...]
    dos[...] = dot(pick_any, d_out.astype(BF16)).astype(BF16).reshape(dos.shape)
    dos_copies = blk_copies(dos, doa, dos_send, dos_recv)
    start(dos_copies)
    doa[blk] = dos[blk]

    weight_out = jnp.concatenate(
        [wo_ref[(b ^ 1) * HALF : ((b ^ 1) + 1) * HALF, 0:model] for b in range(blks)], axis=0
    )
    small = wo_ref[:, model : model + LANES]
    small_across = jnp.concatenate(
        [
            jnp.transpose(small[i * LANES : (i + 1) * LANES].astype(F32))
            for i in range(model // LANES)
        ],
        axis=1,
    )
    gain = small_across[blks : blks + 1, :]

    finish(o_copies)
    low_lanes = lanes[:HALF] < HALF
    for piece in range(heads):
        columns = slice(piece * LANES, (piece + 1) * LANES)
        first, second = o_all[1, piece].astype(F32), o_all[0, piece].astype(F32)
        mix[:HALF, columns] = jnp.where(low_lanes, first, second).astype(BF16)
        swapped = pltpu.roll(jnp.where(low_lanes, second, first), HALF, 1)
        mix[HALF:, columns] = swapped.astype(BF16)
    mixed = mix[...]
    hidden = x_ref[...].astype(F32) + dot(mixed, weight_out)
    xhat, scale = centre(hidden)
    routed = (xhat * gain).astype(BF16)
    rs[...] = dot(pick_any, routed).astype(BF16).reshape(rs.shape)
    r_copies = blk_copies(rs, ra, r_send, r_recv)
    start(r_copies)
    ra[blk] = rs[blk]
    logits = jnp.where(lanes < blks, dot(routed, small), MASKED)
    powers = jnp.exp(logits - jnp.max(logits, axis=1, keepdims=True))
    probs = powers / jnp.sum(powers, axis=1, keepdims=True)
    lanes_f = lanes.astype(F32)
    hots = [lanes_f == e for e in e_cols]
    gates = [jnp.sum(jnp.where(hot, probs, 0.0), axis=1, keepdims=True) for hot in hots]
    gate_high = [g.astype(BF16).astype(F32) for g in gates]
    gate_across = jnp.transpose(
        jnp.where(lanes == 0, gate_high[0], jnp.where(lanes == 1, gates[0] - gate_high[0], 0.0))
        + jnp.where(lanes == 2, gate_high[1], jnp.where(lanes == 3, gates[1] - gate_high[1], 0.0))
    ).astype(BF16)
    by_slot = (dot(gate_across, put[0]), dot(gate_across, put[1]))
    gate_rows[blk] = by_slot[0][0:1] + by_slot[0][1:2] + by_slot[1][2:3] + by_slot[1][3:4]
    g_copies = [
        remote(
            gate_rows.at[blk], gate_rows.at[blk],
            g_send.at[k], g_recv.at[k], head, around(blk, k, blks),
        )
        for k in range(1, blks)
    ]
    start(g_copies)
    finish(dos_copies)
    finish(r_copies)

    out_rows = doa[...].reshape(slots, model)
    rx[head, :, 0:model] = ra[...].reshape(slots, model)
    finish(g_copies)
    gate_col = own_columns(gate_rows, turned, blk, capacity)
    rx[head, :, model : 2 * model] = (out_rows.astype(F32) * gate_col).astype(BF16)
    core = lax.rem(head, 2)
    sibling, across = head - core + 1 - core, around(head, 2, heads)

    def half_rows(source, half):
        return rx.at[source, pl.ds(half * slots // 2, slots // 2)]

    to_across = [
        remote(
            half_rows(head, half), half_rows(head, half),
            rx_send.at[1 + half], rx_recv.at[1 + half], across, blk,
        )
        for half in range(2)
    ]
    to_sibling = remote(rx.at[head], rx.at[head], rx_send.at[0], rx_recv.at[0], sibling, blk)
    forwards = [
        remote(
            half_rows(across, half), half_rows(across, half),
            rx_send.at[3 + half], rx_recv.at[3 + half], sibling, blk,
        )
        for half in range(2)
    ]
    start(to_across)
    to_sibling.start()
    for copy in fetched[4:]:
        copy.wait()
    act, slope = gelu_parts(dot(rx[head, :, 0:model], win_ref[...]))
    d_act = dot(rx[head, :, model : 2 * model], wout_ref[...], (1, 1))
    row_grads = dot((slope * d_act).astype(BF16), win_ref[...], (1, 1))
    dr[...] = row_grads.astype(BF16).reshape(dr.shape)
    dr_copies = blk_copies(dr, da, dr_send, dr_recv)
    start(dr_copies)
    result = dot(act.astype(BF16), wout_ref[...]).astype(BF16)
    d_gate = jnp.sum(out_rows.astype(F32) * result.astype(F32), axis=1, keepdims=True)
    da[blk] = dr[blk]
    d_wide = jnp.broadcast_to(d_gate, (slots, LANES))
    d_gate_rows[blk] = jnp.concatenate(
        [jnp.transpose(d_wide[i * LANES : (i + 1) * LANES])[0:1] for i in range(slots // LANES)],
        axis=1,
    )
    dg_copies = [
        remote(
            d_gate_rows.at[blk], d_gate_rows.at[blk],
            dg_send.at[k], dg_recv.at[k], head, around(blk, k, blks),
        )
        for k in range(1, blks)
    ]
    start(dg_copies)
    po[...] = result.reshape(blks, capacity, model)

    finish(dg_copies)
    back_gate = own_columns(d_gate_rows, turned, blk, capacity)
    back_gate = split_high_low(back_gate, lane_ids((slots, LANES)))
    d_gates = [join_high_low(dot(p, back_gate), 0) for p in put]
    d_probs = jnp.where(hots[0], d_gates[0], 0.0) + jnp.where(hots[1], d_gates[1], 0.0)
    d_logits = probs * (d_probs - jnp.sum(probs * d_probs, axis=1, keepdims=True))
    d_high = d_logits.astype(BF16)
    d_low = (d_logits - d_high.astype(F32)).astype(BF16)
    d_router_part = dot(d_high, small, (1, 1)) + dot(d_low, small, (1, 1))
    finish(dr_copies)
    d_routed = dot(put_any, da[...].reshape(slots, model)) + d_router_part
    d_hidden = d_out + centre_back(d_routed * gain, xhat, scale)
    dh_ref[...] = d_hidden
    d_attn = d_hidden.astype(BF16)
    d_mixed = dot(d_attn, weight_out, (1, 1))
    for piece in range(heads):
        block = d_mixed[:, piece * LANES : (piece + 1) * LANES]
        for to_y in range(2):
            dms[to_y, piece] = halves(block, low_lanes == (to_y == 1)).astype(BF16)
    dm_copies = plane_copies(lambda to_y, to_head: dms.at[to_y, to_head], dma_all.at[y, head], dm_send, dm_recv)
    start(dm_copies)
    dma_all[y, head] = dms[y, head]
    arrived(half_rows(across, 0), rx_recv.at[1])
    forwards[0].start()

    d_weight = dot(mixed, d_attn, (0, 0)).astype(BF16)
    for b in range(blks):
        grads_ref[b, :, 0:model] = d_weight[(b ^ 1) * HALF : ((b ^ 1) + 1) * HALF, :]
    last = (lanes == blks).astype(BF16)
    d_small = dot(routed, d_high, (0, 0)) + dot((d_routed * xhat).astype(BF16), last, (0, 0))
    grads_ref[:, :, model : model + LANES] = d_small.astype(BF16).reshape(blks, HALF, LANES)
    share = gates[0] * put[0].astype(F32) + gates[1] * put[1].astype(F32)
    share_ref[0] = share.astype(BF16)
    share_ref[1] = (share - share_ref[0].astype(F32)).astype(BF16)
    hidden_ref[...] = hidden

    arrived(half_rows(across, 1), rx_recv.at[2])
    forwards[1].start()
    finish(dm_copies)
    to_sibling.wait()
    for copy in to_across:
        copy.wait_send()
    finish(forwards)


def call_middle(x, o, wo, routes, rank, d_out, win, wout, heads, blks):
    tokens, model = x.shape
    capacity = 2 * tokens // blks
    slots = capacity * blks
    wide = model + LANES

    def rows(width):
        return pltpu.VMEM((blks, capacity, width), BF16)

    def block(*lead):
        return pltpu.VMEM((*lead, tokens // 2, LANES), BF16)

    return pl.pallas_call(
        functools.partial(middle_kernel, heads, blks),
        out_shape=(
            jax.ShapeDtypeStruct((blks, capacity, model), BF16),
            jax.ShapeDtypeStruct((tokens, model), F32),
            jax.ShapeDtypeStruct((2, tokens, slots), BF16),
            jax.ShapeDtypeStruct((tokens, model), F32),
            jax.ShapeDtypeStruct((2, heads, tokens // 2, LANES), BF16),
            jax.ShapeDtypeStruct((blks, model // blks, wide), BF16),
            jax.ShapeDtypeStruct((heads, slots, 2 * model), BF16),
        ),
        in_specs=hbm_specs(1) + vmem_specs(2) + hbm_specs(5),
        out_specs=tuple(vmem_specs(7)),
        scratch_shapes=[
            pltpu.VMEM((tokens, model), BF16),
            pltpu.VMEM((2, tokens), jnp.int32),
            pltpu.VMEM((1, tokens), jnp.int32),
            pltpu.VMEM((tokens, model), F32),
            pltpu.VMEM(win.shape, BF16),
            pltpu.VMEM(wout.shape, BF16),
            pltpu.VMEM((tokens, tokens), F32),
            dma(6),
            block(2, heads), rows(model), rows(model), rows(model), rows(model),
            rows(model), rows(model), block(2, heads),
            pltpu.VMEM((tokens, model), BF16),
            pltpu.VMEM((blks, 1, slots), F32), pltpu.VMEM((blks, 1, slots), F32),
            pltpu.VMEM((slots, LANES), F32),
            dma(2 * heads), dma(2 * heads), dma(blks), dma(blks), dma(blks), dma(blks),
            dma(blks), dma(blks), dma(2 * heads), dma(2 * heads), dma(5), dma(5),
            dma(blks), dma(blks), dma(blks), dma(blks),
        ],
        compiler_params=pltpu.CompilerParams(
            collective_id=2, has_side_effects=True, vmem_limit_bytes=20 * MIB
        ),
        name="experts",
    )(*in_hbm(x), o, wo, *in_hbm(routes.T, rank, d_out, win, wout))


def last_kernel(
    heads, blks,
    x_hbm, dh_ref, begun_ref, dkv_ref, xa_ref, wa_ref, w_hbm, g1_hbm, grads_ref, rx_ref, win_hbm, wout_hbm,
    po_ref, hidden_ref, share_ref, bounds_ref, q_ref, kv_ref, kvt_ref, do_ref, lse_ref, delta_ref,
    y_ref, dx_ref, dw_ref, shared_ref, din_ref, dout_ref,
    x_ref, w_ref, g1_ref, win_ref, wout_ref, in_sem,
    gain_tile, far_all, near_send_buf, near_all, pair_all, dq_all, dq_ref, dq_packed, dkv_own, pair_buf, us, ua, gs, ga, gqs, gqa, u_part, xat, pa, gh, ghq, w1, w2s, w2, w3,
    q_send, q_recv, pair_send, pair_recv, far_send, far_recv, near_send, near_recv,
    u_send, u_recv, g_send, g_recv, gh_send, gh_recv, w1_send, w1_recv, w2_send, w2_recv,
    w3_send, w3_recv, e_send, e_recv, gq_send, gq_recv, po_send, po_recv, ghq_send, ghq_recv,
    din_half, dout_half,
):
    head, blk, z, y = place()
    planes = blks // 2
    tokens, model = x_ref.shape
    rows = w_ref.shape[0]
    wanted = (
        (win_hbm, win_ref), (wout_hbm, wout_ref), (x_hbm, x_ref), (w_hbm, w_ref), (g1_hbm, g1_ref)
    )
    fetched = [
        pltpu.make_async_copy(src, dst, in_sem.at[i]) for i, (src, dst) in enumerate(wanted)
    ]
    for copy in fetched:
        copy.start()
    met = greet(
        [(around(head, k, heads), blk) for k in range(1, heads)]
        + [(head, around(blk, k, blks)) for k in range(1, blks)]
    )
    meet(met)

    def start(copies):
        for copy in copies:
            copy.start()

    def finish(copies):
        for copy in copies:
            copy.wait()

    other_y = around(y, 1, 2)
    pair = 2 * z + other_y
    above, below = z < planes - 1, z > 0
    directions = ((1, above, below, 0), (-1, below, above, 2))

    half_span = dkv_ref.shape[1] // 2

    def half_of(ref, half):
        return ref.at[pl.ds(half * half_span, half_span)]

    def far_copy(step, slot, side, half):
        span = 2 * (z + 2 * step) + side
        return remote(
            half_of(dkv_ref.at[span], half), half_of(far_all.at[slot + side], half),
            far_send.at[slot + side, half], far_recv.at[slot + side, half], head, 2 * (z + step) + y,
        )

    def near_copy(step, slot, side, half):
        return remote(
            half_of(near_send_buf.at[slot + side], half), half_of(near_all.at[slot // 2, y], half),
            near_send.at[slot + side, half], near_recv.at[slot // 2, y, half],
            head, 2 * (z + step) + side,
        )

    def two_away(step):
        return z + 2 * step < planes if step > 0 else z + 2 * step >= 0

    for half in range(2):
        for step, there, back, slot in directions:

            @pl.when(two_away(step))
            def _():
                for side in range(2):
                    far_copy(step, slot, side, half).start()

    w1_copies = [
        remote(
            grads_ref.at[:, around(head, k, heads)], w1.at[head],
            w1_send.at[k], w1_recv.at[k], around(head, k, heads), blk,
        )
        for k in range(1, heads)
    ]
    start(w1_copies)
    w1[head] = grads_ref[:, head]

    core = lax.rem(head, 2)
    sibling = head - core + 1 - core
    ff_half = wout_ref.shape[0] // 2
    ff_step = ff_half // 4

    def expert_chunk(chunk):
        here = pl.multiple_of(core * ff_half + chunk * ff_step, ff_step)
        there = pl.multiple_of(chunk * ff_step, ff_step)
        into = win_ref[:, pl.ds(here, ff_step)]
        outof = wout_ref[pl.ds(here, ff_step), :]
        d_in = jnp.zeros((model, ff_step), F32)
        d_out = jnp.zeros((ff_step, model), F32)
        for source in range(heads):
            rows_in = rx_ref[source, :, 0:model]
            grads_out = rx_ref[source, :, model : 2 * model]
            act, slope = gelu_parts(dot(rows_in, into))
            d_act = dot(grads_out, outof, (1, 1))
            d_in = d_in + dot(rows_in, (slope * d_act).astype(BF16), (0, 0))
            d_out = d_out + dot(act.astype(BF16), grads_out, (0, 0))
        din_ref[:, pl.ds(here, ff_step)] = d_in
        dout_ref[pl.ds(here, ff_step), :] = d_out
        din_half[core, :, pl.ds(there, ff_step)] = d_in.astype(BF16)
        dout_half[core, pl.ds(there, ff_step), :] = d_out.astype(BF16)

    key_tile = kv_ref.shape[1]
    for group in range(2 * key_tile // (CHAINS * QUERY_TILE)):
        tiles, queries = query_group(q_ref, group, y)
        known = (
            queries,
            group_grads(do_ref, tiles, y),
            [delta_ref[tile, 0:1, :] for tile in tiles],
            [lse_ref[tile, 0:1, :] for tile in tiles],
        )
        carry = tuple(begun_ref[tile] for tile in tiles)
        for side in range(2):
            first = pl.multiple_of((2 * z + side) * key_tile, key_tile)
            keys_across = kvt_ref[:, pl.ds(first, key_tile)]
            given, carry = attend_back(
                bounds_ref, tiles, first, kv_ref[2 * z + side], keys_across, known, carry
            )
            dkv_own[side] = given if group == 0 else dkv_own[side] + given
        for tile, total in zip(tiles, carry):
            at = tile * QUERY_TILE % key_tile
            dq_ref[tile * QUERY_TILE // key_tile, at : at + QUERY_TILE] = jnp.transpose(total)
    pair_buf[...] = dkv_own[other_y].astype(BF16)
    pair_copy = remote(pair_buf, pair_all, pair_send, pair_recv, head, pair)
    pair_copy.start()
    own_lanes = (lane_ids(dq_packed.shape) < HALF) == (y == 0)
    dq_packed[...] = halves(dq_ref[other_y], own_lanes).astype(BF16)
    q_copy = remote(dq_packed, dq_all, q_send, q_recv, head, pair)
    q_copy.start()
    for half in range(2):
        rows_here = slice(half * half_span, (half + 1) * half_span)
        for step, there, back, slot in directions:

            @pl.when(there)
            def _():
                for side in range(2):
                    near_send_buf[slot + side, rows_here] = dkv_ref[2 * (z + step) + side, rows_here]

            @pl.when(jnp.logical_and(there, back))
            def _():
                for side in range(2):
                    arrived(half_of(far_all.at[slot + side], half), far_recv.at[slot + side, half])
                    near_send_buf[slot + side, rows_here] = (
                        near_send_buf[slot + side, rows_here].astype(F32)
                        + far_all[slot + side, rows_here].astype(F32)
                    ).astype(BF16)

            @pl.when(there)
            def _():
                for side in range(2):
                    near_copy(step, slot, side, half).start()

    finish(fetched[:2])
    weight = wa_ref[...].reshape(model, 3 * LANES)
    for piece in range(heads):
        xat[:, piece * tokens : (piece + 1) * tokens] = jnp.transpose(xa_ref[piece])
    even = y == 0


    @pl.loop(0, 2)
    def _(chunk):
        expert_chunk(chunk)

    q_copy.wait()
    landed = dq_all[...].astype(F32)
    landed = jnp.concatenate([landed, pltpu.roll(landed, HALF, 1)], axis=0)
    own_lanes = (lane_ids(landed.shape) < HALF) == even
    q_grads = jnp.where(own_lanes, dq_ref[y], landed).astype(BF16)
    gqs[...] = dot(xat[...], q_grads).astype(BF16).reshape(gqs.shape)
    gq_copies = [
        remote(
            gqs.at[around(blk, k, blks)], gqa.at[blk],
            gq_send.at[k], gq_recv.at[k], head, around(blk, k, blks),
        )
        for k in range(1, blks)
    ]
    start(gq_copies)
    gqa[blk] = gqs[blk]
    u_part[...] = dot(q_grads, weight[:, 2 * LANES : 3 * LANES], (1, 1)).reshape(u_part.shape)

    finish(w1_copies)
    summed = w1[0].astype(F32)
    for source in range(1, heads):
        summed = summed + w1[source].astype(F32)
    w2s[...] = summed.astype(BF16)
    w2_copies = [
        remote(
            w2s.at[around(blk, k, blks)], w2.at[blk],
            w2_send.at[k], w2_recv.at[k], head, around(blk, k, blks),
        )
        for k in range(1, blks)
    ]
    start(w2_copies)
    w2[blk] = w2s[blk]

    @pl.loop(2, 4)
    def _(chunk):
        expert_chunk(chunk)

    e_copies = [
        remote(din_half.at[core], din_half.at[core], e_send.at[0], e_recv.at[0], sibling, blk),
        remote(dout_half.at[core], dout_half.at[core], e_send.at[1], e_recv.at[1], sibling, blk),
    ]
    start(e_copies)

    pair_copy.wait()
    for step, there, back, slot in directions:

        @pl.when(back)
        def _():
            for side in range(2):
                for half in range(2):
                    arrived(
                        half_of(near_all.at[slot // 2, side], half),
                        near_recv.at[slot // 2, side, half],
                    )

        @pl.when(jnp.logical_not(back))
        def _():
            near_all[slot // 2] = jnp.zeros(near_all.shape[1:], BF16)

    own = dkv_own[y]
    other = pair_all[...].astype(F32)
    made = jnp.concatenate(
        [
            (
                jnp.where(even == (side == 0), own, other)
                + near_all[0, side].astype(F32)
                + near_all[1, side].astype(F32)
            ).astype(BF16)
            for side in range(2)
        ],
        axis=1,
    )
    gs[...] = dot(xat[...], made).astype(BF16).reshape(gs.shape)
    g_copies = [
        remote(
            gs.at[around(blk, k, blks)], ga.at[blk],
            g_send.at[k], g_recv.at[k], head, around(blk, k, blks),
        )
        for k in range(1, blks)
    ]
    start(g_copies)
    ga[blk] = gs[blk]
    us[...] = (
        u_part[...] + dot(made, weight[:, 0 : 2 * LANES], (1, 1)).reshape(us.shape)
    ).astype(BF16)
    u_copies = [
        remote(
            us.at[around(head, k, heads)], ua.at[head],
            u_send.at[k], u_recv.at[k], around(head, k, heads), blk,
        )
        for k in range(1, heads)
    ]
    start(u_copies)
    ua[head] = us[head]
    finish(fetched[2:])
    finish(gq_copies)
    total = gqa[0].astype(F32)
    for source in range(1, blks):
        total = total + gqa[source].astype(F32)
    ghq[head] = total.astype(BF16)
    ghq_copies = [
        remote(ghq.at[head], ghq.at[head], ghq_send.at[k], ghq_recv.at[k], around(head, k, heads), blk)
        for k in range(1, heads)
    ]
    start(ghq_copies)

    finish(w2_copies)
    part = w2[0].astype(F32)
    for source in range(1, blks):
        part = part + w2[source].astype(F32)
    w3[head] = part.astype(BF16)
    w3_copies = [
        remote(w3.at[head], w3.at[head], w3_send.at[k], w3_recv.at[k], around(head, k, heads), blk)
        for k in range(1, heads)
    ]
    start(w3_copies)

    xhat, scale = centre(x_ref[...].astype(F32))
    finish(e_copies)
    there = pl.multiple_of((1 - core) * ff_half, ff_half)
    din_ref[:, pl.ds(there, ff_half)] = din_half[1 - core].astype(F32)
    dout_ref[pl.ds(there, ff_half), :] = dout_half[1 - core].astype(F32)
    finish(g_copies)
    total = ga[0].astype(F32)
    for source in range(1, blks):
        total = total + ga[source].astype(F32)
    gh[head] = total.astype(BF16)
    gh_copies = [
        remote(gh.at[head], gh.at[head], gh_send.at[k], gh_recv.at[k], around(head, k, heads), blk)
        for k in range(1, heads)
    ]
    start(gh_copies)
    po_copies = [
        remote(
            po_ref.at[around(blk, k, blks)], pa.at[blk],
            po_send.at[k], po_recv.at[k], head, around(blk, k, blks),
        )
        for k in range(1, blks)
    ]
    start(po_copies)
    pa[blk] = po_ref[blk]
    finish(u_copies)
    grad = ua[0].astype(F32)
    for source in range(1, heads):
        grad = grad + ua[source].astype(F32)
    dx_ref[...] = dh_ref[...] + centre_back(grad, xhat, scale)

    gain_tile[...] = jnp.zeros_like(gain_tile)
    gain_tile[0:1, 0:rows] = g1_ref[...].astype(F32)
    gain = jnp.transpose(jnp.broadcast_to(gain_tile[0:1, :], (LANES, LANES)))[:rows]
    low_half = lane_ids((rows, LANES)) < HALF
    finish(ghq_copies)
    finish(gh_copies)
    d_gain = jnp.zeros((rows, LANES), F32)
    for source in range(heads):
        both = [gh[source, :, i * LANES : (i + 1) * LANES].astype(F32) for i in range(2)]
        grads = (
            ghq[source].astype(F32) * HS ** (-0.5),
            jnp.where(low_half, both[0], both[1]),
            pltpu.roll(jnp.where(low_half, both[1], both[0]), HALF, 1),
        )
        for which, value in enumerate(grads):
            columns = slice(which * model + source * LANES, which * model + (source + 1) * LANES)
            d_gain = d_gain + value * w_ref[:, columns].astype(F32)
            dw_ref[:, columns] = value * gain
    finish(w3_copies)
    shared = w3[...].reshape(rows, w3.shape[-1]).astype(F32)
    shared_ref[:, 0:model] = shared[:, 0:model]
    gain_col = jnp.sum(d_gain, axis=1, keepdims=True)
    shared_ref[:, model : model + LANES] = jnp.where(
        lane_ids((rows, LANES)) == blks + 1, gain_col, shared[:, model : model + LANES]
    )
    finish(po_copies)
    parts = pa[...].reshape(share_ref.shape[2], model)
    mixture = dot(share_ref[0], parts) + dot(share_ref[1], parts)
    y_ref[...] = (hidden_ref[...] + mixture).astype(BF16)

    for step, there, back, slot in directions:

        @pl.when(two_away(step))
        def _():
            for side in range(2):
                for half in range(2):
                    far_copy(step, slot, side, half).wait_send()

        @pl.when(there)
        def _():
            for side in range(2):
                for half in range(2):
                    near_copy(step, slot, side, half).wait_send()


def call_last(
    x, dh, dq, dkv, xa, wa, w_qkv, g1, grads, rx, win, wout, po, hidden, share,
    bounds, q, kv, kvt, d_o, lse, delta, heads, blks,
):
    tokens, model = x.shape
    span = tokens * heads
    rows = w_qkv.shape[0]
    wide = model + LANES
    part = rows // heads
    ff = wout.shape[0]

    def block(*lead):
        return pltpu.VMEM((*lead, span, LANES), BF16)

    return pl.pallas_call(
        functools.partial(last_kernel, heads, blks),
        out_shape=(
            jax.ShapeDtypeStruct((tokens, model), BF16),
            jax.ShapeDtypeStruct((tokens, model), F32),
            jax.ShapeDtypeStruct((rows, 3 * model), F32),
            jax.ShapeDtypeStruct((rows, wide), F32),
            jax.ShapeDtypeStruct((model, ff), F32),
            jax.ShapeDtypeStruct((ff, model), F32),
        ),
        in_specs=hbm_specs(1) + vmem_specs(5) + hbm_specs(2) + vmem_specs(2) + hbm_specs(2) + vmem_specs(10),
        out_specs=tuple(vmem_specs(6)),
        scratch_shapes=[
            pltpu.VMEM((tokens, model), BF16),
            pltpu.VMEM((rows, 3 * model), BF16),
            pltpu.VMEM((1, rows), BF16),
            pltpu.VMEM(win.shape, BF16),
            pltpu.VMEM(wout.shape, BF16),
            dma(5),
            pltpu.VMEM((8, LANES), F32),
            block(4), block(4), block(2, 2), block(), pltpu.VMEM((span // 2, LANES), BF16),
            pltpu.VMEM((2, span, LANES), F32), pltpu.VMEM((span // 2, LANES), BF16),
            pltpu.VMEM((2, span, LANES), F32), block(),
            pltpu.VMEM((heads, tokens, model), BF16), pltpu.VMEM((heads, tokens, model), BF16),
            pltpu.VMEM((blks, rows, 2 * LANES), BF16), pltpu.VMEM((blks, rows, 2 * LANES), BF16),
            pltpu.VMEM((blks, rows, LANES), BF16), pltpu.VMEM((blks, rows, LANES), BF16),
            pltpu.VMEM((heads, tokens, model), F32), pltpu.VMEM((model, span), BF16),
            pltpu.VMEM(po.shape, BF16),
            pltpu.VMEM((heads, rows, 2 * LANES), BF16), pltpu.VMEM((heads, rows, LANES), BF16),
            pltpu.VMEM((heads, blks, part, wide), BF16), pltpu.VMEM((blks, part, wide), BF16),
            pltpu.VMEM((blks, part, wide), BF16), pltpu.VMEM((heads, part, wide), BF16),
            pltpu.SemaphoreType.DMA, pltpu.SemaphoreType.DMA, pltpu.SemaphoreType.DMA, pltpu.SemaphoreType.DMA,
            dma(4, 2), dma(4, 2), dma(4, 2), dma(2, 2, 2),
            dma(heads), dma(heads), dma(blks), dma(blks), dma(heads), dma(heads), dma(heads), dma(heads),
            dma(blks), dma(blks), dma(heads), dma(heads), dma(2), dma(2), dma(blks), dma(blks), dma(blks), dma(blks), dma(heads), dma(heads),
            pltpu.VMEM((2, model, ff // 2), BF16), pltpu.VMEM((2, ff // 2, model), BF16),
        ],
        compiler_params=pltpu.CompilerParams(
            collective_id=3, has_side_effects=True, vmem_limit_bytes=36 * MIB
        ),
        name="last",
    )(
        *in_hbm(x), dh, dq, dkv, xa, wa, *in_hbm(w_qkv, g1.reshape(1, rows)),
        grads.reshape(blks, heads, part, wide), rx, *in_hbm(win, wout), po, hidden, share,
        bounds, q, kv, kvt, d_o, lse, delta,
    )


def finish_kernel(
    experts,
    y_ref, dx_ref, dw_ref, shared_ref, din_ref, dout_ref,
    y_out, dx_out, g1_out, dw_out, dwo_out, g2_out, wr_out, din_out, dout_out,
    tile, wr, g2, g1, sem,
):
    rows = shared_ref.shape[0]
    model = dx_ref.shape[1]
    copies = [
        pltpu.make_async_copy(dx_ref, dx_out, sem.at[0]),
        pltpu.make_async_copy(dw_ref, dw_out, sem.at[1]),
        pltpu.make_async_copy(shared_ref.at[:, pl.ds(0, model)], dwo_out, sem.at[2]),
        pltpu.make_async_copy(y_ref, y_out, sem.at[6]),
        pltpu.make_async_copy(din_ref, din_out, sem.at[7]),
        pltpu.make_async_copy(dout_ref, dout_out, sem.at[8]),
    ]
    for copy in copies:
        copy.start()
    tile[...] = jnp.zeros_like(tile)
    tile[0:rows, :] = shared_ref[:, model : model + LANES]
    across = jnp.transpose(tile[...])[:, 0:rows]
    wr[...] = across[0:experts]
    g2[...] = across[experts : experts + 1]
    g1[...] = across[experts + 1 : experts + 2]
    for index, (src, dst) in enumerate(((wr, wr_out), (g2, g2_out), (g1, g1_out))):
        copies.append(pltpu.make_async_copy(src, dst, sem.at[3 + index]))
        copies[-1].start()
    for copy in copies:
        copy.wait()


def call_finish(output, dx, dw, shared, d_in, d_out):
    rows = shared.shape[0]
    model = dx.shape[1]
    experts = model // rows
    return pl.pallas_call(
        functools.partial(finish_kernel, experts),
        out_shape=(
            jax.ShapeDtypeStruct(output.shape, BF16),
            jax.ShapeDtypeStruct(dx.shape, F32),
            jax.ShapeDtypeStruct((1, rows), F32),
            jax.ShapeDtypeStruct(dw.shape, F32),
            jax.ShapeDtypeStruct((rows, model), F32),
            jax.ShapeDtypeStruct((1, rows), F32),
            jax.ShapeDtypeStruct((experts, rows), F32),
            jax.ShapeDtypeStruct(d_in.shape, F32),
            jax.ShapeDtypeStruct(d_out.shape, F32),
        ),
        in_specs=vmem_specs(6),
        out_specs=tuple(hbm_specs(9)),
        scratch_shapes=[
            pltpu.VMEM((LANES, LANES), F32),
            pltpu.VMEM((experts, rows), F32),
            pltpu.VMEM((1, rows), F32),
            pltpu.VMEM((1, rows), F32),
            dma(9),
        ],
        compiler_params=pltpu.CompilerParams(vmem_limit_bytes=16 * MIB),
        name="finish",
    )(output, dx, dw, shared, d_in, d_out)


def local_kernels(
    inputs, ln1_gain, w_qkv, w_out, ln2_gain, w_router,
    expert_in, expert_out, routes, priority, doc_lengths, d_out,
):
    heads, blks = lax.axis_size("head"), lax.axis_size("blk")
    model = inputs.shape[1]
    tokens = inputs.shape[0]
    win, wout = expert_in[0], expert_out[0]
    q, kv, xa, wa, wo, kvt, bounds, begun = call_qkv(
        inputs, w_qkv, ln1_gain, w_out, w_router, ln2_gain, doc_lengths, heads, blks
    )
    o, o_low, lse = call_forward(bounds, q, kv, kvt, begun)
    po, hidden, share, dh, d_o, grads, rx = call_middle(
        inputs, o_low.reshape(2, heads, tokens // 2, LANES), wo.reshape(model, model + LANES),
        routes, priority, d_out, win, wout, heads, blks,
    )
    d_o = d_o.reshape(2 * heads * tokens // QUERY_TILE, -1, HALF, LANES)
    dq, dkv, delta = call_backward(bounds, q, kv, kvt, d_o, o, lse)
    ends = call_last(
        inputs, dh, dq, dkv, xa, wa, w_qkv, ln1_gain, grads, rx, win, wout,
        po, hidden, share, bounds, q, kv, kvt, d_o, lse, delta, heads, blks,
    )
    output, d_inputs, d_gain_one, d_qkv, d_out_proj, d_gain_two, d_router, d_in, d_out_weight = call_finish(*ends)
    return (
        output,
        d_inputs,
        d_gain_one.reshape(-1),
        d_qkv,
        d_out_proj,
        d_gain_two.reshape(-1),
        d_router.T,
        d_in[None],
        d_out_weight[None],
    )


def solution(mesh):
    in_specs = (
        P(("blk", "head"), None),
        P("blk"),
        P("blk", None),
        P("blk", None),
        P("blk"),
        P("blk", None),
        P("blk", None, None),
        P("blk", None, None),
        P(("blk", "head"), None),
        P(("blk", "head"), None),
        P(),
        P(("blk", "head"), None),
    )
    out_specs = (
        P(("blk", "head"), None),
        P(("blk", "head"), None),
        P("blk"),
        P("blk", None),
        P("blk", None),
        P("blk"),
        P("blk", None),
        P("blk", None, None),
        P("blk", None, None),
    )
    fits = mesh.shape["head"] == 4 and mesh.shape["blk"] == 8
    body = local_kernels if fits else local
    return jax.shard_map(body, mesh=mesh, in_specs=in_specs, out_specs=out_specs, check_vma=False)
```

```python
import functools
import math

import jax
import jax.numpy as jnp
from jax import lax
from jax.experimental import pallas as pl
from jax.experimental.pallas import tpu as pltpu
from jax.sharding import PartitionSpec as P

HS = 64
KEY_BLOCK = 2048


PRECISE = lax.Precision.HIGHEST
MASKED = -1e30
EPSILON = 1e-06


def layer_norm(values, gain):
    average = jnp.mean(values, axis=-1, keepdims=True)
    centred = values - average
    spread = jnp.mean(centred * centred, axis=-1, keepdims=True)
    return centred * lax.rsqrt(spread + EPSILON) * gain


def gelu_exact(values):
    return jax.nn.gelu(values, approximate=False)


def router(row_block, weight):
    return jax.nn.softmax(jnp.dot(row_block, weight, precision=PRECISE), axis=-1)


def doc_index(positions, doc_lengths):
    places = jnp.arange(doc_lengths.shape[0], dtype=jnp.int32)
    starts = jnp.sum(jnp.where(places[None, :] < places[:, None], doc_lengths[None, :], 0), axis=1)
    at_most = (starts[None, :] <= positions[:, None]).astype(jnp.int32)
    return jnp.sum(at_most, axis=1) - 1


def slot_table(route_rows, ranking, capacity):
    token_count = route_rows.shape[0]
    expert = jnp.transpose(route_rows).reshape(-1)
    pair_order = (jnp.arange(2, dtype=jnp.int32)[:, None] * token_count + ranking[None, :]).reshape(
        -1
    )
    before = (expert[:, None] == expert[None, :]) & (pair_order[None, :] < pair_order[:, None])
    position = jnp.sum(before.astype(jnp.int32), axis=1)
    slot_ids = jnp.where(position < capacity, expert * capacity + position, -1)
    return slot_ids.reshape(2, token_count)


def keep_state(current):
    return current


def local(
    inputs,
    ln1_gain,
    w_qkv,
    w_out,
    ln2_gain,
    w_router,
    expert_in,
    expert_out,
    routes,
    priority,
    doc_lengths,
    d_out,
):
    blk_size = lax.axis_size("blk")
    tok_rows = inputs.shape[0]
    model_width = inputs.shape[1]
    capacity = 2 * tok_rows // blk_size
    slot_total = blk_size * capacity
    gain_one, qkv_weight, out_weight, gain_two, router_weight = (
        lax.all_gather(ln1_gain, "blk", axis=0, tiled=True),
        lax.all_gather(w_qkv, "blk", axis=0, tiled=True),
        lax.all_gather(w_out, "blk", axis=0, tiled=True),
        lax.all_gather(ln2_gain, "blk", axis=0, tiled=True),
        lax.all_gather(w_router, "blk", axis=0, tiled=True),
    )
    input_rows = inputs.astype(jnp.float32)
    normed_one, norm_one_pull = jax.vjp(layer_norm, input_rows, gain_one.astype(jnp.float32))
    normed_low = normed_one.astype(jnp.bfloat16)
    qkv_rows = jnp.dot(normed_low, qkv_weight, preferred_element_type=jnp.float32).astype(
        jnp.bfloat16
    )
    query_heads, key_heads, value_heads = (
        lax.all_to_all(qkv_rows[:, :model_width], "head", split_axis=1, concat_axis=0, tiled=True),
        lax.all_to_all(
            qkv_rows[:, model_width : 2 * model_width],
            "head",
            split_axis=1,
            concat_axis=0,
            tiled=True,
        ),
        lax.all_to_all(
            qkv_rows[:, 2 * model_width :], "head", split_axis=1, concat_axis=0, tiled=True
        ),
    )
    span_rows = query_heads.shape[0]
    head_count = query_heads.shape[1] // HS
    key_all, value_all = (
        lax.all_gather(key_heads, "blk", axis=0, tiled=True),
        lax.all_gather(value_heads, "blk", axis=0, tiled=True),
    )
    total_rows = key_all.shape[0]
    block_count = total_rows // KEY_BLOCK
    scale_factor = HS ** (-0.5)
    query_pos = lax.axis_index("blk") * span_rows + jnp.arange(span_rows, dtype=jnp.int32)
    query_docs = doc_index(query_pos, doc_lengths)
    queries = query_heads.reshape(span_rows, head_count, HS)

    def block_parts(block_index, key_source, value_source):
        first_key = block_index * KEY_BLOCK
        key_rows = lax.dynamic_slice_in_dim(key_source, first_key, KEY_BLOCK, 0).reshape(
            KEY_BLOCK, head_count, HS
        )
        value_rows = lax.dynamic_slice_in_dim(value_source, first_key, KEY_BLOCK, 0).reshape(
            KEY_BLOCK, head_count, HS
        )
        key_docs = doc_index(first_key + jnp.arange(KEY_BLOCK, dtype=jnp.int32), doc_lengths)
        is_live = (key_docs[0] <= query_docs[-1]) & (key_docs[-1] >= query_docs[0])
        same_doc = query_docs[:, None] == key_docs[None, :]
        return (first_key, key_rows, value_rows, same_doc, is_live)

    def block_scores(key_rows, same_doc):
        raw_scores = (
            jnp.einsum("qhd,khd->hqk", queries, key_rows, preferred_element_type=jnp.float32)
            * scale_factor
        )
        return jnp.where(same_doc[None], raw_scores, MASKED)

    def stat_step(block_index, loop_state):
        first_key, key_rows, value_rows, same_doc, is_live = block_parts(
            block_index, key_all, value_all
        )

        def stat_update(current):
            running_max, running_sum = current
            scores = block_scores(key_rows, same_doc)
            new_max = jnp.maximum(running_max, jnp.max(scores, axis=2))
            exp_terms = jnp.where(same_doc[None], jnp.exp(scores - new_max[:, :, None]), 0.0)
            return (
                new_max,
                running_sum * jnp.exp(running_max - new_max) + jnp.sum(exp_terms, axis=2),
            )

        return lax.cond(is_live, stat_update, keep_state, loop_state)

    start_state = (
        jnp.full((head_count, span_rows), MASKED, jnp.float32),
        jnp.zeros((head_count, span_rows), jnp.float32),
    )
    running_max, running_sum = lax.fori_loop(0, block_count, stat_step, start_state)
    log_total = running_max + jnp.log(running_sum)

    def out_step(block_index, loop_state):
        first_key, key_rows, value_rows, same_doc, is_live = block_parts(
            block_index, key_all, value_all
        )

        def out_update(current):
            scores = block_scores(key_rows, same_doc)
            weights = jnp.where(
                same_doc[None], jnp.exp(scores - log_total[:, :, None]), 0.0
            ).astype(jnp.bfloat16)
            return current + jnp.einsum(
                "hqk,khd->qhd", weights, value_rows, preferred_element_type=jnp.float32
            )

        return lax.cond(is_live, out_update, keep_state, loop_state)

    mixed_full = lax.fori_loop(
        0, block_count, out_step, jnp.zeros((span_rows, head_count, HS), jnp.float32)
    )
    mixed_low = mixed_full.reshape(span_rows, head_count * HS).astype(jnp.bfloat16)
    mixed_tokens = lax.all_to_all(mixed_low, "head", split_axis=0, concat_axis=1, tiled=True)
    attended = jnp.dot(mixed_tokens, out_weight, preferred_element_type=jnp.float32)
    hidden_one = input_rows + attended
    normed_two, norm_two_pull = jax.vjp(layer_norm, hidden_one, gain_two.astype(jnp.float32))
    routed_low = normed_two.astype(jnp.bfloat16)
    router_probs, router_pull = jax.vjp(
        router, routed_low.astype(jnp.float32), router_weight.astype(jnp.float32)
    )
    slot_ids = slot_table(routes, priority[0], capacity)
    select = (
        slot_ids[:, :, None] == jnp.arange(slot_total, dtype=jnp.int32)[None, None, :]
    ).astype(jnp.bfloat16)
    send_rows = jnp.einsum(
        "kts,td->sd", select, routed_low, preferred_element_type=jnp.float32
    ).astype(jnp.bfloat16)
    expert_rows = lax.all_to_all(
        send_rows.reshape(blk_size, capacity, model_width),
        "blk",
        split_axis=0,
        concat_axis=0,
        tiled=True,
    ).reshape(slot_total, model_width)
    weight_in = expert_in[0]
    weight_out = expert_out[0]
    pre_act = jnp.dot(expert_rows, weight_in, preferred_element_type=jnp.float32)
    hidden_act, gelu_pull = jax.vjp(gelu_exact, pre_act)
    hidden_low = hidden_act.astype(jnp.bfloat16)
    expert_result = jnp.dot(hidden_low, weight_out, preferred_element_type=jnp.float32).astype(
        jnp.bfloat16
    )
    slot_result = lax.all_to_all(
        expert_result.reshape(blk_size, capacity, model_width),
        "blk",
        split_axis=0,
        concat_axis=0,
        tiled=True,
    ).reshape(slot_total, model_width)
    pair_result = jnp.einsum("kts,sd->ktd", select, slot_result, preferred_element_type=jnp.float32)
    route_hot = (routes[:, :, None] == jnp.arange(blk_size, dtype=jnp.int32)[None, None, :]).astype(
        jnp.float32
    )
    gate_vals = jnp.sum(router_probs[:, None, :] * route_hot, axis=2)
    mixture = gate_vals[:, 0, None] * pair_result[0] + gate_vals[:, 1, None] * pair_result[1]
    output = (hidden_one + mixture).astype(jnp.bfloat16)
    d_gates = jnp.transpose(jnp.sum(d_out[None] * pair_result, axis=2))
    d_probs = jnp.sum(d_gates[:, :, None] * route_hot, axis=1)
    pair_grads = (jnp.transpose(gate_vals)[:, :, None] * d_out[None]).astype(jnp.bfloat16)
    slot_grads = jnp.einsum(
        "kts,ktd->sd", select, pair_grads, preferred_element_type=jnp.float32
    ).astype(jnp.bfloat16)
    result_grads = lax.all_to_all(
        slot_grads.reshape(blk_size, capacity, model_width),
        "blk",
        split_axis=0,
        concat_axis=0,
        tiled=True,
    ).reshape(slot_total, model_width)
    d_hidden_act = jnp.dot(result_grads, weight_out.T, preferred_element_type=jnp.float32)
    d_weight_out = jnp.dot(hidden_low.T, result_grads, preferred_element_type=jnp.float32)
    d_preact = gelu_pull(d_hidden_act)[0].astype(jnp.bfloat16)
    d_weight_in = jnp.dot(expert_rows.T, d_preact, preferred_element_type=jnp.float32)
    row_grads = jnp.dot(d_preact, weight_in.T, preferred_element_type=jnp.float32).astype(
        jnp.bfloat16
    )
    slot_back = lax.all_to_all(
        row_grads.reshape(blk_size, capacity, model_width),
        "blk",
        split_axis=0,
        concat_axis=0,
        tiled=True,
    ).reshape(slot_total, model_width)
    d_routed = jnp.einsum("kts,sd->td", select, slot_back, preferred_element_type=jnp.float32)
    d_routed_router, d_router = router_pull(d_probs)
    d_hidden_norm, d_gain_two = norm_two_pull(d_routed + d_routed_router)
    d_hidden_one = d_out + d_hidden_norm
    attn_grads = d_hidden_one.astype(jnp.bfloat16)
    d_out_weight = jnp.dot(mixed_tokens.T, attn_grads, preferred_element_type=jnp.float32)
    mixed_grads = jnp.dot(attn_grads, out_weight.T, preferred_element_type=jnp.float32).astype(
        jnp.bfloat16
    )
    head_grads = lax.all_to_all(mixed_grads, "head", split_axis=1, concat_axis=0, tiled=True)
    out_grads = head_grads.reshape(span_rows, head_count, HS)
    row_delta = jnp.transpose(jnp.sum(out_grads.astype(jnp.float32) * mixed_full, axis=2))
    key_back, value_back = (
        lax.all_gather(key_heads, "blk", axis=0, tiled=True),
        lax.all_gather(value_heads, "blk", axis=0, tiled=True),
    )

    def grad_step(block_index, loop_state):
        first_key, key_rows, value_rows, same_doc, is_live = block_parts(
            block_index, key_back, value_back
        )

        def grad_update(current):
            query_grad, key_grad, value_grad = current
            scores = block_scores(key_rows, same_doc)
            weights = jnp.where(same_doc[None], jnp.exp(scores - log_total[:, :, None]), 0.0)
            value_part = jnp.einsum(
                "hqk,qhd->khd",
                weights.astype(jnp.bfloat16),
                out_grads,
                preferred_element_type=jnp.float32,
            )
            weight_grads = jnp.einsum(
                "qhd,khd->hqk", out_grads, value_rows, preferred_element_type=jnp.float32
            )
            score_grads = (weights * (weight_grads - row_delta[:, :, None])).astype(jnp.bfloat16)
            query_grad = (
                query_grad
                + jnp.einsum(
                    "hqk,khd->qhd", score_grads, key_rows, preferred_element_type=jnp.float32
                )
                * scale_factor
            )
            key_part = (
                jnp.einsum("hqk,qhd->khd", score_grads, queries, preferred_element_type=jnp.float32)
                * scale_factor
            )
            key_grad = lax.dynamic_update_slice_in_dim(
                key_grad, key_part.reshape(KEY_BLOCK, head_count * HS), first_key, 0
            )
            value_grad = lax.dynamic_update_slice_in_dim(
                value_grad, value_part.reshape(KEY_BLOCK, head_count * HS), first_key, 0
            )
            return (query_grad, key_grad, value_grad)

        return lax.cond(is_live, grad_update, keep_state, loop_state)

    start_grads = (
        jnp.zeros((span_rows, head_count, HS), jnp.float32),
        jnp.zeros((total_rows, head_count * HS), jnp.float32),
        jnp.zeros((total_rows, head_count * HS), jnp.float32),
    )
    query_grad, key_grad, value_grad = lax.fori_loop(0, block_count, grad_step, start_grads)
    key_own, value_own = (
        lax.psum_scatter(
            key_grad.astype(jnp.bfloat16), "blk", scatter_dimension=0, tiled=True
        ).astype(jnp.float32),
        lax.psum_scatter(
            value_grad.astype(jnp.bfloat16), "blk", scatter_dimension=0, tiled=True
        ).astype(jnp.float32),
    )
    query_tokens_grad, key_tokens_grad, value_tokens_grad = (
        lax.all_to_all(
            query_grad.reshape(span_rows, head_count * HS).astype(jnp.bfloat16),
            "head",
            split_axis=0,
            concat_axis=1,
            tiled=True,
        ),
        lax.all_to_all(
            key_own.astype(jnp.bfloat16), "head", split_axis=0, concat_axis=1, tiled=True
        ),
        lax.all_to_all(
            value_own.astype(jnp.bfloat16), "head", split_axis=0, concat_axis=1, tiled=True
        ),
    )
    qkv_grads = jnp.concatenate([query_tokens_grad, key_tokens_grad, value_tokens_grad], axis=1)
    d_qkv_weight = jnp.dot(normed_low.T, qkv_grads, preferred_element_type=jnp.float32)
    normed_grads = jnp.dot(qkv_grads, qkv_weight.T, preferred_element_type=jnp.float32)
    d_inputs_norm, d_gain_one = norm_one_pull(normed_grads)
    d_inputs = d_hidden_one + d_inputs_norm
    gain_one_sum, qkv_sum, out_sum, gain_two_sum, router_sum = (
        lax.psum_scatter(
            d_gain_one.astype(jnp.bfloat16), "blk", scatter_dimension=0, tiled=True
        ).astype(jnp.float32),
        lax.psum_scatter(
            d_qkv_weight.astype(jnp.bfloat16), "blk", scatter_dimension=0, tiled=True
        ).astype(jnp.float32),
        lax.psum_scatter(
            d_out_weight.astype(jnp.bfloat16), "blk", scatter_dimension=0, tiled=True
        ).astype(jnp.float32),
        lax.psum_scatter(
            d_gain_two.astype(jnp.bfloat16), "blk", scatter_dimension=0, tiled=True
        ).astype(jnp.float32),
        lax.psum_scatter(
            d_router.astype(jnp.bfloat16), "blk", scatter_dimension=0, tiled=True
        ).astype(jnp.float32),
    )
    gain_one_all, qkv_all, out_all, gain_two_all, router_all, expert_in_all, expert_out_all = (
        lax.psum(gain_one_sum.astype(jnp.bfloat16), "head").astype(jnp.float32),
        lax.psum(qkv_sum.astype(jnp.bfloat16), "head").astype(jnp.float32),
        lax.psum(out_sum.astype(jnp.bfloat16), "head").astype(jnp.float32),
        lax.psum(gain_two_sum.astype(jnp.bfloat16), "head").astype(jnp.float32),
        lax.psum(router_sum.astype(jnp.bfloat16), "head").astype(jnp.float32),
        lax.psum(d_weight_in[None].astype(jnp.bfloat16), "head").astype(jnp.float32),
        lax.psum(d_weight_out[None].astype(jnp.bfloat16), "head").astype(jnp.float32),
    )
    return (
        output,
        d_inputs,
        gain_one_all,
        qkv_all,
        out_all,
        gain_two_all,
        router_all,
        expert_in_all,
        expert_out_all,
    )


MESH = pl.DeviceIdType.MESH
LANES = 128
HALF = LANES // 2
MIB = 2**20
F32 = jnp.float32
BF16 = jnp.bfloat16


def dot(left, right, dims=(1, 0)):
    return lax.dot_general(
        left, right, (((dims[0],), (dims[1],)), ((), ())), preferred_element_type=F32
    )


def remote(src, dst, send_sem, recv_sem, head, blk):
    return pltpu.make_async_remote_copy(
        src_ref=src,
        dst_ref=dst,
        send_sem=send_sem,
        recv_sem=recv_sem,
        device_id={"head": head, "blk": blk},
        device_id_type=MESH,
    )


def arrived(ref, sem):
    pltpu.make_async_copy(ref, ref, sem).wait()


def greet(peers):
    barrier = pltpu.get_barrier_semaphore()
    for head, blk in peers:
        pl.semaphore_signal(
            barrier, inc=1, device_id={"head": head, "blk": blk}, device_id_type=MESH
        )
    return len(peers)


def meet(count):
    pl.semaphore_wait(pltpu.get_barrier_semaphore(), count)


def halves(values, lanes_kept):
    rows = values.shape[0] // 2
    moved = pltpu.roll(values[rows:], HALF, 1)
    return jnp.where(lanes_kept, values[:rows], moved)


def lane_ids(shape):
    return lax.broadcasted_iota(jnp.int32, shape, len(shape) - 1)


def centre(values):
    average = jnp.mean(values, axis=-1, keepdims=True)
    centred = values - average
    spread = jnp.mean(centred * centred, axis=-1, keepdims=True)
    scale = lax.rsqrt(spread + EPSILON)
    return centred * scale, scale


def centre_back(grad, xhat, scale):
    middle = jnp.mean(grad, axis=-1, keepdims=True)
    along = jnp.mean(grad * xhat, axis=-1, keepdims=True)
    return (grad - middle - xhat * along) * scale


def split_high_low(column, lanes):
    high = column.astype(BF16)
    low = (column - high.astype(F32)).astype(BF16)
    return jnp.where(lanes < HALF, high.astype(F32), low.astype(F32)).astype(BF16)


def join_high_low(matrix, start):
    return matrix[:, start : start + 1].astype(F32) + matrix[
        :, start + HALF : start + HALF + 1
    ].astype(F32)


def place():
    head, blk = lax.axis_index("head"), lax.axis_index("blk")
    return head, blk, blk // 2, lax.rem(blk, 2)


def around(index, step, size):
    return lax.rem(index + step, size)


QUERY_TILE = 256
CHAINS = 2


def masked_queries(q_ref, tile, key_lanes, query_tile):
    tiles_per_span = q_ref.shape[1] // query_tile
    inner = tile % tiles_per_span * query_tile
    query = q_ref[tile // tiles_per_span, inner : inner + query_tile, :]
    return jnp.where(key_lanes, query, jnp.zeros_like(query))


def group_blocks(bounds_ref, group, size, key_tile):
    first, last = group * size, (group + 1) * size
    low = jnp.min(bounds_ref[0:1, first : first + LANES])
    high = jnp.max(bounds_ref[1:2, last - LANES : last])
    return low // key_tile, (high + key_tile - 1) // key_tile


def inside_document(bounds_ref, tile, first, shape):
    key = first + lax.broadcasted_iota(jnp.int32, shape, 0)
    columns = slice(tile * shape[1], (tile + 1) * shape[1])
    return jnp.logical_and(key >= bounds_ref[0:1, columns], key < bounds_ref[1:2, columns])


def query_group(q_ref, group, y):
    key_lanes = (lane_ids((QUERY_TILE, LANES)) < HALF) == (y == 0)
    tiles = range(group * CHAINS, (group + 1) * CHAINS)
    return tiles, [masked_queries(q_ref, tile, key_lanes, QUERY_TILE) for tile in tiles]


def attend(bounds_ref, tiles, first, keys, keys_across, queries, carry):
    scores = [dot(keys, query, (1, 1)) for query in queries]
    made = []
    for tile, score, (biggest, weight, mixed) in zip(tiles, scores, carry):
        inside = inside_document(bounds_ref, tile, first, score.shape)
        score = jnp.where(inside, score, MASKED)
        bigger = jnp.maximum(biggest, jnp.max(score, axis=0, keepdims=True))
        fade = jnp.exp(biggest - bigger)
        terms = jnp.exp(score - bigger)
        weight = weight * fade + jnp.sum(terms, axis=0, keepdims=True)
        made.append((bigger, weight, mixed * fade + dot(keys_across, terms.astype(BF16))))
    return tuple(made)


def nothing_attended():
    return (
        jnp.full((1, QUERY_TILE), MASKED, F32),
        jnp.zeros((1, QUERY_TILE), F32),
        jnp.zeros((LANES, QUERY_TILE), F32),
    )


def attend_back(bounds_ref, tiles, first, keys, keys_across, group, carry):
    queries, out_grads, deltas, log_totals = group
    scores = [dot(keys, query, (1, 1)) for query in queries]
    weight_grads = [dot(keys, out_grad, (1, 1)) for out_grad in out_grads]
    pieces, score_grads = [], []
    for i, tile in enumerate(tiles):
        inside = inside_document(bounds_ref, tile, first, scores[i].shape)
        weights = jnp.exp(jnp.where(inside, scores[i], MASKED) - log_totals[i])
        score_grads.append((weights * (weight_grads[i] - deltas[i])).astype(BF16))
        pieces.append(weights.astype(BF16))
    wide = jnp.concatenate(score_grads + pieces, axis=1)
    given = dot(wide, jnp.concatenate(queries + out_grads, axis=0))
    return given, tuple(c + dot(keys_across, g) for c, g in zip(carry, score_grads))


def group_grads(do_ref, tiles, y):
    key_lanes = (lane_ids((QUERY_TILE, LANES)) < HALF) == (y == 0)
    out_grads = []
    for tile in tiles:
        parts = []
        for part in range(QUERY_TILE // LANES):
            packed = do_ref[tile, part].astype(F32)
            parts += [packed, pltpu.roll(packed, HALF, 1)]
        out_grads.append(jnp.where(key_lanes, 0.0, jnp.concatenate(parts, axis=0)).astype(BF16))
    return out_grads


def qkv_kernel(
    heads, blks,
    x_hbm, w_hbm, g1_hbm, wo_hbm, wr_hbm, g2_hbm, docs_hbm,
    qall, kvall, xall, wall, wo_all, kvt, bounds, begun,
    x_ref, w_ref, rows_in, g1_ref, g2_ref, wr_ref, docs_ref, wo_own, kv_other, q_packed, q_landed, in_sem,
    x_send, x_recv, w_send, w_recv, o_send, o_recv, p_send, p_recv,
    k_send, k_recv, q_recv,
):
    head, blk, z, y = place()
    planes = blks // 2
    model = x_ref.shape[1]
    rows = w_ref.shape[0]
    part = rows // heads
    experts = wr_ref.shape[0]
    wanted = (
        (w_hbm, w_ref), (g1_hbm, g1_ref), (g2_hbm, g2_ref), (wr_hbm, wr_ref), (x_hbm, x_ref),
        (wo_hbm, wo_own.at[:, pl.ds(0, model)]), (docs_hbm, docs_ref),
    )
    fetched = [
        pltpu.make_async_copy(src, dst, in_sem.at[i]) for i, (src, dst) in enumerate(wanted)
    ]
    for copy in fetched:
        copy.start()
    rows_in[...] = jnp.zeros_like(rows_in)
    met = greet(
        [(around(head, k, heads), blk) for k in range(1, heads)]
        + [(head, around(blk, k, blks)) for k in range(1, blks)]
    )
    lanes = lane_ids((rows, LANES))
    for copy in fetched:
        copy.wait()
    rows_in[0:experts, 0:rows] = wr_ref[...].astype(F32)
    rows_in[experts : experts + 1, 0:rows] = g2_ref[...].astype(F32)
    rows_in[experts + 1 : experts + 2, 0:rows] = g1_ref[...].astype(F32)
    vectors = jnp.transpose(rows_in[...])[:rows]
    gain = vectors[:, experts + 1 : experts + 2]

    def columns(which):
        start = pl.multiple_of(which * model + head * LANES, LANES)
        return w_ref[:, pl.ds(start, LANES)].astype(F32) * gain

    key_cols = columns(1)
    value_cols = pltpu.roll(columns(2), HALF, 1)
    wall[blk, :, 0:LANES] = jnp.where(lanes < HALF, key_cols, value_cols).astype(BF16)
    wall[blk, :, LANES : 2 * LANES] = jnp.where(lanes < HALF, value_cols, key_cols).astype(BF16)
    wall[blk, :, 2 * LANES : 3 * LANES] = (columns(0) * HS ** (-0.5)).astype(BF16)
    def slice_copy(slot, source, target):
        ref = wall.at[source]
        return remote(ref, ref, w_send.at[slot], w_recv.at[source], head, target)

    pair = 2 * z + around(y, 1, 2)
    line = [2 * around(z, step, planes) + y for step in (1, planes - 1, *range(2, planes - 1))]
    w_copies = [slice_copy(slot, blk, target) for slot, target in enumerate((*line, pair))]
    w_onward = [slice_copy(planes + slot, source, pair) for slot, source in enumerate(line)]
    xhat, _ = centre(x_ref[...].astype(F32))
    xall[head] = xhat.astype(BF16)
    meet(met)
    for copy in w_copies:
        copy.start()
    x_copies = [
        remote(xall.at[head], xall.at[head], x_send.at[k], x_recv.at[k], around(head, k, heads), blk)
        for k in range(1, heads)
    ]
    for copy in x_copies:
        copy.start()
    wo_own[:, model : model + LANES] = vectors.astype(BF16)
    wo_all[blk, head] = wo_own[pl.ds(pl.multiple_of(head * part, part), part), :]
    o_copies = [
        remote(
            wo_all.at[blk, head], wo_all.at[blk, head],
            o_send.at[k], o_recv.at[k], head, around(blk, k, blks),
        )
        for k in range(1, blks)
    ]
    document_bounds(docs_ref, bounds, z)
    for source, copy in zip(line, w_onward):
        arrived(wall.at[source], w_recv.at[source])
        copy.start()
    for copy in o_copies:
        copy.start()
    for source in (pair, *[other - y + around(y, 1, 2) for other in line]):
        arrived(wall.at[source], w_recv.at[source])
    for copy in w_copies + w_onward:
        copy.wait_send()
    for copy in x_copies:
        copy.wait()
    weight = wall[...].reshape(model, 3 * LANES)
    tokens = x_ref.shape[0]
    even = y == 0
    above, below = z < planes - 1, z > 0
    half_span = kvall.shape[1] // 2
    sides = ((1, above, below, 0), (-1, below, above, 4))

    def half_of(ref, half):
        return ref.at[pl.ds(half * half_span, half_span)]

    def outward(slot, step, across, half):
        target = 2 * (z + step) + around(y, across, 2)
        return remote(
            half_of(kv_other if across else kvall.at[blk], half), half_of(kvall.at[blk], half),
            k_send.at[slot], k_recv.at[blk, half], head, target,
        )

    def onward(slot, step, side, half):
        from_span = 2 * (z - step) + side
        ref = half_of(kvall.at[from_span], half)
        return remote(ref, ref, k_send.at[slot], k_recv.at[from_span, half], head, 2 * (z + step) + y)

    def await_half(span, half):
        arrived(half_of(kvall.at[span], half), k_recv.at[span, half])

    def turn(span):
        size = kvall.shape[1]
        kvt[:, pl.ds(pl.multiple_of(span * size, size), size)] = jnp.transpose(kvall[span])

    for half in range(2):
        for piece in range(half * heads // 2, (half + 1) * heads // 2):
            made = dot(xall[piece], weight).astype(BF16)
            first, second = made[:, 0:LANES], made[:, LANES : 2 * LANES]
            span = slice(piece * tokens, (piece + 1) * tokens)
            kvall[blk, span, :] = jnp.where(even, first, second)
            kv_other[span, :] = jnp.where(even, second, first)
            qall[y, span, :] = made[:, 2 * LANES : 3 * LANES]
        outward(8 + half, 0, 1, half).start()
        for step, there, _, slot in sides:

            @pl.when(there)
            def _():
                outward(slot + 2 * half, step, 0, half).start()
                outward(slot + 2 * half + 1, step, 1, half).start()

    other_y = around(y, 1, 2)
    kept = (lane_ids(q_packed.shape) < HALF) == (y == 1)
    q_packed[...] = halves(qall[y].astype(F32), kept).astype(BF16)
    q_pair = remote(q_packed, q_landed, k_send.at[10], q_recv, head, 2 * z + other_y)
    q_pair.start()
    turn(blk)
    for copy in o_copies:
        copy.wait()
    core = lax.rem(head, 2)
    sibling, across = head - core + 1 - core, around(head, 2, heads)

    def quarter_copy(index, quarter, to_head):
        ref = wo_all.at[:, quarter]
        return remote(ref, ref, p_send.at[index], p_recv.at[index], to_head, blk)

    p_copies = [quarter_copy(0, head, sibling), quarter_copy(1, head, across)]
    for copy in p_copies:
        copy.start()
    p_copies.append(quarter_copy(2, across, sibling))
    for half in range(2):
        for step, there, back, slot in sides:

            @pl.when(back)
            def _():
                for side in range(2):
                    await_half(2 * (z - step) + side, half)

            @pl.when(jnp.logical_and(there, back))
            def _():
                for side in range(2):
                    onward(11 + slot + 2 * half + side, step, side, half).start()

    arrived(wo_all.at[:, across], p_recv.at[1])
    p_copies[2].start()
    for half in range(2):
        await_half(pair, half)
    turn(pair)
    q_pair.wait()
    landed = q_landed[...]
    qall[other_y, 0:half_span, :] = landed
    qall[other_y, half_span : 2 * half_span, :] = pltpu.roll(landed.astype(F32), HALF, 1).astype(BF16)
    key_tile = kvall.shape[1]
    for group in range(2 * key_tile // (CHAINS * QUERY_TILE)):
        tiles, queries = query_group(qall, group, y)
        carry = (nothing_attended(),) * CHAINS
        for side in range(2):
            first = pl.multiple_of((2 * z + side) * key_tile, key_tile)
            keys_across = kvt[:, pl.ds(first, key_tile)]
            carry = attend(bounds, tiles, first, kvall[2 * z + side], keys_across, queries, carry)
        for tile, (biggest, weight, mixed) in zip(tiles, carry):
            begun[tile, 0:LANES] = mixed
            begun[tile, LANES : LANES + 8] = jnp.broadcast_to(biggest, (8, QUERY_TILE))
            begun[tile, LANES + 8 : LANES + 16] = jnp.broadcast_to(weight, (8, QUERY_TILE))
    for step, there, back, slot in sides:

        @pl.when(back)
        def _():
            for side in range(2):
                turn(2 * (z - step) + side)

    for other in range(planes):
        for side in range(2):
            span = 2 * other + side

            @pl.when(jnp.logical_or(z - other == 2, other - z == 2))
            def _():
                for half in range(2):
                    await_half(span, half)
                    rows_here = slice(half * half_span, (half + 1) * half_span)
                    columns = slice(
                        span * kvall.shape[1] + half * half_span,
                        span * kvall.shape[1] + (half + 1) * half_span,
                    )
                    kvt[:, columns] = jnp.transpose(kvall[span, rows_here])

    for index, quarter in ((0, sibling), (2, around(sibling, 2, heads))):
        arrived(wo_all.at[:, quarter], p_recv.at[index])
    for copy in p_copies:
        copy.wait_send()
    for half in range(2):
        outward(8 + half, 0, 1, half).wait_send()
        for step, there, back, slot in sides:

            @pl.when(there)
            def _():
                outward(slot + 2 * half, step, 0, half).wait_send()
                outward(slot + 2 * half + 1, step, 1, half).wait_send()

            @pl.when(jnp.logical_and(there, back))
            def _():
                for side in range(2):
                    onward(11 + slot + 2 * half + side, step, side, half).wait_send()


def document_bounds(docs_ref, bounds, z):
    count = docs_ref.shape[1]
    lengths = docs_ref[...].astype(F32)
    doc = lax.broadcasted_iota(jnp.int32, (count, count), 0)
    other = lane_ids((count, count))
    start = jnp.sum(jnp.where(other < doc, lengths, 0.0), axis=1, keepdims=True)
    end = jnp.sum(jnp.where(other <= doc, lengths, 0.0), axis=1, keepdims=True)
    queries = bounds.shape[1]
    token = (z * queries + lane_ids((count, queries))).astype(F32)
    begun = start <= token
    bounds[...] = jnp.zeros_like(bounds)
    bounds[0:1, :] = jnp.max(jnp.where(begun, start, 0.0), axis=0, keepdims=True).astype(jnp.int32)
    bounds[1:2, :] = jnp.max(jnp.where(begun, end, 0.0), axis=0, keepdims=True).astype(jnp.int32)


def vmem_specs(count):
    return [pl.BlockSpec(memory_space=pltpu.VMEM)] * count


def hbm_specs(count):
    return [pl.BlockSpec(memory_space=pltpu.HBM)] * count


def in_hbm(*arrays):
    return [pltpu.with_memory_space_constraint(array, pltpu.HBM) for array in arrays]


def dma(*shape):
    return pltpu.SemaphoreType.DMA(shape)


def call_qkv(x, w_qkv, g1, w_out, w_router, g2, doc_lengths, heads, blks):
    tokens, model = x.shape
    rows = w_qkv.shape[0]
    span = tokens * heads
    wide = model + LANES
    part = rows // heads
    return pl.pallas_call(
        functools.partial(qkv_kernel, heads, blks),
        out_shape=(
            jax.ShapeDtypeStruct((2, span, LANES), BF16),
            jax.ShapeDtypeStruct((blks, span, LANES), BF16),
            jax.ShapeDtypeStruct((heads, tokens, model), BF16),
            jax.ShapeDtypeStruct((blks, rows, 3 * LANES), BF16),
            jax.ShapeDtypeStruct((blks, heads, part, wide), BF16),
            jax.ShapeDtypeStruct((LANES, blks * span), BF16),
            jax.ShapeDtypeStruct((8, 2 * span), jnp.int32),
            jax.ShapeDtypeStruct((2 * span // QUERY_TILE, LANES + 16, QUERY_TILE), F32),
        ),
        in_specs=hbm_specs(7),
        out_specs=tuple(vmem_specs(8)),
        scratch_shapes=[
            pltpu.VMEM((tokens, model), BF16),
            pltpu.VMEM((rows, 3 * model), BF16),
            pltpu.VMEM((LANES, LANES), F32),
            pltpu.VMEM((1, rows), BF16),
            pltpu.VMEM((1, rows), BF16),
            pltpu.VMEM((w_router.shape[1], rows), BF16),
            pltpu.VMEM((1, doc_lengths.shape[0]), jnp.int32),
            pltpu.VMEM((rows, wide), BF16),
            pltpu.VMEM((span, LANES), BF16),
            pltpu.VMEM((span // 2, LANES), BF16),
            pltpu.VMEM((span // 2, LANES), BF16),
            dma(7),
            dma(heads), dma(heads), dma(blks), dma(blks), dma(blks), dma(blks), dma(heads), dma(heads),
            dma(19), dma(blks, 2), pltpu.SemaphoreType.DMA,
        ],
        compiler_params=pltpu.CompilerParams(
            collective_id=1, has_side_effects=True, vmem_limit_bytes=16 * MIB
        ),
        name="qkv",
    )(
        *in_hbm(
            x, w_qkv, g1.reshape(1, rows), w_out, w_router.T, g2.reshape(1, rows),
            doc_lengths.reshape(1, -1),
        )
    )


def other_blocks(bounds_ref, group, key_tile, z, step, carry):
    low, high = group_blocks(bounds_ref, group, CHAINS * QUERY_TILE, key_tile)
    carry = lax.fori_loop(low, 2 * z, step, carry)
    return lax.fori_loop(2 * z + 2, high, step, carry)


def forward_kernel(bounds_ref, q_ref, kv_ref, kvt_ref, begun_ref, o_out, ob_out, lse_out):
    _, _, z, y = place()
    key_tile = kv_ref.shape[1]
    value_lanes = (lane_ids((HALF, LANES)) < HALF) == (y == 1)
    for group in range(q_ref.shape[0] * q_ref.shape[1] // (CHAINS * QUERY_TILE)):
        tiles, queries = query_group(q_ref, group, y)

        def step(block, carry, queries=queries, tiles=tiles):
            first = pl.multiple_of(block * key_tile, key_tile)
            across = kvt_ref[:, pl.ds(first, key_tile)]
            return attend(bounds_ref, tiles, first, kv_ref[block], across, queries, carry)

        start = tuple(
            (begun_ref[t, LANES : LANES + 1], begun_ref[t, LANES + 8 : LANES + 9], begun_ref[t, 0:LANES])
            for t in tiles
        )
        ends = other_blocks(bounds_ref, group, key_tile, z, step, start)
        for tile, (biggest, weight, mixed) in zip(tiles, ends):
            result = jnp.transpose(mixed / weight)
            o_out[tile] = result
            for part in range(QUERY_TILE // LANES):
                block = result[part * LANES : (part + 1) * LANES]
                ob_out[tile, part] = halves(block, value_lanes).astype(BF16)
            lse_out[tile] = jnp.broadcast_to(biggest + jnp.log(weight), (8, QUERY_TILE))


def call_forward(bounds, q, kv, kvt, begun):
    blks, span, _ = kv.shape
    tiles = 2 * span // QUERY_TILE
    return pl.pallas_call(
        forward_kernel,
        out_shape=(
            jax.ShapeDtypeStruct((tiles, QUERY_TILE, LANES), F32),
            jax.ShapeDtypeStruct((tiles, QUERY_TILE // LANES, HALF, LANES), BF16),
            jax.ShapeDtypeStruct((tiles, 8, QUERY_TILE), F32),
        ),
        in_specs=vmem_specs(5),
        out_specs=tuple(vmem_specs(3)),
        compiler_params=pltpu.CompilerParams(vmem_limit_bytes=16 * MIB),
        name="attend",
    )(bounds, q, kv, kvt, begun)


def backward_kernel(
    bounds_ref, q_ref, kv_ref, kvt_ref, do_ref, o_ref, lse_ref, dq_out, dkv_out, delta_out, dkv
):
    _, _, z, y = place()
    key_tile = kv_ref.shape[1]
    for block in range(dkv.shape[0]):

        @pl.when(block // 2 != z)
        def _():
            dkv[block] = jnp.zeros(dkv.shape[1:], F32)

    for group in range(q_ref.shape[0] * q_ref.shape[1] // (CHAINS * QUERY_TILE)):
        tiles, queries = query_group(q_ref, group, y)
        out_grads = group_grads(do_ref, tiles, y)
        deltas, log_totals = [], []
        for tile, out_grad in zip(tiles, out_grads):
            product = jnp.transpose(out_grad.astype(F32) * o_ref[tile])
            deltas.append(jnp.sum(product, axis=0, keepdims=True))
            delta_out[tile] = jnp.broadcast_to(deltas[-1], delta_out.shape[1:])
            log_totals.append(lse_ref[tile, 0:1, :])
        known = (queries, out_grads, deltas, log_totals)

        def step(block, carry, tiles=tiles, known=known):
            first = pl.multiple_of(block * key_tile, key_tile)
            across = kvt_ref[:, pl.ds(first, key_tile)]
            given, carry = attend_back(bounds_ref, tiles, first, kv_ref[block], across, known, carry)
            dkv[block] += given
            return carry

        zero = jnp.zeros((LANES, QUERY_TILE), F32)
        ends = other_blocks(bounds_ref, group, key_tile, z, step, (zero,) * CHAINS)
        for tile, mixed in zip(tiles, ends):
            dq_out[tile] = mixed
    for block in range(dkv.shape[0]):

        @pl.when(block // 2 != z)
        def _():
            dkv_out[block] = dkv[block].astype(BF16)


def call_backward(bounds, q, kv, kvt, d_o, o, lse):
    blks, span, _ = kv.shape
    tiles = 2 * span // QUERY_TILE
    return pl.pallas_call(
        backward_kernel,
        out_shape=(
            jax.ShapeDtypeStruct((tiles, LANES, QUERY_TILE), F32),
            jax.ShapeDtypeStruct((blks, span, LANES), BF16),
            jax.ShapeDtypeStruct((tiles, 8, QUERY_TILE), F32),
        ),
        in_specs=vmem_specs(7),
        out_specs=tuple(vmem_specs(3)),
        scratch_shapes=[pltpu.VMEM((blks, span, LANES), F32)],
        compiler_params=pltpu.CompilerParams(vmem_limit_bytes=16 * MIB),
        name="attend_back",
    )(bounds, q, kv, kvt, d_o, o, lse)


def gelu_parts(values):
    share = 0.5 * (1.0 + lax.erf(values * (2.0**-0.5)))
    slope = share + values * jnp.exp(-0.5 * values * values) * (2.0 * math.pi) ** -0.5
    return values * share, slope


def positions(expert_rows, expert_cols, rank_row, rank_col):
    def count(mask, axis):
        return jnp.sum(mask.astype(F32), axis=axis, keepdims=True)

    row = [None, None]
    col = [None, None]
    before = rank_col < rank_row
    after = rank_row < rank_col
    for choice in range(2):
        row[choice] = count((expert_cols[choice] == expert_rows[choice]) & before, 0)
        col[choice] = count((expert_rows[choice] == expert_cols[choice]) & after, 1)
    row[1] = row[1] + count(expert_cols[0] == expert_rows[1], 0)
    col[1] = col[1] + count(expert_rows[0] == expert_cols[1], 1)
    return row, col


def own_columns(rows_ref, turned, blk, capacity):
    blks, _, slots = rows_ref.shape
    rows = jnp.concatenate(
        [rows_ref[...].reshape(blks, slots), jnp.zeros((LANES - blks, slots), F32)], axis=0
    )
    for piece in range(slots // LANES):
        columns = slice(piece * LANES, (piece + 1) * LANES)
        turned[columns, :] = jnp.transpose(rows[:, columns])
    own = turned[pl.ds(pl.multiple_of(blk * capacity, capacity), capacity), :]
    return jnp.concatenate([own[:, source : source + 1] for source in range(blks)], axis=0)


def middle_kernel(
    heads, blks,
    x_hbm, o_ref, wo_ref, routes_hbm, rank_hbm, d_out_hbm, win_hbm, wout_hbm,
    po, hidden_ref, share_ref, dh_ref, dma_all, grads_ref, rx,
    x_ref, routes_ref, rank_ref, d_out_ref, win_ref, wout_ref, rows_in, in_sem,
    o_all, dos, doa, rs, ra, dr, da, dms, mix, gate_rows, d_gate_rows, turned,
    o_send, o_recv, dos_send, dos_recv, r_send, r_recv,
    dr_send, dr_recv, dm_send, dm_recv, rx_send, rx_recv, g_send, g_recv, dg_send, dg_recv,
):
    head, blk, z, y = place()
    tokens, model = x_ref.shape
    capacity = 2 * tokens // blks
    slots = capacity * blks
    plane = [(k % heads, k // heads) for k in range(1, 2 * heads)]
    wanted = (
        (routes_hbm, routes_ref), (rank_hbm, rank_ref), (d_out_hbm, d_out_ref), (x_hbm, x_ref),
        (win_hbm, win_ref), (wout_hbm, wout_ref),
    )
    fetched = [
        pltpu.make_async_copy(src, dst, in_sem.at[i]) for i, (src, dst) in enumerate(wanted)
    ]
    for copy in fetched:
        copy.start()
    met = greet(
        [(around(head, kh, heads), 2 * z + around(y, ky, 2)) for kh, ky in plane]
        + [(head, around(blk, k, blks)) for k in range(1, blks)]
    )
    meet(met)

    def plane_copies(src_of, dst, send, recv):
        copies = []
        for k, (kh, ky) in enumerate(plane):
            to_head, to_y = around(head, kh, heads), around(y, ky, 2)
            copies.append(
                remote(src_of(to_y, to_head), dst, send.at[k], recv.at[k], to_head, 2 * z + to_y)
            )
        return copies

    def blk_copies(src, dst, send, recv):
        return [
            remote(
                src.at[around(blk, k, blks)], dst.at[blk],
                send.at[k], recv.at[k], head, around(blk, k, blks),
            )
            for k in range(1, blks)
        ]

    def start(copies):
        for copy in copies:
            copy.start()

    def finish(copies):
        for copy in copies:
            copy.wait()

    o_copies = plane_copies(lambda to_y, to_head: o_ref.at[to_y, to_head], o_all.at[y, head], o_send, o_recv)
    start(o_copies)
    o_all[y, head] = o_ref[y, head]

    lanes = lane_ids((tokens, LANES))
    for copy in fetched[:4]:
        copy.wait()
    e_rows = [routes_ref[i : i + 1, :].astype(F32) for i in range(2)]
    rank_row = rank_ref[...].astype(F32)
    rows_in[...] = jnp.zeros_like(rows_in)
    rows_in[0:1, :], rows_in[1:2, :], rows_in[2:3, :] = *e_rows, rank_row
    columns = jnp.transpose(rows_in[...])
    e_cols = [columns[:, 0:1], columns[:, 1:2]]
    rank_col = columns[:, 2:3]
    pos_rows, pos_cols = positions(e_rows, e_cols, rank_row, rank_col)

    def slot_of(expert, position):
        return jnp.where(position < capacity, expert * capacity + position, -1.0).astype(jnp.int32)

    slot_rows = [slot_of(e, p) for e, p in zip(e_rows, pos_rows)]
    slot_cols = [slot_of(e, p) for e, p in zip(e_cols, pos_cols)]
    slot_down = lax.broadcasted_iota(jnp.int32, (slots, tokens), 0)
    slot_across = lane_ids((tokens, slots))
    pick = [(slot_down == s).astype(BF16) for s in slot_rows]
    put = [(slot_across == s).astype(BF16) for s in slot_cols]
    pick_any = pick[0] + pick[1]
    put_any = put[0] + put[1]

    d_out = d_out_ref[...]
    dos[...] = dot(pick_any, d_out.astype(BF16)).astype(BF16).reshape(dos.shape)
    dos_copies = blk_copies(dos, doa, dos_send, dos_recv)
    start(dos_copies)
    doa[blk] = dos[blk]

    weight_out = jnp.concatenate(
        [wo_ref[(b ^ 1) * HALF : ((b ^ 1) + 1) * HALF, 0:model] for b in range(blks)], axis=0
    )
    small = wo_ref[:, model : model + LANES]
    small_across = jnp.concatenate(
        [
            jnp.transpose(small[i * LANES : (i + 1) * LANES].astype(F32))
            for i in range(model // LANES)
        ],
        axis=1,
    )
    gain = small_across[blks : blks + 1, :]

    finish(o_copies)
    low_lanes = lanes[:HALF] < HALF
    for piece in range(heads):
        columns = slice(piece * LANES, (piece + 1) * LANES)
        first, second = o_all[1, piece].astype(F32), o_all[0, piece].astype(F32)
        mix[:HALF, columns] = jnp.where(low_lanes, first, second).astype(BF16)
        swapped = pltpu.roll(jnp.where(low_lanes, second, first), HALF, 1)
        mix[HALF:, columns] = swapped.astype(BF16)
    mixed = mix[...]
    hidden = x_ref[...].astype(F32) + dot(mixed, weight_out)
    xhat, scale = centre(hidden)
    routed = (xhat * gain).astype(BF16)
    rs[...] = dot(pick_any, routed).astype(BF16).reshape(rs.shape)
    r_copies = blk_copies(rs, ra, r_send, r_recv)
    start(r_copies)
    ra[blk] = rs[blk]
    logits = jnp.where(lanes < blks, dot(routed, small), MASKED)
    powers = jnp.exp(logits - jnp.max(logits, axis=1, keepdims=True))
    probs = powers / jnp.sum(powers, axis=1, keepdims=True)
    lanes_f = lanes.astype(F32)
    hots = [lanes_f == e for e in e_cols]
    gates = [jnp.sum(jnp.where(hot, probs, 0.0), axis=1, keepdims=True) for hot in hots]
    gate_high = [g.astype(BF16).astype(F32) for g in gates]
    gate_across = jnp.transpose(
        jnp.where(lanes == 0, gate_high[0], jnp.where(lanes == 1, gates[0] - gate_high[0], 0.0))
        + jnp.where(lanes == 2, gate_high[1], jnp.where(lanes == 3, gates[1] - gate_high[1], 0.0))
    ).astype(BF16)
    by_slot = (dot(gate_across, put[0]), dot(gate_across, put[1]))
    gate_rows[blk] = by_slot[0][0:1] + by_slot[0][1:2] + by_slot[1][2:3] + by_slot[1][3:4]
    g_copies = [
        remote(
            gate_rows.at[blk], gate_rows.at[blk],
            g_send.at[k], g_recv.at[k], head, around(blk, k, blks),
        )
        for k in range(1, blks)
    ]
    start(g_copies)
    finish(dos_copies)
    finish(r_copies)

    out_rows = doa[...].reshape(slots, model)
    rx[head, :, 0:model] = ra[...].reshape(slots, model)
    finish(g_copies)
    gate_col = own_columns(gate_rows, turned, blk, capacity)
    rx[head, :, model : 2 * model] = (out_rows.astype(F32) * gate_col).astype(BF16)
    core = lax.rem(head, 2)
    sibling, across = head - core + 1 - core, around(head, 2, heads)

    def half_rows(source, half):
        return rx.at[source, pl.ds(half * slots // 2, slots // 2)]

    to_across = [
        remote(
            half_rows(head, half), half_rows(head, half),
            rx_send.at[1 + half], rx_recv.at[1 + half], across, blk,
        )
        for half in range(2)
    ]
    to_sibling = remote(rx.at[head], rx.at[head], rx_send.at[0], rx_recv.at[0], sibling, blk)
    forwards = [
        remote(
            half_rows(across, half), half_rows(across, half),
            rx_send.at[3 + half], rx_recv.at[3 + half], sibling, blk,
        )
        for half in range(2)
    ]
    start(to_across)
    to_sibling.start()
    for copy in fetched[4:]:
        copy.wait()
    act, slope = gelu_parts(dot(rx[head, :, 0:model], win_ref[...]))
    d_act = dot(rx[head, :, model : 2 * model], wout_ref[...], (1, 1))
    row_grads = dot((slope * d_act).astype(BF16), win_ref[...], (1, 1))
    dr[...] = row_grads.astype(BF16).reshape(dr.shape)
    dr_copies = blk_copies(dr, da, dr_send, dr_recv)
    start(dr_copies)
    result = dot(act.astype(BF16), wout_ref[...]).astype(BF16)
    d_gate = jnp.sum(out_rows.astype(F32) * result.astype(F32), axis=1, keepdims=True)
    da[blk] = dr[blk]
    d_wide = jnp.broadcast_to(d_gate, (slots, LANES))
    d_gate_rows[blk] = jnp.concatenate(
        [jnp.transpose(d_wide[i * LANES : (i + 1) * LANES])[0:1] for i in range(slots // LANES)],
        axis=1,
    )
    dg_copies = [
        remote(
            d_gate_rows.at[blk], d_gate_rows.at[blk],
            dg_send.at[k], dg_recv.at[k], head, around(blk, k, blks),
        )
        for k in range(1, blks)
    ]
    start(dg_copies)
    po[...] = result.reshape(blks, capacity, model)

    finish(dg_copies)
    back_gate = own_columns(d_gate_rows, turned, blk, capacity)
    back_gate = split_high_low(back_gate, lane_ids((slots, LANES)))
    d_gates = [join_high_low(dot(p, back_gate), 0) for p in put]
    d_probs = jnp.where(hots[0], d_gates[0], 0.0) + jnp.where(hots[1], d_gates[1], 0.0)
    d_logits = probs * (d_probs - jnp.sum(probs * d_probs, axis=1, keepdims=True))
    d_high = d_logits.astype(BF16)
    d_low = (d_logits - d_high.astype(F32)).astype(BF16)
    d_router_part = dot(d_high, small, (1, 1)) + dot(d_low, small, (1, 1))
    finish(dr_copies)
    d_routed = dot(put_any, da[...].reshape(slots, model)) + d_router_part
    d_hidden = d_out + centre_back(d_routed * gain, xhat, scale)
    dh_ref[...] = d_hidden
    d_attn = d_hidden.astype(BF16)
    d_mixed = dot(d_attn, weight_out, (1, 1))
    for piece in range(heads):
        block = d_mixed[:, piece * LANES : (piece + 1) * LANES]
        for to_y in range(2):
            dms[to_y, piece] = halves(block, low_lanes == (to_y == 1)).astype(BF16)
    dm_copies = plane_copies(lambda to_y, to_head: dms.at[to_y, to_head], dma_all.at[y, head], dm_send, dm_recv)
    start(dm_copies)
    dma_all[y, head] = dms[y, head]
    arrived(half_rows(across, 0), rx_recv.at[1])
    forwards[0].start()

    d_weight = dot(mixed, d_attn, (0, 0)).astype(BF16)
    for b in range(blks):
        grads_ref[b, :, 0:model] = d_weight[(b ^ 1) * HALF : ((b ^ 1) + 1) * HALF, :]
    last = (lanes == blks).astype(BF16)
    d_small = dot(routed, d_high, (0, 0)) + dot((d_routed * xhat).astype(BF16), last, (0, 0))
    grads_ref[:, :, model : model + LANES] = d_small.astype(BF16).reshape(blks, HALF, LANES)
    share = gates[0] * put[0].astype(F32) + gates[1] * put[1].astype(F32)
    share_ref[0] = share.astype(BF16)
    share_ref[1] = (share - share_ref[0].astype(F32)).astype(BF16)
    hidden_ref[...] = hidden

    arrived(half_rows(across, 1), rx_recv.at[2])
    forwards[1].start()
    finish(dm_copies)
    to_sibling.wait()
    for copy in to_across:
        copy.wait_send()
    finish(forwards)


def call_middle(x, o, wo, routes, rank, d_out, win, wout, heads, blks):
    tokens, model = x.shape
    capacity = 2 * tokens // blks
    slots = capacity * blks
    wide = model + LANES

    def rows(width):
        return pltpu.VMEM((blks, capacity, width), BF16)

    def block(*lead):
        return pltpu.VMEM((*lead, tokens // 2, LANES), BF16)

    return pl.pallas_call(
        functools.partial(middle_kernel, heads, blks),
        out_shape=(
            jax.ShapeDtypeStruct((blks, capacity, model), BF16),
            jax.ShapeDtypeStruct((tokens, model), F32),
            jax.ShapeDtypeStruct((2, tokens, slots), BF16),
            jax.ShapeDtypeStruct((tokens, model), F32),
            jax.ShapeDtypeStruct((2, heads, tokens // 2, LANES), BF16),
            jax.ShapeDtypeStruct((blks, model // blks, wide), BF16),
            jax.ShapeDtypeStruct((heads, slots, 2 * model), BF16),
        ),
        in_specs=hbm_specs(1) + vmem_specs(2) + hbm_specs(5),
        out_specs=tuple(vmem_specs(7)),
        scratch_shapes=[
            pltpu.VMEM((tokens, model), BF16),
            pltpu.VMEM((2, tokens), jnp.int32),
            pltpu.VMEM((1, tokens), jnp.int32),
            pltpu.VMEM((tokens, model), F32),
            pltpu.VMEM(win.shape, BF16),
            pltpu.VMEM(wout.shape, BF16),
            pltpu.VMEM((tokens, tokens), F32),
            dma(6),
            block(2, heads), rows(model), rows(model), rows(model), rows(model),
            rows(model), rows(model), block(2, heads),
            pltpu.VMEM((tokens, model), BF16),
            pltpu.VMEM((blks, 1, slots), F32), pltpu.VMEM((blks, 1, slots), F32),
            pltpu.VMEM((slots, LANES), F32),
            dma(2 * heads), dma(2 * heads), dma(blks), dma(blks), dma(blks), dma(blks),
            dma(blks), dma(blks), dma(2 * heads), dma(2 * heads), dma(5), dma(5),
            dma(blks), dma(blks), dma(blks), dma(blks),
        ],
        compiler_params=pltpu.CompilerParams(
            collective_id=2, has_side_effects=True, vmem_limit_bytes=20 * MIB
        ),
        name="experts",
    )(*in_hbm(x), o, wo, *in_hbm(routes.T, rank, d_out, win, wout))


def last_kernel(
    heads, blks,
    x_hbm, dh_ref, begun_ref, dkv_ref, xa_ref, wa_ref, w_hbm, g1_hbm, grads_ref, rx_ref, win_hbm, wout_hbm,
    po_ref, hidden_ref, share_ref, bounds_ref, q_ref, kv_ref, kvt_ref, do_ref, lse_ref, delta_ref,
    y_ref, dx_ref, dw_ref, shared_ref, din_ref, dout_ref,
    x_ref, w_ref, g1_ref, win_ref, wout_ref, in_sem,
    gain_tile, far_all, near_send_buf, near_all, pair_all, dq_all, dq_ref, dq_packed, dkv_own, pair_buf, us, ua, gs, ga, gqs, gqa, u_part, xat, pa, gh, ghq, w1, w2s, w2, w3,
    q_send, q_recv, pair_send, pair_recv, far_send, far_recv, near_send, near_recv,
    u_send, u_recv, g_send, g_recv, gh_send, gh_recv, w1_send, w1_recv, w2_send, w2_recv,
    w3_send, w3_recv, e_send, e_recv, gq_send, gq_recv, po_send, po_recv, ghq_send, ghq_recv,
    din_half, dout_half,
):
    head, blk, z, y = place()
    planes = blks // 2
    tokens, model = x_ref.shape
    rows = w_ref.shape[0]
    wanted = (
        (win_hbm, win_ref), (wout_hbm, wout_ref), (x_hbm, x_ref), (w_hbm, w_ref), (g1_hbm, g1_ref)
    )
    fetched = [
        pltpu.make_async_copy(src, dst, in_sem.at[i]) for i, (src, dst) in enumerate(wanted)
    ]
    for copy in fetched:
        copy.start()
    met = greet(
        [(around(head, k, heads), blk) for k in range(1, heads)]
        + [(head, around(blk, k, blks)) for k in range(1, blks)]
    )
    meet(met)

    def start(copies):
        for copy in copies:
            copy.start()

    def finish(copies):
        for copy in copies:
            copy.wait()

    other_y = around(y, 1, 2)
    pair = 2 * z + other_y
    above, below = z < planes - 1, z > 0
    directions = ((1, above, below, 0), (-1, below, above, 2))

    half_span = dkv_ref.shape[1] // 2

    def half_of(ref, half):
        return ref.at[pl.ds(half * half_span, half_span)]

    def far_copy(step, slot, side, half):
        span = 2 * (z + 2 * step) + side
        return remote(
            half_of(dkv_ref.at[span], half), half_of(far_all.at[slot + side], half),
            far_send.at[slot + side, half], far_recv.at[slot + side, half], head, 2 * (z + step) + y,
        )

    def near_copy(step, slot, side, half):
        return remote(
            half_of(near_send_buf.at[slot + side], half), half_of(near_all.at[slot // 2, y], half),
            near_send.at[slot + side, half], near_recv.at[slot // 2, y, half],
            head, 2 * (z + step) + side,
        )

    def two_away(step):
        return z + 2 * step < planes if step > 0 else z + 2 * step >= 0

    for half in range(2):
        for step, there, back, slot in directions:

            @pl.when(two_away(step))
            def _():
                for side in range(2):
                    far_copy(step, slot, side, half).start()

    w1_copies = [
        remote(
            grads_ref.at[:, around(head, k, heads)], w1.at[head],
            w1_send.at[k], w1_recv.at[k], around(head, k, heads), blk,
        )
        for k in range(1, heads)
    ]
    start(w1_copies)
    w1[head] = grads_ref[:, head]

    core = lax.rem(head, 2)
    sibling = head - core + 1 - core
    ff_half = wout_ref.shape[0] // 2
    ff_step = ff_half // 2

    def expert_chunk(chunk):
        here = pl.multiple_of(core * ff_half + chunk * ff_step, ff_step)
        there = pl.multiple_of(chunk * ff_step, ff_step)
        into = win_ref[:, pl.ds(here, ff_step)]
        outof = wout_ref[pl.ds(here, ff_step), :]
        d_in = jnp.zeros((model, ff_step), F32)
        d_out = jnp.zeros((ff_step, model), F32)
        for source in range(heads):
            rows_in = rx_ref[source, :, 0:model]
            grads_out = rx_ref[source, :, model : 2 * model]
            act, slope = gelu_parts(dot(rows_in, into))
            d_act = dot(grads_out, outof, (1, 1))
            d_in = d_in + dot(rows_in, (slope * d_act).astype(BF16), (0, 0))
            d_out = d_out + dot(act.astype(BF16), grads_out, (0, 0))
        din_ref[:, pl.ds(here, ff_step)] = d_in
        dout_ref[pl.ds(here, ff_step), :] = d_out
        din_half[core, :, pl.ds(there, ff_step)] = d_in.astype(BF16)
        dout_half[core, pl.ds(there, ff_step), :] = d_out.astype(BF16)

    key_tile = kv_ref.shape[1]
    for group in range(2 * key_tile // (CHAINS * QUERY_TILE)):
        tiles, queries = query_group(q_ref, group, y)
        known = (
            queries,
            group_grads(do_ref, tiles, y),
            [delta_ref[tile, 0:1, :] for tile in tiles],
            [lse_ref[tile, 0:1, :] for tile in tiles],
        )
        carry = tuple(begun_ref[tile] for tile in tiles)
        for side in range(2):
            first = pl.multiple_of((2 * z + side) * key_tile, key_tile)
            keys_across = kvt_ref[:, pl.ds(first, key_tile)]
            given, carry = attend_back(
                bounds_ref, tiles, first, kv_ref[2 * z + side], keys_across, known, carry
            )
            dkv_own[side] = given if group == 0 else dkv_own[side] + given
        for tile, total in zip(tiles, carry):
            at = tile * QUERY_TILE % key_tile
            dq_ref[tile * QUERY_TILE // key_tile, at : at + QUERY_TILE] = jnp.transpose(total)
    pair_buf[...] = dkv_own[other_y].astype(BF16)
    pair_copy = remote(pair_buf, pair_all, pair_send, pair_recv, head, pair)
    pair_copy.start()
    own_lanes = (lane_ids(dq_packed.shape) < HALF) == (y == 0)
    dq_packed[...] = halves(dq_ref[other_y], own_lanes).astype(BF16)
    q_copy = remote(dq_packed, dq_all, q_send, q_recv, head, pair)
    q_copy.start()
    for half in range(2):
        rows_here = slice(half * half_span, (half + 1) * half_span)
        for step, there, back, slot in directions:

            @pl.when(there)
            def _():
                for side in range(2):
                    near_send_buf[slot + side, rows_here] = dkv_ref[2 * (z + step) + side, rows_here]

            @pl.when(jnp.logical_and(there, back))
            def _():
                for side in range(2):
                    arrived(half_of(far_all.at[slot + side], half), far_recv.at[slot + side, half])
                    near_send_buf[slot + side, rows_here] = (
                        near_send_buf[slot + side, rows_here].astype(F32)
                        + far_all[slot + side, rows_here].astype(F32)
                    ).astype(BF16)

            @pl.when(there)
            def _():
                for side in range(2):
                    near_copy(step, slot, side, half).start()

    finish(fetched[:2])
    weight = wa_ref[...].reshape(model, 3 * LANES)
    for piece in range(heads):
        xat[:, piece * tokens : (piece + 1) * tokens] = jnp.transpose(xa_ref[piece])
    even = y == 0


    expert_chunk(0)

    q_copy.wait()
    landed = dq_all[...].astype(F32)
    landed = jnp.concatenate([landed, pltpu.roll(landed, HALF, 1)], axis=0)
    own_lanes = (lane_ids(landed.shape) < HALF) == even
    q_grads = jnp.where(own_lanes, dq_ref[y], landed).astype(BF16)
    gqs[...] = dot(xat[...], q_grads).astype(BF16).reshape(gqs.shape)
    gq_copies = [
        remote(
            gqs.at[around(blk, k, blks)], gqa.at[blk],
            gq_send.at[k], gq_recv.at[k], head, around(blk, k, blks),
        )
        for k in range(1, blks)
    ]
    start(gq_copies)
    gqa[blk] = gqs[blk]
    u_part[...] = dot(q_grads, weight[:, 2 * LANES : 3 * LANES], (1, 1)).reshape(u_part.shape)

    finish(w1_copies)
    summed = w1[0].astype(F32)
    for source in range(1, heads):
        summed = summed + w1[source].astype(F32)
    w2s[...] = summed.astype(BF16)
    w2_copies = [
        remote(
            w2s.at[around(blk, k, blks)], w2.at[blk],
            w2_send.at[k], w2_recv.at[k], head, around(blk, k, blks),
        )
        for k in range(1, blks)
    ]
    start(w2_copies)
    w2[blk] = w2s[blk]

    expert_chunk(1)

    e_copies = [
        remote(din_half.at[core], din_half.at[core], e_send.at[0], e_recv.at[0], sibling, blk),
        remote(dout_half.at[core], dout_half.at[core], e_send.at[1], e_recv.at[1], sibling, blk),
    ]
    start(e_copies)

    pair_copy.wait()
    for step, there, back, slot in directions:

        @pl.when(back)
        def _():
            for side in range(2):
                for half in range(2):
                    arrived(
                        half_of(near_all.at[slot // 2, side], half),
                        near_recv.at[slot // 2, side, half],
                    )

        @pl.when(jnp.logical_not(back))
        def _():
            near_all[slot // 2] = jnp.zeros(near_all.shape[1:], BF16)

    own = dkv_own[y]
    other = pair_all[...].astype(F32)
    made = jnp.concatenate(
        [
            (
                jnp.where(even == (side == 0), own, other)
                + near_all[0, side].astype(F32)
                + near_all[1, side].astype(F32)
            ).astype(BF16)
            for side in range(2)
        ],
        axis=1,
    )
    gs[...] = dot(xat[...], made).astype(BF16).reshape(gs.shape)
    g_copies = [
        remote(
            gs.at[around(blk, k, blks)], ga.at[blk],
            g_send.at[k], g_recv.at[k], head, around(blk, k, blks),
        )
        for k in range(1, blks)
    ]
    start(g_copies)
    ga[blk] = gs[blk]
    us[...] = (
        u_part[...] + dot(made, weight[:, 0 : 2 * LANES], (1, 1)).reshape(us.shape)
    ).astype(BF16)
    u_copies = [
        remote(
            us.at[around(head, k, heads)], ua.at[head],
            u_send.at[k], u_recv.at[k], around(head, k, heads), blk,
        )
        for k in range(1, heads)
    ]
    start(u_copies)
    ua[head] = us[head]
    finish(fetched[2:])
    finish(gq_copies)
    total = gqa[0].astype(F32)
    for source in range(1, blks):
        total = total + gqa[source].astype(F32)
    ghq[head] = total.astype(BF16)
    ghq_copies = [
        remote(ghq.at[head], ghq.at[head], ghq_send.at[k], ghq_recv.at[k], around(head, k, heads), blk)
        for k in range(1, heads)
    ]
    start(ghq_copies)

    finish(w2_copies)
    part = w2[0].astype(F32)
    for source in range(1, blks):
        part = part + w2[source].astype(F32)
    w3[head] = part.astype(BF16)
    w3_copies = [
        remote(w3.at[head], w3.at[head], w3_send.at[k], w3_recv.at[k], around(head, k, heads), blk)
        for k in range(1, heads)
    ]
    start(w3_copies)

    xhat, scale = centre(x_ref[...].astype(F32))
    finish(e_copies)
    there = pl.multiple_of((1 - core) * ff_half, ff_half)
    din_ref[:, pl.ds(there, ff_half)] = din_half[1 - core].astype(F32)
    dout_ref[pl.ds(there, ff_half), :] = dout_half[1 - core].astype(F32)
    finish(g_copies)
    total = ga[0].astype(F32)
    for source in range(1, blks):
        total = total + ga[source].astype(F32)
    gh[head] = total.astype(BF16)
    gh_copies = [
        remote(gh.at[head], gh.at[head], gh_send.at[k], gh_recv.at[k], around(head, k, heads), blk)
        for k in range(1, heads)
    ]
    start(gh_copies)
    po_copies = [
        remote(
            po_ref.at[around(blk, k, blks)], pa.at[blk],
            po_send.at[k], po_recv.at[k], head, around(blk, k, blks),
        )
        for k in range(1, blks)
    ]
    start(po_copies)
    pa[blk] = po_ref[blk]
    finish(u_copies)
    grad = ua[0].astype(F32)
    for source in range(1, heads):
        grad = grad + ua[source].astype(F32)
    dx_ref[...] = dh_ref[...] + centre_back(grad, xhat, scale)

    gain_tile[...] = jnp.zeros_like(gain_tile)
    gain_tile[0:1, 0:rows] = g1_ref[...].astype(F32)
    gain = jnp.transpose(jnp.broadcast_to(gain_tile[0:1, :], (LANES, LANES)))[:rows]
    low_half = lane_ids((rows, LANES)) < HALF
    finish(ghq_copies)
    finish(gh_copies)
    d_gain = jnp.zeros((rows, LANES), F32)
    for source in range(heads):
        both = [gh[source, :, i * LANES : (i + 1) * LANES].astype(F32) for i in range(2)]
        grads = (
            ghq[source].astype(F32) * HS ** (-0.5),
            jnp.where(low_half, both[0], both[1]),
            pltpu.roll(jnp.where(low_half, both[1], both[0]), HALF, 1),
        )
        for which, value in enumerate(grads):
            columns = slice(which * model + source * LANES, which * model + (source + 1) * LANES)
            d_gain = d_gain + value * w_ref[:, columns].astype(F32)
            dw_ref[:, columns] = value * gain
    finish(w3_copies)
    shared = w3[...].reshape(rows, w3.shape[-1]).astype(F32)
    shared_ref[:, 0:model] = shared[:, 0:model]
    gain_col = jnp.sum(d_gain, axis=1, keepdims=True)
    shared_ref[:, model : model + LANES] = jnp.where(
        lane_ids((rows, LANES)) == blks + 1, gain_col, shared[:, model : model + LANES]
    )
    finish(po_copies)
    parts = pa[...].reshape(share_ref.shape[2], model)
    mixture = dot(share_ref[0], parts) + dot(share_ref[1], parts)
    y_ref[...] = (hidden_ref[...] + mixture).astype(BF16)

    for step, there, back, slot in directions:

        @pl.when(two_away(step))
        def _():
            for side in range(2):
                for half in range(2):
                    far_copy(step, slot, side, half).wait_send()

        @pl.when(there)
        def _():
            for side in range(2):
                for half in range(2):
                    near_copy(step, slot, side, half).wait_send()


def call_last(
    x, dh, dq, dkv, xa, wa, w_qkv, g1, grads, rx, win, wout, po, hidden, share,
    bounds, q, kv, kvt, d_o, lse, delta, heads, blks,
):
    tokens, model = x.shape
    span = tokens * heads
    rows = w_qkv.shape[0]
    wide = model + LANES
    part = rows // heads
    ff = wout.shape[0]

    def block(*lead):
        return pltpu.VMEM((*lead, span, LANES), BF16)

    return pl.pallas_call(
        functools.partial(last_kernel, heads, blks),
        out_shape=(
            jax.ShapeDtypeStruct((tokens, model), BF16),
            jax.ShapeDtypeStruct((tokens, model), F32),
            jax.ShapeDtypeStruct((rows, 3 * model), F32),
            jax.ShapeDtypeStruct((rows, wide), F32),
            jax.ShapeDtypeStruct((model, ff), F32),
            jax.ShapeDtypeStruct((ff, model), F32),
        ),
        in_specs=hbm_specs(1) + vmem_specs(5) + hbm_specs(2) + vmem_specs(2) + hbm_specs(2) + vmem_specs(10),
        out_specs=tuple(vmem_specs(6)),
        scratch_shapes=[
            pltpu.VMEM((tokens, model), BF16),
            pltpu.VMEM((rows, 3 * model), BF16),
            pltpu.VMEM((1, rows), BF16),
            pltpu.VMEM(win.shape, BF16),
            pltpu.VMEM(wout.shape, BF16),
            dma(5),
            pltpu.VMEM((8, LANES), F32),
            block(4), block(4), block(2, 2), block(), pltpu.VMEM((span // 2, LANES), BF16),
            pltpu.VMEM((2, span, LANES), F32), pltpu.VMEM((span // 2, LANES), BF16),
            pltpu.VMEM((2, span, LANES), F32), block(),
            pltpu.VMEM((heads, tokens, model), BF16), pltpu.VMEM((heads, tokens, model), BF16),
            pltpu.VMEM((blks, rows, 2 * LANES), BF16), pltpu.VMEM((blks, rows, 2 * LANES), BF16),
            pltpu.VMEM((blks, rows, LANES), BF16), pltpu.VMEM((blks, rows, LANES), BF16),
            pltpu.VMEM((heads, tokens, model), F32), pltpu.VMEM((model, span), BF16),
            pltpu.VMEM(po.shape, BF16),
            pltpu.VMEM((heads, rows, 2 * LANES), BF16), pltpu.VMEM((heads, rows, LANES), BF16),
            pltpu.VMEM((heads, blks, part, wide), BF16), pltpu.VMEM((blks, part, wide), BF16),
            pltpu.VMEM((blks, part, wide), BF16), pltpu.VMEM((heads, part, wide), BF16),
            pltpu.SemaphoreType.DMA, pltpu.SemaphoreType.DMA, pltpu.SemaphoreType.DMA, pltpu.SemaphoreType.DMA,
            dma(4, 2), dma(4, 2), dma(4, 2), dma(2, 2, 2),
            dma(heads), dma(heads), dma(blks), dma(blks), dma(heads), dma(heads), dma(heads), dma(heads),
            dma(blks), dma(blks), dma(heads), dma(heads), dma(2), dma(2), dma(blks), dma(blks), dma(blks), dma(blks), dma(heads), dma(heads),
            pltpu.VMEM((2, model, ff // 2), BF16), pltpu.VMEM((2, ff // 2, model), BF16),
        ],
        compiler_params=pltpu.CompilerParams(
            collective_id=3, has_side_effects=True, vmem_limit_bytes=36 * MIB
        ),
        name="last",
    )(
        *in_hbm(x), dh, dq, dkv, xa, wa, *in_hbm(w_qkv, g1.reshape(1, rows)),
        grads.reshape(blks, heads, part, wide), rx, *in_hbm(win, wout), po, hidden, share,
        bounds, q, kv, kvt, d_o, lse, delta,
    )


def finish_kernel(
    experts,
    y_ref, dx_ref, dw_ref, shared_ref, din_ref, dout_ref,
    y_out, dx_out, g1_out, dw_out, dwo_out, g2_out, wr_out, din_out, dout_out,
    tile, wr, g2, g1, sem,
):
    rows = shared_ref.shape[0]
    model = dx_ref.shape[1]
    copies = [
        pltpu.make_async_copy(dx_ref, dx_out, sem.at[0]),
        pltpu.make_async_copy(dw_ref, dw_out, sem.at[1]),
        pltpu.make_async_copy(shared_ref.at[:, pl.ds(0, model)], dwo_out, sem.at[2]),
        pltpu.make_async_copy(y_ref, y_out, sem.at[6]),
        pltpu.make_async_copy(din_ref, din_out, sem.at[7]),
        pltpu.make_async_copy(dout_ref, dout_out, sem.at[8]),
    ]
    for copy in copies:
        copy.start()
    tile[...] = jnp.zeros_like(tile)
    tile[0:rows, :] = shared_ref[:, model : model + LANES]
    across = jnp.transpose(tile[...])[:, 0:rows]
    wr[...] = across[0:experts]
    g2[...] = across[experts : experts + 1]
    g1[...] = across[experts + 1 : experts + 2]
    for index, (src, dst) in enumerate(((wr, wr_out), (g2, g2_out), (g1, g1_out))):
        copies.append(pltpu.make_async_copy(src, dst, sem.at[3 + index]))
        copies[-1].start()
    for copy in copies:
        copy.wait()


def call_finish(output, dx, dw, shared, d_in, d_out):
    rows = shared.shape[0]
    model = dx.shape[1]
    experts = model // rows
    return pl.pallas_call(
        functools.partial(finish_kernel, experts),
        out_shape=(
            jax.ShapeDtypeStruct(output.shape, BF16),
            jax.ShapeDtypeStruct(dx.shape, F32),
            jax.ShapeDtypeStruct((1, rows), F32),
            jax.ShapeDtypeStruct(dw.shape, F32),
            jax.ShapeDtypeStruct((rows, model), F32),
            jax.ShapeDtypeStruct((1, rows), F32),
            jax.ShapeDtypeStruct((experts, rows), F32),
            jax.ShapeDtypeStruct(d_in.shape, F32),
            jax.ShapeDtypeStruct(d_out.shape, F32),
        ),
        in_specs=vmem_specs(6),
        out_specs=tuple(hbm_specs(9)),
        scratch_shapes=[
            pltpu.VMEM((LANES, LANES), F32),
            pltpu.VMEM((experts, rows), F32),
            pltpu.VMEM((1, rows), F32),
            pltpu.VMEM((1, rows), F32),
            dma(9),
        ],
        compiler_params=pltpu.CompilerParams(vmem_limit_bytes=16 * MIB),
        name="finish",
    )(output, dx, dw, shared, d_in, d_out)


def local_kernels(
    inputs, ln1_gain, w_qkv, w_out, ln2_gain, w_router,
    expert_in, expert_out, routes, priority, doc_lengths, d_out,
):
    heads, blks = lax.axis_size("head"), lax.axis_size("blk")
    model = inputs.shape[1]
    tokens = inputs.shape[0]
    win, wout = expert_in[0], expert_out[0]
    q, kv, xa, wa, wo, kvt, bounds, begun = call_qkv(
        inputs, w_qkv, ln1_gain, w_out, w_router, ln2_gain, doc_lengths, heads, blks
    )
    o, o_low, lse = call_forward(bounds, q, kv, kvt, begun)
    po, hidden, share, dh, d_o, grads, rx = call_middle(
        inputs, o_low.reshape(2, heads, tokens // 2, LANES), wo.reshape(model, model + LANES),
        routes, priority, d_out, win, wout, heads, blks,
    )
    d_o = d_o.reshape(2 * heads * tokens // QUERY_TILE, -1, HALF, LANES)
    dq, dkv, delta = call_backward(bounds, q, kv, kvt, d_o, o, lse)
    ends = call_last(
        inputs, dh, dq, dkv, xa, wa, w_qkv, ln1_gain, grads, rx, win, wout,
        po, hidden, share, bounds, q, kv, kvt, d_o, lse, delta, heads, blks,
    )
    output, d_inputs, d_gain_one, d_qkv, d_out_proj, d_gain_two, d_router, d_in, d_out_weight = call_finish(*ends)
    return (
        output,
        d_inputs,
        d_gain_one.reshape(-1),
        d_qkv,
        d_out_proj,
        d_gain_two.reshape(-1),
        d_router.T,
        d_in[None],
        d_out_weight[None],
    )


def solution(mesh):
    in_specs = (
        P(("blk", "head"), None),
        P("blk"),
        P("blk", None),
        P("blk", None),
        P("blk"),
        P("blk", None),
        P("blk", None, None),
        P("blk", None, None),
        P(("blk", "head"), None),
        P(("blk", "head"), None),
        P(),
        P(("blk", "head"), None),
    )
    out_specs = (
        P(("blk", "head"), None),
        P(("blk", "head"), None),
        P("blk"),
        P("blk", None),
        P("blk", None),
        P("blk"),
        P("blk", None),
        P("blk", None, None),
        P("blk", None, None),
    )
    fits = mesh.shape["head"] == 4 and mesh.shape["blk"] == 8
    body = local_kernels if fits else local
    return jax.shard_map(body, mesh=mesh, in_specs=in_specs, out_specs=out_specs, check_vma=False)
```
